32 devices in a mesh: dp: 8 (over z, x), mp: 4 (over y, core).
Axes of the slice: x: 2, y: 2, z: 4, core: 2. Of those that a mesh axis runs over, the one named last changes fastest.
Arguments:
- residual: bfloat16 [8, 512, 2048], P(None, 'dp', 'mp'), may hold values from -61 to 61
- attention_gain: bfloat16 [2048], P('mp'), may hold values from 0.25 to 1.75
- query_matrix: bfloat16 [2048, 2048], P(None, 'mp'), may hold values from -0.125 to 0.125
- key_value_matrix: bfloat16 [2, 2048, 512], P(None, None, 'mp'), may hold values from -0.125 to 0.125
- output_matrix: bfloat16 [2048, 2048], P('mp'), may hold values from -0.5 to 0.5
- feedfwd_gain: bfloat16 [2048], P('mp'), may hold values from 0.25 to 1.75
- gate_up_matrix: bfloat16 [2, 2048, 8192], P(None, None, 'mp'), may hold values from -0.125 to 0.125
- down_matrix: bfloat16 [8192, 2048], P('mp'), may hold values from -0.0625 to 0.0625
- attention_adapter_input: bfloat16 [8, 48, 2048], replicated, may hold values from -0.125 to 0.125
- query_adapter_output: bfloat16 [8, 16, 2048], P(None, None, 'mp'), may hold values from -0.75 to 0.75
- key_value_adapter_output: bfloat16 [8, 2, 16, 512], P(None, None, None, 'mp'), may hold values from -0.75 to 0.75
- output_adapter_input: bfloat16 [8, 16, 2048], P(None, None, 'mp'), may hold values from -0.5 to 0.5
- output_adapter_output: bfloat16 [8, 16, 2048], replicated, may hold values from -0.75 to 0.75
- feedfwd_adapter_input: bfloat16 [8, 32, 2048], replicated, may hold values from -0.125 to 0.125
- feedfwd_adapter_output: bfloat16 [8, 2, 16, 8192], P(None, None, None, 'mp'), may hold values from -0.75 to 0.75
- down_adapter_input: bfloat16 [8, 16, 8192], P(None, None, 'mp'), may hold values from -0.0625 to 0.0625
- down_adapter_output: bfloat16 [8, 16, 2048], replicated, may hold values from -0.75 to 0.75
- lengths: int32 [8], replicated, may hold values from 1 to 512, 2560 in all
- adapter_index: int32 [8], replicated, may hold values from 0 to 7
- dealing_slots: int32 [8], replicated, may hold values from 0 to 7, each once
- cotangent: bfloat16 [8, 512, 2048], P('dp', None, 'mp'), may hold values from -6 to 6
Outputs:
- output: bfloat16 [8, 512, 2048], P(None, 'dp', 'mp')
- input_grad: bfloat16 [8, 512, 2048], P(None, 'dp', 'mp')
- qkv_lora_a_grad: float32 [8, 48, 2048], replicated
- query_lora_b_grad: float32 [8, 16, 2048], P(None, None, 'mp')
- kv_lora_b_grad: float32 [8, 2, 16, 512], P(None, None, None, 'mp')
- out_lora_a_grad: float32 [8, 16, 2048], P(None, None, 'mp')
- out_lora_b_grad: float32 [8, 16, 2048], replicated
- ffn_lora_a_grad: float32 [8, 32, 2048], replicated
- ffn_lora_b_grad: float32 [8, 2, 16, 8192], P(None, None, None, 'mp')
- down_lora_a_grad: float32 [8, 16, 8192], P(None, None, 'mp')
- down_lora_b_grad: float32 [8, 16, 2048], replicated
The draws below stay inside these ranges and needn't reach their ends.
Inputs may be any that keep to these rules, and one draw needn't show every extreme that they name: `lengths`: the longest sequence has exactly 512 valid positions. `dealing_slots`: each slot receives exactly one sequence.
All inputs are finite; a program needn't handle non-finite values.
Results may differ from the reference program's by a relative error of at most 0.023.
Values may be sent and summed in bfloat16 or wider, within the bound.
No kernel may reach another device: no remote copies, remote signals or barrier semaphores. Data moves between devices by JAX's collectives and lax.ppermute only.
A program may use at most 192 MiB of HBM per device.

```python
import math
import jax
import jax.numpy as jnp
import numpy as np
from jax import lax

MODEL_WIDTH = 2048
QUERY_HEADS = 32
KEY_VALUE_HEADS = 8
HEAD_SIZE = 64
FEEDFWD_UNITS = 8192
ADAPTER_RANK = 16
ADAPTER_COUNT = 8
PADDED_LENGTH = 512
SEQS = 8
KEY_VALUE_COLS = 512
TOTAL = 2560


def draw_residual(key, part):
    base_key, row_key, col_key, column_key, sign_key, wobble_key = jax.random.split(key, 6)
    col_rise = jnp.exp(jnp.arange(MODEL_WIDTH, dtype=jnp.float32) * (jnp.log(3.0) / MODEL_WIDTH))
    base_draw = jnp.clip(jax.random.normal(base_key, (SEQS, PADDED_LENGTH, MODEL_WIDTH), jnp.float32), -6.0, 6.0)
    peak_factor = 2.0
    row_scale = jnp.exp(jax.random.uniform(row_key, (SEQS, PADDED_LENGTH, 1), jnp.float32, jnp.log(0.2), jnp.log(2.0)))
    col_scale = col_rise * jax.random.uniform(col_key, (MODEL_WIDTH,), jnp.float32, 0.7, 1.4)
    column_spot = jax.random.randint(column_key, (), 0, MODEL_WIDTH)
    spot_mask = (jnp.arange(MODEL_WIDTH) == column_spot).astype(jnp.float32)
    seq_sign = jnp.where(jax.random.bernoulli(sign_key, 0.5, (SEQS, 1, 1)), 1.0, -1.0)
    wobble_rows = 1.0 + 0.3 * jax.random.uniform(wobble_key, (SEQS, PADDED_LENGTH, 1), jnp.float32, -1.0, 1.0)
    peak_value = 0.25 * math.sqrt(MODEL_WIDTH) * peak_factor * seq_sign * wobble_rows
    values = base_draw * col_scale * (1.0 - spot_mask) + peak_value * spot_mask
    return (0.6 * values * row_scale).astype(jnp.bfloat16)


def with_ends(values, stream_key, least, top_value):
    extent = values.shape
    index_at = [jax.random.randint(jax.random.fold_in(stream_key, axis), (), 0, extent[axis]) for axis in range(len(extent))]
    values = values.at[tuple(index_at)].set(least)
    longest = extent.index(max(extent))
    index_at[longest] = (index_at[longest] + 1) % extent[longest]
    return values.at[tuple(index_at)].set(top_value)


def shard_levels(stream_key, dims, shards, smallest, top_value):
    loudness, own = 1.0, jax.random.fold_in(stream_key, 6)
    for position, parts in shards:
        heights = jnp.exp(jax.random.uniform(jax.random.fold_in(own, position), (parts,), jnp.float32, smallest / len(shards), top_value / len(shards)))
        loudness = loudness * jnp.repeat(heights, dims[position] // parts).reshape([-1 if axis == position else 1 for axis in range(len(dims))])
    return loudness


def profile(number_of, total, reach, skew):
    weights = [(1 << 20) // math.isqrt(rank ** skew) + 1 for rank in range(2, number_of + 1)]
    surplus, counts = total - reach - (number_of - 1), [1] * (number_of - 1)
    while surplus > 0:
        free = [i for i in range(number_of - 1) if counts[i] < reach]
        mass, budget = sum([weights[i] for i in free]), surplus
        for i in free:
            extra = min(reach - counts[i], max(1, budget * weights[i] // mass), surplus)
            counts[i] = counts[i] + extra
            surplus = surplus - extra
    return np.array([reach] + counts)


def uneven(stream_key, number_of, total, reach, lean):
    if number_of == 2:
        one = jax.random.randint(stream_key, (), max(1, total - reach), min(reach, total - 1) + 1)
        return jnp.stack([one, total - one])
    sizes = jnp.asarray(profile(number_of, total, reach, lean), jnp.int32)
    pairs = (number_of - 1) // 2
    source_of, sink = sizes[1:1 + 2 * pairs:2], sizes[2:2 + 2 * pairs:2]
    margin = jnp.minimum(source_of - 1, reach - sink)
    moved = jax.random.randint(jax.random.fold_in(stream_key, 1), (pairs,), 0, 1 << 20) % (margin + 1)
    sizes = sizes.at[1:1 + 2 * pairs:2].set(source_of - moved).at[2:2 + 2 * pairs:2].set(sink + moved)
    return sizes[jax.random.permutation(jax.random.fold_in(stream_key, 2), number_of)]


def bell_draw(stream_key, shape, spread, limit, shards=(), kind=jnp.bfloat16):
    values = jax.random.normal(stream_key, shape, jnp.float32) * spread
    if len(shards) > 0:
        values = shard_levels(stream_key, shape, shards, -0.22, 0.18) * values
    return jnp.clip(values, min=-limit, max=limit).astype(kind)


def setup_inputs(seed: int = 0) -> dict:
    key_list = jax.random.split(jax.random.key(seed), 22)
    residual = draw_residual(jax.random.fold_in(key_list[21], 71), 0)
    attention_gain = jnp.clip(1.0 + 0.15 * jax.random.normal(key_list[1], (MODEL_WIDTH,), jnp.float32), 0.25, 1.75).astype(jnp.bfloat16)
    query_matrix = bell_draw(key_list[2], (MODEL_WIDTH, MODEL_WIDTH), MODEL_WIDTH ** -0.5, 0.125, ((1, 4),))
    key_value_matrix = bell_draw(key_list[3], (2, MODEL_WIDTH, KEY_VALUE_COLS), MODEL_WIDTH ** -0.5, 0.125, ((2, 4),))
    output_matrix = bell_draw(key_list[4], (MODEL_WIDTH, MODEL_WIDTH), (MODEL_WIDTH // 16) ** -0.5, 0.5, ((0, 4),))
    feedfwd_gain = jnp.clip(1.0 + 0.15 * jax.random.normal(key_list[5], (MODEL_WIDTH,), jnp.float32), 0.25, 1.75).astype(jnp.bfloat16)
    gate_up_matrix = bell_draw(key_list[6], (2, MODEL_WIDTH, FEEDFWD_UNITS), MODEL_WIDTH ** -0.5, 0.125, ((2, 4),))
    down_matrix = bell_draw(key_list[7], (FEEDFWD_UNITS, MODEL_WIDTH), FEEDFWD_UNITS ** -0.5, 0.0625, ((0, 4),))
    attention_adapter_input = bell_draw(key_list[8], (ADAPTER_COUNT, 3 * ADAPTER_RANK, MODEL_WIDTH), MODEL_WIDTH ** -0.5, 0.125)
    query_adapter_output = bell_draw(key_list[9], (ADAPTER_COUNT, ADAPTER_RANK, MODEL_WIDTH), (4 * ADAPTER_RANK) ** -0.5, 0.75, ((2, 4),))
    key_value_adapter_output = bell_draw(key_list[10], (ADAPTER_COUNT, 2, ADAPTER_RANK, KEY_VALUE_COLS), (4 * ADAPTER_RANK) ** -0.5, 0.75, ((3, 4),))
    output_adapter_input = bell_draw(key_list[11], (ADAPTER_COUNT, ADAPTER_RANK, MODEL_WIDTH), (MODEL_WIDTH // 16) ** -0.5, 0.5, ((2, 4),))
    output_adapter_output = bell_draw(key_list[12], (ADAPTER_COUNT, ADAPTER_RANK, MODEL_WIDTH), (4 * ADAPTER_RANK) ** -0.5, 0.75)
    feedfwd_adapter_input = bell_draw(key_list[13], (ADAPTER_COUNT, 2 * ADAPTER_RANK, MODEL_WIDTH), MODEL_WIDTH ** -0.5, 0.125)
    feedfwd_adapter_output = bell_draw(key_list[14], (ADAPTER_COUNT, 2, ADAPTER_RANK, FEEDFWD_UNITS), (4 * ADAPTER_RANK) ** -0.5, 0.75, ((3, 4),))
    down_adapter_input = bell_draw(key_list[15], (ADAPTER_COUNT, ADAPTER_RANK, FEEDFWD_UNITS), FEEDFWD_UNITS ** -0.5, 0.0625, ((2, 4),))
    down_adapter_output = bell_draw(key_list[16], (ADAPTER_COUNT, ADAPTER_RANK, MODEL_WIDTH), (4 * ADAPTER_RANK) ** -0.5, 0.75)
    lengths = uneven(key_list[17], SEQS, TOTAL, PADDED_LENGTH, 1).astype(jnp.int32)
    adapter_index = with_ends(jax.random.randint(key_list[18], (SEQS,), 0, ADAPTER_COUNT), jax.random.fold_in(key_list[18], 1), 0, ADAPTER_COUNT - 1).astype(jnp.int32)
    dealing_slots = jax.random.permutation(key_list[19], SEQS).astype(jnp.int32)
    cotangent = bell_draw(key_list[20], (SEQS, PADDED_LENGTH, MODEL_WIDTH), 1.0, 6.0, ((0, 8), (2, 4)))
    return dict(residual=residual, attention_gain=attention_gain, query_matrix=query_matrix, key_value_matrix=key_value_matrix, output_matrix=output_matrix, feedfwd_gain=feedfwd_gain, gate_up_matrix=gate_up_matrix, down_matrix=down_matrix, attention_adapter_input=attention_adapter_input, query_adapter_output=query_adapter_output, key_value_adapter_output=key_value_adapter_output, output_adapter_input=output_adapter_input, output_adapter_output=output_adapter_output, feedfwd_adapter_input=feedfwd_adapter_input, feedfwd_adapter_output=feedfwd_adapter_output, down_adapter_input=down_adapter_input, down_adapter_output=down_adapter_output, lengths=lengths, adapter_index=adapter_index, dealing_slots=dealing_slots, cotangent=cotangent)


@jax.custom_vjp
def lowrank_rows(v):
    return lax.optimization_barrier(v.astype(jnp.bfloat16)).astype(jnp.float32)

@jax.custom_vjp
def low_back(v):
    return v

def low_keep(v):
    return (lowrank_rows(v), None)

def low_pass(kept, grad):
    return (grad,)

def back_keep(v):
    return (v, None)

def back_low(kept, grad):
    return (lowrank_rows(grad),)
lowrank_rows.defvjp(low_keep, low_pass)
low_back.defvjp(back_keep, back_low)
NORM_EPS = 1e-05
ROPE_BASE = 500000.0
NEG_FILL = -1e+30

def hi_dot(left_arr, right_arr):
    return jnp.dot(left_arr, right_arr, precision=lax.Precision.HIGHEST)

def rope_tables(length):
    half_dim = HEAD_SIZE // 2
    frequencies = ROPE_BASE ** (-jnp.arange(half_dim, dtype=jnp.float32) * (2.0 / HEAD_SIZE))
    angles = jnp.arange(length, dtype=jnp.float32)[:, None] * frequencies[None, :]
    cosine_table = jnp.cos(angles)
    sine_table = jnp.sin(angles)
    return (jnp.concatenate([cosine_table, cosine_table], -1), jnp.concatenate([sine_table, sine_table], -1))

def apply_rotation(vec, cosine_table, sine_table):
    half_dim = vec.shape[-1] // 2
    turned = jnp.concatenate([-vec[..., half_dim:], vec[..., :half_dim]], -1)
    return vec * cosine_table[:, None, :] + turned * sine_table[:, None, :]

def rms_scale(values):
    return lax.rsqrt(lax.optimization_barrier(jnp.mean(values * values, axis=-1, keepdims=True)) + NORM_EPS)

def one_layer(inputs, adapt, weights, length):
    attention_gain, query_matrix, key_value_matrix, output_matrix, feedfwd_gain, gate_up_matrix, down_matrix = weights
    attention_input_map, query_b, kv_b, out_a, output_map, feedfwd_input_map, ffn_b, down_a, down_output_map = adapt
    positions = jnp.arange(PADDED_LENGTH)
    valid_mask = (positions < length).astype(inputs.dtype)[:, None]
    normed = lowrank_rows(inputs * rms_scale(inputs) * attention_gain)
    first_lowrank = hi_dot(normed, attention_input_map.T)
    query_val = low_back(hi_dot(normed, query_matrix) + hi_dot(first_lowrank[:, :ADAPTER_RANK], query_b))
    key_rows = low_back(hi_dot(normed, key_value_matrix[0]) + hi_dot(first_lowrank[:, ADAPTER_RANK:2 * ADAPTER_RANK], kv_b[0]))
    value_rows = low_back(hi_dot(normed, key_value_matrix[1]) + hi_dot(first_lowrank[:, 2 * ADAPTER_RANK:], kv_b[1]))
    cosine_table, sine_table = rope_tables(PADDED_LENGTH)
    query_rot = lowrank_rows(apply_rotation(query_val.reshape(PADDED_LENGTH, QUERY_HEADS, HEAD_SIZE), cosine_table, sine_table))
    rotated_key = lowrank_rows(apply_rotation(key_rows.reshape(PADDED_LENGTH, KEY_VALUE_HEADS, HEAD_SIZE), cosine_table, sine_table))
    value_lowrank = lowrank_rows(value_rows.reshape(PADDED_LENGTH, KEY_VALUE_HEADS, HEAD_SIZE))
    query_group_count = QUERY_HEADS // KEY_VALUE_HEADS
    key_wide = jnp.repeat(rotated_key, query_group_count, axis=1)
    value_wide = jnp.repeat(value_lowrank, query_group_count, axis=1)
    raw_scores = low_back(jnp.einsum('qhd,khd->hqk', query_rot, key_wide, precision=lax.Precision.HIGHEST))
    visible = (positions[None, :] <= positions[:, None]) & (positions[None, :] < length)
    scores = jnp.where(visible[None], raw_scores * HEAD_SIZE ** (-0.5), NEG_FILL)
    row_max = lax.optimization_barrier(jnp.max(scores, axis=-1, keepdims=True))
    log_total = row_max + jnp.log(lax.optimization_barrier(jnp.sum(jnp.exp(scores - row_max), axis=-1, keepdims=True)))
    probs = lowrank_rows(jnp.exp(scores - log_total))
    attn_out = jnp.einsum('hqk,khd->qhd', probs, value_wide, precision=lax.Precision.HIGHEST).reshape(PADDED_LENGTH, MODEL_WIDTH)
    attn_out = lowrank_rows(low_back(attn_out))
    output_lowrank = hi_dot(attn_out, out_a.T)
    middle = inputs + low_back(hi_dot(attn_out, output_matrix) + hi_dot(output_lowrank, output_map))
    normed_two = lowrank_rows(middle * rms_scale(middle) * feedfwd_gain)
    second_lowrank = hi_dot(normed_two, feedfwd_input_map.T)
    gate_val = low_back(hi_dot(normed_two, gate_up_matrix[0]) + hi_dot(second_lowrank[:, :ADAPTER_RANK], ffn_b[0]))
    up_val = low_back(hi_dot(normed_two, gate_up_matrix[1]) + hi_dot(second_lowrank[:, ADAPTER_RANK:], ffn_b[1]))
    activation = lowrank_rows(gate_val / (1.0 + jnp.exp(-gate_val)) * up_val)
    down_lowrank = hi_dot(activation, down_a.T)
    branch = low_back(hi_dot(activation, down_matrix) + hi_dot(down_lowrank, down_output_map))
    return (middle + branch) * valid_mask

def reference(residual, attention_gain, query_matrix, key_value_matrix, output_matrix, feedfwd_gain, gate_up_matrix, down_matrix, attention_adapter_input, query_adapter_output, key_value_adapter_output, output_adapter_input, output_adapter_output, feedfwd_adapter_input, feedfwd_adapter_output, down_adapter_input, down_adapter_output, lengths, adapter_index, dealing_slots, cotangent):
    weights = tuple((w_arr.astype(jnp.float32) for w_arr in (attention_gain, query_matrix, key_value_matrix, output_matrix, feedfwd_gain, gate_up_matrix, down_matrix)))
    stacked_arrays = tuple((sequence_array.astype(jnp.float32) for sequence_array in (attention_adapter_input, query_adapter_output, key_value_adapter_output, output_adapter_input, output_adapter_output, feedfwd_adapter_input, feedfwd_adapter_output, down_adapter_input, down_adapter_output)))
    given_cot = jnp.take(cotangent, dealing_slots.astype(jnp.int32), axis=0)

    def per_sequence(carry, seq_item):
        inputs, cot_rows, length, which = seq_item
        chosen = tuple((sequence_array[which] for sequence_array in stacked_arrays))

        def apply_layer(in_rows, adapt):
            return one_layer(in_rows, adapt, weights, length)
        result, pullback = jax.vjp(apply_layer, inputs.astype(jnp.float32), chosen)
        grad_in, grad_adapt = pullback(cot_rows.astype(jnp.float32))
        carry = tuple((c_arr.at[which].add(g_arr) for c_arr, g_arr in zip(carry, grad_adapt)))
        return (carry, (result.astype(jnp.bfloat16), grad_in.astype(jnp.bfloat16)))
    start_grads = tuple((jnp.zeros_like(sequence_array) for sequence_array in stacked_arrays))
    grads, (outputs, input_grads) = lax.scan(per_sequence, start_grads, (residual, given_cot, lengths, adapter_index))
    return (outputs, input_grads, grads[0], grads[1], grads[2], grads[3], grads[4], grads[5], grads[6], grads[7], grads[8])
```

```python
import functools

import jax
import jax.numpy as jnp
import numpy as np
from jax import lax
from jax.experimental import pallas as pl
from jax.experimental.pallas import tpu as pltpu
from jax.sharding import PartitionSpec as P

WIDTH = 2048
HEAD = 64
HALF = HEAD // 2
RANK = 16
EPS = 1e-05
ROPE_BASE = 500000.0
NEG_FILL = -1e30
PARTS = 4
QUARTER = WIDTH // PARTS
UNIT_BLOCK = 512
VMEM_LIMIT = 60 * 1024 * 1024
F32 = jnp.float32
BF16 = jnp.bfloat16


def nn(a, b):
    return lax.dot_general(a, b, (((1,), (0,)), ((), ())), preferred_element_type=F32)


def nt(a, b):
    return lax.dot_general(a, b, (((1,), (1,)), ((), ())), preferred_element_type=F32)


def rope_tables(length):
    freq = ROPE_BASE ** (-np.arange(HALF, dtype=np.float32) * np.float32(2.0 / HEAD))
    angles = (np.arange(length, dtype=np.float32)[None, :] * freq.astype(np.float32)[:, None]).astype(np.float32)
    return np.cos(angles).astype(np.float32), np.sin(angles).astype(np.float32)


def quarter(me, rel):
    return pl.ds(pl.multiple_of((me ^ rel) * QUARTER, QUARTER), QUARTER)


def total_block(rel, own, own_y, oth, oth_y):
    near, far = (own, own_y) if rel in (0, 2) else (oth, oth_y)
    lo, hi = slice(0, QUARTER), slice(QUARTER, 2 * QUARTER)
    first, second = (lo, hi) if rel in (0, 1) else (hi, lo)
    return near[:, first].astype(F32) + far[:, second].astype(F32)


def put_halves(me, whole, keep_ref, send_ref):
    lo, hi = slice(0, QUARTER), slice(QUARTER, 2 * QUARTER)
    keep_ref[:, lo] = whole[:, quarter(me, 0)].astype(keep_ref.dtype)
    keep_ref[:, hi] = whole[:, quarter(me, 2)].astype(keep_ref.dtype)
    send_ref[:, lo] = whole[:, quarter(me, 1)].astype(send_ref.dtype)
    send_ref[:, hi] = whole[:, quarter(me, 3)].astype(send_ref.dtype)


def attention_forward_kernel(
    info, x0, x1, x2, x3, gains, a1, qb, kvb, wq, wkv, oa, ob, wo, cos_t, sin_t,
    z_keep, z_send, h_out, t1t_out, qt_out, kn_out, vn_out, kt_out, ot_out, lse_out, tot_out,
    vt_s, acc_s,
):
    me, length = info[0], info[1]
    rows = x0.shape[0]
    kv_heads = kn_out.shape[0]
    heads = qt_out.shape[0] // HEAD
    group = heads // kv_heads
    xs = (x0, x1, x2, x3)
    square = jnp.zeros((rows, 1), F32)
    for r in range(PARTS):
        v = xs[r][...].astype(F32)
        square = square + jnp.sum(v * v, axis=1, keepdims=True)
    inv = lax.rsqrt(square / WIDTH + EPS)
    for r in range(PARTS):
        v = xs[r][...].astype(F32)
        h_out[:, quarter(me, r)] = (v * inv * gains[r, 0:1, :].astype(F32)).astype(BF16)
    h = h_out[...]
    t1 = nt(h, a1[0])
    t1t_out[...] = t1.T.astype(BF16)
    t1b = t1.astype(BF16)
    cos, sin = cos_t[...], sin_t[...]
    q = nn(h, wq[...]) + nn(t1b[:, :RANK], qb[0])
    q_t = q.T * (HEAD ** -0.5)
    for i in range(heads):
        u1, u2 = q_t[i * HEAD:i * HEAD + HALF], q_t[i * HEAD + HALF:(i + 1) * HEAD]
        qt_out[i * HEAD:i * HEAD + HALF, :] = (u1 * cos - u2 * sin).astype(BF16)
        qt_out[i * HEAD + HALF:(i + 1) * HEAD, :] = (u2 * cos + u1 * sin).astype(BF16)
    k_t = (nn(h, wkv[0]) + nn(t1b[:, RANK:2 * RANK], kvb[0, 0])).T
    for i in range(kv_heads):
        u1, u2 = k_t[i * HEAD:i * HEAD + HALF], k_t[i * HEAD + HALF:(i + 1) * HEAD]
        kt_out[i * HEAD:i * HEAD + HALF, :] = (u1 * cos - u2 * sin).astype(BF16)
        kt_out[i * HEAD + HALF:(i + 1) * HEAD, :] = (u2 * cos + u1 * sin).astype(BF16)
    k_n = kt_out[...].T
    v_n = (nn(h, wkv[1]) + nn(t1b[:, 2 * RANK:], kvb[0, 1])).astype(BF16)
    for i in range(kv_heads):
        kn_out[i] = k_n[:, i * HEAD:(i + 1) * HEAD]
        vn_out[i] = v_n[:, i * HEAD:(i + 1) * HEAD]
    vt_s[...] = v_n.T
    kpos = lax.broadcasted_iota(jnp.int32, (rows, rows), 0)
    qpos = lax.broadcasted_iota(jnp.int32, (rows, rows), 1)
    kept = (kpos <= qpos) & (kpos < length)

    def one_head(i, carry):
        j = i // group
        scores = nn(kn_out[j], qt_out[pl.ds(pl.multiple_of(i * HEAD, HEAD), HEAD), :])
        scores = jnp.where(kept, scores, NEG_FILL)
        top = jnp.max(scores, axis=0, keepdims=True)
        e = jnp.exp(scores - top)
        total = jnp.sum(e, axis=0, keepdims=True)
        lse_out[pl.ds(i, 1), :] = top + jnp.log(total)
        o_t = nn(vt_s[pl.ds(pl.multiple_of(j * HEAD, HEAD), HEAD), :], e.astype(BF16)) / total
        ot_out[pl.ds(pl.multiple_of(i * HEAD, HEAD), HEAD), :] = o_t.astype(BF16)
        return carry

    lax.fori_loop(0, heads, one_head, 0)
    o = ot_out[...].T
    to = nt(o, oa[0])
    tot_out[...] = to.T.astype(BF16)
    acc_s[...] = nn(o, wo[...]) + nn(to.astype(BF16), ob[0])
    put_halves(me, acc_s, z_keep, z_send)


def feedforward_kernel(
    info, x0, x1, x2, x3, zo, zoy, zp, zpy, g0, g1, g2, g3, gains, a2, bd, fb, da, wgu, wd,
    x_out, xq_out, z_keep, z_send, d_keep, d_send, b_out, a_keep, a_send,
    h_s, g_s, z_s, d_s, t2_s, t2t_s, dtd_s, dtdt_s, td_s, dt2_s, ga_s,
):
    me, length = info[0], info[1]
    rows = x0.shape[0]
    step = pl.program_id(0)

    @pl.when(step == 0)
    def _():
        xs, gs = (x0, x1, x2, x3), (g0, g1, g2, g3)
        square = jnp.zeros((rows, 1), F32)
        valid = lax.broadcasted_iota(jnp.int32, (rows, 1), 0) < length
        for r in range(PARTS):
            v = xs[r][...].astype(F32) + total_block(r, zo, zoy, zp, zpy)
            if r == 0:
                xq_out[...] = v
            z_s[:, quarter(me, r)] = v
            square = square + jnp.sum(v * v, axis=1, keepdims=True)
            g_s[:, quarter(me, r)] = jnp.where(valid, gs[r][...], jnp.zeros((), BF16))
        inv = lax.rsqrt(square / WIDTH + EPS)
        for r in range(PARTS):
            v = z_s[:, quarter(me, r)]
            x_out[:, quarter(me, r)] = v.astype(BF16)
            h_s[:, quarter(me, r)] = (v * inv * gains[r, 1:2, :].astype(F32)).astype(BF16)
        t2 = nt(h_s[...], a2[0])
        t2_s[...] = t2.astype(BF16)
        t2t_s[...] = t2.T.astype(BF16)
        dtd = nt(g_s[...], bd[0])
        dtd_s[...] = dtd.astype(BF16)
        dtdt_s[...] = dtd.T.astype(BF16)
        z_s[...] = jnp.zeros_like(z_s)
        d_s[...] = jnp.zeros_like(d_s)
        td_s[...] = jnp.zeros_like(td_s)
        dt2_s[...] = jnp.zeros_like(dt2_s)

    h, g = h_s[...], g_s[...]
    fb0, fb1, dab = fb[0, 0], fb[0, 1], da[0]
    gate = nn(h, wgu[0]) + nn(t2_s[:, :RANK], fb0)
    up = nn(h, wgu[1]) + nn(t2_s[:, RANK:], fb1)
    dact = nt(g, wd[...]) + nn(dtd_s[...], dab)
    sig = 1.0 / (1.0 + jnp.exp(-gate))
    silu = gate * sig
    act = (silu * up).astype(BF16)
    dgate = (dact * up * sig * (1.0 + gate * (1.0 - sig))).astype(BF16)
    dup = (dact * silu).astype(BF16)
    z_s[...] += nn(act, wd[...])
    d_s[...] += nt(dgate, wgu[0]) + nt(dup, wgu[1])
    td_s[...] += nt(act, dab)
    dt2_s[:, :RANK] += nt(dgate, fb0)
    dt2_s[:, RANK:] += nt(dup, fb1)
    b_out[0:RANK, :] = nn(t2t_s[:RANK, :], dgate).astype(BF16)
    b_out[RANK:2 * RANK, :] = nn(t2t_s[RANK:, :], dup).astype(BF16)
    b_out[2 * RANK:, :] = nn(dtdt_s[...], act).astype(BF16)

    @pl.when(step == pl.num_programs(0) - 1)
    def _():
        td, dt2 = td_s[...], dt2_s[...]
        z_s[...] += nn(td.astype(BF16), bd[0])
        put_halves(me, z_s, z_keep, z_send)
        d_s[...] += nn(dt2.astype(BF16), a2[0])
        put_halves(me, d_s, d_keep, d_send)
        ga_s[0:2 * RANK, :] = nn(dt2.T.astype(BF16), h_s[...])
        ga_s[2 * RANK:, :] = nn(td.T.astype(BF16), g_s[...])
        put_halves(me, ga_s, a_keep, a_send)


def attention_backward_kernel(
    info, x0, x1, x2, x3, g0, g1, g2, g3, xm, do_, doy, dp, dpy, gains, a1, qb, kvb, wq, wkv, oa, ob, wo,
    cos_t, sin_t, h_in, t1t, qt, kn, vn, kt, ot, lse, tot,
    dxq_out, h_keep, h_send, dot_out, b_out, a_keep, a_send,
    z_s, acc_s, dot_s, dqt_s, dkt_s, dvt_s, dq_s, ga_s,
):
    me, length = info[0], info[1]
    rows = x0.shape[0]
    kv_heads = kn.shape[0]
    heads = qt.shape[0] // HEAD
    group = heads // kv_heads
    xs, gs = (x0, x1, x2, x3), (g0, g1, g2, g3)
    valid = lax.broadcasted_iota(jnp.int32, (rows, 1), 0) < length
    square = jnp.zeros((rows, 1), F32)
    inner = jnp.zeros((rows, 1), F32)
    for r in range(PARTS):
        v = xm[:, quarter(me, r)].astype(F32)
        square = square + jnp.sum(v * v, axis=1, keepdims=True)
        w = total_block(r, do_, doy, dp, dpy) * gains[r, 1:2, :].astype(F32)
        acc_s[:, quarter(me, r)] = w
        inner = inner + jnp.sum(v * w, axis=1, keepdims=True)
    inv = lax.rsqrt(square / WIDTH + EPS)
    back = inv * inv * inv * inner / WIDTH
    for r in range(PARTS):
        v = xm[:, quarter(me, r)].astype(F32)
        g = jnp.where(valid, gs[r][...].astype(F32), 0.0)
        d = g + inv * acc_s[:, quarter(me, r)] - v * back
        if r == 0:
            dxq_out[...] = d
        z_s[:, quarter(me, r)] = d.astype(BF16)
    dz = z_s[...]
    dto = nt(dz, ob[0])
    dto_t = dto.T.astype(BF16)
    d_o = nt(dz, wo[...]) + nn(dto.astype(BF16), oa[0])
    dot_s[...] = d_o.T.astype(BF16)
    b_out[RANK:2 * RANK, :] = nt(dto_t, ot[...]).astype(BF16)
    ga_s[3 * RANK:, :] = nn(tot[...], dz)
    dkt_s[...] = jnp.zeros_like(dkt_s)
    dvt_s[...] = jnp.zeros_like(dvt_s)
    kpos = lax.broadcasted_iota(jnp.int32, (rows, rows), 0)
    qpos = lax.broadcasted_iota(jnp.int32, (rows, rows), 1)
    kept = (kpos <= qpos) & (kpos < length)

    def one_head(i, carry):
        j = i // group
        at = pl.ds(pl.multiple_of(i * HEAD, HEAD), HEAD)
        kv_at = pl.ds(pl.multiple_of(j * HEAD, HEAD), HEAD)
        q_h, do_h = qt[at, :], dot_s[at, :]
        scores = nn(kn[j], q_h)
        prob = jnp.where(kept, jnp.exp(scores - lse[pl.ds(i, 1), :]), 0.0)
        dprob = nn(vn[j], do_h)
        dots = jnp.sum(do_h.astype(F32) * ot[at, :].astype(F32), axis=0, keepdims=True)
        ds = (prob * (dprob - dots)).astype(BF16)
        dqt_s[at, :] = nn(kt[kv_at, :], ds)
        dkt_s[kv_at, :] += nt(q_h, ds)
        dvt_s[kv_at, :] += nt(do_h, prob.astype(BF16))
        return carry

    lax.fori_loop(0, heads, one_head, 0)
    cos, sin = cos_t[...], sin_t[...]
    cos_q, sin_q = cos * (HEAD ** -0.5), sin * (HEAD ** -0.5)
    for i in range(heads):
        lo, hi = slice(i * HEAD, i * HEAD + HALF), slice(i * HEAD + HALF, (i + 1) * HEAD)
        w1, w2 = dqt_s[lo, :], dqt_s[hi, :]
        dot_s[lo, :] = (w1 * cos_q + w2 * sin_q).astype(BF16)
        dot_s[hi, :] = (w2 * cos_q - w1 * sin_q).astype(BF16)
    q_cols = heads * HEAD
    kv_cols = kv_heads * HEAD
    dq_s[:, :q_cols] = dot_s[...].T
    for i in range(kv_heads):
        lo, hi = slice(i * HEAD, i * HEAD + HALF), slice(i * HEAD + HALF, (i + 1) * HEAD)
        w1, w2 = dkt_s[lo, :], dkt_s[hi, :]
        dkt_s[lo, :] = w1 * cos + w2 * sin
        dkt_s[hi, :] = w2 * cos - w1 * sin
    dq_s[:, q_cols:q_cols + kv_cols] = dkt_s[...].T.astype(BF16)
    dq_s[:, q_cols + kv_cols:] = dvt_s[...].T.astype(BF16)
    dq, dk, dv = dq_s[:, :q_cols], dq_s[:, q_cols:q_cols + kv_cols], dq_s[:, q_cols + kv_cols:]
    dt1 = jnp.concatenate([nt(dq, qb[0]), nt(dk, kvb[0, 0]), nt(dv, kvb[0, 1])], axis=1)
    b_out[0:RANK, :] = nn(t1t[:RANK, :], dq).astype(BF16)
    b_out[2 * RANK:, :] = jnp.zeros_like(b_out[2 * RANK:, :])
    b_out[2 * RANK:, :kv_cols] = nn(t1t[RANK:2 * RANK, :], dk).astype(BF16)
    b_out[2 * RANK:, kv_cols:2 * kv_cols] = nn(t1t[2 * RANK:, :], dv).astype(BF16)
    ga_s[:3 * RANK, :] = nn(dt1.T.astype(BF16), h_in[...])
    put_halves(me, ga_s, a_keep, a_send)
    acc_s[...] = nt(dq, wq[...]) + nt(dk, wkv[0]) + nt(dv, wkv[1]) + nn(dt1.astype(BF16), a1[0])
    inner = jnp.zeros((rows, 1), F32)
    for r in range(PARTS):
        w = acc_s[:, quarter(me, r)] * gains[r, 0:1, :].astype(F32)
        inner = inner + jnp.sum(w * xs[r][...].astype(F32), axis=1, keepdims=True)
    dot_out[...] = inner
    put_halves(me, acc_s, h_keep, h_send)


def feedforward_sum_kernel(info, owners, b0, a0, a1, a2, a3, ga, gdb, gb, gda):
    adapter = pl.program_id(0)
    me, place = info[0], info[3]
    slots = b0.shape[0]
    blocks = gda.shape[2] // UNIT_BLOCK
    for ref in (ga, gdb, gb, gda):
        ref[...] = jnp.zeros_like(ref)

    def add(slot, carry):
        @pl.when(owners[slot] == adapter)
        def _():
            at = slot ^ place
            for i in range(blocks):
                cols = slice(i * UNIT_BLOCK, (i + 1) * UNIT_BLOCK)
                base = i * 3 * RANK
                gb[0, 0, :, cols] += b0[at, base:base + RANK, :].astype(F32)
                gb[0, 1, :, cols] += b0[at, base + RANK:base + 2 * RANK, :].astype(F32)
                gda[0, :, cols] += b0[at, base + 2 * RANK:base + 3 * RANK, :].astype(F32)
            for r, ref in enumerate((a0, a1, a2, a3)):
                ga[0, :, quarter(me, r)] += ref[at, :2 * RANK, :].astype(F32)
                gdb[0, :, quarter(me, r)] += ref[at, 2 * RANK:, :].astype(F32)
        return carry

    lax.fori_loop(0, slots, add, 0)


def attention_sum_kernel(info, owners, b0, a0, a1, a2, a3, ga, gob, gq, gkv, goa):
    adapter = pl.program_id(0)
    me, place = info[0], info[3]
    slots = b0.shape[0]
    kv_cols = gkv.shape[3]
    for ref in (ga, gob, gq, gkv, goa):
        ref[...] = jnp.zeros_like(ref)

    def add(slot, carry):
        @pl.when(owners[slot] == adapter)
        def _():
            at = slot ^ place
            gq[0] += b0[at, :RANK, :].astype(F32)
            goa[0] += b0[at, RANK:2 * RANK, :].astype(F32)
            gkv[0, 0] += b0[at, 2 * RANK:, :kv_cols].astype(F32)
            gkv[0, 1] += b0[at, 2 * RANK:, kv_cols:2 * kv_cols].astype(F32)
            for r, ref in enumerate((a0, a1, a2, a3)):
                ga[0, :, quarter(me, r)] += ref[at, :3 * RANK, :].astype(F32)
                gob[0, :, quarter(me, r)] += ref[at, 3 * RANK:, :].astype(F32)
        return carry

    lax.fori_loop(0, slots, add, 0)


def whole_spec(shape):
    zeros = (0,) * len(shape)
    return pl.BlockSpec(tuple(shape), lambda i, *_: zeros)


def adapter_spec(shape, tile=None):
    zeros = (0,) * (len(shape) - 1)
    block = (1,) + tuple(shape[1:])
    if tile is None:
        return pl.BlockSpec(block, lambda i, info, *_: (info[2],) + zeros)
    return pl.BlockSpec(block[:-1] + (tile,), lambda i, info, *_: (info[2],) + zeros[:-1] + (i,))


def call(kernel, grid, scalars, args, in_specs, out_shapes, out_specs, scratch, name):
    return pl.pallas_call(
        kernel,
        grid_spec=pltpu.PrefetchScalarGridSpec(
            num_scalar_prefetch=len(scalars),
            grid=(grid,),
            in_specs=in_specs,
            out_specs=out_specs,
            scratch_shapes=scratch,
        ),
        out_shape=out_shapes,
        compiler_params=pltpu.CompilerParams(
            dimension_semantics=("arbitrary",), vmem_limit_bytes=VMEM_LIMIT
        ),
        name=name,
    )(*scalars, *args)


def sds(shape, dtype):
    return jax.ShapeDtypeStruct(tuple(shape), dtype)


def swap(value, bit, axis, size):
    return lax.ppermute(value, axis, [(i, i ^ bit) for i in range(size)])


def near(value):
    return swap(value, 1, "mp", PARTS)


def far(value):
    return swap(value, 2, "mp", PARTS)


def spread(value):
    there = far(value)
    return (value, near(value), there, near(there))


def chip_sum(keep, send):
    got = near(send)
    lo = keep[:, :QUARTER].astype(F32) + got[:, :QUARTER].astype(F32)
    hi = keep[:, QUARTER:].astype(F32) + got[:, QUARTER:].astype(F32)
    return lo, hi.astype(BF16)


def reduce_scatter(keep, send):
    lo, hi = chip_sum(keep, send)
    return lo + far(hi).astype(F32)


def reduce_all(keep, send):
    own = (keep.astype(F32) + near(send).astype(F32)).astype(BF16)
    own_y = far(own)
    return own, own_y, near(own), near(own_y)


def gather_slots(value, size):
    stack = value[None]
    bits = [1 << b for b in range(size.bit_length() - 1)]
    for bit in bits:
        stack = jnp.concatenate([stack, swap(stack, bit, "dp", size)], axis=0)
    return stack


def shards(dp, residual, attention_gain, query_matrix, key_value_matrix, output_matrix, feedfwd_gain,
           gate_up_matrix, down_matrix, attention_adapter_input, query_adapter_output,
           key_value_adapter_output, output_adapter_input, output_adapter_output, feedfwd_adapter_input,
           feedfwd_adapter_output, down_adapter_input, down_adapter_output, lengths, adapter_index,
           dealing_slots, cotangent):
    seqs = residual.shape[0]
    rows = cotangent.shape[1]
    units = down_matrix.shape[0]
    adapters = attention_adapter_input.shape[0]
    q_cols = query_matrix.shape[1]
    kv_cols = key_value_matrix.shape[2]
    kv_heads = kv_cols // HEAD
    heads = q_cols // HEAD
    me = lax.axis_index("mp")
    place = lax.axis_index("dp")

    is_there = dealing_slots[None, :] == jnp.arange(seqs, dtype=jnp.int32)[:, None]
    seq_of_slot = jnp.sum(jnp.where(is_there, jnp.arange(seqs, dtype=jnp.int32)[None, :], 0), axis=1)
    owners = jnp.sum(jnp.where(is_there, adapter_index[None, :], 0), axis=1)
    spans = jnp.sum(jnp.where(is_there, lengths[None, :], 0), axis=1)
    mine = jnp.arange(seqs, dtype=jnp.int32) == place
    my_length = jnp.sum(jnp.where(mine, spans, 0))
    my_adapter = jnp.sum(jnp.where(mine, owners, 0))
    info = jnp.stack([me.astype(jnp.int32), my_length, my_adapter, place.astype(jnp.int32)])

    dealt = lax.all_to_all(
        jnp.take(residual, seq_of_slot, axis=0), "dp", split_axis=0, concat_axis=1, tiled=True
    )[0]
    gs = spread(cotangent[0])
    gains = jnp.stack(spread(jnp.stack([attention_gain, feedfwd_gain])))
    xs = spread(dealt)
    cos_np, sin_np = rope_tables(rows)
    cos_t, sin_t = jnp.asarray(cos_np), jnp.asarray(sin_np)

    half = 2 * QUARTER
    col = (rows, half)
    block = (rows, QUARTER)

    fwd_args = (*xs, gains, attention_adapter_input, query_adapter_output, key_value_adapter_output, query_matrix,
                key_value_matrix, output_adapter_input, output_adapter_output, output_matrix, cos_t, sin_t)
    by_adapter = (attention_adapter_input, query_adapter_output, key_value_adapter_output, output_adapter_input,
                  output_adapter_output, feedfwd_adapter_input, feedfwd_adapter_output, down_adapter_input,
                  down_adapter_output)

    def specs(args):
        return [adapter_spec(a.shape) if any(a is b for b in by_adapter) else whole_spec(a.shape) for a in args]

    outs = [sds(col, F32), sds(col, BF16), sds((rows, WIDTH), BF16), sds((3 * RANK, rows), BF16),
            sds((q_cols, rows), BF16), sds((kv_heads, rows, HEAD), BF16), sds((kv_heads, rows, HEAD), BF16),
            sds((kv_cols, rows), BF16), sds((q_cols, rows), BF16), sds((heads, rows), F32), sds((RANK, rows), BF16)]
    z_keep, z_send, h1, t1t, qt, kn, vn, kt, ot, lse, tot = call(
        attention_forward_kernel, 1, (info,), fwd_args, specs(fwd_args), outs, [whole_spec(o.shape) for o in outs],
        [pltpu.VMEM((kv_cols, rows), BF16), pltpu.VMEM((rows, WIDTH), F32)], "attention_forward")
    branch = reduce_all(z_keep, z_send)

    ffn_args = (*xs, *branch, *gs, gains, feedfwd_adapter_input, down_adapter_output, feedfwd_adapter_output,
                down_adapter_input, gate_up_matrix, down_matrix)
    ffn_specs = specs(ffn_args)
    ffn_specs[-4] = adapter_spec(feedfwd_adapter_output.shape, UNIT_BLOCK)
    ffn_specs[-3] = adapter_spec(down_adapter_input.shape, UNIT_BLOCK)
    ffn_specs[-2] = pl.BlockSpec((2, WIDTH, UNIT_BLOCK), lambda i, *_: (0, 0, i))
    ffn_specs[-1] = pl.BlockSpec((UNIT_BLOCK, WIDTH), lambda i, *_: (i, 0))
    steps = units // UNIT_BLOCK
    outs = [sds((rows, WIDTH), BF16), sds(block, F32), sds(col, F32), sds(col, BF16), sds(col, F32), sds(col, BF16),
            sds((steps * 3 * RANK, UNIT_BLOCK), BF16), sds((3 * RANK, half), BF16), sds((3 * RANK, half), BF16)]
    out_specs = [whole_spec(o.shape) for o in outs]
    out_specs[6] = pl.BlockSpec((3 * RANK, UNIT_BLOCK), lambda i, *_: (i, 0))
    middle, middle_q, y_keep, y_send, d_keep, d_send, ffn_b, fa_keep, fa_send = call(
        feedforward_kernel, steps, (info,), ffn_args, ffn_specs, outs, out_specs,
        [pltpu.VMEM((rows, WIDTH), BF16), pltpu.VMEM((rows, WIDTH), BF16), pltpu.VMEM((rows, WIDTH), F32),
         pltpu.VMEM((rows, WIDTH), F32), pltpu.VMEM((rows, 2 * RANK), BF16), pltpu.VMEM((2 * RANK, rows), BF16),
         pltpu.VMEM((rows, RANK), BF16), pltpu.VMEM((RANK, rows), BF16), pltpu.VMEM((rows, RANK), F32),
         pltpu.VMEM((rows, 2 * RANK), F32), pltpu.VMEM((3 * RANK, WIDTH), F32)], "feedforward")
    back = reduce_all(d_keep, d_send)

    valid = (jnp.arange(rows, dtype=jnp.int32) < my_length)[:, None]
    result = jnp.where(valid, middle_q + reduce_scatter(y_keep, y_send), 0.0).astype(BF16)
    back_out = lax.all_to_all(
        result.reshape(dp, rows // dp, QUARTER), "dp", split_axis=0, concat_axis=0, tiled=True)
    output = jnp.take(back_out, dealing_slots, axis=0)

    ffn_pack = gather_slots(jnp.concatenate([ffn_b, reduce_scatter(fa_keep, fa_send).astype(BF16)], axis=0), dp)
    n_b = ffn_b.shape[0]
    fa = spread(ffn_pack[:, n_b:])
    sum_args = (ffn_pack[:, :n_b], *fa)
    outs = [sds((adapters, 2 * RANK, WIDTH), F32), sds((adapters, RANK, WIDTH), F32),
            sds((adapters, 2, RANK, units), F32), sds((adapters, RANK, units), F32)]
    ga_ffn, g_down_b, g_ffn_b, g_down_a = call(
        feedforward_sum_kernel, adapters, (info, owners), sum_args, [whole_spec(a.shape) for a in sum_args], outs,
        [pl.BlockSpec((1,) + o.shape[1:], (lambda n: lambda i, *_: (i,) + (0,) * n)(len(o.shape) - 1)) for o in outs],
        [], "feedforward_sum")

    bwd_args = (*xs, *gs, middle, *back, *fwd_args[4:], h1, t1t, qt, kn, vn, kt, ot, lse, tot)
    outs = [sds(block, F32), sds(col, F32), sds(col, BF16), sds((rows, 1), F32), sds((3 * RANK, QUARTER), BF16),
            sds((4 * RANK, half), BF16), sds((4 * RANK, half), BF16)]
    dmiddle_q, h_keep, h_send, inner, att_b, aa_keep, aa_send = call(
        attention_backward_kernel, 1, (info,), bwd_args, specs(bwd_args), outs, [whole_spec(o.shape) for o in outs],
        [pltpu.VMEM((rows, WIDTH), BF16), pltpu.VMEM((rows, WIDTH), F32), pltpu.VMEM((q_cols, rows), BF16),
         pltpu.VMEM((q_cols, rows), F32), pltpu.VMEM((kv_cols, rows), F32), pltpu.VMEM((kv_cols, rows), F32),
         pltpu.VMEM((rows, q_cols + 2 * kv_cols), BF16), pltpu.VMEM((4 * RANK, WIDTH), F32)], "attention_backward")

    inner = inner + near(inner)
    inner = inner + far(inner)
    square = sum(jnp.sum(jnp.square(x.astype(F32)), axis=1, keepdims=True) for x in xs)
    inv = lax.rsqrt(square / WIDTH + EPS)
    normed = reduce_scatter(h_keep, h_send) * attention_gain.astype(F32)[None, :]
    dinput = (dmiddle_q + inv * normed - dealt.astype(F32) * (inv * inv * inv * inner / WIDTH)).astype(BF16)
    back_grad = lax.all_to_all(
        dinput.reshape(dp, rows // dp, QUARTER), "dp", split_axis=0, concat_axis=0, tiled=True)
    input_grad = jnp.take(back_grad, dealing_slots, axis=0)

    att_pack = gather_slots(jnp.concatenate([att_b, reduce_scatter(aa_keep, aa_send).astype(BF16)], axis=0), dp)
    n_b = att_b.shape[0]
    sum_args = (att_pack[:, :n_b], *spread(att_pack[:, n_b:]))
    outs = [sds((adapters, 3 * RANK, WIDTH), F32), sds((adapters, RANK, WIDTH), F32),
            sds((adapters, RANK, q_cols), F32), sds((adapters, 2, RANK, kv_cols), F32),
            sds((adapters, RANK, q_cols), F32)]
    ga_att, g_out_b, g_query_b, g_kv_b, g_out_a = call(
        attention_sum_kernel, adapters, (info, owners), sum_args, [whole_spec(a.shape) for a in sum_args], outs,
        [pl.BlockSpec((1,) + o.shape[1:], (lambda n: lambda i, *_: (i,) + (0,) * n)(len(o.shape) - 1)) for o in outs],
        [], "attention_sum")
    return (output, input_grad, ga_att, g_query_b, g_kv_b, g_out_a, g_out_b, ga_ffn, g_ffn_b, g_down_a, g_down_b)


def solution(mesh):
    in_specs = (
        P(None, "dp", "mp"), P("mp"), P(None, "mp"), P(None, None, "mp"), P("mp", None), P("mp"),
        P(None, None, "mp"), P("mp", None), P(), P(None, None, "mp"), P(None, None, None, "mp"),
        P(None, None, "mp"), P(), P(), P(None, None, None, "mp"), P(None, None, "mp"), P(), P(), P(), P(),
        P("dp", None, "mp"),
    )
    out_specs = (
        P(None, "dp", "mp"), P(None, "dp", "mp"), P(), P(None, None, "mp"), P(None, None, None, "mp"),
        P(None, None, "mp"), P(), P(), P(None, None, None, "mp"), P(None, None, "mp"), P(),
    )
    return jax.shard_map(
        functools.partial(shards, mesh.shape["dp"]), mesh=mesh, in_specs=in_specs, out_specs=out_specs,
        check_vma=False)
```

```python
import functools

import jax
import jax.numpy as jnp
import numpy as np
from jax import lax
from jax.experimental import pallas as pl
from jax.experimental.pallas import tpu as pltpu
from jax.sharding import PartitionSpec as P

WIDTH = 2048
HEAD = 64
HALF = HEAD // 2
RANK = 16
EPS = 1e-05
ROPE_BASE = 500000.0
NEG_FILL = -1e30
PARTS = 4
QUARTER = WIDTH // PARTS
CHUNKS = 2
MIB = 1024 * 1024
F32 = jnp.float32
BF16 = jnp.bfloat16


def nn(a, b):
    return lax.dot_general(a, b, (((1,), (0,)), ((), ())), preferred_element_type=F32)


def nt(a, b):
    return lax.dot_general(a, b, (((1,), (1,)), ((), ())), preferred_element_type=F32)


def rope_tables(length):
    freq = ROPE_BASE ** (-np.arange(HALF, dtype=np.float32) * np.float32(2.0 / HEAD))
    angles = (np.arange(length, dtype=np.float32)[None, :] * freq.astype(np.float32)[:, None]).astype(np.float32)
    return np.cos(angles).astype(np.float32), np.sin(angles).astype(np.float32)


def quarter(me, rel):
    return pl.ds(pl.multiple_of((me ^ rel) * QUARTER, QUARTER), QUARTER)


LO, HI = slice(0, QUARTER), slice(QUARTER, 2 * QUARTER)


def total_block(rel, own, own_y, oth, oth_y):
    near, far = (own, own_y) if rel in (0, 2) else (oth, oth_y)
    first, second = (LO, HI) if rel in (0, 1) else (HI, LO)
    return near[:, first].astype(F32) + far[:, second].astype(F32)


def put_block(rel, value, keep_ref, send_ref):
    ref = keep_ref if rel in (0, 2) else send_ref
    ref[:, LO if rel in (0, 1) else HI] = value.astype(ref.dtype)


def rotate(value, cos, sin, out_ref):
    for i in range(value.shape[0] // HEAD):
        u1, u2 = value[i * HEAD:i * HEAD + HALF], value[i * HEAD + HALF:(i + 1) * HEAD]
        out_ref[i * HEAD:i * HEAD + HALF, :] = (u1 * cos - u2 * sin).astype(BF16)
        out_ref[i * HEAD + HALF:(i + 1) * HEAD, :] = (u2 * cos + u1 * sin).astype(BF16)


def turn_back(value, cos, sin, out_ref):
    for i in range(value.shape[0] // HEAD):
        w1, w2 = value[i * HEAD:i * HEAD + HALF], value[i * HEAD + HALF:(i + 1) * HEAD]
        out_ref[i * HEAD:i * HEAD + HALF, :] = (w1 * cos + w2 * sin).astype(BF16)
        out_ref[i * HEAD + HALF:(i + 1) * HEAD, :] = (w2 * cos - w1 * sin).astype(BF16)


def head_rows(i):
    return pl.ds(pl.multiple_of(i * HEAD, HEAD), HEAD)


def visible(key_start, query_start, rows, length):
    kpos = key_start + lax.broadcasted_iota(jnp.int32, (rows, rows), 0)
    qpos = query_start + lax.broadcasted_iota(jnp.int32, (rows, rows), 1)
    return (kpos <= qpos) & (kpos < length)


def project_kernel(info, x0, x1, x2, x3, gains, a1, qb, kvb, wq, wkv, cos_t, sin_t, *rest):
    h_out, t1t_out, qt_out, kn_out, vn_out, kt_out, vt_out = rest[-7:]
    me = info[0]
    rows = x0.shape[0]
    kv_heads = kn_out.shape[0]
    xs = (x0, x1, x2, x3)
    square = jnp.zeros((rows, 1), F32)
    for r in range(PARTS):
        v = xs[r][...].astype(F32)
        square = square + jnp.sum(v * v, axis=1, keepdims=True)
    inv = lax.rsqrt(square / WIDTH + EPS)
    for r in range(PARTS):
        v = xs[r][...].astype(F32)
        h_out[:, quarter(me, r)] = (v * inv * gains[r, 0:1, :].astype(F32)).astype(BF16)
    h = h_out[...]
    t1 = nt(h, a1[...])
    t1t_out[...] = t1.T.astype(BF16)
    t1b = t1.astype(BF16)
    cos, sin = cos_t[...], sin_t[...]
    k = nn(h, wkv[0]) + nn(t1b[:, RANK:2 * RANK], kvb[0])
    rotate(k.T, cos, sin, kt_out)
    k_n = kt_out[...].T
    v_n = (nn(h, wkv[1]) + nn(t1b[:, 2 * RANK:], kvb[1])).astype(BF16)
    vt_out[...] = v_n.T
    for i in range(kv_heads):
        kn_out[i] = k_n[:, i * HEAD:(i + 1) * HEAD]
        vn_out[i] = v_n[:, i * HEAD:(i + 1) * HEAD]
    q = nn(h, wq[...]) + nn(t1b[:, :RANK], qb[...])
    rotate(q.T * (HEAD ** -0.5), cos, sin, qt_out)


def attend_kernel(chunk, info, qt, oa, ob, wo, *rest):
    pairs, rest = rest[:2 * (chunk + 1)], rest[2 * (chunk + 1):]
    z_keep, z_send, ot_out, lse_out, tot_out = rest[-5:]
    keys, values = pairs[0::2], pairs[1::2]
    me, length = info[0], info[1]
    rows = qt.shape[1]
    kv_heads = keys[0].shape[0]
    heads = qt.shape[0] // HEAD
    group = heads // kv_heads

    def one_head(i, carry):
        j = i // group
        q_h = qt[head_rows(i), :]
        parts = []
        for c, key in enumerate(keys):
            s = nn(key[j], q_h)
            parts.append(jnp.where(visible(c * rows, chunk * rows, rows, length), s, NEG_FILL))
        top = functools.reduce(jnp.maximum, [jnp.max(s, axis=0, keepdims=True) for s in parts])
        es = [jnp.exp(s - top) for s in parts]
        total = sum(jnp.sum(e, axis=0, keepdims=True) for e in es)
        lse_out[pl.ds(i, 1), :] = top + jnp.log(total)
        o_t = sum(nn(value[head_rows(j), :], e.astype(BF16)) for value, e in zip(values, es))
        ot_out[head_rows(i), :] = (o_t / total).astype(BF16)
        return carry

    lax.fori_loop(0, heads, one_head, 0, unroll=2)
    o = ot_out[...].T
    to = nt(o, oa[...])
    tot_out[...] = to.T.astype(BF16)
    to = to.astype(BF16)
    for r in range(PARTS):
        at = quarter(me, r)
        put_block(r, nn(o, wo[:, at]) + nn(to, ob[:, at]), z_keep, z_send)


def feedforward_kernel(chunk, last, info, x0, x1, x2, x3, zo, zoy, zp, zpy, g0, g1, g2, g3, gains, a2, bd, fb, da,
                       wgu, wd, *rest):
    scratch, rest = rest[-8:], rest[:-8]
    f_s, h_s, g_s, act_s, dg_s, du_s, t2_s, dtd_s = scratch
    outs, rest = (rest[-9:], rest[:-9]) if last else (rest[-8:], rest[:-8])
    xm_out, xq_out, z_keep, z_send, d_keep, d_send, b_out = outs[:7]
    me, length = info[0], info[1]
    rows = x0.shape[0]
    units = wd.shape[0]
    xs, gs = (x0, x1, x2, x3), (g0, g1, g2, g3)
    valid = chunk * rows + lax.broadcasted_iota(jnp.int32, (rows, 1), 0) < length
    square = jnp.zeros((rows, 1), F32)
    for r in range(PARTS):
        v = xs[r][...].astype(F32) + total_block(r, zo, zoy, zp, zpy)
        if r == 0:
            xq_out[...] = v
        f_s[:, quarter(me, r)] = v
        square = square + jnp.sum(v * v, axis=1, keepdims=True)
        g_s[:, quarter(me, r)] = jnp.where(valid, gs[r][...], jnp.zeros((), BF16))
    inv = lax.rsqrt(square / WIDTH + EPS)
    for r in range(PARTS):
        v = f_s[:, quarter(me, r)]
        xm_out[:, quarter(me, r)] = v.astype(BF16)
        h_s[:, quarter(me, r)] = (v * inv * gains[r, 1:2, :].astype(F32)).astype(BF16)
    h, g = h_s[...], g_s[...]
    t2 = nt(h, a2[...])
    t2_s[...] = t2.astype(BF16)
    dtd = nt(g, bd[...])
    dtd_s[...] = dtd.astype(BF16)
    for i in range(units // QUARTER):
        c = slice(i * QUARTER, (i + 1) * QUARTER)
        gate = nn(h, wgu[0, :, c]) + nn(t2_s[:, :RANK], fb[0, :, c])
        up = nn(h, wgu[1, :, c]) + nn(t2_s[:, RANK:], fb[1, :, c])
        dact = nt(g, wd[c, :]) + nn(dtd_s[...], da[:, c])
        sig = 1.0 / (1.0 + jnp.exp(-gate))
        silu = gate * sig
        act_s[:, c] = (silu * up).astype(BF16)
        dg_s[:, c] = (dact * up * sig * (1.0 + gate * (1.0 - sig))).astype(BF16)
        du_s[:, c] = (dact * silu).astype(BF16)
    dgate, dup, act = dg_s[...], du_s[...], act_s[...]
    dt2 = jnp.concatenate([nt(dgate, fb[0]), nt(dup, fb[1])], axis=1)
    dt2b = dt2.astype(BF16)
    for r in range(PARTS):
        at = quarter(me, r)
        put_block(r, nt(dgate, wgu[0, at, :]) + nt(dup, wgu[1, at, :]) + nn(dt2b, a2[:, at]), d_keep, d_send)
    td = nt(act, da[...])
    tdb = td.astype(BF16)
    for r in range(PARTS):
        at = quarter(me, r)
        put_block(r, nn(act, wd[:, at]) + nn(tdb, bd[:, at]), z_keep, z_send)
    t2t, dtdt, dt2t, tdt = (t.T.astype(BF16) for t in (t2, dtd, dt2, td))
    for i in range(units // QUARTER):
        c = slice(i * QUARTER, (i + 1) * QUARTER)
        for k, value in enumerate((nn(t2t[:RANK], dgate[:, c]), nn(t2t[RANK:], dup[:, c]), nn(dtdt, act[:, c]))):
            at = slice((3 * i + k) * RANK, (3 * i + k + 1) * RANK)
            if last:
                value = value + rest[0][at, :]
            b_out[at, :] = value.astype(b_out.dtype)
    for r in range(PARTS):
        at = quarter(me, r)
        for rows_at, left, right in ((slice(0, 2 * RANK), dt2t, h_s), (slice(2 * RANK, 3 * RANK), tdt, g_s)):
            value = nn(left, right[:, at])
            if last:
                value = value + rest[1][rows_at, at]
                ref = outs[7] if r in (0, 2) else outs[8]
                ref[rows_at, LO if r in (0, 1) else HI] = value.astype(BF16)
            else:
                outs[7][rows_at, at] = value


def attend_back_kernel(chunk, last, info, x0, x1, x2, x3, g0, g1, g2, g3, xm, do_, doy, dp, dpy, gains, a1, qb, kvb, wq,
                       wkv, oa, ob, wo, cos_t, sin_t, h_in, t1t, qt, ot, lse, tot, *rest):
    scratch, rest = rest[-7:], rest[:-7]
    z_s, f_s, dot_s, dqt_s, dkt_s, dvt_s, dq_s = scratch
    n_out = 8 if last else 9
    outs, rest = rest[-n_out:], rest[:-n_out]
    dxq_out, h_keep, h_send, inner_out, inv_out, b_out = outs[:6]
    triples, rest = rest[:3 * (chunk + 1)], rest[3 * (chunk + 1):]
    keys, values, keys_t = triples[0::3], triples[1::3], triples[2::3]
    me, length = info[0], info[1]
    rows = x0.shape[0]
    kv_heads = keys[0].shape[0]
    heads = qt.shape[0] // HEAD
    group = heads // kv_heads
    q_cols, kv_cols = heads * HEAD, kv_heads * HEAD
    xs, gs = (x0, x1, x2, x3), (g0, g1, g2, g3)
    valid = chunk * rows + lax.broadcasted_iota(jnp.int32, (rows, 1), 0) < length
    square = jnp.zeros((rows, 1), F32)
    first = jnp.zeros((rows, 1), F32)
    inner = jnp.zeros((rows, 1), F32)
    for r in range(PARTS):
        v = xm[:, quarter(me, r)].astype(F32)
        square = square + jnp.sum(v * v, axis=1, keepdims=True)
        w = total_block(r, do_, doy, dp, dpy) * gains[r, 1:2, :].astype(F32)
        f_s[:, quarter(me, r)] = w
        inner = inner + jnp.sum(v * w, axis=1, keepdims=True)
        u = xs[r][...].astype(F32)
        first = first + jnp.sum(u * u, axis=1, keepdims=True)
    inv_out[...] = lax.rsqrt(first / WIDTH + EPS)
    inv = lax.rsqrt(square / WIDTH + EPS)
    back = inv * inv * inv * inner / WIDTH
    for r in range(PARTS):
        v = xm[:, quarter(me, r)].astype(F32)
        g = jnp.where(valid, gs[r][...].astype(F32), 0.0)
        d = g + inv * f_s[:, quarter(me, r)] - v * back
        if r == 0:
            dxq_out[...] = d
        z_s[:, quarter(me, r)] = d.astype(BF16)
    dz = z_s[...]
    dto = nt(dz, ob[...])
    d_o = nt(dz, wo[...]) + nn(dto.astype(BF16), oa[...])
    dot_s[...] = d_o.T.astype(BF16)
    if last:
        for c in range(chunk + 1):
            dkt_s[c], dvt_s[c] = rest[2][...], rest[3][...]
    else:
        dkt_s[...] = jnp.zeros_like(dkt_s)
        dvt_s[...] = jnp.zeros_like(dvt_s)

    def one_head(i, carry):
        j = i // group
        q_h, do_h = qt[head_rows(i), :], dot_s[head_rows(i), :]
        dots = jnp.sum(do_h.astype(F32) * ot[head_rows(i), :].astype(F32), axis=0, keepdims=True)
        low = lse[pl.ds(i, 1), :]
        dq_h = jnp.zeros((HEAD, rows), F32)
        for c in range(chunk + 1):
            prob = jnp.exp(nn(keys[c][j], q_h) - low)
            prob = jnp.where(visible(c * rows, chunk * rows, rows, length), prob, 0.0)
            ds = (prob * (nn(values[c][j], do_h) - dots)).astype(BF16)
            dq_h = dq_h + nn(keys_t[c][head_rows(j), :], ds)
            dkt_s[c, head_rows(j), :] += nt(q_h, ds)
            dvt_s[c, head_rows(j), :] += nt(do_h, prob.astype(BF16))
        dqt_s[head_rows(i), :] = dq_h
        return carry

    lax.fori_loop(0, heads, one_head, 0, unroll=2)
    if not last:
        outs[7][...], outs[8][...] = dkt_s[0], dvt_s[0]
    cos, sin = cos_t[...], sin_t[...]
    dto_t, o_t = dto.T.astype(BF16), ot[...]
    d_out_a = nt(dto_t, o_t)
    turn_back(dqt_s[...], cos * (HEAD ** -0.5), sin * (HEAD ** -0.5), dot_s)
    dq_s[:, :q_cols] = dot_s[...].T
    turn_back(dkt_s[chunk], cos, sin, dot_s)
    dq_s[:, q_cols:q_cols + kv_cols] = dot_s[:kv_cols, :].T
    dq_s[:, q_cols + kv_cols:] = dvt_s[chunk].T.astype(BF16)
    dq, dk, dv = dq_s[:, :q_cols], dq_s[:, q_cols:q_cols + kv_cols], dq_s[:, q_cols + kv_cols:]
    dt1 = jnp.concatenate([nt(dq, qb[...]), nt(dk, kvb[0]), nt(dv, kvb[1])], axis=1)
    dt1b = dt1.astype(BF16)
    inner = jnp.zeros((rows, 1), F32)
    for r in range(PARTS):
        at = quarter(me, r)
        d = nt(dq, wq[at, :]) + nt(dk, wkv[0, at, :]) + nt(dv, wkv[1, at, :]) + nn(dt1b, a1[:, at])
        put_block(r, d, h_keep, h_send)
        inner = inner + jnp.sum(d * gains[r, 0:1, :].astype(F32) * xs[r][...].astype(F32), axis=1, keepdims=True)
    inner_out[...] = inner
    kv_pad = jnp.zeros((RANK, QUARTER - 2 * kv_cols), F32)
    d_kv = jnp.concatenate([nn(t1t[RANK:2 * RANK, :], dk), nn(t1t[2 * RANK:, :], dv), kv_pad], axis=1)
    for k, value in enumerate((nn(t1t[:RANK, :], dq), d_out_a, d_kv)):
        at = slice(k * RANK, (k + 1) * RANK)
        if last:
            value = value + rest[0][at, :]
        b_out[at, :] = value.astype(b_out.dtype)
    dt1t = dt1.T.astype(BF16)
    for r in range(PARTS):
        at = quarter(me, r)
        for rows_at, left, right in ((slice(0, 3 * RANK), dt1t, h_in), (slice(3 * RANK, 4 * RANK), tot[...], z_s)):
            value = nn(left, right[:, at])
            if last:
                value = value + rest[1][rows_at, at]
                ref = outs[6] if r in (0, 2) else outs[7]
                ref[rows_at, LO if r in (0, 1) else HI] = value.astype(BF16)
            else:
                outs[6][rows_at, at] = value


def finish_kernel(*refs):
    out = refs[-1]
    gain = refs[0][0, 0:1, :].astype(F32)
    for c in range(CHUNKS):
        x, dx, low, got, inv, inner, inner_y = refs[1 + 7 * c:8 + 7 * c]
        rows = x.shape[0]
        inv = inv[...]
        scale = inv * inv * inv * (inner[...] + inner_y[...]) / WIDTH
        grad = inv * (gain * (low[...] + got[...].astype(F32))) - x[...].astype(F32) * scale
        out[c * rows:(c + 1) * rows, :] = (dx[...] + grad).astype(BF16)


def feedforward_sum_kernel(info, owners, b0, a0, a1, a2, a3, *outs):
    ga, gdb, gb, gda = outs[-4:]
    adapter = pl.program_id(0)
    me, place = info[0], info[3]
    slots = b0.shape[0]
    blocks = gda.shape[2] // QUARTER
    for ref in (ga, gdb, gb, gda):
        ref[...] = jnp.zeros_like(ref)

    def add(slot, carry):
        @pl.when(owners[slot] == adapter)
        def _():
            at = slot ^ place
            for i in range(blocks):
                cols = slice(i * QUARTER, (i + 1) * QUARTER)
                base = i * 3 * RANK
                gb[0, 0, :, cols] += b0[at, base:base + RANK, :].astype(F32)
                gb[0, 1, :, cols] += b0[at, base + RANK:base + 2 * RANK, :].astype(F32)
                gda[0, :, cols] += b0[at, base + 2 * RANK:base + 3 * RANK, :].astype(F32)
            for r, ref in enumerate((a0, a1, a2, a3)):
                ga[0, :, quarter(me, r)] += ref[at, :2 * RANK, :].astype(F32)
                gdb[0, :, quarter(me, r)] += ref[at, 2 * RANK:, :].astype(F32)
        return carry

    lax.fori_loop(0, slots, add, 0)


def attention_sum_kernel(info, owners, b0, a0, a1, a2, a3, ga, gob, gq, gkv, goa):
    adapter = pl.program_id(0)
    me, place = info[0], info[3]
    slots = b0.shape[0]
    kv_cols = gkv.shape[3]
    for ref in (ga, gob, gq, gkv, goa):
        ref[...] = jnp.zeros_like(ref)

    def add(slot, carry):
        @pl.when(owners[slot] == adapter)
        def _():
            at = slot ^ place
            gq[0] += b0[at, :RANK, :].astype(F32)
            goa[0] += b0[at, RANK:2 * RANK, :].astype(F32)
            gkv[0, 0] += b0[at, 2 * RANK:, :kv_cols].astype(F32)
            gkv[0, 1] += b0[at, 2 * RANK:, kv_cols:2 * kv_cols].astype(F32)
            for r, ref in enumerate((a0, a1, a2, a3)):
                ga[0, :, quarter(me, r)] += ref[at, :3 * RANK, :].astype(F32)
                gob[0, :, quarter(me, r)] += ref[at, 3 * RANK:, :].astype(F32)
        return carry

    lax.fori_loop(0, slots, add, 0)


def sds(shape, dtype):
    return jax.ShapeDtypeStruct(tuple(shape), dtype)


def in_vmem(value):
    return pltpu.with_memory_space_constraint(value, pltpu.VMEM)


def call(kernel, info, args, outs, scratch, name, flops, mib, after=(), hbm_out=()):
    vmem = pl.BlockSpec(memory_space=pltpu.VMEM)
    scalars = () if info is None else (info,)
    return pl.pallas_call(
        kernel,
        in_specs=[pl.BlockSpec(memory_space=pltpu.SMEM)] * len(scalars) + [vmem] * len(args)
        + [pl.BlockSpec(memory_space=pl.ANY)] * len(after),
        out_specs=[vmem] * len(outs),
        out_shape=[pltpu.VMEM(tuple(s), d) for s, d in outs],
        scratch_shapes=[pltpu.VMEM(s, d) for s, d in scratch],
        compiler_params=pltpu.CompilerParams(vmem_limit_bytes=mib * MIB),
        cost_estimate=pl.CostEstimate(flops=flops, transcendentals=0, bytes_accessed=0),
        name=name,
    )(*scalars, *(in_vmem(a) for a in args), *after)


def sum_call(kernel, scalars, args, outs, name):
    specs = [pl.BlockSpec((1,) + o.shape[1:], (lambda n: lambda i, *_: (i,) + (0,) * n)(len(o.shape) - 1)) for o in outs]
    return pl.pallas_call(
        kernel,
        grid_spec=pltpu.PrefetchScalarGridSpec(
            num_scalar_prefetch=len(scalars), grid=(outs[0].shape[0],),
            in_specs=[pl.BlockSpec(memory_space=pltpu.VMEM)] * len(args), out_specs=specs),
        out_shape=outs,
        compiler_params=pltpu.CompilerParams(dimension_semantics=("arbitrary",), vmem_limit_bytes=12 * MIB),
        cost_estimate=pl.CostEstimate(flops=0, transcendentals=0, bytes_accessed=12000000),
        name=name,
    )(*scalars, *(in_vmem(a) for a in args))


def swap(value, bit, axis, size):
    return lax.ppermute(value, axis, [(i, i ^ bit) for i in range(size)])


def near(value):
    return swap(value, 1, "mp", PARTS)


def far(value):
    return swap(value, 2, "mp", PARTS)


def spread(value):
    there = far(value)
    return (value, near(value), there, near(there))


def chip_sum(keep, send):
    got = near(send)
    lo = keep[:, :QUARTER].astype(F32) + got[:, :QUARTER].astype(F32)
    hi = keep[:, QUARTER:].astype(F32) + got[:, QUARTER:].astype(F32)
    return lo, hi.astype(BF16)


def reduce_scatter(keep, send):
    lo, hi = chip_sum(keep, send)
    return lo + far(hi).astype(F32)


def reduce_all(keep, send):
    own = (keep.astype(F32) + near(send).astype(F32)).astype(BF16)
    own_y = far(own)
    return own, own_y, near(own), near(own_y)


def gather_slots(value, size):
    stack = value[None]
    bits = [1 << b for b in range(size.bit_length() - 1)]
    for bit in bits:
        stack = jnp.concatenate([stack, swap(stack, bit, "dp", size)], axis=0)
    return stack


def shards(dp, residual, attention_gain, query_matrix, key_value_matrix, output_matrix, feedfwd_gain,
           gate_up_matrix, down_matrix, attention_adapter_input, query_adapter_output,
           key_value_adapter_output, output_adapter_input, output_adapter_output, feedfwd_adapter_input,
           feedfwd_adapter_output, down_adapter_input, down_adapter_output, lengths, adapter_index,
           dealing_slots, cotangent):
    seqs = residual.shape[0]
    length = cotangent.shape[1]
    units = down_matrix.shape[0]
    adapters = attention_adapter_input.shape[0]
    q_cols = query_matrix.shape[1]
    kv_cols = key_value_matrix.shape[2]
    kv_heads = kv_cols // HEAD
    heads = q_cols // HEAD
    rows = length // CHUNKS
    half = 2 * QUARTER
    me = lax.axis_index("mp")
    place = lax.axis_index("dp")

    is_there = dealing_slots[None, :] == jnp.arange(seqs, dtype=jnp.int32)[:, None]
    seq_of_slot = jnp.sum(jnp.where(is_there, jnp.arange(seqs, dtype=jnp.int32)[None, :], 0), axis=1)
    owners = jnp.sum(jnp.where(is_there, adapter_index[None, :], 0), axis=1)
    spans = jnp.sum(jnp.where(is_there, lengths[None, :], 0), axis=1)
    mine = jnp.arange(seqs, dtype=jnp.int32) == place
    my_length = jnp.sum(jnp.where(mine, spans, 0))
    my_adapter = jnp.sum(jnp.where(mine, owners, 0))
    info = jnp.stack([me.astype(jnp.int32), my_length, my_adapter, place.astype(jnp.int32)])

    def cut(value):
        return [value[c * rows:(c + 1) * rows] for c in range(CHUNKS)]

    gs = list(zip(*[cut(v) for v in spread(cotangent[0])]))
    gains = jnp.stack(spread(jnp.stack([attention_gain, feedfwd_gain])))
    dealt = lax.all_to_all(
        jnp.take(residual, seq_of_slot, axis=0), "dp", split_axis=0, concat_axis=1, tiled=True
    )[0]
    xs = [spread(v) for v in cut(dealt)]
    cos_np, sin_np = rope_tables(length)
    cos = [jnp.asarray(cos_np[:, c * rows:(c + 1) * rows]) for c in range(CHUNKS)]
    sin = [jnp.asarray(sin_np[:, c * rows:(c + 1) * rows]) for c in range(CHUNKS)]
    a1, qb, kvb, oa, ob, a2, fb, da, bd = (
        lax.dynamic_index_in_dim(v, my_adapter, 0, keepdims=False) for v in (
            attention_adapter_input, query_adapter_output, key_value_adapter_output, output_adapter_input,
            output_adapter_output, feedfwd_adapter_input, feedfwd_adapter_output, down_adapter_input,
            down_adapter_output))
    wq, wkv, wo, wgu, wd = (
        in_vmem(v) for v in (query_matrix, key_value_matrix, output_matrix, gate_up_matrix, down_matrix))

    wide, col, block, thin = (rows, WIDTH), (rows, half), (rows, QUARTER), (rows, 1)
    proj_flops = 2 * rows * WIDTH * (q_cols + 2 * kv_cols)
    out_flops = 2 * rows * WIDTH * q_cols
    ffn_flops = 12 * rows * WIDTH * units
    saved = [None] * CHUNKS
    order = ()
    for c in range(CHUNKS):
        outs = [(wide, BF16), ((3 * RANK, rows), BF16), ((q_cols, rows), BF16), ((kv_heads, rows, HEAD), BF16),
                ((kv_heads, rows, HEAD), BF16), ((kv_cols, rows), BF16), ((kv_cols, rows), BF16)]
        saved[c] = call(project_kernel, info, (*xs[c], gains, a1, qb, kvb, wq, wkv, cos[c], sin[c]), outs, [],
                        "project_%d" % c, proj_flops * 2, 8, order)
        order = (saved[c][1],)

    branch, kept = [None] * CHUNKS, [None] * CHUNKS
    for c in reversed(range(CHUNKS)):
        outs = [(col, F32), (col, BF16), ((q_cols, rows), BF16), ((heads, rows), F32), ((RANK, rows), BF16)]
        pairs = [v for p in saved[:c + 1] for v in (p[3], p[6])]
        z_keep, z_send, *kept[c] = call(
            functools.partial(attend_kernel, c), info, (saved[c][2], oa, ob, wo, *pairs), outs, [], "attend_%d" % c,
            out_flops * 4, 8, order)
        order = (kept[c][1],)
        branch[c] = reduce_all(z_keep, z_send)

    back, middle, middle_q, z_parts = ([None] * CHUNKS for _ in range(4))
    sums = ()
    for c in reversed(range(CHUNKS)):
        last = c == 0
        outs = [(wide, BF16), (block, F32), (col, F32), (col, BF16), (col, F32), (col, BF16),
                ((3 * RANK * units // QUARTER, QUARTER), BF16 if last else F32)]
        outs += [((3 * RANK, half), BF16)] * 2 if last else [((3 * RANK, WIDTH), F32)]
        scratch = [(wide, F32), (wide, BF16), (wide, BF16), ((rows, units), BF16), ((rows, units), BF16),
                   ((rows, units), BF16), ((rows, 2 * RANK), BF16), ((rows, RANK), BF16)]
        middle[c], middle_q[c], z_keep, z_send, d_keep, d_send, *sums = call(
            functools.partial(feedforward_kernel, c, last), info,
            (*xs[c], *branch[c], *gs[c], gains, a2, bd, fb, da, wgu, wd, *sums), outs, scratch, "feedforward_%d" % c,
            ffn_flops, 16, order)
        order = (middle_q[c],)
        z_parts[c] = (z_keep, z_send)
        back[c] = reduce_all(d_keep, d_send)
    ffn_b, fa_keep, fa_send = sums

    sums, carried = (), ()
    final = [None] * CHUNKS
    for c in reversed(range(CHUNKS)):
        last = c == 0
        outs = [(block, F32), (col, F32), (col, BF16), (thin, F32), (thin, F32),
                ((3 * RANK, QUARTER), BF16 if last else F32)]
        outs += ([((4 * RANK, half), BF16)] * 2 if last
                 else [((4 * RANK, WIDTH), F32), ((kv_cols, rows), F32), ((kv_cols, rows), F32)])
        scratch = [(wide, BF16), (wide, F32), ((q_cols, rows), BF16), ((q_cols, rows), F32),
                   ((c + 1, kv_cols, rows), F32), ((c + 1, kv_cols, rows), F32), ((rows, q_cols + 2 * kv_cols), BF16)]
        triples = [v for p in saved[:c + 1] for v in (p[3], p[4], p[5])]
        h1, t1t, qt = saved[c][:3]
        ot, lse, tot = kept[c]
        dxq, h_keep, h_send, inner, inv, *sums = call(
            functools.partial(attend_back_kernel, c, last), info,
            (*xs[c], *gs[c], middle[c], *back[c], gains, a1, qb, kvb, wq, wkv, oa, ob, wo, cos[c], sin[c], h1, t1t, qt,
             ot, lse, tot, *triples, *sums), outs, scratch, "attend_back_%d" % c,
            2 * (proj_flops + out_flops) + out_flops * 4, 12, order)
        order = (inv,)
        lo, hi = chip_sum(h_keep, h_send)
        inner = inner + near(inner)
        final[c] = (xs[c][0], dxq, lo, far(hi), inv, inner, far(inner))
    att_b, aa_keep, aa_send = sums

    valid = (jnp.arange(length, dtype=jnp.int32) < my_length)[:, None]
    result = jnp.concatenate([middle_q[c] + reduce_scatter(*z_parts[c]) for c in range(CHUNKS)], axis=0)
    result = jnp.where(valid, result, 0.0).astype(BF16)
    back_out = lax.all_to_all(
        result.reshape(dp, length // dp, QUARTER), "dp", split_axis=0, concat_axis=0, tiled=True)
    output = jnp.take(back_out, dealing_slots, axis=0)

    dinput, = call(finish_kernel, None, (gains, *(v for f in final for v in f)), [((length, QUARTER), BF16)], [],
                   "finish", 4 * length * QUARTER, 8)
    back_grad = lax.all_to_all(
        dinput.reshape(dp, length // dp, QUARTER), "dp", split_axis=0, concat_axis=0, tiled=True)
    input_grad = jnp.take(back_grad, dealing_slots, axis=0)

    n_b = ffn_b.shape[0]
    pack = gather_slots(jnp.concatenate([ffn_b, reduce_scatter(fa_keep, fa_send).astype(BF16)], axis=0), dp)
    outs = [sds((adapters, 2 * RANK, WIDTH), F32), sds((adapters, RANK, WIDTH), F32),
            sds((adapters, 2, RANK, units), F32), sds((adapters, RANK, units), F32)]
    ga_ffn, g_down_b, g_ffn_b, g_down_a = sum_call(
        feedforward_sum_kernel, (info, owners), (pack[:, :n_b], *spread(pack[:, n_b:])), outs, "feedforward_sum")

    n_b = att_b.shape[0]
    pack = gather_slots(jnp.concatenate([att_b, reduce_scatter(aa_keep, aa_send).astype(BF16)], axis=0), dp)
    outs = [sds((adapters, 3 * RANK, WIDTH), F32), sds((adapters, RANK, WIDTH), F32),
            sds((adapters, RANK, q_cols), F32), sds((adapters, 2, RANK, kv_cols), F32),
            sds((adapters, RANK, q_cols), F32)]
    ga_att, g_out_b, g_query_b, g_kv_b, g_out_a = sum_call(
        attention_sum_kernel, (info, owners), (pack[:, :n_b], *spread(pack[:, n_b:])), outs, "attention_sum")
    return (output, input_grad, ga_att, g_query_b, g_kv_b, g_out_a, g_out_b, ga_ffn, g_ffn_b, g_down_a, g_down_b)


def solution(mesh):
    in_specs = (
        P(None, "dp", "mp"), P("mp"), P(None, "mp"), P(None, None, "mp"), P("mp", None), P("mp"),
        P(None, None, "mp"), P("mp", None), P(), P(None, None, "mp"), P(None, None, None, "mp"),
        P(None, None, "mp"), P(), P(), P(None, None, None, "mp"), P(None, None, "mp"), P(), P(), P(), P(),
        P("dp", None, "mp"),
    )
    out_specs = (
        P(None, "dp", "mp"), P(None, "dp", "mp"), P(), P(None, None, "mp"), P(None, None, None, "mp"),
        P(None, None, "mp"), P(), P(), P(None, None, None, "mp"), P(None, None, "mp"), P(),
    )
    return jax.shard_map(
        functools.partial(shards, mesh.shape["dp"]), mesh=mesh, in_specs=in_specs, out_specs=out_specs,
        check_vma=False)
```

```python
import functools

import jax
import jax.numpy as jnp
import numpy as np
from jax import lax
from jax.experimental import pallas as pl
from jax.experimental.pallas import tpu as pltpu
from jax.sharding import PartitionSpec as P

WIDTH = 2048
HEAD = 64
HALF = HEAD // 2
RANK = 16
EPS = 1e-05
ROPE_BASE = 500000.0
NEG_FILL = -1e30
PARTS = 4
QUARTER = WIDTH // PARTS
CHUNKS = 2
MIB = 1024 * 1024
F32 = jnp.float32
BF16 = jnp.bfloat16


def nn(a, b):
    return lax.dot_general(a, b, (((1,), (0,)), ((), ())), preferred_element_type=F32)


def nt(a, b):
    return lax.dot_general(a, b, (((1,), (1,)), ((), ())), preferred_element_type=F32)


def rope_tables(length):
    freq = ROPE_BASE ** (-np.arange(HALF, dtype=np.float32) * np.float32(2.0 / HEAD))
    angles = (np.arange(length, dtype=np.float32)[None, :] * freq.astype(np.float32)[:, None]).astype(np.float32)
    return np.cos(angles).astype(np.float32), np.sin(angles).astype(np.float32)


def quarter(me, rel):
    return pl.ds(pl.multiple_of((me ^ rel) * QUARTER, QUARTER), QUARTER)


LO, HI = slice(0, QUARTER), slice(QUARTER, 2 * QUARTER)


def total_block(rel, own, own_y, oth, oth_y):
    near, far = (own, own_y) if rel in (0, 2) else (oth, oth_y)
    first, second = (LO, HI) if rel in (0, 1) else (HI, LO)
    return near[:, first].astype(F32) + far[:, second].astype(F32)


def put_block(rel, value, keep_ref, send_ref):
    ref = keep_ref if rel in (0, 2) else send_ref
    ref[:, LO if rel in (0, 1) else HI] = value.astype(ref.dtype)


def rotate(value, cos, sin, out_ref):
    for i in range(value.shape[0] // HEAD):
        u1, u2 = value[i * HEAD:i * HEAD + HALF], value[i * HEAD + HALF:(i + 1) * HEAD]
        out_ref[i * HEAD:i * HEAD + HALF, :] = (u1 * cos - u2 * sin).astype(BF16)
        out_ref[i * HEAD + HALF:(i + 1) * HEAD, :] = (u2 * cos + u1 * sin).astype(BF16)


def turn_back(value, cos, sin, out_ref):
    for i in range(value.shape[0] // HEAD):
        w1, w2 = value[i * HEAD:i * HEAD + HALF], value[i * HEAD + HALF:(i + 1) * HEAD]
        out_ref[i * HEAD:i * HEAD + HALF, :] = (w1 * cos + w2 * sin).astype(BF16)
        out_ref[i * HEAD + HALF:(i + 1) * HEAD, :] = (w2 * cos - w1 * sin).astype(BF16)


def head_rows(i):
    return pl.ds(pl.multiple_of(i * HEAD, HEAD), HEAD)


def visible(key_start, query_start, rows, length):
    kpos = key_start + lax.broadcasted_iota(jnp.int32, (rows, rows), 0)
    qpos = query_start + lax.broadcasted_iota(jnp.int32, (rows, rows), 1)
    return (kpos <= qpos) & (kpos < length)


def project_kernel(info, wq, wkv, x0, x1, x2, x3, gains, a1, qb, kvb, cos_t, sin_t,
                   h_out, t1t_out, qt_out, kn_out, vn_out, kt_out, vt_out):
    me = info[0]
    rows = x0.shape[0]
    kv_heads = kn_out.shape[0]
    xs = (x0, x1, x2, x3)
    square = jnp.zeros((rows, 1), F32)
    for r in range(PARTS):
        v = xs[r][...].astype(F32)
        square = square + jnp.sum(v * v, axis=1, keepdims=True)
    inv = lax.rsqrt(square / WIDTH + EPS)
    for r in range(PARTS):
        v = xs[r][...].astype(F32)
        h_out[:, quarter(me, r)] = (v * inv * gains[r, 0:1, :].astype(F32)).astype(BF16)
    h = h_out[...]
    t1 = nt(h, a1[...])
    t1t_out[...] = t1.T.astype(BF16)
    t1b = t1.astype(BF16)
    cos, sin = cos_t[...], sin_t[...]
    k = nn(h, wkv[0]) + nn(t1b[:, RANK:2 * RANK], kvb[0])
    rotate(k.T, cos, sin, kt_out)
    k_n = kt_out[...].T
    v_n = (nn(h, wkv[1]) + nn(t1b[:, 2 * RANK:], kvb[1])).astype(BF16)
    vt_out[...] = v_n.T
    for i in range(kv_heads):
        kn_out[i] = k_n[:, i * HEAD:(i + 1) * HEAD]
        vn_out[i] = v_n[:, i * HEAD:(i + 1) * HEAD]
    q = nn(h, wq[...]) + nn(t1b[:, :RANK], qb[...])
    rotate(q.T * (HEAD ** -0.5), cos, sin, qt_out)


def attend_kernel(chunk, info, wo, qt, oa, ob, *rest):
    pairs, rest = rest[:2 * (chunk + 1)], rest[2 * (chunk + 1):]
    z_keep, z_send, ot_out, lse_out, tot_out = rest[-5:]
    keys, values = pairs[0::2], pairs[1::2]
    me, length = info[0], info[1]
    rows = qt.shape[1]
    kv_heads = keys[0].shape[0]
    heads = qt.shape[0] // HEAD
    group = heads // kv_heads

    def one_head(i, carry):
        j = i // group
        q_h = qt[head_rows(i), :]
        parts = []
        for c, key in enumerate(keys):
            s = nn(key[j], q_h)
            parts.append(jnp.where(visible(c * rows, chunk * rows, rows, length), s, NEG_FILL))
        top = functools.reduce(jnp.maximum, [jnp.max(s, axis=0, keepdims=True) for s in parts])
        es = [jnp.exp(s - top) for s in parts]
        total = sum(jnp.sum(e, axis=0, keepdims=True) for e in es)
        lse_out[pl.ds(i, 1), :] = top + jnp.log(total)
        o_t = sum(nn(value[head_rows(j), :], e.astype(BF16)) for value, e in zip(values, es))
        ot_out[head_rows(i), :] = (o_t / total).astype(BF16)
        return carry

    lax.fori_loop(0, heads, one_head, 0, unroll=2)
    o = ot_out[...].T
    to = nt(o, oa[...])
    tot_out[...] = to.T.astype(BF16)
    to = to.astype(BF16)
    for r in range(PARTS):
        at = quarter(me, r)
        put_block(r, nn(o, wo[:, at]) + nn(to, ob[:, at]), z_keep, z_send)


def front_kernel(chunk, last, info, wgu, wd, x0, x1, x2, x3, zo, zoy, zp, zpy, g0, g1, g2, g3, gains, a2, bd, fb, da,
                 *rest):
    f_s = rest[-1]
    xm_out, xq_out, h_out, g_out, act_out, dg_out, du_out, t2_s, dtd_s, b_out = rest[-11:-1]
    me, length = info[0], info[1]
    rows = x0.shape[0]
    units = wd.shape[0]
    xs, gs = (x0, x1, x2, x3), (g0, g1, g2, g3)
    valid = chunk * rows + lax.broadcasted_iota(jnp.int32, (rows, 1), 0) < length
    square = jnp.zeros((rows, 1), F32)
    for r in range(PARTS):
        v = xs[r][...].astype(F32) + total_block(r, zo, zoy, zp, zpy)
        if r == 0:
            xq_out[...] = v
        f_s[:, quarter(me, r)] = v
        square = square + jnp.sum(v * v, axis=1, keepdims=True)
        g_out[:, quarter(me, r)] = jnp.where(valid, gs[r][...], jnp.zeros((), BF16))
    inv = lax.rsqrt(square / WIDTH + EPS)
    for r in range(PARTS):
        v = f_s[:, quarter(me, r)]
        xm_out[:, quarter(me, r)] = v.astype(BF16)
        h_out[:, quarter(me, r)] = (v * inv * gains[r, 1:2, :].astype(F32)).astype(BF16)
    t2 = nt(h_out[...], a2[...])
    t2_s[...] = t2.astype(BF16)
    dtd = nt(g_out[...], bd[...])
    dtd_s[...] = dtd.astype(BF16)
    t2t, dtdt = t2.T.astype(BF16), dtd.T.astype(BF16)

    def block(i, carry):
        c = pl.ds(pl.multiple_of(i * QUARTER, QUARTER), QUARTER)
        h, g = h_out[...], g_out[...]
        gate = nn(h, wgu[0, :, c]) + nn(t2_s[:, :RANK], fb[0, :, c])
        up = nn(h, wgu[1, :, c]) + nn(t2_s[:, RANK:], fb[1, :, c])
        dact = nt(g, wd[c, :]) + nn(dtd_s[...], da[:, c])
        sig = 1.0 / (1.0 + jnp.exp(-gate))
        silu = gate * sig
        act = (silu * up).astype(BF16)
        dgate = (dact * up * sig * (1.0 + gate * (1.0 - sig))).astype(BF16)
        dup = (dact * silu).astype(BF16)
        act_out[:, c], dg_out[:, c], du_out[:, c] = act, dgate, dup
        for k, value in enumerate((nn(t2t[:RANK], dgate), nn(t2t[RANK:], dup), nn(dtdt, act))):
            at = pl.ds(pl.multiple_of((3 * i + k) * RANK, RANK), RANK)
            if last:
                value = value + rest[0][at, :]
            b_out[at, :] = value.astype(b_out.dtype)
        return carry

    lax.fori_loop(0, units // QUARTER, block, 0)


def back_kernel(last, info, wgu, wd, h, g, act, dg, du, a2, bd, fb, da, *rest):
    outs, rest = (rest[-6:], rest[:-6]) if last else (rest[-5:], rest[:-5])
    d_keep, d_send, z_keep, z_send = outs[:4]
    me = info[0]
    dt2 = jnp.concatenate([nt(dg[...], fb[0]), nt(du[...], fb[1])], axis=1)
    dt2b = dt2.astype(BF16)
    td = nt(act[...], da[...])
    tdb = td.astype(BF16)
    dt2t, tdt = dt2.T.astype(BF16), td.T.astype(BF16)

    def pair(i, carry):
        to = pl.ds(pl.multiple_of(i * QUARTER, QUARTER), QUARTER)
        for r, d_ref, z_ref in ((2 * i, d_keep, z_keep), (2 * i + 1, d_send, z_send)):
            at = quarter(me, r)
            d = nt(dg[...], wgu[0, at, :]) + nt(du[...], wgu[1, at, :]) + nn(dt2b, a2[:, at])
            d_ref[:, to] = d.astype(d_ref.dtype)
            z_ref[:, to] = (nn(act[...], wd[:, at]) + nn(tdb, bd[:, at])).astype(z_ref.dtype)
        return carry

    lax.fori_loop(0, PARTS // 2, pair, 0)
    for r in range(PARTS):
        at = quarter(me, r)
        for rows_at, left, right in ((slice(0, 2 * RANK), dt2t, h), (slice(2 * RANK, 3 * RANK), tdt, g)):
            value = nn(left, right[:, at])
            if last:
                value = value + rest[0][rows_at, at]
                ref = outs[4] if r in (0, 2) else outs[5]
                ref[rows_at, LO if r in (0, 1) else HI] = value.astype(BF16)
            else:
                outs[4][rows_at, at] = value


def attend_back_kernel(chunk, last, info, wq, wkv, wo, x0, x1, x2, x3, g0, g1, g2, g3, xm, do_, doy, dp, dpy, gains, a1,
                       qb, kvb, oa, ob, cos_t, sin_t, h_in, t1t, qt, ot, lse, tot, *rest):
    scratch, rest = rest[-7:], rest[:-7]
    z_s, f_s, dot_s, dqt_s, dkt_s, dvt_s, dq_s = scratch
    n_out = 8 if last else 9
    outs, rest = rest[-n_out:], rest[:-n_out]
    dxq_out, h_keep, h_send, inner_out, inv_out, b_out = outs[:6]
    triples, rest = rest[:3 * (chunk + 1)], rest[3 * (chunk + 1):]
    keys, values, keys_t = triples[0::3], triples[1::3], triples[2::3]
    me, length = info[0], info[1]
    rows = x0.shape[0]
    kv_heads = keys[0].shape[0]
    heads = qt.shape[0] // HEAD
    group = heads // kv_heads
    q_cols, kv_cols = heads * HEAD, kv_heads * HEAD
    xs, gs = (x0, x1, x2, x3), (g0, g1, g2, g3)
    valid = chunk * rows + lax.broadcasted_iota(jnp.int32, (rows, 1), 0) < length
    square = jnp.zeros((rows, 1), F32)
    first = jnp.zeros((rows, 1), F32)
    inner = jnp.zeros((rows, 1), F32)
    for r in range(PARTS):
        v = xm[:, quarter(me, r)].astype(F32)
        square = square + jnp.sum(v * v, axis=1, keepdims=True)
        w = total_block(r, do_, doy, dp, dpy) * gains[r, 1:2, :].astype(F32)
        f_s[:, quarter(me, r)] = w
        inner = inner + jnp.sum(v * w, axis=1, keepdims=True)
        u = xs[r][...].astype(F32)
        first = first + jnp.sum(u * u, axis=1, keepdims=True)
    inv_out[...] = lax.rsqrt(first / WIDTH + EPS)
    inv = lax.rsqrt(square / WIDTH + EPS)
    back = inv * inv * inv * inner / WIDTH
    for r in range(PARTS):
        v = xm[:, quarter(me, r)].astype(F32)
        g = jnp.where(valid, gs[r][...].astype(F32), 0.0)
        d = g + inv * f_s[:, quarter(me, r)] - v * back
        if r == 0:
            dxq_out[...] = d
        z_s[:, quarter(me, r)] = d.astype(BF16)
    dz = z_s[...]
    dto = nt(dz, ob[...])
    d_o = nt(dz, wo[...]) + nn(dto.astype(BF16), oa[...])
    dot_s[...] = d_o.T.astype(BF16)
    if last:
        for c in range(chunk + 1):
            dkt_s[c], dvt_s[c] = rest[2][...], rest[3][...]
    else:
        dkt_s[...] = jnp.zeros_like(dkt_s)
        dvt_s[...] = jnp.zeros_like(dvt_s)

    def one_head(i, carry):
        j = i // group
        q_h, do_h = qt[head_rows(i), :], dot_s[head_rows(i), :]
        dots = jnp.sum(do_h.astype(F32) * ot[head_rows(i), :].astype(F32), axis=0, keepdims=True)
        low = lse[pl.ds(i, 1), :]
        dq_h = jnp.zeros((HEAD, rows), F32)
        for c in range(chunk + 1):
            prob = jnp.exp(nn(keys[c][j], q_h) - low)
            prob = jnp.where(visible(c * rows, chunk * rows, rows, length), prob, 0.0)
            ds = (prob * (nn(values[c][j], do_h) - dots)).astype(BF16)
            dq_h = dq_h + nn(keys_t[c][head_rows(j), :], ds)
            dkt_s[c, head_rows(j), :] += nt(q_h, ds)
            dvt_s[c, head_rows(j), :] += nt(do_h, prob.astype(BF16))
        dqt_s[head_rows(i), :] = dq_h
        return carry

    lax.fori_loop(0, heads, one_head, 0, unroll=2)
    if not last:
        outs[7][...], outs[8][...] = dkt_s[0], dvt_s[0]
    cos, sin = cos_t[...], sin_t[...]
    dto_t, o_t = dto.T.astype(BF16), ot[...]
    d_out_a = nt(dto_t, o_t)
    turn_back(dqt_s[...], cos * (HEAD ** -0.5), sin * (HEAD ** -0.5), dot_s)
    dq_s[:, :q_cols] = dot_s[...].T
    turn_back(dkt_s[chunk], cos, sin, dot_s)
    dq_s[:, q_cols:q_cols + kv_cols] = dot_s[:kv_cols, :].T
    dq_s[:, q_cols + kv_cols:] = dvt_s[chunk].T.astype(BF16)
    dq, dk, dv = dq_s[:, :q_cols], dq_s[:, q_cols:q_cols + kv_cols], dq_s[:, q_cols + kv_cols:]
    dt1 = jnp.concatenate([nt(dq, qb[...]), nt(dk, kvb[0]), nt(dv, kvb[1])], axis=1)
    dt1b = dt1.astype(BF16)
    inner = jnp.zeros((rows, 1), F32)
    for r in range(PARTS):
        at = quarter(me, r)
        d = nt(dq, wq[at, :]) + nt(dk, wkv[0, at, :]) + nt(dv, wkv[1, at, :]) + nn(dt1b, a1[:, at])
        put_block(r, d, h_keep, h_send)
        inner = inner + jnp.sum(d * gains[r, 0:1, :].astype(F32) * xs[r][...].astype(F32), axis=1, keepdims=True)
    inner_out[...] = inner
    kv_pad = jnp.zeros((RANK, QUARTER - 2 * kv_cols), F32)
    d_kv = jnp.concatenate([nn(t1t[RANK:2 * RANK, :], dk), nn(t1t[2 * RANK:, :], dv), kv_pad], axis=1)
    for k, value in enumerate((nn(t1t[:RANK, :], dq), d_out_a, d_kv)):
        at = slice(k * RANK, (k + 1) * RANK)
        if last:
            value = value + rest[0][at, :]
        b_out[at, :] = value.astype(b_out.dtype)
    dt1t = dt1.T.astype(BF16)
    for r in range(PARTS):
        at = quarter(me, r)
        for rows_at, left, right in ((slice(0, 3 * RANK), dt1t, h_in), (slice(3 * RANK, 4 * RANK), tot[...], z_s)):
            value = nn(left, right[:, at])
            if last:
                value = value + rest[1][rows_at, at]
                ref = outs[6] if r in (0, 2) else outs[7]
                ref[rows_at, LO if r in (0, 1) else HI] = value.astype(BF16)
            else:
                outs[6][rows_at, at] = value


def finish_kernel(*refs):
    out = refs[-1]
    gain = refs[0][0, 0:1, :].astype(F32)
    for c in range(CHUNKS):
        x, dx, low, got, inv, inner, inner_y = refs[1 + 7 * c:8 + 7 * c]
        rows = x.shape[0]
        inv = inv[...]
        scale = inv * inv * inv * (inner[...] + inner_y[...]) / WIDTH
        grad = inv * (gain * (low[...] + got[...].astype(F32))) - x[...].astype(F32) * scale
        out[c * rows:(c + 1) * rows, :] = (dx[...] + grad).astype(BF16)


def feedforward_sum_kernel(info, owners, b0, a0, a1, a2, a3, *outs):
    ga, gdb, gb, gda = outs[-4:]
    adapter = pl.program_id(0)
    me, place = info[0], info[3]
    slots = b0.shape[0]
    blocks = gda.shape[2] // QUARTER
    for ref in (ga, gdb, gb, gda):
        ref[...] = jnp.zeros_like(ref)

    def add(slot, carry):
        @pl.when(owners[slot] == adapter)
        def _():
            at = entry_of(slot, place, slots)
            for i in range(blocks):
                cols = slice(i * QUARTER, (i + 1) * QUARTER)
                base = i * 3 * RANK
                gb[0, 0, :, cols] += b0[at, base:base + RANK, :].astype(F32)
                gb[0, 1, :, cols] += b0[at, base + RANK:base + 2 * RANK, :].astype(F32)
                gda[0, :, cols] += b0[at, base + 2 * RANK:base + 3 * RANK, :].astype(F32)
            for r, ref in enumerate((a0, a1, a2, a3)):
                ga[0, :, quarter(me, r)] += ref[at, :2 * RANK, :].astype(F32)
                gdb[0, :, quarter(me, r)] += ref[at, 2 * RANK:, :].astype(F32)
        return carry

    lax.fori_loop(0, slots, add, 0)


def attention_sum_kernel(info, owners, b0, a0, a1, a2, a3, ga, gob, gq, gkv, goa):
    adapter = pl.program_id(0)
    me, place = info[0], info[3]
    slots = b0.shape[0]
    kv_cols = gkv.shape[3]
    for ref in (ga, gob, gq, gkv, goa):
        ref[...] = jnp.zeros_like(ref)

    def add(slot, carry):
        @pl.when(owners[slot] == adapter)
        def _():
            at = entry_of(slot, place, slots)
            gq[0] += b0[at, :RANK, :].astype(F32)
            goa[0] += b0[at, RANK:2 * RANK, :].astype(F32)
            gkv[0, 0] += b0[at, 2 * RANK:, :kv_cols].astype(F32)
            gkv[0, 1] += b0[at, 2 * RANK:, kv_cols:2 * kv_cols].astype(F32)
            for r, ref in enumerate((a0, a1, a2, a3)):
                ga[0, :, quarter(me, r)] += ref[at, :3 * RANK, :].astype(F32)
                gob[0, :, quarter(me, r)] += ref[at, 3 * RANK:, :].astype(F32)
        return carry

    lax.fori_loop(0, slots, add, 0)


def sds(shape, dtype):
    return jax.ShapeDtypeStruct(tuple(shape), dtype)


def in_vmem(value):
    return pltpu.with_memory_space_constraint(value, pltpu.VMEM)


def call(kernel, info, weights, args, outs, scratch, name, mib, after=()):
    vmem = pl.BlockSpec(memory_space=pltpu.VMEM)
    scalars = () if info is None else (info,)
    n, w = len(scalars), len(weights)

    def body(*refs):
        at = n + w + len(args)
        kernel(*refs[:at], *refs[at + len(after):])

    return pl.pallas_call(
        body,
        in_specs=[pl.BlockSpec(memory_space=pltpu.SMEM)] * n + [vmem] * (w + len(args))
        + [pl.BlockSpec(memory_space=pl.ANY)] * len(after),
        out_specs=[vmem] * len(outs),
        out_shape=[pltpu.VMEM(tuple(s), d) for s, d in outs],
        scratch_shapes=[pltpu.VMEM(s, d) for s, d in scratch],
        compiler_params=pltpu.CompilerParams(vmem_limit_bytes=mib * MIB),
        cost_estimate=pl.CostEstimate(flops=1000, transcendentals=0, bytes_accessed=1000),
        name=name,
    )(*scalars, *(in_vmem(a) for a in (*weights, *args)), *after)


def load_kernel(*refs):
    half = (len(refs) - 1) // 2
    copies = [pltpu.make_async_copy(refs[i], refs[half + i], refs[-1].at[i]) for i in range(half)]
    for copy in copies:
        copy.start()
    for copy in copies:
        copy.wait()


def load(*arrays):
    return pl.pallas_call(
        load_kernel,
        in_specs=[pl.BlockSpec(memory_space=pltpu.HBM)] * len(arrays),
        out_specs=[pl.BlockSpec(memory_space=pltpu.VMEM)] * len(arrays),
        out_shape=[pltpu.VMEM(a.shape, a.dtype) for a in arrays],
        scratch_shapes=[pltpu.SemaphoreType.DMA((len(arrays),))],
        compiler_params=pltpu.CompilerParams(vmem_limit_bytes=MIB),
        cost_estimate=pl.CostEstimate(
            flops=0, transcendentals=0, bytes_accessed=sum(a.size * a.dtype.itemsize for a in arrays)),
        name="load",
    )(*arrays)


def sum_call(kernel, scalars, args, outs, name):
    specs = [pl.BlockSpec((1,) + o.shape[1:], (lambda n: lambda i, *_: (i,) + (0,) * n)(len(o.shape) - 1)) for o in outs]
    return pl.pallas_call(
        kernel,
        grid_spec=pltpu.PrefetchScalarGridSpec(
            num_scalar_prefetch=len(scalars), grid=(outs[0].shape[0],),
            in_specs=[pl.BlockSpec(memory_space=pltpu.VMEM)] * len(args), out_specs=specs),
        out_shape=outs,
        compiler_params=pltpu.CompilerParams(dimension_semantics=("arbitrary",), vmem_limit_bytes=12 * MIB),
        cost_estimate=pl.CostEstimate(flops=0, transcendentals=0, bytes_accessed=12000000),
        name=name,
    )(*scalars, *(in_vmem(a) for a in args))


def swap(value, bit, axis, size):
    return lax.ppermute(value, axis, [(i, i ^ bit) for i in range(size)])


def near(value):
    return swap(value, 1, "mp", PARTS)


def far(value):
    return swap(value, 2, "mp", PARTS)


def spread(value):
    there = far(value)
    return (value, near(value), there, near(there))


def chip_sum(keep, send):
    got = near(send)
    lo = keep[:, :QUARTER].astype(F32) + got[:, :QUARTER].astype(F32)
    hi = keep[:, QUARTER:].astype(F32) + got[:, QUARTER:].astype(F32)
    return lo, hi.astype(BF16)


def reduce_scatter(keep, send):
    lo, hi = chip_sum(keep, send)
    return (lo + far(hi).astype(F32)).astype(BF16)


def pair_sum(keep, send):
    return (keep.astype(F32) + near(send).astype(F32)).astype(BF16)


def pick(value, index):
    return value.at[index].get(mode="promise_in_bounds")


def late(value, *others):
    return lax.optimization_barrier((value, *others))[0]


def along(value, k, size):
    return lax.ppermute(value, "dp", [(i, (i + 2 * k) % size) for i in range(size)])


def across(value, size):
    return swap(value, 1, "dp", size)


def gather_slots(value, size):
    own = value[None]
    rest = jnp.concatenate([along(own, k, size) for k in range(1, size // 2)], axis=0)
    return jnp.concatenate([own, rest, across(own, size), across(rest, size)], axis=0)


def entry_of(slot, place, size):
    side = (slot ^ place) & 1
    ahead = (place ^ side) - slot
    ahead = jnp.where(ahead < 0, ahead + size, ahead)
    return side * (size // 2) + ahead // 2


def shards(dp, residual, attention_gain, query_matrix, key_value_matrix, output_matrix, feedfwd_gain,
           gate_up_matrix, down_matrix, attention_adapter_input, query_adapter_output,
           key_value_adapter_output, output_adapter_input, output_adapter_output, feedfwd_adapter_input,
           feedfwd_adapter_output, down_adapter_input, down_adapter_output, lengths, adapter_index,
           dealing_slots, cotangent):
    seqs = residual.shape[0]
    length = cotangent.shape[1]
    units = down_matrix.shape[0]
    adapters = attention_adapter_input.shape[0]
    q_cols = query_matrix.shape[1]
    kv_cols = key_value_matrix.shape[2]
    kv_heads = kv_cols // HEAD
    heads = q_cols // HEAD
    rows = length // CHUNKS
    half = 2 * QUARTER
    me = lax.axis_index("mp")
    place = lax.axis_index("dp")

    is_there = dealing_slots[None, :] == jnp.arange(seqs, dtype=jnp.int32)[:, None]
    seq_of_slot = jnp.sum(jnp.where(is_there, jnp.arange(seqs, dtype=jnp.int32)[None, :], 0), axis=1)
    owners = jnp.sum(jnp.where(is_there, adapter_index[None, :], 0), axis=1)
    spans = jnp.sum(jnp.where(is_there, lengths[None, :], 0), axis=1)
    mine = jnp.arange(seqs, dtype=jnp.int32) == place
    my_length = jnp.sum(jnp.where(mine, spans, 0))
    my_adapter = jnp.sum(jnp.where(mine, owners, 0))
    info = jnp.stack([me.astype(jnp.int32), my_length, my_adapter, place.astype(jnp.int32)])

    def cut(value):
        return [value[c * rows:(c + 1) * rows] for c in range(CHUNKS)]

    gs = list(zip(*[cut(v) for v in spread(cotangent[0])]))
    gains = jnp.stack(spread(jnp.stack([attention_gain, feedfwd_gain])))
    dealt = lax.all_to_all(
        pick(residual, seq_of_slot), "dp", split_axis=0, concat_axis=1, tiled=True
    )[0]
    wq, wkv, wo, wgu, wd = load(query_matrix, key_value_matrix, output_matrix, gate_up_matrix, down_matrix)
    xs = [spread(v) for v in cut(late(dealt, wkv))]
    cos_np, sin_np = rope_tables(length)
    cos = [jnp.asarray(cos_np[:, c * rows:(c + 1) * rows]) for c in range(CHUNKS)]
    sin = [jnp.asarray(sin_np[:, c * rows:(c + 1) * rows]) for c in range(CHUNKS)]
    a1, qb, kvb, oa, ob, a2, fba, da, bd = (
        lax.dynamic_index_in_dim(v, my_adapter, 0, keepdims=False) for v in (
            attention_adapter_input, query_adapter_output, key_value_adapter_output, output_adapter_input,
            output_adapter_output, feedfwd_adapter_input, feedfwd_adapter_output, down_adapter_input,
            down_adapter_output))
    wide, col, block, thin = (rows, WIDTH), (rows, half), (rows, QUARTER), (rows, 1)
    saved = [None] * CHUNKS
    order = ()
    for c in range(CHUNKS):
        outs = [(wide, BF16), ((3 * RANK, rows), BF16), ((q_cols, rows), BF16), ((kv_heads, rows, HEAD), BF16),
                ((kv_heads, rows, HEAD), BF16), ((kv_cols, rows), BF16), ((kv_cols, rows), BF16)]
        saved[c] = call(
            project_kernel, info, (wq, wkv), (*xs[c], gains, a1, qb, kvb, cos[c], sin[c]), outs, [], "project_%d" % c,
            8, order)
        order = (saved[c][1],)

    kept, z_own = [None] * CHUNKS, [None] * CHUNKS
    for c in reversed(range(CHUNKS)):
        outs = [(col, F32), (col, BF16), ((q_cols, rows), BF16), ((heads, rows), F32), ((RANK, rows), BF16)]
        pairs = [v for p in saved[:c + 1] for v in (p[3], p[6])]
        z_keep, z_send, *kept[c] = call(
            functools.partial(attend_kernel, c), info, (wo,), (saved[c][2], oa, ob, *pairs), outs, [], "attend_%d" % c,
            8, order)
        order = (kept[c][1],)
        z_own[c] = pair_sum(z_keep, z_send)
    z_far = [far(v) for v in z_own]

    def front(c, z_there, partial, order):
        hidden = (rows, units)
        outs = [(wide, BF16), (block, F32), (wide, BF16), (wide, BF16), (hidden, BF16), (hidden, BF16), (hidden, BF16),
                ((rows, 2 * RANK), BF16), ((rows, RANK), BF16),
                ((3 * RANK * units // QUARTER, QUARTER), F32 if c else BF16)]
        return call(
            functools.partial(front_kernel, c, c == 0), info, (wgu, wd),
            (*xs[c], z_own[c], z_far[c], near(z_own[c]), z_there, *gs[c], gains, a2, bd, fba, da, *partial), outs,
            [(wide, F32)], "front_%d" % c, 10, order)

    def back(c, hidden, partial, order):
        outs = [(col, F32), (col, BF16), (col, F32), (col, BF16)]
        outs += [((3 * RANK, WIDTH), F32)] if c else [((3 * RANK, half), BF16)] * 2
        return call(
            functools.partial(back_kernel, c == 0), info, (wgu, wd), (*hidden[2:7], a2, bd, fba, da, *partial), outs, [],
            "back_%d" % c, 8, order)

    def attend_back(c, d_there, partial, order):
        outs = [(block, F32), (col, F32), (col, BF16), (thin, F32), (thin, F32),
                ((3 * RANK, QUARTER), F32 if c else BF16)]
        outs += ([((4 * RANK, WIDTH), F32), ((kv_cols, rows), F32), ((kv_cols, rows), F32)] if c
                 else [((4 * RANK, half), BF16)] * 2)
        scratch = [(wide, BF16), (wide, F32), ((q_cols, rows), BF16), ((q_cols, rows), F32),
                   ((c + 1, kv_cols, rows), F32), ((c + 1, kv_cols, rows), F32), ((rows, q_cols + 2 * kv_cols), BF16)]
        triples = [v for p in saved[:c + 1] for v in (p[3], p[4], p[5])]
        return call(
            functools.partial(attend_back_kernel, c, c == 0), info, (wq, wkv, wo),
            (*xs[c], *gs[c], hidden[c][0], d_own[c], d_far[c], near(d_own[c]), d_there, gains, a1, qb, kvb, oa, ob,
             cos[c], sin[c], *saved[c][:3], *kept[c], *triples, *partial), outs, scratch, "attend_back_%d" % c, 12,
            order)

    hidden, d_own, d_far, y_low, y_high = ([None] * CHUNKS for _ in range(5))
    hidden[1] = front(1, near(z_far[1]), (), order)
    step = hidden[1][8]
    z_there = near(late(z_far[0], step))
    d_keep, d_send, y_keep, y_send, fa = back(1, hidden[1], (), (step,))
    d_own[1] = pair_sum(d_keep, d_send)
    d_far[1] = far(d_own[1])
    hidden[0] = front(0, z_there, hidden[1][9:], (d_own[1],))
    step = hidden[0][8]
    line = dp // 2
    fb = {0: hidden[0][9][None]}
    fb.update({k: along(fb[0], k, dp) for k in range(1, line)})
    early, mid = [k for k in range(line) if k != line // 2], line // 2
    fb_side = {0: across(fb[0], dp)}
    y_low[1], y_high[1] = chip_sum(y_keep, late(y_send, step))
    d_keep, d_send, y_keep, y_send, fa_keep, fa_send = back(0, hidden[0], (fa,), (step, y_high[1]))
    d_there = near(late(d_far[1], fa_send))
    d_own[0] = pair_sum(d_keep, d_send)
    d_far[0] = far(d_own[0])
    fa_low, fa_high = chip_sum(fa_keep, fa_send)
    dxq, h_keep, h_send, inner, inv, *sums = attend_back(
        1, d_there, (), (d_own[0], fa_high, *(fb[k] for k in early), fb_side[0]))
    fb_side.update({k: across(late(fb[k], inv) if k == mid else fb[k], dp) for k in range(1, line)})
    h_low, h_high = chip_sum(h_keep, h_send)
    inner = inner + near(inner)
    final = [None, (xs[1][0], dxq, h_low, far(h_high), inv, inner, far(inner))]
    d_there = near(late(d_far[0], inv))
    y_low[0], y_high[0] = chip_sum(y_keep, late(y_send, inv))
    ffn_a = (fa_low + far(fa_high).astype(F32)).astype(BF16)
    dxq, h_keep, h_send, inner, inv, att_b, aa_keep, aa_send = attend_back(
        0, d_there, sums, (h_high, y_high[0], ffn_a, fb[mid], *(fb_side[k] for k in early)))
    h_low, h_high = chip_sum(h_keep, h_send)
    inner = inner + near(inner)
    final[0] = (xs[0][0], dxq, h_low, far(h_high), inv, inner, far(inner))
    pack = jnp.concatenate([att_b, reduce_scatter(aa_keep, late(aa_send, h_high, inner))], axis=0)

    dinput, = call(finish_kernel, None, (), (gains, *(v for f in final for v in f)), [((length, QUARTER), BF16)], [],
                   "finish", 8, (pack, fb_side[mid]))
    back_grad = lax.all_to_all(
        dinput.reshape(dp, length // dp, QUARTER), "dp", split_axis=0, concat_axis=0, tiled=True)
    input_grad = pick(back_grad, dealing_slots)

    valid = (jnp.arange(length, dtype=jnp.int32) < my_length)[:, None]
    result = jnp.concatenate([hidden[c][1] + y_low[c] + far(late(y_high[c], h_high if c else dinput)).astype(F32) for c in range(CHUNKS)], axis=0)
    result = late(jnp.where(valid, result, 0.0).astype(BF16), dinput)
    back_out = lax.all_to_all(
        result.reshape(dp, length // dp, QUARTER), "dp", split_axis=0, concat_axis=0, tiled=True)
    output = pick(back_out, dealing_slots)

    outs = [sds((adapters, 2 * RANK, WIDTH), F32), sds((adapters, RANK, WIDTH), F32),
            sds((adapters, 2, RANK, units), F32), sds((adapters, RANK, units), F32)]
    ga_ffn, g_down_b, g_ffn_b, g_down_a = sum_call(
        feedforward_sum_kernel, (info, owners), (jnp.concatenate([d[k] for d in (fb, fb_side) for k in range(line)], axis=0),
         *spread(gather_slots(late(ffn_a, dinput), dp))), outs,
        "feedforward_sum")

    n_b = att_b.shape[0]
    pack = gather_slots(pack, dp)
    outs = [sds((adapters, 3 * RANK, WIDTH), F32), sds((adapters, RANK, WIDTH), F32),
            sds((adapters, RANK, q_cols), F32), sds((adapters, 2, RANK, kv_cols), F32),
            sds((adapters, RANK, q_cols), F32)]
    ga_att, g_out_b, g_query_b, g_kv_b, g_out_a = sum_call(
        attention_sum_kernel, (info, owners), (pack[:, :n_b], *spread(pack[:, n_b:])), outs, "attention_sum")
    return (output, input_grad, ga_att, g_query_b, g_kv_b, g_out_a, g_out_b, ga_ffn, g_ffn_b, g_down_a, g_down_b)


def solution(mesh):
    in_specs = (
        P(None, "dp", "mp"), P("mp"), P(None, "mp"), P(None, None, "mp"), P("mp", None), P("mp"),
        P(None, None, "mp"), P("mp", None), P(), P(None, None, "mp"), P(None, None, None, "mp"),
        P(None, None, "mp"), P(), P(), P(None, None, None, "mp"), P(None, None, "mp"), P(), P(), P(), P(),
        P("dp", None, "mp"),
    )
    out_specs = (
        P(None, "dp", "mp"), P(None, "dp", "mp"), P(), P(None, None, "mp"), P(None, None, None, "mp"),
        P(None, None, "mp"), P(), P(), P(None, None, None, "mp"), P(None, None, "mp"), P(),
    )
    return jax.shard_map(
        functools.partial(shards, mesh.shape["dp"]), mesh=mesh, in_specs=in_specs, out_specs=out_specs,
        check_vma=False)
```

```python
import functools

import jax
import jax.numpy as jnp
import numpy as np
from jax import lax
from jax.experimental import pallas as pl
from jax.experimental.pallas import tpu as pltpu
from jax.sharding import PartitionSpec as P

WIDTH = 2048
HEAD = 64
HALF = HEAD // 2
RANK = 16
EPS = 1e-05
ROPE_BASE = 500000.0
NEG_FILL = -1e30
PARTS = 4
LANES = 128
QUARTER = WIDTH // PARTS
CHUNKS = 2
MIB = 1024 * 1024
F32 = jnp.float32
BF16 = jnp.bfloat16


def nn(a, b):
    return lax.dot_general(a, b, (((1,), (0,)), ((), ())), preferred_element_type=F32)


def nt(a, b):
    return lax.dot_general(a, b, (((1,), (1,)), ((), ())), preferred_element_type=F32)


def rope_tables(length):
    freq = ROPE_BASE ** (-np.arange(HALF, dtype=np.float32) * np.float32(2.0 / HEAD))
    angles = (np.arange(length, dtype=np.float32)[None, :] * freq.astype(np.float32)[:, None]).astype(np.float32)
    return np.cos(angles).astype(np.float32), np.sin(angles).astype(np.float32)


def quarter(me, rel):
    return pl.ds(pl.multiple_of((me ^ rel) * QUARTER, QUARTER), QUARTER)


LO, HI = slice(0, QUARTER), slice(QUARTER, 2 * QUARTER)


def total_block(rel, own, oth):
    return (own if rel in (0, 2) else oth)[:, LO if rel in (0, 1) else HI].astype(F32)


def chunk_of(ref, chunk, rows):
    return ref if ref.shape[0] == rows else ref.at[chunk * rows:(chunk + 1) * rows]


def copies_of(pairs, sems):
    made = [pltpu.make_async_copy(source, target, sems.at[i]) for i, (source, target) in enumerate(pairs)]
    for copy in made:
        copy.start()
    return made


def put_block(rel, value, keep_ref, send_ref):
    ref = keep_ref if rel in (0, 2) else send_ref
    ref[:, LO if rel in (0, 1) else HI] = value.astype(ref.dtype)


def rotate(value, cos, sin, out_ref):
    for i in range(value.shape[0] // HEAD):
        u1, u2 = value[i * HEAD:i * HEAD + HALF], value[i * HEAD + HALF:(i + 1) * HEAD]
        out_ref[i * HEAD:i * HEAD + HALF, :] = (u1 * cos - u2 * sin).astype(BF16)
        out_ref[i * HEAD + HALF:(i + 1) * HEAD, :] = (u2 * cos + u1 * sin).astype(BF16)


def turn_back(value, cos, sin, out_ref):
    for i in range(value.shape[0] // HEAD):
        w1, w2 = value[i * HEAD:i * HEAD + HALF], value[i * HEAD + HALF:(i + 1) * HEAD]
        out_ref[i * HEAD:i * HEAD + HALF, :] = (w1 * cos + w2 * sin).astype(BF16)
        out_ref[i * HEAD + HALF:(i + 1) * HEAD, :] = (w2 * cos - w1 * sin).astype(BF16)


def head_rows(i):
    return pl.ds(pl.multiple_of(i * HEAD, HEAD), HEAD)


def visible(key_start, query_start, rows, length):
    kpos = key_start + lax.broadcasted_iota(jnp.int32, (rows, rows), 0)
    qpos = query_start + lax.broadcasted_iota(jnp.int32, (rows, rows), 1)
    return (kpos <= qpos) & (kpos < length)


def project_kernel(chunk, info, wq_h, wkv_h, x0, x1, x2, x3, gains, a1, qb, kvb, cos_t, sin_t,
                   h_out, t1t_out, qt_out, kn_out, vn_out, kt_out, vt_out, wq, wkv, sems):
    copies = copies_of(((wkv_h, wkv), (wq_h, wq)), sems)
    me = info[0]
    rows = h_out.shape[0]
    kv_heads = kn_out.shape[0]
    xs = [chunk_of(x, chunk, rows) for x in (x0, x1, x2, x3)]
    square = jnp.zeros((rows, 1), F32)
    for r in range(PARTS):
        v = xs[r][...].astype(F32)
        square = square + jnp.sum(v * v, axis=1, keepdims=True)
    inv = lax.rsqrt(square / WIDTH + EPS)
    for r in range(PARTS):
        v = xs[r][...].astype(F32)
        h_out[:, quarter(me, r)] = (v * inv * gains[r, 0:1, :].astype(F32)).astype(BF16)
    h = h_out[...]
    t1 = nt(h, a1[...])
    t1t_out[...] = t1.T.astype(BF16)
    t1b = t1.astype(BF16)
    cos, sin = cos_t[...], sin_t[...]
    copies[0].wait()
    k = nn(h, wkv[0]) + nn(t1b[:, RANK:2 * RANK], kvb[0])
    rotate(k.T, cos, sin, kt_out)
    k_n = kt_out[...].T
    v_n = (nn(h, wkv[1]) + nn(t1b[:, 2 * RANK:], kvb[1])).astype(BF16)
    vt_out[...] = v_n.T
    for i in range(kv_heads):
        kn_out[i] = k_n[:, i * HEAD:(i + 1) * HEAD]
        vn_out[i] = v_n[:, i * HEAD:(i + 1) * HEAD]
    copies[1].wait()
    q = nn(h, wq[...]) + nn(t1b[:, :RANK], qb[...])
    rotate(q.T * (HEAD ** -0.5), cos, sin, qt_out)


def attend_kernel(chunk, info, wo_h, qt, oa, ob, *rest):
    pairs, rest = rest[:2 * (chunk + 1)], rest[2 * (chunk + 1):]
    z_keep, z_send, ot_out, lse_out, tot_out, wo, sems = rest
    copies = copies_of(((wo_h, wo),), sems)
    keys, values = pairs[0::2], pairs[1::2]
    me, length = info[0], info[1]
    rows = qt.shape[1]
    kv_heads = keys[0].shape[0]
    heads = qt.shape[0] // HEAD
    group = heads // kv_heads

    def one_head(i, carry):
        j = i // group
        q_h = qt[head_rows(i), :]
        parts = []
        for c, key in enumerate(keys):
            s = nn(key[j], q_h)
            parts.append(jnp.where(visible(c * rows, chunk * rows, rows, length), s, NEG_FILL))
        top = functools.reduce(jnp.maximum, [jnp.max(s, axis=0, keepdims=True) for s in parts])
        es = [jnp.exp(s - top) for s in parts]
        total = sum(jnp.sum(e, axis=0, keepdims=True) for e in es)
        lse_out[pl.ds(i, 1), :] = top + jnp.log(total)
        o_t = sum(nn(value[head_rows(j), :], e.astype(BF16)) for value, e in zip(values, es))
        ot_out[head_rows(i), :] = (o_t / total).astype(BF16)
        return carry

    lax.fori_loop(0, heads, one_head, 0, unroll=2)
    o = ot_out[...].T
    to = nt(o, oa[...])
    tot_out[...] = to.T.astype(BF16)
    to = to.astype(BF16)
    copies[0].wait()
    for r in range(PARTS):
        at = quarter(me, r)
        put_block(r, nn(o, wo[:, at]) + nn(to, ob[:, at]), z_keep, z_send)


def front_kernel(chunk, last, info, wgu_h, wd_h, x0, x1, x2, x3, zo, zp, g0, g1, g2, g3, gains, a2, bd, fb, da,
                 *rest):
    f_s, wgu, wd, sems = rest[-4:]
    xm_out, xq_out, h_out, g_out, act_out, dg_out, du_out, t2_s, dtd_s, b_out = rest[-14:-4]
    units = wd.shape[0]

    def copies(i):
        c = pl.ds(pl.multiple_of(i * QUARTER, QUARTER), QUARTER)
        return (pltpu.make_async_copy(wgu_h.at[:, :, c], wgu.at[:, :, c], sems.at[0, i]),
                pltpu.make_async_copy(wd_h.at[c, :], wd.at[c, :], sems.at[1, i]))

    for i in range(units // QUARTER):
        for copy in copies(i):
            copy.start()
    me, length = info[0], info[1]
    rows = h_out.shape[0]
    xs, gs = ([chunk_of(v, chunk, rows) for v in vs] for vs in ((x0, x1, x2, x3), (g0, g1, g2, g3)))
    valid = chunk * rows + lax.broadcasted_iota(jnp.int32, (rows, 1), 0) < length
    square = jnp.zeros((rows, 1), F32)
    for r in range(PARTS):
        v = xs[r][...].astype(F32) + total_block(r, zo, zp)
        if r == 0:
            xq_out[...] = v
        f_s[:, quarter(me, r)] = v
        square = square + jnp.sum(v * v, axis=1, keepdims=True)
        g_out[:, quarter(me, r)] = jnp.where(valid, gs[r][...], jnp.zeros((), BF16))
    inv = lax.rsqrt(square / WIDTH + EPS)
    for r in range(PARTS):
        v = f_s[:, quarter(me, r)]
        xm_out[:, quarter(me, r)] = v.astype(BF16)
        h_out[:, quarter(me, r)] = (v * inv * gains[r, 1:2, :].astype(F32)).astype(BF16)
    t2 = nt(h_out[...], a2[...])
    t2_s[...] = t2.astype(BF16)
    dtd = nt(g_out[...], bd[...])
    dtd_s[...] = dtd.astype(BF16)
    t2t, dtdt = t2.T.astype(BF16), dtd.T.astype(BF16)

    def block(i, carry):
        c = pl.ds(pl.multiple_of(i * QUARTER, QUARTER), QUARTER)
        for copy in copies(i):
            copy.wait()
        h, g = h_out[...], g_out[...]
        gate = nn(h, wgu[0, :, c]) + nn(t2_s[:, :RANK], fb[0, :, c])
        up = nn(h, wgu[1, :, c]) + nn(t2_s[:, RANK:], fb[1, :, c])
        dact = nt(g, wd[c, :]) + nn(dtd_s[...], da[:, c])
        sig = 1.0 / (1.0 + jnp.exp(-gate))
        silu = gate * sig
        act = (silu * up).astype(BF16)
        dgate = (dact * up * sig * (1.0 + gate * (1.0 - sig))).astype(BF16)
        dup = (dact * silu).astype(BF16)
        act_out[:, c], dg_out[:, c], du_out[:, c] = act, dgate, dup
        for k, value in enumerate((nn(t2t[:RANK], dgate), nn(t2t[RANK:], dup), nn(dtdt, act))):
            at = pl.ds(pl.multiple_of((3 * i + k) * RANK, RANK), RANK)
            if last:
                value = value + rest[0][at, :]
            b_out[at, :] = value.astype(b_out.dtype)
        return carry

    lax.fori_loop(0, units // QUARTER, block, 0)


def back_kernel(last, info, wgu_h, wd_h, h, g, act, dg, du, a2, bd, fb, da, *rest):
    (wgu, wd, sems), rest = rest[-3:], rest[:-3]
    outs, rest = (rest[-6:], rest[:-6]) if last else (rest[-5:], rest[:-5])
    d_keep, d_send, z_keep, z_send = outs[:4]
    me = info[0]

    def copies(r):
        at = quarter(me, r)
        return (pltpu.make_async_copy(wgu_h.at[:, at, :], wgu.at[:, at, :], sems.at[0, r]),
                pltpu.make_async_copy(wd_h.at[:, at], wd.at[:, at], sems.at[1, r]))

    for r in range(PARTS):
        for copy in copies(r):
            copy.start()
    dt2 = jnp.concatenate([nt(dg[...], fb[0]), nt(du[...], fb[1])], axis=1)
    dt2b = dt2.astype(BF16)
    td = nt(act[...], da[...])
    tdb = td.astype(BF16)
    dt2t, tdt = dt2.T.astype(BF16), td.T.astype(BF16)

    def pair(i, carry):
        to = pl.ds(pl.multiple_of(i * QUARTER, QUARTER), QUARTER)
        for r, d_ref, z_ref in ((2 * i, d_keep, z_keep), (2 * i + 1, d_send, z_send)):
            at = quarter(me, r)
            for copy in copies(r):
                copy.wait()
            d = nt(dg[...], wgu[0, at, :]) + nt(du[...], wgu[1, at, :]) + nn(dt2b, a2[:, at])
            d_ref[:, to] = d.astype(d_ref.dtype)
            z_ref[:, to] = (nn(act[...], wd[:, at]) + nn(tdb, bd[:, at])).astype(z_ref.dtype)
        return carry

    lax.fori_loop(0, PARTS // 2, pair, 0)
    for r in range(PARTS):
        at = quarter(me, r)
        for rows_at, left, right in ((slice(0, 2 * RANK), dt2t, h), (slice(2 * RANK, 3 * RANK), tdt, g)):
            value = nn(left, right[:, at])
            if last:
                value = value + rest[0][rows_at, at]
                ref = outs[4] if r in (0, 2) else outs[5]
                ref[rows_at, LO if r in (0, 1) else HI] = value.astype(BF16)
            else:
                outs[4][rows_at, at] = value


def attend_back_kernel(chunk, last, info, wq_h, wkv_h, wo_h, x0, x1, x2, x3, g0, g1, g2, g3, xm, do_, dp, gains, a1,
                       qb, kvb, oa, ob, cos_t, sin_t, h_in, t1t, qt, ot, lse, tot, *rest):
    scratch, rest = rest[-11:], rest[:-11]
    z_s, f_s, dot_s, dqt_s, dkt_s, dvt_s, dq_s, wq, wkv, wo, sems = scratch
    copies = copies_of(((wo_h, wo), (wq_h, wq), (wkv_h, wkv)), sems)
    n_out = 7 if last else 8
    outs, rest = rest[-n_out:], rest[:-n_out]
    dxq_out, h_keep, h_send, inv_out, b_out = outs[:5]
    triples, rest = rest[:3 * (chunk + 1)], rest[3 * (chunk + 1):]
    keys, values, keys_t = triples[0::3], triples[1::3], triples[2::3]
    me, length = info[0], info[1]
    rows = xm.shape[0]
    kv_heads = keys[0].shape[0]
    heads = qt.shape[0] // HEAD
    group = heads // kv_heads
    q_cols, kv_cols = heads * HEAD, kv_heads * HEAD
    xs, gs = ([chunk_of(v, chunk, rows) for v in vs] for vs in ((x0, x1, x2, x3), (g0, g1, g2, g3)))
    valid = chunk * rows + lax.broadcasted_iota(jnp.int32, (rows, 1), 0) < length
    square = jnp.zeros((rows, 1), F32)
    first = jnp.zeros((rows, 1), F32)
    inner = jnp.zeros((rows, 1), F32)
    for r in range(PARTS):
        v = xm[:, quarter(me, r)].astype(F32)
        square = square + jnp.sum(v * v, axis=1, keepdims=True)
        w = total_block(r, do_, dp) * gains[r, 1:2, :].astype(F32)
        f_s[:, quarter(me, r)] = w
        inner = inner + jnp.sum(v * w, axis=1, keepdims=True)
        u = xs[r][...].astype(F32)
        first = first + jnp.sum(u * u, axis=1, keepdims=True)
    inv_out[...] = lax.rsqrt(first / WIDTH + EPS)
    inv = lax.rsqrt(square / WIDTH + EPS)
    back = inv * inv * inv * inner / WIDTH
    for r in range(PARTS):
        v = xm[:, quarter(me, r)].astype(F32)
        g = jnp.where(valid, gs[r][...].astype(F32), 0.0)
        d = g + inv * f_s[:, quarter(me, r)] - v * back
        if r == 0:
            dxq_out[...] = d
        z_s[:, quarter(me, r)] = d.astype(BF16)
    dz = z_s[...]
    dto = nt(dz, ob[...])
    copies[0].wait()
    d_o = nt(dz, wo[...]) + nn(dto.astype(BF16), oa[...])
    dot_s[...] = d_o.T.astype(BF16)
    if last:
        for c in range(chunk + 1):
            dkt_s[c], dvt_s[c] = rest[2][...], rest[3][...]
    else:
        dkt_s[...] = jnp.zeros_like(dkt_s)
        dvt_s[...] = jnp.zeros_like(dvt_s)

    def one_head(i, carry):
        j = i // group
        q_h, do_h = qt[head_rows(i), :], dot_s[head_rows(i), :]
        dots = jnp.sum(do_h.astype(F32) * ot[head_rows(i), :].astype(F32), axis=0, keepdims=True)
        low = lse[pl.ds(i, 1), :]
        dq_h = jnp.zeros((HEAD, rows), F32)
        for c in range(chunk + 1):
            prob = jnp.exp(nn(keys[c][j], q_h) - low)
            prob = jnp.where(visible(c * rows, chunk * rows, rows, length), prob, 0.0)
            ds = (prob * (nn(values[c][j], do_h) - dots)).astype(BF16)
            dq_h = dq_h + nn(keys_t[c][head_rows(j), :], ds)
            dkt_s[c, head_rows(j), :] += nt(q_h, ds)
            dvt_s[c, head_rows(j), :] += nt(do_h, prob.astype(BF16))
        dqt_s[head_rows(i), :] = dq_h
        return carry

    lax.fori_loop(0, heads, one_head, 0, unroll=2)
    if not last:
        outs[6][...], outs[7][...] = dkt_s[0], dvt_s[0]
    cos, sin = cos_t[...], sin_t[...]
    dto_t, o_t = dto.T.astype(BF16), ot[...]
    d_out_a = nt(dto_t, o_t)
    turn_back(dqt_s[...], cos * (HEAD ** -0.5), sin * (HEAD ** -0.5), dot_s)
    dq_s[:, :q_cols] = dot_s[...].T
    turn_back(dkt_s[chunk], cos, sin, dot_s)
    dq_s[:, q_cols:q_cols + kv_cols] = dot_s[:kv_cols, :].T
    dq_s[:, q_cols + kv_cols:] = dvt_s[chunk].T.astype(BF16)
    dq, dk, dv = dq_s[:, :q_cols], dq_s[:, q_cols:q_cols + kv_cols], dq_s[:, q_cols + kv_cols:]
    dt1 = jnp.concatenate([nt(dq, qb[...]), nt(dk, kvb[0]), nt(dv, kvb[1])], axis=1)
    dt1b = dt1.astype(BF16)
    inner = jnp.zeros((rows, 1), F32)
    copies[1].wait()
    copies[2].wait()
    for r in range(PARTS):
        at = quarter(me, r)
        d = nt(dq, wq[at, :]) + nt(dk, wkv[0, at, :]) + nt(dv, wkv[1, at, :]) + nn(dt1b, a1[:, at])
        put_block(r, d, h_keep, h_send)
        inner = inner + jnp.sum(d * gains[r, 0:1, :].astype(F32) * xs[r][...].astype(F32), axis=1, keepdims=True)
    for ref in (h_keep, h_send):
        ref[:, 2 * QUARTER:] = jnp.broadcast_to(inner, (rows, LANES)).astype(ref.dtype)
    kv_pad = jnp.zeros((RANK, QUARTER - 2 * kv_cols), F32)
    d_kv = jnp.concatenate([nn(t1t[RANK:2 * RANK, :], dk), nn(t1t[2 * RANK:, :], dv), kv_pad], axis=1)
    for k, value in enumerate((nn(t1t[:RANK, :], dq), d_out_a, d_kv)):
        at = slice(k * RANK, (k + 1) * RANK)
        if last:
            value = value + rest[0][at, :]
        b_out[at, :] = value.astype(b_out.dtype)
    dt1t = dt1.T.astype(BF16)
    for r in range(PARTS):
        at = quarter(me, r)
        for rows_at, left, right in ((slice(0, 3 * RANK), dt1t, h_in), (slice(3 * RANK, 4 * RANK), tot[...], z_s)):
            value = nn(left, right[:, at])
            if last:
                value = value + rest[1][rows_at, at]
                ref = outs[5] if r in (0, 2) else outs[6]
                ref[rows_at, LO if r in (0, 1) else HI] = value.astype(BF16)
            else:
                outs[5][rows_at, at] = value


def finish_kernel(gains, x_all, *refs):
    out = refs[-1]
    gain = gains[0, 0:1, :].astype(F32)
    rows = out.shape[0] // CHUNKS
    for c in range(CHUNKS):
        dx, low, high, got, inv = refs[5 * c:5 * (c + 1)]
        x = chunk_of(x_all, c, rows)
        inv = inv[...]
        inner = high[:, QUARTER:QUARTER + 1].astype(F32) + got[:, QUARTER:QUARTER + 1].astype(F32)
        scale = inv * inv * inv * inner / WIDTH
        grad = inv * (gain * (low[...] + got[:, :QUARTER].astype(F32))) - x[...].astype(F32) * scale
        out[c * rows:(c + 1) * rows, :] = (dx[...] + grad).astype(BF16)


def feedforward_sum_kernel(info, owners, b0, a0, a1, a2, a3, *outs):
    ga, gdb, gb, gda = outs[-4:]
    adapter = pl.program_id(0)
    me, place = info[0], info[3]
    slots = b0.shape[0]
    blocks = gda.shape[2] // QUARTER
    for ref in (ga, gdb, gb, gda):
        ref[...] = jnp.zeros_like(ref)

    def add(slot, carry):
        @pl.when(owners[slot] == adapter)
        def _():
            at = entry_of(slot, place, slots)
            for i in range(blocks):
                cols = slice(i * QUARTER, (i + 1) * QUARTER)
                base = i * 3 * RANK
                gb[0, 0, :, cols] += b0[at, base:base + RANK, :].astype(F32)
                gb[0, 1, :, cols] += b0[at, base + RANK:base + 2 * RANK, :].astype(F32)
                gda[0, :, cols] += b0[at, base + 2 * RANK:base + 3 * RANK, :].astype(F32)
            for r, ref in enumerate((a0, a1, a2, a3)):
                ga[0, :, quarter(me, r)] += ref[at, :2 * RANK, :].astype(F32)
                gdb[0, :, quarter(me, r)] += ref[at, 2 * RANK:, :].astype(F32)
        return carry

    lax.fori_loop(0, slots, add, 0)


def attention_sum_kernel(info, owners, b0, a0, a1, a2, a3, ga, gob, gq, gkv, goa):
    adapter = pl.program_id(0)
    me, place = info[0], info[3]
    slots = b0.shape[0]
    kv_cols = gkv.shape[3]
    for ref in (ga, gob, gq, gkv, goa):
        ref[...] = jnp.zeros_like(ref)

    def add(slot, carry):
        @pl.when(owners[slot] == adapter)
        def _():
            at = entry_of(slot, place, slots)
            gq[0] += b0[at, :RANK, :].astype(F32)
            goa[0] += b0[at, RANK:2 * RANK, :].astype(F32)
            gkv[0, 0] += b0[at, 2 * RANK:, :kv_cols].astype(F32)
            gkv[0, 1] += b0[at, 2 * RANK:, kv_cols:2 * kv_cols].astype(F32)
            for r, ref in enumerate((a0, a1, a2, a3)):
                ga[0, :, quarter(me, r)] += ref[at, :3 * RANK, :].astype(F32)
                gob[0, :, quarter(me, r)] += ref[at, 3 * RANK:, :].astype(F32)
        return carry

    lax.fori_loop(0, slots, add, 0)


def sds(shape, dtype):
    return jax.ShapeDtypeStruct(tuple(shape), dtype)


def in_vmem(value):
    return pltpu.with_memory_space_constraint(value, pltpu.VMEM)


def in_hbm(value):
    return pltpu.with_memory_space_constraint(value, pltpu.HBM)


def call(kernel, info, weights, args, outs, scratch, name, mib, after=(), sems=()):
    vmem = pl.BlockSpec(memory_space=pltpu.VMEM)
    scalars = () if info is None else (info,)
    n, w = len(scalars), len(weights)

    def body(*refs):
        at = n + w + len(args)
        kernel(*refs[:at], *refs[at + len(after):])

    return pl.pallas_call(
        body,
        in_specs=[pl.BlockSpec(memory_space=pltpu.SMEM)] * n + [pl.BlockSpec(memory_space=pltpu.HBM)] * w + [vmem] * len(args)
        + [pl.BlockSpec(memory_space=pl.ANY)] * len(after),
        out_specs=[vmem] * len(outs),
        out_shape=[pltpu.VMEM(tuple(s), d) for s, d in outs],
        scratch_shapes=[pltpu.VMEM(s, d) for s, d in scratch] + ([pltpu.SemaphoreType.DMA(sems)] if sems else []),
        compiler_params=pltpu.CompilerParams(vmem_limit_bytes=mib * MIB),
        cost_estimate=pl.CostEstimate(flops=1000, transcendentals=0, bytes_accessed=1000),
        name=name,
    )(*scalars, *(in_hbm(a) for a in weights), *(in_vmem(a) for a in args), *after)


def sum_call(kernel, scalars, args, outs, name):
    specs = [pl.BlockSpec((1,) + o.shape[1:], (lambda n: lambda i, *_: (i,) + (0,) * n)(len(o.shape) - 1)) for o in outs]
    return pl.pallas_call(
        kernel,
        grid_spec=pltpu.PrefetchScalarGridSpec(
            num_scalar_prefetch=len(scalars), grid=(outs[0].shape[0],),
            in_specs=[pl.BlockSpec(memory_space=pltpu.VMEM)] * len(args), out_specs=specs),
        out_shape=outs,
        compiler_params=pltpu.CompilerParams(
            dimension_semantics=("arbitrary",),
            vmem_limit_bytes=12 * MIB + sum(a.size * a.dtype.itemsize for a in args)),
        cost_estimate=pl.CostEstimate(flops=0, transcendentals=0, bytes_accessed=12000000),
        name=name,
    )(*scalars, *(in_vmem(a) for a in args))


def swap(value, bit, axis, size):
    return lax.ppermute(value, axis, [(i, i ^ bit) for i in range(size)])


def near(value):
    return swap(value, 1, "mp", PARTS)


def far(value):
    return swap(value, 2, "mp", PARTS)


def spread(value):
    there = far(value)
    return (value, near(value), there, near(there))


def chip_sum(keep, send):
    got = near(send)
    lo = keep[:, :QUARTER].astype(F32) + got[:, :QUARTER].astype(F32)
    hi = keep[:, QUARTER:].astype(F32) + got[:, QUARTER:].astype(F32)
    return lo, hi.astype(BF16)


def far_sum_kernel(own, got, out):
    for to, other in ((LO, HI), (HI, LO)):
        out[:, to] = (own[:, to].astype(F32) + got[:, other].astype(F32)).astype(BF16)


def far_sum(own, got):
    return call(far_sum_kernel, None, (), (own, got), [(own.shape, BF16)], [], "far_sum", 6)[0]


def reduce_scatter(keep, send):
    lo, hi = chip_sum(keep, send)
    return (lo + far(hi).astype(F32)).astype(BF16)


def pair_sum_kernel(keep, got, out):
    out[...] = (keep[...] + got[...].astype(F32)).astype(BF16)


def pair_sum(keep, send):
    return call(pair_sum_kernel, None, (), (keep, near(send)), [(send.shape, BF16)], [], "pair_sum", 6)[0]


def pick(value, index):
    return value.at[index].get(mode="promise_in_bounds")


def late(value, *others):
    return lax.optimization_barrier((value, *others))[0]


def doubled(stack, bit, size):
    return jnp.concatenate([stack, swap(stack, bit, "dp", size)], axis=0)


def gather_slots(value, size):
    stack = value[None]
    for b in reversed(range(size.bit_length() - 1)):
        stack = doubled(stack, 1 << b, size)
    return stack


def entry_of(slot, place, size):
    bits = size.bit_length() - 1
    apart = slot ^ place
    return sum(((apart >> b) & 1) << (bits - 1 - b) for b in range(bits))


def shards(dp, residual, attention_gain, query_matrix, key_value_matrix, output_matrix, feedfwd_gain,
           gate_up_matrix, down_matrix, attention_adapter_input, query_adapter_output,
           key_value_adapter_output, output_adapter_input, output_adapter_output, feedfwd_adapter_input,
           feedfwd_adapter_output, down_adapter_input, down_adapter_output, lengths, adapter_index,
           dealing_slots, cotangent):
    seqs = residual.shape[0]
    length = cotangent.shape[1]
    units = down_matrix.shape[0]
    adapters = attention_adapter_input.shape[0]
    q_cols = query_matrix.shape[1]
    kv_cols = key_value_matrix.shape[2]
    kv_heads = kv_cols // HEAD
    heads = q_cols // HEAD
    rows = length // CHUNKS
    half = 2 * QUARTER
    me = lax.axis_index("mp")
    place = lax.axis_index("dp")

    is_there = dealing_slots[None, :] == jnp.arange(seqs, dtype=jnp.int32)[:, None]
    seq_of_slot = jnp.sum(jnp.where(is_there, jnp.arange(seqs, dtype=jnp.int32)[None, :], 0), axis=1)
    owners = jnp.sum(jnp.where(is_there, adapter_index[None, :], 0), axis=1)
    spans = jnp.sum(jnp.where(is_there, lengths[None, :], 0), axis=1)
    mine = jnp.arange(seqs, dtype=jnp.int32) == place
    my_length = jnp.sum(jnp.where(mine, spans, 0))
    my_adapter = jnp.sum(jnp.where(mine, owners, 0))
    info = jnp.stack([me.astype(jnp.int32), my_length, my_adapter, place.astype(jnp.int32)])

    gs = spread(cotangent[0])
    gains = jnp.stack(spread(jnp.stack([attention_gain, feedfwd_gain])))
    dealt = lax.all_to_all(
        pick(residual, seq_of_slot), "dp", split_axis=0, concat_axis=1, tiled=True
    )[0]
    beside = near(dealt)
    there = [far(dealt[c * rows:(c + 1) * rows]) for c in range(CHUNKS)]
    xs = [(dealt, beside, v, near(v)) for v in there]
    cos_np, sin_np = rope_tables(length)
    cos = [jnp.asarray(cos_np[:, c * rows:(c + 1) * rows]) for c in range(CHUNKS)]
    sin = [jnp.asarray(sin_np[:, c * rows:(c + 1) * rows]) for c in range(CHUNKS)]
    a1, qb, kvb, oa, ob, a2, fba, da, bd = (
        lax.dynamic_index_in_dim(v, my_adapter, 0, keepdims=False) for v in (
            attention_adapter_input, query_adapter_output, key_value_adapter_output, output_adapter_input,
            output_adapter_output, feedfwd_adapter_input, feedfwd_adapter_output, down_adapter_input,
            down_adapter_output))
    wq, wkv, wo, wgu, wd = query_matrix, key_value_matrix, output_matrix, gate_up_matrix, down_matrix
    def like(*arrays):
        return [(a.shape, a.dtype) for a in arrays]

    wide, col, block, thin = (rows, WIDTH), (rows, half), (rows, QUARTER), (rows, 1)
    saved = [None] * CHUNKS
    order = ()
    for c in range(CHUNKS):
        outs = [(wide, BF16), ((3 * RANK, rows), BF16), ((q_cols, rows), BF16), ((kv_heads, rows, HEAD), BF16),
                ((kv_heads, rows, HEAD), BF16), ((kv_cols, rows), BF16), ((kv_cols, rows), BF16)]
        saved[c] = call(
            functools.partial(project_kernel, c), info, (wq, wkv), (*xs[c], gains, a1, qb, kvb, cos[c], sin[c]), outs,
            like(wq, wkv), "project_%d" % c, 12, order, (2,))
        order = (saved[c][1],)

    kept, z_own = [None] * CHUNKS, [None] * CHUNKS
    for c in reversed(range(CHUNKS)):
        outs = [(col, F32), (col, BF16), ((q_cols, rows), BF16), ((heads, rows), F32), ((RANK, rows), BF16)]
        pairs = [v for p in saved[:c + 1] for v in (p[3], p[6])]
        z_keep, z_send, *kept[c] = call(
            functools.partial(attend_kernel, c), info, (wo,), (saved[c][2], oa, ob, *pairs), outs, like(wo),
            "attend_%d" % c, 10, order, (1,))
        z_own[c] = pair_sum(z_keep, z_send)
        order = (kept[c][1], z_own[1])
    z_far = [far(v) for v in z_own]

    def front(c, total, partial, order):
        hidden = (rows, units)
        outs = [(wide, BF16), (block, F32), (wide, BF16), (wide, BF16), (hidden, BF16), (hidden, BF16), (hidden, BF16),
                ((rows, 2 * RANK), BF16), ((rows, RANK), BF16),
                ((3 * RANK * units // QUARTER, QUARTER), F32 if c else BF16)]
        return call(
            functools.partial(front_kernel, c, c == 0), info, (wgu, wd),
            (*xs[c], total, near(total), *gs, gains, a2, bd, fba, da, *partial), outs, [(wide, F32)] + like(wgu, wd),
            "front_%d" % c, 34, order, (2, units // QUARTER))

    def back(c, hidden, partial, order):
        outs = [(col, F32), (col, BF16), (col, F32), (col, BF16)]
        outs += [((3 * RANK, WIDTH), F32)] if c else [((3 * RANK, half), BF16)] * 2
        return call(
            functools.partial(back_kernel, c == 0), info, (wgu, wd), (*hidden[2:7], a2, bd, fba, da, *partial), outs,
            like(wgu, wd), "back_%d" % c, 32, order, (2, PARTS))

    def attend_back(c, total, partial, order):
        padded = (rows, half + LANES)
        outs = [(block, F32), (padded, F32), (padded, BF16), (thin, F32), ((3 * RANK, QUARTER), F32 if c else BF16)]
        outs += ([((4 * RANK, WIDTH), F32), ((kv_cols, rows), F32), ((kv_cols, rows), F32)] if c
                 else [((4 * RANK, half), BF16)] * 2)
        scratch = [(wide, BF16), (wide, F32), ((q_cols, rows), BF16), ((q_cols, rows), F32),
                   ((c + 1, kv_cols, rows), F32), ((c + 1, kv_cols, rows), F32), ((rows, q_cols + 2 * kv_cols), BF16)]
        triples = [v for p in saved[:c + 1] for v in (p[3], p[4], p[5])]
        return call(
            functools.partial(attend_back_kernel, c, c == 0), info, (wq, wkv, wo),
            (*xs[c], *gs, hidden[c][0], total, near(total), gains, a1, qb, kvb, oa, ob, cos[c], sin[c], *saved[c][:3],
             *kept[c], *triples, *partial), outs, scratch + like(wq, wkv, wo), "attend_back_%d" % c, 18, order, (3,))

    hidden, d_own, d_far, y_low, y_high = ([None] * CHUNKS for _ in range(5))
    hidden[1] = front(1, far_sum(z_own[1], z_far[1]), (), order)
    step = hidden[1][8]
    total = far_sum(z_own[0], late(z_far[0], step))
    d_keep, d_send, y_keep, y_send, fa = back(1, hidden[1], (), (step, total))
    d_own[1] = pair_sum(d_keep, d_send)
    d_far[1] = far(d_own[1])
    hidden[0] = front(0, total, hidden[1][9:], (d_own[1],))
    step = hidden[0][8]
    total = far_sum(d_own[1], late(d_far[1], step))
    fb = hidden[0][9][None]
    fb_first = swap(fb, dp // 2, "dp", dp)
    y_first = (y_keep, y_send)
    d_keep, d_send, y_keep, y_send, fa_keep, fa_send = back(0, hidden[0], (fa,), (step, total))
    d_own[0] = pair_sum(d_keep, late(d_send, fb_first))
    d_far[0] = far(d_own[0])
    fb = jnp.concatenate([fb, fb_first], axis=0)
    fb_more = fb
    for b in reversed(range(1, dp.bit_length() - 2)):
        fb_more = doubled(fb_more, 1 << b, dp)
    fb_more = fb_more[2:]
    fb_side = swap(fb, 1, "dp", dp)
    y_low[1], y_high[1] = chip_sum(y_first[0], late(y_first[1], fa_send))
    fa_low, fa_high = chip_sum(fa_keep, fa_send)
    dxq, h_keep, h_send, inv, *sums = attend_back(1, total, (), (d_own[0], fa_high, y_high[1]))
    total = far_sum(d_own[0], late(d_far[0], inv))
    h_low, h_high = chip_sum(h_keep, late(h_send, fb_more, fb_side))
    final = [None, (dxq, h_low, h_high, far(h_high), inv)]
    y_low[0], y_high[0] = chip_sum(y_keep, late(y_send, inv))
    ffn_a = (fa_low + far(fa_high).astype(F32)).astype(BF16)[None]
    fa_first = swap(ffn_a, dp // 2, "dp", dp)
    dxq, h_keep, h_send, inv, att_b, aa_keep, aa_send = attend_back(0, total, sums, (h_high, y_high[0], ffn_a))
    fb_more_side = swap(fb_more, 1, "dp", dp)
    h_low, h_high = chip_sum(h_keep, late(h_send, fa_first))
    final[0] = (dxq, h_low, h_high, far(h_high), inv)
    pack = jnp.concatenate([att_b, reduce_scatter(aa_keep, late(aa_send, h_high))], axis=0)

    dinput, = call(finish_kernel, None, (), (gains, dealt, *(v for f in final for v in f)), [((length, QUARTER), BF16)],
                   [], "finish", 8, (pack, fb_more_side))
    back_grad = lax.all_to_all(
        dinput.reshape(dp, length // dp, QUARTER), "dp", split_axis=0, concat_axis=0, tiled=True)
    input_grad = pick(back_grad, dealing_slots)

    valid = (jnp.arange(length, dtype=jnp.int32) < my_length)[:, None]
    result = jnp.concatenate([hidden[c][1] + y_low[c] for c in range(CHUNKS)], axis=0)
    result = result + far(late(jnp.concatenate(y_high, axis=0), h_high)).astype(F32)
    result = late(jnp.where(valid, result, 0.0).astype(BF16), dinput)
    back_out = lax.all_to_all(
        result.reshape(dp, length // dp, QUARTER), "dp", split_axis=0, concat_axis=0, tiled=True)
    output = pick(back_out, dealing_slots)

    fa_all = jnp.concatenate([ffn_a, fa_first], axis=0)
    for b in reversed(range(dp.bit_length() - 2)):
        fa_all = doubled(fa_all, 1 << b, dp)
    outs = [sds((adapters, 2 * RANK, WIDTH), F32), sds((adapters, RANK, WIDTH), F32),
            sds((adapters, 2, RANK, units), F32), sds((adapters, RANK, units), F32)]
    ga_ffn, g_down_b, g_ffn_b, g_down_a = sum_call(
        feedforward_sum_kernel, (info, owners), (jnp.concatenate([fb, fb_more, fb_side, fb_more_side], axis=0), *spread(fa_all)), outs,
        "feedforward_sum")

    n_b = att_b.shape[0]
    pack = gather_slots(pack, dp)
    outs = [sds((adapters, 3 * RANK, WIDTH), F32), sds((adapters, RANK, WIDTH), F32),
            sds((adapters, RANK, q_cols), F32), sds((adapters, 2, RANK, kv_cols), F32),
            sds((adapters, RANK, q_cols), F32)]
    ga_att, g_out_b, g_query_b, g_kv_b, g_out_a = sum_call(
        attention_sum_kernel, (info, owners), (pack[:, :n_b], *spread(pack[:, n_b:])), outs, "attention_sum")
    return (output, input_grad, ga_att, g_query_b, g_kv_b, g_out_a, g_out_b, ga_ffn, g_ffn_b, g_down_a, g_down_b)


def solution(mesh):
    in_specs = (
        P(None, "dp", "mp"), P("mp"), P(None, "mp"), P(None, None, "mp"), P("mp", None), P("mp"),
        P(None, None, "mp"), P("mp", None), P(), P(None, None, "mp"), P(None, None, None, "mp"),
        P(None, None, "mp"), P(), P(), P(None, None, None, "mp"), P(None, None, "mp"), P(), P(), P(), P(),
        P("dp", None, "mp"),
    )
    out_specs = (
        P(None, "dp", "mp"), P(None, "dp", "mp"), P(), P(None, None, "mp"), P(None, None, None, "mp"),
        P(None, None, "mp"), P(), P(), P(None, None, None, "mp"), P(None, None, "mp"), P(),
    )
    return jax.shard_map(
        functools.partial(shards, mesh.shape["dp"]), mesh=mesh, in_specs=in_specs, out_specs=out_specs,
        check_vma=False)
```

```python
import functools

import jax
import jax.numpy as jnp
import numpy as np
from jax import lax
from jax.experimental import pallas as pl
from jax.experimental.pallas import tpu as pltpu
from jax.sharding import PartitionSpec as P

WIDTH = 2048
HEAD = 64
HALF = HEAD // 2
RANK = 16
EPS = 1e-05
ROPE_BASE = 500000.0
NEG_FILL = -1e30
PARTS = 4
LANES = 128
ROW_BLOCK = 64
QUARTER = WIDTH // PARTS
CHUNKS = 2
MIB = 1024 * 1024
F32 = jnp.float32
BF16 = jnp.bfloat16


def nn(a, b):
    return lax.dot_general(a, b, (((1,), (0,)), ((), ())), preferred_element_type=F32)


def nt(a, b):
    return lax.dot_general(a, b, (((1,), (1,)), ((), ())), preferred_element_type=F32)


def rope_tables(length):
    freq = ROPE_BASE ** (-np.arange(HALF, dtype=np.float32) * np.float32(2.0 / HEAD))
    angles = (np.arange(length, dtype=np.float32)[None, :] * freq.astype(np.float32)[:, None]).astype(np.float32)
    return np.cos(angles).astype(np.float32), np.sin(angles).astype(np.float32)


def quarter(me, rel):
    return pl.ds(pl.multiple_of((me ^ rel) * QUARTER, QUARTER), QUARTER)


LO, HI = slice(0, QUARTER), slice(QUARTER, 2 * QUARTER)


def total_block(rel, rows_at, own, oth):
    return (own if rel in (0, 2) else oth)[rows_at, LO if rel in (0, 1) else HI].astype(F32)


def store_block(rel, value, rows_at, keep_ref, send_ref):
    to = pl.ds(pl.multiple_of((rel // 2) * QUARTER, QUARTER), QUARTER)

    @pl.when(rel % 2 == 0)
    def _():
        keep_ref[rows_at, to] = value[...]

    @pl.when(rel % 2 == 1)
    def _():
        send_ref[rows_at, to] = value[...].astype(BF16)


def chunk_of(ref, chunk, rows):
    return ref if ref.shape[0] == rows else ref.at[chunk * rows:(chunk + 1) * rows]


def row_block(i):
    return pl.ds(pl.multiple_of(i * ROW_BLOCK, ROW_BLOCK), ROW_BLOCK)


def is_valid(chunk, i, rows, length):
    return chunk * rows + i * ROW_BLOCK + lax.broadcasted_iota(jnp.int32, (ROW_BLOCK, 1), 0) < length


def copies_of(pairs, sems):
    made = [pltpu.make_async_copy(source, target, sems.at[i]) for i, (source, target) in enumerate(pairs)]
    for copy in made:
        copy.start()
    return made


def put_block(rel, value, keep_ref, send_ref):
    ref = keep_ref if rel in (0, 2) else send_ref
    ref[:, LO if rel in (0, 1) else HI] = value.astype(ref.dtype)


def rotate(value, cos, sin, out_ref):
    for i in range(value.shape[0] // HEAD):
        u1, u2 = value[i * HEAD:i * HEAD + HALF], value[i * HEAD + HALF:(i + 1) * HEAD]
        out_ref[i * HEAD:i * HEAD + HALF, :] = (u1 * cos - u2 * sin).astype(BF16)
        out_ref[i * HEAD + HALF:(i + 1) * HEAD, :] = (u2 * cos + u1 * sin).astype(BF16)


def turn_back(value, cos, sin, out_ref):
    for i in range(value.shape[0] // HEAD):
        w1, w2 = value[i * HEAD:i * HEAD + HALF], value[i * HEAD + HALF:(i + 1) * HEAD]
        out_ref[i * HEAD:i * HEAD + HALF, :] = (w1 * cos + w2 * sin).astype(BF16)
        out_ref[i * HEAD + HALF:(i + 1) * HEAD, :] = (w2 * cos - w1 * sin).astype(BF16)


def head_rows(i):
    return pl.ds(pl.multiple_of(i * HEAD, HEAD), HEAD)


def visible(key_start, query_start, rows, length):
    kpos = key_start + lax.broadcasted_iota(jnp.int32, (rows, rows), 0)
    qpos = query_start + lax.broadcasted_iota(jnp.int32, (rows, rows), 1)
    return (kpos <= qpos) & (kpos < length)


def project_kernel(chunk, info, wq_h, wkv_h, x0, x1, x2, x3, gains, a1, qb, kvb, cos_t, sin_t,
                   h_out, t1t_out, qt_out, kn_out, vn_out, kt_out, vt_out, wq, wkv, sems):
    copies = copies_of(((wkv_h, wkv), (wq_h, wq)), sems)
    me = info[0]
    rows = h_out.shape[0]
    kv_heads = kn_out.shape[0]
    xs = [chunk_of(x, chunk, rows) for x in (x0, x1, x2, x3)]

    def norm(i, carry):
        at = row_block(i)
        square = jnp.zeros((ROW_BLOCK, 1), F32)
        for r in range(PARTS):
            v = xs[r][at, :].astype(F32)
            square = square + jnp.sum(v * v, axis=1, keepdims=True)
        inv = lax.rsqrt(square / WIDTH + EPS)
        for r in range(PARTS):
            v = xs[r][at, :].astype(F32)
            h_out[at, quarter(me, r)] = (v * inv * gains[r, 0:1, :].astype(F32)).astype(BF16)
        return carry

    lax.fori_loop(0, rows // ROW_BLOCK, norm, 0)
    h = h_out[...]
    t1 = nt(h, a1[...])
    t1t_out[...] = t1.T.astype(BF16)
    t1b = t1.astype(BF16)
    cos, sin = cos_t[...], sin_t[...]
    copies[0].wait()
    k = nn(h, wkv[0]) + nn(t1b[:, RANK:2 * RANK], kvb[0])
    rotate(k.T, cos, sin, kt_out)
    k_n = kt_out[...].T
    v_n = (nn(h, wkv[1]) + nn(t1b[:, 2 * RANK:], kvb[1])).astype(BF16)
    vt_out[...] = v_n.T
    for i in range(kv_heads):
        kn_out[i] = k_n[:, i * HEAD:(i + 1) * HEAD]
        vn_out[i] = v_n[:, i * HEAD:(i + 1) * HEAD]
    copies[1].wait()
    q = nn(h, wq[...]) + nn(t1b[:, :RANK], qb[...])
    rotate(q.T * (HEAD ** -0.5), cos, sin, qt_out)


def attend_kernel(chunk, info, wo_h, qt, oa, ob, *rest):
    pairs, rest = rest[:2 * (chunk + 1)], rest[2 * (chunk + 1):]
    z_keep, z_send, ot_out, lse_out, tot_out, wo, sems = rest
    copies = copies_of(((wo_h, wo),), sems)
    keys, values = pairs[0::2], pairs[1::2]
    me, length = info[0], info[1]
    rows = qt.shape[1]
    kv_heads = keys[0].shape[0]
    heads = qt.shape[0] // HEAD
    group = heads // kv_heads

    def one_head(i, carry):
        j = i // group
        q_h = qt[head_rows(i), :]
        parts = []
        for c, key in enumerate(keys):
            s = nn(key[j], q_h)
            parts.append(jnp.where(visible(c * rows, chunk * rows, rows, length), s, NEG_FILL))
        top = functools.reduce(jnp.maximum, [jnp.max(s, axis=0, keepdims=True) for s in parts])
        es = [jnp.exp(s - top) for s in parts]
        total = sum(jnp.sum(e, axis=0, keepdims=True) for e in es)
        lse_out[pl.ds(i, 1), :] = top + jnp.log(total)
        o_t = sum(nn(value[head_rows(j), :], e.astype(BF16)) for value, e in zip(values, es))
        ot_out[head_rows(i), :] = (o_t / total).astype(BF16)
        return carry

    lax.fori_loop(0, heads, one_head, 0, unroll=2)
    o = ot_out[...].T
    to = nt(o, oa[...])
    tot_out[...] = to.T.astype(BF16)
    to = to.astype(BF16)
    copies[0].wait()
    for r in range(PARTS):
        at = quarter(me, r)
        put_block(r, nn(o, wo[:, at]) + nn(to, ob[:, at]), z_keep, z_send)


def front_kernel(chunk, last, info, wgu_h, wd_h, x0, x1, x2, x3, zo, zp, g0, g1, g2, g3, gains, a2, bd, fb, da,
                 *rest):
    f_s, wgu, wd, sems = rest[-4:]
    xm_out, xq_out, h_out, g_out, act_out, dg_out, du_out, t2_s, dtd_s, b_out = rest[-14:-4]
    units = wd.shape[0]

    def copies(i):
        c = pl.ds(pl.multiple_of(i * QUARTER, QUARTER), QUARTER)
        return (pltpu.make_async_copy(wgu_h.at[:, :, c], wgu.at[:, :, c], sems.at[0, i]),
                pltpu.make_async_copy(wd_h.at[c, :], wd.at[c, :], sems.at[1, i]))

    for i in range(units // QUARTER):
        for copy in copies(i):
            copy.start()
    me, length = info[0], info[1]
    rows = h_out.shape[0]
    xs, gs = ([chunk_of(v, chunk, rows) for v in vs] for vs in ((x0, x1, x2, x3), (g0, g1, g2, g3)))

    def norm(i, carry):
        at = row_block(i)
        valid = is_valid(chunk, i, rows, length)
        square = jnp.zeros((ROW_BLOCK, 1), F32)
        for r in range(PARTS):
            v = xs[r][at, :].astype(F32) + total_block(r, at, zo, zp)
            if r == 0:
                xq_out[at, :] = v
            f_s[:, quarter(me, r)] = v
            square = square + jnp.sum(v * v, axis=1, keepdims=True)
            g_out[at, quarter(me, r)] = jnp.where(valid, gs[r][at, :], jnp.zeros((), BF16))
        inv = lax.rsqrt(square / WIDTH + EPS)
        for r in range(PARTS):
            v = f_s[:, quarter(me, r)]
            xm_out[at, quarter(me, r)] = v.astype(BF16)
            h_out[at, quarter(me, r)] = (v * inv * gains[r, 1:2, :].astype(F32)).astype(BF16)
        return carry

    lax.fori_loop(0, rows // ROW_BLOCK, norm, 0)
    t2 = nt(h_out[...], a2[...])
    t2_s[...] = t2.astype(BF16)
    dtd = nt(g_out[...], bd[...])
    dtd_s[...] = dtd.astype(BF16)
    t2t, dtdt = t2.T.astype(BF16), dtd.T.astype(BF16)

    def block(i, carry):
        c = pl.ds(pl.multiple_of(i * QUARTER, QUARTER), QUARTER)
        for copy in copies(i):
            copy.wait()
        h, g = h_out[...], g_out[...]
        gate = nn(h, wgu[0, :, c]) + nn(t2_s[:, :RANK], fb[0, :, c])
        up = nn(h, wgu[1, :, c]) + nn(t2_s[:, RANK:], fb[1, :, c])
        dact = nt(g, wd[c, :]) + nn(dtd_s[...], da[:, c])
        sig = 1.0 / (1.0 + jnp.exp(-gate))
        silu = gate * sig
        act = (silu * up).astype(BF16)
        dgate = (dact * up * sig * (1.0 + gate * (1.0 - sig))).astype(BF16)
        dup = (dact * silu).astype(BF16)
        act_out[:, c], dg_out[:, c], du_out[:, c] = act, dgate, dup
        for k, value in enumerate((nn(t2t[:RANK], dgate), nn(t2t[RANK:], dup), nn(dtdt, act))):
            at = pl.ds(pl.multiple_of((3 * i + k) * RANK, RANK), RANK)
            if last:
                value = value + rest[0][at, :]
            b_out[at, :] = value.astype(b_out.dtype)
        return carry

    lax.fori_loop(0, units // QUARTER, block, 0)


def back_kernel(last, info, wgu_h, wd_h, h, g, act, dg, du, a2, bd, fb, da, *rest):
    (value_s, low_s, wgu, wd, sems), rest = rest[-5:], rest[:-5]
    outs, rest = (rest[-4:], rest[:-4]) if last else (rest[-5:], rest[:-5])
    d_keep, d_send, y_keep, y_send = outs[:4]
    me = info[0]
    rows = h.shape[0]
    own = slice(0, rows)

    def copies(r):
        at = quarter(me, r)
        return (pltpu.make_async_copy(wgu_h.at[:, at, :], wgu.at[:, at, :], sems.at[0, r]),
                pltpu.make_async_copy(wd_h.at[:, at], wd.at[:, at], sems.at[1, r]))

    for r in range(PARTS):
        for copy in copies(r):
            copy.start()
    if last:
        y_keep[rows:, :], y_send[rows:, :] = rest[1][...], rest[2][...]
    dt2 = jnp.concatenate([nt(dg[...], fb[0]), nt(du[...], fb[1])], axis=1)
    dt2b = dt2.astype(BF16)
    td = nt(act[...], da[...])
    tdb = td.astype(BF16)
    dt2t, tdt = dt2.T.astype(BF16), td.T.astype(BF16)

    def block(r, carry):
        at = quarter(me, r)
        for copy in copies(r):
            copy.wait()
        value_s[...] = nt(dg[...], wgu[0, at, :]) + nt(du[...], wgu[1, at, :]) + nn(dt2b, a2[:, at])
        store_block(r, value_s, own, d_keep, d_send)
        value_s[...] = nn(act[...], wd[:, at]) + nn(tdb, bd[:, at])
        store_block(r, value_s, own, y_keep, y_send)
        low_s[:2 * RANK, :] = nn(dt2t, h[:, at])
        low_s[2 * RANK:, :] = nn(tdt, g[:, at])
        if last:
            low_s[...] += rest[0][:, at]
            store_block(r, low_s, slice(rows, rows + 3 * RANK), d_keep, d_send)
        else:
            outs[4][:, at] = low_s[...]
        return carry

    lax.fori_loop(0, PARTS, block, 0)


def attend_back_kernel(chunk, last, info, wq_h, wkv_h, wo_h, x0, x1, x2, x3, g0, g1, g2, g3, xm, do_, dp, gains, a1,
                       qb, kvb, oa, ob, cos_t, sin_t, h_in, t1t, qt, ot, lse, tot, *rest):
    scratch, rest = rest[-13:], rest[:-13]
    z_s, f_s, dot_s, dqt_s, dkt_s, dvt_s, dq_s, value_s, low_s, wq, wkv, wo, sems = scratch
    copies = copies_of(((wo_h, wo), (wq_h, wq), (wkv_h, wkv)), sems)
    n_out = 5 if last else 8
    outs, rest = rest[-n_out:], rest[:-n_out]
    dxq_out, h_keep, h_send, inv_out, b_out = outs[:5]
    triples, rest = rest[:3 * (chunk + 1)], rest[3 * (chunk + 1):]
    keys, values, keys_t = triples[0::3], triples[1::3], triples[2::3]
    me, length = info[0], info[1]
    rows = xm.shape[0]
    kv_heads = keys[0].shape[0]
    heads = qt.shape[0] // HEAD
    group = heads // kv_heads
    q_cols, kv_cols = heads * HEAD, kv_heads * HEAD
    xs, gs = ([chunk_of(v, chunk, rows) for v in vs] for vs in ((x0, x1, x2, x3), (g0, g1, g2, g3)))

    def norm_back(i, carry):
        at = row_block(i)
        valid = is_valid(chunk, i, rows, length)
        square, first, inner = (jnp.zeros((ROW_BLOCK, 1), F32) for _ in range(3))
        for r in range(PARTS):
            v = xm[at, quarter(me, r)].astype(F32)
            square = square + jnp.sum(v * v, axis=1, keepdims=True)
            w = total_block(r, at, do_, dp) * gains[r, 1:2, :].astype(F32)
            f_s[:, quarter(me, r)] = w
            inner = inner + jnp.sum(v * w, axis=1, keepdims=True)
            u = xs[r][at, :].astype(F32)
            first = first + jnp.sum(u * u, axis=1, keepdims=True)
        inv_out[at, :] = lax.rsqrt(first / WIDTH + EPS)
        inv = lax.rsqrt(square / WIDTH + EPS)
        back = inv * inv * inv * inner / WIDTH
        for r in range(PARTS):
            v = xm[at, quarter(me, r)].astype(F32)
            g = jnp.where(valid, gs[r][at, :].astype(F32), 0.0)
            d = g + inv * f_s[:, quarter(me, r)] - v * back
            if r == 0:
                dxq_out[at, :] = d
            z_s[at, quarter(me, r)] = d.astype(BF16)
        return carry

    lax.fori_loop(0, rows // ROW_BLOCK, norm_back, 0)
    dz = z_s[...]
    dto = nt(dz, ob[...])
    copies[0].wait()
    d_o = nt(dz, wo[...]) + nn(dto.astype(BF16), oa[...])
    dot_s[...] = d_o.T.astype(BF16)
    if last:
        for c in range(chunk + 1):
            dkt_s[c], dvt_s[c] = rest[2][...], rest[3][...]
    else:
        dkt_s[...] = jnp.zeros_like(dkt_s)
        dvt_s[...] = jnp.zeros_like(dvt_s)

    def one_head(i, carry):
        j = i // group
        q_h, do_h = qt[head_rows(i), :], dot_s[head_rows(i), :]
        dots = jnp.sum(do_h.astype(F32) * ot[head_rows(i), :].astype(F32), axis=0, keepdims=True)
        low = lse[pl.ds(i, 1), :]
        dq_h = jnp.zeros((HEAD, rows), F32)
        for c in range(chunk + 1):
            prob = jnp.exp(nn(keys[c][j], q_h) - low)
            prob = jnp.where(visible(c * rows, chunk * rows, rows, length), prob, 0.0)
            ds = (prob * (nn(values[c][j], do_h) - dots)).astype(BF16)
            dq_h = dq_h + nn(keys_t[c][head_rows(j), :], ds)
            dkt_s[c, head_rows(j), :] += nt(q_h, ds)
            dvt_s[c, head_rows(j), :] += nt(do_h, prob.astype(BF16))
        dqt_s[head_rows(i), :] = dq_h
        return carry

    lax.fori_loop(0, heads, one_head, 0, unroll=2)
    if not last:
        outs[6][...], outs[7][...] = dkt_s[0], dvt_s[0]
    cos, sin = cos_t[...], sin_t[...]
    dto_t, o_t = dto.T.astype(BF16), ot[...]
    d_out_a = nt(dto_t, o_t)
    turn_back(dqt_s[...], cos * (HEAD ** -0.5), sin * (HEAD ** -0.5), dot_s)
    dq_s[:, :q_cols] = dot_s[...].T
    turn_back(dkt_s[chunk], cos, sin, dot_s)
    dq_s[:, q_cols:q_cols + kv_cols] = dot_s[:kv_cols, :].T
    dq_s[:, q_cols + kv_cols:] = dvt_s[chunk].T.astype(BF16)
    dq, dk, dv = dq_s[:, :q_cols], dq_s[:, q_cols:q_cols + kv_cols], dq_s[:, q_cols + kv_cols:]
    dt1 = jnp.concatenate([nt(dq, qb[...]), nt(dk, kvb[0]), nt(dv, kvb[1])], axis=1)
    dt1b = dt1.astype(BF16)
    kv_pad = jnp.zeros((RANK, QUARTER - 2 * kv_cols), F32)
    d_kv = jnp.concatenate([nn(t1t[RANK:2 * RANK, :], dk), nn(t1t[2 * RANK:, :], dv), kv_pad], axis=1)
    for k, value in enumerate((nn(t1t[:RANK, :], dq), d_out_a, d_kv)):
        at = slice(k * RANK, (k + 1) * RANK)
        if last:
            value = value + rest[0][at, :]
        b_out[at, :] = value.astype(b_out.dtype)
    dt1t = dt1.T.astype(BF16)
    copies[1].wait()
    copies[2].wait()

    def block(r, inner):
        at = quarter(me, r)
        d = nt(dq_s[:, :q_cols], wq[at, :]) + nn(dt1b, a1[:, at])
        d = d + nt(dq_s[:, q_cols:q_cols + kv_cols], wkv[0, at, :]) + nt(dq_s[:, q_cols + kv_cols:], wkv[1, at, :])
        value_s[...] = d
        store_block(r, value_s, slice(0, rows), h_keep, h_send)
        low_s[:3 * RANK, :] = nn(dt1t, h_in[:, at])
        low_s[3 * RANK:, :] = nn(tot[...], z_s[:, at])
        if last:
            low_s[...] += rest[1][:, at]
            store_block(r, low_s, slice(rows, rows + 4 * RANK), h_keep, h_send)
        else:
            outs[5][:, at] = low_s[...]
        return inner + jnp.sum(d * h_in[:, at].astype(F32), axis=1, keepdims=True)

    inner = lax.fori_loop(0, PARTS, block, jnp.zeros((rows, 1), F32))
    for ref in (h_keep, h_send):
        ref[:rows, 2 * QUARTER:] = jnp.broadcast_to(inner, (rows, LANES)).astype(ref.dtype)
        if last:
            ref[rows:, 2 * QUARTER:] = jnp.zeros((4 * RANK, LANES), ref.dtype)


def finish_kernel(gains, x_all, *refs):
    out = refs[-1]
    gain = gains[0, 0:1, :].astype(F32)
    rows = out.shape[0] // CHUNKS
    for c in range(CHUNKS):
        dx, low, high, got, inv = refs[5 * c:5 * (c + 1)]
        x = chunk_of(x_all, c, rows)
        inv = inv[...]
        inner = high[:rows, QUARTER:QUARTER + 1].astype(F32) + got[:rows, QUARTER:QUARTER + 1].astype(F32)
        scale = inv * inv * inner / WIDTH
        grad = inv * (gain * (low[:rows, :] + got[:rows, :QUARTER].astype(F32))) - x[...].astype(F32) * scale
        out[c * rows:(c + 1) * rows, :] = (dx[...] + grad).astype(BF16)


def split_refs(refs, counts):
    groups = []
    for count in counts:
        groups.append(refs[:count])
        refs = refs[count:]
    return groups, refs


def with_entry(parts, at, use):
    start = 0
    for ref in parts:
        @pl.when((at >= start) & (at < start + ref.shape[0]))
        def _(ref=ref, start=start):
            use(ref, at - start)
        start += ref.shape[0]


def sum_slots(info, owners, out_refs, one_slot):
    count = out_refs[0].shape[0]
    base = pl.program_id(0) * count
    slots = owners.shape[0]
    for ref in out_refs:
        ref[...] = jnp.zeros_like(ref)

    def add(slot, carry):
        owner = owners[slot] - base

        @pl.when((owner >= 0) & (owner < count))
        def _():
            one_slot(owner, entry_of(slot, info[3], slots))
        return carry

    lax.fori_loop(0, slots, add, 0)


def feedforward_sum_kernel(counts, info, owners, *refs):
    (b_parts, *a_parts), outs = split_refs(refs, counts)
    ga, gdb, gb, gda = outs
    me = info[0]

    def one_slot(owner, at):
        def add_b(ref, e):
            for i in range(gda.shape[2] // QUARTER):
                cols = slice(i * QUARTER, (i + 1) * QUARTER)
                base = i * 3 * RANK
                gb[owner, 0, :, cols] += ref[e, base:base + RANK, :].astype(F32)
                gb[owner, 1, :, cols] += ref[e, base + RANK:base + 2 * RANK, :].astype(F32)
                gda[owner, :, cols] += ref[e, base + 2 * RANK:base + 3 * RANK, :].astype(F32)

        with_entry(b_parts, at, add_b)
        for r, parts in enumerate(a_parts):
            def add_a(ref, e, r=r):
                ga[owner, :, quarter(me, r)] += ref[e, :2 * RANK, :].astype(F32)
                gdb[owner, :, quarter(me, r)] += ref[e, 2 * RANK:, :].astype(F32)

            with_entry(parts, at, add_a)

    sum_slots(info, owners, outs, one_slot)


def attention_sum_kernel(counts, info, owners, *refs):
    (b_parts, *a_parts), outs = split_refs(refs, counts)
    ga, gob, gq, gkv, goa = outs
    me = info[0]
    kv_cols = gkv.shape[3]

    def one_slot(owner, at):
        def add_b(ref, e):
            gq[owner] += ref[e, :RANK, :].astype(F32)
            goa[owner] += ref[e, RANK:2 * RANK, :].astype(F32)
            gkv[owner, 0] += ref[e, 2 * RANK:3 * RANK, :kv_cols].astype(F32)
            gkv[owner, 1] += ref[e, 2 * RANK:3 * RANK, kv_cols:2 * kv_cols].astype(F32)

        with_entry(b_parts, at, add_b)
        for r, parts in enumerate(a_parts):
            def add_a(ref, e, r=r):
                ga[owner, :, quarter(me, r)] += ref[e, :3 * RANK, :].astype(F32)
                gob[owner, :, quarter(me, r)] += ref[e, 3 * RANK:, :].astype(F32)

            with_entry(parts, at, add_a)

    sum_slots(info, owners, outs, one_slot)


def deal_kernel(slots, source, out, sems):
    made = [pltpu.make_async_copy(source.at[i], out.at[slots[i]], sems.at[i]) for i in range(source.shape[0])]
    for copy in made:
        copy.start()
    for copy in made:
        copy.wait()


def collect_kernel(slots, source, out, sems):
    made = [pltpu.make_async_copy(source.at[slots[i]], out.at[i], sems.at[i]) for i in range(source.shape[0])]
    for copy in made:
        copy.start()
    for copy in made:
        copy.wait()


def move_rows(kernel, value, slots, name):
    return pl.pallas_call(
        kernel,
        in_specs=[pl.BlockSpec(memory_space=pltpu.SMEM), pl.BlockSpec(memory_space=pl.ANY)],
        out_specs=pl.BlockSpec(memory_space=pl.ANY),
        out_shape=jax.ShapeDtypeStruct(value.shape, value.dtype),
        scratch_shapes=[pltpu.SemaphoreType.DMA((value.shape[0],))],
        compiler_params=pltpu.CompilerParams(vmem_limit_bytes=MIB),
        cost_estimate=pl.CostEstimate(flops=1000, transcendentals=0, bytes_accessed=1000),
        name=name,
    )(slots, value)


def sds(shape, dtype):
    return jax.ShapeDtypeStruct(tuple(shape), dtype)


def in_vmem(value):
    return pltpu.with_memory_space_constraint(value, pltpu.VMEM)


def in_hbm(value):
    return pltpu.with_memory_space_constraint(value, pltpu.HBM)


def call(kernel, info, weights, args, outs, scratch, name, mib, after=(), sems=()):
    vmem = pl.BlockSpec(memory_space=pltpu.VMEM)
    scalars = () if info is None else (info,)
    n, w = len(scalars), len(weights)

    def body(*refs):
        at = n + w + len(args)
        kernel(*refs[:at], *refs[at + len(after):])

    return pl.pallas_call(
        body,
        in_specs=[pl.BlockSpec(memory_space=pltpu.SMEM)] * n + [pl.BlockSpec(memory_space=pltpu.HBM)] * w + [vmem] * len(args)
        + [pl.BlockSpec(memory_space=pl.ANY)] * len(after),
        out_specs=[vmem] * len(outs),
        out_shape=[pltpu.VMEM(tuple(s), d) for s, d in outs],
        scratch_shapes=[pltpu.VMEM(s, d) for s, d in scratch] + ([pltpu.SemaphoreType.DMA(sems)] if sems else []),
        compiler_params=pltpu.CompilerParams(vmem_limit_bytes=mib * MIB),
        cost_estimate=pl.CostEstimate(flops=1000, transcendentals=0, bytes_accessed=1000),
        name=name,
    )(*scalars, *(in_hbm(a) for a in weights), *(in_vmem(a) for a in args), *after)


def sum_call(kernel, scalars, groups, outs, name):
    args = [v for group in groups for v in group]
    steps = 2
    specs = [pl.BlockSpec((o.shape[0] // steps,) + o.shape[1:], (lambda n: lambda i, *_: (i,) + (0,) * n)(o.ndim - 1))
             for o in outs]
    return pl.pallas_call(
        functools.partial(kernel, [len(group) for group in groups]),
        grid_spec=pltpu.PrefetchScalarGridSpec(
            num_scalar_prefetch=len(scalars), grid=(steps,),
            in_specs=[pl.BlockSpec(memory_space=pltpu.VMEM)] * len(args), out_specs=specs),
        out_shape=outs,
        compiler_params=pltpu.CompilerParams(
            dimension_semantics=("arbitrary",),
            vmem_limit_bytes=4 * MIB + sum(a.size * a.dtype.itemsize for a in args)
            + sum(o.size * o.dtype.itemsize for o in outs)),
        cost_estimate=pl.CostEstimate(flops=0, transcendentals=0, bytes_accessed=12000000),
        name=name,
    )(*scalars, *(in_vmem(a) for a in args))


def swap(value, bit, axis, size):
    return lax.ppermute(value, axis, [(i, i ^ bit) for i in range(size)])


def near(value):
    return swap(value, 1, "mp", PARTS)


def far(value):
    return swap(value, 2, "mp", PARTS)


def spread(value):
    there = far(value)
    return (value, near(value), there, near(there))


def chip_sum(keep, send):
    got = near(send)
    lo = keep[:, :QUARTER].astype(F32) + got[:, :QUARTER].astype(F32)
    hi = keep[:, QUARTER:].astype(F32) + got[:, QUARTER:].astype(F32)
    return lo, hi.astype(BF16)


def far_sum_kernel(own, got, out):
    for to, other in ((LO, HI), (HI, LO)):
        out[:, to] = (own[:, to].astype(F32) + got[:, other].astype(F32)).astype(BF16)


def far_sum(own, got):
    return call(far_sum_kernel, None, (), (own, got), [(own.shape, BF16)], [], "far_sum", 6)[0]


def pair_sum_kernel(keep, got, out):
    out[...] = (keep[...] + got[...].astype(F32)).astype(BF16)


def pair_sum(keep, send):
    return call(pair_sum_kernel, None, (), (keep, near(send)), [(send.shape, BF16)], [], "pair_sum", 6)[0]


def late(value, *others):
    return lax.optimization_barrier((value, *others))[0]


def doubled(stack, bit, size):
    return jnp.concatenate([stack, swap(stack, bit, "dp", size)], axis=0)


def entry_of(slot, place, size):
    bits = size.bit_length() - 1
    apart = slot ^ place
    return sum(((apart >> b) & 1) << (bits - 1 - b) for b in range(bits))


def shards(dp, residual, attention_gain, query_matrix, key_value_matrix, output_matrix, feedfwd_gain,
           gate_up_matrix, down_matrix, attention_adapter_input, query_adapter_output,
           key_value_adapter_output, output_adapter_input, output_adapter_output, feedfwd_adapter_input,
           feedfwd_adapter_output, down_adapter_input, down_adapter_output, lengths, adapter_index,
           dealing_slots, cotangent):
    seqs = residual.shape[0]
    length = cotangent.shape[1]
    units = down_matrix.shape[0]
    adapters = attention_adapter_input.shape[0]
    q_cols = query_matrix.shape[1]
    kv_cols = key_value_matrix.shape[2]
    kv_heads = kv_cols // HEAD
    heads = q_cols // HEAD
    rows = length // CHUNKS
    half = 2 * QUARTER
    me = lax.axis_index("mp")
    place = lax.axis_index("dp")

    is_there = dealing_slots[None, :] == jnp.arange(seqs, dtype=jnp.int32)[:, None]
    owners = jnp.sum(jnp.where(is_there, adapter_index[None, :], 0), axis=1)
    spans = jnp.sum(jnp.where(is_there, lengths[None, :], 0), axis=1)
    mine = jnp.arange(seqs, dtype=jnp.int32) == place
    my_length = jnp.sum(jnp.where(mine, spans, 0))
    my_adapter = jnp.sum(jnp.where(mine, owners, 0))
    info = jnp.stack([me.astype(jnp.int32), my_length, my_adapter, place.astype(jnp.int32)])

    gs = spread(cotangent[0])
    gains = jnp.stack(spread(jnp.stack([attention_gain, feedfwd_gain])))
    dealt = lax.all_to_all(
        move_rows(deal_kernel, residual, dealing_slots, "deal"), "dp", split_axis=0, concat_axis=1, tiled=True
    )[0]
    dealt = late(dealt, gs[2])
    beside = near(dealt)
    there = [far(dealt[c * rows:(c + 1) * rows]) for c in range(CHUNKS)]
    xs = [None] * CHUNKS
    cos_np, sin_np = rope_tables(length)
    cos = [jnp.asarray(cos_np[:, c * rows:(c + 1) * rows]) for c in range(CHUNKS)]
    sin = [jnp.asarray(sin_np[:, c * rows:(c + 1) * rows]) for c in range(CHUNKS)]
    a1, qb, kvb, oa, ob, a2, fba, da, bd = (
        lax.dynamic_index_in_dim(v, my_adapter, 0, keepdims=False) for v in (
            attention_adapter_input, query_adapter_output, key_value_adapter_output, output_adapter_input,
            output_adapter_output, feedfwd_adapter_input, feedfwd_adapter_output, down_adapter_input,
            down_adapter_output))
    wq, wkv, wo, wgu, wd = query_matrix, key_value_matrix, output_matrix, gate_up_matrix, down_matrix

    def like(*arrays):
        return [(a.shape, a.dtype) for a in arrays]

    wide, col, block, thin = (rows, WIDTH), (rows, half), (rows, QUARTER), (rows, 1)
    saved = [None] * CHUNKS
    order = ()
    for c in range(CHUNKS):
        xs[c] = (dealt, beside, there[c], near(late(there[c], *order)))
        outs = [(wide, BF16), ((3 * RANK, rows), BF16), ((q_cols, rows), BF16), ((kv_heads, rows, HEAD), BF16),
                ((kv_heads, rows, HEAD), BF16), ((kv_cols, rows), BF16), ((kv_cols, rows), BF16)]
        saved[c] = call(
            functools.partial(project_kernel, c), info, (wq, wkv), (*xs[c], gains, a1, qb, kvb, cos[c], sin[c]), outs,
            like(wq, wkv), "project_%d" % c, 12, order, (2,))
        order = (saved[c][1],)

    kept, z_own = [None] * CHUNKS, [None] * CHUNKS
    for c in reversed(range(CHUNKS)):
        outs = [(col, F32), (col, BF16), ((q_cols, rows), BF16), ((heads, rows), F32), ((RANK, rows), BF16)]
        pairs = [v for p in saved[:c + 1] for v in (p[3], p[6])]
        z_keep, z_send, *kept[c] = call(
            functools.partial(attend_kernel, c), info, (wo,), (saved[c][2], oa, ob, *pairs), outs, like(wo),
            "attend_%d" % c, 10, order, (1,))
        z_own[c] = pair_sum(z_keep, z_send)
        order = (kept[c][1], z_own[1])
    z_far = [far(v) for v in z_own]

    def front(c, total, partial, order):
        hidden = (rows, units)
        outs = [(wide, BF16), (block, F32), (wide, BF16), (wide, BF16), (hidden, BF16), (hidden, BF16), (hidden, BF16),
                ((rows, 2 * RANK), BF16), ((rows, RANK), BF16),
                ((3 * RANK * units // QUARTER, QUARTER), F32 if c else BF16)]
        return call(
            functools.partial(front_kernel, c, c == 0), info, (wgu, wd),
            (*xs[c], total, near(total), *gs, gains, a2, bd, fba, da, *partial), outs,
            [((ROW_BLOCK, WIDTH), F32)] + like(wgu, wd),
            "front_%d" % c, 34, order, (2, units // QUARTER))

    def back(c, hidden, partial, order):
        first, second = (col, col) if c else ((rows + 3 * RANK, half), (length, half))
        outs = [(first, F32), (first, BF16), (second, F32), (second, BF16)]
        outs += [((3 * RANK, WIDTH), F32)] if c else []
        return call(
            functools.partial(back_kernel, c == 0), info, (wgu, wd), (*hidden[2:7], a2, bd, fba, da, *partial), outs,
            [(block, F32), ((3 * RANK, QUARTER), F32)] + like(wgu, wd), "back_%d" % c, 32, order, (2, PARTS))

    def attend_back(c, total, partial, order):
        padded = (rows if c else rows + 4 * RANK, half + LANES)
        outs = [(block, F32), (padded, F32), (padded, BF16), (thin, F32), ((3 * RANK, QUARTER), F32 if c else BF16)]
        outs += [((4 * RANK, WIDTH), F32), ((kv_cols, rows), F32), ((kv_cols, rows), F32)] if c else []
        scratch = [(wide, BF16), ((ROW_BLOCK, WIDTH), F32), ((q_cols, rows), BF16), ((q_cols, rows), F32),
                   ((c + 1, kv_cols, rows), F32), ((c + 1, kv_cols, rows), F32), ((rows, q_cols + 2 * kv_cols), BF16),
                   (block, F32), ((4 * RANK, QUARTER), F32)]
        triples = [v for p in saved[:c + 1] for v in (p[3], p[4], p[5])]
        return call(
            functools.partial(attend_back_kernel, c, c == 0), info, (wq, wkv, wo),
            (*xs[c], *gs, hidden[c][0], total, near(total), gains, a1, qb, kvb, oa, ob, cos[c], sin[c], *saved[c][:3],
             *kept[c], *triples, *partial), outs, scratch + like(wq, wkv, wo), "attend_back_%d" % c, 18, order, (3,))

    bits = [1 << b for b in reversed(range(dp.bit_length() - 1))]
    hidden, d_own, d_far = ([None] * CHUNKS for _ in range(3))
    hidden[1] = front(1, far_sum(z_own[1], z_far[1]), (), order)
    step = hidden[1][8]
    total = far_sum(z_own[0], late(z_far[0], step))
    d_keep, d_send, y_keep, y_send, fa = back(1, hidden[1], (), (step, total))
    d_own[1] = pair_sum(d_keep, d_send)
    d_far[1] = far(d_own[1])
    hidden[0] = front(0, total, hidden[1][9:], (d_own[1],))
    step = hidden[0][8]
    total = far_sum(d_own[1], late(d_far[1], step))
    fb = hidden[0][9][None]
    fb_first = swap(fb, bits[0], "dp", dp)
    d_keep, d_send, y_keep, y_send = back(0, hidden[0], (fa, y_keep, y_send), (step, total))
    d_own[0] = pair_sum(d_keep, late(d_send, fb_first))
    d_far[0] = far(d_own[0])
    fb = fb_more = jnp.concatenate([fb, fb_first], axis=0)
    for bit in bits[1:-1]:
        fb_more = doubled(fb_more, bit, dp)
    fb_more = fb_more[2:]
    fb_side = swap(fb, bits[-1], "dp", dp)
    dxq, h_keep, h_send, inv, *sums = attend_back(1, total, (), (d_own[0],))
    total = far_sum(d_own[0], late(d_far[0], inv))
    h_low, h_high = chip_sum(h_keep, late(h_send, fb_more, fb_side))
    h_far = far(h_high)
    final = [None, (dxq, h_low, h_high, h_far, inv)]
    y_send = late(y_send, inv)
    fa = total[rows:, :QUARTER][None]
    fa_first = swap(fa, bits[0], "dp", dp)
    fb_more_side = swap(fb_more, bits[-1], "dp", dp)
    dxq, h_keep, h_send, inv, att_b = attend_back(0, total, sums, (h_high,))
    h_low, h_high = chip_sum(h_keep, late(h_send, fa_first, fb_more_side, h_far))
    h_far = far(h_high)
    final[0] = (dxq, h_low, h_high, h_far, inv)
    att_a = (h_low[rows:] + h_far[rows:, :QUARTER].astype(F32)).astype(BF16)
    att = jnp.concatenate([att_b, att_a], axis=0)[None]

    dinput, = call(finish_kernel, None, (), (gains, dealt, *(v for f in final for v in f)), [((length, QUARTER), BF16)],
                   [], "finish", 8)
    back_grad = lax.all_to_all(
        dinput.reshape(dp, length // dp, QUARTER), "dp", split_axis=0, concat_axis=0, tiled=True)
    input_grad = move_rows(collect_kernel, back_grad, dealing_slots, "collect_grad")

    valid = (jnp.arange(length, dtype=jnp.int32) < my_length)[:, None]
    y_low, y_high = chip_sum(y_keep, y_send)
    result = jnp.concatenate([h[1] for h in hidden], axis=0) + y_low + far(late(y_high, h_high)).astype(F32)
    result = late(jnp.where(valid, result, 0.0).astype(BF16), dinput)
    back_out = lax.all_to_all(
        result.reshape(dp, length // dp, QUARTER), "dp", split_axis=0, concat_axis=0, tiled=True)
    output = move_rows(collect_kernel, back_out, dealing_slots, "collect_out")

    n_b = att_b.shape[0]
    for bit in bits[:-1]:
        att = doubled(att, bit, dp)
    att_side = swap(att, bits[-1], "dp", dp)
    a_parts = [att[:, n_b:], att_side[:, n_b:]]
    a_far = [far(v) for v in a_parts]
    outs = [sds((adapters, 3 * RANK, WIDTH), F32), sds((adapters, RANK, WIDTH), F32),
            sds((adapters, RANK, q_cols), F32), sds((adapters, 2, RANK, kv_cols), F32),
            sds((adapters, RANK, q_cols), F32)]
    ga_att, g_out_b, g_query_b, g_kv_b, g_out_a = sum_call(
        attention_sum_kernel, (info, owners),
        ((att, att_side), a_parts, [near(v) for v in a_parts], a_far, [near(v) for v in a_far]), outs, "attention_sum")

    fa = late(jnp.concatenate([fa, fa_first], axis=0), h_high)
    for bit in bits[1:]:
        fa = doubled(fa, bit, dp)
    outs = [sds((adapters, 2 * RANK, WIDTH), F32), sds((adapters, RANK, WIDTH), F32),
            sds((adapters, 2, RANK, units), F32), sds((adapters, RANK, units), F32)]
    ga_ffn, g_down_b, g_ffn_b, g_down_a = sum_call(
        feedforward_sum_kernel, (info, owners), ((fb, fb_more, fb_side, fb_more_side), *([v] for v in spread(fa))), outs,
        "feedforward_sum")
    return (output, input_grad, ga_att, g_query_b, g_kv_b, g_out_a, g_out_b, ga_ffn, g_ffn_b, g_down_a, g_down_b)


def solution(mesh):
    in_specs = (
        P(None, "dp", "mp"), P("mp"), P(None, "mp"), P(None, None, "mp"), P("mp", None), P("mp"),
        P(None, None, "mp"), P("mp", None), P(), P(None, None, "mp"), P(None, None, None, "mp"),
        P(None, None, "mp"), P(), P(), P(None, None, None, "mp"), P(None, None, "mp"), P(), P(), P(), P(),
        P("dp", None, "mp"),
    )
    out_specs = (
        P(None, "dp", "mp"), P(None, "dp", "mp"), P(), P(None, None, "mp"), P(None, None, None, "mp"),
        P(None, None, "mp"), P(), P(), P(None, None, None, "mp"), P(None, None, "mp"), P(),
    )
    return jax.shard_map(
        functools.partial(shards, mesh.shape["dp"]), mesh=mesh, in_specs=in_specs, out_specs=out_specs,
        check_vma=False)
```

```python
import functools

import jax
import jax.numpy as jnp
import numpy as np
from jax import lax
from jax.experimental import pallas as pl
from jax.experimental.pallas import tpu as pltpu
from jax.sharding import PartitionSpec as P

WIDTH = 2048
HEAD = 64
HALF = HEAD // 2
RANK = 16
EPS = 1e-05
ROPE_BASE = 500000.0
NEG_FILL = -1e30
PARTS = 4
LANES = 128
ROW_BLOCK = 64
QUARTER = WIDTH // PARTS
CHUNKS = 2
MIB = 1024 * 1024
F32 = jnp.float32
BF16 = jnp.bfloat16


def nn(a, b):
    return lax.dot_general(a, b, (((1,), (0,)), ((), ())), preferred_element_type=F32)


def nt(a, b):
    return lax.dot_general(a, b, (((1,), (1,)), ((), ())), preferred_element_type=F32)


def rope_tables(length):
    freq = ROPE_BASE ** (-np.arange(HALF, dtype=np.float32) * np.float32(2.0 / HEAD))
    angles = (np.arange(length, dtype=np.float32)[None, :] * freq.astype(np.float32)[:, None]).astype(np.float32)
    return np.cos(angles).astype(np.float32), np.sin(angles).astype(np.float32)


def quarter(me, rel):
    return pl.ds(pl.multiple_of((me ^ rel) * QUARTER, QUARTER), QUARTER)


LO, HI = slice(0, QUARTER), slice(QUARTER, 2 * QUARTER)


def total_block(rel, rows_at, own, oth):
    return (own if rel in (0, 2) else oth)[rows_at, LO if rel in (0, 1) else HI].astype(F32)


def store_block(rel, value, rows_at, keep_ref, send_ref):
    to = pl.ds(pl.multiple_of((rel // 2) * QUARTER, QUARTER), QUARTER)

    @pl.when(rel % 2 == 0)
    def _():
        keep_ref[rows_at, to] = value[...]

    @pl.when(rel % 2 == 1)
    def _():
        send_ref[rows_at, to] = value[...].astype(BF16)


def chunk_of(ref, chunk, rows):
    return ref if ref.shape[0] == rows else ref.at[chunk * rows:(chunk + 1) * rows]


def row_block(i):
    return pl.ds(pl.multiple_of(i * ROW_BLOCK, ROW_BLOCK), ROW_BLOCK)


def is_valid(chunk, i, rows, length):
    return chunk * rows + i * ROW_BLOCK + lax.broadcasted_iota(jnp.int32, (ROW_BLOCK, 1), 0) < length


def copies_of(pairs, sems):
    made = [pltpu.make_async_copy(source, target, sems.at[i]) for i, (source, target) in enumerate(pairs)]
    for copy in made:
        copy.start()
    return made


def put_block(rel, value, keep_ref, send_ref):
    ref = keep_ref if rel in (0, 2) else send_ref
    ref[:, LO if rel in (0, 1) else HI] = value.astype(ref.dtype)


def rotate(value, cos, sin, out_ref):
    for i in range(value.shape[0] // HEAD):
        u1, u2 = value[i * HEAD:i * HEAD + HALF], value[i * HEAD + HALF:(i + 1) * HEAD]
        out_ref[i * HEAD:i * HEAD + HALF, :] = (u1 * cos - u2 * sin).astype(BF16)
        out_ref[i * HEAD + HALF:(i + 1) * HEAD, :] = (u2 * cos + u1 * sin).astype(BF16)


def turn_back(value, cos, sin, out_ref):
    for i in range(value.shape[0] // HEAD):
        w1, w2 = value[i * HEAD:i * HEAD + HALF], value[i * HEAD + HALF:(i + 1) * HEAD]
        out_ref[i * HEAD:i * HEAD + HALF, :] = (w1 * cos + w2 * sin).astype(BF16)
        out_ref[i * HEAD + HALF:(i + 1) * HEAD, :] = (w2 * cos - w1 * sin).astype(BF16)


def head_rows(i):
    return pl.ds(pl.multiple_of(i * HEAD, HEAD), HEAD)


def visible(key_start, query_start, rows, length):
    kpos = key_start + lax.broadcasted_iota(jnp.int32, (rows, rows), 0)
    qpos = query_start + lax.broadcasted_iota(jnp.int32, (rows, rows), 1)
    return (kpos <= qpos) & (kpos < length)


def project_kernel(chunk, info, wq_h, wkv_h, x0, x1, x2, x3, gains, a1, qb, kvb, cos_t, sin_t,
                   h_out, t1t_out, qt_out, kn_out, vn_out, kt_out, vt_out, wq, wkv, sems):
    copies = copies_of(((wkv_h, wkv), (wq_h, wq)), sems)
    me = info[0]
    rows = h_out.shape[0]
    kv_heads = kn_out.shape[0]
    xs = [chunk_of(x, chunk, rows) for x in (x0, x1, x2, x3)]

    def norm(i, carry):
        at = row_block(i)
        square = jnp.zeros((ROW_BLOCK, 1), F32)
        for r in range(PARTS):
            v = xs[r][at, :].astype(F32)
            square = square + jnp.sum(v * v, axis=1, keepdims=True)
        inv = lax.rsqrt(square / WIDTH + EPS)
        for r in range(PARTS):
            v = xs[r][at, :].astype(F32)
            h_out[at, quarter(me, r)] = (v * inv * gains[r, 0:1, :].astype(F32)).astype(BF16)
        return carry

    lax.fori_loop(0, rows // ROW_BLOCK, norm, 0)
    h = h_out[...]
    t1 = nt(h, a1[...])
    t1t_out[...] = t1.T.astype(BF16)
    t1b = t1.astype(BF16)
    cos, sin = cos_t[...], sin_t[...]
    copies[0].wait()
    k = nn(h, wkv[0]) + nn(t1b[:, RANK:2 * RANK], kvb[0])
    rotate(k.T, cos, sin, kt_out)
    k_n = kt_out[...].T
    v_n = (nn(h, wkv[1]) + nn(t1b[:, 2 * RANK:], kvb[1])).astype(BF16)
    vt_out[...] = v_n.T
    for i in range(kv_heads):
        kn_out[i] = k_n[:, i * HEAD:(i + 1) * HEAD]
        vn_out[i] = v_n[:, i * HEAD:(i + 1) * HEAD]
    copies[1].wait()
    q = nn(h, wq[...]) + nn(t1b[:, :RANK], qb[...])
    rotate(q.T * (HEAD ** -0.5), cos, sin, qt_out)


def attend_kernel(chunk, info, wo_h, qt, oa, ob, *rest):
    pairs, rest = rest[:2 * (chunk + 1)], rest[2 * (chunk + 1):]
    z_keep, z_send, ot_out, lse_out, tot_out, wo, sems = rest
    copies = copies_of(((wo_h, wo),), sems)
    keys, values = pairs[0::2], pairs[1::2]
    me, length = info[0], info[1]
    rows = qt.shape[1]
    kv_heads = keys[0].shape[0]
    heads = qt.shape[0] // HEAD
    group = heads // kv_heads

    def one_head(i, carry):
        j = i // group
        q_h = qt[head_rows(i), :]
        parts = []
        for c, key in enumerate(keys):
            s = nn(key[j], q_h)
            parts.append(jnp.where(visible(c * rows, chunk * rows, rows, length), s, NEG_FILL))
        top = functools.reduce(jnp.maximum, [jnp.max(s, axis=0, keepdims=True) for s in parts])
        es = [jnp.exp(s - top) for s in parts]
        total = sum(jnp.sum(e, axis=0, keepdims=True) for e in es)
        lse_out[pl.ds(i, 1), :] = top + jnp.log(total)
        o_t = sum(nn(value[head_rows(j), :], e.astype(BF16)) for value, e in zip(values, es))
        ot_out[head_rows(i), :] = (o_t / total).astype(BF16)
        return carry

    lax.fori_loop(0, heads, one_head, 0, unroll=2)
    o = ot_out[...].T
    to = nt(o, oa[...])
    tot_out[...] = to.T.astype(BF16)
    to = to.astype(BF16)
    copies[0].wait()
    for r in range(PARTS):
        at = quarter(me, r)
        put_block(r, nn(o, wo[:, at]) + nn(to, ob[:, at]), z_keep, z_send)


def front_kernel(chunk, last, info, wgu, wd, x0, x1, x2, x3, zo, zp, g0, g1, g2, g3, gains, a2, bd, fb, da,
                 *rest):
    f_s = rest[-1]
    xm_out, xq_out, h_out, g_out, act_out, dg_out, du_out, t2_s, dtd_s, b_out = rest[-11:-1]
    units = wd.shape[0]
    me, length = info[0], info[1]
    rows = h_out.shape[0]
    xs, gs = ([chunk_of(v, chunk, rows) for v in vs] for vs in ((x0, x1, x2, x3), (g0, g1, g2, g3)))

    def norm(i, carry):
        at = row_block(i)
        valid = is_valid(chunk, i, rows, length)
        square = jnp.zeros((ROW_BLOCK, 1), F32)
        for r in range(PARTS):
            v = xs[r][at, :].astype(F32) + total_block(r, at, zo, zp)
            if r == 0:
                xq_out[at, :] = v
            f_s[:, quarter(me, r)] = v
            square = square + jnp.sum(v * v, axis=1, keepdims=True)
            g_out[at, quarter(me, r)] = jnp.where(valid, gs[r][at, :], jnp.zeros((), BF16))
        inv = lax.rsqrt(square / WIDTH + EPS)
        for r in range(PARTS):
            v = f_s[:, quarter(me, r)]
            xm_out[at, quarter(me, r)] = v.astype(BF16)
            h_out[at, quarter(me, r)] = (v * inv * gains[r, 1:2, :].astype(F32)).astype(BF16)
        return carry

    lax.fori_loop(0, rows // ROW_BLOCK, norm, 0)
    t2 = nt(h_out[...], a2[...])
    t2_s[...] = t2.astype(BF16)
    dtd = nt(g_out[...], bd[...])
    dtd_s[...] = dtd.astype(BF16)
    t2t, dtdt = t2.T.astype(BF16), dtd.T.astype(BF16)

    def block(i, carry):
        c = pl.ds(pl.multiple_of(i * QUARTER, QUARTER), QUARTER)
        h, g = h_out[...], g_out[...]
        gate = nn(h, wgu[0, :, c]) + nn(t2_s[:, :RANK], fb[0, :, c])
        up = nn(h, wgu[1, :, c]) + nn(t2_s[:, RANK:], fb[1, :, c])
        dact = nt(g, wd[c, :]) + nn(dtd_s[...], da[:, c])
        sig = 1.0 / (1.0 + jnp.exp(-gate))
        silu = gate * sig
        act = (silu * up).astype(BF16)
        dgate = (dact * up * sig * (1.0 + gate * (1.0 - sig))).astype(BF16)
        dup = (dact * silu).astype(BF16)
        act_out[:, c], dg_out[:, c], du_out[:, c] = act, dgate, dup
        for k, value in enumerate((nn(t2t[:RANK], dgate), nn(t2t[RANK:], dup), nn(dtdt, act))):
            at = pl.ds(pl.multiple_of((3 * i + k) * RANK, RANK), RANK)
            if last:
                value = value + rest[0][at, :]
            b_out[at, :] = value.astype(b_out.dtype)
        return carry

    lax.fori_loop(0, units // QUARTER, block, 0)


def back_kernel(last, info, wgu, wd, h, g, act, dg, du, a2, bd, fb, da, *rest):
    (value_s, low_s), rest = rest[-2:], rest[:-2]
    outs, rest = (rest[-4:], rest[:-4]) if last else (rest[-5:], rest[:-5])
    d_keep, d_send, y_keep, y_send = outs[:4]
    me = info[0]
    rows = h.shape[0]
    own = slice(0, rows)

    dt2 = jnp.concatenate([nt(dg[...], fb[0]), nt(du[...], fb[1])], axis=1)
    dt2b = dt2.astype(BF16)
    td = nt(act[...], da[...])
    tdb = td.astype(BF16)
    dt2t, tdt = dt2.T.astype(BF16), td.T.astype(BF16)

    def block(r, carry):
        at = quarter(me, r)
        value_s[...] = nt(dg[...], wgu[0, at, :]) + nt(du[...], wgu[1, at, :]) + nn(dt2b, a2[:, at])
        store_block(r, value_s, own, d_keep, d_send)
        value_s[...] = nn(act[...], wd[:, at]) + nn(tdb, bd[:, at])
        store_block(r, value_s, own, y_keep, y_send)
        low_s[:2 * RANK, :] = nn(dt2t, h[:, at])
        low_s[2 * RANK:, :] = nn(tdt, g[:, at])
        if last:
            low_s[...] += rest[0][:, at]
            store_block(r, low_s, slice(rows, rows + 3 * RANK), d_keep, d_send)
        else:
            outs[4][:, at] = low_s[...]
        return carry

    lax.fori_loop(0, PARTS, block, 0)


def attend_back_kernel(chunk, last, info, wq_h, wkv_h, wo_h, x0, x1, x2, x3, g0, g1, g2, g3, xm, do_, dp, gains, a1,
                       qb, kvb, oa, ob, cos_t, sin_t, h_in, t1t, qt, ot, lse, tot, *rest):
    scratch, rest = rest[-13:], rest[:-13]
    z_s, f_s, dot_s, dqt_s, dkt_s, dvt_s, dq_s, value_s, low_s, wq, wkv, wo, sems = scratch
    copies = copies_of(((wo_h, wo), (wq_h, wq), (wkv_h, wkv)), sems)
    n_out = 7 if last else 8
    outs, rest = rest[-n_out:], rest[:-n_out]
    dxq_out, h_keep, h_send, inv_out, b_out = outs[:5]
    triples, rest = rest[:3 * (chunk + 1)], rest[3 * (chunk + 1):]
    keys, values, keys_t = triples[0::3], triples[1::3], triples[2::3]
    me, length = info[0], info[1]
    rows = xm.shape[0]
    kv_heads = keys[0].shape[0]
    heads = qt.shape[0] // HEAD
    group = heads // kv_heads
    q_cols, kv_cols = heads * HEAD, kv_heads * HEAD
    xs, gs = ([chunk_of(v, chunk, rows) for v in vs] for vs in ((x0, x1, x2, x3), (g0, g1, g2, g3)))

    def norm_back(i, carry):
        at = row_block(i)
        valid = is_valid(chunk, i, rows, length)
        square, first, inner = (jnp.zeros((ROW_BLOCK, 1), F32) for _ in range(3))
        for r in range(PARTS):
            v = xm[at, quarter(me, r)].astype(F32)
            square = square + jnp.sum(v * v, axis=1, keepdims=True)
            w = total_block(r, at, do_, dp) * gains[r, 1:2, :].astype(F32)
            f_s[:, quarter(me, r)] = w
            inner = inner + jnp.sum(v * w, axis=1, keepdims=True)
            u = xs[r][at, :].astype(F32)
            first = first + jnp.sum(u * u, axis=1, keepdims=True)
        inv_out[at, :] = lax.rsqrt(first / WIDTH + EPS)
        inv = lax.rsqrt(square / WIDTH + EPS)
        back = inv * inv * inv * inner / WIDTH
        for r in range(PARTS):
            v = xm[at, quarter(me, r)].astype(F32)
            g = jnp.where(valid, gs[r][at, :].astype(F32), 0.0)
            d = g + inv * f_s[:, quarter(me, r)] - v * back
            if r == 0:
                dxq_out[at, :] = d
            z_s[at, quarter(me, r)] = d.astype(BF16)
        return carry

    lax.fori_loop(0, rows // ROW_BLOCK, norm_back, 0)
    dz = z_s[...]
    dto = nt(dz, ob[...])
    copies[0].wait()
    d_o = nt(dz, wo[...]) + nn(dto.astype(BF16), oa[...])
    dot_s[...] = d_o.T.astype(BF16)
    if last:
        for c in range(chunk + 1):
            dkt_s[c], dvt_s[c] = rest[2][...], rest[3][...]
    else:
        dkt_s[...] = jnp.zeros_like(dkt_s)
        dvt_s[...] = jnp.zeros_like(dvt_s)

    def one_head(i, carry):
        j = i // group
        q_h, do_h = qt[head_rows(i), :], dot_s[head_rows(i), :]
        dots = jnp.sum(do_h.astype(F32) * ot[head_rows(i), :].astype(F32), axis=0, keepdims=True)
        low = lse[pl.ds(i, 1), :]
        dq_h = jnp.zeros((HEAD, rows), F32)
        for c in range(chunk + 1):
            prob = jnp.exp(nn(keys[c][j], q_h) - low)
            prob = jnp.where(visible(c * rows, chunk * rows, rows, length), prob, 0.0)
            ds = (prob * (nn(values[c][j], do_h) - dots)).astype(BF16)
            dq_h = dq_h + nn(keys_t[c][head_rows(j), :], ds)
            dkt_s[c, head_rows(j), :] += nt(q_h, ds)
            dvt_s[c, head_rows(j), :] += nt(do_h, prob.astype(BF16))
        dqt_s[head_rows(i), :] = dq_h
        return carry

    lax.fori_loop(0, heads, one_head, 0, unroll=2)
    if not last:
        outs[6][...], outs[7][...] = dkt_s[0], dvt_s[0]
    cos, sin = cos_t[...], sin_t[...]
    dto_t, o_t = dto.T.astype(BF16), ot[...]
    d_out_a = nt(dto_t, o_t)
    turn_back(dqt_s[...], cos * (HEAD ** -0.5), sin * (HEAD ** -0.5), dot_s)
    dq_s[:, :q_cols] = dot_s[...].T
    turn_back(dkt_s[chunk], cos, sin, dot_s)
    dq_s[:, q_cols:q_cols + kv_cols] = dot_s[:kv_cols, :].T
    dq_s[:, q_cols + kv_cols:] = dvt_s[chunk].T.astype(BF16)
    dq, dk, dv = dq_s[:, :q_cols], dq_s[:, q_cols:q_cols + kv_cols], dq_s[:, q_cols + kv_cols:]
    dt1 = jnp.concatenate([nt(dq, qb[...]), nt(dk, kvb[0]), nt(dv, kvb[1])], axis=1)
    dt1b = dt1.astype(BF16)
    kv_pad = jnp.zeros((RANK, QUARTER - 2 * kv_cols), F32)
    d_kv = jnp.concatenate([nn(t1t[RANK:2 * RANK, :], dk), nn(t1t[2 * RANK:, :], dv), kv_pad], axis=1)
    for k, value in enumerate((nn(t1t[:RANK, :], dq), d_out_a, d_kv)):
        at = slice(k * RANK, (k + 1) * RANK)
        if last:
            value = value + rest[0][at, :]
        b_out[at, :] = value.astype(b_out.dtype)
    dt1t = dt1.T.astype(BF16)
    copies[1].wait()
    copies[2].wait()

    def block(r, inner):
        at = quarter(me, r)
        d = nt(dq_s[:, :q_cols], wq[at, :]) + nn(dt1b, a1[:, at])
        d = d + nt(dq_s[:, q_cols:q_cols + kv_cols], wkv[0, at, :]) + nt(dq_s[:, q_cols + kv_cols:], wkv[1, at, :])
        value_s[...] = d
        store_block(r, value_s, slice(0, rows), h_keep, h_send)
        low_s[:3 * RANK, :] = nn(dt1t, h_in[:, at])
        low_s[3 * RANK:, :] = nn(tot[...], z_s[:, at])
        if last:
            low_s[...] += rest[1][:, at]
            store_block(r, low_s, slice(0, 4 * RANK), outs[5], outs[6])
        else:
            outs[5][:, at] = low_s[...]
        return inner + jnp.sum(d * h_in[:, at].astype(F32), axis=1, keepdims=True)

    inner = lax.fori_loop(0, PARTS, block, jnp.zeros((rows, 1), F32))
    for ref in (h_keep, h_send):
        ref[:, 2 * QUARTER:] = jnp.broadcast_to(inner, (rows, LANES)).astype(ref.dtype)


def finish_kernel(gains, x_all, *refs):
    out = refs[-1]
    gain = gains[0, 0:1, :].astype(F32)
    rows = out.shape[0] // CHUNKS
    for c in range(CHUNKS):
        dx, low, high, got, inv = refs[5 * c:5 * (c + 1)]
        x = chunk_of(x_all, c, rows)
        inv = inv[...]
        inner = high[:rows, QUARTER:QUARTER + 1].astype(F32) + got[:rows, QUARTER:QUARTER + 1].astype(F32)
        scale = inv * inv * inner / WIDTH
        grad = inv * (gain * (low[:rows, :] + got[:rows, :QUARTER].astype(F32))) - x[...].astype(F32) * scale
        out[c * rows:(c + 1) * rows, :] = (dx[...] + grad).astype(BF16)


def split_refs(refs, counts):
    groups = []
    for count in counts:
        groups.append(refs[:count])
        refs = refs[count:]
    return groups, refs


def with_entry(parts, at, use):
    start = 0
    for ref in parts:
        @pl.when((at >= start) & (at < start + ref.shape[0]))
        def _(ref=ref, start=start):
            use(ref, at - start)
        start += ref.shape[0]


def sum_slots(info, owners, out_refs, one_slot):
    count = out_refs[0].shape[0]
    base = pl.program_id(0) * count
    slots = owners.shape[0]
    for ref in out_refs:
        ref[...] = jnp.zeros_like(ref)

    def add(slot, carry):
        owner = owners[slot] - base

        @pl.when((owner >= 0) & (owner < count))
        def _():
            one_slot(owner, entry_of(slot, info[3], slots))
        return carry

    lax.fori_loop(0, slots, add, 0)


def feedforward_sum_kernel(counts, info, owners, *refs):
    (b_parts, *a_parts), outs = split_refs(refs, counts)
    ga, gdb, gb, gda = outs
    me = info[0]

    def one_slot(owner, at):
        def add_b(ref, e):
            for i in range(gda.shape[2] // QUARTER):
                cols = slice(i * QUARTER, (i + 1) * QUARTER)
                base = i * 3 * RANK
                gb[owner, 0, :, cols] += ref[e, base:base + RANK, :].astype(F32)
                gb[owner, 1, :, cols] += ref[e, base + RANK:base + 2 * RANK, :].astype(F32)
                gda[owner, :, cols] += ref[e, base + 2 * RANK:base + 3 * RANK, :].astype(F32)

        with_entry(b_parts, at, add_b)
        for near_bit, parts in enumerate(a_parts):
            def add_a(ref, e, near_bit=near_bit):
                for r, cols in ((near_bit, LO), (near_bit ^ 2, HI)):
                    ga[owner, :, quarter(me, r)] += ref[e, :2 * RANK, cols].astype(F32)
                    gdb[owner, :, quarter(me, r)] += ref[e, 2 * RANK:, cols].astype(F32)

            with_entry(parts, at, add_a)

    sum_slots(info, owners, outs, one_slot)


def attention_sum_kernel(counts, info, owners, *refs):
    (b_parts, *a_parts), outs = split_refs(refs, counts)
    ga, gob, gq, gkv, goa = outs
    me = info[0]
    kv_cols = gkv.shape[3]

    def one_slot(owner, at):
        def add_b(ref, e):
            gq[owner] += ref[e, :RANK, :].astype(F32)
            goa[owner] += ref[e, RANK:2 * RANK, :].astype(F32)
            gkv[owner, 0] += ref[e, 2 * RANK:3 * RANK, :kv_cols].astype(F32)
            gkv[owner, 1] += ref[e, 2 * RANK:3 * RANK, kv_cols:2 * kv_cols].astype(F32)

        with_entry(b_parts, at, add_b)
        for r, parts in enumerate(a_parts):
            def add_a(ref, e, r=r):
                ga[owner, :, quarter(me, r)] += ref[e, :3 * RANK, :].astype(F32)
                gob[owner, :, quarter(me, r)] += ref[e, 3 * RANK:, :].astype(F32)

            with_entry(parts, at, add_a)

    sum_slots(info, owners, outs, one_slot)


def deal_kernel(slots, source, out, sems):
    made = [pltpu.make_async_copy(source.at[i], out.at[slots[i]], sems.at[i]) for i in range(source.shape[0])]
    for copy in made:
        copy.start()
    for copy in made:
        copy.wait()


def collect_kernel(slots, source, out, sems):
    made = [pltpu.make_async_copy(source.at[slots[i]], out.at[i], sems.at[i]) for i in range(source.shape[0])]
    for copy in made:
        copy.start()
    for copy in made:
        copy.wait()


def load_kernel(count, *refs):
    made = [pltpu.make_async_copy(refs[i], refs[count + i], refs[-1].at[i]) for i in range(count)]
    for copy in made:
        copy.start()
    for copy in made:
        copy.wait()


def adapter_kernel(count, info, *refs):
    made = [pltpu.make_async_copy(refs[i].at[info[2]], refs[count + i], refs[-1].at[i]) for i in range(count)]
    for copy in made:
        copy.start()
    for copy in made:
        copy.wait()


def load(arrays, name, info=None, after=()):
    count = len(arrays)
    scalars = () if info is None else (info,)
    kernel = load_kernel if info is None else adapter_kernel
    shapes = [a.shape if info is None else a.shape[1:] for a in arrays]

    def body(*refs):
        at = len(scalars) + count
        kernel(count, *refs[:at], *refs[at + len(after):])

    return pl.pallas_call(
        body,
        in_specs=[pl.BlockSpec(memory_space=pltpu.SMEM)] * len(scalars) + [pl.BlockSpec(memory_space=pltpu.HBM)] * count
        + [pl.BlockSpec(memory_space=pl.ANY)] * len(after),
        out_specs=[pl.BlockSpec(memory_space=pltpu.VMEM)] * count,
        out_shape=[pltpu.VMEM(tuple(s), a.dtype) for s, a in zip(shapes, arrays)],
        scratch_shapes=[pltpu.SemaphoreType.DMA((count,))],
        compiler_params=pltpu.CompilerParams(vmem_limit_bytes=MIB),
        cost_estimate=pl.CostEstimate(flops=1000, transcendentals=0, bytes_accessed=1000),
        name=name,
    )(*scalars, *(in_hbm(a) for a in arrays), *after)


def move_rows(kernel, value, slots, name):
    return pl.pallas_call(
        kernel,
        in_specs=[pl.BlockSpec(memory_space=pltpu.SMEM), pl.BlockSpec(memory_space=pl.ANY)],
        out_specs=pl.BlockSpec(memory_space=pl.ANY),
        out_shape=jax.ShapeDtypeStruct(value.shape, value.dtype),
        scratch_shapes=[pltpu.SemaphoreType.DMA((value.shape[0],))],
        compiler_params=pltpu.CompilerParams(vmem_limit_bytes=MIB),
        cost_estimate=pl.CostEstimate(flops=1000, transcendentals=0, bytes_accessed=1000),
        name=name,
    )(slots, value)


def sds(shape, dtype):
    return jax.ShapeDtypeStruct(tuple(shape), dtype)


def in_vmem(value):
    return pltpu.with_memory_space_constraint(value, pltpu.VMEM)


def in_hbm(value):
    return pltpu.with_memory_space_constraint(value, pltpu.HBM)


def call(kernel, info, weights, args, outs, scratch, name, mib, after=(), sems=()):
    vmem = pl.BlockSpec(memory_space=pltpu.VMEM)
    scalars = () if info is None else (info,)
    n, w = len(scalars), len(weights)

    def body(*refs):
        at = n + w + len(args)
        kernel(*refs[:at], *refs[at + len(after):])

    return pl.pallas_call(
        body,
        in_specs=[pl.BlockSpec(memory_space=pltpu.SMEM)] * n + [pl.BlockSpec(memory_space=pltpu.HBM)] * w + [vmem] * len(args)
        + [pl.BlockSpec(memory_space=pl.ANY)] * len(after),
        out_specs=[vmem] * len(outs),
        out_shape=[pltpu.VMEM(tuple(s), d) for s, d in outs],
        scratch_shapes=[pltpu.VMEM(s, d) for s, d in scratch] + ([pltpu.SemaphoreType.DMA(sems)] if sems else []),
        compiler_params=pltpu.CompilerParams(vmem_limit_bytes=mib * MIB),
        cost_estimate=pl.CostEstimate(flops=1000, transcendentals=0, bytes_accessed=1000),
        name=name,
    )(*scalars, *(in_hbm(a) for a in weights), *(in_vmem(a) for a in args), *after)


def sum_call(kernel, scalars, groups, outs, name):
    args = [v for group in groups for v in group]
    steps = 2
    specs = [pl.BlockSpec((o.shape[0] // steps,) + o.shape[1:], (lambda n: lambda i, *_: (i,) + (0,) * n)(o.ndim - 1))
             for o in outs]
    return pl.pallas_call(
        functools.partial(kernel, [len(group) for group in groups]),
        grid_spec=pltpu.PrefetchScalarGridSpec(
            num_scalar_prefetch=len(scalars), grid=(steps,),
            in_specs=[pl.BlockSpec(memory_space=pltpu.VMEM)] * len(args), out_specs=specs),
        out_shape=outs,
        compiler_params=pltpu.CompilerParams(
            dimension_semantics=("arbitrary",),
            vmem_limit_bytes=4 * MIB + sum(a.size * a.dtype.itemsize for a in args)
            + sum(o.size * o.dtype.itemsize for o in outs)),
        cost_estimate=pl.CostEstimate(flops=0, transcendentals=0, bytes_accessed=12000000),
        name=name,
    )(*scalars, *(in_vmem(a) for a in args))


def swap(value, bit, axis, size):
    return lax.ppermute(value, axis, [(i, i ^ bit) for i in range(size)])


def near(value):
    return swap(value, 1, "mp", PARTS)


def far(value):
    return swap(value, 2, "mp", PARTS)


def spread(value):
    there = far(value)
    return (value, near(value), there, near(there))


def chip_sum(keep, send):
    got = near(send)
    lo = keep[:, :QUARTER].astype(F32) + got[:, :QUARTER].astype(F32)
    hi = keep[:, QUARTER:].astype(F32) + got[:, QUARTER:].astype(F32)
    return lo, hi.astype(BF16)


def far_sum_kernel(own, got, out):
    for to, other in ((LO, HI), (HI, LO)):
        out[:, to] = (own[:, to].astype(F32) + got[:, other].astype(F32)).astype(BF16)


def far_sum(own, got):
    return call(far_sum_kernel, None, (), (own, got), [(own.shape, BF16)], [], "far_sum", 6)[0]


def pair_sum_kernel(keep, got, out):
    out[...] = (keep[...] + got[...].astype(F32)).astype(BF16)


def pair_sum(keep, send):
    return call(pair_sum_kernel, None, (), (keep, near(send)), [(send.shape, BF16)], [], "pair_sum", 6)[0]


def late(value, *others):
    return lax.optimization_barrier((value, *others))[0]


def doubled(stack, bit, size):
    return jnp.concatenate([stack, swap(stack, bit, "dp", size)], axis=0)


def entry_of(slot, place, size):
    bits = size.bit_length() - 1
    apart = slot ^ place
    return sum(((apart >> b) & 1) << (bits - 1 - b) for b in range(bits))


def shards(dp, residual, attention_gain, query_matrix, key_value_matrix, output_matrix, feedfwd_gain,
           gate_up_matrix, down_matrix, attention_adapter_input, query_adapter_output,
           key_value_adapter_output, output_adapter_input, output_adapter_output, feedfwd_adapter_input,
           feedfwd_adapter_output, down_adapter_input, down_adapter_output, lengths, adapter_index,
           dealing_slots, cotangent):
    seqs = residual.shape[0]
    length = cotangent.shape[1]
    units = down_matrix.shape[0]
    adapters = attention_adapter_input.shape[0]
    q_cols = query_matrix.shape[1]
    kv_cols = key_value_matrix.shape[2]
    kv_heads = kv_cols // HEAD
    heads = q_cols // HEAD
    rows = length // CHUNKS
    half = 2 * QUARTER
    me = lax.axis_index("mp")
    place = lax.axis_index("dp")

    is_there = dealing_slots[None, :] == jnp.arange(seqs, dtype=jnp.int32)[:, None]
    owners = jnp.sum(jnp.where(is_there, adapter_index[None, :], 0), axis=1)
    spans = jnp.sum(jnp.where(is_there, lengths[None, :], 0), axis=1)
    mine = jnp.arange(seqs, dtype=jnp.int32) == place
    my_length = jnp.sum(jnp.where(mine, spans, 0))
    my_adapter = jnp.sum(jnp.where(mine, owners, 0))
    info = jnp.stack([me.astype(jnp.int32), my_length, my_adapter, place.astype(jnp.int32)])

    gs = spread(cotangent[0])
    gains = jnp.stack(spread(jnp.stack([attention_gain, feedfwd_gain])))
    dealt = lax.all_to_all(
        move_rows(deal_kernel, in_hbm(residual), dealing_slots, "deal"), "dp", split_axis=0, concat_axis=1, tiled=True
    )[0]
    dealt = late(dealt, gs[2])
    beside = near(dealt)
    there = [far(dealt[c * rows:(c + 1) * rows]) for c in range(CHUNKS)]
    xs = [None] * CHUNKS
    cos_np, sin_np = rope_tables(length)
    cos = [jnp.asarray(cos_np[:, c * rows:(c + 1) * rows]) for c in range(CHUNKS)]
    sin = [jnp.asarray(sin_np[:, c * rows:(c + 1) * rows]) for c in range(CHUNKS)]
    adapters_here = load(
        (attention_adapter_input, query_adapter_output, key_value_adapter_output, output_adapter_input,
         output_adapter_output, feedfwd_adapter_input, feedfwd_adapter_output, down_adapter_input,
         down_adapter_output), "adapters", info)
    a1, qb, kvb, oa, ob, a2, fba, da, bd = adapters_here
    wq, wkv, wo, wgu, wd = query_matrix, key_value_matrix, output_matrix, gate_up_matrix, down_matrix

    def like(*arrays):
        return [(a.shape, a.dtype) for a in arrays]

    wide, col, block, thin = (rows, WIDTH), (rows, half), (rows, QUARTER), (rows, 1)
    saved = [None] * CHUNKS
    order = ()
    for c in range(CHUNKS):
        xs[c] = (dealt, beside, there[c], near(late(there[c], *order)))
        outs = [(wide, BF16), ((3 * RANK, rows), BF16), ((q_cols, rows), BF16), ((kv_heads, rows, HEAD), BF16),
                ((kv_heads, rows, HEAD), BF16), ((kv_cols, rows), BF16), ((kv_cols, rows), BF16)]
        saved[c] = call(
            functools.partial(project_kernel, c), info, (wq, wkv), (*xs[c], gains, a1, qb, kvb, cos[c], sin[c]), outs,
            like(wq, wkv), "project_%d" % c, 12, order, (2,))
        order = (saved[c][1],)

    kept, z_own = [None] * CHUNKS, [None] * CHUNKS
    for c in reversed(range(CHUNKS)):
        outs = [(col, F32), (col, BF16), ((q_cols, rows), BF16), ((heads, rows), F32), ((RANK, rows), BF16)]
        pairs = [v for p in saved[:c + 1] for v in (p[3], p[6])]
        z_keep, z_send, *kept[c] = call(
            functools.partial(attend_kernel, c), info, (wo,), (saved[c][2], oa, ob, *pairs), outs, like(wo),
            "attend_%d" % c, 10, order, (1,))
        z_own[c] = pair_sum(z_keep, z_send)
        order = (kept[c][1], z_own[1])
    z_far = [far(v) for v in z_own]
    wgu, wd = load((wgu, wd), "load", None, order)

    def front(c, total, partial, order):
        hidden = (rows, units)
        outs = [(wide, BF16), (block, F32), (wide, BF16), (wide, BF16), (hidden, BF16), (hidden, BF16), (hidden, BF16),
                ((rows, 2 * RANK), BF16), ((rows, RANK), BF16),
                ((3 * RANK * units // QUARTER, QUARTER), F32 if c else BF16)]
        return call(
            functools.partial(front_kernel, c, c == 0), info, (),
            (wgu, wd, *xs[c], total, near(total), *gs, gains, a2, bd, fba, da, *partial), outs,
            [((ROW_BLOCK, WIDTH), F32)], "front_%d" % c, 8, order)

    def back(c, hidden, partial, order):
        first = col if c else (rows + 3 * RANK, half)
        outs = [(first, F32), (first, BF16), (col, F32), (col, BF16)]
        outs += [((3 * RANK, WIDTH), F32)] if c else []
        return call(
            functools.partial(back_kernel, c == 0), info, (), (wgu, wd, *hidden[2:7], a2, bd, fba, da, *partial), outs,
            [(block, F32), ((3 * RANK, QUARTER), F32)], "back_%d" % c, 8, order)

    def attend_back(c, total, partial, order):
        padded = (rows, half + LANES)
        outs = [(block, F32), (padded, F32), (padded, BF16), (thin, F32), ((3 * RANK, QUARTER), F32 if c else BF16)]
        outs += ([((4 * RANK, WIDTH), F32), ((kv_cols, rows), F32), ((kv_cols, rows), F32)] if c
                 else [((4 * RANK, half), F32), ((4 * RANK, half), BF16)])
        scratch = [(wide, BF16), ((ROW_BLOCK, WIDTH), F32), ((q_cols, rows), BF16), ((q_cols, rows), F32),
                   ((c + 1, kv_cols, rows), F32), ((c + 1, kv_cols, rows), F32), ((rows, q_cols + 2 * kv_cols), BF16),
                   (block, F32), ((4 * RANK, QUARTER), F32)]
        triples = [v for p in saved[:c + 1] for v in (p[3], p[4], p[5])]
        return call(
            functools.partial(attend_back_kernel, c, c == 0), info, (wq, wkv, wo),
            (*xs[c], *gs, hidden[c][0], total, near(total), gains, a1, qb, kvb, oa, ob, cos[c], sin[c], *saved[c][:3],
             *kept[c], *triples, *partial), outs, scratch + like(wq, wkv, wo), "attend_back_%d" % c, 18, order, (3,))

    bits = [1 << b for b in reversed(range(dp.bit_length() - 1))]
    hidden, d_own, d_far = ([None] * CHUNKS for _ in range(3))
    hidden[1] = front(1, far_sum(z_own[1], z_far[1]), (), order)
    step = hidden[1][8]
    total = far_sum(z_own[0], late(z_far[0], step))
    d_keep, d_send, y_keep_1, y_send_1, fa = back(1, hidden[1], (), (step, total))
    d_own[1] = pair_sum(d_keep, d_send)
    d_far[1] = far(d_own[1])
    hidden[0] = front(0, total, hidden[1][9:], (d_own[1],))
    step = hidden[0][8]
    total = far_sum(d_own[1], late(d_far[1], step))
    fb = hidden[0][9][None]
    fb_first = swap(fb, bits[0], "dp", dp)
    d_keep, d_send, y_keep_0, y_send_0 = back(0, hidden[0], (fa,), (step, total))
    d_own[0] = pair_sum(d_keep, late(d_send, fb_first))
    d_far[0] = far(d_own[0])
    fb = fb_more = jnp.concatenate([fb, fb_first], axis=0)
    for bit in bits[1:-1]:
        fb_more = doubled(fb_more, bit, dp)
    fb_more = fb_more[2:]
    fb_side = swap(fb, bits[-1], "dp", dp)
    y_keep, y_got = (y_keep_0, y_keep_1), (near(y_send_0), near(late(y_send_1, step)))
    dxq, h_keep, h_send, inv, *sums = attend_back(1, total, (), (d_own[0],))
    total = far_sum(d_own[0], late(d_far[0], inv))
    h_low, h_high = chip_sum(h_keep, late(h_send, fb_more, fb_side, d_far[0]))
    h_far = far(h_high)
    final = [None, (dxq, h_low, h_high, h_far, inv)]
    y_high = [(k[:, QUARTER:] + late(g, h_high)[:, QUARTER:].astype(F32)).astype(BF16) for k, g in zip(y_keep, y_got)]
    y_high = jnp.concatenate(y_high, axis=0)
    fa = total[rows:][None]
    fa_first = swap(fa, bits[0], "dp", dp)
    fb_more_side = swap(fb_more, bits[-1], "dp", dp)
    dxq, h_keep, h_send, inv, att_b, aa_keep, aa_send = attend_back(0, total, sums, (h_high, y_high))
    ready = (fa_first, fb_more_side, h_far)
    aa_low, aa_high = chip_sum(aa_keep, late(aa_send, *ready))
    aa_far = far(aa_high)
    h_low, h_high = chip_sum(h_keep, late(h_send, *ready))
    h_far = far(h_high)
    final[0] = (dxq, h_low, h_high, h_far, inv)
    att = jnp.concatenate([att_b, (aa_low + late(aa_far, h_high).astype(F32)).astype(BF16)], axis=0)[None]
    att = doubled(att, bits[0], dp)

    dinput, = call(finish_kernel, None, (), (gains, dealt, *(v for f in final for v in f)), [((length, QUARTER), BF16)],
                   [], "finish", 8, (att,))
    back_grad = lax.all_to_all(
        dinput.reshape(dp, length // dp, QUARTER), "dp", split_axis=0, concat_axis=0, tiled=True)
    input_grad = move_rows(collect_kernel, back_grad, dealing_slots, "collect_grad")

    valid = (jnp.arange(length, dtype=jnp.int32) < my_length)[:, None]
    result = [h[1] + k[:, :QUARTER] + g[:, :QUARTER].astype(F32) for h, k, g in zip(hidden, y_keep, y_got)]
    result = jnp.concatenate(result, axis=0) + late(far(late(y_high, h_high)), dinput).astype(F32)
    result = jnp.where(valid, result, 0.0).astype(BF16)
    back_out = lax.all_to_all(
        result.reshape(dp, length // dp, QUARTER), "dp", split_axis=0, concat_axis=0, tiled=True)
    output = move_rows(collect_kernel, back_out, late(dealing_slots, input_grad), "collect_out")

    n_b = att_b.shape[0]
    for bit in bits[1:-1]:
        att = doubled(att, bit, dp)
    att_side = swap(att, bits[-1], "dp", dp)
    a_parts = [att[:, n_b:], att_side[:, n_b:]]
    a_far = [far(v) for v in a_parts]
    fa = late(jnp.concatenate([fa, fa_first], axis=0), h_high)
    for bit in bits[1:-1]:
        fa = doubled(fa, bit, dp)
    fa_side = swap(fa, bits[-1], "dp", dp)
    outs = [sds((adapters, 2 * RANK, WIDTH), F32), sds((adapters, RANK, WIDTH), F32),
            sds((adapters, 2, RANK, units), F32), sds((adapters, RANK, units), F32)]
    ga_ffn, g_down_b, g_ffn_b, g_down_a = sum_call(
        feedforward_sum_kernel, (info, owners),
        ((fb, fb_more, fb_side, fb_more_side), (fa, fa_side), (near(fa), near(fa_side))), outs, "feedforward_sum")

    outs = [sds((adapters, 3 * RANK, WIDTH), F32), sds((adapters, RANK, WIDTH), F32),
            sds((adapters, RANK, q_cols), F32), sds((adapters, 2, RANK, kv_cols), F32),
            sds((adapters, RANK, q_cols), F32)]
    ga_att, g_out_b, g_query_b, g_kv_b, g_out_a = sum_call(
        attention_sum_kernel, (info, owners),
        ((att, att_side), a_parts, [near(v) for v in a_parts], a_far, (near(a_far[0]), near(late(a_far[1], g_down_a)))), outs, "attention_sum")
    return (output, input_grad, ga_att, g_query_b, g_kv_b, g_out_a, g_out_b, ga_ffn, g_ffn_b, g_down_a, g_down_b)


def solution(mesh):
    in_specs = (
        P(None, "dp", "mp"), P("mp"), P(None, "mp"), P(None, None, "mp"), P("mp", None), P("mp"),
        P(None, None, "mp"), P("mp", None), P(), P(None, None, "mp"), P(None, None, None, "mp"),
        P(None, None, "mp"), P(), P(), P(None, None, None, "mp"), P(None, None, "mp"), P(), P(), P(), P(),
        P("dp", None, "mp"),
    )
    out_specs = (
        P(None, "dp", "mp"), P(None, "dp", "mp"), P(), P(None, None, "mp"), P(None, None, None, "mp"),
        P(None, None, "mp"), P(), P(), P(None, None, None, "mp"), P(None, None, "mp"), P(),
    )
    return jax.shard_map(
        functools.partial(shards, mesh.shape["dp"]), mesh=mesh, in_specs=in_specs, out_specs=out_specs,
        check_vma=False)
```

```python
import functools

import jax
import jax.numpy as jnp
import numpy as np
from jax import lax
from jax.experimental import pallas as pl
from jax.experimental.pallas import tpu as pltpu
from jax.sharding import PartitionSpec as P

WIDTH = 2048
HEAD = 64
HALF = HEAD // 2
RANK = 16
EPS = 1e-05
ROPE_BASE = 500000.0
NEG_FILL = -1e30
PARTS = 4
LANES = 128
ROW_BLOCK = 64
QUARTER = WIDTH // PARTS
CHUNKS = 2
MIB = 1024 * 1024
F32 = jnp.float32
BF16 = jnp.bfloat16


def nn(a, b):
    return lax.dot_general(a, b, (((1,), (0,)), ((), ())), preferred_element_type=F32)


def nt(a, b):
    return lax.dot_general(a, b, (((1,), (1,)), ((), ())), preferred_element_type=F32)


def rope_tables(length):
    freq = ROPE_BASE ** (-np.arange(HALF, dtype=np.float32) * np.float32(2.0 / HEAD))
    angles = (np.arange(length, dtype=np.float32)[None, :] * freq.astype(np.float32)[:, None]).astype(np.float32)
    return np.cos(angles).astype(np.float32), np.sin(angles).astype(np.float32)


def quarter(me, rel):
    return pl.ds(pl.multiple_of((me ^ rel) * QUARTER, QUARTER), QUARTER)


LO, HI = slice(0, QUARTER), slice(QUARTER, 2 * QUARTER)


def total_block(rel, rows_at, own, oth):
    return (own if rel in (0, 2) else oth)[rows_at, LO if rel in (0, 1) else HI].astype(F32)


def store_block(rel, value, rows_at, keep_ref, send_ref):
    to = pl.ds(pl.multiple_of((rel // 2) * QUARTER, QUARTER), QUARTER)

    @pl.when(rel % 2 == 0)
    def _():
        keep_ref[rows_at, to] = value[...]

    @pl.when(rel % 2 == 1)
    def _():
        send_ref[rows_at, to] = value[...].astype(BF16)


def chunk_of(ref, chunk, rows):
    return ref if ref.shape[0] == rows else ref.at[chunk * rows:(chunk + 1) * rows]


def row_block(i):
    return pl.ds(pl.multiple_of(i * ROW_BLOCK, ROW_BLOCK), ROW_BLOCK)


def is_valid(chunk, i, rows, length):
    return chunk * rows + i * ROW_BLOCK + lax.broadcasted_iota(jnp.int32, (ROW_BLOCK, 1), 0) < length


def copies_of(pairs, sems):
    made = [pltpu.make_async_copy(source, target, sems.at[i]) for i, (source, target) in enumerate(pairs)]
    for copy in made:
        copy.start()
    return made


def put_block(rel, value, keep_ref, send_ref):
    ref = keep_ref if rel in (0, 2) else send_ref
    ref[:, LO if rel in (0, 1) else HI] = value.astype(ref.dtype)


def rotate(value, cos, sin, out_ref):
    for i in range(value.shape[0] // HEAD):
        u1, u2 = value[i * HEAD:i * HEAD + HALF], value[i * HEAD + HALF:(i + 1) * HEAD]
        out_ref[i * HEAD:i * HEAD + HALF, :] = (u1 * cos - u2 * sin).astype(BF16)
        out_ref[i * HEAD + HALF:(i + 1) * HEAD, :] = (u2 * cos + u1 * sin).astype(BF16)


def turn_back(value, cos, sin, out_ref):
    for i in range(value.shape[0] // HEAD):
        w1, w2 = value[i * HEAD:i * HEAD + HALF], value[i * HEAD + HALF:(i + 1) * HEAD]
        out_ref[i * HEAD:i * HEAD + HALF, :] = (w1 * cos + w2 * sin).astype(BF16)
        out_ref[i * HEAD + HALF:(i + 1) * HEAD, :] = (w2 * cos - w1 * sin).astype(BF16)


def head_rows(i):
    return pl.ds(pl.multiple_of(i * HEAD, HEAD), HEAD)


def visible(key_start, query_start, rows, length):
    kpos = key_start + lax.broadcasted_iota(jnp.int32, (rows, rows), 0)
    qpos = query_start + lax.broadcasted_iota(jnp.int32, (rows, rows), 1)
    return (kpos <= qpos) & (kpos < length)


def project_kernel(chunk, info, wq_h, wkv_h, x0, x1, x2, x3, gains, a1, qb, kvb, cos_t, sin_t,
                   h_out, t1t_out, qt_out, kn_out, vn_out, kt_out, vt_out, wq, wkv, sems):
    copies = copies_of(((wkv_h, wkv), (wq_h, wq)), sems)
    me = info[0]
    rows = h_out.shape[0]
    kv_heads = kn_out.shape[0]
    xs = [chunk_of(x, chunk, rows) for x in (x0, x1, x2, x3)]

    def norm(i, carry):
        at = row_block(i)
        square = jnp.zeros((ROW_BLOCK, 1), F32)
        for r in range(PARTS):
            v = xs[r][at, :].astype(F32)
            square = square + jnp.sum(v * v, axis=1, keepdims=True)
        inv = lax.rsqrt(square / WIDTH + EPS)
        for r in range(PARTS):
            v = xs[r][at, :].astype(F32)
            h_out[at, quarter(me, r)] = (v * inv * gains[r, 0:1, :].astype(F32)).astype(BF16)
        return carry

    lax.fori_loop(0, rows // ROW_BLOCK, norm, 0)
    h = h_out[...]
    t1 = nt(h, a1[...])
    t1t_out[...] = t1.T.astype(BF16)
    t1b = t1.astype(BF16)
    cos, sin = cos_t[...], sin_t[...]
    copies[0].wait()
    k = nn(h, wkv[0]) + nn(t1b[:, RANK:2 * RANK], kvb[0])
    rotate(k.T, cos, sin, kt_out)
    k_n = kt_out[...].T
    v_n = (nn(h, wkv[1]) + nn(t1b[:, 2 * RANK:], kvb[1])).astype(BF16)
    vt_out[...] = v_n.T
    for i in range(kv_heads):
        kn_out[i] = k_n[:, i * HEAD:(i + 1) * HEAD]
        vn_out[i] = v_n[:, i * HEAD:(i + 1) * HEAD]
    copies[1].wait()
    q = nn(h, wq[...]) + nn(t1b[:, :RANK], qb[...])
    rotate(q.T * (HEAD ** -0.5), cos, sin, qt_out)


def attend_kernel(chunk, info, wo_h, qt, oa, ob, *rest):
    pairs, rest = rest[:2 * (chunk + 1)], rest[2 * (chunk + 1):]
    z_keep, z_send, ot_out, lse_out, tot_out, wo, sems = rest
    copies = copies_of(((wo_h, wo),), sems)
    keys, values = pairs[0::2], pairs[1::2]
    me, length = info[0], info[1]
    rows = qt.shape[1]
    kv_heads = keys[0].shape[0]
    heads = qt.shape[0] // HEAD
    group = heads // kv_heads

    def one_head(i, carry):
        j = i // group
        q_h = qt[head_rows(i), :]
        parts = []
        for c, key in enumerate(keys):
            s = nn(key[j], q_h)
            parts.append(jnp.where(visible(c * rows, chunk * rows, rows, length), s, NEG_FILL))
        top = functools.reduce(jnp.maximum, [jnp.max(s, axis=0, keepdims=True) for s in parts])
        es = [jnp.exp(s - top) for s in parts]
        total = sum(jnp.sum(e, axis=0, keepdims=True) for e in es)
        lse_out[pl.ds(i, 1), :] = top + jnp.log(total)
        o_t = sum(nn(value[head_rows(j), :], e.astype(BF16)) for value, e in zip(values, es))
        ot_out[head_rows(i), :] = (o_t / total).astype(BF16)
        return carry

    lax.fori_loop(0, heads, one_head, 0, unroll=2)
    o = ot_out[...].T
    to = nt(o, oa[...])
    tot_out[...] = to.T.astype(BF16)
    to = to.astype(BF16)
    copies[0].wait()
    for r in range(PARTS):
        at = quarter(me, r)
        put_block(r, nn(o, wo[:, at]) + nn(to, ob[:, at]), z_keep, z_send)


def front_kernel(chunk, last, info, wgu, wd, x0, x1, x2, x3, zo, zp, g0, g1, g2, g3, gains, a2, bd, fb, da,
                 *rest):
    f_s = rest[-1]
    xm_out, xq_out, h_out, g_out, act_out, dg_out, du_out, t2_s, dtd_s, b_out = rest[-11:-1]
    units = wd.shape[0]
    me, length = info[0], info[1]
    rows = h_out.shape[0]
    xs, gs = ([chunk_of(v, chunk, rows) for v in vs] for vs in ((x0, x1, x2, x3), (g0, g1, g2, g3)))

    def norm(i, carry):
        at = row_block(i)
        valid = is_valid(chunk, i, rows, length)
        square = jnp.zeros((ROW_BLOCK, 1), F32)
        for r in range(PARTS):
            v = xs[r][at, :].astype(F32) + total_block(r, at, zo, zp)
            if r == 0:
                xq_out[at, :] = v
            f_s[:, quarter(me, r)] = v
            square = square + jnp.sum(v * v, axis=1, keepdims=True)
            g_out[at, quarter(me, r)] = jnp.where(valid, gs[r][at, :], jnp.zeros((), BF16))
        inv = lax.rsqrt(square / WIDTH + EPS)
        for r in range(PARTS):
            v = f_s[:, quarter(me, r)]
            xm_out[at, quarter(me, r)] = v.astype(BF16)
            h_out[at, quarter(me, r)] = (v * inv * gains[r, 1:2, :].astype(F32)).astype(BF16)
        return carry

    lax.fori_loop(0, rows // ROW_BLOCK, norm, 0)
    t2 = nt(h_out[...], a2[...])
    t2_s[...] = t2.astype(BF16)
    dtd = nt(g_out[...], bd[...])
    dtd_s[...] = dtd.astype(BF16)
    t2t, dtdt = t2.T.astype(BF16), dtd.T.astype(BF16)

    def block(i, carry):
        c = pl.ds(pl.multiple_of(i * QUARTER, QUARTER), QUARTER)
        h, g = h_out[...], g_out[...]
        gate = nn(h, wgu[0, :, c]) + nn(t2_s[:, :RANK], fb[0, :, c])
        up = nn(h, wgu[1, :, c]) + nn(t2_s[:, RANK:], fb[1, :, c])
        dact = nt(g, wd[c, :]) + nn(dtd_s[...], da[:, c])
        sig = 1.0 / (1.0 + jnp.exp(-gate))
        silu = gate * sig
        act = (silu * up).astype(BF16)
        dgate = (dact * up * sig * (1.0 + gate * (1.0 - sig))).astype(BF16)
        dup = (dact * silu).astype(BF16)
        act_out[:, c], dg_out[:, c], du_out[:, c] = act, dgate, dup
        for k, value in enumerate((nn(t2t[:RANK], dgate), nn(t2t[RANK:], dup), nn(dtdt, act))):
            at = pl.ds(pl.multiple_of((3 * i + k) * RANK, RANK), RANK)
            if last:
                value = value + rest[0][at, :]
            b_out[at, :] = value.astype(b_out.dtype)
        return carry

    lax.fori_loop(0, units // QUARTER, block, 0)


def back_kernel(last, info, wgu, wd, h, g, act, dg, du, a2, bd, fb, da, *rest):
    (value_s, low_s), rest = rest[-2:], rest[:-2]
    outs, rest = (rest[-4:], rest[:-4]) if last else (rest[-5:], rest[:-5])
    d_keep, d_send, y_keep, y_send = outs[:4]
    me = info[0]
    rows = h.shape[0]
    own = slice(0, rows)

    dt2 = jnp.concatenate([nt(dg[...], fb[0]), nt(du[...], fb[1])], axis=1)
    dt2b = dt2.astype(BF16)
    td = nt(act[...], da[...])
    tdb = td.astype(BF16)
    dt2t, tdt = dt2.T.astype(BF16), td.T.astype(BF16)

    def block(r, carry):
        at = quarter(me, r)
        value_s[...] = nt(dg[...], wgu[0, at, :]) + nt(du[...], wgu[1, at, :]) + nn(dt2b, a2[:, at])
        store_block(r, value_s, own, d_keep, d_send)
        value_s[...] = nn(act[...], wd[:, at]) + nn(tdb, bd[:, at])
        store_block(r, value_s, own, y_keep, y_send)
        low_s[:2 * RANK, :] = nn(dt2t, h[:, at])
        low_s[2 * RANK:, :] = nn(tdt, g[:, at])
        if last:
            low_s[...] += rest[0][:, at]
            store_block(r, low_s, slice(rows, rows + 3 * RANK), d_keep, d_send)
        else:
            outs[4][:, at] = low_s[...]
        return carry

    lax.fori_loop(0, PARTS, block, 0)


def attend_back_kernel(chunk, last, info, wq_h, wkv_h, wo_h, x0, x1, x2, x3, g0, g1, g2, g3, xm, do_, dp, gains, a1,
                       qb, kvb, oa, ob, cos_t, sin_t, h_in, t1t, qt, ot, lse, tot, *rest):
    scratch, rest = rest[-13:], rest[:-13]
    z_s, f_s, dot_s, dqt_s, dkt_s, dvt_s, dq_s, value_s, low_s, wq, wkv, wo, sems = scratch
    copies = copies_of(((wo_h, wo), (wq_h, wq), (wkv_h, wkv)), sems)
    n_out = 7 if last else 8
    outs, rest = rest[-n_out:], rest[:-n_out]
    dxq_out, h_keep, h_send, inv_out, b_out = outs[:5]
    triples, rest = rest[:3 * (chunk + 1)], rest[3 * (chunk + 1):]
    keys, values, keys_t = triples[0::3], triples[1::3], triples[2::3]
    me, length = info[0], info[1]
    rows = xm.shape[0]
    kv_heads = keys[0].shape[0]
    heads = qt.shape[0] // HEAD
    group = heads // kv_heads
    q_cols, kv_cols = heads * HEAD, kv_heads * HEAD
    xs, gs = ([chunk_of(v, chunk, rows) for v in vs] for vs in ((x0, x1, x2, x3), (g0, g1, g2, g3)))

    def norm_back(i, carry):
        at = row_block(i)
        valid = is_valid(chunk, i, rows, length)
        square, first, inner = (jnp.zeros((ROW_BLOCK, 1), F32) for _ in range(3))
        for r in range(PARTS):
            v = xm[at, quarter(me, r)].astype(F32)
            square = square + jnp.sum(v * v, axis=1, keepdims=True)
            w = total_block(r, at, do_, dp) * gains[r, 1:2, :].astype(F32)
            f_s[:, quarter(me, r)] = w
            inner = inner + jnp.sum(v * w, axis=1, keepdims=True)
            u = xs[r][at, :].astype(F32)
            first = first + jnp.sum(u * u, axis=1, keepdims=True)
        inv_out[at, :] = lax.rsqrt(first / WIDTH + EPS)
        inv = lax.rsqrt(square / WIDTH + EPS)
        back = inv * inv * inv * inner / WIDTH
        for r in range(PARTS):
            v = xm[at, quarter(me, r)].astype(F32)
            g = jnp.where(valid, gs[r][at, :].astype(F32), 0.0)
            d = g + inv * f_s[:, quarter(me, r)] - v * back
            if r == 0:
                dxq_out[at, :] = d
            z_s[at, quarter(me, r)] = d.astype(BF16)
        return carry

    lax.fori_loop(0, rows // ROW_BLOCK, norm_back, 0)
    dz = z_s[...]
    dto = nt(dz, ob[...])
    copies[0].wait()
    d_o = nt(dz, wo[...]) + nn(dto.astype(BF16), oa[...])
    dot_s[...] = d_o.T.astype(BF16)
    if last:
        for c in range(chunk + 1):
            dkt_s[c], dvt_s[c] = rest[2][...], rest[3][...]
    else:
        dkt_s[...] = jnp.zeros_like(dkt_s)
        dvt_s[...] = jnp.zeros_like(dvt_s)

    def one_head(i, carry):
        j = i // group
        q_h, do_h = qt[head_rows(i), :], dot_s[head_rows(i), :]
        dots = jnp.sum(do_h.astype(F32) * ot[head_rows(i), :].astype(F32), axis=0, keepdims=True)
        low = lse[pl.ds(i, 1), :]
        dq_h = jnp.zeros((HEAD, rows), F32)
        for c in range(chunk + 1):
            prob = jnp.exp(nn(keys[c][j], q_h) - low)
            prob = jnp.where(visible(c * rows, chunk * rows, rows, length), prob, 0.0)
            ds = (prob * (nn(values[c][j], do_h) - dots)).astype(BF16)
            dq_h = dq_h + nn(keys_t[c][head_rows(j), :], ds)
            dkt_s[c, head_rows(j), :] += nt(q_h, ds)
            dvt_s[c, head_rows(j), :] += nt(do_h, prob.astype(BF16))
        dqt_s[head_rows(i), :] = dq_h
        return carry

    lax.fori_loop(0, heads, one_head, 0, unroll=2)
    if not last:
        outs[6][...], outs[7][...] = dkt_s[0], dvt_s[0]
    cos, sin = cos_t[...], sin_t[...]
    dto_t, o_t = dto.T.astype(BF16), ot[...]
    d_out_a = nt(dto_t, o_t)
    turn_back(dqt_s[...], cos * (HEAD ** -0.5), sin * (HEAD ** -0.5), dot_s)
    dq_s[:, :q_cols] = dot_s[...].T
    turn_back(dkt_s[chunk], cos, sin, dot_s)
    dq_s[:, q_cols:q_cols + kv_cols] = dot_s[:kv_cols, :].T
    dq_s[:, q_cols + kv_cols:] = dvt_s[chunk].T.astype(BF16)
    dq, dk, dv = dq_s[:, :q_cols], dq_s[:, q_cols:q_cols + kv_cols], dq_s[:, q_cols + kv_cols:]
    dt1 = jnp.concatenate([nt(dq, qb[...]), nt(dk, kvb[0]), nt(dv, kvb[1])], axis=1)
    dt1b = dt1.astype(BF16)
    kv_pad = jnp.zeros((RANK, QUARTER - 2 * kv_cols), F32)
    d_kv = jnp.concatenate([nn(t1t[RANK:2 * RANK, :], dk), nn(t1t[2 * RANK:, :], dv), kv_pad], axis=1)
    for k, value in enumerate((nn(t1t[:RANK, :], dq), d_out_a, d_kv)):
        at = slice(k * RANK, (k + 1) * RANK)
        if last:
            value = value + rest[0][at, :]
        b_out[at, :] = value.astype(b_out.dtype)
    dt1t = dt1.T.astype(BF16)
    copies[1].wait()
    copies[2].wait()

    def block(r, inner):
        at = quarter(me, r)
        d = nt(dq_s[:, :q_cols], wq[at, :]) + nn(dt1b, a1[:, at])
        d = d + nt(dq_s[:, q_cols:q_cols + kv_cols], wkv[0, at, :]) + nt(dq_s[:, q_cols + kv_cols:], wkv[1, at, :])
        value_s[...] = d
        store_block(r, value_s, slice(0, rows), h_keep, h_send)
        low_s[:3 * RANK, :] = nn(dt1t, h_in[:, at])
        low_s[3 * RANK:, :] = nn(tot[...], z_s[:, at])
        if last:
            low_s[...] += rest[1][:, at]
            store_block(r, low_s, slice(0, 4 * RANK), outs[5], outs[6])
        else:
            outs[5][:, at] = low_s[...]
        return inner + jnp.sum(d * h_in[:, at].astype(F32), axis=1, keepdims=True)

    inner = lax.fori_loop(0, PARTS, block, jnp.zeros((rows, 1), F32))
    for ref in (h_keep, h_send):
        ref[:, 2 * QUARTER:] = jnp.broadcast_to(inner, (rows, LANES)).astype(ref.dtype)


def finish_kernel(gains, x_all, *refs):
    out = refs[-1]
    gain = gains[0, 0:1, :].astype(F32)
    rows = out.shape[0] // CHUNKS
    for c in range(CHUNKS):
        dx, low, high, got, inv = refs[5 * c:5 * (c + 1)]
        x = chunk_of(x_all, c, rows)
        inv = inv[...]
        inner = high[:rows, QUARTER:QUARTER + 1].astype(F32) + got[:rows, QUARTER:QUARTER + 1].astype(F32)
        scale = inv * inv * inner / WIDTH
        grad = inv * (gain * (low[:rows, :] + got[:rows, :QUARTER].astype(F32))) - x[...].astype(F32) * scale
        out[c * rows:(c + 1) * rows, :] = (dx[...] + grad).astype(BF16)


def split_refs(refs, counts):
    groups = []
    for count in counts:
        groups.append(refs[:count])
        refs = refs[count:]
    return groups, refs


def with_entry(parts, at, use):
    start = 0
    for ref in parts:
        @pl.when((at >= start) & (at < start + ref.shape[0]))
        def _(ref=ref, start=start):
            use(ref, at - start)
        start += ref.shape[0]


def sum_slots(info, owners, out_refs, one_slot):
    count = out_refs[0].shape[0]
    base = pl.program_id(0) * count
    slots = owners.shape[0]
    for ref in out_refs:
        ref[...] = jnp.zeros_like(ref)

    def add(slot, carry):
        owner = owners[slot] - base

        @pl.when((owner >= 0) & (owner < count))
        def _():
            one_slot(owner, entry_of(slot, info[3], slots))
        return carry

    lax.fori_loop(0, slots, add, 0)


def feedforward_sum_kernel(counts, info, owners, *refs):
    (b_parts, *a_parts), outs = split_refs(refs, counts)
    ga, gdb, gb, gda = outs
    me = info[0]

    def one_slot(owner, at):
        def add_b(ref, e):
            for i in range(gda.shape[2] // QUARTER):
                cols = slice(i * QUARTER, (i + 1) * QUARTER)
                base = i * 3 * RANK
                gb[owner, 0, :, cols] += ref[e, base:base + RANK, :].astype(F32)
                gb[owner, 1, :, cols] += ref[e, base + RANK:base + 2 * RANK, :].astype(F32)
                gda[owner, :, cols] += ref[e, base + 2 * RANK:base + 3 * RANK, :].astype(F32)

        with_entry(b_parts, at, add_b)
        for near_bit, parts in enumerate(a_parts):
            def add_a(ref, e, near_bit=near_bit):
                for r, cols in ((near_bit, LO), (near_bit ^ 2, HI)):
                    ga[owner, :, quarter(me, r)] += ref[e, :2 * RANK, cols].astype(F32)
                    gdb[owner, :, quarter(me, r)] += ref[e, 2 * RANK:, cols].astype(F32)

            with_entry(parts, at, add_a)

    sum_slots(info, owners, outs, one_slot)


def attention_sum_kernel(counts, info, owners, *refs):
    (b_parts, *a_parts), outs = split_refs(refs, counts)
    ga, gob, gq, gkv, goa = outs
    me = info[0]
    kv_cols = gkv.shape[3]

    def one_slot(owner, at):
        def add_b(ref, e):
            gq[owner] += ref[e, :RANK, :].astype(F32)
            goa[owner] += ref[e, RANK:2 * RANK, :].astype(F32)
            gkv[owner, 0] += ref[e, 2 * RANK:3 * RANK, :kv_cols].astype(F32)
            gkv[owner, 1] += ref[e, 2 * RANK:3 * RANK, kv_cols:2 * kv_cols].astype(F32)

        with_entry(b_parts, at, add_b)
        for r, parts in enumerate(a_parts):
            def add_a(ref, e, r=r):
                ga[owner, :, quarter(me, r)] += ref[e, :3 * RANK, :].astype(F32)
                gob[owner, :, quarter(me, r)] += ref[e, 3 * RANK:, :].astype(F32)

            with_entry(parts, at, add_a)

    sum_slots(info, owners, outs, one_slot)


def deal_kernel(slots, source, out, sems):
    made = [pltpu.make_async_copy(source.at[i], out.at[slots[i]], sems.at[i]) for i in range(source.shape[0])]
    for copy in made:
        copy.start()
    for copy in made:
        copy.wait()


def collect_kernel(slots, source, out, sems):
    made = [pltpu.make_async_copy(source.at[slots[i]], out.at[i], sems.at[i]) for i in range(source.shape[0])]
    for copy in made:
        copy.start()
    for copy in made:
        copy.wait()


def load_kernel(count, *refs):
    made = [pltpu.make_async_copy(refs[i], refs[count + i], refs[-1].at[i]) for i in range(count)]
    for copy in made:
        copy.start()
    for copy in made:
        copy.wait()


def adapter_kernel(count, info, *refs):
    made = [pltpu.make_async_copy(refs[i].at[info[2]], refs[count + i], refs[-1].at[i]) for i in range(count)]
    for copy in made:
        copy.start()
    for copy in made:
        copy.wait()


def load(arrays, name, info=None, after=()):
    count = len(arrays)
    scalars = () if info is None else (info,)
    kernel = load_kernel if info is None else adapter_kernel
    shapes = [a.shape if info is None else a.shape[1:] for a in arrays]

    def body(*refs):
        at = len(scalars) + count
        kernel(count, *refs[:at], *refs[at + len(after):])

    return pl.pallas_call(
        body,
        in_specs=[pl.BlockSpec(memory_space=pltpu.SMEM)] * len(scalars) + [pl.BlockSpec(memory_space=pltpu.HBM)] * count
        + [pl.BlockSpec(memory_space=pl.ANY)] * len(after),
        out_specs=[pl.BlockSpec(memory_space=pltpu.VMEM)] * count,
        out_shape=[pltpu.VMEM(tuple(s), a.dtype) for s, a in zip(shapes, arrays)],
        scratch_shapes=[pltpu.SemaphoreType.DMA((count,))],
        compiler_params=pltpu.CompilerParams(vmem_limit_bytes=MIB),
        cost_estimate=pl.CostEstimate(flops=1000, transcendentals=0, bytes_accessed=1000),
        name=name,
    )(*scalars, *(in_hbm(a) for a in arrays), *after)


def move_rows(kernel, value, slots, name, here):
    space = pltpu.VMEM if here else pl.ANY
    return pl.pallas_call(
        kernel,
        in_specs=[pl.BlockSpec(memory_space=pltpu.SMEM), pl.BlockSpec(memory_space=pl.ANY if here else pltpu.VMEM)],
        out_specs=pl.BlockSpec(memory_space=space),
        out_shape=(pltpu.VMEM if here else jax.ShapeDtypeStruct)(value.shape, value.dtype),
        scratch_shapes=[pltpu.SemaphoreType.DMA((value.shape[0],))],
        compiler_params=pltpu.CompilerParams(vmem_limit_bytes=MIB),
        cost_estimate=pl.CostEstimate(flops=1000, transcendentals=0, bytes_accessed=1000),
        name=name,
    )(slots, in_hbm(value) if here else in_vmem(value))


def sds(shape, dtype):
    return jax.ShapeDtypeStruct(tuple(shape), dtype)


def in_vmem(value):
    return pltpu.with_memory_space_constraint(value, pltpu.VMEM)


def in_hbm(value):
    return pltpu.with_memory_space_constraint(value, pltpu.HBM)


def call(kernel, info, weights, args, outs, scratch, name, mib, after=(), sems=()):
    vmem = pl.BlockSpec(memory_space=pltpu.VMEM)
    scalars = () if info is None else (info,)
    n, w = len(scalars), len(weights)

    def body(*refs):
        at = n + w + len(args)
        kernel(*refs[:at], *refs[at + len(after):])

    return pl.pallas_call(
        body,
        in_specs=[pl.BlockSpec(memory_space=pltpu.SMEM)] * n + [pl.BlockSpec(memory_space=pltpu.HBM)] * w + [vmem] * len(args)
        + [pl.BlockSpec(memory_space=pl.ANY)] * len(after),
        out_specs=[vmem] * len(outs),
        out_shape=[pltpu.VMEM(tuple(s), d) for s, d in outs],
        scratch_shapes=[pltpu.VMEM(s, d) for s, d in scratch] + ([pltpu.SemaphoreType.DMA(sems)] if sems else []),
        compiler_params=pltpu.CompilerParams(vmem_limit_bytes=mib * MIB),
        cost_estimate=pl.CostEstimate(flops=1000, transcendentals=0, bytes_accessed=1000),
        name=name,
    )(*scalars, *(in_hbm(a) for a in weights), *(in_vmem(a) for a in args), *after)


def sum_call(kernel, scalars, groups, outs, name):
    args = [v for group in groups for v in group]
    steps = 2
    specs = [pl.BlockSpec((o.shape[0] // steps,) + o.shape[1:], (lambda n: lambda i, *_: (i,) + (0,) * n)(o.ndim - 1))
             for o in outs]
    return pl.pallas_call(
        functools.partial(kernel, [len(group) for group in groups]),
        grid_spec=pltpu.PrefetchScalarGridSpec(
            num_scalar_prefetch=len(scalars), grid=(steps,),
            in_specs=[pl.BlockSpec(memory_space=pltpu.VMEM)] * len(args), out_specs=specs),
        out_shape=outs,
        compiler_params=pltpu.CompilerParams(
            dimension_semantics=("arbitrary",),
            vmem_limit_bytes=4 * MIB + sum(a.size * a.dtype.itemsize for a in args)
            + sum(o.size * o.dtype.itemsize for o in outs)),
        cost_estimate=pl.CostEstimate(flops=0, transcendentals=0, bytes_accessed=12000000),
        name=name,
    )(*scalars, *(in_vmem(a) for a in args))


def swap(value, bit, axis, size):
    return lax.ppermute(value, axis, [(i, i ^ bit) for i in range(size)])


def near(value):
    return swap(value, 1, "mp", PARTS)


def far(value):
    return swap(value, 2, "mp", PARTS)


def spread(value):
    there = far(value)
    return (value, near(value), there, near(there))


def chip_sum(keep, send):
    got = near(send)
    lo = keep[:, :QUARTER].astype(F32) + got[:, :QUARTER].astype(F32)
    hi = keep[:, QUARTER:].astype(F32) + got[:, QUARTER:].astype(F32)
    return lo, hi.astype(BF16)


def far_sum_kernel(own, got, out):
    for to, other in ((LO, HI), (HI, LO)):
        out[:, to] = (own[:, to].astype(F32) + got[:, other].astype(F32)).astype(BF16)


def far_sum(own, got):
    return call(far_sum_kernel, None, (), (own, got), [(own.shape, BF16)], [], "far_sum", 6)[0]


def pair_sum_kernel(keep, got, out):
    out[...] = (keep[...] + got[...].astype(F32)).astype(BF16)


def pair_sum(keep, send):
    return call(pair_sum_kernel, None, (), (keep, near(send)), [(send.shape, BF16)], [], "pair_sum", 6)[0]


def late(value, *others):
    return lax.optimization_barrier((value, *others))[0]


def doubled(stack, bit, size):
    return jnp.concatenate([stack, swap(stack, bit, "dp", size)], axis=0)


def entry_of(slot, place, size):
    bits = size.bit_length() - 1
    apart = slot ^ place
    return sum(((apart >> b) & 1) << (bits - 1 - b) for b in range(bits))


def shards(dp, residual, attention_gain, query_matrix, key_value_matrix, output_matrix, feedfwd_gain,
           gate_up_matrix, down_matrix, attention_adapter_input, query_adapter_output,
           key_value_adapter_output, output_adapter_input, output_adapter_output, feedfwd_adapter_input,
           feedfwd_adapter_output, down_adapter_input, down_adapter_output, lengths, adapter_index,
           dealing_slots, cotangent):
    seqs = residual.shape[0]
    length = cotangent.shape[1]
    units = down_matrix.shape[0]
    adapters = attention_adapter_input.shape[0]
    q_cols = query_matrix.shape[1]
    kv_cols = key_value_matrix.shape[2]
    kv_heads = kv_cols // HEAD
    heads = q_cols // HEAD
    rows = length // CHUNKS
    half = 2 * QUARTER
    me = lax.axis_index("mp")
    place = lax.axis_index("dp")

    is_there = dealing_slots[None, :] == jnp.arange(seqs, dtype=jnp.int32)[:, None]
    owners = jnp.sum(jnp.where(is_there, adapter_index[None, :], 0), axis=1)
    spans = jnp.sum(jnp.where(is_there, lengths[None, :], 0), axis=1)
    mine = jnp.arange(seqs, dtype=jnp.int32) == place
    my_length = jnp.sum(jnp.where(mine, spans, 0))
    my_adapter = jnp.sum(jnp.where(mine, owners, 0))
    info = jnp.stack([me.astype(jnp.int32), my_length, my_adapter, place.astype(jnp.int32)])

    gs = spread(cotangent[0])
    gains = jnp.stack(spread(jnp.stack([attention_gain, feedfwd_gain])))
    dealt = lax.all_to_all(
        move_rows(deal_kernel, residual, dealing_slots, "deal", True), "dp", split_axis=0, concat_axis=1, tiled=True
    )[0]
    adapters_here = load(
        (attention_adapter_input, query_adapter_output, key_value_adapter_output, output_adapter_input,
         output_adapter_output, feedfwd_adapter_input, feedfwd_adapter_output, down_adapter_input,
         down_adapter_output), "adapters", info)
    a1, qb, kvb, oa, ob, a2, fba, da, bd = adapters_here
    dealt = late(dealt, gs[2], a1)
    beside = near(dealt)
    there = [far(dealt[c * rows:(c + 1) * rows]) for c in range(CHUNKS)]
    xs = [None] * CHUNKS
    cos_np, sin_np = rope_tables(length)
    cos = [jnp.asarray(cos_np[:, c * rows:(c + 1) * rows]) for c in range(CHUNKS)]
    sin = [jnp.asarray(sin_np[:, c * rows:(c + 1) * rows]) for c in range(CHUNKS)]
    wq, wkv, wo, wgu, wd = query_matrix, key_value_matrix, output_matrix, gate_up_matrix, down_matrix

    def like(*arrays):
        return [(a.shape, a.dtype) for a in arrays]

    wide, col, block, thin = (rows, WIDTH), (rows, half), (rows, QUARTER), (rows, 1)
    saved = [None] * CHUNKS
    order = ()
    for c in range(CHUNKS):
        xs[c] = (dealt, beside, there[c], near(late(there[c], *order)))
        outs = [(wide, BF16), ((3 * RANK, rows), BF16), ((q_cols, rows), BF16), ((kv_heads, rows, HEAD), BF16),
                ((kv_heads, rows, HEAD), BF16), ((kv_cols, rows), BF16), ((kv_cols, rows), BF16)]
        saved[c] = call(
            functools.partial(project_kernel, c), info, (wq, wkv), (*xs[c], gains, a1, qb, kvb, cos[c], sin[c]), outs,
            like(wq, wkv), "project_%d" % c, 12, order, (2,))
        order = (saved[c][1],)

    kept, z_own = [None] * CHUNKS, [None] * CHUNKS
    for c in reversed(range(CHUNKS)):
        outs = [(col, F32), (col, BF16), ((q_cols, rows), BF16), ((heads, rows), F32), ((RANK, rows), BF16)]
        pairs = [v for p in saved[:c + 1] for v in (p[3], p[6])]
        z_keep, z_send, *kept[c] = call(
            functools.partial(attend_kernel, c), info, (wo,), (saved[c][2], oa, ob, *pairs), outs, like(wo),
            "attend_%d" % c, 10, order, (1,))
        z_own[c] = pair_sum(z_keep, z_send)
        order = (kept[c][1], z_own[1])
    z_far = [far(v) for v in z_own]
    wgu, wd = load((wgu, wd), "load", None, order)

    def front(c, total, partial, order):
        hidden = (rows, units)
        outs = [(wide, BF16), (block, F32), (wide, BF16), (wide, BF16), (hidden, BF16), (hidden, BF16), (hidden, BF16),
                ((rows, 2 * RANK), BF16), ((rows, RANK), BF16),
                ((3 * RANK * units // QUARTER, QUARTER), F32 if c else BF16)]
        return call(
            functools.partial(front_kernel, c, c == 0), info, (),
            (wgu, wd, *xs[c], total, near(total), *gs, gains, a2, bd, fba, da, *partial), outs,
            [((ROW_BLOCK, WIDTH), F32)], "front_%d" % c, 8, order)

    def back(c, hidden, partial, order):
        first = col if c else (rows + 3 * RANK, half)
        outs = [(first, F32), (first, BF16), (col, F32), (col, BF16)]
        outs += [((3 * RANK, WIDTH), F32)] if c else []
        return call(
            functools.partial(back_kernel, c == 0), info, (), (wgu, wd, *hidden[2:7], a2, bd, fba, da, *partial), outs,
            [(block, F32), ((3 * RANK, QUARTER), F32)], "back_%d" % c, 8, order)

    def attend_back(c, total, partial, order):
        padded = (rows, half + LANES)
        outs = [(block, F32), (padded, F32), (padded, BF16), (thin, F32), ((3 * RANK, QUARTER), F32 if c else BF16)]
        outs += ([((4 * RANK, WIDTH), F32), ((kv_cols, rows), F32), ((kv_cols, rows), F32)] if c
                 else [((4 * RANK, half), F32), ((4 * RANK, half), BF16)])
        scratch = [(wide, BF16), ((ROW_BLOCK, WIDTH), F32), ((q_cols, rows), BF16), ((q_cols, rows), F32),
                   ((c + 1, kv_cols, rows), F32), ((c + 1, kv_cols, rows), F32), ((rows, q_cols + 2 * kv_cols), BF16),
                   (block, F32), ((4 * RANK, QUARTER), F32)]
        triples = [v for p in saved[:c + 1] for v in (p[3], p[4], p[5])]
        return call(
            functools.partial(attend_back_kernel, c, c == 0), info, (wq, wkv, wo),
            (*xs[c], *gs, hidden[c][0], total, near(total), gains, a1, qb, kvb, oa, ob, cos[c], sin[c], *saved[c][:3],
             *kept[c], *triples, *partial), outs, scratch + like(wq, wkv, wo), "attend_back_%d" % c, 18, order, (3,))

    bits = [1 << b for b in reversed(range(dp.bit_length() - 1))]
    hidden, d_own, d_far = ([None] * CHUNKS for _ in range(3))
    hidden[1] = front(1, far_sum(z_own[1], late(z_far[1], wd)), (), order)
    step = hidden[1][8]
    total = far_sum(z_own[0], late(z_far[0], step))
    d_keep, d_send, y_keep_1, y_send_1, fa = back(1, hidden[1], (), (step, total))
    d_own[1] = pair_sum(d_keep, d_send)
    d_far[1] = far(d_own[1])
    hidden[0] = front(0, total, hidden[1][9:], (d_own[1],))
    step = hidden[0][8]
    total = far_sum(d_own[1], late(d_far[1], step))
    fb = hidden[0][9][None]
    fb_first = swap(fb, bits[0], "dp", dp)
    y_keep, y_got = [None, y_keep_1], [None, near(y_send_1)]

    def y_high(c, *others):
        return (y_keep[c][:, QUARTER:] + late(y_got[c], *others)[:, QUARTER:].astype(F32)).astype(BF16)

    high = y_high(1, step)
    y_far = [None, far(high)]
    d_keep, d_send, y_keep[0], y_send_0 = back(0, hidden[0], (fa,), (step, total, high))
    d_own[0] = pair_sum(d_keep, late(d_send, fb_first, y_far[1]))
    d_far[0] = far(d_own[0])
    fb = fb_more = jnp.concatenate([fb, fb_first], axis=0)
    for bit in bits[1:-1]:
        fb_more = doubled(fb_more, bit, dp)
    fb_more = fb_more[2:]
    fb_side = swap(fb, bits[-1], "dp", dp)
    y_got[0] = near(y_send_0)
    dxq, h_keep, h_send, inv, *sums = attend_back(1, total, (), (d_own[0],))
    total = far_sum(d_own[0], late(d_far[0], inv))
    h_low, h_high = chip_sum(h_keep, late(h_send, fb_more, fb_side, d_far[0]))
    h_far = far(h_high)
    final = [None, (dxq, h_low, h_high, h_far, inv)]
    high = y_high(0, h_high)
    y_far[0] = far(high)
    fa = total[rows:][None]
    fa_first = swap(fa, bits[0], "dp", dp)
    fb_more_side = swap(fb_more, bits[-1], "dp", dp)
    dxq, h_keep, h_send, inv, att_b, aa_keep, aa_send = attend_back(0, total, sums, (h_high, high))
    ready = (fa_first, fb_more_side, h_far, y_far[0])
    aa_low, aa_high = chip_sum(aa_keep, late(aa_send, *ready))
    aa_far = far(aa_high)
    h_low, h_high = chip_sum(h_keep, late(h_send, *ready))
    h_far = far(h_high)
    final[0] = (dxq, h_low, h_high, h_far, inv)
    att = jnp.concatenate([att_b, (aa_low + late(aa_far, h_high).astype(F32)).astype(BF16)], axis=0)[None]
    att = doubled(att, bits[0], dp)

    valid = (jnp.arange(length, dtype=jnp.int32) < my_length)[:, None]
    result = jnp.concatenate(
        [hidden[c][1] + y_keep[c][:, :QUARTER] + late(y_got[c], h_high)[:, :QUARTER].astype(F32) + y_far[c].astype(F32)
         for c in range(CHUNKS)], axis=0)
    result = jnp.where(valid, result, 0.0).astype(BF16)
    back_out = lax.all_to_all(
        result.reshape(dp, length // dp, QUARTER), "dp", split_axis=0, concat_axis=0, tiled=True)
    output = move_rows(collect_kernel, back_out, dealing_slots, "collect_out", False)

    dinput, = call(finish_kernel, None, (), (gains, dealt, *(v for f in final for v in f)), [((length, QUARTER), BF16)],
                   [], "finish", 8, (att,))
    back_grad = lax.all_to_all(
        dinput.reshape(dp, length // dp, QUARTER), "dp", split_axis=0, concat_axis=0, tiled=True)
    input_grad = move_rows(collect_kernel, back_grad, late(dealing_slots, output), "collect_grad", False)

    n_b = att_b.shape[0]
    att = late(att, h_far)
    for bit in bits[1:-1]:
        att = doubled(att, bit, dp)
    att_side = swap(att, bits[-1], "dp", dp)
    a_parts = [att[:, n_b:], att_side[:, n_b:]]
    a_far = [far(v) for v in a_parts]
    fa = late(jnp.concatenate([fa, fa_first], axis=0), h_high)
    for bit in bits[1:-1]:
        fa = doubled(fa, bit, dp)
    fa_side = swap(fa, bits[-1], "dp", dp)
    outs = [sds((adapters, 2 * RANK, WIDTH), F32), sds((adapters, RANK, WIDTH), F32),
            sds((adapters, 2, RANK, units), F32), sds((adapters, RANK, units), F32)]
    ga_ffn, g_down_b, g_ffn_b, g_down_a = sum_call(
        feedforward_sum_kernel, (info, owners),
        ((fb, fb_more, fb_side, fb_more_side), (fa, fa_side), (near(fa), near(fa_side))), outs, "feedforward_sum")

    outs = [sds((adapters, 3 * RANK, WIDTH), F32), sds((adapters, RANK, WIDTH), F32),
            sds((adapters, RANK, q_cols), F32), sds((adapters, 2, RANK, kv_cols), F32),
            sds((adapters, RANK, q_cols), F32)]
    ga_att, g_out_b, g_query_b, g_kv_b, g_out_a = sum_call(
        attention_sum_kernel, (info, owners),
        ((att, att_side), a_parts, [near(v) for v in a_parts], a_far, (near(a_far[0]), near(late(a_far[1], g_down_a)))), outs, "attention_sum")
    return (output, input_grad, ga_att, g_query_b, g_kv_b, g_out_a, g_out_b, ga_ffn, g_ffn_b, g_down_a, g_down_b)


def solution(mesh):
    in_specs = (
        P(None, "dp", "mp"), P("mp"), P(None, "mp"), P(None, None, "mp"), P("mp", None), P("mp"),
        P(None, None, "mp"), P("mp", None), P(), P(None, None, "mp"), P(None, None, None, "mp"),
        P(None, None, "mp"), P(), P(), P(None, None, None, "mp"), P(None, None, "mp"), P(), P(), P(), P(),
        P("dp", None, "mp"),
    )
    out_specs = (
        P(None, "dp", "mp"), P(None, "dp", "mp"), P(), P(None, None, "mp"), P(None, None, None, "mp"),
        P(None, None, "mp"), P(), P(), P(None, None, None, "mp"), P(None, None, "mp"), P(),
    )
    return jax.shard_map(
        functools.partial(shards, mesh.shape["dp"]), mesh=mesh, in_specs=in_specs, out_specs=out_specs,
        check_vma=False)
```

```python
import functools

import jax
import jax.numpy as jnp
import numpy as np
from jax import lax
from jax.experimental import pallas as pl
from jax.experimental.pallas import tpu as pltpu
from jax.sharding import PartitionSpec as P

WIDTH = 2048
HEAD = 64
HALF = HEAD // 2
RANK = 16
EPS = 1e-05
ROPE_BASE = 500000.0
NEG_FILL = -1e30
PARTS = 4
LANES = 128
ROW_BLOCK = 64
QUARTER = WIDTH // PARTS
CHUNKS = 2
MIB = 1024 * 1024
F32 = jnp.float32
BF16 = jnp.bfloat16


def nn(a, b):
    return lax.dot_general(a, b, (((1,), (0,)), ((), ())), preferred_element_type=F32)


def nt(a, b):
    return lax.dot_general(a, b, (((1,), (1,)), ((), ())), preferred_element_type=F32)


def rope_tables(length):
    freq = ROPE_BASE ** (-np.arange(HALF, dtype=np.float32) * np.float32(2.0 / HEAD))
    angles = (np.arange(length, dtype=np.float32)[None, :] * freq.astype(np.float32)[:, None]).astype(np.float32)
    return np.cos(angles).astype(np.float32), np.sin(angles).astype(np.float32)


def quarter(me, rel):
    return pl.ds(pl.multiple_of((me ^ rel) * QUARTER, QUARTER), QUARTER)


LO, HI = slice(0, QUARTER), slice(QUARTER, 2 * QUARTER)


def total_block(rel, rows_at, own, oth):
    return (own if rel in (0, 2) else oth)[rows_at, LO if rel in (0, 1) else HI].astype(F32)


def store_block(rel, value, rows_at, keep_ref, send_ref):
    to = pl.ds(pl.multiple_of((rel // 2) * QUARTER, QUARTER), QUARTER)

    @pl.when(rel % 2 == 0)
    def _():
        keep_ref[rows_at, to] = value[...]

    @pl.when(rel % 2 == 1)
    def _():
        send_ref[rows_at, to] = value[...].astype(BF16)


def chunk_of(ref, chunk, rows):
    return ref if ref.shape[0] == rows else ref.at[chunk * rows:(chunk + 1) * rows]


def row_block(i):
    return pl.ds(pl.multiple_of(i * ROW_BLOCK, ROW_BLOCK), ROW_BLOCK)


def is_valid(chunk, i, rows, length):
    return chunk * rows + i * ROW_BLOCK + lax.broadcasted_iota(jnp.int32, (ROW_BLOCK, 1), 0) < length


def copies_of(pairs, sems):
    made = [pltpu.make_async_copy(source, target, sems.at[i]) for i, (source, target) in enumerate(pairs)]
    for copy in made:
        copy.start()
    return made


def put_block(rel, value, keep_ref, send_ref):
    ref = keep_ref if rel in (0, 2) else send_ref
    ref[:, LO if rel in (0, 1) else HI] = value.astype(ref.dtype)


def rotate(value, cos, sin, out_ref):
    for i in range(value.shape[0] // HEAD):
        u1, u2 = value[i * HEAD:i * HEAD + HALF], value[i * HEAD + HALF:(i + 1) * HEAD]
        out_ref[i * HEAD:i * HEAD + HALF, :] = (u1 * cos - u2 * sin).astype(BF16)
        out_ref[i * HEAD + HALF:(i + 1) * HEAD, :] = (u2 * cos + u1 * sin).astype(BF16)


def turn_back(value, cos, sin, out_ref):
    for i in range(value.shape[0] // HEAD):
        w1, w2 = value[i * HEAD:i * HEAD + HALF], value[i * HEAD + HALF:(i + 1) * HEAD]
        out_ref[i * HEAD:i * HEAD + HALF, :] = (w1 * cos + w2 * sin).astype(BF16)
        out_ref[i * HEAD + HALF:(i + 1) * HEAD, :] = (w2 * cos - w1 * sin).astype(BF16)


def head_rows(i):
    return pl.ds(pl.multiple_of(i * HEAD, HEAD), HEAD)


def visible(key_start, query_start, rows, length):
    kpos = key_start + lax.broadcasted_iota(jnp.int32, (rows, rows), 0)
    qpos = query_start + lax.broadcasted_iota(jnp.int32, (rows, rows), 1)
    return (kpos <= qpos) & (kpos < length)


def project_kernel(chunk, info, wq_h, wkv_h, x0, x1, x2, x3, gains, a1, qb, kvb, cos_t, sin_t,
                   h_out, t1t_out, qt_out, kn_out, vn_out, kt_out, vt_out, wq, wkv, sems):
    copies = copies_of(((wkv_h, wkv), (wq_h, wq)), sems)
    me = info[0]
    rows = h_out.shape[0]
    kv_heads = kn_out.shape[0]
    xs = [chunk_of(x, chunk, rows) for x in (x0, x1, x2, x3)]

    def norm(i, carry):
        at = row_block(i)
        square = jnp.zeros((ROW_BLOCK, 1), F32)
        for r in range(PARTS):
            v = xs[r][at, :].astype(F32)
            square = square + jnp.sum(v * v, axis=1, keepdims=True)
        inv = lax.rsqrt(square / WIDTH + EPS)
        for r in range(PARTS):
            v = xs[r][at, :].astype(F32)
            h_out[at, quarter(me, r)] = (v * inv * gains[r, 0:1, :].astype(F32)).astype(BF16)
        return carry

    lax.fori_loop(0, rows // ROW_BLOCK, norm, 0)
    h = h_out[...]
    t1 = nt(h, a1[...])
    t1t_out[...] = t1.T.astype(BF16)
    t1b = t1.astype(BF16)
    cos, sin = cos_t[...], sin_t[...]
    copies[0].wait()
    k = nn(h, wkv[0]) + nn(t1b[:, RANK:2 * RANK], kvb[0])
    rotate(k.T, cos, sin, kt_out)
    k_n = kt_out[...].T
    v_n = (nn(h, wkv[1]) + nn(t1b[:, 2 * RANK:], kvb[1])).astype(BF16)
    vt_out[...] = v_n.T
    for i in range(kv_heads):
        kn_out[i] = k_n[:, i * HEAD:(i + 1) * HEAD]
        vn_out[i] = v_n[:, i * HEAD:(i + 1) * HEAD]
    copies[1].wait()
    q = nn(h, wq[...]) + nn(t1b[:, :RANK], qb[...])
    rotate(q.T * (HEAD ** -0.5), cos, sin, qt_out)


def attend_kernel(chunk, info, wo_h, qt, oa, ob, *rest):
    pairs, rest = rest[:2 * (chunk + 1)], rest[2 * (chunk + 1):]
    z_keep, z_send, ot_out, lse_out, tot_out, wo, sems = rest
    copies = copies_of(((wo_h, wo),), sems)
    keys, values = pairs[0::2], pairs[1::2]
    me, length = info[0], info[1]
    rows = qt.shape[1]
    kv_heads = keys[0].shape[0]
    heads = qt.shape[0] // HEAD
    group = heads // kv_heads

    kept = [jnp.concatenate([visible(c * rows, chunk * rows, rows, length)] * group, axis=1) for c in range(chunk + 1)]

    def one_group(j, carry):
        q_g = jnp.concatenate([qt[head_rows(j * group + g), :] for g in range(group)], axis=1)
        parts = [jnp.where(kept[c], nn(keys[c][j], q_g), NEG_FILL) for c in range(chunk + 1)]
        top = functools.reduce(jnp.maximum, [jnp.max(s, axis=0, keepdims=True) for s in parts])
        es = [jnp.exp(s - top) for s in parts]
        total = sum(jnp.sum(e, axis=0, keepdims=True) for e in es)
        low = top + jnp.log(total)
        o_t = sum(nn(value[head_rows(j), :], e.astype(BF16)) for value, e in zip(values, es))
        o_t = (o_t / total).astype(BF16)
        for g in range(group):
            cols = slice(g * rows, (g + 1) * rows)
            lse_out[pl.ds(j * group + g, 1), :] = low[:, cols]
            ot_out[head_rows(j * group + g), :] = o_t[:, cols]
        return carry

    lax.fori_loop(0, kv_heads, one_group, 0)
    o = ot_out[...].T
    to = nt(o, oa[...])
    tot_out[...] = to.T.astype(BF16)
    to = to.astype(BF16)
    copies[0].wait()
    for r in range(PARTS):
        at = quarter(me, r)
        put_block(r, nn(o, wo[:, at]) + nn(to, ob[:, at]), z_keep, z_send)


def front_kernel(chunk, last, info, wgu, wd, x0, x1, x2, x3, zo, zp, g0, g1, g2, g3, gains, a2, bd, fb, da,
                 *rest):
    f_s = rest[-1]
    xm_out, xq_out, h_out, g_out, act_out, dg_out, du_out, t2_s, dtd_s, b_out = rest[-11:-1]
    units = wd.shape[0]
    me, length = info[0], info[1]
    rows = h_out.shape[0]
    xs, gs = ([chunk_of(v, chunk, rows) for v in vs] for vs in ((x0, x1, x2, x3), (g0, g1, g2, g3)))

    def norm(i, carry):
        at = row_block(i)
        valid = is_valid(chunk, i, rows, length)
        square = jnp.zeros((ROW_BLOCK, 1), F32)
        for r in range(PARTS):
            v = xs[r][at, :].astype(F32) + total_block(r, at, zo, zp)
            if r == 0:
                xq_out[at, :] = v
            f_s[:, quarter(me, r)] = v
            square = square + jnp.sum(v * v, axis=1, keepdims=True)
            g_out[at, quarter(me, r)] = jnp.where(valid, gs[r][at, :], jnp.zeros((), BF16))
        inv = lax.rsqrt(square / WIDTH + EPS)
        for r in range(PARTS):
            v = f_s[:, quarter(me, r)]
            xm_out[at, quarter(me, r)] = v.astype(BF16)
            h_out[at, quarter(me, r)] = (v * inv * gains[r, 1:2, :].astype(F32)).astype(BF16)
        return carry

    lax.fori_loop(0, rows // ROW_BLOCK, norm, 0)
    t2 = nt(h_out[...], a2[...])
    t2_s[...] = t2.astype(BF16)
    dtd = nt(g_out[...], bd[...])
    dtd_s[...] = dtd.astype(BF16)
    t2t, dtdt = t2.T.astype(BF16), dtd.T.astype(BF16)

    def block(i, carry):
        c = pl.ds(pl.multiple_of(i * QUARTER, QUARTER), QUARTER)
        h, g = h_out[...], g_out[...]
        gate = nn(h, wgu[0, :, c]) + nn(t2_s[:, :RANK], fb[0, :, c])
        up = nn(h, wgu[1, :, c]) + nn(t2_s[:, RANK:], fb[1, :, c])
        dact = nt(g, wd[c, :]) + nn(dtd_s[...], da[:, c])
        sig = 1.0 / (1.0 + jnp.exp(-gate))
        silu = gate * sig
        act = (silu * up).astype(BF16)
        dgate = (dact * up * sig * (1.0 + gate * (1.0 - sig))).astype(BF16)
        dup = (dact * silu).astype(BF16)
        act_out[:, c], dg_out[:, c], du_out[:, c] = act, dgate, dup
        for k, value in enumerate((nn(t2t[:RANK], dgate), nn(t2t[RANK:], dup), nn(dtdt, act))):
            at = pl.ds(pl.multiple_of((3 * i + k) * RANK, RANK), RANK)
            if last:
                value = value + rest[0][at, :]
            b_out[at, :] = value.astype(b_out.dtype)
        return carry

    lax.fori_loop(0, units // QUARTER, block, 0)


def back_kernel(last, info, wgu, wd, h, g, act, dg, du, a2, bd, fb, da, *rest):
    (value_s, low_s), rest = rest[-2:], rest[:-2]
    outs, rest = (rest[-4:], rest[:-4]) if last else (rest[-5:], rest[:-5])
    d_keep, d_send, y_keep, y_send = outs[:4]
    me = info[0]
    rows = h.shape[0]
    own = slice(0, rows)

    dt2 = jnp.concatenate([nt(dg[...], fb[0]), nt(du[...], fb[1])], axis=1)
    dt2b = dt2.astype(BF16)
    td = nt(act[...], da[...])
    tdb = td.astype(BF16)
    dt2t, tdt = dt2.T.astype(BF16), td.T.astype(BF16)

    def block(r, carry):
        at = quarter(me, r)
        value_s[...] = nt(dg[...], wgu[0, at, :]) + nt(du[...], wgu[1, at, :]) + nn(dt2b, a2[:, at])
        store_block(r, value_s, own, d_keep, d_send)
        value_s[...] = nn(act[...], wd[:, at]) + nn(tdb, bd[:, at])
        store_block(r, value_s, own, y_keep, y_send)
        low_s[:2 * RANK, :] = nn(dt2t, h[:, at])
        low_s[2 * RANK:, :] = nn(tdt, g[:, at])
        if last:
            low_s[...] += rest[0][:, at]
            store_block(r, low_s, slice(rows, rows + 3 * RANK), d_keep, d_send)
        else:
            outs[4][:, at] = low_s[...]
        return carry

    lax.fori_loop(0, PARTS, block, 0)


def attend_back_kernel(chunk, last, info, wq_h, wkv_h, wo_h, x0, x1, x2, x3, g0, g1, g2, g3, xm, do_, dp, gains, a1,
                       qb, kvb, oa, ob, cos_t, sin_t, h_in, t1t, qt, ot, lse, tot, *rest):
    scratch, rest = rest[-13:], rest[:-13]
    z_s, f_s, dot_s, dqt_s, dkt_s, dvt_s, dq_s, value_s, low_s, wq, wkv, wo, sems = scratch
    copies = copies_of(((wo_h, wo), (wq_h, wq), (wkv_h, wkv)), sems)
    n_out = 7 if last else 8
    outs, rest = rest[-n_out:], rest[:-n_out]
    dxq_out, h_keep, h_send, inv_out, b_out = outs[:5]
    triples, rest = rest[:3 * (chunk + 1)], rest[3 * (chunk + 1):]
    keys, values, keys_t = triples[0::3], triples[1::3], triples[2::3]
    me, length = info[0], info[1]
    rows = xm.shape[0]
    kv_heads = keys[0].shape[0]
    heads = qt.shape[0] // HEAD
    group = heads // kv_heads
    q_cols, kv_cols = heads * HEAD, kv_heads * HEAD
    xs, gs = ([chunk_of(v, chunk, rows) for v in vs] for vs in ((x0, x1, x2, x3), (g0, g1, g2, g3)))

    def norm_back(i, carry):
        at = row_block(i)
        valid = is_valid(chunk, i, rows, length)
        square, first, inner = (jnp.zeros((ROW_BLOCK, 1), F32) for _ in range(3))
        for r in range(PARTS):
            v = xm[at, quarter(me, r)].astype(F32)
            square = square + jnp.sum(v * v, axis=1, keepdims=True)
            w = total_block(r, at, do_, dp) * gains[r, 1:2, :].astype(F32)
            f_s[:, quarter(me, r)] = w
            inner = inner + jnp.sum(v * w, axis=1, keepdims=True)
            u = xs[r][at, :].astype(F32)
            first = first + jnp.sum(u * u, axis=1, keepdims=True)
        inv_out[at, :] = lax.rsqrt(first / WIDTH + EPS)
        inv = lax.rsqrt(square / WIDTH + EPS)
        back = inv * inv * inv * inner / WIDTH
        for r in range(PARTS):
            v = xm[at, quarter(me, r)].astype(F32)
            g = jnp.where(valid, gs[r][at, :].astype(F32), 0.0)
            d = g + inv * f_s[:, quarter(me, r)] - v * back
            if r == 0:
                dxq_out[at, :] = d
            z_s[at, quarter(me, r)] = d.astype(BF16)
        return carry

    lax.fori_loop(0, rows // ROW_BLOCK, norm_back, 0)
    dz = z_s[...]
    dto = nt(dz, ob[...])
    copies[0].wait()
    d_o = nt(dz, wo[...]) + nn(dto.astype(BF16), oa[...])
    dot_s[...] = d_o.T.astype(BF16)
    kept = [jnp.concatenate([visible(c * rows, chunk * rows, rows, length)] * group, axis=1) for c in range(chunk + 1)]

    def one_group(j, carry):
        places = [head_rows(j * group + g) for g in range(group)]
        q_g = jnp.concatenate([qt[at, :] for at in places], axis=1)
        do_g = jnp.concatenate([dot_s[at, :] for at in places], axis=1)
        o_g = jnp.concatenate([ot[at, :] for at in places], axis=1)
        low = jnp.concatenate([lse[pl.ds(j * group + g, 1), :] for g in range(group)], axis=1)
        dots = jnp.sum(do_g.astype(F32) * o_g.astype(F32), axis=0, keepdims=True)
        dq_g = 0.0
        for c in range(chunk + 1):
            prob = jnp.where(kept[c], jnp.exp(nn(keys[c][j], q_g) - low), 0.0)
            ds = (prob * (nn(values[c][j], do_g) - dots)).astype(BF16)
            dq_g = dq_g + nn(keys_t[c][head_rows(j), :], ds)
            dk, dv = nt(q_g, ds), nt(do_g, prob.astype(BF16))
            if last:
                dk, dv = dk + rest[2][head_rows(j), :], dv + rest[3][head_rows(j), :]
            dkt_s[c, head_rows(j), :], dvt_s[c, head_rows(j), :] = dk, dv
        for g in range(group):
            dqt_s[places[g], :] = dq_g[:, g * rows:(g + 1) * rows]
        return carry

    lax.fori_loop(0, kv_heads, one_group, 0)
    if not last:
        outs[6][...], outs[7][...] = dkt_s[0], dvt_s[0]
    cos, sin = cos_t[...], sin_t[...]
    dto_t, o_t = dto.T.astype(BF16), ot[...]
    d_out_a = nt(dto_t, o_t)
    turn_back(dqt_s[...], cos * (HEAD ** -0.5), sin * (HEAD ** -0.5), dot_s)
    dq_s[:, :q_cols] = dot_s[...].T
    turn_back(dkt_s[chunk], cos, sin, dot_s)
    dq_s[:, q_cols:q_cols + kv_cols] = dot_s[:kv_cols, :].T
    dq_s[:, q_cols + kv_cols:] = dvt_s[chunk].T.astype(BF16)
    dq, dk, dv = dq_s[:, :q_cols], dq_s[:, q_cols:q_cols + kv_cols], dq_s[:, q_cols + kv_cols:]
    dt1 = jnp.concatenate([nt(dq, qb[...]), nt(dk, kvb[0]), nt(dv, kvb[1])], axis=1)
    dt1b = dt1.astype(BF16)
    kv_pad = jnp.zeros((RANK, QUARTER - 2 * kv_cols), F32)
    d_kv = jnp.concatenate([nn(t1t[RANK:2 * RANK, :], dk), nn(t1t[2 * RANK:, :], dv), kv_pad], axis=1)
    for k, value in enumerate((nn(t1t[:RANK, :], dq), d_out_a, d_kv)):
        at = slice(k * RANK, (k + 1) * RANK)
        if last:
            value = value + rest[0][at, :]
        b_out[at, :] = value.astype(b_out.dtype)
    dt1t = dt1.T.astype(BF16)
    copies[1].wait()
    copies[2].wait()

    def block(r, inner):
        at = quarter(me, r)
        d = nt(dq_s[:, :q_cols], wq[at, :]) + nn(dt1b, a1[:, at])
        d = d + nt(dq_s[:, q_cols:q_cols + kv_cols], wkv[0, at, :]) + nt(dq_s[:, q_cols + kv_cols:], wkv[1, at, :])
        value_s[...] = d
        store_block(r, value_s, slice(0, rows), h_keep, h_send)
        low_s[:3 * RANK, :] = nn(dt1t, h_in[:, at])
        low_s[3 * RANK:, :] = nn(tot[...], z_s[:, at])
        if last:
            low_s[...] += rest[1][:, at]
            store_block(r, low_s, slice(0, 4 * RANK), outs[5], outs[6])
        else:
            outs[5][:, at] = low_s[...]
        return inner + jnp.sum(d * h_in[:, at].astype(F32), axis=1, keepdims=True)

    inner = lax.fori_loop(0, PARTS, block, jnp.zeros((rows, 1), F32))
    for ref in (h_keep, h_send):
        ref[:, 2 * QUARTER:] = jnp.broadcast_to(inner, (rows, LANES)).astype(ref.dtype)


def finish_kernel(gains, x_all, *refs):
    out = refs[-1]
    gain = gains[0, 0:1, :].astype(F32)
    rows = out.shape[0] // CHUNKS
    for c in range(CHUNKS):
        dx, low, high, got, inv = refs[5 * c:5 * (c + 1)]
        x = chunk_of(x_all, c, rows)
        inv = inv[...]
        inner = high[:rows, QUARTER:QUARTER + 1].astype(F32) + got[:rows, QUARTER:QUARTER + 1].astype(F32)
        scale = inv * inv * inner / WIDTH
        grad = inv * (gain * (low[:rows, :] + got[:rows, :QUARTER].astype(F32))) - x[...].astype(F32) * scale
        out[c * rows:(c + 1) * rows, :] = (dx[...] + grad).astype(BF16)


def split_refs(refs, counts):
    groups = []
    for count in counts:
        groups.append(refs[:count])
        refs = refs[count:]
    return groups, refs


def with_entry(parts, at, use):
    start = 0
    for ref in parts:
        @pl.when((at >= start) & (at < start + ref.shape[0]))
        def _(ref=ref, start=start):
            use(ref, at - start)
        start += ref.shape[0]


def sum_slots(info, owners, out_refs, one_slot):
    count = out_refs[0].shape[0]
    base = pl.program_id(0) * count
    slots = owners.shape[0]
    for ref in out_refs:
        ref[...] = jnp.zeros_like(ref)

    def add(slot, carry):
        owner = owners[slot] - base

        @pl.when((owner >= 0) & (owner < count))
        def _():
            one_slot(owner, entry_of(slot, info[3], slots))
        return carry

    lax.fori_loop(0, slots, add, 0)


def feedforward_sum_kernel(counts, info, owners, *refs):
    (b_parts, *a_parts), outs = split_refs(refs, counts)
    ga, gdb, gb, gda = outs
    me = info[0]

    def one_slot(owner, at):
        def add_b(ref, e):
            for i in range(gda.shape[2] // QUARTER):
                cols = slice(i * QUARTER, (i + 1) * QUARTER)
                base = i * 3 * RANK
                gb[owner, 0, :, cols] += ref[e, base:base + RANK, :].astype(F32)
                gb[owner, 1, :, cols] += ref[e, base + RANK:base + 2 * RANK, :].astype(F32)
                gda[owner, :, cols] += ref[e, base + 2 * RANK:base + 3 * RANK, :].astype(F32)

        with_entry(b_parts, at, add_b)
        for near_bit, parts in enumerate(a_parts):
            def add_a(ref, e, near_bit=near_bit):
                for r, cols in ((near_bit, LO), (near_bit ^ 2, HI)):
                    ga[owner, :, quarter(me, r)] += ref[e, :2 * RANK, cols].astype(F32)
                    gdb[owner, :, quarter(me, r)] += ref[e, 2 * RANK:, cols].astype(F32)

            with_entry(parts, at, add_a)

    sum_slots(info, owners, outs, one_slot)


def attention_sum_kernel(counts, info, owners, *refs):
    (b_parts, *a_parts), outs = split_refs(refs, counts)
    ga, gob, gq, gkv, goa = outs
    me = info[0]
    kv_cols = gkv.shape[3]

    def one_slot(owner, at):
        def add_b(ref, e):
            gq[owner] += ref[e, :RANK, :].astype(F32)
            goa[owner] += ref[e, RANK:2 * RANK, :].astype(F32)
            gkv[owner, 0] += ref[e, 2 * RANK:3 * RANK, :kv_cols].astype(F32)
            gkv[owner, 1] += ref[e, 2 * RANK:3 * RANK, kv_cols:2 * kv_cols].astype(F32)

        with_entry(b_parts, at, add_b)
        for r, parts in enumerate(a_parts):
            def add_a(ref, e, r=r):
                ga[owner, :, quarter(me, r)] += ref[e, :3 * RANK, :].astype(F32)
                gob[owner, :, quarter(me, r)] += ref[e, 3 * RANK:, :].astype(F32)

            with_entry(parts, at, add_a)

    sum_slots(info, owners, outs, one_slot)


def deal_kernel(slots, source, out, sems):
    made = [pltpu.make_async_copy(source.at[i], out.at[slots[i]], sems.at[i]) for i in range(source.shape[0])]
    for copy in made:
        copy.start()
    for copy in made:
        copy.wait()


def collect_kernel(slots, source, out, sems):
    made = [pltpu.make_async_copy(source.at[slots[i]], out.at[i], sems.at[i]) for i in range(source.shape[0])]
    for copy in made:
        copy.start()
    for copy in made:
        copy.wait()


def load_kernel(count, *refs):
    made = [pltpu.make_async_copy(refs[i], refs[count + i], refs[-1].at[i]) for i in range(count)]
    for copy in made:
        copy.start()
    for copy in made:
        copy.wait()


def adapter_kernel(count, info, *refs):
    made = [pltpu.make_async_copy(refs[i].at[info[2]], refs[count + i], refs[-1].at[i]) for i in range(count)]
    for copy in made:
        copy.start()
    for copy in made:
        copy.wait()


def load(arrays, name, info=None, after=()):
    count = len(arrays)
    scalars = () if info is None else (info,)
    kernel = load_kernel if info is None else adapter_kernel
    shapes = [a.shape if info is None else a.shape[1:] for a in arrays]

    def body(*refs):
        at = len(scalars) + count
        kernel(count, *refs[:at], *refs[at + len(after):])

    return pl.pallas_call(
        body,
        in_specs=[pl.BlockSpec(memory_space=pltpu.SMEM)] * len(scalars) + [pl.BlockSpec(memory_space=pltpu.HBM)] * count
        + [pl.BlockSpec(memory_space=pl.ANY)] * len(after),
        out_specs=[pl.BlockSpec(memory_space=pltpu.VMEM)] * count,
        out_shape=[pltpu.VMEM(tuple(s), a.dtype) for s, a in zip(shapes, arrays)],
        scratch_shapes=[pltpu.SemaphoreType.DMA((count,))],
        compiler_params=pltpu.CompilerParams(vmem_limit_bytes=MIB),
        cost_estimate=pl.CostEstimate(flops=1000, transcendentals=0, bytes_accessed=1000),
        name=name,
    )(*scalars, *(in_hbm(a) for a in arrays), *after)


def move_rows(kernel, value, slots, name, here):
    space = pltpu.VMEM if here else pl.ANY
    return pl.pallas_call(
        kernel,
        in_specs=[pl.BlockSpec(memory_space=pltpu.SMEM), pl.BlockSpec(memory_space=pl.ANY if here else pltpu.VMEM)],
        out_specs=pl.BlockSpec(memory_space=space),
        out_shape=(pltpu.VMEM if here else jax.ShapeDtypeStruct)(value.shape, value.dtype),
        scratch_shapes=[pltpu.SemaphoreType.DMA((value.shape[0],))],
        compiler_params=pltpu.CompilerParams(vmem_limit_bytes=MIB),
        cost_estimate=pl.CostEstimate(flops=1000, transcendentals=0, bytes_accessed=1000),
        name=name,
    )(slots, in_hbm(value) if here else in_vmem(value))


def sds(shape, dtype):
    return jax.ShapeDtypeStruct(tuple(shape), dtype)


def in_vmem(value):
    return pltpu.with_memory_space_constraint(value, pltpu.VMEM)


def in_hbm(value):
    return pltpu.with_memory_space_constraint(value, pltpu.HBM)


def call(kernel, info, weights, args, outs, scratch, name, mib, after=(), sems=()):
    vmem = pl.BlockSpec(memory_space=pltpu.VMEM)
    scalars = () if info is None else (info,)
    n, w = len(scalars), len(weights)

    def body(*refs):
        at = n + w + len(args)
        kernel(*refs[:at], *refs[at + len(after):])

    return pl.pallas_call(
        body,
        in_specs=[pl.BlockSpec(memory_space=pltpu.SMEM)] * n + [pl.BlockSpec(memory_space=pltpu.HBM)] * w + [vmem] * len(args)
        + [pl.BlockSpec(memory_space=pl.ANY)] * len(after),
        out_specs=[vmem] * len(outs),
        out_shape=[pltpu.VMEM(tuple(s), d) for s, d in outs],
        scratch_shapes=[pltpu.VMEM(s, d) for s, d in scratch] + ([pltpu.SemaphoreType.DMA(sems)] if sems else []),
        compiler_params=pltpu.CompilerParams(vmem_limit_bytes=mib * MIB),
        cost_estimate=pl.CostEstimate(flops=1000, transcendentals=0, bytes_accessed=1000),
        name=name,
    )(*scalars, *(in_hbm(a) for a in weights), *(in_vmem(a) for a in args), *after)


def sum_call(kernel, scalars, groups, outs, name):
    args = [v for group in groups for v in group]
    steps = 2
    specs = [pl.BlockSpec((o.shape[0] // steps,) + o.shape[1:], (lambda n: lambda i, *_: (i,) + (0,) * n)(o.ndim - 1))
             for o in outs]
    return pl.pallas_call(
        functools.partial(kernel, [len(group) for group in groups]),
        grid_spec=pltpu.PrefetchScalarGridSpec(
            num_scalar_prefetch=len(scalars), grid=(steps,),
            in_specs=[pl.BlockSpec(memory_space=pltpu.VMEM)] * len(args), out_specs=specs),
        out_shape=outs,
        compiler_params=pltpu.CompilerParams(
            dimension_semantics=("arbitrary",),
            vmem_limit_bytes=4 * MIB + sum(a.size * a.dtype.itemsize for a in args)
            + sum(o.size * o.dtype.itemsize for o in outs)),
        cost_estimate=pl.CostEstimate(flops=0, transcendentals=0, bytes_accessed=12000000),
        name=name,
    )(*scalars, *(in_vmem(a) for a in args))


def swap(value, bit, axis, size):
    return lax.ppermute(value, axis, [(i, i ^ bit) for i in range(size)])


def near(value):
    return swap(value, 1, "mp", PARTS)


def far(value):
    return swap(value, 2, "mp", PARTS)


def spread(value):
    there = far(value)
    return (value, near(value), there, near(there))


def chip_sum(keep, send):
    got = near(send)
    lo = keep[:, :QUARTER].astype(F32) + got[:, :QUARTER].astype(F32)
    hi = keep[:, QUARTER:].astype(F32) + got[:, QUARTER:].astype(F32)
    return lo, hi.astype(BF16)


def far_sum_kernel(own, got, out):
    for to, other in ((LO, HI), (HI, LO)):
        out[:, to] = (own[:, to].astype(F32) + got[:, other].astype(F32)).astype(BF16)


def far_sum(own, got):
    return call(far_sum_kernel, None, (), (own, got), [(own.shape, BF16)], [], "far_sum", 6)[0]


def pair_sum_kernel(keep, got, out):
    out[...] = (keep[...] + got[...].astype(F32)).astype(BF16)


def pair_sum(keep, send):
    return call(pair_sum_kernel, None, (), (keep, near(send)), [(send.shape, BF16)], [], "pair_sum", 6)[0]


def late(value, *others):
    return lax.optimization_barrier((value, *others))[0]


def doubled(stack, bit, size):
    return jnp.concatenate([stack, swap(stack, bit, "dp", size)], axis=0)


def entry_of(slot, place, size):
    bits = size.bit_length() - 1
    apart = slot ^ place
    return sum(((apart >> b) & 1) << (bits - 1 - b) for b in range(bits))


def shards(dp, residual, attention_gain, query_matrix, key_value_matrix, output_matrix, feedfwd_gain,
           gate_up_matrix, down_matrix, attention_adapter_input, query_adapter_output,
           key_value_adapter_output, output_adapter_input, output_adapter_output, feedfwd_adapter_input,
           feedfwd_adapter_output, down_adapter_input, down_adapter_output, lengths, adapter_index,
           dealing_slots, cotangent):
    seqs = residual.shape[0]
    length = cotangent.shape[1]
    units = down_matrix.shape[0]
    adapters = attention_adapter_input.shape[0]
    q_cols = query_matrix.shape[1]
    kv_cols = key_value_matrix.shape[2]
    kv_heads = kv_cols // HEAD
    heads = q_cols // HEAD
    rows = length // CHUNKS
    half = 2 * QUARTER
    me = lax.axis_index("mp")
    place = lax.axis_index("dp")

    is_there = dealing_slots[None, :] == jnp.arange(seqs, dtype=jnp.int32)[:, None]
    owners = jnp.sum(jnp.where(is_there, adapter_index[None, :], 0), axis=1)
    spans = jnp.sum(jnp.where(is_there, lengths[None, :], 0), axis=1)
    mine = jnp.arange(seqs, dtype=jnp.int32) == place
    my_length = jnp.sum(jnp.where(mine, spans, 0))
    my_adapter = jnp.sum(jnp.where(mine, owners, 0))
    info = jnp.stack([me.astype(jnp.int32), my_length, my_adapter, place.astype(jnp.int32)])

    gs = spread(cotangent[0])
    gains = jnp.stack(spread(jnp.stack([attention_gain, feedfwd_gain])))
    dealt = lax.all_to_all(
        move_rows(deal_kernel, residual, dealing_slots, "deal", True), "dp", split_axis=0, concat_axis=1, tiled=True
    )[0]
    adapters_here = load(
        (attention_adapter_input, query_adapter_output, key_value_adapter_output, output_adapter_input,
         output_adapter_output, feedfwd_adapter_input, feedfwd_adapter_output, down_adapter_input,
         down_adapter_output), "adapters", info)
    a1, qb, kvb, oa, ob, a2, fba, da, bd = adapters_here
    dealt = late(dealt, gs[2], a1, gains)
    beside = near(dealt)
    there = [far(dealt[c * rows:(c + 1) * rows]) for c in range(CHUNKS)]
    xs = [None] * CHUNKS
    cos_np, sin_np = rope_tables(length)
    cos = [jnp.asarray(cos_np[:, c * rows:(c + 1) * rows]) for c in range(CHUNKS)]
    sin = [jnp.asarray(sin_np[:, c * rows:(c + 1) * rows]) for c in range(CHUNKS)]
    wq, wkv, wo, wgu, wd = query_matrix, key_value_matrix, output_matrix, gate_up_matrix, down_matrix

    def like(*arrays):
        return [(a.shape, a.dtype) for a in arrays]

    wide, col, block, thin = (rows, WIDTH), (rows, half), (rows, QUARTER), (rows, 1)
    saved = [None] * CHUNKS
    order = ()
    for c in range(CHUNKS):
        xs[c] = (dealt, beside, there[c], near(late(there[c], *order)))
        outs = [(wide, BF16), ((3 * RANK, rows), BF16), ((q_cols, rows), BF16), ((kv_heads, rows, HEAD), BF16),
                ((kv_heads, rows, HEAD), BF16), ((kv_cols, rows), BF16), ((kv_cols, rows), BF16)]
        saved[c] = call(
            functools.partial(project_kernel, c), info, (wq, wkv), (*xs[c], gains, a1, qb, kvb, cos[c], sin[c]), outs,
            like(wq, wkv), "project_%d" % c, 12, order, (2,))
        order = (saved[c][1],)

    kept, z_own = [None] * CHUNKS, [None] * CHUNKS
    for c in reversed(range(CHUNKS)):
        outs = [(col, F32), (col, BF16), ((q_cols, rows), BF16), ((heads, rows), F32), ((RANK, rows), BF16)]
        pairs = [v for p in saved[:c + 1] for v in (p[3], p[6])]
        z_keep, z_send, *kept[c] = call(
            functools.partial(attend_kernel, c), info, (wo,), (saved[c][2], oa, ob, *pairs), outs, like(wo),
            "attend_%d" % c, 10, order, (1,))
        z_own[c] = pair_sum(z_keep, z_send)
        order = (kept[c][1], z_own[1])
    z_far = [far(v) for v in z_own]
    wgu, wd = load((wgu, wd), "load", None, order)

    def front(c, total, partial, order):
        hidden = (rows, units)
        outs = [(wide, BF16), (block, F32), (wide, BF16), (wide, BF16), (hidden, BF16), (hidden, BF16), (hidden, BF16),
                ((rows, 2 * RANK), BF16), ((rows, RANK), BF16),
                ((3 * RANK * units // QUARTER, QUARTER), F32 if c else BF16)]
        return call(
            functools.partial(front_kernel, c, c == 0), info, (),
            (wgu, wd, *xs[c], total, near(total), *gs, gains, a2, bd, fba, da, *partial), outs,
            [((ROW_BLOCK, WIDTH), F32)], "front_%d" % c, 8, order)

    def back(c, hidden, partial, order):
        first = col if c else (rows + 3 * RANK, half)
        outs = [(first, F32), (first, BF16), (col, F32), (col, BF16)]
        outs += [((3 * RANK, WIDTH), F32)] if c else []
        return call(
            functools.partial(back_kernel, c == 0), info, (), (wgu, wd, *hidden[2:7], a2, bd, fba, da, *partial), outs,
            [(block, F32), ((3 * RANK, QUARTER), F32)], "back_%d" % c, 8, order)

    def attend_back(c, total, partial, order):
        padded = (rows, half + LANES)
        outs = [(block, F32), (padded, F32), (padded, BF16), (thin, F32), ((3 * RANK, QUARTER), F32 if c else BF16)]
        outs += ([((4 * RANK, WIDTH), F32), ((kv_cols, rows), F32), ((kv_cols, rows), F32)] if c
                 else [((4 * RANK, half), F32), ((4 * RANK, half), BF16)])
        scratch = [(wide, BF16), ((ROW_BLOCK, WIDTH), F32), ((q_cols, rows), BF16), ((q_cols, rows), F32),
                   ((c + 1, kv_cols, rows), F32), ((c + 1, kv_cols, rows), F32), ((rows, q_cols + 2 * kv_cols), BF16),
                   (block, F32), ((4 * RANK, QUARTER), F32)]
        triples = [v for p in saved[:c + 1] for v in (p[3], p[4], p[5])]
        return call(
            functools.partial(attend_back_kernel, c, c == 0), info, (wq, wkv, wo),
            (*xs[c], *gs, hidden[c][0], total, near(total), gains, a1, qb, kvb, oa, ob, cos[c], sin[c], *saved[c][:3],
             *kept[c], *triples, *partial), outs, scratch + like(wq, wkv, wo), "attend_back_%d" % c, 18, order, (3,))

    bits = [1 << b for b in reversed(range(dp.bit_length() - 1))]
    hidden, d_own, d_far = ([None] * CHUNKS for _ in range(3))
    hidden[1] = front(1, far_sum(z_own[1], late(z_far[1], wd)), (), order)
    step = hidden[1][8]
    total = far_sum(z_own[0], late(z_far[0], step))
    d_keep, d_send, y_keep_1, y_send_1, fa = back(1, hidden[1], (), (step, total))
    d_own[1] = pair_sum(d_keep, d_send)
    d_far[1] = far(d_own[1])
    hidden[0] = front(0, total, hidden[1][9:], (d_own[1],))
    step = hidden[0][8]
    total = far_sum(d_own[1], late(d_far[1], step))
    fb = hidden[0][9][None]
    fb_first = swap(fb, bits[0], "dp", dp)
    y_keep, y_got = [None, y_keep_1], [None, near(y_send_1)]

    def y_high(c, *others):
        return (y_keep[c][:, QUARTER:] + late(y_got[c], *others)[:, QUARTER:].astype(F32)).astype(BF16)

    high = y_high(1, step)
    y_far = [None, far(high)]
    d_keep, d_send, y_keep[0], y_send_0 = back(0, hidden[0], (fa,), (step, total, high))
    d_own[0] = pair_sum(d_keep, late(d_send, fb_first, y_far[1]))
    d_far[0] = far(d_own[0])
    fb = fb_more = jnp.concatenate([fb, fb_first], axis=0)
    for bit in bits[1:-1]:
        fb_more = doubled(fb_more, bit, dp)
    fb_more = fb_more[2:]
    fb_side = swap(fb, bits[-1], "dp", dp)
    y_got[0] = near(y_send_0)
    dxq, h_keep, h_send, inv, *sums = attend_back(1, total, (), (d_own[0],))
    total = far_sum(d_own[0], late(d_far[0], inv))
    h_low, h_high = chip_sum(h_keep, late(h_send, fb_more, fb_side, d_far[0]))
    h_far = far(h_high)
    final = [None, (dxq, h_low, h_high, h_far, inv)]
    high = y_high(0, h_high)
    y_far[0] = far(high)
    fa = total[rows:][None]
    fa_first = swap(fa, bits[0], "dp", dp)
    fb_more_side = swap(fb_more, bits[-1], "dp", dp)
    dxq, h_keep, h_send, inv, att_b, aa_keep, aa_send = attend_back(0, total, sums, (h_high, high))
    ready = (fa_first, fb_more_side, h_far, y_far[0])
    aa_low, aa_high = chip_sum(aa_keep, late(aa_send, *ready))
    aa_far = far(aa_high)
    h_low, h_high = chip_sum(h_keep, late(h_send, *ready))
    h_far = far(h_high)
    final[0] = (dxq, h_low, h_high, h_far, inv)
    att = jnp.concatenate([att_b, (aa_low + late(aa_far, h_high).astype(F32)).astype(BF16)], axis=0)[None]
    att = doubled(att, bits[0], dp)

    dinput, = call(finish_kernel, None, (), (gains, dealt, *(v for f in final for v in f)), [((length, QUARTER), BF16)],
                   [], "finish", 8, (att,))
    back_grad = lax.all_to_all(
        dinput.reshape(dp, length // dp, QUARTER), "dp", split_axis=0, concat_axis=0, tiled=True)
    input_grad = move_rows(collect_kernel, back_grad, dealing_slots, "collect_grad", False)

    valid = (jnp.arange(length, dtype=jnp.int32) < my_length)[:, None]
    result = jnp.concatenate(
        [hidden[c][1] + y_keep[c][:, :QUARTER] + late(y_got[c], h_high)[:, :QUARTER].astype(F32) + y_far[c].astype(F32)
         for c in range(CHUNKS)], axis=0)
    result = late(jnp.where(valid, result, 0.0).astype(BF16), dinput)
    back_out = lax.all_to_all(
        result.reshape(dp, length // dp, QUARTER), "dp", split_axis=0, concat_axis=0, tiled=True)
    output = move_rows(collect_kernel, back_out, late(dealing_slots, input_grad), "collect_out", False)

    n_b = att_b.shape[0]
    for bit in bits[1:-1]:
        att = doubled(att, bit, dp)
    att_side = swap(att, bits[-1], "dp", dp)
    a_parts = [att[:, n_b:], att_side[:, n_b:]]
    a_far = [far(v) for v in a_parts]
    fa = late(jnp.concatenate([fa, fa_first], axis=0), h_high)
    for bit in bits[1:-1]:
        fa = doubled(fa, bit, dp)
    fa_side = swap(fa, bits[-1], "dp", dp)
    outs = [sds((adapters, 2 * RANK, WIDTH), F32), sds((adapters, RANK, WIDTH), F32),
            sds((adapters, 2, RANK, units), F32), sds((adapters, RANK, units), F32)]
    ga_ffn, g_down_b, g_ffn_b, g_down_a = sum_call(
        feedforward_sum_kernel, (info, owners),
        ((fb, fb_more, fb_side, fb_more_side), (fa, fa_side), (near(fa), near(fa_side))), outs, "feedforward_sum")

    outs = [sds((adapters, 3 * RANK, WIDTH), F32), sds((adapters, RANK, WIDTH), F32),
            sds((adapters, RANK, q_cols), F32), sds((adapters, 2, RANK, kv_cols), F32),
            sds((adapters, RANK, q_cols), F32)]
    ga_att, g_out_b, g_query_b, g_kv_b, g_out_a = sum_call(
        attention_sum_kernel, (info, owners),
        ((att, att_side), a_parts, [near(v) for v in a_parts], a_far, (near(a_far[0]), near(late(a_far[1], g_down_a)))), outs, "attention_sum")
    return (output, input_grad, ga_att, g_query_b, g_kv_b, g_out_a, g_out_b, ga_ffn, g_ffn_b, g_down_a, g_down_b)


def solution(mesh):
    in_specs = (
        P(None, "dp", "mp"), P("mp"), P(None, "mp"), P(None, None, "mp"), P("mp", None), P("mp"),
        P(None, None, "mp"), P("mp", None), P(), P(None, None, "mp"), P(None, None, None, "mp"),
        P(None, None, "mp"), P(), P(), P(None, None, None, "mp"), P(None, None, "mp"), P(), P(), P(), P(),
        P("dp", None, "mp"),
    )
    out_specs = (
        P(None, "dp", "mp"), P(None, "dp", "mp"), P(), P(None, None, "mp"), P(None, None, None, "mp"),
        P(None, None, "mp"), P(), P(), P(None, None, None, "mp"), P(None, None, "mp"), P(),
    )
    return jax.shard_map(
        functools.partial(shards, mesh.shape["dp"]), mesh=mesh, in_specs=in_specs, out_specs=out_specs,
        check_vma=False)
```

```python
import functools

import jax
import jax.numpy as jnp
import numpy as np
from jax import lax
from jax.experimental import pallas as pl
from jax.experimental.pallas import tpu as pltpu
from jax.sharding import PartitionSpec as P

WIDTH = 2048
HEAD = 64
HALF = HEAD // 2
RANK = 16
EPS = 1e-05
ROPE_BASE = 500000.0
NEG_FILL = -1e30
PARTS = 4
LANES = 128
ROW_BLOCK = 64
QUARTER = WIDTH // PARTS
CHUNKS = 2
MIB = 1024 * 1024
F32 = jnp.float32
BF16 = jnp.bfloat16


def nn(a, b):
    return lax.dot_general(a, b, (((1,), (0,)), ((), ())), preferred_element_type=F32)


def nt(a, b):
    return lax.dot_general(a, b, (((1,), (1,)), ((), ())), preferred_element_type=F32)


def rope_tables(length):
    freq = ROPE_BASE ** (-np.arange(HALF, dtype=np.float32) * np.float32(2.0 / HEAD))
    angles = (np.arange(length, dtype=np.float32)[None, :] * freq.astype(np.float32)[:, None]).astype(np.float32)
    return np.cos(angles).astype(np.float32), np.sin(angles).astype(np.float32)


def quarter(me, rel):
    return pl.ds(pl.multiple_of((me ^ rel) * QUARTER, QUARTER), QUARTER)


LO, HI = slice(0, QUARTER), slice(QUARTER, 2 * QUARTER)


def total_block(rel, rows_at, own, oth):
    return (own if rel in (0, 2) else oth)[rows_at, LO if rel in (0, 1) else HI].astype(F32)


def store_block(rel, value, rows_at, keep_ref, send_ref):
    to = pl.ds(pl.multiple_of((rel // 2) * QUARTER, QUARTER), QUARTER)

    @pl.when(rel % 2 == 0)
    def _():
        keep_ref[rows_at, to] = value[...]

    @pl.when(rel % 2 == 1)
    def _():
        send_ref[rows_at, to] = value[...].astype(BF16)


def chunk_of(ref, chunk, rows):
    return ref if ref.shape[0] == rows else ref.at[chunk * rows:(chunk + 1) * rows]


def row_block(i):
    return pl.ds(pl.multiple_of(i * ROW_BLOCK, ROW_BLOCK), ROW_BLOCK)


def is_valid(chunk, i, rows, length):
    return chunk * rows + i * ROW_BLOCK + lax.broadcasted_iota(jnp.int32, (ROW_BLOCK, 1), 0) < length


def copies_of(pairs, sems):
    made = [pltpu.make_async_copy(source, target, sems.at[i]) for i, (source, target) in enumerate(pairs)]
    for copy in made:
        copy.start()
    return made


def put_block(rel, value, keep_ref, send_ref):
    ref = keep_ref if rel in (0, 2) else send_ref
    ref[:, LO if rel in (0, 1) else HI] = value.astype(ref.dtype)


def rotate(value, cos, sin, out_ref):
    for i in range(value.shape[0] // HEAD):
        u1, u2 = value[i * HEAD:i * HEAD + HALF], value[i * HEAD + HALF:(i + 1) * HEAD]
        out_ref[i * HEAD:i * HEAD + HALF, :] = (u1 * cos - u2 * sin).astype(BF16)
        out_ref[i * HEAD + HALF:(i + 1) * HEAD, :] = (u2 * cos + u1 * sin).astype(BF16)


def turn_back(value, cos, sin, out_ref):
    for i in range(value.shape[0] // HEAD):
        w1, w2 = value[i * HEAD:i * HEAD + HALF], value[i * HEAD + HALF:(i + 1) * HEAD]
        out_ref[i * HEAD:i * HEAD + HALF, :] = (w1 * cos + w2 * sin).astype(BF16)
        out_ref[i * HEAD + HALF:(i + 1) * HEAD, :] = (w2 * cos - w1 * sin).astype(BF16)


def head_rows(i):
    return pl.ds(pl.multiple_of(i * HEAD, HEAD), HEAD)


def visible(key_start, query_start, rows, length):
    kpos = key_start + lax.broadcasted_iota(jnp.int32, (rows, rows), 0)
    qpos = query_start + lax.broadcasted_iota(jnp.int32, (rows, rows), 1)
    return (kpos <= qpos) & (kpos < length)


def project_kernel(chunk, info, wq_h, wkv_h, x0, x1, x2, x3, gains, a1, qb, kvb, cos_t, sin_t,
                   t1t_out, qt_out, kn_out, vn_out, kt_out, vt_out, h_out, wq, wkv, sems):
    copies = copies_of(((wkv_h, wkv), (wq_h, wq)), sems)
    me = info[0]
    rows = h_out.shape[0]
    kv_heads = kn_out.shape[0]
    xs = [chunk_of(x, chunk, rows) for x in (x0, x1, x2, x3)]

    def norm(i, carry):
        at = row_block(i)
        square = jnp.zeros((ROW_BLOCK, 1), F32)
        for r in range(PARTS):
            v = xs[r][at, :].astype(F32)
            square = square + jnp.sum(v * v, axis=1, keepdims=True)
        inv = lax.rsqrt(square / WIDTH + EPS)
        for r in range(PARTS):
            v = xs[r][at, :].astype(F32)
            h_out[at, quarter(me, r)] = (v * inv * gains[r, 0:1, :].astype(F32)).astype(BF16)
        return carry

    lax.fori_loop(0, rows // ROW_BLOCK, norm, 0)
    h = h_out[...]
    t1 = nt(h, a1[...])
    t1t_out[...] = t1.T.astype(BF16)
    t1b = t1.astype(BF16)
    cos, sin = cos_t[...], sin_t[...]
    copies[0].wait()
    k = nn(h, wkv[0]) + nn(t1b[:, RANK:2 * RANK], kvb[0])
    rotate(k.T, cos, sin, kt_out)
    k_n = kt_out[...].T
    v_n = (nn(h, wkv[1]) + nn(t1b[:, 2 * RANK:], kvb[1])).astype(BF16)
    vt_out[...] = v_n.T
    for i in range(kv_heads):
        kn_out[i] = k_n[:, i * HEAD:(i + 1) * HEAD]
        vn_out[i] = v_n[:, i * HEAD:(i + 1) * HEAD]
    copies[1].wait()
    q = nn(h, wq[...]) + nn(t1b[:, :RANK], qb[...])
    rotate(q.T * (HEAD ** -0.5), cos, sin, qt_out)


def attend_kernel(chunk, info, wo_h, qt, oa, ob, *rest):
    pairs, rest = rest[:2 * (chunk + 1)], rest[2 * (chunk + 1):]
    z_keep, z_send, ot_out, lse_out, tot_out, wo, sems = rest
    copies = copies_of(((wo_h, wo),), sems)
    keys, values = pairs[0::2], pairs[1::2]
    me, length = info[0], info[1]
    rows = qt.shape[1]
    kv_heads = keys[0].shape[0]
    heads = qt.shape[0] // HEAD
    group = heads // kv_heads

    kept = [jnp.concatenate([visible(c * rows, chunk * rows, rows, length)] * group, axis=1) for c in range(chunk + 1)]

    def one_group(j, carry):
        q_g = jnp.concatenate([qt[head_rows(j * group + g), :] for g in range(group)], axis=1)
        parts = [jnp.where(kept[c], nn(keys[c][j], q_g), NEG_FILL) for c in range(chunk + 1)]
        top = functools.reduce(jnp.maximum, [jnp.max(s, axis=0, keepdims=True) for s in parts])
        es = [jnp.exp(s - top) for s in parts]
        total = sum(jnp.sum(e, axis=0, keepdims=True) for e in es)
        low = top + jnp.log(total)
        o_t = sum(nn(value[head_rows(j), :], e.astype(BF16)) for value, e in zip(values, es))
        o_t = (o_t / total).astype(BF16)
        for g in range(group):
            cols = slice(g * rows, (g + 1) * rows)
            lse_out[pl.ds(j * group + g, 1), :] = low[:, cols]
            ot_out[head_rows(j * group + g), :] = o_t[:, cols]
        return carry

    lax.fori_loop(0, kv_heads, one_group, 0)
    o = ot_out[...].T
    to = nt(o, oa[...])
    tot_out[...] = to.T.astype(BF16)
    to = to.astype(BF16)
    copies[0].wait()
    for r in range(PARTS):
        at = quarter(me, r)
        put_block(r, nn(o, wo[:, at]) + nn(to, ob[:, at]), z_keep, z_send)


def front_kernel(chunk, last, info, wgu_in, wd_in, x0, x1, x2, x3, zo, zp, g0, g1, g2, g3, gains, a2, bd, fb, da,
                 *rest):
    units = wd_in.shape[0]
    if chunk:
        wgu, wd = wgu_in, wd_in
    else:
        (wgu, wd, f_s, sems), rest = rest[-4:], rest[:-4]
        rest = (*rest, f_s)

    def copies(i):
        c = pl.ds(pl.multiple_of(i * QUARTER, QUARTER), QUARTER)
        return (pltpu.make_async_copy(wgu_in.at[:, :, c], wgu.at[:, :, c], sems.at[0, i]),
                pltpu.make_async_copy(wd_in.at[c, :], wd.at[c, :], sems.at[1, i]))

    if not chunk:
        for i in range(units // QUARTER):
            for copy in copies(i):
                copy.start()
    f_s = rest[-1]
    xm_out, xq_out, h_out, g_out, act_out, dg_out, du_out, t2_s, dtd_s, b_out = rest[-11:-1]
    me, length = info[0], info[1]
    rows = h_out.shape[0]
    xs, gs = ([chunk_of(v, chunk, rows) for v in vs] for vs in ((x0, x1, x2, x3), (g0, g1, g2, g3)))

    def norm(i, carry):
        at = row_block(i)
        valid = is_valid(chunk, i, rows, length)
        square = jnp.zeros((ROW_BLOCK, 1), F32)
        for r in range(PARTS):
            v = xs[r][at, :].astype(F32) + total_block(r, at, zo, zp)
            if r == 0:
                xq_out[at, :] = v
            f_s[:, quarter(me, r)] = v
            square = square + jnp.sum(v * v, axis=1, keepdims=True)
            g_out[at, quarter(me, r)] = jnp.where(valid, gs[r][at, :], jnp.zeros((), BF16))
        inv = lax.rsqrt(square / WIDTH + EPS)
        for r in range(PARTS):
            v = f_s[:, quarter(me, r)]
            xm_out[at, quarter(me, r)] = v.astype(BF16)
            h_out[at, quarter(me, r)] = (v * inv * gains[r, 1:2, :].astype(F32)).astype(BF16)
        return carry

    lax.fori_loop(0, rows // ROW_BLOCK, norm, 0)
    t2 = nt(h_out[...], a2[...])
    t2_s[...] = t2.astype(BF16)
    dtd = nt(g_out[...], bd[...])
    dtd_s[...] = dtd.astype(BF16)
    t2t, dtdt = t2.T.astype(BF16), dtd.T.astype(BF16)

    def block(i, carry):
        c = pl.ds(pl.multiple_of(i * QUARTER, QUARTER), QUARTER)
        if not chunk:
            for copy in copies(i):
                copy.wait()
        h, g = h_out[...], g_out[...]
        gate = nn(h, wgu[0, :, c]) + nn(t2_s[:, :RANK], fb[0, :, c])
        up = nn(h, wgu[1, :, c]) + nn(t2_s[:, RANK:], fb[1, :, c])
        dact = nt(g, wd[c, :]) + nn(dtd_s[...], da[:, c])
        sig = 1.0 / (1.0 + jnp.exp(-gate))
        silu = gate * sig
        act = (silu * up).astype(BF16)
        dgate = (dact * up * sig * (1.0 + gate * (1.0 - sig))).astype(BF16)
        dup = (dact * silu).astype(BF16)
        act_out[:, c], dg_out[:, c], du_out[:, c] = act, dgate, dup
        for k, value in enumerate((nn(t2t[:RANK], dgate), nn(t2t[RANK:], dup), nn(dtdt, act))):
            at = pl.ds(pl.multiple_of((3 * i + k) * RANK, RANK), RANK)
            if last:
                value = value + rest[0][at, :]
            b_out[at, :] = value.astype(b_out.dtype)
        return carry

    lax.fori_loop(0, units // QUARTER, block, 0)


def back_kernel(last, info, wgu, wd, h, g, act, dg, du, a2, bd, fb, da, *rest):
    (value_s, low_s), rest = rest[-2:], rest[:-2]
    outs, rest = (rest[-4:], rest[:-4]) if last else (rest[-5:], rest[:-5])
    d_keep, d_send, y_keep, y_send = outs[:4]
    me = info[0]
    rows = h.shape[0]
    own = slice(0, rows)

    dt2 = jnp.concatenate([nt(dg[...], fb[0]), nt(du[...], fb[1])], axis=1)
    dt2b = dt2.astype(BF16)
    td = nt(act[...], da[...])
    tdb = td.astype(BF16)
    dt2t, tdt = dt2.T.astype(BF16), td.T.astype(BF16)

    def block(r, carry):
        at = quarter(me, r)
        value_s[...] = nt(dg[...], wgu[0, at, :]) + nt(du[...], wgu[1, at, :]) + nn(dt2b, a2[:, at])
        store_block(r, value_s, own, d_keep, d_send)
        value_s[...] = nn(act[...], wd[:, at]) + nn(tdb, bd[:, at])
        store_block(r, value_s, own, y_keep, y_send)
        low_s[:2 * RANK, :] = nn(dt2t, h[:, at])
        low_s[2 * RANK:, :] = nn(tdt, g[:, at])
        if last:
            low_s[...] += rest[0][:, at]
            store_block(r, low_s, slice(rows, rows + 3 * RANK), d_keep, d_send)
        else:
            outs[4][:, at] = low_s[...]
        return carry

    lax.fori_loop(0, PARTS, block, 0)


def attend_back_kernel(chunk, last, info, wq_h, wkv_h, wo_h, x0, x1, x2, x3, g0, g1, g2, g3, xm, do_, dp, gains, a1,
                       qb, kvb, oa, ob, cos_t, sin_t, t1t, qt, ot, lse, tot, *rest):
    scratch, rest = rest[-14:], rest[:-14]
    h_in, z_s, f_s, dot_s, dqt_s, dkt_s, dvt_s, dq_s, value_s, low_s, wq, wkv, wo, sems = scratch
    copies = copies_of(((wo_h, wo), (wq_h, wq), (wkv_h, wkv)), sems)
    n_out = 7 if last else 8
    outs, rest = rest[-n_out:], rest[:-n_out]
    dxq_out, h_keep, h_send, inv_out, b_out = outs[:5]
    triples, rest = rest[:3 * (chunk + 1)], rest[3 * (chunk + 1):]
    keys, values, keys_t = triples[0::3], triples[1::3], triples[2::3]
    me, length = info[0], info[1]
    rows = xm.shape[0]
    kv_heads = keys[0].shape[0]
    heads = qt.shape[0] // HEAD
    group = heads // kv_heads
    q_cols, kv_cols = heads * HEAD, kv_heads * HEAD
    xs, gs = ([chunk_of(v, chunk, rows) for v in vs] for vs in ((x0, x1, x2, x3), (g0, g1, g2, g3)))

    def norm_back(i, carry):
        at = row_block(i)
        valid = is_valid(chunk, i, rows, length)
        square, first, inner = (jnp.zeros((ROW_BLOCK, 1), F32) for _ in range(3))
        for r in range(PARTS):
            v = xm[at, quarter(me, r)].astype(F32)
            square = square + jnp.sum(v * v, axis=1, keepdims=True)
            w = total_block(r, at, do_, dp) * gains[r, 1:2, :].astype(F32)
            f_s[:, quarter(me, r)] = w
            inner = inner + jnp.sum(v * w, axis=1, keepdims=True)
            u = xs[r][at, :].astype(F32)
            first = first + jnp.sum(u * u, axis=1, keepdims=True)
        inv_one = lax.rsqrt(first / WIDTH + EPS)
        inv_out[at, :] = inv_one
        inv = lax.rsqrt(square / WIDTH + EPS)
        back = inv * inv * inv * inner / WIDTH
        for r in range(PARTS):
            v = xm[at, quarter(me, r)].astype(F32)
            g = jnp.where(valid, gs[r][at, :].astype(F32), 0.0)
            d = g + inv * f_s[:, quarter(me, r)] - v * back
            if r == 0:
                dxq_out[at, :] = d
            z_s[at, quarter(me, r)] = d.astype(BF16)
            u = xs[r][at, :].astype(F32)
            h_in[at, quarter(me, r)] = (u * inv_one * gains[r, 0:1, :].astype(F32)).astype(BF16)
        return carry

    lax.fori_loop(0, rows // ROW_BLOCK, norm_back, 0)
    dz = z_s[...]
    dto = nt(dz, ob[...])
    copies[0].wait()
    d_o = nt(dz, wo[...]) + nn(dto.astype(BF16), oa[...])
    dot_s[...] = d_o.T.astype(BF16)
    kept = [jnp.concatenate([visible(c * rows, chunk * rows, rows, length)] * group, axis=1) for c in range(chunk + 1)]

    def one_group(j, carry):
        places = [head_rows(j * group + g) for g in range(group)]
        q_g = jnp.concatenate([qt[at, :] for at in places], axis=1)
        do_g = jnp.concatenate([dot_s[at, :] for at in places], axis=1)
        o_g = jnp.concatenate([ot[at, :] for at in places], axis=1)
        low = jnp.concatenate([lse[pl.ds(j * group + g, 1), :] for g in range(group)], axis=1)
        dots = jnp.sum(do_g.astype(F32) * o_g.astype(F32), axis=0, keepdims=True)
        dq_g = 0.0
        for c in range(chunk + 1):
            prob = jnp.where(kept[c], jnp.exp(nn(keys[c][j], q_g) - low), 0.0)
            ds = (prob * (nn(values[c][j], do_g) - dots)).astype(BF16)
            dq_g = dq_g + nn(keys_t[c][head_rows(j), :], ds)
            dk, dv = nt(q_g, ds), nt(do_g, prob.astype(BF16))
            if last:
                dk, dv = dk + rest[2][head_rows(j), :], dv + rest[3][head_rows(j), :]
            dkt_s[c, head_rows(j), :], dvt_s[c, head_rows(j), :] = dk, dv
        for g in range(group):
            dqt_s[places[g], :] = dq_g[:, g * rows:(g + 1) * rows]
        return carry

    lax.fori_loop(0, kv_heads, one_group, 0)
    if not last:
        outs[6][...], outs[7][...] = dkt_s[0], dvt_s[0]
    cos, sin = cos_t[...], sin_t[...]
    dto_t, o_t = dto.T.astype(BF16), ot[...]
    d_out_a = nt(dto_t, o_t)
    turn_back(dqt_s[...], cos * (HEAD ** -0.5), sin * (HEAD ** -0.5), dot_s)
    dq_s[:, :q_cols] = dot_s[...].T
    turn_back(dkt_s[chunk], cos, sin, dot_s)
    dq_s[:, q_cols:q_cols + kv_cols] = dot_s[:kv_cols, :].T
    dq_s[:, q_cols + kv_cols:] = dvt_s[chunk].T.astype(BF16)
    dq, dk, dv = dq_s[:, :q_cols], dq_s[:, q_cols:q_cols + kv_cols], dq_s[:, q_cols + kv_cols:]
    dt1 = jnp.concatenate([nt(dq, qb[...]), nt(dk, kvb[0]), nt(dv, kvb[1])], axis=1)
    dt1b = dt1.astype(BF16)
    kv_pad = jnp.zeros((RANK, QUARTER - 2 * kv_cols), F32)
    d_kv = jnp.concatenate([nn(t1t[RANK:2 * RANK, :], dk), nn(t1t[2 * RANK:, :], dv), kv_pad], axis=1)
    for k, value in enumerate((nn(t1t[:RANK, :], dq), d_out_a, d_kv)):
        at = slice(k * RANK, (k + 1) * RANK)
        if last:
            value = value + rest[0][at, :]
        b_out[at, :] = value.astype(b_out.dtype)
    dt1t = dt1.T.astype(BF16)
    copies[1].wait()
    copies[2].wait()

    def block(r, inner):
        at = quarter(me, r)
        d = nt(dq_s[:, :q_cols], wq[at, :]) + nn(dt1b, a1[:, at])
        d = d + nt(dq_s[:, q_cols:q_cols + kv_cols], wkv[0, at, :]) + nt(dq_s[:, q_cols + kv_cols:], wkv[1, at, :])
        value_s[...] = d
        store_block(r, value_s, slice(0, rows), h_keep, h_send)
        low_s[:3 * RANK, :] = nn(dt1t, h_in[:, at])
        low_s[3 * RANK:, :] = nn(tot[...], z_s[:, at])
        if last:
            low_s[...] += rest[1][:, at]
            store_block(r, low_s, slice(0, 4 * RANK), outs[5], outs[6])
        else:
            outs[5][:, at] = low_s[...]
        return inner + jnp.sum(d * h_in[:, at].astype(F32), axis=1, keepdims=True)

    inner = lax.fori_loop(0, PARTS, block, jnp.zeros((rows, 1), F32))
    for ref in (h_keep, h_send):
        ref[:, 2 * QUARTER:] = jnp.broadcast_to(inner, (rows, LANES)).astype(ref.dtype)


def finish_kernel(gains, x_all, *refs):
    out = refs[-1]
    gain = gains[0, 0:1, :].astype(F32)
    rows = out.shape[0] // CHUNKS
    for c in range(CHUNKS):
        dx, low, high, got, inv = refs[5 * c:5 * (c + 1)]
        x = chunk_of(x_all, c, rows)
        inv = inv[...]
        inner = high[:rows, QUARTER:QUARTER + 1].astype(F32) + got[:rows, QUARTER:QUARTER + 1].astype(F32)
        scale = inv * inv * inner / WIDTH
        grad = inv * (gain * (low[:rows, :] + got[:rows, :QUARTER].astype(F32))) - x[...].astype(F32) * scale
        out[c * rows:(c + 1) * rows, :] = (dx[...] + grad).astype(BF16)


def split_refs(refs, counts):
    groups = []
    for count in counts:
        groups.append(refs[:count])
        refs = refs[count:]
    return groups, refs


def with_entry(parts, at, use):
    start = 0
    for ref in parts:
        @pl.when((at >= start) & (at < start + ref.shape[0]))
        def _(ref=ref, start=start):
            use(ref, at - start)
        start += ref.shape[0]


def sum_slots(info, owners, out_refs, one_slot):
    count = out_refs[0].shape[0]
    base = pl.program_id(0) * count
    slots = owners.shape[0]
    for ref in out_refs:
        ref[...] = jnp.zeros_like(ref)

    def add(slot, carry):
        owner = owners[slot] - base

        @pl.when((owner >= 0) & (owner < count))
        def _():
            one_slot(owner, entry_of(slot, info[3], slots))
        return carry

    lax.fori_loop(0, slots, add, 0)


def feedforward_sum_kernel(counts, info, owners, *refs):
    (b_parts, *a_parts), outs = split_refs(refs, counts)
    ga, gdb, gb, gda = outs
    me = info[0]

    def one_slot(owner, at):
        def add_b(ref, e):
            for i in range(gda.shape[2] // QUARTER):
                cols = slice(i * QUARTER, (i + 1) * QUARTER)
                base = i * 3 * RANK
                gb[owner, 0, :, cols] += ref[e, base:base + RANK, :].astype(F32)
                gb[owner, 1, :, cols] += ref[e, base + RANK:base + 2 * RANK, :].astype(F32)
                gda[owner, :, cols] += ref[e, base + 2 * RANK:base + 3 * RANK, :].astype(F32)

        with_entry(b_parts, at, add_b)
        for near_bit, parts in enumerate(a_parts):
            def add_a(ref, e, near_bit=near_bit):
                for r, cols in ((near_bit, LO), (near_bit ^ 2, HI)):
                    ga[owner, :, quarter(me, r)] += ref[e, :2 * RANK, cols].astype(F32)
                    gdb[owner, :, quarter(me, r)] += ref[e, 2 * RANK:, cols].astype(F32)

            with_entry(parts, at, add_a)

    sum_slots(info, owners, outs, one_slot)


def attention_sum_kernel(counts, info, owners, *refs):
    (b_parts, *a_parts), outs = split_refs(refs, counts)
    ga, gob, gq, gkv, goa = outs
    me = info[0]
    kv_cols = gkv.shape[3]

    def one_slot(owner, at):
        def add_b(ref, e):
            gq[owner] += ref[e, :RANK, :].astype(F32)
            goa[owner] += ref[e, RANK:2 * RANK, :].astype(F32)
            gkv[owner, 0] += ref[e, 2 * RANK:3 * RANK, :kv_cols].astype(F32)
            gkv[owner, 1] += ref[e, 2 * RANK:3 * RANK, kv_cols:2 * kv_cols].astype(F32)

        with_entry(b_parts, at, add_b)
        for r, parts in enumerate(a_parts):
            def add_a(ref, e, r=r):
                ga[owner, :, quarter(me, r)] += ref[e, :3 * RANK, :].astype(F32)
                gob[owner, :, quarter(me, r)] += ref[e, 3 * RANK:, :].astype(F32)

            with_entry(parts, at, add_a)

    sum_slots(info, owners, outs, one_slot)


def deal_kernel(slots, source, out, sems):
    made = [pltpu.make_async_copy(source.at[i], out.at[slots[i]], sems.at[i]) for i in range(source.shape[0])]
    for copy in made:
        copy.start()
    for copy in made:
        copy.wait()


def collect_kernel(slots, source, out, sems):
    made = [pltpu.make_async_copy(source.at[slots[i]], out.at[i], sems.at[i]) for i in range(source.shape[0])]
    for copy in made:
        copy.start()
    for copy in made:
        copy.wait()


def adapter_kernel(count, info, *refs):
    made = [pltpu.make_async_copy(refs[i].at[info[2]], refs[count + i], refs[-1].at[i]) for i in range(count)]
    for copy in made:
        copy.start()
    for copy in made:
        copy.wait()


def load_adapters(arrays, info):
    count = len(arrays)
    return pl.pallas_call(
        functools.partial(adapter_kernel, count),
        in_specs=[pl.BlockSpec(memory_space=pltpu.SMEM)] + [pl.BlockSpec(memory_space=pltpu.HBM)] * count,
        out_specs=[pl.BlockSpec(memory_space=pltpu.VMEM)] * count,
        out_shape=[pltpu.VMEM(a.shape[1:], a.dtype) for a in arrays],
        scratch_shapes=[pltpu.SemaphoreType.DMA((count,))],
        compiler_params=pltpu.CompilerParams(vmem_limit_bytes=MIB),
        cost_estimate=pl.CostEstimate(flops=1000, transcendentals=0, bytes_accessed=1000),
        name="adapters",
    )(info, *(in_hbm(a) for a in arrays))


def move_rows(kernel, value, slots, name, here):
    space = pltpu.VMEM if here else pl.ANY
    return pl.pallas_call(
        kernel,
        in_specs=[pl.BlockSpec(memory_space=pltpu.SMEM), pl.BlockSpec(memory_space=pl.ANY if here else pltpu.VMEM)],
        out_specs=pl.BlockSpec(memory_space=space),
        out_shape=(pltpu.VMEM if here else jax.ShapeDtypeStruct)(value.shape, value.dtype),
        scratch_shapes=[pltpu.SemaphoreType.DMA((value.shape[0],))],
        compiler_params=pltpu.CompilerParams(vmem_limit_bytes=MIB),
        cost_estimate=pl.CostEstimate(flops=1000, transcendentals=0, bytes_accessed=1000),
        name=name,
    )(slots, in_hbm(value) if here else in_vmem(value))


def sds(shape, dtype):
    return jax.ShapeDtypeStruct(tuple(shape), dtype)


def in_vmem(value):
    return pltpu.with_memory_space_constraint(value, pltpu.VMEM)


def in_hbm(value):
    return pltpu.with_memory_space_constraint(value, pltpu.HBM)


def call(kernel, info, weights, args, outs, scratch, name, mib, after=(), sems=()):
    vmem = pl.BlockSpec(memory_space=pltpu.VMEM)
    scalars = () if info is None else (info,)
    n, w = len(scalars), len(weights)

    def body(*refs):
        at = n + w + len(args)
        kernel(*refs[:at], *refs[at + len(after):])

    return pl.pallas_call(
        body,
        in_specs=[pl.BlockSpec(memory_space=pltpu.SMEM)] * n + [pl.BlockSpec(memory_space=pltpu.HBM)] * w + [vmem] * len(args)
        + [pl.BlockSpec(memory_space=pl.ANY)] * len(after),
        out_specs=[vmem] * len(outs),
        out_shape=[pltpu.VMEM(tuple(s), d) for s, d in outs],
        scratch_shapes=[pltpu.VMEM(s, d) for s, d in scratch] + ([pltpu.SemaphoreType.DMA(sems)] if sems else []),
        compiler_params=pltpu.CompilerParams(vmem_limit_bytes=mib * MIB),
        cost_estimate=pl.CostEstimate(flops=1000, transcendentals=0, bytes_accessed=1000),
        name=name,
    )(*scalars, *(in_hbm(a) for a in weights), *(in_vmem(a) for a in args), *after)


def whole_spec(value):
    zeros = (0,) * value.ndim
    return pl.BlockSpec(value.shape, lambda i, *_: zeros)


def sum_call(kernel, scalars, groups, outs, name):
    args = [v for group in groups for v in group]
    steps = 2
    specs = [pl.BlockSpec((o.shape[0] // steps,) + o.shape[1:], (lambda n: lambda i, *_: (i,) + (0,) * n)(o.ndim - 1))
             for o in outs]
    return pl.pallas_call(
        functools.partial(kernel, [len(group) for group in groups]),
        grid_spec=pltpu.PrefetchScalarGridSpec(
            num_scalar_prefetch=len(scalars), grid=(steps,),
            in_specs=[whole_spec(a) for a in args], out_specs=specs),
        out_shape=outs,
        compiler_params=pltpu.CompilerParams(
            dimension_semantics=("arbitrary",),
            vmem_limit_bytes=4 * MIB + 2 * sum(a.size * a.dtype.itemsize for a in args)
            + sum(o.size * o.dtype.itemsize for o in outs)),
        cost_estimate=pl.CostEstimate(flops=0, transcendentals=0, bytes_accessed=12000000),
        name=name,
    )(*scalars, *args)


def swap(value, bit, axis, size):
    return lax.ppermute(value, axis, [(i, i ^ bit) for i in range(size)])


def near(value):
    return swap(value, 1, "mp", PARTS)


def far(value):
    return swap(value, 2, "mp", PARTS)


def spread(value):
    there = far(value)
    return (value, near(value), there, near(there))


def chip_sum(keep, send):
    got = near(send)
    lo = keep[:, :QUARTER].astype(F32) + got[:, :QUARTER].astype(F32)
    hi = keep[:, QUARTER:].astype(F32) + got[:, QUARTER:].astype(F32)
    return lo, hi.astype(BF16)


def far_sum_kernel(own, got, out):
    for to, other in ((LO, HI), (HI, LO)):
        out[:, to] = (own[:, to].astype(F32) + got[:, other].astype(F32)).astype(BF16)


def far_sum(own, got):
    return call(far_sum_kernel, None, (), (own, got), [(own.shape, BF16)], [], "far_sum", 6)[0]


def pair_sum_kernel(keep, got, out):
    out[...] = (keep[...] + got[...].astype(F32)).astype(BF16)


def pair_sum(keep, send):
    return call(pair_sum_kernel, None, (), (keep, near(send)), [(send.shape, BF16)], [], "pair_sum", 6)[0]


def late(value, *others):
    return lax.optimization_barrier((value, *others))[0]


def doubled(stack, bit, size):
    return jnp.concatenate([stack, swap(stack, bit, "dp", size)], axis=0)


def entry_of(slot, place, size):
    bits = size.bit_length() - 1
    apart = slot ^ place
    return sum(((apart >> b) & 1) << (bits - 1 - b) for b in range(bits))


def shards(dp, residual, attention_gain, query_matrix, key_value_matrix, output_matrix, feedfwd_gain,
           gate_up_matrix, down_matrix, attention_adapter_input, query_adapter_output,
           key_value_adapter_output, output_adapter_input, output_adapter_output, feedfwd_adapter_input,
           feedfwd_adapter_output, down_adapter_input, down_adapter_output, lengths, adapter_index,
           dealing_slots, cotangent):
    seqs = residual.shape[0]
    length = cotangent.shape[1]
    units = down_matrix.shape[0]
    adapters = attention_adapter_input.shape[0]
    q_cols = query_matrix.shape[1]
    kv_cols = key_value_matrix.shape[2]
    kv_heads = kv_cols // HEAD
    heads = q_cols // HEAD
    rows = length // CHUNKS
    half = 2 * QUARTER
    me = lax.axis_index("mp")
    place = lax.axis_index("dp")

    is_there = dealing_slots[None, :] == jnp.arange(seqs, dtype=jnp.int32)[:, None]
    owners = jnp.sum(jnp.where(is_there, adapter_index[None, :], 0), axis=1)
    spans = jnp.sum(jnp.where(is_there, lengths[None, :], 0), axis=1)
    mine = jnp.arange(seqs, dtype=jnp.int32) == place
    my_length = jnp.sum(jnp.where(mine, spans, 0))
    my_adapter = jnp.sum(jnp.where(mine, owners, 0))
    info = jnp.stack([me.astype(jnp.int32), my_length, my_adapter, place.astype(jnp.int32)])

    gs = spread(cotangent[0])
    gains = jnp.stack(spread(jnp.stack([attention_gain, feedfwd_gain])))
    dealt = lax.all_to_all(
        move_rows(deal_kernel, residual, dealing_slots, "deal", True), "dp", split_axis=0, concat_axis=1, tiled=True
    )[0]
    adapters_here = load_adapters(
        (attention_adapter_input, query_adapter_output, key_value_adapter_output, output_adapter_input,
         output_adapter_output, feedfwd_adapter_input, feedfwd_adapter_output, down_adapter_input,
         down_adapter_output), info)
    a1, qb, kvb, oa, ob, a2, fba, da, bd = adapters_here
    dealt = late(dealt, gs[2], a1, gains)
    beside = near(dealt)
    there = [far(dealt[c * rows:(c + 1) * rows]) for c in range(CHUNKS)]
    xs = [None] * CHUNKS
    cos_np, sin_np = rope_tables(length)
    cos = [jnp.asarray(cos_np[:, c * rows:(c + 1) * rows]) for c in range(CHUNKS)]
    sin = [jnp.asarray(sin_np[:, c * rows:(c + 1) * rows]) for c in range(CHUNKS)]
    wq, wkv, wo = query_matrix, key_value_matrix, output_matrix

    def like(*arrays):
        return [(a.shape, a.dtype) for a in arrays]

    wide, col, block, thin = (rows, WIDTH), (rows, half), (rows, QUARTER), (rows, 1)
    saved, kept, z_own, z_far = ([None] * CHUNKS for _ in range(4))
    order = ()
    for c in range(CHUNKS):
        xs[c] = (dealt, beside, there[c], near(late(there[c], saved[0][0]) if c else there[c]))
        outs = [((3 * RANK, rows), BF16), ((q_cols, rows), BF16), ((kv_heads, rows, HEAD), BF16),
                ((kv_heads, rows, HEAD), BF16), ((kv_cols, rows), BF16), ((kv_cols, rows), BF16)]
        saved[c] = call(
            functools.partial(project_kernel, c), info, (wq, wkv), (*xs[c], gains, a1, qb, kvb, cos[c], sin[c]), outs,
            [(wide, BF16)] + like(wq, wkv), "project_%d" % c, 12, order, (2,))
        outs = [(col, F32), (col, BF16), ((q_cols, rows), BF16), ((heads, rows), F32), ((RANK, rows), BF16)]
        pairs = [v for p in saved[:c + 1] for v in (p[2], p[5])]
        z_keep, z_send, *kept[c] = call(
            functools.partial(attend_kernel, c), info, (wo,), (saved[c][1], oa, ob, *pairs), outs, like(wo),
            "attend_%d" % c, 10, (saved[c][0], there[-1]), (1,))
        z_own[c] = pair_sum(z_keep, late(z_send, z_far[0]) if c else z_send)
        z_far[c] = far(z_own[c])
        order = (kept[c][1], z_own[c])
    def front(c, total, partial, order):
        hidden = (rows, units)
        outs = [(wide, BF16), (block, F32), (wide, BF16), (wide, BF16), (hidden, BF16), (hidden, BF16), (hidden, BF16),
                ((rows, 2 * RANK), BF16), ((rows, RANK), BF16),
                ((3 * RANK * units // QUARTER, QUARTER), BF16 if c else F32)]
        args = (*xs[c], total, near(total), *gs, gains, a2, bd, fba, da, *partial)
        weights = () if c else (gate_up_matrix, down_matrix)
        outs += like(*weights)
        return call(
            functools.partial(front_kernel, c, c == CHUNKS - 1), info, weights, (wgu, wd, *args) if c else args, outs,
            [((ROW_BLOCK, WIDTH), F32)], "front_%d" % c, 8, order, () if c else (2, units // QUARTER))

    def back(c, hidden, partial, order):
        first = col if c else (rows + 3 * RANK, half)
        outs = [(first, F32), (first, BF16), (col, F32), (col, BF16)]
        outs += [((3 * RANK, WIDTH), F32)] if c else []
        return call(
            functools.partial(back_kernel, c == 0), info, (), (wgu, wd, *hidden[2:7], a2, bd, fba, da, *partial), outs,
            [(block, F32), ((3 * RANK, QUARTER), F32)], "back_%d" % c, 8, order)

    def attend_back(c, total, partial, order):
        padded = (rows, half + LANES)
        outs = [(block, F32), (padded, F32), (padded, BF16), (thin, F32), ((3 * RANK, QUARTER), F32 if c else BF16)]
        outs += ([((4 * RANK, WIDTH), F32), ((kv_cols, rows), F32), ((kv_cols, rows), F32)] if c
                 else [((4 * RANK, half), F32), ((4 * RANK, half), BF16)])
        scratch = [(wide, BF16), (wide, BF16), ((ROW_BLOCK, WIDTH), F32), ((q_cols, rows), BF16), ((q_cols, rows), F32),
                   ((c + 1, kv_cols, rows), F32), ((c + 1, kv_cols, rows), F32), ((rows, q_cols + 2 * kv_cols), BF16),
                   (block, F32), ((4 * RANK, QUARTER), F32)]
        triples = [v for p in saved[:c + 1] for v in (p[2], p[3], p[4])]
        return call(
            functools.partial(attend_back_kernel, c, c == 0), info, (wq, wkv, wo),
            (*xs[c], *gs, hidden[c][0], total, near(total), gains, a1, qb, kvb, oa, ob, cos[c], sin[c], *saved[c][:2],
             *kept[c], *triples, *partial), outs, scratch + like(wq, wkv, wo), "attend_back_%d" % c, 18, order, (3,))

    bits = [1 << b for b in reversed(range(dp.bit_length() - 1))]
    hidden, d_own, d_far, y_keep, y_send = ([None] * CHUNKS for _ in range(5))
    *hidden[0], wgu, wd = front(0, far_sum(z_own[0], z_far[0]), (), order)
    step = hidden[0][8]
    hidden[1] = front(1, far_sum(z_own[1], late(z_far[1], step)), hidden[0][9:], (step,))
    fb = hidden[1][9][None]
    fb_first = swap(fb, bits[0], "dp", dp)
    d_keep, d_send, y_keep[1], y_send[1], fa = back(1, hidden[1], (), (hidden[1][8],))
    d_own[1] = pair_sum(d_keep, late(d_send, fb_first))
    d_far[1] = far(d_own[1])
    fb = fb_more = jnp.concatenate([fb, fb_first], axis=0)
    for bit in bits[1:-1]:
        fb_more = doubled(fb_more, bit, dp)
    fb_more = fb_more[2:]
    fb_side = swap(fb, bits[-1], "dp", dp)
    d_keep, d_send, y_keep[0], y_send[0] = back(0, hidden[0], (fa,), (d_own[1],))
    total = far_sum(d_own[1], late(d_far[1], d_send))
    d_own[0] = pair_sum(d_keep, late(d_send, fb_more, fb_side))
    d_far[0] = far(d_own[0])
    fb_more_side = swap(fb_more, bits[-1], "dp", dp)
    dxq, h_keep, h_send, inv, *sums = attend_back(1, total, (), (d_own[0],))
    total = far_sum(d_own[0], late(d_far[0], inv))
    h_low, h_high = chip_sum(h_keep, late(h_send, fb_more_side))
    h_far = far(h_high)
    final = [None, (dxq, h_low, h_high, h_far, inv)]
    y_got = [near(late(v, inv)) for v in y_send]
    fa = total[rows:][None]
    fa_first = swap(fa, bits[0], "dp", dp)
    dxq, h_keep, h_send, inv, att_b, aa_keep, aa_send = attend_back(0, total, sums, (h_high, *y_got))
    ready = (fa_first, h_far)
    aa_low, aa_high = chip_sum(aa_keep, late(aa_send, *ready))
    aa_far = far(aa_high)
    h_low, h_high = chip_sum(h_keep, late(h_send, *ready))
    h_far = far(h_high)
    final[0] = (dxq, h_low, h_high, h_far, inv)
    y_sums = [k + late(g, h_high).astype(F32) for k, g in zip(y_keep, y_got)]
    y_far = far(jnp.concatenate([v[:, QUARTER:] for v in y_sums], axis=0).astype(BF16))
    att = jnp.concatenate([att_b, (aa_low + late(aa_far, h_high).astype(F32)).astype(BF16)], axis=0)[None]
    att = doubled(att, bits[0], dp)

    dinput, = call(finish_kernel, None, (), (gains, dealt, *(v for f in final for v in f)), [((length, QUARTER), BF16)],
                   [], "finish", 8, (att,))
    back_grad = lax.all_to_all(
        dinput.reshape(dp, length // dp, QUARTER), "dp", split_axis=0, concat_axis=0, tiled=True)
    input_grad = move_rows(collect_kernel, back_grad, dealing_slots, "collect_grad", False)

    valid = (jnp.arange(length, dtype=jnp.int32) < my_length)[:, None]
    result = jnp.concatenate([h[1] + v[:, :QUARTER] for h, v in zip(hidden, y_sums)], axis=0)
    result = result + late(y_far, dinput).astype(F32)
    result = jnp.where(valid, result, 0.0).astype(BF16)
    back_out = lax.all_to_all(
        result.reshape(dp, length // dp, QUARTER), "dp", split_axis=0, concat_axis=0, tiled=True)
    output = move_rows(collect_kernel, back_out, late(dealing_slots, input_grad), "collect_out", False)

    fa = late(jnp.concatenate([fa, fa_first], axis=0), h_high)
    for bit in bits[1:-1]:
        fa = doubled(fa, bit, dp)
    fa_side = swap(fa, bits[-1], "dp", dp)
    outs = [sds((adapters, 2 * RANK, WIDTH), F32), sds((adapters, RANK, WIDTH), F32),
            sds((adapters, 2, RANK, units), F32), sds((adapters, RANK, units), F32)]
    ga_ffn, g_down_b, g_ffn_b, g_down_a = sum_call(
        feedforward_sum_kernel, (info, owners),
        ((fb, fb_more, fb_side, fb_more_side), (fa, fa_side), (near(fa), near(fa_side))), outs, "feedforward_sum")

    n_b = att_b.shape[0]
    for bit in bits[1:-1]:
        att = doubled(att, bit, dp)
    att_side = swap(att, bits[-1], "dp", dp)
    att_side = late(att_side, g_down_a, input_grad)
    a_parts = [att[:, n_b:], att_side[:, n_b:]]
    a_far = [far(v) for v in a_parts]
    outs = [sds((adapters, 3 * RANK, WIDTH), F32), sds((adapters, RANK, WIDTH), F32),
            sds((adapters, RANK, q_cols), F32), sds((adapters, 2, RANK, kv_cols), F32),
            sds((adapters, RANK, q_cols), F32)]
    ga_att, g_out_b, g_query_b, g_kv_b, g_out_a = sum_call(
        attention_sum_kernel, (info, owners),
        ((att, att_side), a_parts, [near(v) for v in a_parts], a_far, [near(v) for v in a_far]), outs, "attention_sum")
    return (output, input_grad, ga_att, g_query_b, g_kv_b, g_out_a, g_out_b, ga_ffn, g_ffn_b, g_down_a, g_down_b)


def solution(mesh):
    in_specs = (
        P(None, "dp", "mp"), P("mp"), P(None, "mp"), P(None, None, "mp"), P("mp", None), P("mp"),
        P(None, None, "mp"), P("mp", None), P(), P(None, None, "mp"), P(None, None, None, "mp"),
        P(None, None, "mp"), P(), P(), P(None, None, None, "mp"), P(None, None, "mp"), P(), P(), P(), P(),
        P("dp", None, "mp"),
    )
    out_specs = (
        P(None, "dp", "mp"), P(None, "dp", "mp"), P(), P(None, None, "mp"), P(None, None, None, "mp"),
        P(None, None, "mp"), P(), P(), P(None, None, None, "mp"), P(None, None, "mp"), P(),
    )
    return jax.shard_map(
        functools.partial(shards, mesh.shape["dp"]), mesh=mesh, in_specs=in_specs, out_specs=out_specs,
        check_vma=False)
```

```python
import functools

import jax
import jax.numpy as jnp
import numpy as np
from jax import lax
from jax.experimental import pallas as pl
from jax.experimental.pallas import tpu as pltpu
from jax.sharding import PartitionSpec as P

WIDTH = 2048
HEAD = 64
HALF = HEAD // 2
RANK = 16
EPS = 1e-05
ROPE_BASE = 500000.0
NEG_FILL = -1e30
PARTS = 4
LANES = 128
SPARE = 32
ROW_BLOCK = 64
QUARTER = WIDTH // PARTS
CHUNKS = 2
MIB = 1024 * 1024
F32 = jnp.float32
BF16 = jnp.bfloat16


def nn(a, b):
    return lax.dot_general(a, b, (((1,), (0,)), ((), ())), preferred_element_type=F32)


def nt(a, b):
    return lax.dot_general(a, b, (((1,), (1,)), ((), ())), preferred_element_type=F32)


def rope_tables(length):
    freq = ROPE_BASE ** (-np.arange(HALF, dtype=np.float32) * np.float32(2.0 / HEAD))
    angles = (np.arange(length, dtype=np.float32)[None, :] * freq.astype(np.float32)[:, None]).astype(np.float32)
    return np.cos(angles).astype(np.float32), np.sin(angles).astype(np.float32)


def quarter(me, rel):
    return pl.ds(pl.multiple_of((me ^ rel) * QUARTER, QUARTER), QUARTER)


LO, HI = slice(0, QUARTER), slice(QUARTER, 2 * QUARTER)


def total_block(rel, rows_at, own, oth):
    return (own if rel in (0, 2) else oth)[rows_at, LO if rel in (0, 1) else HI].astype(F32)


def store_block(rel, value, rows_at, keep_ref, send_ref):
    to = pl.ds(pl.multiple_of((rel // 2) * QUARTER, QUARTER), QUARTER)

    @pl.when(rel % 2 == 0)
    def _():
        keep_ref[rows_at, to] = value[...]

    @pl.when(rel % 2 == 1)
    def _():
        send_ref[rows_at, to] = value[...].astype(BF16)


def chunk_of(ref, chunk, rows):
    return ref if ref.shape[0] == rows else ref.at[chunk * rows:(chunk + 1) * rows]


def row_block(i):
    return pl.ds(pl.multiple_of(i * ROW_BLOCK, ROW_BLOCK), ROW_BLOCK)


def is_valid(chunk, i, rows, length):
    return chunk * rows + i * ROW_BLOCK + lax.broadcasted_iota(jnp.int32, (ROW_BLOCK, 1), 0) < length


def copies_of(pairs, sems):
    made = [pltpu.make_async_copy(source, target, sems.at[i]) for i, (source, target) in enumerate(pairs)]
    for copy in made:
        copy.start()
    return made


def put_block(rel, value, keep_ref, send_ref):
    ref = keep_ref if rel in (0, 2) else send_ref
    ref[:, LO if rel in (0, 1) else HI] = value.astype(ref.dtype)


def rotate(value, cos, sin, out_ref):
    for i in range(value.shape[0] // HEAD):
        u1, u2 = value[i * HEAD:i * HEAD + HALF], value[i * HEAD + HALF:(i + 1) * HEAD]
        out_ref[i * HEAD:i * HEAD + HALF, :] = (u1 * cos - u2 * sin).astype(BF16)
        out_ref[i * HEAD + HALF:(i + 1) * HEAD, :] = (u2 * cos + u1 * sin).astype(BF16)


def turn_back(value, cos, sin, out_ref):
    for i in range(value.shape[0] // HEAD):
        w1, w2 = value[i * HEAD:i * HEAD + HALF], value[i * HEAD + HALF:(i + 1) * HEAD]
        out_ref[i * HEAD:i * HEAD + HALF, :] = (w1 * cos + w2 * sin).astype(BF16)
        out_ref[i * HEAD + HALF:(i + 1) * HEAD, :] = (w2 * cos - w1 * sin).astype(BF16)


def head_rows(i):
    return pl.ds(pl.multiple_of(i * HEAD, HEAD), HEAD)


def visible(key_start, query_start, rows, length):
    kpos = key_start + lax.broadcasted_iota(jnp.int32, (rows, rows), 0)
    qpos = query_start + lax.broadcasted_iota(jnp.int32, (rows, rows), 1)
    return (kpos <= qpos) & (kpos < length)


def project_kernel(chunk, info, wq_h, wkv_h, x0, x1, x2, x3, gains, a1, qb, kvb, cos_t, sin_t,
                   t1t_out, qt_out, kn_out, vn_out, kt_out, vt_out, h_out, wq, wkv, sems):
    copies = copies_of(((wkv_h, wkv), (wq_h, wq)), sems)
    me = info[0]
    rows = h_out.shape[0]
    kv_heads = kn_out.shape[0]
    xs = [chunk_of(x, chunk, rows) for x in (x0, x1, x2, x3)]

    def norm(i, carry):
        at = row_block(i)
        square = jnp.zeros((ROW_BLOCK, 1), F32)
        for r in range(PARTS):
            v = xs[r][at, :].astype(F32)
            square = square + jnp.sum(v * v, axis=1, keepdims=True)
        inv = lax.rsqrt(square / WIDTH + EPS)
        for r in range(PARTS):
            v = xs[r][at, :].astype(F32)
            h_out[at, quarter(me, r)] = (v * inv * gains[r, 0:1, :].astype(F32)).astype(BF16)
        return carry

    lax.fori_loop(0, rows // ROW_BLOCK, norm, 0)
    h = h_out[...]
    t1 = nt(h, a1[...])
    t1t_out[...] = t1.T.astype(BF16)
    t1b = t1.astype(BF16)
    cos, sin = cos_t[...], sin_t[...]
    copies[0].wait()
    k = nn(h, wkv[0]) + nn(t1b[:, RANK:2 * RANK], kvb[0])
    rotate(k.T, cos, sin, kt_out)
    k_n = kt_out[...].T
    v_n = (nn(h, wkv[1]) + nn(t1b[:, 2 * RANK:], kvb[1])).astype(BF16)
    vt_out[...] = v_n.T
    for i in range(kv_heads):
        kn_out[i] = k_n[:, i * HEAD:(i + 1) * HEAD]
        vn_out[i] = v_n[:, i * HEAD:(i + 1) * HEAD]
    copies[1].wait()
    q = nn(h, wq[...]) + nn(t1b[:, :RANK], qb[...])
    rotate(q.T * (HEAD ** -0.5), cos, sin, qt_out)


def attend_kernel(chunk, info, wo_h, qt, oa, ob, *rest):
    pairs, rest = rest[:2 * (chunk + 1)], rest[2 * (chunk + 1):]
    z_keep, z_send, ot_out, lse_out, tot_out, wo, sems = rest
    copies = copies_of(((wo_h, wo),), sems)
    keys, values = pairs[0::2], pairs[1::2]
    me, length = info[0], info[1]
    rows = qt.shape[1]
    kv_heads = keys[0].shape[0]
    heads = qt.shape[0] // HEAD
    group = heads // kv_heads

    kept = [jnp.concatenate([visible(c * rows, chunk * rows, rows, length)] * group, axis=1) for c in range(chunk + 1)]

    def one_group(j, carry):
        q_g = jnp.concatenate([qt[head_rows(j * group + g), :] for g in range(group)], axis=1)
        parts = [jnp.where(kept[c], nn(keys[c][j], q_g), NEG_FILL) for c in range(chunk + 1)]
        top = functools.reduce(jnp.maximum, [jnp.max(s, axis=0, keepdims=True) for s in parts])
        es = [jnp.exp(s - top) for s in parts]
        total = sum(jnp.sum(e, axis=0, keepdims=True) for e in es)
        low = top + jnp.log(total)
        o_t = sum(nn(value[head_rows(j), :], e.astype(BF16)) for value, e in zip(values, es))
        o_t = (o_t / total).astype(BF16)
        for g in range(group):
            cols = slice(g * rows, (g + 1) * rows)
            lse_out[pl.ds(j * group + g, 1), :] = low[:, cols]
            ot_out[head_rows(j * group + g), :] = o_t[:, cols]
        return carry

    lax.fori_loop(0, kv_heads, one_group, 0)
    o = ot_out[...].T
    to = nt(o, oa[...])
    tot_out[...] = to.T.astype(BF16)
    to = to.astype(BF16)
    copies[0].wait()
    for r in range(PARTS):
        at = quarter(me, r)
        put_block(r, nn(o, wo[:, at]) + nn(to, ob[:, at]), z_keep, z_send)


def front_kernel(chunk, last, info, wgu_in, wd_in, x0, x1, x2, x3, zo, zp, g0, g1, g2, g3, gains, a2, bd, fb, da,
                 *rest):
    units = wd_in.shape[0]
    if chunk:
        wgu, wd = wgu_in, wd_in
    else:
        (wgu, wd, f_s, sems), rest = rest[-4:], rest[:-4]
        rest = (*rest, f_s)

    def copies(i):
        c = pl.ds(pl.multiple_of(i * QUARTER, QUARTER), QUARTER)
        return (pltpu.make_async_copy(wgu_in.at[:, :, c], wgu.at[:, :, c], sems.at[0, i]),
                pltpu.make_async_copy(wd_in.at[c, :], wd.at[c, :], sems.at[1, i]))

    if not chunk:
        for i in range(units // QUARTER):
            for copy in copies(i):
                copy.start()
    f_s = rest[-1]
    xm_out, xq_out, h_out, g_out, act_out, dg_out, du_out, t2_s, dtd_s, b_out = rest[-11:-1]
    me, length = info[0], info[1]
    rows = h_out.shape[0]
    xs, gs = ([chunk_of(v, chunk, rows) for v in vs] for vs in ((x0, x1, x2, x3), (g0, g1, g2, g3)))

    def norm(i, carry):
        at = row_block(i)
        valid = is_valid(chunk, i, rows, length)
        square = jnp.zeros((ROW_BLOCK, 1), F32)
        for r in range(PARTS):
            v = xs[r][at, :].astype(F32) + total_block(r, at, zo, zp)
            if r == 0:
                xq_out[at, :] = v
            f_s[:, quarter(me, r)] = v
            square = square + jnp.sum(v * v, axis=1, keepdims=True)
            g_out[at, quarter(me, r)] = jnp.where(valid, gs[r][at, :], jnp.zeros((), BF16))
        inv = lax.rsqrt(square / WIDTH + EPS)
        for r in range(PARTS):
            v = f_s[:, quarter(me, r)]
            xm_out[at, quarter(me, r)] = v.astype(BF16)
            h_out[at, quarter(me, r)] = (v * inv * gains[r, 1:2, :].astype(F32)).astype(BF16)
        return carry

    lax.fori_loop(0, rows // ROW_BLOCK, norm, 0)
    t2 = nt(h_out[...], a2[...])
    t2_s[...] = t2.astype(BF16)
    dtd = nt(g_out[...], bd[...])
    dtd_s[...] = dtd.astype(BF16)
    t2t, dtdt = t2.T.astype(BF16), dtd.T.astype(BF16)

    def block(i, carry):
        c = pl.ds(pl.multiple_of(i * QUARTER, QUARTER), QUARTER)
        if not chunk:
            for copy in copies(i):
                copy.wait()
        h, g = h_out[...], g_out[...]
        gate = nn(h, wgu[0, :, c]) + nn(t2_s[:, :RANK], fb[0, :, c])
        up = nn(h, wgu[1, :, c]) + nn(t2_s[:, RANK:], fb[1, :, c])
        dact = nt(g, wd[c, :]) + nn(dtd_s[...], da[:, c])
        sig = 1.0 / (1.0 + jnp.exp(-gate))
        silu = gate * sig
        act = (silu * up).astype(BF16)
        dgate = (dact * up * sig * (1.0 + gate * (1.0 - sig))).astype(BF16)
        dup = (dact * silu).astype(BF16)
        act_out[:, c], dg_out[:, c], du_out[:, c] = act, dgate, dup
        for k, value in enumerate((nn(t2t[:RANK], dgate), nn(t2t[RANK:], dup), nn(dtdt, act))):
            at = pl.ds(pl.multiple_of((3 * i + k) * RANK, RANK), RANK)
            if last:
                value = value + rest[0][at, :]
            b_out[at, :] = value.astype(b_out.dtype)
        return carry

    lax.fori_loop(0, units // QUARTER, block, 0)


def back_kernel(last, info, wgu, wd, h, g, act, dg, du, a2, bd, fb, da, *rest):
    (value_s, low_s), rest = rest[-2:], rest[:-2]
    outs, rest = (rest[-4:], rest[:-4]) if last else (rest[-5:], rest[:-5])
    d_keep, d_send, y_keep, y_send = outs[:4]
    me = info[0]
    rows = h.shape[0]
    own = slice(0, rows)

    dt2 = jnp.concatenate([nt(dg[...], fb[0]), nt(du[...], fb[1])], axis=1)
    dt2b = dt2.astype(BF16)
    td = nt(act[...], da[...])
    tdb = td.astype(BF16)
    dt2t, tdt = dt2.T.astype(BF16), td.T.astype(BF16)

    def block(r, carry):
        at = quarter(me, r)
        value_s[...] = nt(dg[...], wgu[0, at, :]) + nt(du[...], wgu[1, at, :]) + nn(dt2b, a2[:, at])
        store_block(r, value_s, own, d_keep, d_send)
        value_s[...] = nn(act[...], wd[:, at]) + nn(tdb, bd[:, at])
        store_block(r, value_s, own, y_keep, y_send)
        low_s[:2 * RANK, :] = nn(dt2t, h[:, at])
        low_s[2 * RANK:, :] = nn(tdt, g[:, at])
        if last:
            low_s[...] += rest[0][:, at]
            store_block(r, low_s, slice(rows, rows + 3 * RANK), d_keep, d_send)
        else:
            outs[4][:, at] = low_s[...]
        return carry

    lax.fori_loop(0, PARTS, block, 0)


def attend_back_kernel(chunk, last, info, wq_h, wkv_h, wo_h, x0, x1, x2, x3, g0, g1, g2, g3, xm, do_, dp, gains, a1,
                       qb, kvb, oa, ob, cos_t, sin_t, t1t, qt, ot, lse, tot, *rest):
    scratch, rest = rest[-14:], rest[:-14]
    h_in, z_s, f_s, dot_s, dqt_s, dkt_s, dvt_s, dq_s, value_s, low_s, wq, wkv, wo, sems = scratch
    copies = copies_of(((wo_h, wo), (wq_h, wq), (wkv_h, wkv)), sems)
    n_out = 7 if last else 9
    outs, rest = rest[-n_out:], rest[:-n_out]
    dxq_out, h_keep, h_send, inv_out, b_out = outs[:5]
    triples, rest = rest[:3 * (chunk + 1)], rest[3 * (chunk + 1):]
    keys, values, keys_t = triples[0::3], triples[1::3], triples[2::3]
    me, length = info[0], info[1]
    rows = xm.shape[0]
    kv_heads = keys[0].shape[0]
    heads = qt.shape[0] // HEAD
    group = heads // kv_heads
    q_cols, kv_cols = heads * HEAD, kv_heads * HEAD
    xs, gs = ([chunk_of(v, chunk, rows) for v in vs] for vs in ((x0, x1, x2, x3), (g0, g1, g2, g3)))

    def norm_back(i, carry):
        at = row_block(i)
        valid = is_valid(chunk, i, rows, length)
        square, first, inner = (jnp.zeros((ROW_BLOCK, 1), F32) for _ in range(3))
        for r in range(PARTS):
            v = xm[at, quarter(me, r)].astype(F32)
            square = square + jnp.sum(v * v, axis=1, keepdims=True)
            w = total_block(r, at, do_, dp) * gains[r, 1:2, :].astype(F32)
            f_s[:, quarter(me, r)] = w
            inner = inner + jnp.sum(v * w, axis=1, keepdims=True)
            u = xs[r][at, :].astype(F32)
            first = first + jnp.sum(u * u, axis=1, keepdims=True)
        inv_one = lax.rsqrt(first / WIDTH + EPS)
        inv_out[at, :] = inv_one
        inv = lax.rsqrt(square / WIDTH + EPS)
        back = inv * inv * inv * inner / WIDTH
        for r in range(PARTS):
            v = xm[at, quarter(me, r)].astype(F32)
            g = jnp.where(valid, gs[r][at, :].astype(F32), 0.0)
            d = g + inv * f_s[:, quarter(me, r)] - v * back
            if r == 0:
                dxq_out[at, :] = d
            z_s[at, quarter(me, r)] = d.astype(BF16)
            u = xs[r][at, :].astype(F32)
            h_in[at, quarter(me, r)] = (u * inv_one * gains[r, 0:1, :].astype(F32)).astype(BF16)
        return carry

    lax.fori_loop(0, rows // ROW_BLOCK, norm_back, 0)
    dz = z_s[...]
    dto = nt(dz, ob[...])
    copies[0].wait()
    d_o = nt(dz, wo[...]) + nn(dto.astype(BF16), oa[...])
    dot_s[...] = d_o.T.astype(BF16)
    kept = [jnp.concatenate([visible(c * rows, chunk * rows, rows, length)] * group, axis=1) for c in range(chunk + 1)]

    def one_group(j, carry):
        places = [head_rows(j * group + g) for g in range(group)]
        q_g = jnp.concatenate([qt[at, :] for at in places], axis=1)
        do_g = jnp.concatenate([dot_s[at, :] for at in places], axis=1)
        o_g = jnp.concatenate([ot[at, :] for at in places], axis=1)
        low = jnp.concatenate([lse[pl.ds(j * group + g, 1), :] for g in range(group)], axis=1)
        dots = jnp.sum(do_g.astype(F32) * o_g.astype(F32), axis=0, keepdims=True)
        dq_g = 0.0
        for c in range(chunk + 1):
            prob = jnp.where(kept[c], jnp.exp(nn(keys[c][j], q_g) - low), 0.0)
            ds = (prob * (nn(values[c][j], do_g) - dots)).astype(BF16)
            dq_g = dq_g + nn(keys_t[c][head_rows(j), :], ds)
            dk, dv = nt(q_g, ds), nt(do_g, prob.astype(BF16))
            if last:
                dk, dv = dk + rest[2][head_rows(j), :], dv + rest[3][head_rows(j), :]
            dkt_s[c, head_rows(j), :], dvt_s[c, head_rows(j), :] = dk, dv
        for g in range(group):
            dqt_s[places[g], :] = dq_g[:, g * rows:(g + 1) * rows]
        return carry

    lax.fori_loop(0, kv_heads, one_group, 0)
    if not last:
        outs[6][...], outs[7][...] = dkt_s[0], dvt_s[0]
    cos, sin = cos_t[...], sin_t[...]
    dto_t, o_t = dto.T.astype(BF16), ot[...]
    d_out_a = nt(dto_t, o_t)
    turn_back(dqt_s[...], cos * (HEAD ** -0.5), sin * (HEAD ** -0.5), dot_s)
    dq_s[:, :q_cols] = dot_s[...].T
    turn_back(dkt_s[chunk], cos, sin, dot_s)
    dq_s[:, q_cols:q_cols + kv_cols] = dot_s[:kv_cols, :].T
    dq_s[:, q_cols + kv_cols:] = dvt_s[chunk].T.astype(BF16)
    dq, dk, dv = dq_s[:, :q_cols], dq_s[:, q_cols:q_cols + kv_cols], dq_s[:, q_cols + kv_cols:]
    dt1 = jnp.concatenate([nt(dq, qb[...]), nt(dk, kvb[0]), nt(dv, kvb[1])], axis=1)
    dt1b = dt1.astype(BF16)
    kv_pad = jnp.zeros((RANK, QUARTER - 2 * kv_cols), F32)
    d_kv = jnp.concatenate([nn(t1t[RANK:2 * RANK, :], dk), nn(t1t[2 * RANK:, :], dv), kv_pad], axis=1)
    for k, value in enumerate((nn(t1t[:RANK, :], dq), d_out_a, d_kv)):
        at = slice(k * RANK, (k + 1) * RANK)
        if last:
            value = value + rest[0][at, :]
        b_out[at, :] = value.astype(b_out.dtype)
    dt1t = dt1.T.astype(BF16)
    copies[1].wait()
    copies[2].wait()

    def block(r, inner):
        at = quarter(me, r)
        d = nt(dq_s[:, :q_cols], wq[at, :]) + nn(dt1b, a1[:, at])
        d = d + nt(dq_s[:, q_cols:q_cols + kv_cols], wkv[0, at, :]) + nt(dq_s[:, q_cols + kv_cols:], wkv[1, at, :])
        value_s[...] = d
        store_block(r, value_s, slice(0, rows), h_keep, h_send)
        low_s[:3 * RANK, :] = nn(dt1t, h_in[:, at])
        low_s[3 * RANK:, :] = nn(tot[...], z_s[:, at])
        if last:
            low_s[...] += rest[1][:, at]
            store_block(r, low_s, slice(0, 4 * RANK), outs[5], outs[6])
        else:
            outs[5][:, at] = low_s[...]
        return inner + jnp.sum(d * h_in[:, at].astype(F32), axis=1, keepdims=True)

    inner = lax.fori_loop(0, PARTS, block, jnp.zeros((rows, 1), F32))
    inner = jnp.broadcast_to(inner, (rows, LANES)).T[:SPARE // 2, :]
    if last:
        for ref in outs[5:7]:
            for c, value in enumerate((inner, rest[4][...])):
                at = slice(4 * RANK + c * SPARE // 2, 4 * RANK + (c + 1) * SPARE // 2)
                ref[at, QUARTER:QUARTER + rows] = value.astype(ref.dtype)
                ref[at, QUARTER + rows:] = jnp.zeros((SPARE // 2, QUARTER - rows), ref.dtype)
                ref[at, :QUARTER] = jnp.zeros((SPARE // 2, QUARTER), ref.dtype)
    else:
        outs[8][...] = inner


def finish_kernel(info, gains, x_all, aa_high, aa_far, y_far, *refs):
    out = refs[-1]
    gain = gains[0, 0:1, :].astype(F32)
    rows = out.shape[0] // CHUNKS
    inner = aa_high[4 * RANK:, :].astype(F32) + aa_far[4 * RANK:, :].astype(F32)
    for c in range(CHUNKS):
        dx, keep, got, there, inv, xq, y_keep, y_got = refs[8 * c:8 * (c + 1)]
        x = chunk_of(x_all, c, rows)
        at = slice(c * rows, (c + 1) * rows)
        mine = inner[c * SPARE // 2:c * SPARE // 2 + 8, :rows].T[:, 0:1]
        inv = inv[...]
        grad = keep[:, LO] + got[:, LO].astype(F32) + there[...].astype(F32)
        grad = inv * (gain * grad) - x[...].astype(F32) * (inv * inv * mine / WIDTH)
        out[at, LO] = (dx[...] + grad).astype(BF16)
        valid = c * rows + lax.broadcasted_iota(jnp.int32, (rows, 1), 0) < info[1]
        y = xq[...] + y_keep[:, LO] + y_got[:, LO].astype(F32) + y_far[at, :].astype(F32)
        out[at, HI] = jnp.where(valid, y, 0.0).astype(BF16)


def high_sum_kernel(*refs):
    out = refs[-1]
    rows = out.shape[0] // (len(refs) // 2)
    for c in range(len(refs) // 2):
        keep, got = refs[2 * c:2 * c + 2]
        out[c * rows:(c + 1) * rows, :] = (keep[:, HI] + got[:, HI].astype(F32)).astype(BF16)


def high_sum(*pairs):
    args = [v for pair in pairs for v in pair]
    rows = sum(keep.shape[0] for keep, _ in pairs)
    return call(high_sum_kernel, None, (), args, [((rows, QUARTER), BF16)], [], "high_sum", 8)[0]


def split_refs(refs, counts):
    groups = []
    for count in counts:
        groups.append(refs[:count])
        refs = refs[count:]
    return groups, refs


def with_entry(parts, at, use):
    start = 0
    for ref in parts:
        @pl.when((at >= start) & (at < start + ref.shape[0]))
        def _(ref=ref, start=start):
            use(ref, at - start)
        start += ref.shape[0]


def sum_slots(info, owners, out_refs, one_slot):
    count = out_refs[0].shape[0]
    base = pl.program_id(0) * count
    slots = owners.shape[0]
    for ref in out_refs:
        ref[...] = jnp.zeros_like(ref)

    def add(slot, carry):
        owner = owners[slot] - base

        @pl.when((owner >= 0) & (owner < count))
        def _():
            one_slot(owner, entry_of(slot, info[3], slots))
        return carry

    lax.fori_loop(0, slots, add, 0)


def feedforward_sum_kernel(counts, info, owners, *refs):
    (b_parts, *a_parts), outs = split_refs(refs, counts)
    ga, gdb, gb, gda = outs
    me = info[0]

    def one_slot(owner, at):
        def add_b(ref, e):
            for i in range(gda.shape[2] // QUARTER):
                cols = slice(i * QUARTER, (i + 1) * QUARTER)
                base = i * 3 * RANK
                gb[owner, 0, :, cols] += ref[e, base:base + RANK, :].astype(F32)
                gb[owner, 1, :, cols] += ref[e, base + RANK:base + 2 * RANK, :].astype(F32)
                gda[owner, :, cols] += ref[e, base + 2 * RANK:base + 3 * RANK, :].astype(F32)

        with_entry(b_parts, at, add_b)
        for near_bit, parts in enumerate(a_parts):
            def add_a(ref, e, near_bit=near_bit):
                for r, cols in ((near_bit, LO), (near_bit ^ 2, HI)):
                    ga[owner, :, quarter(me, r)] += ref[e, :2 * RANK, cols].astype(F32)
                    gdb[owner, :, quarter(me, r)] += ref[e, 2 * RANK:, cols].astype(F32)

            with_entry(parts, at, add_a)

    sum_slots(info, owners, outs, one_slot)


def attention_sum_kernel(counts, info, owners, *refs):
    (b_parts, *a_parts), outs = split_refs(refs, counts)
    ga, gob, gq, gkv, goa = outs
    me = info[0]
    kv_cols = gkv.shape[3]

    def one_slot(owner, at):
        def add_b(ref, e):
            gq[owner] += ref[e, :RANK, :].astype(F32)
            goa[owner] += ref[e, RANK:2 * RANK, :].astype(F32)
            gkv[owner, 0] += ref[e, 2 * RANK:3 * RANK, :kv_cols].astype(F32)
            gkv[owner, 1] += ref[e, 2 * RANK:3 * RANK, kv_cols:2 * kv_cols].astype(F32)

        with_entry(b_parts, at, add_b)
        for r, parts in enumerate(a_parts):
            def add_a(ref, e, r=r):
                ga[owner, :, quarter(me, r)] += ref[e, :3 * RANK, :].astype(F32)
                gob[owner, :, quarter(me, r)] += ref[e, 3 * RANK:, :].astype(F32)

            with_entry(parts, at, add_a)

    sum_slots(info, owners, outs, one_slot)


def deal_kernel(slots, source, out, sems):
    made = [pltpu.make_async_copy(source.at[i], out.at[slots[i]], sems.at[i]) for i in range(source.shape[0])]
    for copy in made:
        copy.start()
    for copy in made:
        copy.wait()


def collect_kernel(slots, source, *refs):
    sems = refs[-1]
    made = [pltpu.make_async_copy(source.at[slots[i], :, cols], ref.at[i], sems.at[k, i])
            for i in range(source.shape[0]) for k, (ref, cols) in enumerate(zip(refs, (LO, HI)))]
    for copy in made:
        copy.start()
    for copy in made:
        copy.wait()


def adapter_kernel(count, info, *refs):
    made = [pltpu.make_async_copy(refs[i].at[info[2]], refs[count + i], refs[-1].at[i]) for i in range(count)]
    for copy in made:
        copy.start()
    for copy in made:
        copy.wait()


def load_adapters(arrays, info):
    count = len(arrays)
    return pl.pallas_call(
        functools.partial(adapter_kernel, count),
        in_specs=[pl.BlockSpec(memory_space=pltpu.SMEM)] + [pl.BlockSpec(memory_space=pltpu.HBM)] * count,
        out_specs=[pl.BlockSpec(memory_space=pltpu.VMEM)] * count,
        out_shape=[pltpu.VMEM(a.shape[1:], a.dtype) for a in arrays],
        scratch_shapes=[pltpu.SemaphoreType.DMA((count,))],
        compiler_params=pltpu.CompilerParams(vmem_limit_bytes=MIB),
        cost_estimate=pl.CostEstimate(flops=1000, transcendentals=0, bytes_accessed=1000),
        name="adapters",
    )(info, *(in_hbm(a) for a in arrays))


def move_rows(kernel, value, slots, name, outs, in_space, out_space, sems):
    return pl.pallas_call(
        kernel,
        in_specs=[pl.BlockSpec(memory_space=pltpu.SMEM), pl.BlockSpec(memory_space=in_space)],
        out_specs=[pl.BlockSpec(memory_space=out_space)] * len(outs),
        out_shape=outs,
        scratch_shapes=[pltpu.SemaphoreType.DMA(sems)],
        compiler_params=pltpu.CompilerParams(vmem_limit_bytes=MIB),
        cost_estimate=pl.CostEstimate(flops=1000, transcendentals=0, bytes_accessed=1000),
        name=name,
    )(slots, pltpu.with_memory_space_constraint(value, in_space))


def sds(shape, dtype):
    return jax.ShapeDtypeStruct(tuple(shape), dtype)


def in_vmem(value):
    return pltpu.with_memory_space_constraint(value, pltpu.VMEM)


def in_hbm(value):
    return pltpu.with_memory_space_constraint(value, pltpu.HBM)


def call(kernel, info, weights, args, outs, scratch, name, mib, after=(), sems=()):
    vmem = pl.BlockSpec(memory_space=pltpu.VMEM)
    scalars = () if info is None else (info,)
    n, w = len(scalars), len(weights)

    def body(*refs):
        at = n + w + len(args)
        kernel(*refs[:at], *refs[at + len(after):])

    return pl.pallas_call(
        body,
        in_specs=[pl.BlockSpec(memory_space=pltpu.SMEM)] * n + [pl.BlockSpec(memory_space=pltpu.HBM)] * w + [vmem] * len(args)
        + [pl.BlockSpec(memory_space=pl.ANY)] * len(after),
        out_specs=[vmem] * len(outs),
        out_shape=[pltpu.VMEM(tuple(s), d) for s, d in outs],
        scratch_shapes=[pltpu.VMEM(s, d) for s, d in scratch] + ([pltpu.SemaphoreType.DMA(sems)] if sems else []),
        compiler_params=pltpu.CompilerParams(vmem_limit_bytes=mib * MIB),
        cost_estimate=pl.CostEstimate(flops=1000, transcendentals=0, bytes_accessed=1000),
        name=name,
    )(*scalars, *(in_hbm(a) for a in weights), *(in_vmem(a) for a in args), *after)


def whole_spec(value):
    zeros = (0,) * value.ndim
    return pl.BlockSpec(value.shape, lambda i, *_: zeros)


def sum_call(kernel, scalars, groups, outs, name):
    args = [v for group in groups for v in group]
    steps = 2
    specs = [pl.BlockSpec((o.shape[0] // steps,) + o.shape[1:], (lambda n: lambda i, *_: (i,) + (0,) * n)(o.ndim - 1))
             for o in outs]
    return pl.pallas_call(
        functools.partial(kernel, [len(group) for group in groups]),
        grid_spec=pltpu.PrefetchScalarGridSpec(
            num_scalar_prefetch=len(scalars), grid=(steps,),
            in_specs=[whole_spec(a) for a in args], out_specs=specs),
        out_shape=outs,
        compiler_params=pltpu.CompilerParams(
            dimension_semantics=("arbitrary",),
            vmem_limit_bytes=4 * MIB + 2 * sum(a.size * a.dtype.itemsize for a in args)
            + sum(o.size * o.dtype.itemsize for o in outs)),
        cost_estimate=pl.CostEstimate(flops=0, transcendentals=0, bytes_accessed=12000000),
        name=name,
    )(*scalars, *args)


def swap(value, bit, axis, size):
    return lax.ppermute(value, axis, [(i, i ^ bit) for i in range(size)])


def near(value):
    return swap(value, 1, "mp", PARTS)


def far(value):
    return swap(value, 2, "mp", PARTS)


def spread(value):
    there = far(value)
    return (value, near(value), there, near(there))


def far_sum_kernel(own, got, out):
    for to, other in ((LO, HI), (HI, LO)):
        out[:, to] = (own[:, to].astype(F32) + got[:, other].astype(F32)).astype(BF16)


def far_sum(own, got):
    return call(far_sum_kernel, None, (), (own, got), [(own.shape, BF16)], [], "far_sum", 6)[0]


def pair_sum_kernel(keep, got, out):
    out[...] = (keep[...] + got[...].astype(F32)).astype(BF16)


def pair_sum(keep, send):
    return call(pair_sum_kernel, None, (), (keep, near(send)), [(send.shape, BF16)], [], "pair_sum", 6)[0]


def late(value, *others):
    return lax.optimization_barrier((value, *others))[0]


def doubled(stack, bit, size):
    return jnp.concatenate([stack, swap(stack, bit, "dp", size)], axis=0)


def entry_of(slot, place, size):
    bits = size.bit_length() - 1
    apart = slot ^ place
    return sum(((apart >> b) & 1) << (bits - 1 - b) for b in range(bits))


def shards(dp, residual, attention_gain, query_matrix, key_value_matrix, output_matrix, feedfwd_gain,
           gate_up_matrix, down_matrix, attention_adapter_input, query_adapter_output,
           key_value_adapter_output, output_adapter_input, output_adapter_output, feedfwd_adapter_input,
           feedfwd_adapter_output, down_adapter_input, down_adapter_output, lengths, adapter_index,
           dealing_slots, cotangent):
    seqs = residual.shape[0]
    length = cotangent.shape[1]
    units = down_matrix.shape[0]
    adapters = attention_adapter_input.shape[0]
    q_cols = query_matrix.shape[1]
    kv_cols = key_value_matrix.shape[2]
    kv_heads = kv_cols // HEAD
    heads = q_cols // HEAD
    rows = length // CHUNKS
    half = 2 * QUARTER
    me = lax.axis_index("mp")
    place = lax.axis_index("dp")

    is_there = dealing_slots[None, :] == jnp.arange(seqs, dtype=jnp.int32)[:, None]
    owners = jnp.sum(jnp.where(is_there, adapter_index[None, :], 0), axis=1)
    spans = jnp.sum(jnp.where(is_there, lengths[None, :], 0), axis=1)
    mine = jnp.arange(seqs, dtype=jnp.int32) == place
    my_length = jnp.sum(jnp.where(mine, spans, 0))
    my_adapter = jnp.sum(jnp.where(mine, owners, 0))
    info = jnp.stack([me.astype(jnp.int32), my_length, my_adapter, place.astype(jnp.int32)])

    both = jnp.stack([attention_gain, feedfwd_gain])
    gs = spread(jnp.concatenate([cotangent[0], both, jnp.zeros((14, QUARTER), BF16)], axis=0))
    gains = jnp.stack([v[length:length + 2] for v in gs])
    ordered, = move_rows(deal_kernel, residual, dealing_slots, "deal", [pltpu.VMEM(residual.shape, BF16)], pltpu.HBM,
                         pltpu.VMEM, (seqs,))
    dealt = lax.all_to_all(ordered, "dp", split_axis=0, concat_axis=1, tiled=True)[0]
    adapters_here = load_adapters(
        (attention_adapter_input, query_adapter_output, key_value_adapter_output, output_adapter_input,
         output_adapter_output, feedfwd_adapter_input, feedfwd_adapter_output, down_adapter_input,
         down_adapter_output), info)
    a1, qb, kvb, oa, ob, a2, fba, da, bd = adapters_here
    dealt = late(dealt, gs[2], a1)
    beside = near(dealt)
    there = [far(dealt[c * rows:(c + 1) * rows]) for c in range(CHUNKS)]
    xs = [None] * CHUNKS
    cos_np, sin_np = rope_tables(length)
    cos = [jnp.asarray(cos_np[:, c * rows:(c + 1) * rows]) for c in range(CHUNKS)]
    sin = [jnp.asarray(sin_np[:, c * rows:(c + 1) * rows]) for c in range(CHUNKS)]
    wq, wkv, wo = query_matrix, key_value_matrix, output_matrix

    def like(*arrays):
        return [(a.shape, a.dtype) for a in arrays]

    wide, col, block, thin = (rows, WIDTH), (rows, half), (rows, QUARTER), (rows, 1)
    saved, kept, z_own, z_far = ([None] * CHUNKS for _ in range(4))
    order = ()
    for c in range(CHUNKS):
        xs[c] = (dealt, beside, there[c], near(late(there[c], saved[0][0]) if c else there[c]))
        outs = [((3 * RANK, rows), BF16), ((q_cols, rows), BF16), ((kv_heads, rows, HEAD), BF16),
                ((kv_heads, rows, HEAD), BF16), ((kv_cols, rows), BF16), ((kv_cols, rows), BF16)]
        saved[c] = call(
            functools.partial(project_kernel, c), info, (wq, wkv), (*xs[c], gains, a1, qb, kvb, cos[c], sin[c]), outs,
            [(wide, BF16)] + like(wq, wkv), "project_%d" % c, 12, order, (2,))
        outs = [(col, F32), (col, BF16), ((q_cols, rows), BF16), ((heads, rows), F32), ((RANK, rows), BF16)]
        pairs = [v for p in saved[:c + 1] for v in (p[2], p[5])]
        z_keep, z_send, *kept[c] = call(
            functools.partial(attend_kernel, c), info, (wo,), (saved[c][1], oa, ob, *pairs), outs, like(wo),
            "attend_%d" % c, 10, (saved[c][0],), (1,))
        z_own[c] = pair_sum(z_keep, late(z_send, z_far[0] if c else there[-1]))
        z_far[c] = far(z_own[c])
        order = (kept[c][1], z_own[c])
    def front(c, total, partial, order):
        hidden = (rows, units)
        outs = [(wide, BF16), (block, F32), (wide, BF16), (wide, BF16), (hidden, BF16), (hidden, BF16), (hidden, BF16),
                ((rows, 2 * RANK), BF16), ((rows, RANK), BF16),
                ((3 * RANK * units // QUARTER, QUARTER), BF16 if c else F32)]
        args = (*xs[c], total, near(total), *gs, gains, a2, bd, fba, da, *partial)
        weights = () if c else (gate_up_matrix, down_matrix)
        outs += like(*weights)
        return call(
            functools.partial(front_kernel, c, c == CHUNKS - 1), info, weights, (wgu, wd, *args) if c else args, outs,
            [((ROW_BLOCK, WIDTH), F32)], "front_%d" % c, 8, order, () if c else (2, units // QUARTER))

    def back(c, hidden, partial, order):
        first = col if c else (rows + 3 * RANK, half)
        outs = [(first, F32), (first, BF16), (col, F32), (col, BF16)]
        outs += [((3 * RANK, WIDTH), F32)] if c else []
        return call(
            functools.partial(back_kernel, c == 0), info, (), (wgu, wd, *hidden[2:7], a2, bd, fba, da, *partial), outs,
            [(block, F32), ((3 * RANK, QUARTER), F32)], "back_%d" % c, 8, order)

    def attend_back(c, total, partial, order):
        outs = [(block, F32), (col, F32), (col, BF16), (thin, F32), ((3 * RANK, QUARTER), F32 if c else BF16)]
        low = (4 * RANK + SPARE, half)
        outs += ([((4 * RANK, WIDTH), F32), ((kv_cols, rows), F32), ((kv_cols, rows), F32), ((SPARE // 2, rows), F32)]
                 if c else [(low, F32), (low, BF16)])
        scratch = [(wide, BF16), (wide, BF16), ((ROW_BLOCK, WIDTH), F32), ((q_cols, rows), BF16), ((q_cols, rows), F32),
                   ((c + 1, kv_cols, rows), F32), ((c + 1, kv_cols, rows), F32), ((rows, q_cols + 2 * kv_cols), BF16),
                   (block, F32), ((4 * RANK, QUARTER), F32)]
        triples = [v for p in saved[:c + 1] for v in (p[2], p[3], p[4])]
        return call(
            functools.partial(attend_back_kernel, c, c == 0), info, (wq, wkv, wo),
            (*xs[c], *gs, hidden[c][0], total, near(total), gains, a1, qb, kvb, oa, ob, cos[c], sin[c], *saved[c][:2],
             *kept[c], *triples, *partial), outs, scratch + like(wq, wkv, wo), "attend_back_%d" % c, 18, order, (3,))

    bits = [1 << b for b in reversed(range(dp.bit_length() - 1))]
    hidden, d_own, d_far, y_keep, y_send = ([None] * CHUNKS for _ in range(5))
    *hidden[0], wgu, wd = front(0, far_sum(z_own[0], z_far[0]), (), order)
    step = hidden[0][8]
    hidden[1] = front(1, far_sum(z_own[1], late(z_far[1], step)), hidden[0][9:], (step,))
    fb = hidden[1][9][None]
    fb_first = swap(fb, bits[0], "dp", dp)
    d_keep, d_send, y_keep[1], y_send[1], fa = back(1, hidden[1], (), (hidden[1][8],))
    d_own[1] = pair_sum(d_keep, late(d_send, fb_first))
    d_far[1] = far(d_own[1])
    fb = fb_more = jnp.concatenate([fb, fb_first], axis=0)
    for bit in bits[1:-1]:
        fb_more = doubled(fb_more, bit, dp)
    fb_more = fb_more[2:]
    fb_side = swap(fb, bits[-1], "dp", dp)
    d_keep, d_send, y_keep[0], y_send[0] = back(0, hidden[0], (fa,), (d_own[1],))
    total = far_sum(d_own[1], late(d_far[1], d_send))
    d_own[0] = pair_sum(d_keep, late(d_send, fb_more, fb_side))
    d_far[0] = far(d_own[0])
    fb_more_side = swap(fb_more, bits[-1], "dp", dp)
    y_got = [near(late(v, d_own[0])) for v in y_send]
    dxq, h_keep, h_send, inv, *sums = attend_back(1, total, (), (d_own[0],))
    total = far_sum(d_own[0], late(d_far[0], inv))
    y_high = high_sum(*((y_keep[c], late(y_got[c], inv)) for c in range(CHUNKS)))
    y_far = far(y_high)
    h_got = near(late(h_send, fb_more_side))
    h_high = high_sum((h_keep, h_got))
    h_far = far(h_high)
    final = [None, (dxq, h_keep, h_got, h_far, inv)]
    fa = total[rows:][None]
    fa_first = swap(fa, bits[0], "dp", dp)
    dxq, h_keep, h_send, inv, att_b, aa_keep, aa_send = attend_back(0, total, sums, (h_high, y_high))
    ready = (fa_first, h_far, y_far)
    aa_got = near(late(aa_send, *ready))
    aa_high = high_sum((aa_keep, aa_got))
    aa_far = far(aa_high)
    h_got = near(late(h_send, *ready))
    h_high = high_sum((h_keep, h_got))
    h_far = far(h_high)
    final[0] = (dxq, h_keep, h_got, h_far, inv)
    att_a = aa_keep[:4 * RANK, :QUARTER] + aa_got[:4 * RANK, :QUARTER].astype(F32)
    att_a = (att_a + late(aa_far, h_high)[:4 * RANK].astype(F32)).astype(BF16)
    n_b = att_b.shape[0]
    att = jnp.concatenate([att_b, att_a], axis=0)[None]
    att = doubled(att, bits[0], dp)
    att = late(att, h_far)
    for bit in bits[1:-1]:
        att = doubled(att, bit, dp)
    fa = late(jnp.concatenate([fa, fa_first], axis=0), aa_high)
    for bit in bits[1:-1]:
        fa = doubled(fa, bit, dp)
    fa_side = swap(fa, bits[-1], "dp", dp)

    parts = [v for c in range(CHUNKS) for v in (*final[c], hidden[c][1], y_keep[c], y_got[c])]
    both, = call(finish_kernel, info, (), (gains, dealt, aa_high, aa_far, y_far, *parts), [((length, half), BF16)], [],
                 "finish", 12, (att, fa_side))
    both = lax.all_to_all(both.reshape(dp, length // dp, half), "dp", split_axis=0, concat_axis=0, tiled=True)
    rows_out = sds((seqs, length // dp, QUARTER), BF16)
    input_grad, output = move_rows(collect_kernel, both, dealing_slots, "collect", [rows_out, rows_out], pltpu.VMEM,
                                   pl.ANY, (2, seqs))

    outs = [sds((adapters, 2 * RANK, WIDTH), F32), sds((adapters, RANK, WIDTH), F32),
            sds((adapters, 2, RANK, units), F32), sds((adapters, RANK, units), F32)]
    ga_ffn, g_down_b, g_ffn_b, g_down_a = sum_call(
        feedforward_sum_kernel, (info, owners),
        ((fb, fb_more, fb_side, fb_more_side), (fa, fa_side), (near(fa), near(fa_side))), outs, "feedforward_sum")

    att_side = swap(att, bits[-1], "dp", dp)
    att_side = late(att_side, g_down_a)
    a_parts = [att[:, n_b:], att_side[:, n_b:]]
    a_far = [far(v) for v in a_parts]
    outs = [sds((adapters, 3 * RANK, WIDTH), F32), sds((adapters, RANK, WIDTH), F32),
            sds((adapters, RANK, q_cols), F32), sds((adapters, 2, RANK, kv_cols), F32),
            sds((adapters, RANK, q_cols), F32)]
    ga_att, g_out_b, g_query_b, g_kv_b, g_out_a = sum_call(
        attention_sum_kernel, (info, owners),
        ((att, att_side), a_parts, [near(v) for v in a_parts], a_far, [near(v) for v in a_far]), outs, "attention_sum")
    return (output, input_grad, ga_att, g_query_b, g_kv_b, g_out_a, g_out_b, ga_ffn, g_ffn_b, g_down_a, g_down_b)


def solution(mesh):
    in_specs = (
        P(None, "dp", "mp"), P("mp"), P(None, "mp"), P(None, None, "mp"), P("mp", None), P("mp"),
        P(None, None, "mp"), P("mp", None), P(), P(None, None, "mp"), P(None, None, None, "mp"),
        P(None, None, "mp"), P(), P(), P(None, None, None, "mp"), P(None, None, "mp"), P(), P(), P(), P(),
        P("dp", None, "mp"),
    )
    out_specs = (
        P(None, "dp", "mp"), P(None, "dp", "mp"), P(), P(None, None, "mp"), P(None, None, None, "mp"),
        P(None, None, "mp"), P(), P(), P(None, None, None, "mp"), P(None, None, "mp"), P(),
    )
    return jax.shard_map(
        functools.partial(shards, mesh.shape["dp"]), mesh=mesh, in_specs=in_specs, out_specs=out_specs,
        check_vma=False)
```

```python
import functools

import jax
import jax.numpy as jnp
import numpy as np
from jax import lax
from jax.experimental import pallas as pl
from jax.experimental.pallas import tpu as pltpu
from jax.sharding import PartitionSpec as P

WIDTH = 2048
HEAD = 64
HALF = HEAD // 2
RANK = 16
EPS = 1e-05
ROPE_BASE = 500000.0
NEG_FILL = -1e30
PARTS = 4
LANES = 128
SPARE = 32
ROW_BLOCK = 64
QUARTER = WIDTH // PARTS
CHUNKS = 2
MIB = 1024 * 1024
F32 = jnp.float32
BF16 = jnp.bfloat16


def nn(a, b):
    return lax.dot_general(a, b, (((1,), (0,)), ((), ())), preferred_element_type=F32)


def nt(a, b):
    return lax.dot_general(a, b, (((1,), (1,)), ((), ())), preferred_element_type=F32)


def rope_tables(length):
    freq = ROPE_BASE ** (-np.arange(HALF, dtype=np.float32) * np.float32(2.0 / HEAD))
    angles = (np.arange(length, dtype=np.float32)[None, :] * freq.astype(np.float32)[:, None]).astype(np.float32)
    return np.cos(angles).astype(np.float32), np.sin(angles).astype(np.float32)


def quarter(me, rel):
    return pl.ds(pl.multiple_of((me ^ rel) * QUARTER, QUARTER), QUARTER)


LO, HI = slice(0, QUARTER), slice(QUARTER, 2 * QUARTER)


def total_block(rel, rows_at, own, oth):
    return (own if rel in (0, 2) else oth)[rows_at, LO if rel in (0, 1) else HI].astype(F32)


def store_block(rel, value, rows_at, keep_ref, send_ref):
    to = pl.ds(pl.multiple_of((rel // 2) * QUARTER, QUARTER), QUARTER)

    @pl.when(rel % 2 == 0)
    def _():
        keep_ref[rows_at, to] = value[...]

    @pl.when(rel % 2 == 1)
    def _():
        send_ref[rows_at, to] = value[...].astype(BF16)


def chunk_of(ref, chunk, rows):
    return ref if ref.shape[0] == rows else ref.at[chunk * rows:(chunk + 1) * rows]


def row_block(i):
    return pl.ds(pl.multiple_of(i * ROW_BLOCK, ROW_BLOCK), ROW_BLOCK)


def is_valid(chunk, i, rows, length):
    return chunk * rows + i * ROW_BLOCK + lax.broadcasted_iota(jnp.int32, (ROW_BLOCK, 1), 0) < length


def copies_of(pairs, sems):
    made = [pltpu.make_async_copy(source, target, sems.at[i]) for i, (source, target) in enumerate(pairs)]
    for copy in made:
        copy.start()
    return made


def put_block(rel, value, keep_ref, send_ref):
    ref = keep_ref if rel in (0, 2) else send_ref
    ref[:, LO if rel in (0, 1) else HI] = value.astype(ref.dtype)


def rotate(value, cos, sin, out_ref):
    for i in range(value.shape[0] // HEAD):
        u1, u2 = value[i * HEAD:i * HEAD + HALF], value[i * HEAD + HALF:(i + 1) * HEAD]
        out_ref[i * HEAD:i * HEAD + HALF, :] = (u1 * cos - u2 * sin).astype(BF16)
        out_ref[i * HEAD + HALF:(i + 1) * HEAD, :] = (u2 * cos + u1 * sin).astype(BF16)


def turn_back(value, cos, sin, out_ref):
    for i in range(value.shape[0] // HEAD):
        w1, w2 = value[i * HEAD:i * HEAD + HALF], value[i * HEAD + HALF:(i + 1) * HEAD]
        out_ref[i * HEAD:i * HEAD + HALF, :] = (w1 * cos + w2 * sin).astype(BF16)
        out_ref[i * HEAD + HALF:(i + 1) * HEAD, :] = (w2 * cos - w1 * sin).astype(BF16)


def head_rows(i):
    return pl.ds(pl.multiple_of(i * HEAD, HEAD), HEAD)


def visible(key_start, query_start, rows, length):
    kpos = key_start + lax.broadcasted_iota(jnp.int32, (rows, rows), 0)
    qpos = query_start + lax.broadcasted_iota(jnp.int32, (rows, rows), 1)
    return (kpos <= qpos) & (kpos < length)


def project_kernel(chunk, info, wq_h, wkv_h, x0, x1, x2, x3, gains, a1, qb, kvb, cos_t, sin_t,
                   t1t_out, qt_out, kn_out, vn_out, kt_out, vt_out, h_out, wq, wkv, sems):
    copies = copies_of(((wkv_h, wkv), (wq_h, wq)), sems)
    me = info[0]
    rows = h_out.shape[0]
    kv_heads = kn_out.shape[0]
    xs = [chunk_of(x, chunk, rows) for x in (x0, x1, x2, x3)]

    def norm(i, carry):
        at = row_block(i)
        square = jnp.zeros((ROW_BLOCK, 1), F32)
        for r in range(PARTS):
            v = xs[r][at, :].astype(F32)
            square = square + jnp.sum(v * v, axis=1, keepdims=True)
        inv = lax.rsqrt(square / WIDTH + EPS)
        for r in range(PARTS):
            v = xs[r][at, :].astype(F32)
            h_out[at, quarter(me, r)] = (v * inv * gains[r, 0:1, :].astype(F32)).astype(BF16)
        return carry

    lax.fori_loop(0, rows // ROW_BLOCK, norm, 0)
    h = h_out[...]
    t1 = nt(h, a1[...])
    t1t_out[...] = t1.T.astype(BF16)
    t1b = t1.astype(BF16)
    cos, sin = cos_t[...], sin_t[...]
    copies[0].wait()
    k = nn(h, wkv[0]) + nn(t1b[:, RANK:2 * RANK], kvb[0])
    rotate(k.T, cos, sin, kt_out)
    k_n = kt_out[...].T
    v_n = (nn(h, wkv[1]) + nn(t1b[:, 2 * RANK:], kvb[1])).astype(BF16)
    vt_out[...] = v_n.T
    for i in range(kv_heads):
        kn_out[i] = k_n[:, i * HEAD:(i + 1) * HEAD]
        vn_out[i] = v_n[:, i * HEAD:(i + 1) * HEAD]
    copies[1].wait()
    q = nn(h, wq[...]) + nn(t1b[:, :RANK], qb[...])
    rotate(q.T * (HEAD ** -0.5), cos, sin, qt_out)


def attend_kernel(chunk, info, wo_h, qt, oa, ob, *rest):
    pairs, rest = rest[:2 * (chunk + 1)], rest[2 * (chunk + 1):]
    z_keep, z_send, ot_out, lse_out, tot_out, wo, sems = rest
    copies = copies_of(((wo_h, wo),), sems)
    keys, values = pairs[0::2], pairs[1::2]
    me, length = info[0], info[1]
    rows = qt.shape[1]
    kv_heads = keys[0].shape[0]
    heads = qt.shape[0] // HEAD
    group = heads // kv_heads

    kept = [jnp.concatenate([visible(c * rows, chunk * rows, rows, length)] * group, axis=1) for c in range(chunk + 1)]

    def one_group(j, carry):
        q_g = jnp.concatenate([qt[head_rows(j * group + g), :] for g in range(group)], axis=1)
        parts = [jnp.where(kept[c], nn(keys[c][j], q_g), NEG_FILL) for c in range(chunk + 1)]
        top = functools.reduce(jnp.maximum, [jnp.max(s, axis=0, keepdims=True) for s in parts])
        es = [jnp.exp(s - top) for s in parts]
        total = sum(jnp.sum(e, axis=0, keepdims=True) for e in es)
        low = top + jnp.log(total)
        o_t = sum(nn(value[head_rows(j), :], e.astype(BF16)) for value, e in zip(values, es))
        o_t = (o_t / total).astype(BF16)
        for g in range(group):
            cols = slice(g * rows, (g + 1) * rows)
            lse_out[pl.ds(j * group + g, 1), :] = low[:, cols]
            ot_out[head_rows(j * group + g), :] = o_t[:, cols]
        return carry

    lax.fori_loop(0, kv_heads, one_group, 0)
    o = ot_out[...].T
    to = nt(o, oa[...])
    tot_out[...] = to.T.astype(BF16)
    to = to.astype(BF16)
    copies[0].wait()
    for r in range(PARTS):
        at = quarter(me, r)
        put_block(r, nn(o, wo[:, at]) + nn(to, ob[:, at]), z_keep, z_send)


def front_kernel(chunk, last, info, wgu_in, wd_in, x0, x1, x2, x3, zo, zp, g0, g1, g2, g3, gains, a2, bd, fb, da,
                 *rest):
    units = wd_in.shape[0]
    if chunk:
        wgu, wd = wgu_in, wd_in
        outs, (f_s, value_s) = rest[-15:-2], rest[-2:]
    else:
        outs, (wgu, wd, f_s, value_s, sems) = rest[-18:-5], rest[-5:]
    xm_out, xq_out, h_out, g_out, act_out, dg_out, du_out, t2_s, dtd_s, b_out, y_keep, y_send, td_out = outs

    def copies(i):
        c = pl.ds(pl.multiple_of(i * QUARTER, QUARTER), QUARTER)
        return (pltpu.make_async_copy(wgu_in.at[:, :, c], wgu.at[:, :, c], sems.at[0, i]),
                pltpu.make_async_copy(wd_in.at[c, :], wd.at[c, :], sems.at[1, i]))

    if not chunk:
        for i in range(units // QUARTER):
            for copy in copies(i):
                copy.start()
    me, length = info[0], info[1]
    rows = h_out.shape[0]
    xs, gs = ([chunk_of(v, chunk, rows) for v in vs] for vs in ((x0, x1, x2, x3), (g0, g1, g2, g3)))

    def norm(i, carry):
        at = row_block(i)
        valid = is_valid(chunk, i, rows, length)
        square = jnp.zeros((ROW_BLOCK, 1), F32)
        for r in range(PARTS):
            v = xs[r][at, :].astype(F32) + total_block(r, at, zo, zp)
            if r == 0:
                xq_out[at, :] = v
            f_s[:, quarter(me, r)] = v
            square = square + jnp.sum(v * v, axis=1, keepdims=True)
            g_out[at, quarter(me, r)] = jnp.where(valid, gs[r][at, :], jnp.zeros((), BF16))
        inv = lax.rsqrt(square / WIDTH + EPS)
        for r in range(PARTS):
            v = f_s[:, quarter(me, r)]
            xm_out[at, quarter(me, r)] = v.astype(BF16)
            h_out[at, quarter(me, r)] = (v * inv * gains[r, 1:2, :].astype(F32)).astype(BF16)
        return carry

    lax.fori_loop(0, rows // ROW_BLOCK, norm, 0)
    t2 = nt(h_out[...], a2[...])
    t2_s[...] = t2.astype(BF16)
    dtd = nt(g_out[...], bd[...])
    dtd_s[...] = dtd.astype(BF16)
    t2t, dtdt = t2.T.astype(BF16), dtd.T.astype(BF16)

    def block(i, carry):
        c = pl.ds(pl.multiple_of(i * QUARTER, QUARTER), QUARTER)
        if not chunk:
            for copy in copies(i):
                copy.wait()
        h, g = h_out[...], g_out[...]
        gate = nn(h, wgu[0, :, c]) + nn(t2_s[:, :RANK], fb[0, :, c])
        up = nn(h, wgu[1, :, c]) + nn(t2_s[:, RANK:], fb[1, :, c])
        dact = nt(g, wd[c, :]) + nn(dtd_s[...], da[:, c])
        sig = 1.0 / (1.0 + jnp.exp(-gate))
        silu = gate * sig
        act = (silu * up).astype(BF16)
        dgate = (dact * up * sig * (1.0 + gate * (1.0 - sig))).astype(BF16)
        dup = (dact * silu).astype(BF16)
        act_out[:, c], dg_out[:, c], du_out[:, c] = act, dgate, dup
        for k, value in enumerate((nn(t2t[:RANK], dgate), nn(t2t[RANK:], dup), nn(dtdt, act))):
            at = pl.ds(pl.multiple_of((3 * i + k) * RANK, RANK), RANK)
            if last:
                value = value + rest[0][at, :]
            b_out[at, :] = value.astype(b_out.dtype)
        return carry

    lax.fori_loop(0, units // QUARTER, block, 0)
    td = nt(act_out[...], da[...])
    td_out[...] = td
    tdb = td.astype(BF16)

    def down(r, carry):
        at = quarter(me, r)
        value_s[...] = nn(act_out[...], wd[:, at]) + nn(tdb, bd[:, at])
        store_block(r, value_s, slice(0, rows), y_keep, y_send)
        return carry

    lax.fori_loop(0, PARTS, down, 0)


def back_kernel(last, info, wgu, h, g, td, dg, du, a2, fb, *rest):
    (value_s, low_s), rest = rest[-2:], rest[:-2]
    outs, rest = (rest[-2:], rest[:-2]) if last else (rest[-3:], rest[:-3])
    d_keep, d_send = outs[:2]
    me = info[0]
    rows = h.shape[0]
    dt2 = jnp.concatenate([nt(dg[...], fb[0]), nt(du[...], fb[1])], axis=1)
    dt2b = dt2.astype(BF16)
    dt2t, tdt = dt2.T.astype(BF16), td[...].T.astype(BF16)

    def block(r, carry):
        at = quarter(me, r)
        value_s[...] = nt(dg[...], wgu[0, at, :]) + nt(du[...], wgu[1, at, :]) + nn(dt2b, a2[:, at])
        store_block(r, value_s, slice(0, rows), d_keep, d_send)
        low_s[:2 * RANK, :] = nn(dt2t, h[:, at])
        low_s[2 * RANK:, :] = nn(tdt, g[:, at])
        if last:
            low_s[...] += rest[0][:, at]
            store_block(r, low_s, slice(rows, rows + 3 * RANK), d_keep, d_send)
        else:
            outs[2][:, at] = low_s[...]
        return carry

    lax.fori_loop(0, PARTS, block, 0)


def attend_back_kernel(chunk, last, info, wq_h, wkv_h, wo_h, x0, x1, x2, x3, g0, g1, g2, g3, xm, do_, dp, gains, a1,
                       qb, kvb, oa, ob, cos_t, sin_t, t1t, qt, ot, lse, tot, *rest):
    scratch, rest = rest[-14:], rest[:-14]
    h_in, z_s, f_s, dot_s, dqt_s, dkt_s, dvt_s, dq_s, value_s, low_s, wq, wkv, wo, sems = scratch
    copies = copies_of(((wo_h, wo), (wq_h, wq), (wkv_h, wkv)), sems)
    n_out = 7 if last else 9
    outs, rest = rest[-n_out:], rest[:-n_out]
    dxq_out, h_keep, h_send, inv_out, b_out = outs[:5]
    triples, rest = rest[:3 * (chunk + 1)], rest[3 * (chunk + 1):]
    keys, values, keys_t = triples[0::3], triples[1::3], triples[2::3]
    me, length = info[0], info[1]
    rows = xm.shape[0]
    kv_heads = keys[0].shape[0]
    heads = qt.shape[0] // HEAD
    group = heads // kv_heads
    q_cols, kv_cols = heads * HEAD, kv_heads * HEAD
    xs, gs = ([chunk_of(v, chunk, rows) for v in vs] for vs in ((x0, x1, x2, x3), (g0, g1, g2, g3)))

    def norm_back(i, carry):
        at = row_block(i)
        valid = is_valid(chunk, i, rows, length)
        square, first, inner = (jnp.zeros((ROW_BLOCK, 1), F32) for _ in range(3))
        for r in range(PARTS):
            v = xm[at, quarter(me, r)].astype(F32)
            square = square + jnp.sum(v * v, axis=1, keepdims=True)
            w = total_block(r, at, do_, dp) * gains[r, 1:2, :].astype(F32)
            f_s[:, quarter(me, r)] = w
            inner = inner + jnp.sum(v * w, axis=1, keepdims=True)
            u = xs[r][at, :].astype(F32)
            first = first + jnp.sum(u * u, axis=1, keepdims=True)
        inv_one = lax.rsqrt(first / WIDTH + EPS)
        inv_out[at, :] = inv_one
        inv = lax.rsqrt(square / WIDTH + EPS)
        back = inv * inv * inv * inner / WIDTH
        for r in range(PARTS):
            v = xm[at, quarter(me, r)].astype(F32)
            g = jnp.where(valid, gs[r][at, :].astype(F32), 0.0)
            d = g + inv * f_s[:, quarter(me, r)] - v * back
            if r == 0:
                dxq_out[at, :] = d
            z_s[at, quarter(me, r)] = d.astype(BF16)
            u = xs[r][at, :].astype(F32)
            h_in[at, quarter(me, r)] = (u * inv_one * gains[r, 0:1, :].astype(F32)).astype(BF16)
        return carry

    lax.fori_loop(0, rows // ROW_BLOCK, norm_back, 0)
    dz = z_s[...]
    dto = nt(dz, ob[...])
    copies[0].wait()
    d_o = nt(dz, wo[...]) + nn(dto.astype(BF16), oa[...])
    dot_s[...] = d_o.T.astype(BF16)
    kept = [jnp.concatenate([visible(c * rows, chunk * rows, rows, length)] * group, axis=1) for c in range(chunk + 1)]

    def one_group(j, carry):
        places = [head_rows(j * group + g) for g in range(group)]
        q_g = jnp.concatenate([qt[at, :] for at in places], axis=1)
        do_g = jnp.concatenate([dot_s[at, :] for at in places], axis=1)
        o_g = jnp.concatenate([ot[at, :] for at in places], axis=1)
        low = jnp.concatenate([lse[pl.ds(j * group + g, 1), :] for g in range(group)], axis=1)
        dots = jnp.sum(do_g.astype(F32) * o_g.astype(F32), axis=0, keepdims=True)
        dq_g = 0.0
        for c in range(chunk + 1):
            prob = jnp.where(kept[c], jnp.exp(nn(keys[c][j], q_g) - low), 0.0)
            ds = (prob * (nn(values[c][j], do_g) - dots)).astype(BF16)
            dq_g = dq_g + nn(keys_t[c][head_rows(j), :], ds)
            dk, dv = nt(q_g, ds), nt(do_g, prob.astype(BF16))
            if last:
                dk, dv = dk + rest[2][head_rows(j), :], dv + rest[3][head_rows(j), :]
            dkt_s[c, head_rows(j), :], dvt_s[c, head_rows(j), :] = dk, dv
        for g in range(group):
            dqt_s[places[g], :] = dq_g[:, g * rows:(g + 1) * rows]
        return carry

    lax.fori_loop(0, kv_heads, one_group, 0)
    if not last:
        outs[6][...], outs[7][...] = dkt_s[0], dvt_s[0]
    cos, sin = cos_t[...], sin_t[...]
    dto_t, o_t = dto.T.astype(BF16), ot[...]
    d_out_a = nt(dto_t, o_t)
    turn_back(dqt_s[...], cos * (HEAD ** -0.5), sin * (HEAD ** -0.5), dot_s)
    dq_s[:, :q_cols] = dot_s[...].T
    turn_back(dkt_s[chunk], cos, sin, dot_s)
    dq_s[:, q_cols:q_cols + kv_cols] = dot_s[:kv_cols, :].T
    dq_s[:, q_cols + kv_cols:] = dvt_s[chunk].T.astype(BF16)
    dq, dk, dv = dq_s[:, :q_cols], dq_s[:, q_cols:q_cols + kv_cols], dq_s[:, q_cols + kv_cols:]
    dt1 = jnp.concatenate([nt(dq, qb[...]), nt(dk, kvb[0]), nt(dv, kvb[1])], axis=1)
    dt1b = dt1.astype(BF16)
    kv_pad = jnp.zeros((RANK, QUARTER - 2 * kv_cols), F32)
    d_kv = jnp.concatenate([nn(t1t[RANK:2 * RANK, :], dk), nn(t1t[2 * RANK:, :], dv), kv_pad], axis=1)
    for k, value in enumerate((nn(t1t[:RANK, :], dq), d_out_a, d_kv)):
        at = slice(k * RANK, (k + 1) * RANK)
        if last:
            value = value + rest[0][at, :]
        b_out[at, :] = value.astype(b_out.dtype)
    dt1t = dt1.T.astype(BF16)
    copies[1].wait()
    copies[2].wait()

    def block(r, inner):
        at = quarter(me, r)
        d = nt(dq_s[:, :q_cols], wq[at, :]) + nn(dt1b, a1[:, at])
        d = d + nt(dq_s[:, q_cols:q_cols + kv_cols], wkv[0, at, :]) + nt(dq_s[:, q_cols + kv_cols:], wkv[1, at, :])
        value_s[...] = d
        store_block(r, value_s, slice(0, rows), h_keep, h_send)
        low_s[:3 * RANK, :] = nn(dt1t, h_in[:, at])
        low_s[3 * RANK:, :] = nn(tot[...], z_s[:, at])
        if last:
            low_s[...] += rest[1][:, at]
            store_block(r, low_s, slice(0, 4 * RANK), outs[5], outs[6])
        else:
            outs[5][:, at] = low_s[...]
        return inner + jnp.sum(d * h_in[:, at].astype(F32), axis=1, keepdims=True)

    inner = lax.fori_loop(0, PARTS, block, jnp.zeros((rows, 1), F32))
    inner = jnp.broadcast_to(inner, (rows, LANES)).T[:SPARE // 2, :]
    if last:
        for ref in outs[5:7]:
            for c, value in enumerate((inner, rest[4][...])):
                at = slice(4 * RANK + c * SPARE // 2, 4 * RANK + (c + 1) * SPARE // 2)
                ref[at, QUARTER:QUARTER + rows] = value.astype(ref.dtype)
                ref[at, QUARTER + rows:] = jnp.zeros((SPARE // 2, QUARTER - rows), ref.dtype)
                ref[at, :QUARTER] = jnp.zeros((SPARE // 2, QUARTER), ref.dtype)
    else:
        outs[8][...] = inner


def output_kernel(info, y_far, *refs):
    out = refs[-1]
    rows = out.shape[0] // CHUNKS
    for c in range(CHUNKS):
        xq, y_keep, y_got = refs[3 * c:3 * (c + 1)]
        at = slice(c * rows, (c + 1) * rows)
        valid = c * rows + lax.broadcasted_iota(jnp.int32, (rows, 1), 0) < info[1]
        y = xq[...] + y_keep[:, LO] + y_got[:, LO].astype(F32) + y_far[at, :].astype(F32)
        out[at, :] = jnp.where(valid, y, 0.0).astype(BF16)


def finish_kernel(gains, x_all, aa_high, aa_far, *refs):
    out = refs[-1]
    gain = gains[0, 0:1, :].astype(F32)
    rows = out.shape[0] // CHUNKS
    inner = aa_high[4 * RANK:, :].astype(F32) + aa_far[4 * RANK:, :].astype(F32)
    for c in range(CHUNKS):
        dx, keep, got, there, inv = refs[5 * c:5 * (c + 1)]
        x = chunk_of(x_all, c, rows)
        mine = inner[c * SPARE // 2:c * SPARE // 2 + 8, :rows].T[:, 0:1]
        inv = inv[...]
        grad = keep[:, LO] + got[:, LO].astype(F32) + there[...].astype(F32)
        grad = inv * (gain * grad) - x[...].astype(F32) * (inv * inv * mine / WIDTH)
        out[c * rows:(c + 1) * rows, :] = (dx[...] + grad).astype(BF16)


def high_sum_kernel(*refs):
    out = refs[-1]
    rows = out.shape[0] // (len(refs) // 2)
    for c in range(len(refs) // 2):
        keep, got = refs[2 * c:2 * c + 2]
        out[c * rows:(c + 1) * rows, :] = (keep[:, HI] + got[:, HI].astype(F32)).astype(BF16)


def high_sum(*pairs):
    args = [v for pair in pairs for v in pair]
    rows = sum(keep.shape[0] for keep, _ in pairs)
    return call(high_sum_kernel, None, (), args, [((rows, QUARTER), BF16)], [], "high_sum", 8)[0]


def split_refs(refs, counts):
    groups = []
    for count in counts:
        groups.append(refs[:count])
        refs = refs[count:]
    return groups, refs


def with_entry(parts, at, use):
    start = 0
    for ref in parts:
        @pl.when((at >= start) & (at < start + ref.shape[0]))
        def _(ref=ref, start=start):
            use(ref, at - start)
        start += ref.shape[0]


def sum_slots(info, owners, out_refs, one_slot):
    count = out_refs[0].shape[0]
    base = pl.program_id(0) * count
    slots = owners.shape[0]
    for ref in out_refs:
        ref[...] = jnp.zeros_like(ref)

    def add(slot, carry):
        owner = owners[slot] - base

        @pl.when((owner >= 0) & (owner < count))
        def _():
            one_slot(owner, entry_of(slot, info[3], slots))
        return carry

    lax.fori_loop(0, slots, add, 0)


def feedforward_sum_kernel(counts, info, owners, *refs):
    (b_parts, *a_parts), outs = split_refs(refs, counts)
    ga, gdb, gb, gda = outs
    me = info[0]

    def one_slot(owner, at):
        def add_b(ref, e):
            for i in range(gda.shape[2] // QUARTER):
                cols = slice(i * QUARTER, (i + 1) * QUARTER)
                base = i * 3 * RANK
                gb[owner, 0, :, cols] += ref[e, base:base + RANK, :].astype(F32)
                gb[owner, 1, :, cols] += ref[e, base + RANK:base + 2 * RANK, :].astype(F32)
                gda[owner, :, cols] += ref[e, base + 2 * RANK:base + 3 * RANK, :].astype(F32)

        with_entry(b_parts, at, add_b)
        for near_bit, parts in enumerate(a_parts):
            def add_a(ref, e, near_bit=near_bit):
                for r, cols in ((near_bit, LO), (near_bit ^ 2, HI)):
                    ga[owner, :, quarter(me, r)] += ref[e, :2 * RANK, cols].astype(F32)
                    gdb[owner, :, quarter(me, r)] += ref[e, 2 * RANK:, cols].astype(F32)

            with_entry(parts, at, add_a)

    sum_slots(info, owners, outs, one_slot)


def attention_sum_kernel(counts, info, owners, *refs):
    (b_parts, *a_parts), outs = split_refs(refs, counts)
    ga, gob, gq, gkv, goa = outs
    me = info[0]
    kv_cols = gkv.shape[3]

    def one_slot(owner, at):
        def add_b(ref, e):
            gq[owner] += ref[e, :RANK, :].astype(F32)
            goa[owner] += ref[e, RANK:2 * RANK, :].astype(F32)
            gkv[owner, 0] += ref[e, 2 * RANK:3 * RANK, :kv_cols].astype(F32)
            gkv[owner, 1] += ref[e, 2 * RANK:3 * RANK, kv_cols:2 * kv_cols].astype(F32)

        with_entry(b_parts, at, add_b)
        for r, parts in enumerate(a_parts):
            def add_a(ref, e, r=r):
                ga[owner, :, quarter(me, r)] += ref[e, :3 * RANK, :].astype(F32)
                gob[owner, :, quarter(me, r)] += ref[e, 3 * RANK:, :].astype(F32)

            with_entry(parts, at, add_a)

    sum_slots(info, owners, outs, one_slot)


def deal_kernel(slots, source, out, sems):
    made = [pltpu.make_async_copy(source.at[i], out.at[slots[i]], sems.at[i]) for i in range(source.shape[0])]
    for copy in made:
        copy.start()
    for copy in made:
        copy.wait()


def collect_kernel(slots, source, out, sems):
    made = [pltpu.make_async_copy(source.at[slots[i]], out.at[i], sems.at[i]) for i in range(source.shape[0])]
    for copy in made:
        copy.start()
    for copy in made:
        copy.wait()


def adapter_kernel(count, info, *refs):
    made = [pltpu.make_async_copy(refs[i].at[info[2]], refs[count + i], refs[-1].at[i]) for i in range(count)]
    for copy in made:
        copy.start()
    for copy in made:
        copy.wait()


def load_adapters(arrays, info):
    count = len(arrays)
    return pl.pallas_call(
        functools.partial(adapter_kernel, count),
        in_specs=[pl.BlockSpec(memory_space=pltpu.SMEM)] + [pl.BlockSpec(memory_space=pltpu.HBM)] * count,
        out_specs=[pl.BlockSpec(memory_space=pltpu.VMEM)] * count,
        out_shape=[pltpu.VMEM(a.shape[1:], a.dtype) for a in arrays],
        scratch_shapes=[pltpu.SemaphoreType.DMA((count,))],
        compiler_params=pltpu.CompilerParams(vmem_limit_bytes=MIB),
        cost_estimate=pl.CostEstimate(flops=1000, transcendentals=0, bytes_accessed=1000),
        name="adapters",
    )(info, *(in_hbm(a) for a in arrays))


def move_rows(kernel, value, slots, name, outs, in_space, out_space, sems):
    return pl.pallas_call(
        kernel,
        in_specs=[pl.BlockSpec(memory_space=pltpu.SMEM), pl.BlockSpec(memory_space=in_space)],
        out_specs=[pl.BlockSpec(memory_space=out_space)] * len(outs),
        out_shape=outs,
        scratch_shapes=[pltpu.SemaphoreType.DMA(sems)],
        compiler_params=pltpu.CompilerParams(vmem_limit_bytes=MIB),
        cost_estimate=pl.CostEstimate(flops=1000, transcendentals=0, bytes_accessed=1000),
        name=name,
    )(slots, pltpu.with_memory_space_constraint(value, in_space))


def sds(shape, dtype):
    return jax.ShapeDtypeStruct(tuple(shape), dtype)


def in_vmem(value):
    return pltpu.with_memory_space_constraint(value, pltpu.VMEM)


def in_hbm(value):
    return pltpu.with_memory_space_constraint(value, pltpu.HBM)


def call(kernel, info, weights, args, outs, scratch, name, mib, after=(), sems=()):
    vmem = pl.BlockSpec(memory_space=pltpu.VMEM)
    scalars = () if info is None else (info,)
    n, w = len(scalars), len(weights)

    def body(*refs):
        at = n + w + len(args)
        kernel(*refs[:at], *refs[at + len(after):])

    return pl.pallas_call(
        body,
        in_specs=[pl.BlockSpec(memory_space=pltpu.SMEM)] * n + [pl.BlockSpec(memory_space=pltpu.HBM)] * w + [vmem] * len(args)
        + [pl.BlockSpec(memory_space=pl.ANY)] * len(after),
        out_specs=[vmem] * len(outs),
        out_shape=[pltpu.VMEM(tuple(s), d) for s, d in outs],
        scratch_shapes=[pltpu.VMEM(s, d) for s, d in scratch] + ([pltpu.SemaphoreType.DMA(sems)] if sems else []),
        compiler_params=pltpu.CompilerParams(vmem_limit_bytes=mib * MIB),
        cost_estimate=pl.CostEstimate(flops=1000, transcendentals=0, bytes_accessed=1000),
        name=name,
    )(*scalars, *(in_hbm(a) for a in weights), *(in_vmem(a) for a in args), *after)


def whole_spec(value):
    zeros = (0,) * value.ndim
    return pl.BlockSpec(value.shape, lambda i, *_: zeros)


def sum_call(kernel, scalars, groups, outs, name):
    args = [v for group in groups for v in group]
    steps = 2
    specs = [pl.BlockSpec((o.shape[0] // steps,) + o.shape[1:], (lambda n: lambda i, *_: (i,) + (0,) * n)(o.ndim - 1))
             for o in outs]
    return pl.pallas_call(
        functools.partial(kernel, [len(group) for group in groups]),
        grid_spec=pltpu.PrefetchScalarGridSpec(
            num_scalar_prefetch=len(scalars), grid=(steps,),
            in_specs=[whole_spec(a) for a in args], out_specs=specs),
        out_shape=outs,
        compiler_params=pltpu.CompilerParams(
            dimension_semantics=("arbitrary",),
            vmem_limit_bytes=4 * MIB + 2 * sum(a.size * a.dtype.itemsize for a in args)
            + sum(o.size * o.dtype.itemsize for o in outs)),
        cost_estimate=pl.CostEstimate(flops=0, transcendentals=0, bytes_accessed=12000000),
        name=name,
    )(*scalars, *args)


def swap(value, bit, axis, size):
    return lax.ppermute(value, axis, [(i, i ^ bit) for i in range(size)])


def near(value):
    return swap(value, 1, "mp", PARTS)


def far(value):
    return swap(value, 2, "mp", PARTS)


def spread(value):
    there = far(value)
    return (value, near(value), there, near(there))


def far_sum_kernel(own, got, out):
    for to, other in ((LO, HI), (HI, LO)):
        out[:, to] = (own[:, to].astype(F32) + got[:, other].astype(F32)).astype(BF16)


def far_sum(own, got):
    return call(far_sum_kernel, None, (), (own, got), [(own.shape, BF16)], [], "far_sum", 6)[0]


def pair_sum_kernel(keep, got, out):
    out[...] = (keep[...] + got[...].astype(F32)).astype(BF16)


def pair_sum(keep, send):
    return call(pair_sum_kernel, None, (), (keep, near(send)), [(send.shape, BF16)], [], "pair_sum", 6)[0]


def late(value, *others):
    return lax.optimization_barrier((value, *others))[0]


def doubled(stack, bit, size):
    return jnp.concatenate([stack, swap(stack, bit, "dp", size)], axis=0)


def entry_of(slot, place, size):
    bits = size.bit_length() - 1
    apart = slot ^ place
    return sum(((apart >> b) & 1) << (bits - 1 - b) for b in range(bits))


def shards(dp, residual, attention_gain, query_matrix, key_value_matrix, output_matrix, feedfwd_gain,
           gate_up_matrix, down_matrix, attention_adapter_input, query_adapter_output,
           key_value_adapter_output, output_adapter_input, output_adapter_output, feedfwd_adapter_input,
           feedfwd_adapter_output, down_adapter_input, down_adapter_output, lengths, adapter_index,
           dealing_slots, cotangent):
    seqs = residual.shape[0]
    length = cotangent.shape[1]
    units = down_matrix.shape[0]
    adapters = attention_adapter_input.shape[0]
    q_cols = query_matrix.shape[1]
    kv_cols = key_value_matrix.shape[2]
    kv_heads = kv_cols // HEAD
    heads = q_cols // HEAD
    rows = length // CHUNKS
    half = 2 * QUARTER
    me = lax.axis_index("mp")
    place = lax.axis_index("dp")

    is_there = dealing_slots[None, :] == jnp.arange(seqs, dtype=jnp.int32)[:, None]
    owners = jnp.sum(jnp.where(is_there, adapter_index[None, :], 0), axis=1)
    spans = jnp.sum(jnp.where(is_there, lengths[None, :], 0), axis=1)
    mine = jnp.arange(seqs, dtype=jnp.int32) == place
    my_length = jnp.sum(jnp.where(mine, spans, 0))
    my_adapter = jnp.sum(jnp.where(mine, owners, 0))
    info = jnp.stack([me.astype(jnp.int32), my_length, my_adapter, place.astype(jnp.int32)])

    gs = spread(cotangent[0])
    gains = jnp.stack(spread(jnp.stack([attention_gain, feedfwd_gain])))
    ordered, = move_rows(deal_kernel, residual, dealing_slots, "deal", [pltpu.VMEM(residual.shape, BF16)], pltpu.HBM,
                         pltpu.VMEM, (seqs,))
    dealt = lax.all_to_all(ordered, "dp", split_axis=0, concat_axis=1, tiled=True)[0]
    adapters_here = load_adapters(
        (attention_adapter_input, query_adapter_output, key_value_adapter_output, output_adapter_input,
         output_adapter_output, feedfwd_adapter_input, feedfwd_adapter_output, down_adapter_input,
         down_adapter_output), info)
    a1, qb, kvb, oa, ob, a2, fba, da, bd = adapters_here
    dealt = late(dealt, gs[2], a1, gains)
    beside = near(dealt)
    there = [far(dealt[c * rows:(c + 1) * rows]) for c in range(CHUNKS)]
    xs = [None] * CHUNKS
    cos_np, sin_np = rope_tables(length)
    cos = [jnp.asarray(cos_np[:, c * rows:(c + 1) * rows]) for c in range(CHUNKS)]
    sin = [jnp.asarray(sin_np[:, c * rows:(c + 1) * rows]) for c in range(CHUNKS)]
    wq, wkv, wo = query_matrix, key_value_matrix, output_matrix

    def like(*arrays):
        return [(a.shape, a.dtype) for a in arrays]

    wide, col, block, thin = (rows, WIDTH), (rows, half), (rows, QUARTER), (rows, 1)
    saved, kept, z_own, z_far = ([None] * CHUNKS for _ in range(4))
    order = ()
    for c in range(CHUNKS):
        xs[c] = (dealt, beside, there[c], near(late(there[c], saved[0][0]) if c else there[c]))
        outs = [((3 * RANK, rows), BF16), ((q_cols, rows), BF16), ((kv_heads, rows, HEAD), BF16),
                ((kv_heads, rows, HEAD), BF16), ((kv_cols, rows), BF16), ((kv_cols, rows), BF16)]
        saved[c] = call(
            functools.partial(project_kernel, c), info, (wq, wkv), (*xs[c], gains, a1, qb, kvb, cos[c], sin[c]), outs,
            [(wide, BF16)] + like(wq, wkv), "project_%d" % c, 12, order, (2,))
        outs = [(col, F32), (col, BF16), ((q_cols, rows), BF16), ((heads, rows), F32), ((RANK, rows), BF16)]
        pairs = [v for p in saved[:c + 1] for v in (p[2], p[5])]
        z_keep, z_send, *kept[c] = call(
            functools.partial(attend_kernel, c), info, (wo,), (saved[c][1], oa, ob, *pairs), outs, like(wo),
            "attend_%d" % c, 10, (saved[c][0],), (1,))
        z_own[c] = pair_sum(z_keep, late(z_send, z_far[0] if c else there[-1]))
        z_far[c] = far(z_own[c])
        order = (kept[c][1], z_own[c])
    def front(c, total, partial, order):
        hidden = (rows, units)
        outs = [(wide, BF16), (block, F32), (wide, BF16), (wide, BF16), (hidden, BF16), (hidden, BF16), (hidden, BF16),
                ((rows, 2 * RANK), BF16), ((rows, RANK), BF16),
                ((3 * RANK * units // QUARTER, QUARTER), BF16 if c else F32),
                (col, F32), (col, BF16), ((rows, RANK), F32)]
        args = (*xs[c], total, near(total), *gs, gains, a2, bd, fba, da, *partial)
        weights = () if c else (gate_up_matrix, down_matrix)
        outs += like(*weights)
        return call(
            functools.partial(front_kernel, c, c == CHUNKS - 1), info, weights, (wgu, wd, *args) if c else args, outs,
            [((ROW_BLOCK, WIDTH), F32), (block, F32)], "front_%d" % c, 8, order, () if c else (2, units // QUARTER))

    def back(c, hidden, partial, order):
        first = col if c else (rows + 3 * RANK, half)
        outs = [(first, F32), (first, BF16)]
        outs += [((3 * RANK, WIDTH), F32)] if c else []
        _, _, h2, g2, _, dg, du = hidden[:7]
        return call(
            functools.partial(back_kernel, c == 0), info, (), (wgu, h2, g2, hidden[12], dg, du, a2, fba, *partial), outs,
            [(block, F32), ((3 * RANK, QUARTER), F32)], "back_%d" % c, 8, order)

    def attend_back(c, total, partial, order):
        outs = [(block, F32), (col, F32), (col, BF16), (thin, F32), ((3 * RANK, QUARTER), F32 if c else BF16)]
        low = (4 * RANK + SPARE, half)
        outs += ([((4 * RANK, WIDTH), F32), ((kv_cols, rows), F32), ((kv_cols, rows), F32), ((SPARE // 2, rows), F32)]
                 if c else [(low, F32), (low, BF16)])
        scratch = [(wide, BF16), (wide, BF16), ((ROW_BLOCK, WIDTH), F32), ((q_cols, rows), BF16), ((q_cols, rows), F32),
                   ((c + 1, kv_cols, rows), F32), ((c + 1, kv_cols, rows), F32), ((rows, q_cols + 2 * kv_cols), BF16),
                   (block, F32), ((4 * RANK, QUARTER), F32)]
        triples = [v for p in saved[:c + 1] for v in (p[2], p[3], p[4])]
        return call(
            functools.partial(attend_back_kernel, c, c == 0), info, (wq, wkv, wo),
            (*xs[c], *gs, hidden[c][0], total, near(total), gains, a1, qb, kvb, oa, ob, cos[c], sin[c], *saved[c][:2],
             *kept[c], *triples, *partial), outs, scratch + like(wq, wkv, wo), "attend_back_%d" % c, 18, order, (3,))

    bits = [1 << b for b in reversed(range(dp.bit_length() - 1))]
    def to_bands(value):
        return lax.all_to_all(value.reshape(dp, length // dp, QUARTER), "dp", split_axis=0, concat_axis=0, tiled=True)

    def collect(value, name, *before):
        rows_out = sds((seqs, length // dp, QUARTER), BF16)
        return move_rows(collect_kernel, value, late(dealing_slots, *before), name, [rows_out], pltpu.VMEM, pl.ANY,
                         (seqs,))[0]

    hidden, d_own, d_far = ([None] * CHUNKS for _ in range(3))
    *hidden[0], wgu, wd = front(0, far_sum(z_own[0], z_far[0]), (), order)
    step = hidden[0][8]
    hidden[1] = front(1, far_sum(z_own[1], late(z_far[1], step)), hidden[0][9:10], (step,))
    y_keep, y_got = [h[10] for h in hidden], [near(h[11]) for h in hidden]
    y_high = high_sum(*zip(y_keep, y_got))
    y_far = far(y_high)
    fb = hidden[1][9][None]
    fb_first = swap(fb, bits[0], "dp", dp)
    d_keep, d_send, fa = back(1, hidden[1], (), (y_high,))
    ready = (fb_first, y_far)
    d_own[1] = pair_sum(d_keep, late(d_send, *ready))
    d_far[1] = far(d_own[1])
    fb = fb_more = jnp.concatenate([fb, fb_first], axis=0)
    for bit in bits[1:-1]:
        fb_more = doubled(fb_more, bit, dp)
    fb_more = fb_more[2:]
    fb_side = swap(fb, bits[-1], "dp", dp)
    d_keep, d_send = back(0, hidden[0], (fa,), (d_own[1],))
    total = far_sum(d_own[1], late(d_far[1], d_send))
    d_own[0] = pair_sum(d_keep, late(d_send, fb_more, fb_side))
    d_far[0] = far(d_own[0])
    fb_more_side = swap(fb_more, bits[-1], "dp", dp)
    parts = [v for c in range(CHUNKS) for v in (hidden[c][1], y_keep[c], y_got[c])]
    result, = call(output_kernel, info, (), (y_far, *parts), [((length, QUARTER), BF16)], [], "output", 8, (d_own[0],))
    dxq, h_keep, h_send, inv, *sums = attend_back(1, total, (), (d_own[0],))
    total = far_sum(d_own[0], late(d_far[0], inv))
    h_got = near(late(h_send, fb_more_side))
    h_high = high_sum((h_keep, h_got))
    h_far = far(h_high)
    final = [None, (dxq, h_keep, h_got, h_far, inv)]
    fa = total[rows:][None]
    fa_first = swap(fa, bits[0], "dp", dp)
    dxq, h_keep, h_send, inv, att_b, aa_keep, aa_send = attend_back(0, total, sums, (h_high,))
    ready = (fa_first, h_far)
    aa_got = near(late(aa_send, *ready))
    aa_high = high_sum((aa_keep, aa_got))
    aa_far = far(aa_high)
    h_got = near(late(h_send, *ready))
    h_high = high_sum((h_keep, h_got))
    h_far = far(h_high)
    final[0] = (dxq, h_keep, h_got, h_far, inv)
    att_a = aa_keep[:4 * RANK, :QUARTER] + aa_got[:4 * RANK, :QUARTER].astype(F32)
    att_a = (att_a + late(aa_far, h_high)[:4 * RANK].astype(F32)).astype(BF16)
    n_b = att_b.shape[0]
    att = jnp.concatenate([att_b, att_a], axis=0)[None]
    att = doubled(att, bits[0], dp)
    att = late(att, h_far)
    for bit in bits[1:-1]:
        att = doubled(att, bit, dp)
    fa = late(jnp.concatenate([fa, fa_first], axis=0), aa_high)
    for bit in bits[1:-1]:
        fa = doubled(fa, bit, dp)
    fa_side = swap(fa, bits[-1], "dp", dp)

    dinput, = call(finish_kernel, None, (), (gains, dealt, aa_high, aa_far, *(v for f in final for v in f)),
                   [((length, QUARTER), BF16)], [], "finish", 8, (att, fa_side))
    input_grad = collect(to_bands(dinput), "collect_grad")
    output = collect(to_bands(late(result, dinput)), "collect_out", input_grad)

    outs = [sds((adapters, 2 * RANK, WIDTH), F32), sds((adapters, RANK, WIDTH), F32),
            sds((adapters, 2, RANK, units), F32), sds((adapters, RANK, units), F32)]
    ga_ffn, g_down_b, g_ffn_b, g_down_a = sum_call(
        feedforward_sum_kernel, (info, owners),
        ((fb, fb_more, fb_side, fb_more_side), (fa, fa_side), (near(fa), near(fa_side))), outs, "feedforward_sum")

    att_side = swap(att, bits[-1], "dp", dp)
    att_side = late(att_side, g_down_a)
    a_parts = [att[:, n_b:], att_side[:, n_b:]]
    a_far = [far(v) for v in a_parts]
    outs = [sds((adapters, 3 * RANK, WIDTH), F32), sds((adapters, RANK, WIDTH), F32),
            sds((adapters, RANK, q_cols), F32), sds((adapters, 2, RANK, kv_cols), F32),
            sds((adapters, RANK, q_cols), F32)]
    ga_att, g_out_b, g_query_b, g_kv_b, g_out_a = sum_call(
        attention_sum_kernel, (info, owners),
        ((att, att_side), a_parts, [near(v) for v in a_parts], a_far, [near(v) for v in a_far]), outs, "attention_sum")
    return (output, input_grad, ga_att, g_query_b, g_kv_b, g_out_a, g_out_b, ga_ffn, g_ffn_b, g_down_a, g_down_b)


def solution(mesh):
    in_specs = (
        P(None, "dp", "mp"), P("mp"), P(None, "mp"), P(None, None, "mp"), P("mp", None), P("mp"),
        P(None, None, "mp"), P("mp", None), P(), P(None, None, "mp"), P(None, None, None, "mp"),
        P(None, None, "mp"), P(), P(), P(None, None, None, "mp"), P(None, None, "mp"), P(), P(), P(), P(),
        P("dp", None, "mp"),
    )
    out_specs = (
        P(None, "dp", "mp"), P(None, "dp", "mp"), P(), P(None, None, "mp"), P(None, None, None, "mp"),
        P(None, None, "mp"), P(), P(), P(None, None, None, "mp"), P(None, None, "mp"), P(),
    )
    return jax.shard_map(
        functools.partial(shards, mesh.shape["dp"]), mesh=mesh, in_specs=in_specs, out_specs=out_specs,
        check_vma=False)
```

```python
import functools

import jax
import jax.numpy as jnp
import numpy as np
from jax import lax
from jax.experimental import pallas as pl
from jax.experimental.pallas import tpu as pltpu
from jax.sharding import PartitionSpec as P

WIDTH = 2048
HEAD = 64
HALF = HEAD // 2
RANK = 16
EPS = 1e-05
ROPE_BASE = 500000.0
NEG_FILL = -1e30
PARTS = 4
LANES = 128
SPARE = 32
ROW_BLOCK = 64
QUARTER = WIDTH // PARTS
CHUNKS = 2
MIB = 1024 * 1024
F32 = jnp.float32
BF16 = jnp.bfloat16


def nn(a, b):
    return lax.dot_general(a, b, (((1,), (0,)), ((), ())), preferred_element_type=F32)


def nt(a, b):
    return lax.dot_general(a, b, (((1,), (1,)), ((), ())), preferred_element_type=F32)


def rope_tables(length):
    freq = ROPE_BASE ** (-np.arange(HALF, dtype=np.float32) * np.float32(2.0 / HEAD))
    angles = (np.arange(length, dtype=np.float32)[None, :] * freq.astype(np.float32)[:, None]).astype(np.float32)
    return np.cos(angles).astype(np.float32), np.sin(angles).astype(np.float32)


def quarter(me, rel):
    return pl.ds(pl.multiple_of((me ^ rel) * QUARTER, QUARTER), QUARTER)


LO, HI = slice(0, QUARTER), slice(QUARTER, 2 * QUARTER)


def total_block(rel, rows_at, own, oth):
    return (own if rel in (0, 2) else oth)[rows_at, LO if rel in (0, 1) else HI].astype(F32)


def store_block(rel, value, rows_at, keep_ref, send_ref):
    to = pl.ds(pl.multiple_of((rel // 2) * QUARTER, QUARTER), QUARTER)

    @pl.when(rel % 2 == 0)
    def _():
        keep_ref[rows_at, to] = value[...]

    @pl.when(rel % 2 == 1)
    def _():
        send_ref[rows_at, to] = value[...].astype(BF16)


def chunk_of(ref, chunk, rows):
    return ref if ref.shape[0] == rows else ref.at[chunk * rows:(chunk + 1) * rows]


def row_block(i):
    return pl.ds(pl.multiple_of(i * ROW_BLOCK, ROW_BLOCK), ROW_BLOCK)


def is_valid(chunk, i, rows, length):
    return chunk * rows + i * ROW_BLOCK + lax.broadcasted_iota(jnp.int32, (ROW_BLOCK, 1), 0) < length


def copies_of(pairs, sems):
    made = [pltpu.make_async_copy(source, target, sems.at[i]) for i, (source, target) in enumerate(pairs)]
    for copy in made:
        copy.start()
    return made


def put_block(rel, value, keep_ref, send_ref):
    ref = keep_ref if rel in (0, 2) else send_ref
    ref[:, LO if rel in (0, 1) else HI] = value.astype(ref.dtype)


def rotate(value, cos, sin, out_ref):
    for i in range(value.shape[0] // HEAD):
        u1, u2 = value[i * HEAD:i * HEAD + HALF], value[i * HEAD + HALF:(i + 1) * HEAD]
        out_ref[i * HEAD:i * HEAD + HALF, :] = (u1 * cos - u2 * sin).astype(BF16)
        out_ref[i * HEAD + HALF:(i + 1) * HEAD, :] = (u2 * cos + u1 * sin).astype(BF16)


def turn_back(value, cos, sin, out_ref):
    for i in range(value.shape[0] // HEAD):
        w1, w2 = value[i * HEAD:i * HEAD + HALF], value[i * HEAD + HALF:(i + 1) * HEAD]
        out_ref[i * HEAD:i * HEAD + HALF, :] = (w1 * cos + w2 * sin).astype(BF16)
        out_ref[i * HEAD + HALF:(i + 1) * HEAD, :] = (w2 * cos - w1 * sin).astype(BF16)


def head_rows(i):
    return pl.ds(pl.multiple_of(i * HEAD, HEAD), HEAD)


def visible(key_start, query_start, rows, length):
    kpos = key_start + lax.broadcasted_iota(jnp.int32, (rows, rows), 0)
    qpos = query_start + lax.broadcasted_iota(jnp.int32, (rows, rows), 1)
    return (kpos <= qpos) & (kpos < length)


def project_kernel(chunk, info, wq_h, wkv_h, x0, x1, x2, x3, gains, a1, qb, kvb, cos_t, sin_t,
                   t1t_out, qt_out, kn_out, vn_out, kt_out, vt_out, h_out, wq, wkv, sems):
    copies = copies_of(((wkv_h, wkv), (wq_h, wq)), sems)
    me = info[0]
    rows = h_out.shape[0]
    kv_heads = kn_out.shape[0]
    xs = [chunk_of(x, chunk, rows) for x in (x0, x1, x2, x3)]

    def norm(i, carry):
        at = row_block(i)
        square = jnp.zeros((ROW_BLOCK, 1), F32)
        for r in range(PARTS):
            v = xs[r][at, :].astype(F32)
            square = square + jnp.sum(v * v, axis=1, keepdims=True)
        inv = lax.rsqrt(square / WIDTH + EPS)
        for r in range(PARTS):
            v = xs[r][at, :].astype(F32)
            h_out[at, quarter(me, r)] = (v * inv * gains[r, 0:1, :].astype(F32)).astype(BF16)
        return carry

    lax.fori_loop(0, rows // ROW_BLOCK, norm, 0)
    h = h_out[...]
    t1 = nt(h, a1[...])
    t1t_out[...] = t1.T.astype(BF16)
    t1b = t1.astype(BF16)
    cos, sin = cos_t[...], sin_t[...]
    copies[0].wait()
    k = nn(h, wkv[0]) + nn(t1b[:, RANK:2 * RANK], kvb[0])
    rotate(k.T, cos, sin, kt_out)
    k_n = kt_out[...].T
    v_n = (nn(h, wkv[1]) + nn(t1b[:, 2 * RANK:], kvb[1])).astype(BF16)
    vt_out[...] = v_n.T
    for i in range(kv_heads):
        kn_out[i] = k_n[:, i * HEAD:(i + 1) * HEAD]
        vn_out[i] = v_n[:, i * HEAD:(i + 1) * HEAD]
    copies[1].wait()
    q = nn(h, wq[...]) + nn(t1b[:, :RANK], qb[...])
    rotate(q.T * (HEAD ** -0.5), cos, sin, qt_out)


def attend_kernel(chunk, info, wo_h, qt, oa, ob, *rest):
    pairs, rest = rest[:2 * (chunk + 1)], rest[2 * (chunk + 1):]
    z_keep, z_send, ot_out, lse_out, tot_out, wo, sems = rest
    copies = copies_of(((wo_h, wo),), sems)
    keys, values = pairs[0::2], pairs[1::2]
    me, length = info[0], info[1]
    rows = qt.shape[1]
    kv_heads = keys[0].shape[0]
    heads = qt.shape[0] // HEAD
    group = heads // kv_heads

    kept = [jnp.concatenate([visible(c * rows, chunk * rows, rows, length)] * group, axis=1) for c in range(chunk + 1)]

    def one_group(j, carry):
        q_g = jnp.concatenate([qt[head_rows(j * group + g), :] for g in range(group)], axis=1)
        parts = [jnp.where(kept[c], nn(keys[c][j], q_g), NEG_FILL) for c in range(chunk + 1)]
        top = functools.reduce(jnp.maximum, [jnp.max(s, axis=0, keepdims=True) for s in parts])
        es = [jnp.exp(s - top) for s in parts]
        total = sum(jnp.sum(e, axis=0, keepdims=True) for e in es)
        low = top + jnp.log(total)
        o_t = sum(nn(value[head_rows(j), :], e.astype(BF16)) for value, e in zip(values, es))
        o_t = (o_t / total).astype(BF16)
        for g in range(group):
            cols = slice(g * rows, (g + 1) * rows)
            lse_out[pl.ds(j * group + g, 1), :] = low[:, cols]
            ot_out[head_rows(j * group + g), :] = o_t[:, cols]
        return carry

    lax.fori_loop(0, kv_heads, one_group, 0)
    o = ot_out[...].T
    to = nt(o, oa[...])
    tot_out[...] = to.T.astype(BF16)
    to = to.astype(BF16)
    copies[0].wait()
    for r in range(PARTS):
        at = quarter(me, r)
        put_block(r, nn(o, wo[:, at]) + nn(to, ob[:, at]), z_keep, z_send)


def front_kernel(chunk, last, info, wgu_in, wd_in, x0, x1, x2, x3, zo, zp, g0, g1, g2, g3, gains, a2, bd, fb, da,
                 *rest):
    units = wd_in.shape[0]
    if chunk:
        wgu, wd = wgu_in, wd_in
    else:
        (wgu, wd, f_s, sems), rest = rest[-4:], rest[:-4]
        rest = (*rest, f_s)

    def copies(i):
        c = pl.ds(pl.multiple_of(i * QUARTER, QUARTER), QUARTER)
        return (pltpu.make_async_copy(wgu_in.at[:, :, c], wgu.at[:, :, c], sems.at[0, i]),
                pltpu.make_async_copy(wd_in.at[c, :], wd.at[c, :], sems.at[1, i]))

    if not chunk:
        for i in range(units // QUARTER):
            for copy in copies(i):
                copy.start()
    f_s = rest[-1]
    xm_out, xq_out, h_out, g_out, act_out, dg_out, du_out, t2_s, dtd_s, b_out = rest[-11:-1]
    me, length = info[0], info[1]
    rows = h_out.shape[0]
    xs, gs = ([chunk_of(v, chunk, rows) for v in vs] for vs in ((x0, x1, x2, x3), (g0, g1, g2, g3)))

    def norm(i, carry):
        at = row_block(i)
        valid = is_valid(chunk, i, rows, length)
        square = jnp.zeros((ROW_BLOCK, 1), F32)
        for r in range(PARTS):
            v = xs[r][at, :].astype(F32) + total_block(r, at, zo, zp)
            if r == 0:
                xq_out[at, :] = v
            f_s[:, quarter(me, r)] = v
            square = square + jnp.sum(v * v, axis=1, keepdims=True)
            g_out[at, quarter(me, r)] = jnp.where(valid, gs[r][at, :], jnp.zeros((), BF16))
        inv = lax.rsqrt(square / WIDTH + EPS)
        for r in range(PARTS):
            v = f_s[:, quarter(me, r)]
            xm_out[at, quarter(me, r)] = v.astype(BF16)
            h_out[at, quarter(me, r)] = (v * inv * gains[r, 1:2, :].astype(F32)).astype(BF16)
        return carry

    lax.fori_loop(0, rows // ROW_BLOCK, norm, 0)
    t2 = nt(h_out[...], a2[...])
    t2_s[...] = t2.astype(BF16)
    dtd = nt(g_out[...], bd[...])
    dtd_s[...] = dtd.astype(BF16)
    t2t, dtdt = t2.T.astype(BF16), dtd.T.astype(BF16)

    def block(i, carry):
        c = pl.ds(pl.multiple_of(i * QUARTER, QUARTER), QUARTER)
        if not chunk:
            for copy in copies(i):
                copy.wait()
        h, g = h_out[...], g_out[...]
        gate = nn(h, wgu[0, :, c]) + nn(t2_s[:, :RANK], fb[0, :, c])
        up = nn(h, wgu[1, :, c]) + nn(t2_s[:, RANK:], fb[1, :, c])
        dact = nt(g, wd[c, :]) + nn(dtd_s[...], da[:, c])
        sig = 1.0 / (1.0 + jnp.exp(-gate))
        silu = gate * sig
        act = (silu * up).astype(BF16)
        dgate = (dact * up * sig * (1.0 + gate * (1.0 - sig))).astype(BF16)
        dup = (dact * silu).astype(BF16)
        act_out[:, c], dg_out[:, c], du_out[:, c] = act, dgate, dup
        for k, value in enumerate((nn(t2t[:RANK], dgate), nn(t2t[RANK:], dup), nn(dtdt, act))):
            at = pl.ds(pl.multiple_of((3 * i + k) * RANK, RANK), RANK)
            if last:
                value = value + rest[0][at, :]
            b_out[at, :] = value.astype(b_out.dtype)
        return carry

    lax.fori_loop(0, units // QUARTER, block, 0)


def back_kernel(last, info, wgu, h, g, act, dg, du, a2, fb, da, *rest):
    (value_s, low_s), rest = rest[-2:], rest[:-2]
    outs, rest = (rest[-3:], rest[:-3]) if last else (rest[-4:], rest[:-4])
    td_out, d_keep, d_send = outs[:3]
    me = info[0]
    rows = h.shape[0]
    dt2 = jnp.concatenate([nt(dg[...], fb[0]), nt(du[...], fb[1])], axis=1)
    td = nt(act[...], da[...])
    td_out[...] = td
    dt2b = dt2.astype(BF16)
    dt2t, tdt = dt2.T.astype(BF16), td.T.astype(BF16)

    def block(r, carry):
        at = quarter(me, r)
        value_s[...] = nt(dg[...], wgu[0, at, :]) + nt(du[...], wgu[1, at, :]) + nn(dt2b, a2[:, at])
        store_block(r, value_s, slice(0, rows), d_keep, d_send)
        low_s[:2 * RANK, :] = nn(dt2t, h[:, at])
        low_s[2 * RANK:, :] = nn(tdt, g[:, at])
        if last:
            low_s[...] += rest[0][:, at]
            store_block(r, low_s, slice(rows, rows + 3 * RANK), d_keep, d_send)
        else:
            outs[3][:, at] = low_s[...]
        return carry

    lax.fori_loop(0, PARTS, block, 0)


def down_kernel(info, wd, act, td, bd, xq, y_keep, y_send, value_s):
    me = info[0]
    tdb = td[...].astype(BF16)

    def block(r, carry):
        at = quarter(me, r)
        value_s[...] = nn(act[...], wd[:, at]) + nn(tdb, bd[:, at])
        store_block(r, value_s, slice(0, act.shape[0]), y_keep, y_send)
        return carry

    lax.fori_loop(0, PARTS, block, 0)
    y_keep[:, LO] += xq[...]


def attend_back_kernel(chunk, last, info, wq_h, wkv_h, wo_h, x0, x1, x2, x3, g0, g1, g2, g3, xm, do_, dp, gains, a1,
                       qb, kvb, oa, ob, cos_t, sin_t, t1t, qt, ot, lse, tot, *rest):
    scratch, rest = rest[-14:], rest[:-14]
    h_in, z_s, f_s, dot_s, dqt_s, dkt_s, dvt_s, dq_s, value_s, low_s, wq, wkv, wo, sems = scratch
    copies = copies_of(((wo_h, wo), (wq_h, wq), (wkv_h, wkv)), sems)
    n_out = 7 if last else 9
    outs, rest = rest[-n_out:], rest[:-n_out]
    dxq_out, h_keep, h_send, inv_out, b_out = outs[:5]
    triples, rest = rest[:3 * (chunk + 1)], rest[3 * (chunk + 1):]
    keys, values, keys_t = triples[0::3], triples[1::3], triples[2::3]
    me, length = info[0], info[1]
    rows = xm.shape[0]
    kv_heads = keys[0].shape[0]
    heads = qt.shape[0] // HEAD
    group = heads // kv_heads
    q_cols, kv_cols = heads * HEAD, kv_heads * HEAD
    xs, gs = ([chunk_of(v, chunk, rows) for v in vs] for vs in ((x0, x1, x2, x3), (g0, g1, g2, g3)))

    def norm_back(i, carry):
        at = row_block(i)
        valid = is_valid(chunk, i, rows, length)
        square, first, inner = (jnp.zeros((ROW_BLOCK, 1), F32) for _ in range(3))
        for r in range(PARTS):
            v = xm[at, quarter(me, r)].astype(F32)
            square = square + jnp.sum(v * v, axis=1, keepdims=True)
            w = total_block(r, at, do_, dp) * gains[r, 1:2, :].astype(F32)
            f_s[:, quarter(me, r)] = w
            inner = inner + jnp.sum(v * w, axis=1, keepdims=True)
            u = xs[r][at, :].astype(F32)
            first = first + jnp.sum(u * u, axis=1, keepdims=True)
        inv_one = lax.rsqrt(first / WIDTH + EPS)
        inv_out[at, :] = inv_one
        inv = lax.rsqrt(square / WIDTH + EPS)
        back = inv * inv * inv * inner / WIDTH
        for r in range(PARTS):
            v = xm[at, quarter(me, r)].astype(F32)
            g = jnp.where(valid, gs[r][at, :].astype(F32), 0.0)
            d = g + inv * f_s[:, quarter(me, r)] - v * back
            if r == 0:
                dxq_out[at, :] = d
            z_s[at, quarter(me, r)] = d.astype(BF16)
            u = xs[r][at, :].astype(F32)
            h_in[at, quarter(me, r)] = (u * inv_one * gains[r, 0:1, :].astype(F32)).astype(BF16)
        return carry

    lax.fori_loop(0, rows // ROW_BLOCK, norm_back, 0)
    dz = z_s[...]
    dto = nt(dz, ob[...])
    copies[0].wait()
    d_o = nt(dz, wo[...]) + nn(dto.astype(BF16), oa[...])
    dot_s[...] = d_o.T.astype(BF16)
    kept = [jnp.concatenate([visible(c * rows, chunk * rows, rows, length)] * group, axis=1) for c in range(chunk + 1)]

    def one_group(j, carry):
        places = [head_rows(j * group + g) for g in range(group)]
        q_g = jnp.concatenate([qt[at, :] for at in places], axis=1)
        do_g = jnp.concatenate([dot_s[at, :] for at in places], axis=1)
        o_g = jnp.concatenate([ot[at, :] for at in places], axis=1)
        low = jnp.concatenate([lse[pl.ds(j * group + g, 1), :] for g in range(group)], axis=1)
        dots = jnp.sum(do_g.astype(F32) * o_g.astype(F32), axis=0, keepdims=True)
        dq_g = 0.0
        for c in range(chunk + 1):
            prob = jnp.where(kept[c], jnp.exp(nn(keys[c][j], q_g) - low), 0.0)
            ds = (prob * (nn(values[c][j], do_g) - dots)).astype(BF16)
            dq_g = dq_g + nn(keys_t[c][head_rows(j), :], ds)
            dk, dv = nt(q_g, ds), nt(do_g, prob.astype(BF16))
            if last:
                dk, dv = dk + rest[2][head_rows(j), :], dv + rest[3][head_rows(j), :]
            dkt_s[c, head_rows(j), :], dvt_s[c, head_rows(j), :] = dk, dv
        for g in range(group):
            dqt_s[places[g], :] = dq_g[:, g * rows:(g + 1) * rows]
        return carry

    lax.fori_loop(0, kv_heads, one_group, 0)
    if not last:
        outs[6][...], outs[7][...] = dkt_s[0], dvt_s[0]
    cos, sin = cos_t[...], sin_t[...]
    dto_t, o_t = dto.T.astype(BF16), ot[...]
    d_out_a = nt(dto_t, o_t)
    turn_back(dqt_s[...], cos * (HEAD ** -0.5), sin * (HEAD ** -0.5), dot_s)
    dq_s[:, :q_cols] = dot_s[...].T
    turn_back(dkt_s[chunk], cos, sin, dot_s)
    dq_s[:, q_cols:q_cols + kv_cols] = dot_s[:kv_cols, :].T
    dq_s[:, q_cols + kv_cols:] = dvt_s[chunk].T.astype(BF16)
    dq, dk, dv = dq_s[:, :q_cols], dq_s[:, q_cols:q_cols + kv_cols], dq_s[:, q_cols + kv_cols:]
    dt1 = jnp.concatenate([nt(dq, qb[...]), nt(dk, kvb[0]), nt(dv, kvb[1])], axis=1)
    dt1b = dt1.astype(BF16)
    kv_pad = jnp.zeros((RANK, QUARTER - 2 * kv_cols), F32)
    d_kv = jnp.concatenate([nn(t1t[RANK:2 * RANK, :], dk), nn(t1t[2 * RANK:, :], dv), kv_pad], axis=1)
    for k, value in enumerate((nn(t1t[:RANK, :], dq), d_out_a, d_kv)):
        at = slice(k * RANK, (k + 1) * RANK)
        if last:
            value = value + rest[0][at, :]
        b_out[at, :] = value.astype(b_out.dtype)
    dt1t = dt1.T.astype(BF16)
    copies[1].wait()
    copies[2].wait()

    def block(r, inner):
        at = quarter(me, r)
        d = nt(dq_s[:, :q_cols], wq[at, :]) + nn(dt1b, a1[:, at])
        d = d + nt(dq_s[:, q_cols:q_cols + kv_cols], wkv[0, at, :]) + nt(dq_s[:, q_cols + kv_cols:], wkv[1, at, :])
        value_s[...] = d
        store_block(r, value_s, slice(0, rows), h_keep, h_send)
        low_s[:3 * RANK, :] = nn(dt1t, h_in[:, at])
        low_s[3 * RANK:, :] = nn(tot[...], z_s[:, at])
        if last:
            low_s[...] += rest[1][:, at]
            store_block(r, low_s, slice(0, 4 * RANK), outs[5], outs[6])
        else:
            outs[5][:, at] = low_s[...]
        return inner + jnp.sum(d * h_in[:, at].astype(F32), axis=1, keepdims=True)

    inner = lax.fori_loop(0, PARTS, block, jnp.zeros((rows, 1), F32))
    inner = jnp.broadcast_to(inner, (rows, LANES)).T[:SPARE // 2, :]
    if last:
        for ref in outs[5:7]:
            for c, value in enumerate((inner, rest[4][...])):
                at = slice(4 * RANK + c * SPARE // 2, 4 * RANK + (c + 1) * SPARE // 2)
                ref[at, QUARTER:QUARTER + rows] = value.astype(ref.dtype)
                ref[at, QUARTER + rows:] = jnp.zeros((SPARE // 2, QUARTER - rows), ref.dtype)
                ref[at, :QUARTER] = jnp.zeros((SPARE // 2, QUARTER), ref.dtype)
    else:
        outs[8][...] = inner


def output_kernel(info, y_far, *refs):
    out = refs[-1]
    rows = out.shape[0] // CHUNKS
    for c in range(CHUNKS):
        y_keep, y_got = refs[2 * c:2 * (c + 1)]
        at = slice(c * rows, (c + 1) * rows)
        valid = c * rows + lax.broadcasted_iota(jnp.int32, (rows, 1), 0) < info[1]
        y = y_keep[:, LO] + y_got[:, LO].astype(F32) + y_far[at, :].astype(F32)
        out[at, :] = jnp.where(valid, y, 0.0).astype(BF16)


def finish_kernel(gains, x_all, aa_high, aa_far, *refs):
    out = refs[-1]
    gain = gains[0, 0:1, :].astype(F32)
    rows = out.shape[0] // CHUNKS
    inner = aa_high[4 * RANK:, :].astype(F32) + aa_far[4 * RANK:, :].astype(F32)
    for c in range(CHUNKS):
        dx, keep, got, there, inv = refs[5 * c:5 * (c + 1)]
        x = chunk_of(x_all, c, rows)
        mine = inner[c * SPARE // 2:c * SPARE // 2 + 8, :rows].T[:, 0:1]
        inv = inv[...]
        grad = keep[:, LO] + got[:, LO].astype(F32) + there[...].astype(F32)
        grad = inv * (gain * grad) - x[...].astype(F32) * (inv * inv * mine / WIDTH)
        out[c * rows:(c + 1) * rows, :] = (dx[...] + grad).astype(BF16)


def high_sum_kernel(*refs):
    out = refs[-1]
    rows = out.shape[0] // (len(refs) // 2)
    for c in range(len(refs) // 2):
        keep, got = refs[2 * c:2 * c + 2]
        out[c * rows:(c + 1) * rows, :] = (keep[:, HI] + got[:, HI].astype(F32)).astype(BF16)


def high_sum(*pairs):
    args = [v for pair in pairs for v in pair]
    rows = sum(keep.shape[0] for keep, _ in pairs)
    return call(high_sum_kernel, None, (), args, [((rows, QUARTER), BF16)], [], "high_sum", 8)[0]


def split_refs(refs, counts):
    groups = []
    for count in counts:
        groups.append(refs[:count])
        refs = refs[count:]
    return groups, refs


def with_entry(parts, at, use):
    start = 0
    for ref in parts:
        @pl.when((at >= start) & (at < start + ref.shape[0]))
        def _(ref=ref, start=start):
            use(ref, at - start)
        start += ref.shape[0]


def sum_slots(info, owners, out_refs, one_slot):
    count = out_refs[0].shape[0]
    base = pl.program_id(0) * count
    slots = owners.shape[0]
    for ref in out_refs:
        ref[...] = jnp.zeros_like(ref)

    def add(slot, carry):
        owner = owners[slot] - base

        @pl.when((owner >= 0) & (owner < count))
        def _():
            one_slot(owner, entry_of(slot, info[3], slots))
        return carry

    lax.fori_loop(0, slots, add, 0)


def feedforward_sum_kernel(counts, info, owners, *refs):
    (b_parts, *a_parts), outs = split_refs(refs, counts)
    ga, gdb, gb, gda = outs
    me = info[0]

    def one_slot(owner, at):
        def add_b(ref, e):
            for i in range(gda.shape[2] // QUARTER):
                cols = slice(i * QUARTER, (i + 1) * QUARTER)
                base = i * 3 * RANK
                gb[owner, 0, :, cols] += ref[e, base:base + RANK, :].astype(F32)
                gb[owner, 1, :, cols] += ref[e, base + RANK:base + 2 * RANK, :].astype(F32)
                gda[owner, :, cols] += ref[e, base + 2 * RANK:base + 3 * RANK, :].astype(F32)

        with_entry(b_parts, at, add_b)
        for near_bit, parts in enumerate(a_parts):
            def add_a(ref, e, near_bit=near_bit):
                for r, cols in ((near_bit, LO), (near_bit ^ 2, HI)):
                    ga[owner, :, quarter(me, r)] += ref[e, :2 * RANK, cols].astype(F32)
                    gdb[owner, :, quarter(me, r)] += ref[e, 2 * RANK:, cols].astype(F32)

            with_entry(parts, at, add_a)

    sum_slots(info, owners, outs, one_slot)


def attention_sum_kernel(counts, info, owners, *refs):
    (b_parts, *a_parts), outs = split_refs(refs, counts)
    ga, gob, gq, gkv, goa = outs
    me = info[0]
    kv_cols = gkv.shape[3]

    def one_slot(owner, at):
        def add_b(ref, e):
            gq[owner] += ref[e, :RANK, :].astype(F32)
            goa[owner] += ref[e, RANK:2 * RANK, :].astype(F32)
            gkv[owner, 0] += ref[e, 2 * RANK:3 * RANK, :kv_cols].astype(F32)
            gkv[owner, 1] += ref[e, 2 * RANK:3 * RANK, kv_cols:2 * kv_cols].astype(F32)

        with_entry(b_parts, at, add_b)
        for r, parts in enumerate(a_parts):
            def add_a(ref, e, r=r):
                ga[owner, :, quarter(me, r)] += ref[e, :3 * RANK, :].astype(F32)
                gob[owner, :, quarter(me, r)] += ref[e, 3 * RANK:, :].astype(F32)

            with_entry(parts, at, add_a)

    sum_slots(info, owners, outs, one_slot)


def deal_kernel(slots, source, out, sems):
    made = [pltpu.make_async_copy(source.at[i], out.at[slots[i]], sems.at[i]) for i in range(source.shape[0])]
    for copy in made:
        copy.start()
    for copy in made:
        copy.wait()


def collect_kernel(slots, source, out, sems):
    made = [pltpu.make_async_copy(source.at[slots[i]], out.at[i], sems.at[i]) for i in range(source.shape[0])]
    for copy in made:
        copy.start()
    for copy in made:
        copy.wait()


def adapter_kernel(count, info, *refs):
    made = [pltpu.make_async_copy(refs[i].at[info[2]], refs[count + i], refs[-1].at[i]) for i in range(count)]
    for copy in made:
        copy.start()
    for copy in made:
        copy.wait()


def load_adapters(arrays, info):
    count = len(arrays)
    return pl.pallas_call(
        functools.partial(adapter_kernel, count),
        in_specs=[pl.BlockSpec(memory_space=pltpu.SMEM)] + [pl.BlockSpec(memory_space=pltpu.HBM)] * count,
        out_specs=[pl.BlockSpec(memory_space=pltpu.VMEM)] * count,
        out_shape=[pltpu.VMEM(a.shape[1:], a.dtype) for a in arrays],
        scratch_shapes=[pltpu.SemaphoreType.DMA((count,))],
        compiler_params=pltpu.CompilerParams(vmem_limit_bytes=MIB),
        cost_estimate=pl.CostEstimate(flops=1000, transcendentals=0, bytes_accessed=1000),
        name="adapters",
    )(info, *(in_hbm(a) for a in arrays))


def move_rows(kernel, value, slots, name, outs, in_space, out_space, sems):
    return pl.pallas_call(
        kernel,
        in_specs=[pl.BlockSpec(memory_space=pltpu.SMEM), pl.BlockSpec(memory_space=in_space)],
        out_specs=[pl.BlockSpec(memory_space=out_space)] * len(outs),
        out_shape=outs,
        scratch_shapes=[pltpu.SemaphoreType.DMA(sems)],
        compiler_params=pltpu.CompilerParams(vmem_limit_bytes=MIB),
        cost_estimate=pl.CostEstimate(flops=1000, transcendentals=0, bytes_accessed=1000),
        name=name,
    )(slots, pltpu.with_memory_space_constraint(value, in_space))


def sds(shape, dtype):
    return jax.ShapeDtypeStruct(tuple(shape), dtype)


def in_vmem(value):
    return pltpu.with_memory_space_constraint(value, pltpu.VMEM)


def in_hbm(value):
    return pltpu.with_memory_space_constraint(value, pltpu.HBM)


def call(kernel, info, weights, args, outs, scratch, name, mib, after=(), sems=()):
    vmem = pl.BlockSpec(memory_space=pltpu.VMEM)
    scalars = () if info is None else (info,)
    n, w = len(scalars), len(weights)

    def body(*refs):
        at = n + w + len(args)
        kernel(*refs[:at], *refs[at + len(after):])

    return pl.pallas_call(
        body,
        in_specs=[pl.BlockSpec(memory_space=pltpu.SMEM)] * n + [pl.BlockSpec(memory_space=pltpu.HBM)] * w + [vmem] * len(args)
        + [pl.BlockSpec(memory_space=pl.ANY)] * len(after),
        out_specs=[vmem] * len(outs),
        out_shape=[pltpu.VMEM(tuple(s), d) for s, d in outs],
        scratch_shapes=[pltpu.VMEM(s, d) for s, d in scratch] + ([pltpu.SemaphoreType.DMA(sems)] if sems else []),
        compiler_params=pltpu.CompilerParams(vmem_limit_bytes=mib * MIB),
        cost_estimate=pl.CostEstimate(flops=1000, transcendentals=0, bytes_accessed=1000),
        name=name,
    )(*scalars, *(in_hbm(a) for a in weights), *(in_vmem(a) for a in args), *after)


def whole_spec(value):
    zeros = (0,) * value.ndim
    return pl.BlockSpec(value.shape, lambda i, *_: zeros)


def sum_call(kernel, scalars, groups, outs, name):
    args = [v for group in groups for v in group]
    steps = 2
    specs = [pl.BlockSpec((o.shape[0] // steps,) + o.shape[1:], (lambda n: lambda i, *_: (i,) + (0,) * n)(o.ndim - 1))
             for o in outs]
    return pl.pallas_call(
        functools.partial(kernel, [len(group) for group in groups]),
        grid_spec=pltpu.PrefetchScalarGridSpec(
            num_scalar_prefetch=len(scalars), grid=(steps,),
            in_specs=[whole_spec(a) for a in args], out_specs=specs),
        out_shape=outs,
        compiler_params=pltpu.CompilerParams(
            dimension_semantics=("arbitrary",),
            vmem_limit_bytes=4 * MIB + 2 * sum(a.size * a.dtype.itemsize for a in args)
            + sum(o.size * o.dtype.itemsize for o in outs)),
        cost_estimate=pl.CostEstimate(flops=0, transcendentals=0, bytes_accessed=12000000),
        name=name,
    )(*scalars, *args)


def swap(value, bit, axis, size):
    return lax.ppermute(value, axis, [(i, i ^ bit) for i in range(size)])


def near(value):
    return swap(value, 1, "mp", PARTS)


def far(value):
    return swap(value, 2, "mp", PARTS)


def spread(value):
    there = far(value)
    return (value, near(value), there, near(there))


def far_sum_kernel(own, got, out):
    for to, other in ((LO, HI), (HI, LO)):
        out[:, to] = (own[:, to].astype(F32) + got[:, other].astype(F32)).astype(BF16)


def far_sum(own, got):
    return call(far_sum_kernel, None, (), (own, got), [(own.shape, BF16)], [], "far_sum", 6)[0]


def pair_sum_kernel(keep, got, out):
    out[...] = (keep[...] + got[...].astype(F32)).astype(BF16)


def pair_sum(keep, send, *before):
    got = near(send)
    got = late(got, *before) if before else got
    return call(pair_sum_kernel, None, (), (keep, got), [(send.shape, BF16)], [], "pair_sum", 6)[0]


def late(value, *others):
    return lax.optimization_barrier((value, *others))[0]


def doubled(stack, bit, size):
    return jnp.concatenate([stack, swap(stack, bit, "dp", size)], axis=0)


def entry_of(slot, place, size):
    bits = size.bit_length() - 1
    apart = slot ^ place
    return sum(((apart >> b) & 1) << (bits - 1 - b) for b in range(bits))


def shards(dp, residual, attention_gain, query_matrix, key_value_matrix, output_matrix, feedfwd_gain,
           gate_up_matrix, down_matrix, attention_adapter_input, query_adapter_output,
           key_value_adapter_output, output_adapter_input, output_adapter_output, feedfwd_adapter_input,
           feedfwd_adapter_output, down_adapter_input, down_adapter_output, lengths, adapter_index,
           dealing_slots, cotangent):
    seqs = residual.shape[0]
    length = cotangent.shape[1]
    units = down_matrix.shape[0]
    adapters = attention_adapter_input.shape[0]
    q_cols = query_matrix.shape[1]
    kv_cols = key_value_matrix.shape[2]
    kv_heads = kv_cols // HEAD
    heads = q_cols // HEAD
    rows = length // CHUNKS
    half = 2 * QUARTER
    me = lax.axis_index("mp")
    place = lax.axis_index("dp")

    is_there = dealing_slots[None, :] == jnp.arange(seqs, dtype=jnp.int32)[:, None]
    owners = jnp.sum(jnp.where(is_there, adapter_index[None, :], 0), axis=1)
    spans = jnp.sum(jnp.where(is_there, lengths[None, :], 0), axis=1)
    mine = jnp.arange(seqs, dtype=jnp.int32) == place
    my_length = jnp.sum(jnp.where(mine, spans, 0))
    my_adapter = jnp.sum(jnp.where(mine, owners, 0))
    info = jnp.stack([me.astype(jnp.int32), my_length, my_adapter, place.astype(jnp.int32)])

    gs = spread(cotangent[0])
    gains = jnp.stack(spread(jnp.stack([attention_gain, feedfwd_gain])))
    ordered, = move_rows(deal_kernel, residual, dealing_slots, "deal", [pltpu.VMEM(residual.shape, BF16)], pltpu.HBM,
                         pltpu.VMEM, (seqs,))
    dealt = lax.all_to_all(ordered, "dp", split_axis=0, concat_axis=1, tiled=True)[0]
    adapters_here = load_adapters(
        (attention_adapter_input, query_adapter_output, key_value_adapter_output, output_adapter_input,
         output_adapter_output, feedfwd_adapter_input, feedfwd_adapter_output, down_adapter_input,
         down_adapter_output), info)
    a1, qb, kvb, oa, ob, a2, fba, da, bd = adapters_here
    dealt = late(dealt, gs[2], a1, gains)
    beside = near(dealt)
    there = [far(dealt[c * rows:(c + 1) * rows]) for c in range(CHUNKS)]
    xs = [None] * CHUNKS
    cos_np, sin_np = rope_tables(length)
    cos = [jnp.asarray(cos_np[:, c * rows:(c + 1) * rows]) for c in range(CHUNKS)]
    sin = [jnp.asarray(sin_np[:, c * rows:(c + 1) * rows]) for c in range(CHUNKS)]
    wq, wkv, wo = query_matrix, key_value_matrix, output_matrix

    def like(*arrays):
        return [(a.shape, a.dtype) for a in arrays]

    wide, col, block, thin = (rows, WIDTH), (rows, half), (rows, QUARTER), (rows, 1)
    saved, kept, z_own, z_far = ([None] * CHUNKS for _ in range(4))
    order = ()
    for c in range(CHUNKS):
        xs[c] = (dealt, beside, there[c], near(late(there[c], saved[0][0]) if c else there[c]))
        outs = [((3 * RANK, rows), BF16), ((q_cols, rows), BF16), ((kv_heads, rows, HEAD), BF16),
                ((kv_heads, rows, HEAD), BF16), ((kv_cols, rows), BF16), ((kv_cols, rows), BF16)]
        saved[c] = call(
            functools.partial(project_kernel, c), info, (wq, wkv), (*xs[c], gains, a1, qb, kvb, cos[c], sin[c]), outs,
            [(wide, BF16)] + like(wq, wkv), "project_%d" % c, 12, order, (2,))
        outs = [(col, F32), (col, BF16), ((q_cols, rows), BF16), ((heads, rows), F32), ((RANK, rows), BF16)]
        pairs = [v for p in saved[:c + 1] for v in (p[2], p[5])]
        z_keep, z_send, *kept[c] = call(
            functools.partial(attend_kernel, c), info, (wo,), (saved[c][1], oa, ob, *pairs), outs, like(wo),
            "attend_%d" % c, 10, (saved[c][0],), (1,))
        z_own[c] = pair_sum(z_keep, late(z_send, z_far[0] if c else there[-1]))
        z_far[c] = far(z_own[c])
        order = (kept[c][1], z_own[c])
    def front(c, total, partial, order):
        hidden = (rows, units)
        outs = [(wide, BF16), (block, F32), (wide, BF16), (wide, BF16), (hidden, BF16), (hidden, BF16), (hidden, BF16),
                ((rows, 2 * RANK), BF16), ((rows, RANK), BF16),
                ((3 * RANK * units // QUARTER, QUARTER), BF16 if c else F32)]
        args = (*xs[c], total, near(total), *gs, gains, a2, bd, fba, da, *partial)
        weights = () if c else (gate_up_matrix, down_matrix)
        outs += like(*weights)
        return call(
            functools.partial(front_kernel, c, c == CHUNKS - 1), info, weights, (wgu, wd, *args) if c else args, outs,
            [((ROW_BLOCK, WIDTH), F32)], "front_%d" % c, 8, order, () if c else (2, units // QUARTER))

    def back(c, hidden, partial, order):
        first = col if c else (rows + 3 * RANK, half)
        outs = [((rows, RANK), F32), (first, F32), (first, BF16)]
        outs += [((3 * RANK, WIDTH), F32)] if c else []
        return call(
            functools.partial(back_kernel, c == 0), info, (), (wgu, *hidden[2:7], a2, fba, da, *partial), outs,
            [(block, F32), ((3 * RANK, QUARTER), F32)], "back_%d" % c, 8, order)

    def down(c, td, order):
        return call(down_kernel, info, (), (wd, hidden[c][4], td, bd, hidden[c][1]), [(col, F32), (col, BF16)],
                    [(block, F32)], "down_%d" % c, 6, order)

    def attend_back(c, total, partial, order):
        outs = [(block, F32), (col, F32), (col, BF16), (thin, F32), ((3 * RANK, QUARTER), F32 if c else BF16)]
        low = (4 * RANK + SPARE, half)
        outs += ([((4 * RANK, WIDTH), F32), ((kv_cols, rows), F32), ((kv_cols, rows), F32), ((SPARE // 2, rows), F32)]
                 if c else [(low, F32), (low, BF16)])
        scratch = [(wide, BF16), (wide, BF16), ((ROW_BLOCK, WIDTH), F32), ((q_cols, rows), BF16), ((q_cols, rows), F32),
                   ((c + 1, kv_cols, rows), F32), ((c + 1, kv_cols, rows), F32), ((rows, q_cols + 2 * kv_cols), BF16),
                   (block, F32), ((4 * RANK, QUARTER), F32)]
        triples = [v for p in saved[:c + 1] for v in (p[2], p[3], p[4])]
        return call(
            functools.partial(attend_back_kernel, c, c == 0), info, (wq, wkv, wo),
            (*xs[c], *gs, hidden[c][0], total, near(total), gains, a1, qb, kvb, oa, ob, cos[c], sin[c], *saved[c][:2],
             *kept[c], *triples, *partial), outs, scratch + like(wq, wkv, wo), "attend_back_%d" % c, 18, order, (3,))

    bits = [1 << b for b in reversed(range(dp.bit_length() - 1))]
    def to_bands(value):
        return lax.all_to_all(value.reshape(dp, length // dp, QUARTER), "dp", split_axis=0, concat_axis=0, tiled=True)

    def collect(value, name, *before):
        rows_out = sds((seqs, length // dp, QUARTER), BF16)
        return move_rows(collect_kernel, value, late(dealing_slots, *before), name, [rows_out], pltpu.VMEM, pl.ANY,
                         (seqs,))[0]

    hidden, d_own, d_far, y_keep, y_got = ([None] * CHUNKS for _ in range(5))
    *hidden[0], wgu, wd = front(0, far_sum(z_own[0], z_far[0]), (), order)
    step = hidden[0][8]
    hidden[1] = front(1, far_sum(z_own[1], late(z_far[1], step)), hidden[0][9:], (step,))
    fb = hidden[1][9][None]
    fb_first = swap(fb, bits[0], "dp", dp)
    td, d_keep, d_send, fa = back(1, hidden[1], (), (hidden[1][8],))
    d_own[1] = pair_sum(d_keep, late(d_send, fb_first))
    d_far[1] = far(d_own[1])
    fb = fb_more = jnp.concatenate([fb, fb_first], axis=0)
    for bit in bits[1:-1]:
        fb_more = doubled(fb_more, bit, dp)
    fb_more = fb_more[2:]
    fb_side = swap(fb, bits[-1], "dp", dp)
    td_0, d_keep, d_send = back(0, hidden[0], (fa,), (d_own[1],))
    y_keep[1], y_send = down(1, td, (td_0,))
    total = far_sum(d_own[1], late(d_far[1], y_send))
    d_own[0] = pair_sum(d_keep, late(d_send, fb_more, fb_side), total)
    d_far[0] = far(d_own[0])
    fb_more_side = swap(fb_more, bits[-1], "dp", dp)
    y_got[1] = near(late(y_send, d_own[0]))
    dxq, h_keep, h_send, inv, *sums = attend_back(1, total, (), (d_own[0], y_send))
    total = far_sum(d_own[0], late(d_far[0], inv))
    h_got = near(late(h_send, fb_more_side))
    h_high = high_sum((h_keep, h_got))
    h_far = far(h_high)
    final = [None, (dxq, h_keep, h_got, h_far, inv)]
    fa = total[rows:][None]
    fa_first = swap(fa, bits[0], "dp", dp)
    dxq, h_keep, h_send, inv, att_b, aa_keep, aa_send = attend_back(0, total, sums, (h_high,))
    ready = (fa_first, h_far)
    aa_got = near(late(aa_send, *ready))
    aa_high = high_sum((aa_keep, aa_got))
    aa_far = far(aa_high)
    h_got = near(late(h_send, *ready))
    h_high = high_sum((h_keep, h_got))
    h_far = far(h_high)
    final[0] = (dxq, h_keep, h_got, h_far, inv)
    att_a = aa_keep[:4 * RANK, :QUARTER] + aa_got[:4 * RANK, :QUARTER].astype(F32)
    att_a = (att_a + late(aa_far, h_high)[:4 * RANK].astype(F32)).astype(BF16)
    n_b = att_b.shape[0]
    att = jnp.concatenate([att_b, att_a], axis=0)[None]
    y_keep[0], y_send = down(0, td_0, (att,))
    y_got[0] = near(y_send)
    att = doubled(att, bits[0], dp)
    att = late(att, h_far, y_send)
    for bit in bits[1:-1]:
        att = doubled(att, bit, dp)
    fa = late(jnp.concatenate([fa, fa_first], axis=0), aa_high)
    for bit in bits[1:-1]:
        fa = doubled(fa, bit, dp)
    fa_side = swap(fa, bits[-1], "dp", dp)
    y_far = far(high_sum(*((k, late(g, h_far)) for k, g in zip(y_keep, y_got))))

    dinput, = call(finish_kernel, None, (), (gains, dealt, aa_high, aa_far, *(v for f in final for v in f)),
                   [((length, QUARTER), BF16)], [], "finish", 8, (att, fa_side))
    input_grad = collect(to_bands(dinput), "collect_grad")
    result, = call(output_kernel, info, (), (late(y_far, dinput), *(v for p in zip(y_keep, y_got) for v in p)),
                   [((length, QUARTER), BF16)], [], "output", 8)
    output = collect(to_bands(result), "collect_out", input_grad)

    outs = [sds((adapters, 2 * RANK, WIDTH), F32), sds((adapters, RANK, WIDTH), F32),
            sds((adapters, 2, RANK, units), F32), sds((adapters, RANK, units), F32)]
    ga_ffn, g_down_b, g_ffn_b, g_down_a = sum_call(
        feedforward_sum_kernel, (info, owners),
        ((fb, fb_more, fb_side, fb_more_side), (fa, fa_side), (near(fa), near(fa_side))), outs, "feedforward_sum")

    att_side = swap(att, bits[-1], "dp", dp)
    a_parts = [att[:, n_b:], att_side[:, n_b:]]
    a_far = [far(v) for v in a_parts]
    a_far[1] = late(a_far[1], g_down_a)
    outs = [sds((adapters, 3 * RANK, WIDTH), F32), sds((adapters, RANK, WIDTH), F32),
            sds((adapters, RANK, q_cols), F32), sds((adapters, 2, RANK, kv_cols), F32),
            sds((adapters, RANK, q_cols), F32)]
    ga_att, g_out_b, g_query_b, g_kv_b, g_out_a = sum_call(
        attention_sum_kernel, (info, owners),
        ((att, att_side), a_parts, [near(v) for v in a_parts], a_far, [near(v) for v in a_far]), outs, "attention_sum")
    return (output, input_grad, ga_att, g_query_b, g_kv_b, g_out_a, g_out_b, ga_ffn, g_ffn_b, g_down_a, g_down_b)


def solution(mesh):
    in_specs = (
        P(None, "dp", "mp"), P("mp"), P(None, "mp"), P(None, None, "mp"), P("mp", None), P("mp"),
        P(None, None, "mp"), P("mp", None), P(), P(None, None, "mp"), P(None, None, None, "mp"),
        P(None, None, "mp"), P(), P(), P(None, None, None, "mp"), P(None, None, "mp"), P(), P(), P(), P(),
        P("dp", None, "mp"),
    )
    out_specs = (
        P(None, "dp", "mp"), P(None, "dp", "mp"), P(), P(None, None, "mp"), P(None, None, None, "mp"),
        P(None, None, "mp"), P(), P(), P(None, None, None, "mp"), P(None, None, "mp"), P(),
    )
    return jax.shard_map(
        functools.partial(shards, mesh.shape["dp"]), mesh=mesh, in_specs=in_specs, out_specs=out_specs,
        check_vma=False)
```

```python
import functools

import jax
import jax.numpy as jnp
import numpy as np
from jax import lax
from jax.experimental import pallas as pl
from jax.experimental.pallas import tpu as pltpu
from jax.sharding import PartitionSpec as P

WIDTH = 2048
HEAD = 64
HALF = HEAD // 2
RANK = 16
EPS = 1e-05
ROPE_BASE = 500000.0
NEG_FILL = -1e30
PARTS = 4
LANES = 128
SPARE = 32
ROW_BLOCK = 64
QUARTER = WIDTH // PARTS
CHUNKS = 2
MIB = 1024 * 1024
F32 = jnp.float32
BF16 = jnp.bfloat16


def nn(a, b):
    return lax.dot_general(a, b, (((1,), (0,)), ((), ())), preferred_element_type=F32)


def nt(a, b):
    return lax.dot_general(a, b, (((1,), (1,)), ((), ())), preferred_element_type=F32)


def rope_tables(length):
    freq = ROPE_BASE ** (-np.arange(HALF, dtype=np.float32) * np.float32(2.0 / HEAD))
    angles = (np.arange(length, dtype=np.float32)[None, :] * freq.astype(np.float32)[:, None]).astype(np.float32)
    return np.cos(angles).astype(np.float32), np.sin(angles).astype(np.float32)


def quarter(me, rel):
    return pl.ds(pl.multiple_of((me ^ rel) * QUARTER, QUARTER), QUARTER)


LO, HI = slice(0, QUARTER), slice(QUARTER, 2 * QUARTER)


def total_block(rel, rows_at, own, oth):
    return (own if rel in (0, 2) else oth)[rows_at, LO if rel in (0, 1) else HI].astype(F32)


def store_block(rel, value, rows_at, keep_ref, send_ref):
    to = pl.ds(pl.multiple_of((rel // 2) * QUARTER, QUARTER), QUARTER)

    @pl.when(rel % 2 == 0)
    def _():
        keep_ref[rows_at, to] = value[...]

    @pl.when(rel % 2 == 1)
    def _():
        send_ref[rows_at, to] = value[...].astype(BF16)


def chunk_of(ref, chunk, rows):
    return ref if ref.shape[0] == rows else ref.at[chunk * rows:(chunk + 1) * rows]


def row_block(i):
    return pl.ds(pl.multiple_of(i * ROW_BLOCK, ROW_BLOCK), ROW_BLOCK)


def is_valid(chunk, i, rows, length):
    return chunk * rows + i * ROW_BLOCK + lax.broadcasted_iota(jnp.int32, (ROW_BLOCK, 1), 0) < length


def copies_of(pairs, sems):
    made = [pltpu.make_async_copy(source, target, sems.at[i]) for i, (source, target) in enumerate(pairs)]
    for copy in made:
        copy.start()
    return made


def put_block(rel, value, keep_ref, send_ref):
    ref = keep_ref if rel in (0, 2) else send_ref
    ref[:, LO if rel in (0, 1) else HI] = value.astype(ref.dtype)


def rotate(value, cos, sin, out_ref):
    for i in range(value.shape[0] // HEAD):
        u1, u2 = value[i * HEAD:i * HEAD + HALF], value[i * HEAD + HALF:(i + 1) * HEAD]
        out_ref[i * HEAD:i * HEAD + HALF, :] = (u1 * cos - u2 * sin).astype(BF16)
        out_ref[i * HEAD + HALF:(i + 1) * HEAD, :] = (u2 * cos + u1 * sin).astype(BF16)


def turn_back(value, cos, sin, out_ref):
    for i in range(value.shape[0] // HEAD):
        w1, w2 = value[i * HEAD:i * HEAD + HALF], value[i * HEAD + HALF:(i + 1) * HEAD]
        out_ref[i * HEAD:i * HEAD + HALF, :] = (w1 * cos + w2 * sin).astype(BF16)
        out_ref[i * HEAD + HALF:(i + 1) * HEAD, :] = (w2 * cos - w1 * sin).astype(BF16)


def head_rows(i):
    return pl.ds(pl.multiple_of(i * HEAD, HEAD), HEAD)


def visible(key_start, query_start, rows, length):
    kpos = key_start + lax.broadcasted_iota(jnp.int32, (rows, rows), 0)
    qpos = query_start + lax.broadcasted_iota(jnp.int32, (rows, rows), 1)
    return (kpos <= qpos) & (kpos < length)


def project_kernel(chunk, info, wq_h, wkv_h, x0, x1, x2, x3, gains, a1, qb, kvb, cos_t, sin_t,
                   t1t_out, qt_out, kn_out, vn_out, kt_out, vt_out, h_out, wq, wkv, sems):
    copies = copies_of(((wkv_h, wkv), (wq_h, wq)), sems)
    me = info[0]
    rows = h_out.shape[0]
    kv_heads = kn_out.shape[0]
    xs = [chunk_of(x, chunk, rows) for x in (x0, x1, x2, x3)]

    def norm(i, carry):
        at = row_block(i)
        square = jnp.zeros((ROW_BLOCK, 1), F32)
        for r in range(PARTS):
            v = xs[r][at, :].astype(F32)
            square = square + jnp.sum(v * v, axis=1, keepdims=True)
        inv = lax.rsqrt(square / WIDTH + EPS)
        for r in range(PARTS):
            v = xs[r][at, :].astype(F32)
            h_out[at, quarter(me, r)] = (v * inv * gains[r, 0:1, :].astype(F32)).astype(BF16)
        return carry

    lax.fori_loop(0, rows // ROW_BLOCK, norm, 0)
    h = h_out[...]
    t1 = nt(h, a1[...])
    t1t_out[...] = t1.T.astype(BF16)
    t1b = t1.astype(BF16)
    cos, sin = cos_t[...], sin_t[...]
    copies[0].wait()
    k = nn(h, wkv[0]) + nn(t1b[:, RANK:2 * RANK], kvb[0])
    rotate(k.T, cos, sin, kt_out)
    k_n = kt_out[...].T
    v_n = (nn(h, wkv[1]) + nn(t1b[:, 2 * RANK:], kvb[1])).astype(BF16)
    vt_out[...] = v_n.T
    for i in range(kv_heads):
        kn_out[i] = k_n[:, i * HEAD:(i + 1) * HEAD]
        vn_out[i] = v_n[:, i * HEAD:(i + 1) * HEAD]
    copies[1].wait()
    q = nn(h, wq[...]) + nn(t1b[:, :RANK], qb[...])
    rotate(q.T * (HEAD ** -0.5), cos, sin, qt_out)


def attend_kernel(chunk, info, wo_h, qt, oa, ob, *rest):
    pairs, rest = rest[:2 * (chunk + 1)], rest[2 * (chunk + 1):]
    z_keep, z_send, ot_out, lse_out, tot_out, wo, sems = rest
    copies = copies_of(((wo_h, wo),), sems)
    keys, values = pairs[0::2], pairs[1::2]
    me, length = info[0], info[1]
    rows = qt.shape[1]
    kv_heads = keys[0].shape[0]
    heads = qt.shape[0] // HEAD
    group = heads // kv_heads

    kept = [jnp.concatenate([visible(c * rows, chunk * rows, rows, length)] * group, axis=1) for c in range(chunk + 1)]

    def one_group(j, carry):
        q_g = jnp.concatenate([qt[head_rows(j * group + g), :] for g in range(group)], axis=1)
        parts = [jnp.where(kept[c], nn(keys[c][j], q_g), NEG_FILL) for c in range(chunk + 1)]
        top = functools.reduce(jnp.maximum, [jnp.max(s, axis=0, keepdims=True) for s in parts])
        es = [jnp.exp(s - top) for s in parts]
        total = sum(jnp.sum(e, axis=0, keepdims=True) for e in es)
        low = top + jnp.log(total)
        o_t = sum(nn(value[head_rows(j), :], e.astype(BF16)) for value, e in zip(values, es))
        o_t = (o_t / total).astype(BF16)
        for g in range(group):
            cols = slice(g * rows, (g + 1) * rows)
            lse_out[pl.ds(j * group + g, 1), :] = low[:, cols]
            ot_out[head_rows(j * group + g), :] = o_t[:, cols]
        return carry

    lax.fori_loop(0, kv_heads, one_group, 0)
    o = ot_out[...].T
    to = nt(o, oa[...])
    tot_out[...] = to.T.astype(BF16)
    to = to.astype(BF16)
    copies[0].wait()
    for r in range(PARTS):
        at = quarter(me, r)
        put_block(r, nn(o, wo[:, at]) + nn(to, ob[:, at]), z_keep, z_send)


def front_kernel(chunk, last, info, wgu_in, wd_in, x0, x1, x2, x3, zo, zp, g0, g1, g2, g3, gains, a2, bd, fb, da,
                 *rest):
    units = wd_in.shape[0]
    if chunk:
        wgu, wd = wgu_in, wd_in
    else:
        (wgu, wd, f_s, sems), rest = rest[-4:], rest[:-4]
        rest = (*rest, f_s)

    def copies(i):
        c = pl.ds(pl.multiple_of(i * QUARTER, QUARTER), QUARTER)
        return (pltpu.make_async_copy(wgu_in.at[:, :, c], wgu.at[:, :, c], sems.at[0, i]),
                pltpu.make_async_copy(wd_in.at[c, :], wd.at[c, :], sems.at[1, i]))

    if not chunk:
        for i in range(units // QUARTER):
            for copy in copies(i):
                copy.start()
    f_s = rest[-1]
    xm_out, xq_out, h_out, g_out, act_out, dg_out, du_out, t2_s, dtd_s, b_out = rest[-11:-1]
    me, length = info[0], info[1]
    rows = h_out.shape[0]
    xs, gs = ([chunk_of(v, chunk, rows) for v in vs] for vs in ((x0, x1, x2, x3), (g0, g1, g2, g3)))

    def norm(i, carry):
        at = row_block(i)
        valid = is_valid(chunk, i, rows, length)
        square = jnp.zeros((ROW_BLOCK, 1), F32)
        for r in range(PARTS):
            v = xs[r][at, :].astype(F32) + total_block(r, at, zo, zp)
            if r == 0:
                xq_out[at, :] = v
            f_s[:, quarter(me, r)] = v
            square = square + jnp.sum(v * v, axis=1, keepdims=True)
            g_out[at, quarter(me, r)] = jnp.where(valid, gs[r][at, :], jnp.zeros((), BF16))
        inv = lax.rsqrt(square / WIDTH + EPS)
        for r in range(PARTS):
            v = f_s[:, quarter(me, r)]
            xm_out[at, quarter(me, r)] = v.astype(BF16)
            h_out[at, quarter(me, r)] = (v * inv * gains[r, 1:2, :].astype(F32)).astype(BF16)
        return carry

    lax.fori_loop(0, rows // ROW_BLOCK, norm, 0)
    t2 = nt(h_out[...], a2[...])
    t2_s[...] = t2.astype(BF16)
    dtd = nt(g_out[...], bd[...])
    dtd_s[...] = dtd.astype(BF16)
    t2t, dtdt = t2.T.astype(BF16), dtd.T.astype(BF16)

    def block(i, carry):
        c = pl.ds(pl.multiple_of(i * QUARTER, QUARTER), QUARTER)
        if not chunk:
            for copy in copies(i):
                copy.wait()
        h, g = h_out[...], g_out[...]
        gate = nn(h, wgu[0, :, c]) + nn(t2_s[:, :RANK], fb[0, :, c])
        up = nn(h, wgu[1, :, c]) + nn(t2_s[:, RANK:], fb[1, :, c])
        dact = nt(g, wd[c, :]) + nn(dtd_s[...], da[:, c])
        sig = 1.0 / (1.0 + jnp.exp(-gate))
        silu = gate * sig
        act = (silu * up).astype(BF16)
        dgate = (dact * up * sig * (1.0 + gate * (1.0 - sig))).astype(BF16)
        dup = (dact * silu).astype(BF16)
        act_out[:, c], dg_out[:, c], du_out[:, c] = act, dgate, dup
        for k, value in enumerate((nn(t2t[:RANK], dgate), nn(t2t[RANK:], dup), nn(dtdt, act))):
            at = pl.ds(pl.multiple_of((3 * i + k) * RANK, RANK), RANK)
            if last:
                value = value + rest[0][at, :]
            b_out[at, :] = value.astype(b_out.dtype)
        return carry

    lax.fori_loop(0, units // QUARTER, block, 0)


def back_kernel(last, info, wgu, h, g, act, dg, du, a2, fb, da, *rest):
    (value_s, low_s), rest = rest[-2:], rest[:-2]
    outs, rest = (rest[-3:], rest[:-3]) if last else (rest[-4:], rest[:-4])
    td_out, d_keep, d_send = outs[:3]
    me = info[0]
    rows = h.shape[0]
    dt2 = jnp.concatenate([nt(dg[...], fb[0]), nt(du[...], fb[1])], axis=1)
    td = nt(act[...], da[...])
    td_out[...] = td
    dt2b = dt2.astype(BF16)
    dt2t, tdt = dt2.T.astype(BF16), td.T.astype(BF16)

    def block(r, carry):
        at = quarter(me, r)
        value_s[...] = nt(dg[...], wgu[0, at, :]) + nt(du[...], wgu[1, at, :]) + nn(dt2b, a2[:, at])
        store_block(r, value_s, slice(0, rows), d_keep, d_send)
        low_s[:2 * RANK, :] = nn(dt2t, h[:, at])
        low_s[2 * RANK:, :] = nn(tdt, g[:, at])
        if last:
            low_s[...] += rest[0][:, at]
            store_block(r, low_s, slice(rows, rows + 3 * RANK), d_keep, d_send)
        else:
            outs[3][:, at] = low_s[...]
        return carry

    lax.fori_loop(0, PARTS, block, 0)


def down_kernel(info, wd, act, td, bd, xq, y_keep, y_send, value_s):
    me = info[0]
    tdb = td[...].astype(BF16)

    def block(r, carry):
        at = quarter(me, r)
        value_s[...] = nn(act[...], wd[:, at]) + nn(tdb, bd[:, at])
        store_block(r, value_s, slice(0, act.shape[0]), y_keep, y_send)
        return carry

    lax.fori_loop(0, PARTS, block, 0)
    y_keep[:, LO] += xq[...]


def attend_back_kernel(chunk, last, info, wq_h, wkv_h, wo_h, x0, x1, x2, x3, g0, g1, g2, g3, xm, do_, dp, gains, a1,
                       qb, kvb, oa, ob, cos_t, sin_t, t1t, qt, ot, lse, tot, *rest):
    scratch, rest = rest[-14:], rest[:-14]
    h_in, z_s, f_s, dot_s, dqt_s, dkt_s, dvt_s, dq_s, value_s, low_s, wq, wkv, wo, sems = scratch
    copies = copies_of(((wo_h, wo), (wq_h, wq), (wkv_h, wkv)), sems)
    n_out = 7 if last else 9
    outs, rest = rest[-n_out:], rest[:-n_out]
    dxq_out, h_keep, h_send, inv_out, b_out = outs[:5]
    triples, rest = rest[:3 * (chunk + 1)], rest[3 * (chunk + 1):]
    keys, values, keys_t = triples[0::3], triples[1::3], triples[2::3]
    me, length = info[0], info[1]
    rows = xm.shape[0]
    kv_heads = keys[0].shape[0]
    heads = qt.shape[0] // HEAD
    group = heads // kv_heads
    q_cols, kv_cols = heads * HEAD, kv_heads * HEAD
    xs, gs = ([chunk_of(v, chunk, rows) for v in vs] for vs in ((x0, x1, x2, x3), (g0, g1, g2, g3)))

    def norm_back(i, carry):
        at = row_block(i)
        valid = is_valid(chunk, i, rows, length)
        square, first, inner = (jnp.zeros((ROW_BLOCK, 1), F32) for _ in range(3))
        for r in range(PARTS):
            v = xm[at, quarter(me, r)].astype(F32)
            square = square + jnp.sum(v * v, axis=1, keepdims=True)
            w = total_block(r, at, do_, dp) * gains[r, 1:2, :].astype(F32)
            f_s[:, quarter(me, r)] = w
            inner = inner + jnp.sum(v * w, axis=1, keepdims=True)
            u = xs[r][at, :].astype(F32)
            first = first + jnp.sum(u * u, axis=1, keepdims=True)
        inv_one = lax.rsqrt(first / WIDTH + EPS)
        inv_out[at, :] = inv_one
        inv = lax.rsqrt(square / WIDTH + EPS)
        back = inv * inv * inv * inner / WIDTH
        for r in range(PARTS):
            v = xm[at, quarter(me, r)].astype(F32)
            g = jnp.where(valid, gs[r][at, :].astype(F32), 0.0)
            d = g + inv * f_s[:, quarter(me, r)] - v * back
            if r == 0:
                dxq_out[at, :] = d
            z_s[at, quarter(me, r)] = d.astype(BF16)
            u = xs[r][at, :].astype(F32)
            h_in[at, quarter(me, r)] = (u * inv_one * gains[r, 0:1, :].astype(F32)).astype(BF16)
        return carry

    lax.fori_loop(0, rows // ROW_BLOCK, norm_back, 0)
    dz = z_s[...]
    dto = nt(dz, ob[...])
    copies[0].wait()
    d_o = nt(dz, wo[...]) + nn(dto.astype(BF16), oa[...])
    dot_s[...] = d_o.T.astype(BF16)
    kept = [jnp.concatenate([visible(c * rows, chunk * rows, rows, length)] * group, axis=1) for c in range(chunk + 1)]

    def one_group(j, carry):
        places = [head_rows(j * group + g) for g in range(group)]
        q_g = jnp.concatenate([qt[at, :] for at in places], axis=1)
        do_g = jnp.concatenate([dot_s[at, :] for at in places], axis=1)
        o_g = jnp.concatenate([ot[at, :] for at in places], axis=1)
        low = jnp.concatenate([lse[pl.ds(j * group + g, 1), :] for g in range(group)], axis=1)
        dots = jnp.sum(do_g.astype(F32) * o_g.astype(F32), axis=0, keepdims=True)
        dq_g = 0.0
        for c in range(chunk + 1):
            prob = jnp.where(kept[c], jnp.exp(nn(keys[c][j], q_g) - low), 0.0)
            ds = (prob * (nn(values[c][j], do_g) - dots)).astype(BF16)
            dq_g = dq_g + nn(keys_t[c][head_rows(j), :], ds)
            dk, dv = nt(q_g, ds), nt(do_g, prob.astype(BF16))
            if last:
                dk, dv = dk + rest[2][head_rows(j), :], dv + rest[3][head_rows(j), :]
            dkt_s[c, head_rows(j), :], dvt_s[c, head_rows(j), :] = dk, dv
        for g in range(group):
            dqt_s[places[g], :] = dq_g[:, g * rows:(g + 1) * rows]
        return carry

    lax.fori_loop(0, kv_heads, one_group, 0)
    if not last:
        outs[6][...], outs[7][...] = dkt_s[0], dvt_s[0]
    cos, sin = cos_t[...], sin_t[...]
    dto_t, o_t = dto.T.astype(BF16), ot[...]
    d_out_a = nt(dto_t, o_t)
    turn_back(dqt_s[...], cos * (HEAD ** -0.5), sin * (HEAD ** -0.5), dot_s)
    dq_s[:, :q_cols] = dot_s[...].T
    turn_back(dkt_s[chunk], cos, sin, dot_s)
    dq_s[:, q_cols:q_cols + kv_cols] = dot_s[:kv_cols, :].T
    dq_s[:, q_cols + kv_cols:] = dvt_s[chunk].T.astype(BF16)
    dq, dk, dv = dq_s[:, :q_cols], dq_s[:, q_cols:q_cols + kv_cols], dq_s[:, q_cols + kv_cols:]
    dt1 = jnp.concatenate([nt(dq, qb[...]), nt(dk, kvb[0]), nt(dv, kvb[1])], axis=1)
    dt1b = dt1.astype(BF16)
    kv_pad = jnp.zeros((RANK, QUARTER - 2 * kv_cols), F32)
    d_kv = jnp.concatenate([nn(t1t[RANK:2 * RANK, :], dk), nn(t1t[2 * RANK:, :], dv), kv_pad], axis=1)
    for k, value in enumerate((nn(t1t[:RANK, :], dq), d_out_a, d_kv)):
        at = slice(k * RANK, (k + 1) * RANK)
        if last:
            value = value + rest[0][at, :]
        b_out[at, :] = value.astype(b_out.dtype)
    dt1t = dt1.T.astype(BF16)
    copies[1].wait()
    copies[2].wait()

    def block(r, inner):
        at = quarter(me, r)
        d = nt(dq_s[:, :q_cols], wq[at, :]) + nn(dt1b, a1[:, at])
        d = d + nt(dq_s[:, q_cols:q_cols + kv_cols], wkv[0, at, :]) + nt(dq_s[:, q_cols + kv_cols:], wkv[1, at, :])
        value_s[...] = d
        store_block(r, value_s, slice(0, rows), h_keep, h_send)
        low_s[:3 * RANK, :] = nn(dt1t, h_in[:, at])
        low_s[3 * RANK:, :] = nn(tot[...], z_s[:, at])
        if last:
            low_s[...] += rest[1][:, at]
            store_block(r, low_s, slice(0, 4 * RANK), outs[5], outs[6])
        else:
            outs[5][:, at] = low_s[...]
        return inner + jnp.sum(d * h_in[:, at].astype(F32), axis=1, keepdims=True)

    inner = lax.fori_loop(0, PARTS, block, jnp.zeros((rows, 1), F32))
    inner = jnp.broadcast_to(inner, (rows, LANES)).T[:SPARE // 2, :]
    if last:
        for ref in outs[5:7]:
            for c, value in enumerate((inner, rest[4][...])):
                at = slice(4 * RANK + c * SPARE // 2, 4 * RANK + (c + 1) * SPARE // 2)
                ref[at, QUARTER:QUARTER + rows] = value.astype(ref.dtype)
                ref[at, QUARTER + rows:] = jnp.zeros((SPARE // 2, QUARTER - rows), ref.dtype)
                ref[at, :QUARTER] = jnp.zeros((SPARE // 2, QUARTER), ref.dtype)
    else:
        outs[8][...] = inner


def output_kernel(info, y_far, *refs):
    out = refs[-1]
    rows = out.shape[0] // CHUNKS
    for c in range(CHUNKS):
        y_keep, y_got = refs[2 * c:2 * (c + 1)]
        at = slice(c * rows, (c + 1) * rows)
        valid = c * rows + lax.broadcasted_iota(jnp.int32, (rows, 1), 0) < info[1]
        y = y_keep[:, LO] + y_got[:, LO].astype(F32) + y_far[at, :].astype(F32)
        out[at, :] = jnp.where(valid, y, 0.0).astype(BF16)


def finish_kernel(gains, x_all, aa_high, aa_far, *refs):
    out = refs[-1]
    gain = gains[0, 0:1, :].astype(F32)
    rows = out.shape[0] // CHUNKS
    inner = aa_high[4 * RANK:, :].astype(F32) + aa_far[4 * RANK:, :].astype(F32)
    for c in range(CHUNKS):
        dx, keep, got, there, inv = refs[5 * c:5 * (c + 1)]
        x = chunk_of(x_all, c, rows)
        mine = inner[c * SPARE // 2:c * SPARE // 2 + 8, :rows].T[:, 0:1]
        inv = inv[...]
        grad = keep[:, LO] + got[:, LO].astype(F32) + there[...].astype(F32)
        grad = inv * (gain * grad) - x[...].astype(F32) * (inv * inv * mine / WIDTH)
        out[c * rows:(c + 1) * rows, :] = (dx[...] + grad).astype(BF16)


def high_sum_kernel(*refs):
    out = refs[-1]
    rows = out.shape[0] // (len(refs) // 2)
    for c in range(len(refs) // 2):
        keep, got = refs[2 * c:2 * c + 2]
        out[c * rows:(c + 1) * rows, :] = (keep[:, HI] + got[:, HI].astype(F32)).astype(BF16)


def high_sum(*pairs):
    args = [v for pair in pairs for v in pair]
    rows = sum(keep.shape[0] for keep, _ in pairs)
    return call(high_sum_kernel, None, (), args, [((rows, QUARTER), BF16)], [], "high_sum", 8)[0]


def split_refs(refs, counts):
    groups = []
    for count in counts:
        groups.append(refs[:count])
        refs = refs[count:]
    return groups, refs


def with_entry(parts, at, use):
    start = 0
    for ref in parts:
        @pl.when((at >= start) & (at < start + ref.shape[0]))
        def _(ref=ref, start=start):
            use(ref, at - start)
        start += ref.shape[0]


def sum_slots(info, owners, out_refs, one_slot):
    count = out_refs[0].shape[0]
    base = pl.program_id(0) * count
    slots = owners.shape[0]
    for ref in out_refs:
        ref[...] = jnp.zeros_like(ref)

    def add(slot, carry):
        owner = owners[slot] - base

        @pl.when((owner >= 0) & (owner < count))
        def _():
            one_slot(owner, entry_of(slot, info[3], slots))
        return carry

    lax.fori_loop(0, slots, add, 0)


def feedforward_sum_kernel(counts, info, owners, *refs):
    (b_parts, *a_parts), outs = split_refs(refs, counts)
    ga, gdb, gb, gda = outs
    me = info[0]

    def one_slot(owner, at):
        def add_b(ref, e):
            for i in range(gda.shape[2] // QUARTER):
                cols = slice(i * QUARTER, (i + 1) * QUARTER)
                base = i * 3 * RANK
                gb[owner, 0, :, cols] += ref[e, base:base + RANK, :].astype(F32)
                gb[owner, 1, :, cols] += ref[e, base + RANK:base + 2 * RANK, :].astype(F32)
                gda[owner, :, cols] += ref[e, base + 2 * RANK:base + 3 * RANK, :].astype(F32)

        with_entry(b_parts, at, add_b)
        for near_bit, parts in enumerate(a_parts):
            def add_a(ref, e, near_bit=near_bit):
                for r, cols in ((near_bit, LO), (near_bit ^ 2, HI)):
                    ga[owner, :, quarter(me, r)] += ref[e, :2 * RANK, cols].astype(F32)
                    gdb[owner, :, quarter(me, r)] += ref[e, 2 * RANK:, cols].astype(F32)

            with_entry(parts, at, add_a)

    sum_slots(info, owners, outs, one_slot)


def attention_sum_kernel(counts, info, owners, *refs):
    (b_parts, *a_parts), outs = split_refs(refs, counts)
    ga, gob, gq, gkv, goa = outs
    me = info[0]
    kv_cols = gkv.shape[3]

    def one_slot(owner, at):
        def add_b(ref, e):
            gq[owner] += ref[e, :RANK, :].astype(F32)
            goa[owner] += ref[e, RANK:2 * RANK, :].astype(F32)
            gkv[owner, 0] += ref[e, 2 * RANK:3 * RANK, :kv_cols].astype(F32)
            gkv[owner, 1] += ref[e, 2 * RANK:3 * RANK, kv_cols:2 * kv_cols].astype(F32)

        with_entry(b_parts, at, add_b)
        for r, parts in enumerate(a_parts):
            def add_a(ref, e, r=r):
                ga[owner, :, quarter(me, r)] += ref[e, :3 * RANK, :].astype(F32)
                gob[owner, :, quarter(me, r)] += ref[e, 3 * RANK:, :].astype(F32)

            with_entry(parts, at, add_a)

    sum_slots(info, owners, outs, one_slot)


def deal_kernel(slots, source, out, sems):
    made = [pltpu.make_async_copy(source.at[i], out.at[slots[i]], sems.at[i]) for i in range(source.shape[0])]
    for copy in made:
        copy.start()
    for copy in made:
        copy.wait()


def collect_kernel(slots, source, out, sems):
    made = [pltpu.make_async_copy(source.at[slots[i]], out.at[i], sems.at[i]) for i in range(source.shape[0])]
    for copy in made:
        copy.start()
    for copy in made:
        copy.wait()


def adapter_kernel(count, info, *refs):
    made = [pltpu.make_async_copy(refs[i].at[info[2]], refs[count + i], refs[-1].at[i]) for i in range(count)]
    for copy in made:
        copy.start()
    for copy in made:
        copy.wait()


def load_adapters(arrays, info):
    count = len(arrays)
    return pl.pallas_call(
        functools.partial(adapter_kernel, count),
        in_specs=[pl.BlockSpec(memory_space=pltpu.SMEM)] + [pl.BlockSpec(memory_space=pltpu.HBM)] * count,
        out_specs=[pl.BlockSpec(memory_space=pltpu.VMEM)] * count,
        out_shape=[pltpu.VMEM(a.shape[1:], a.dtype) for a in arrays],
        scratch_shapes=[pltpu.SemaphoreType.DMA((count,))],
        compiler_params=pltpu.CompilerParams(vmem_limit_bytes=MIB),
        cost_estimate=pl.CostEstimate(flops=1000, transcendentals=0, bytes_accessed=1000),
        name="adapters",
    )(info, *(in_hbm(a) for a in arrays))


def move_rows(kernel, value, slots, name, outs, in_space, out_space, sems):
    return pl.pallas_call(
        kernel,
        in_specs=[pl.BlockSpec(memory_space=pltpu.SMEM), pl.BlockSpec(memory_space=in_space)],
        out_specs=[pl.BlockSpec(memory_space=out_space)] * len(outs),
        out_shape=outs,
        scratch_shapes=[pltpu.SemaphoreType.DMA(sems)],
        compiler_params=pltpu.CompilerParams(vmem_limit_bytes=MIB),
        cost_estimate=pl.CostEstimate(flops=1000, transcendentals=0, bytes_accessed=1000),
        name=name,
    )(slots, pltpu.with_memory_space_constraint(value, in_space))


def sds(shape, dtype):
    return jax.ShapeDtypeStruct(tuple(shape), dtype)


def in_vmem(value):
    return pltpu.with_memory_space_constraint(value, pltpu.VMEM)


def in_hbm(value):
    return pltpu.with_memory_space_constraint(value, pltpu.HBM)


def call(kernel, info, weights, args, outs, scratch, name, mib, after=(), sems=()):
    vmem = pl.BlockSpec(memory_space=pltpu.VMEM)
    scalars = () if info is None else (info,)
    n, w = len(scalars), len(weights)

    def body(*refs):
        at = n + w + len(args)
        kernel(*refs[:at], *refs[at + len(after):])

    return pl.pallas_call(
        body,
        in_specs=[pl.BlockSpec(memory_space=pltpu.SMEM)] * n + [pl.BlockSpec(memory_space=pltpu.HBM)] * w + [vmem] * len(args)
        + [pl.BlockSpec(memory_space=pl.ANY)] * len(after),
        out_specs=[vmem] * len(outs),
        out_shape=[pltpu.VMEM(tuple(s), d) for s, d in outs],
        scratch_shapes=[pltpu.VMEM(s, d) for s, d in scratch] + ([pltpu.SemaphoreType.DMA(sems)] if sems else []),
        compiler_params=pltpu.CompilerParams(vmem_limit_bytes=mib * MIB),
        cost_estimate=pl.CostEstimate(flops=1000, transcendentals=0, bytes_accessed=1000),
        name=name,
    )(*scalars, *(in_hbm(a) for a in weights), *(in_vmem(a) for a in args), *after)


def whole_spec(value):
    zeros = (0,) * value.ndim
    return pl.BlockSpec(value.shape, lambda i, *_: zeros)


def sum_call(kernel, scalars, groups, outs, name):
    args = [v for group in groups for v in group]
    steps = 2
    specs = [pl.BlockSpec((o.shape[0] // steps,) + o.shape[1:], (lambda n: lambda i, *_: (i,) + (0,) * n)(o.ndim - 1))
             for o in outs]
    return pl.pallas_call(
        functools.partial(kernel, [len(group) for group in groups]),
        grid_spec=pltpu.PrefetchScalarGridSpec(
            num_scalar_prefetch=len(scalars), grid=(steps,),
            in_specs=[whole_spec(a) for a in args], out_specs=specs),
        out_shape=outs,
        compiler_params=pltpu.CompilerParams(
            dimension_semantics=("arbitrary",),
            vmem_limit_bytes=4 * MIB + 2 * sum(a.size * a.dtype.itemsize for a in args)
            + sum(o.size * o.dtype.itemsize for o in outs)),
        cost_estimate=pl.CostEstimate(flops=0, transcendentals=0, bytes_accessed=12000000),
        name=name,
    )(*scalars, *args)


def swap(value, bit, axis, size):
    return lax.ppermute(value, axis, [(i, i ^ bit) for i in range(size)])


def near(value):
    return swap(value, 1, "mp", PARTS)


def far(value):
    return swap(value, 2, "mp", PARTS)


def spread(value):
    there = far(value)
    return (value, near(value), there, near(there))


def far_sum_kernel(own, got, out):
    for to, other in ((LO, HI), (HI, LO)):
        out[:, to] = (own[:, to].astype(F32) + got[:, other].astype(F32)).astype(BF16)


def far_sum(own, got):
    return call(far_sum_kernel, None, (), (own, got), [(own.shape, BF16)], [], "far_sum", 6)[0]


def pair_sum_kernel(keep, got, out):
    out[...] = (keep[...] + got[...].astype(F32)).astype(BF16)


def pair_sum(keep, send, *before):
    got = near(send)
    got = late(got, *before) if before else got
    return call(pair_sum_kernel, None, (), (keep, got), [(send.shape, BF16)], [], "pair_sum", 6)[0]


def late(value, *others):
    return lax.optimization_barrier((value, *others))[0]


def doubled(stack, bit, size):
    return jnp.concatenate([stack, swap(stack, bit, "dp", size)], axis=0)


def entry_of(slot, place, size):
    bits = size.bit_length() - 1
    apart = slot ^ place
    return sum(((apart >> b) & 1) << (bits - 1 - b) for b in range(bits))


def shards(dp, residual, attention_gain, query_matrix, key_value_matrix, output_matrix, feedfwd_gain,
           gate_up_matrix, down_matrix, attention_adapter_input, query_adapter_output,
           key_value_adapter_output, output_adapter_input, output_adapter_output, feedfwd_adapter_input,
           feedfwd_adapter_output, down_adapter_input, down_adapter_output, lengths, adapter_index,
           dealing_slots, cotangent):
    seqs = residual.shape[0]
    length = cotangent.shape[1]
    units = down_matrix.shape[0]
    adapters = attention_adapter_input.shape[0]
    q_cols = query_matrix.shape[1]
    kv_cols = key_value_matrix.shape[2]
    kv_heads = kv_cols // HEAD
    heads = q_cols // HEAD
    rows = length // CHUNKS
    half = 2 * QUARTER
    me = lax.axis_index("mp")
    place = lax.axis_index("dp")

    is_there = dealing_slots[None, :] == jnp.arange(seqs, dtype=jnp.int32)[:, None]
    owners = jnp.sum(jnp.where(is_there, adapter_index[None, :], 0), axis=1)
    spans = jnp.sum(jnp.where(is_there, lengths[None, :], 0), axis=1)
    mine = jnp.arange(seqs, dtype=jnp.int32) == place
    my_length = jnp.sum(jnp.where(mine, spans, 0))
    my_adapter = jnp.sum(jnp.where(mine, owners, 0))
    info = jnp.stack([me.astype(jnp.int32), my_length, my_adapter, place.astype(jnp.int32)])

    gs = spread(cotangent[0])
    gains = jnp.stack(spread(jnp.stack([attention_gain, feedfwd_gain])))
    ordered, = move_rows(deal_kernel, residual, dealing_slots, "deal", [pltpu.VMEM(residual.shape, BF16)], pltpu.HBM,
                         pltpu.VMEM, (seqs,))
    dealt = lax.all_to_all(ordered, "dp", split_axis=0, concat_axis=1, tiled=True)[0]
    adapters_here = load_adapters(
        (attention_adapter_input, query_adapter_output, key_value_adapter_output, output_adapter_input,
         output_adapter_output, feedfwd_adapter_input, feedfwd_adapter_output, down_adapter_input,
         down_adapter_output), info)
    a1, qb, kvb, oa, ob, a2, fba, da, bd = adapters_here
    dealt = late(dealt, gs[2], a1, gains)
    beside = near(dealt)
    there = [far(dealt[c * rows:(c + 1) * rows]) for c in range(CHUNKS)]
    xs = [None] * CHUNKS
    cos_np, sin_np = rope_tables(length)
    cos = [jnp.asarray(cos_np[:, c * rows:(c + 1) * rows]) for c in range(CHUNKS)]
    sin = [jnp.asarray(sin_np[:, c * rows:(c + 1) * rows]) for c in range(CHUNKS)]
    wq, wkv, wo = query_matrix, key_value_matrix, output_matrix

    def like(*arrays):
        return [(a.shape, a.dtype) for a in arrays]

    wide, col, block, thin = (rows, WIDTH), (rows, half), (rows, QUARTER), (rows, 1)
    saved, kept, z_own, z_far = ([None] * CHUNKS for _ in range(4))
    order = ()
    for c in range(CHUNKS):
        xs[c] = (dealt, beside, there[c], near(late(there[c], saved[0][0]) if c else there[c]))
        outs = [((3 * RANK, rows), BF16), ((q_cols, rows), BF16), ((kv_heads, rows, HEAD), BF16),
                ((kv_heads, rows, HEAD), BF16), ((kv_cols, rows), BF16), ((kv_cols, rows), BF16)]
        saved[c] = call(
            functools.partial(project_kernel, c), info, (wq, wkv), (*xs[c], gains, a1, qb, kvb, cos[c], sin[c]), outs,
            [(wide, BF16)] + like(wq, wkv), "project_%d" % c, 12, order, (2,))
        outs = [(col, F32), (col, BF16), ((q_cols, rows), BF16), ((heads, rows), F32), ((RANK, rows), BF16)]
        pairs = [v for p in saved[:c + 1] for v in (p[2], p[5])]
        z_keep, z_send, *kept[c] = call(
            functools.partial(attend_kernel, c), info, (wo,), (saved[c][1], oa, ob, *pairs), outs, like(wo),
            "attend_%d" % c, 10, (saved[c][0],), (1,))
        z_own[c] = pair_sum(z_keep, late(z_send, z_far[0] if c else there[-1]))
        z_far[c] = far(z_own[c])
        order = (kept[c][1], z_own[c])
    def front(c, total, partial, order):
        hidden = (rows, units)
        outs = [(wide, BF16), (block, F32), (wide, BF16), (wide, BF16), (hidden, BF16), (hidden, BF16), (hidden, BF16),
                ((rows, 2 * RANK), BF16), ((rows, RANK), BF16),
                ((3 * RANK * units // QUARTER, QUARTER), BF16 if c else F32)]
        args = (*xs[c], total, near(total), *gs, gains, a2, bd, fba, da, *partial)
        weights = () if c else (gate_up_matrix, down_matrix)
        outs += like(*weights)
        return call(
            functools.partial(front_kernel, c, c == CHUNKS - 1), info, weights, (wgu, wd, *args) if c else args, outs,
            [((ROW_BLOCK, WIDTH), F32)], "front_%d" % c, 8, order, () if c else (2, units // QUARTER))

    def back(c, hidden, partial, order):
        first = col if c else (rows + 3 * RANK, half)
        outs = [((rows, RANK), F32), (first, F32), (first, BF16)]
        outs += [((3 * RANK, WIDTH), F32)] if c else []
        return call(
            functools.partial(back_kernel, c == 0), info, (), (wgu, *hidden[2:7], a2, fba, da, *partial), outs,
            [(block, F32), ((3 * RANK, QUARTER), F32)], "back_%d" % c, 8, order)

    def down(c, td, order):
        return call(down_kernel, info, (), (wd, hidden[c][4], td, bd, hidden[c][1]), [(col, F32), (col, BF16)],
                    [(block, F32)], "down_%d" % c, 6, order)

    def attend_back(c, total, partial, order):
        outs = [(block, F32), (col, F32), (col, BF16), (thin, F32), ((3 * RANK, QUARTER), F32 if c else BF16)]
        low = (4 * RANK + SPARE, half)
        outs += ([((4 * RANK, WIDTH), F32), ((kv_cols, rows), F32), ((kv_cols, rows), F32), ((SPARE // 2, rows), F32)]
                 if c else [(low, F32), (low, BF16)])
        scratch = [(wide, BF16), (wide, BF16), ((ROW_BLOCK, WIDTH), F32), ((q_cols, rows), BF16), ((q_cols, rows), F32),
                   ((c + 1, kv_cols, rows), F32), ((c + 1, kv_cols, rows), F32), ((rows, q_cols + 2 * kv_cols), BF16),
                   (block, F32), ((4 * RANK, QUARTER), F32)]
        triples = [v for p in saved[:c + 1] for v in (p[2], p[3], p[4])]
        return call(
            functools.partial(attend_back_kernel, c, c == 0), info, (wq, wkv, wo),
            (*xs[c], *gs, hidden[c][0], total, near(total), gains, a1, qb, kvb, oa, ob, cos[c], sin[c], *saved[c][:2],
             *kept[c], *triples, *partial), outs, scratch + like(wq, wkv, wo), "attend_back_%d" % c, 18, order, (3,))

    bits = [1 << b for b in reversed(range(dp.bit_length() - 1))]
    def to_bands(value):
        return lax.all_to_all(value.reshape(dp, length // dp, QUARTER), "dp", split_axis=0, concat_axis=0, tiled=True)

    def collect(value, name, *before):
        rows_out = sds((seqs, length // dp, QUARTER), BF16)
        return move_rows(collect_kernel, value, late(dealing_slots, *before), name, [rows_out], pltpu.VMEM, pl.ANY,
                         (seqs,))[0]

    hidden, d_own, d_far, y_keep, y_got = ([None] * CHUNKS for _ in range(5))
    *hidden[0], wgu, wd = front(0, far_sum(z_own[0], z_far[0]), (), order)
    step = hidden[0][8]
    hidden[1] = front(1, far_sum(z_own[1], late(z_far[1], step)), hidden[0][9:], (step,))
    fb = hidden[1][9][None]
    fb_first = swap(fb, bits[0], "dp", dp)
    td, d_keep, d_send, fa = back(1, hidden[1], (), (hidden[1][8],))
    d_own[1] = pair_sum(d_keep, late(d_send, fb_first))
    d_far[1] = far(d_own[1])
    fb = fb_more = jnp.concatenate([fb, fb_first], axis=0)
    for bit in bits[1:-1]:
        fb_more = doubled(fb_more, bit, dp)
    fb_more = fb_more[2:]
    fb_side = swap(fb, bits[-1], "dp", dp)
    td_0, d_keep, d_send = back(0, hidden[0], (fa,), (d_own[1],))
    total = far_sum(d_own[1], late(d_far[1], td_0))
    d_own[0] = pair_sum(d_keep, late(d_send, fb_more, fb_side), total)
    d_far[0] = far(d_own[0])
    fb_more_side = swap(fb_more, bits[-1], "dp", dp)
    dxq, h_keep, h_send, inv, *sums = attend_back(1, total, (), (d_own[0],))
    y_keep[1], y_send = down(1, td, (inv,))
    total = far_sum(d_own[0], late(d_far[0], inv))
    h_got = near(late(h_send, fb_more_side))
    h_high = high_sum((h_keep, h_got))
    h_far = far(h_high)
    final = [None, (dxq, h_keep, h_got, h_far, inv)]
    fa = total[rows:][None]
    fa_first = swap(fa, bits[0], "dp", dp)
    dxq, h_keep, h_send, inv, att_b, aa_keep, aa_send = attend_back(0, total, sums, (h_high, y_send))
    y_got[1] = near(late(y_send, inv))
    ready = (fa_first, h_far)
    aa_got = near(late(aa_send, *ready))
    aa_high = high_sum((aa_keep, aa_got))
    aa_far = far(aa_high)
    h_got = near(late(h_send, *ready))
    h_high = high_sum((h_keep, h_got))
    h_far = far(h_high)
    final[0] = (dxq, h_keep, h_got, h_far, inv)
    att_a = aa_keep[:4 * RANK, :QUARTER] + aa_got[:4 * RANK, :QUARTER].astype(F32)
    att_a = (att_a + late(aa_far, h_high)[:4 * RANK].astype(F32)).astype(BF16)
    n_b = att_b.shape[0]
    att = jnp.concatenate([att_b, att_a], axis=0)[None]
    y_keep[0], y_send = down(0, td_0, (att,))
    y_got[0] = near(y_send)
    att = first = doubled(att, bits[0], dp)
    att = late(att, h_far, y_send)
    for bit in bits[1:-1]:
        att = doubled(att, bit, dp)
    fa = late(jnp.concatenate([fa, fa_first], axis=0), aa_high)
    for bit in bits[1:-1]:
        fa = doubled(fa, bit, dp)
    fa_side = swap(fa, bits[-1], "dp", dp)

    dinput, = call(finish_kernel, None, (), (gains, dealt, aa_high, aa_far, *(v for f in final for v in f)),
                   [((length, QUARTER), BF16)], [], "finish", 8, (y_send, first, fa))
    y_far = far(high_sum(*((k, late(g, dinput)) for k, g in zip(y_keep, y_got))))
    input_grad = collect(to_bands(dinput), "collect_grad")
    result, = call(output_kernel, info, (), (y_far, *(v for p in zip(y_keep, y_got) for v in p)),
                   [((length, QUARTER), BF16)], [], "output", 8)
    output = collect(to_bands(result), "collect_out", input_grad)

    outs = [sds((adapters, 2 * RANK, WIDTH), F32), sds((adapters, RANK, WIDTH), F32),
            sds((adapters, 2, RANK, units), F32), sds((adapters, RANK, units), F32)]
    ga_ffn, g_down_b, g_ffn_b, g_down_a = sum_call(
        feedforward_sum_kernel, (info, owners),
        ((fb, fb_more, fb_side, fb_more_side), (fa, fa_side), (near(fa), near(fa_side))), outs, "feedforward_sum")

    att_side = swap(att, bits[-1], "dp", dp)
    a_parts = [att[:, n_b:], att_side[:, n_b:]]
    a_far = [far(v) for v in a_parts]
    a_far[1] = late(a_far[1], g_down_a)
    outs = [sds((adapters, 3 * RANK, WIDTH), F32), sds((adapters, RANK, WIDTH), F32),
            sds((adapters, RANK, q_cols), F32), sds((adapters, 2, RANK, kv_cols), F32),
            sds((adapters, RANK, q_cols), F32)]
    ga_att, g_out_b, g_query_b, g_kv_b, g_out_a = sum_call(
        attention_sum_kernel, (info, owners),
        ((att, att_side), a_parts, [near(v) for v in a_parts], a_far, [near(v) for v in a_far]), outs, "attention_sum")
    return (output, input_grad, ga_att, g_query_b, g_kv_b, g_out_a, g_out_b, ga_ffn, g_ffn_b, g_down_a, g_down_b)


def solution(mesh):
    in_specs = (
        P(None, "dp", "mp"), P("mp"), P(None, "mp"), P(None, None, "mp"), P("mp", None), P("mp"),
        P(None, None, "mp"), P("mp", None), P(), P(None, None, "mp"), P(None, None, None, "mp"),
        P(None, None, "mp"), P(), P(), P(None, None, None, "mp"), P(None, None, "mp"), P(), P(), P(), P(),
        P("dp", None, "mp"),
    )
    out_specs = (
        P(None, "dp", "mp"), P(None, "dp", "mp"), P(), P(None, None, "mp"), P(None, None, None, "mp"),
        P(None, None, "mp"), P(), P(), P(None, None, None, "mp"), P(None, None, "mp"), P(),
    )
    return jax.shard_map(
        functools.partial(shards, mesh.shape["dp"]), mesh=mesh, in_specs=in_specs, out_specs=out_specs,
        check_vma=False)
```

```python
import functools

import jax
import jax.numpy as jnp
import numpy as np
from jax import lax
from jax.experimental import pallas as pl
from jax.experimental.pallas import tpu as pltpu
from jax.sharding import PartitionSpec as P

WIDTH = 2048
HEAD = 64
HALF = HEAD // 2
RANK = 16
EPS = 1e-05
ROPE_BASE = 500000.0
NEG_FILL = -1e30
PARTS = 4
LANES = 128
SPARE = 32
ROW_BLOCK = 64
QUARTER = WIDTH // PARTS
CHUNKS = 2
MIB = 1024 * 1024
F32 = jnp.float32
BF16 = jnp.bfloat16


def nn(a, b):
    return lax.dot_general(a, b, (((1,), (0,)), ((), ())), preferred_element_type=F32)


def nt(a, b):
    return lax.dot_general(a, b, (((1,), (1,)), ((), ())), preferred_element_type=F32)


def rope_tables(length):
    freq = ROPE_BASE ** (-np.arange(HALF, dtype=np.float32) * np.float32(2.0 / HEAD))
    angles = (np.arange(length, dtype=np.float32)[None, :] * freq.astype(np.float32)[:, None]).astype(np.float32)
    return np.cos(angles).astype(np.float32), np.sin(angles).astype(np.float32)


def quarter(me, rel):
    return pl.ds(pl.multiple_of((me ^ rel) * QUARTER, QUARTER), QUARTER)


LO, HI = slice(0, QUARTER), slice(QUARTER, 2 * QUARTER)


def total_block(rel, rows_at, own, oth):
    return (own if rel in (0, 2) else oth)[rows_at, LO if rel in (0, 1) else HI].astype(F32)


def store_block(rel, value, rows_at, keep_ref, send_ref):
    to = pl.ds(pl.multiple_of((rel // 2) * QUARTER, QUARTER), QUARTER)

    @pl.when(rel % 2 == 0)
    def _():
        keep_ref[rows_at, to] = value[...]

    @pl.when(rel % 2 == 1)
    def _():
        send_ref[rows_at, to] = value[...].astype(BF16)


def chunk_of(ref, chunk, rows):
    return ref if ref.shape[0] == rows else ref.at[chunk * rows:(chunk + 1) * rows]


def row_block(i):
    return pl.ds(pl.multiple_of(i * ROW_BLOCK, ROW_BLOCK), ROW_BLOCK)


def is_valid(chunk, i, rows, length):
    return chunk * rows + i * ROW_BLOCK + lax.broadcasted_iota(jnp.int32, (ROW_BLOCK, 1), 0) < length


def copies_of(pairs, sems):
    made = [pltpu.make_async_copy(source, target, sems.at[i]) for i, (source, target) in enumerate(pairs)]
    for copy in made:
        copy.start()
    return made


def put_block(rel, value, keep_ref, send_ref):
    ref = keep_ref if rel in (0, 2) else send_ref
    ref[:, LO if rel in (0, 1) else HI] = value.astype(ref.dtype)


def rotate(value, cos, sin, out_ref):
    for i in range(value.shape[0] // HEAD):
        u1, u2 = value[i * HEAD:i * HEAD + HALF], value[i * HEAD + HALF:(i + 1) * HEAD]
        out_ref[i * HEAD:i * HEAD + HALF, :] = (u1 * cos - u2 * sin).astype(BF16)
        out_ref[i * HEAD + HALF:(i + 1) * HEAD, :] = (u2 * cos + u1 * sin).astype(BF16)


def turn_back(value, cos, sin, out_ref):
    for i in range(value.shape[0] // HEAD):
        w1, w2 = value[i * HEAD:i * HEAD + HALF], value[i * HEAD + HALF:(i + 1) * HEAD]
        out_ref[i * HEAD:i * HEAD + HALF, :] = (w1 * cos + w2 * sin).astype(BF16)
        out_ref[i * HEAD + HALF:(i + 1) * HEAD, :] = (w2 * cos - w1 * sin).astype(BF16)


def head_rows(i):
    return pl.ds(pl.multiple_of(i * HEAD, HEAD), HEAD)


def visible(key_start, query_start, rows, length):
    kpos = key_start + lax.broadcasted_iota(jnp.int32, (rows, rows), 0)
    qpos = query_start + lax.broadcasted_iota(jnp.int32, (rows, rows), 1)
    return (kpos <= qpos) & (kpos < length)


def project_kernel(chunk, info, wq_h, wkv_h, x0, x1, x2, x3, gains, a1, qb, kvb, cos_t, sin_t,
                   t1t_out, qt_out, kn_out, vn_out, kt_out, vt_out, h_out, wq, wkv, sems):
    copies = copies_of(((wkv_h, wkv), (wq_h, wq)), sems)
    me = info[0]
    rows = h_out.shape[0]
    kv_heads = kn_out.shape[0]
    xs = [chunk_of(x, chunk, rows) for x in (x0, x1, x2, x3)]

    def norm(i, carry):
        at = row_block(i)
        square = jnp.zeros((ROW_BLOCK, 1), F32)
        for r in range(PARTS):
            v = xs[r][at, :].astype(F32)
            square = square + jnp.sum(v * v, axis=1, keepdims=True)
        inv = lax.rsqrt(square / WIDTH + EPS)
        for r in range(PARTS):
            v = xs[r][at, :].astype(F32)
            h_out[at, quarter(me, r)] = (v * inv * gains[r, 0:1, :].astype(F32)).astype(BF16)
        return carry

    lax.fori_loop(0, rows // ROW_BLOCK, norm, 0)
    h = h_out[...]
    t1 = nt(h, a1[...])
    t1t_out[...] = t1.T.astype(BF16)
    t1b = t1.astype(BF16)
    cos, sin = cos_t[...], sin_t[...]
    copies[0].wait()
    k = nn(h, wkv[0]) + nn(t1b[:, RANK:2 * RANK], kvb[0])
    rotate(k.T, cos, sin, kt_out)
    k_n = kt_out[...].T
    v_n = (nn(h, wkv[1]) + nn(t1b[:, 2 * RANK:], kvb[1])).astype(BF16)
    vt_out[...] = v_n.T
    for i in range(kv_heads):
        kn_out[i] = k_n[:, i * HEAD:(i + 1) * HEAD]
        vn_out[i] = v_n[:, i * HEAD:(i + 1) * HEAD]
    copies[1].wait()
    q = nn(h, wq[...]) + nn(t1b[:, :RANK], qb[...])
    rotate(q.T * (HEAD ** -0.5), cos, sin, qt_out)


def attend_kernel(chunk, info, wo_h, qt, oa, ob, *rest):
    pairs, rest = rest[:2 * (chunk + 1)], rest[2 * (chunk + 1):]
    z_keep, z_send, ot_out, lse_out, tot_out, wo, sems = rest
    copies = copies_of(((wo_h, wo),), sems)
    keys, values = pairs[0::2], pairs[1::2]
    me, length = info[0], info[1]
    rows = qt.shape[1]
    kv_heads = keys[0].shape[0]
    heads = qt.shape[0] // HEAD
    group = heads // kv_heads

    kept = [jnp.concatenate([visible(c * rows, chunk * rows, rows, length)] * group, axis=1) for c in range(chunk + 1)]

    def one_group(j, carry):
        q_g = jnp.concatenate([qt[head_rows(j * group + g), :] for g in range(group)], axis=1)
        parts = [jnp.where(kept[c], nn(keys[c][j], q_g), NEG_FILL) for c in range(chunk + 1)]
        top = functools.reduce(jnp.maximum, [jnp.max(s, axis=0, keepdims=True) for s in parts])
        es = [jnp.exp(s - top) for s in parts]
        total = sum(jnp.sum(e, axis=0, keepdims=True) for e in es)
        low = top + jnp.log(total)
        o_t = sum(nn(value[head_rows(j), :], e.astype(BF16)) for value, e in zip(values, es))
        o_t = (o_t / total).astype(BF16)
        for g in range(group):
            cols = slice(g * rows, (g + 1) * rows)
            lse_out[pl.ds(j * group + g, 1), :] = low[:, cols]
            ot_out[head_rows(j * group + g), :] = o_t[:, cols]
        return carry

    lax.fori_loop(0, kv_heads, one_group, 0)
    o = ot_out[...].T
    to = nt(o, oa[...])
    tot_out[...] = to.T.astype(BF16)
    to = to.astype(BF16)
    copies[0].wait()
    for r in range(PARTS):
        at = quarter(me, r)
        put_block(r, nn(o, wo[:, at]) + nn(to, ob[:, at]), z_keep, z_send)


def front_kernel(chunk, last, info, wgu_in, wd_in, x0, x1, x2, x3, zo, zp, g0, g1, g2, g3, gains, a2, bd, fb, da,
                 *rest):
    units = wd_in.shape[0]
    if chunk:
        wgu, wd = wgu_in, wd_in
    else:
        (wgu, wd, f_s, sems), rest = rest[-4:], rest[:-4]
        rest = (*rest, f_s)

    def copies(i):
        c = pl.ds(pl.multiple_of(i * QUARTER, QUARTER), QUARTER)
        return (pltpu.make_async_copy(wgu_in.at[:, :, c], wgu.at[:, :, c], sems.at[0, i]),
                pltpu.make_async_copy(wd_in.at[c, :], wd.at[c, :], sems.at[1, i]))

    if not chunk:
        for i in range(units // QUARTER):
            for copy in copies(i):
                copy.start()
    f_s = rest[-1]
    xm_out, xq_out, h_out, g_out, act_out, dg_out, du_out, t2_s, dtd_s, b_out = rest[-11:-1]
    me, length = info[0], info[1]
    rows = h_out.shape[0]
    xs, gs = ([chunk_of(v, chunk, rows) for v in vs] for vs in ((x0, x1, x2, x3), (g0, g1, g2, g3)))

    def norm(i, carry):
        at = row_block(i)
        valid = is_valid(chunk, i, rows, length)
        square = jnp.zeros((ROW_BLOCK, 1), F32)
        for r in range(PARTS):
            v = xs[r][at, :].astype(F32) + total_block(r, at, zo, zp)
            if r == 0:
                xq_out[at, :] = v
            f_s[:, quarter(me, r)] = v
            square = square + jnp.sum(v * v, axis=1, keepdims=True)
            g_out[at, quarter(me, r)] = jnp.where(valid, gs[r][at, :], jnp.zeros((), BF16))
        inv = lax.rsqrt(square / WIDTH + EPS)
        for r in range(PARTS):
            v = f_s[:, quarter(me, r)]
            xm_out[at, quarter(me, r)] = v.astype(BF16)
            h_out[at, quarter(me, r)] = (v * inv * gains[r, 1:2, :].astype(F32)).astype(BF16)
        return carry

    lax.fori_loop(0, rows // ROW_BLOCK, norm, 0)
    t2 = nt(h_out[...], a2[...])
    t2_s[...] = t2.astype(BF16)
    dtd = nt(g_out[...], bd[...])
    dtd_s[...] = dtd.astype(BF16)
    t2t, dtdt = t2.T.astype(BF16), dtd.T.astype(BF16)

    def block(i, carry):
        c = pl.ds(pl.multiple_of(i * QUARTER, QUARTER), QUARTER)
        if not chunk:
            for copy in copies(i):
                copy.wait()
        h, g = h_out[...], g_out[...]
        gate = nn(h, wgu[0, :, c]) + nn(t2_s[:, :RANK], fb[0, :, c])
        up = nn(h, wgu[1, :, c]) + nn(t2_s[:, RANK:], fb[1, :, c])
        dact = nt(g, wd[c, :]) + nn(dtd_s[...], da[:, c])
        sig = 1.0 / (1.0 + jnp.exp(-gate))
        silu = gate * sig
        act = (silu * up).astype(BF16)
        dgate = (dact * up * sig * (1.0 + gate * (1.0 - sig))).astype(BF16)
        dup = (dact * silu).astype(BF16)
        act_out[:, c], dg_out[:, c], du_out[:, c] = act, dgate, dup
        for k, value in enumerate((nn(t2t[:RANK], dgate), nn(t2t[RANK:], dup), nn(dtdt, act))):
            at = pl.ds(pl.multiple_of((3 * i + k) * RANK, RANK), RANK)
            if last:
                value = value + rest[0][at, :]
            b_out[at, :] = value.astype(b_out.dtype)
        return carry

    lax.fori_loop(0, units // QUARTER, block, 0)


def back_kernel(last, info, wgu, h, g, act, dg, du, a2, fb, da, *rest):
    (value_s, low_s), rest = rest[-2:], rest[:-2]
    outs, rest = (rest[-3:], rest[:-3]) if last else (rest[-4:], rest[:-4])
    td_out, d_keep, d_send = outs[:3]
    me = info[0]
    rows = h.shape[0]
    dt2 = jnp.concatenate([nt(dg[...], fb[0]), nt(du[...], fb[1])], axis=1)
    td = nt(act[...], da[...])
    td_out[...] = td
    dt2b = dt2.astype(BF16)
    dt2t, tdt = dt2.T.astype(BF16), td.T.astype(BF16)

    def block(r, carry):
        at = quarter(me, r)
        value_s[...] = nt(dg[...], wgu[0, at, :]) + nt(du[...], wgu[1, at, :]) + nn(dt2b, a2[:, at])
        store_block(r, value_s, slice(0, rows), d_keep, d_send)
        low_s[:2 * RANK, :] = nn(dt2t, h[:, at])
        low_s[2 * RANK:, :] = nn(tdt, g[:, at])
        if last:
            low_s[...] += rest[0][:, at]
            store_block(r, low_s, slice(rows, rows + 3 * RANK), d_keep, d_send)
        else:
            outs[3][:, at] = low_s[...]
        return carry

    lax.fori_loop(0, PARTS, block, 0)


def down_kernel(info, wd, act, td, bd, xq, y_keep, y_send, value_s):
    me = info[0]
    tdb = td[...].astype(BF16)

    def block(r, carry):
        at = quarter(me, r)
        value_s[...] = nn(act[...], wd[:, at]) + nn(tdb, bd[:, at])
        store_block(r, value_s, slice(0, act.shape[0]), y_keep, y_send)
        return carry

    lax.fori_loop(0, PARTS, block, 0)
    y_keep[:, LO] += xq[...]


def attend_back_kernel(chunk, last, info, wq_h, wkv_h, wo_h, x0, x1, x2, x3, g0, g1, g2, g3, xm, do_, dp, gains, a1,
                       qb, kvb, oa, ob, cos_t, sin_t, t1t, qt, ot, lse, tot, *rest):
    scratch, rest = rest[-14:], rest[:-14]
    h_in, z_s, f_s, dot_s, dqt_s, dkt_s, dvt_s, dq_s, value_s, low_s, wq, wkv, wo, sems = scratch
    copies = copies_of(((wo_h, wo), (wq_h, wq), (wkv_h, wkv)), sems)
    n_out = 7 if last else 9
    outs, rest = rest[-n_out:], rest[:-n_out]
    dxq_out, h_keep, h_send, inv_out, b_out = outs[:5]
    triples, rest = rest[:3 * (chunk + 1)], rest[3 * (chunk + 1):]
    keys, values, keys_t = triples[0::3], triples[1::3], triples[2::3]
    me, length = info[0], info[1]
    rows = xm.shape[0]
    kv_heads = keys[0].shape[0]
    heads = qt.shape[0] // HEAD
    group = heads // kv_heads
    q_cols, kv_cols = heads * HEAD, kv_heads * HEAD
    xs, gs = ([chunk_of(v, chunk, rows) for v in vs] for vs in ((x0, x1, x2, x3), (g0, g1, g2, g3)))

    def norm_back(i, carry):
        at = row_block(i)
        valid = is_valid(chunk, i, rows, length)
        square, first, inner = (jnp.zeros((ROW_BLOCK, 1), F32) for _ in range(3))
        for r in range(PARTS):
            v = xm[at, quarter(me, r)].astype(F32)
            square = square + jnp.sum(v * v, axis=1, keepdims=True)
            w = total_block(r, at, do_, dp) * gains[r, 1:2, :].astype(F32)
            f_s[:, quarter(me, r)] = w
            inner = inner + jnp.sum(v * w, axis=1, keepdims=True)
            u = xs[r][at, :].astype(F32)
            first = first + jnp.sum(u * u, axis=1, keepdims=True)
        inv_one = lax.rsqrt(first / WIDTH + EPS)
        inv_out[at, :] = inv_one
        inv = lax.rsqrt(square / WIDTH + EPS)
        back = inv * inv * inv * inner / WIDTH
        for r in range(PARTS):
            v = xm[at, quarter(me, r)].astype(F32)
            g = jnp.where(valid, gs[r][at, :].astype(F32), 0.0)
            d = g + inv * f_s[:, quarter(me, r)] - v * back
            if r == 0:
                dxq_out[at, :] = d
            z_s[at, quarter(me, r)] = d.astype(BF16)
            u = xs[r][at, :].astype(F32)
            h_in[at, quarter(me, r)] = (u * inv_one * gains[r, 0:1, :].astype(F32)).astype(BF16)
        return carry

    lax.fori_loop(0, rows // ROW_BLOCK, norm_back, 0)
    dz = z_s[...]
    dto = nt(dz, ob[...])
    copies[0].wait()
    d_o = nt(dz, wo[...]) + nn(dto.astype(BF16), oa[...])
    dot_s[...] = d_o.T.astype(BF16)
    kept = [jnp.concatenate([visible(c * rows, chunk * rows, rows, length)] * group, axis=1) for c in range(chunk + 1)]

    def one_group(j, carry):
        places = [head_rows(j * group + g) for g in range(group)]
        q_g = jnp.concatenate([qt[at, :] for at in places], axis=1)
        do_g = jnp.concatenate([dot_s[at, :] for at in places], axis=1)
        o_g = jnp.concatenate([ot[at, :] for at in places], axis=1)
        low = jnp.concatenate([lse[pl.ds(j * group + g, 1), :] for g in range(group)], axis=1)
        dots = jnp.sum(do_g.astype(F32) * o_g.astype(F32), axis=0, keepdims=True)
        dq_g = 0.0
        for c in range(chunk + 1):
            prob = jnp.where(kept[c], jnp.exp(nn(keys[c][j], q_g) - low), 0.0)
            ds = (prob * (nn(values[c][j], do_g) - dots)).astype(BF16)
            dq_g = dq_g + nn(keys_t[c][head_rows(j), :], ds)
            dk, dv = nt(q_g, ds), nt(do_g, prob.astype(BF16))
            if last:
                dk, dv = dk + rest[2][head_rows(j), :], dv + rest[3][head_rows(j), :]
            dkt_s[c, head_rows(j), :], dvt_s[c, head_rows(j), :] = dk, dv
        for g in range(group):
            dqt_s[places[g], :] = dq_g[:, g * rows:(g + 1) * rows]
        return carry

    lax.fori_loop(0, kv_heads, one_group, 0)
    if not last:
        outs[6][...], outs[7][...] = dkt_s[0], dvt_s[0]
    cos, sin = cos_t[...], sin_t[...]
    dto_t, o_t = dto.T.astype(BF16), ot[...]
    d_out_a = nt(dto_t, o_t)
    turn_back(dqt_s[...], cos * (HEAD ** -0.5), sin * (HEAD ** -0.5), dot_s)
    dq_s[:, :q_cols] = dot_s[...].T
    turn_back(dkt_s[chunk], cos, sin, dot_s)
    dq_s[:, q_cols:q_cols + kv_cols] = dot_s[:kv_cols, :].T
    dq_s[:, q_cols + kv_cols:] = dvt_s[chunk].T.astype(BF16)
    dq, dk, dv = dq_s[:, :q_cols], dq_s[:, q_cols:q_cols + kv_cols], dq_s[:, q_cols + kv_cols:]
    dt1 = jnp.concatenate([nt(dq, qb[...]), nt(dk, kvb[0]), nt(dv, kvb[1])], axis=1)
    dt1b = dt1.astype(BF16)
    kv_pad = jnp.zeros((RANK, QUARTER - 2 * kv_cols), F32)
    d_kv = jnp.concatenate([nn(t1t[RANK:2 * RANK, :], dk), nn(t1t[2 * RANK:, :], dv), kv_pad], axis=1)
    for k, value in enumerate((nn(t1t[:RANK, :], dq), d_out_a, d_kv)):
        at = slice(k * RANK, (k + 1) * RANK)
        if last:
            value = value + rest[0][at, :]
        b_out[at, :] = value.astype(b_out.dtype)
    dt1t = dt1.T.astype(BF16)
    copies[1].wait()
    copies[2].wait()

    def block(r, inner):
        at = quarter(me, r)
        d = nt(dq_s[:, :q_cols], wq[at, :]) + nn(dt1b, a1[:, at])
        d = d + nt(dq_s[:, q_cols:q_cols + kv_cols], wkv[0, at, :]) + nt(dq_s[:, q_cols + kv_cols:], wkv[1, at, :])
        value_s[...] = d
        store_block(r, value_s, slice(0, rows), h_keep, h_send)
        low_s[:3 * RANK, :] = nn(dt1t, h_in[:, at])
        low_s[3 * RANK:, :] = nn(tot[...], z_s[:, at])
        if last:
            low_s[...] += rest[1][:, at]
            store_block(r, low_s, slice(0, 4 * RANK), outs[5], outs[6])
        else:
            outs[5][:, at] = low_s[...]
        return inner + jnp.sum(d * h_in[:, at].astype(F32), axis=1, keepdims=True)

    inner = lax.fori_loop(0, PARTS, block, jnp.zeros((rows, 1), F32))
    inner = jnp.broadcast_to(inner, (rows, LANES)).T[:SPARE // 2, :]
    if last:
        for ref in outs[5:7]:
            for c, value in enumerate((inner, rest[4][...])):
                at = slice(4 * RANK + c * SPARE // 2, 4 * RANK + (c + 1) * SPARE // 2)
                ref[at, QUARTER:QUARTER + rows] = value.astype(ref.dtype)
                ref[at, QUARTER + rows:] = jnp.zeros((SPARE // 2, QUARTER - rows), ref.dtype)
                ref[at, :QUARTER] = jnp.zeros((SPARE // 2, QUARTER), ref.dtype)
    else:
        outs[8][...] = inner


def output_kernel(info, y_far, *refs):
    out = refs[-1]
    rows = out.shape[0] // CHUNKS
    for c in range(CHUNKS):
        y_keep, y_got = refs[2 * c:2 * (c + 1)]
        at = slice(c * rows, (c + 1) * rows)
        valid = c * rows + lax.broadcasted_iota(jnp.int32, (rows, 1), 0) < info[1]
        y = y_keep[:, LO] + y_got[:, LO].astype(F32) + y_far[at, :].astype(F32)
        out[at, :] = jnp.where(valid, y, 0.0).astype(BF16)


def finish_kernel(gains, x_all, aa_high, aa_far, *refs):
    out = refs[-1]
    gain = gains[0, 0:1, :].astype(F32)
    rows = out.shape[0] // CHUNKS
    inner = aa_high[4 * RANK:, :].astype(F32) + aa_far[4 * RANK:, :].astype(F32)
    for c in range(CHUNKS):
        dx, keep, got, there, inv = refs[5 * c:5 * (c + 1)]
        x = chunk_of(x_all, c, rows)
        mine = inner[c * SPARE // 2:c * SPARE // 2 + 8, :rows].T[:, 0:1]
        inv = inv[...]
        grad = keep[:, LO] + got[:, LO].astype(F32) + there[...].astype(F32)
        grad = inv * (gain * grad) - x[...].astype(F32) * (inv * inv * mine / WIDTH)
        out[c * rows:(c + 1) * rows, :] = (dx[...] + grad).astype(BF16)


def high_sum_kernel(*refs):
    out = refs[-1]
    rows = out.shape[0] // (len(refs) // 2)
    for c in range(len(refs) // 2):
        keep, got = refs[2 * c:2 * c + 2]
        out[c * rows:(c + 1) * rows, :] = (keep[:, HI] + got[:, HI].astype(F32)).astype(BF16)


def high_sum(*pairs):
    args = [v for pair in pairs for v in pair]
    rows = sum(keep.shape[0] for keep, _ in pairs)
    return call(high_sum_kernel, None, (), args, [((rows, QUARTER), BF16)], [], "high_sum", 8)[0]


def split_refs(refs, counts):
    groups = []
    for count in counts:
        groups.append(refs[:count])
        refs = refs[count:]
    return groups, refs


def with_entry(parts, at, use):
    start = 0
    for ref in parts:
        @pl.when((at >= start) & (at < start + ref.shape[0]))
        def _(ref=ref, start=start):
            use(ref, at - start)
        start += ref.shape[0]


def sum_slots(info, owners, out_refs, one_slot):
    count = out_refs[0].shape[0]
    base = pl.program_id(0) * count
    slots = owners.shape[0]
    for ref in out_refs:
        ref[...] = jnp.zeros_like(ref)

    def add(slot, carry):
        owner = owners[slot] - base

        @pl.when((owner >= 0) & (owner < count))
        def _():
            one_slot(owner, entry_of(slot, info[3], slots))
        return carry

    lax.fori_loop(0, slots, add, 0)


def feedforward_sum_kernel(counts, info, owners, *refs):
    (b_parts, *a_parts), outs = split_refs(refs, counts)
    ga, gdb, gb, gda = outs
    me = info[0]

    def one_slot(owner, at):
        def add_b(ref, e):
            for i in range(gda.shape[2] // QUARTER):
                cols = slice(i * QUARTER, (i + 1) * QUARTER)
                base = i * 3 * RANK
                gb[owner, 0, :, cols] += ref[e, base:base + RANK, :].astype(F32)
                gb[owner, 1, :, cols] += ref[e, base + RANK:base + 2 * RANK, :].astype(F32)
                gda[owner, :, cols] += ref[e, base + 2 * RANK:base + 3 * RANK, :].astype(F32)

        with_entry(b_parts, at, add_b)
        for near_bit, parts in enumerate(a_parts):
            def add_a(ref, e, near_bit=near_bit):
                for r, cols in ((near_bit, LO), (near_bit ^ 2, HI)):
                    ga[owner, :, quarter(me, r)] += ref[e, :2 * RANK, cols].astype(F32)
                    gdb[owner, :, quarter(me, r)] += ref[e, 2 * RANK:, cols].astype(F32)

            with_entry(parts, at, add_a)

    sum_slots(info, owners, outs, one_slot)


def attention_sum_kernel(counts, info, owners, *refs):
    (b_parts, *a_parts), outs = split_refs(refs, counts)
    ga, gob, gq, gkv, goa = outs
    me = info[0]
    kv_cols = gkv.shape[3]

    def one_slot(owner, at):
        def add_b(ref, e):
            gq[owner] += ref[e, :RANK, :].astype(F32)
            goa[owner] += ref[e, RANK:2 * RANK, :].astype(F32)
            gkv[owner, 0] += ref[e, 2 * RANK:3 * RANK, :kv_cols].astype(F32)
            gkv[owner, 1] += ref[e, 2 * RANK:3 * RANK, kv_cols:2 * kv_cols].astype(F32)

        with_entry(b_parts, at, add_b)
        for r, parts in enumerate(a_parts):
            def add_a(ref, e, r=r):
                ga[owner, :, quarter(me, r)] += ref[e, :3 * RANK, :].astype(F32)
                gob[owner, :, quarter(me, r)] += ref[e, 3 * RANK:, :].astype(F32)

            with_entry(parts, at, add_a)

    sum_slots(info, owners, outs, one_slot)


def deal_kernel(slots, source, out, sems):
    made = [pltpu.make_async_copy(source.at[i], out.at[slots[i]], sems.at[i]) for i in range(source.shape[0])]
    for copy in made:
        copy.start()
    for copy in made:
        copy.wait()


def collect_kernel(slots, source, out, sems):
    made = [pltpu.make_async_copy(source.at[slots[i]], out.at[i], sems.at[i]) for i in range(source.shape[0])]
    for copy in made:
        copy.start()
    for copy in made:
        copy.wait()


def adapter_kernel(count, info, *refs):
    made = [pltpu.make_async_copy(refs[i].at[info[2]], refs[count + i], refs[-1].at[i]) for i in range(count)]
    for copy in made:
        copy.start()
    for copy in made:
        copy.wait()


def load_adapters(arrays, info):
    count = len(arrays)
    return pl.pallas_call(
        functools.partial(adapter_kernel, count),
        in_specs=[pl.BlockSpec(memory_space=pltpu.SMEM)] + [pl.BlockSpec(memory_space=pltpu.HBM)] * count,
        out_specs=[pl.BlockSpec(memory_space=pltpu.VMEM)] * count,
        out_shape=[pltpu.VMEM(a.shape[1:], a.dtype) for a in arrays],
        scratch_shapes=[pltpu.SemaphoreType.DMA((count,))],
        compiler_params=pltpu.CompilerParams(vmem_limit_bytes=MIB),
        cost_estimate=pl.CostEstimate(flops=1000, transcendentals=0, bytes_accessed=1000),
        name="adapters",
    )(info, *(in_hbm(a) for a in arrays))


def move_rows(kernel, value, slots, name, outs, in_space, out_space, sems):
    return pl.pallas_call(
        kernel,
        in_specs=[pl.BlockSpec(memory_space=pltpu.SMEM), pl.BlockSpec(memory_space=in_space)],
        out_specs=[pl.BlockSpec(memory_space=out_space)] * len(outs),
        out_shape=outs,
        scratch_shapes=[pltpu.SemaphoreType.DMA(sems)],
        compiler_params=pltpu.CompilerParams(vmem_limit_bytes=MIB),
        cost_estimate=pl.CostEstimate(flops=1000, transcendentals=0, bytes_accessed=1000),
        name=name,
    )(slots, pltpu.with_memory_space_constraint(value, in_space))


def sds(shape, dtype):
    return jax.ShapeDtypeStruct(tuple(shape), dtype)


def in_vmem(value):
    return pltpu.with_memory_space_constraint(value, pltpu.VMEM)


def in_hbm(value):
    return pltpu.with_memory_space_constraint(value, pltpu.HBM)


def call(kernel, info, weights, args, outs, scratch, name, mib, after=(), sems=()):
    vmem = pl.BlockSpec(memory_space=pltpu.VMEM)
    scalars = () if info is None else (info,)
    n, w = len(scalars), len(weights)

    def body(*refs):
        at = n + w + len(args)
        kernel(*refs[:at], *refs[at + len(after):])

    return pl.pallas_call(
        body,
        in_specs=[pl.BlockSpec(memory_space=pltpu.SMEM)] * n + [pl.BlockSpec(memory_space=pltpu.HBM)] * w + [vmem] * len(args)
        + [pl.BlockSpec(memory_space=pl.ANY)] * len(after),
        out_specs=[vmem] * len(outs),
        out_shape=[pltpu.VMEM(tuple(s), d) for s, d in outs],
        scratch_shapes=[pltpu.VMEM(s, d) for s, d in scratch] + ([pltpu.SemaphoreType.DMA(sems)] if sems else []),
        compiler_params=pltpu.CompilerParams(vmem_limit_bytes=mib * MIB),
        cost_estimate=pl.CostEstimate(flops=1000, transcendentals=0, bytes_accessed=1000),
        name=name,
    )(*scalars, *(in_hbm(a) for a in weights), *(in_vmem(a) for a in args), *after)


def whole_spec(value):
    zeros = (0,) * value.ndim
    return pl.BlockSpec(value.shape, lambda i, *_: zeros)


def sum_call(kernel, scalars, groups, outs, name):
    args = [v for group in groups for v in group]
    steps = 2
    specs = [pl.BlockSpec((o.shape[0] // steps,) + o.shape[1:], (lambda n: lambda i, *_: (i,) + (0,) * n)(o.ndim - 1))
             for o in outs]
    return pl.pallas_call(
        functools.partial(kernel, [len(group) for group in groups]),
        grid_spec=pltpu.PrefetchScalarGridSpec(
            num_scalar_prefetch=len(scalars), grid=(steps,),
            in_specs=[whole_spec(a) for a in args], out_specs=specs),
        out_shape=outs,
        compiler_params=pltpu.CompilerParams(
            dimension_semantics=("arbitrary",),
            vmem_limit_bytes=4 * MIB + 2 * sum(a.size * a.dtype.itemsize for a in args)
            + sum(o.size * o.dtype.itemsize for o in outs)),
        cost_estimate=pl.CostEstimate(flops=0, transcendentals=0, bytes_accessed=12000000),
        name=name,
    )(*scalars, *args)


def swap(value, bit, axis, size):
    return lax.ppermute(value, axis, [(i, i ^ bit) for i in range(size)])


def near(value):
    return swap(value, 1, "mp", PARTS)


def far(value):
    return swap(value, 2, "mp", PARTS)


def spread(value):
    there = far(value)
    return (value, near(value), there, near(there))


def far_sum_kernel(own, got, out):
    for to, other in ((LO, HI), (HI, LO)):
        out[:, to] = (own[:, to].astype(F32) + got[:, other].astype(F32)).astype(BF16)


def far_sum(own, got):
    return call(far_sum_kernel, None, (), (own, got), [(own.shape, BF16)], [], "far_sum", 6)[0]


def pair_sum_kernel(keep, got, out):
    out[...] = (keep[...] + got[...].astype(F32)).astype(BF16)


def pair_sum(keep, send, *before):
    got = near(send)
    got = late(got, *before) if before else got
    return call(pair_sum_kernel, None, (), (keep, got), [(send.shape, BF16)], [], "pair_sum", 6)[0]


def late(value, *others):
    return lax.optimization_barrier((value, *others))[0]


def doubled(stack, bit, size):
    return jnp.concatenate([stack, swap(stack, bit, "dp", size)], axis=0)


def entry_of(slot, place, size):
    bits = size.bit_length() - 1
    apart = slot ^ place
    return sum(((apart >> b) & 1) << (bits - 1 - b) for b in range(bits))


def shards(dp, residual, attention_gain, query_matrix, key_value_matrix, output_matrix, feedfwd_gain,
           gate_up_matrix, down_matrix, attention_adapter_input, query_adapter_output,
           key_value_adapter_output, output_adapter_input, output_adapter_output, feedfwd_adapter_input,
           feedfwd_adapter_output, down_adapter_input, down_adapter_output, lengths, adapter_index,
           dealing_slots, cotangent):
    seqs = residual.shape[0]
    length = cotangent.shape[1]
    units = down_matrix.shape[0]
    adapters = attention_adapter_input.shape[0]
    q_cols = query_matrix.shape[1]
    kv_cols = key_value_matrix.shape[2]
    kv_heads = kv_cols // HEAD
    heads = q_cols // HEAD
    rows = length // CHUNKS
    half = 2 * QUARTER
    me = lax.axis_index("mp")
    place = lax.axis_index("dp")

    is_there = dealing_slots[None, :] == jnp.arange(seqs, dtype=jnp.int32)[:, None]
    owners = jnp.sum(jnp.where(is_there, adapter_index[None, :], 0), axis=1)
    spans = jnp.sum(jnp.where(is_there, lengths[None, :], 0), axis=1)
    mine = jnp.arange(seqs, dtype=jnp.int32) == place
    my_length = jnp.sum(jnp.where(mine, spans, 0))
    my_adapter = jnp.sum(jnp.where(mine, owners, 0))
    info = jnp.stack([me.astype(jnp.int32), my_length, my_adapter, place.astype(jnp.int32)])

    gs = spread(cotangent[0])
    gains = jnp.stack(spread(jnp.stack([attention_gain, feedfwd_gain])))
    ordered, = move_rows(deal_kernel, residual, dealing_slots, "deal", [pltpu.VMEM(residual.shape, BF16)], pltpu.HBM,
                         pltpu.VMEM, (seqs,))
    dealt = lax.all_to_all(ordered, "dp", split_axis=0, concat_axis=1, tiled=True)[0]
    adapters_here = load_adapters(
        (attention_adapter_input, query_adapter_output, key_value_adapter_output, output_adapter_input,
         output_adapter_output, feedfwd_adapter_input, feedfwd_adapter_output, down_adapter_input,
         down_adapter_output), info)
    a1, qb, kvb, oa, ob, a2, fba, da, bd = adapters_here
    dealt = late(dealt, gs[2], a1, gains)
    beside = near(dealt)
    there = [far(dealt[c * rows:(c + 1) * rows]) for c in range(CHUNKS)]
    xs = [None] * CHUNKS
    cos_np, sin_np = rope_tables(length)
    cos = [jnp.asarray(cos_np[:, c * rows:(c + 1) * rows]) for c in range(CHUNKS)]
    sin = [jnp.asarray(sin_np[:, c * rows:(c + 1) * rows]) for c in range(CHUNKS)]
    wq, wkv, wo = query_matrix, key_value_matrix, output_matrix

    def like(*arrays):
        return [(a.shape, a.dtype) for a in arrays]

    wide, col, block, thin = (rows, WIDTH), (rows, half), (rows, QUARTER), (rows, 1)
    saved, kept, z_own, z_far = ([None] * CHUNKS for _ in range(4))
    order = ()
    for c in range(CHUNKS):
        xs[c] = (dealt, beside, there[c], near(late(there[c], saved[0][0]) if c else there[c]))
        outs = [((3 * RANK, rows), BF16), ((q_cols, rows), BF16), ((kv_heads, rows, HEAD), BF16),
                ((kv_heads, rows, HEAD), BF16), ((kv_cols, rows), BF16), ((kv_cols, rows), BF16)]
        saved[c] = call(
            functools.partial(project_kernel, c), info, (wq, wkv), (*xs[c], gains, a1, qb, kvb, cos[c], sin[c]), outs,
            [(wide, BF16)] + like(wq, wkv), "project_%d" % c, 12, order, (2,))
        outs = [(col, F32), (col, BF16), ((q_cols, rows), BF16), ((heads, rows), F32), ((RANK, rows), BF16)]
        pairs = [v for p in saved[:c + 1] for v in (p[2], p[5])]
        z_keep, z_send, *kept[c] = call(
            functools.partial(attend_kernel, c), info, (wo,), (saved[c][1], oa, ob, *pairs), outs, like(wo),
            "attend_%d" % c, 10, (saved[c][0],), (1,))
        z_own[c] = pair_sum(z_keep, late(z_send, z_far[0] if c else there[-1]))
        z_far[c] = far(z_own[c])
        order = (kept[c][1], z_own[c])
    def front(c, total, partial, order):
        hidden = (rows, units)
        outs = [(wide, BF16), (block, F32), (wide, BF16), (wide, BF16), (hidden, BF16), (hidden, BF16), (hidden, BF16),
                ((rows, 2 * RANK), BF16), ((rows, RANK), BF16),
                ((3 * RANK * units // QUARTER, QUARTER), BF16 if c else F32)]
        args = (*xs[c], total, near(total), *gs, gains, a2, bd, fba, da, *partial)
        weights = () if c else (gate_up_matrix, down_matrix)
        outs += like(*weights)
        return call(
            functools.partial(front_kernel, c, c == CHUNKS - 1), info, weights, (wgu, wd, *args) if c else args, outs,
            [((ROW_BLOCK, WIDTH), F32)], "front_%d" % c, 8, order, () if c else (2, units // QUARTER))

    def back(c, hidden, partial, order):
        first = col if c else (rows + 3 * RANK, half)
        outs = [((rows, RANK), F32), (first, F32), (first, BF16)]
        outs += [((3 * RANK, WIDTH), F32)] if c else []
        return call(
            functools.partial(back_kernel, c == 0), info, (), (wgu, *hidden[2:7], a2, fba, da, *partial), outs,
            [(block, F32), ((3 * RANK, QUARTER), F32)], "back_%d" % c, 8, order)

    def down(c, td, order):
        return call(down_kernel, info, (), (wd, hidden[c][4], td, bd, hidden[c][1]), [(col, F32), (col, BF16)],
                    [(block, F32)], "down_%d" % c, 6, order)

    def attend_back(c, total, partial, order):
        outs = [(block, F32), (col, F32), (col, BF16), (thin, F32), ((3 * RANK, QUARTER), F32 if c else BF16)]
        low = (4 * RANK + SPARE, half)
        outs += ([((4 * RANK, WIDTH), F32), ((kv_cols, rows), F32), ((kv_cols, rows), F32), ((SPARE // 2, rows), F32)]
                 if c else [(low, F32), (low, BF16)])
        scratch = [(wide, BF16), (wide, BF16), ((ROW_BLOCK, WIDTH), F32), ((q_cols, rows), BF16), ((q_cols, rows), F32),
                   ((c + 1, kv_cols, rows), F32), ((c + 1, kv_cols, rows), F32), ((rows, q_cols + 2 * kv_cols), BF16),
                   (block, F32), ((4 * RANK, QUARTER), F32)]
        triples = [v for p in saved[:c + 1] for v in (p[2], p[3], p[4])]
        return call(
            functools.partial(attend_back_kernel, c, c == 0), info, (wq, wkv, wo),
            (*xs[c], *gs, hidden[c][0], total, near(total), gains, a1, qb, kvb, oa, ob, cos[c], sin[c], *saved[c][:2],
             *kept[c], *triples, *partial), outs, scratch + like(wq, wkv, wo), "attend_back_%d" % c, 18, order, (3,))

    bits = [1 << b for b in reversed(range(dp.bit_length() - 1))]
    def to_bands(value):
        return lax.all_to_all(value.reshape(dp, length // dp, QUARTER), "dp", split_axis=0, concat_axis=0, tiled=True)

    def collect(value, name, *before):
        rows_out = sds((seqs, length // dp, QUARTER), BF16)
        return move_rows(collect_kernel, value, late(dealing_slots, *before), name, [rows_out], pltpu.VMEM, pl.ANY,
                         (seqs,))[0]

    hidden, d_own, d_far, y_keep, y_got = ([None] * CHUNKS for _ in range(5))
    *hidden[0], wgu, wd = front(0, far_sum(z_own[0], z_far[0]), (), order)
    step = hidden[0][8]
    hidden[1] = front(1, far_sum(z_own[1], late(z_far[1], step)), hidden[0][9:], (step,))
    td, d_keep, d_send, fa = back(1, hidden[1], (), (hidden[1][8],))
    d_own[1] = pair_sum(d_keep, d_send)
    d_far[1] = far(d_own[1])
    fb = late(hidden[1][9], d_own[1])[None]
    fb_first = swap(fb, bits[0], "dp", dp)
    td_0, d_keep, d_send = back(0, hidden[0], (fa,), (d_own[1],))
    total = far_sum(d_own[1], late(d_far[1], td_0))
    d_own[0] = pair_sum(d_keep, late(d_send, fb_first, d_far[1]))
    d_far[0] = far(d_own[0])
    fb = fb_more = jnp.concatenate([fb, late(fb_first, d_own[0])], axis=0)
    for bit in bits[1:-1]:
        fb_more = doubled(fb_more, bit, dp)
    fb_more = fb_more[2:]
    fb_side = swap(fb, bits[-1], "dp", dp)
    y_keep[1], y_send = down(1, td, (d_own[0],))
    y_got[1] = near(late(y_send, d_own[0]))
    dxq, h_keep, h_send, inv, *sums = attend_back(1, total, (), (d_own[0], y_send))
    total = far_sum(d_own[0], late(d_far[0], inv))
    h_got = near(late(h_send, fb_more, fb_side))
    fb_more_side = swap(fb_more, bits[-1], "dp", dp)
    h_high = high_sum((h_keep, h_got))
    h_far = far(h_high)
    final = [None, (dxq, h_keep, h_got, h_far, inv)]
    fa = total[rows:][None]
    fa_first = swap(fa, bits[0], "dp", dp)
    dxq, h_keep, h_send, inv, att_b, aa_keep, aa_send = attend_back(0, total, sums, (h_high,))
    ready = (fa_first, h_far, fb_more_side)
    aa_got = near(late(aa_send, *ready))
    aa_high = high_sum((aa_keep, aa_got))
    aa_far = far(aa_high)
    h_got = near(late(h_send, *ready))
    h_high = high_sum((h_keep, h_got))
    h_far = far(h_high)
    final[0] = (dxq, h_keep, h_got, h_far, inv)
    att_a = aa_keep[:4 * RANK, :QUARTER] + aa_got[:4 * RANK, :QUARTER].astype(F32)
    att_a = (att_a + late(aa_far, h_high)[:4 * RANK].astype(F32)).astype(BF16)
    n_b = att_b.shape[0]
    att = jnp.concatenate([att_b, att_a], axis=0)[None]
    y_keep[0], y_send = down(0, td_0, (att,))
    y_got[0] = near(y_send)
    att = first = doubled(att, bits[0], dp)
    att = late(att, h_far, y_send)
    for bit in bits[1:-1]:
        att = doubled(att, bit, dp)
    fa = late(jnp.concatenate([fa, fa_first], axis=0), aa_high)
    for bit in bits[1:-1]:
        fa = doubled(fa, bit, dp)
    fa_side = swap(fa, bits[-1], "dp", dp)

    dinput, = call(finish_kernel, None, (), (gains, dealt, aa_high, aa_far, *(v for f in final for v in f)),
                   [((length, QUARTER), BF16)], [], "finish", 8, (y_send, first, fa))
    y_far = far(high_sum(*((k, late(g, att)) for k, g in zip(y_keep, y_got))))
    att_side = swap(att, bits[-1], "dp", dp)
    input_grad = collect(to_bands(dinput), "collect_grad")
    result, = call(output_kernel, info, (), (late(y_far, att_side), *(v for p in zip(y_keep, y_got) for v in p)),
                   [((length, QUARTER), BF16)], [], "output", 8)
    output = collect(to_bands(result), "collect_out", input_grad)

    outs = [sds((adapters, 2 * RANK, WIDTH), F32), sds((adapters, RANK, WIDTH), F32),
            sds((adapters, 2, RANK, units), F32), sds((adapters, RANK, units), F32)]
    ga_ffn, g_down_b, g_ffn_b, g_down_a = sum_call(
        feedforward_sum_kernel, (info, owners),
        ((fb, fb_more, fb_side, fb_more_side), (fa, fa_side), (near(fa), near(fa_side))), outs, "feedforward_sum")

    a_parts = [att[:, n_b:], att_side[:, n_b:]]
    a_far = [far(v) for v in a_parts]
    a_far[1] = late(a_far[1], g_down_a)
    outs = [sds((adapters, 3 * RANK, WIDTH), F32), sds((adapters, RANK, WIDTH), F32),
            sds((adapters, RANK, q_cols), F32), sds((adapters, 2, RANK, kv_cols), F32),
            sds((adapters, RANK, q_cols), F32)]
    ga_att, g_out_b, g_query_b, g_kv_b, g_out_a = sum_call(
        attention_sum_kernel, (info, owners),
        ((att, att_side), a_parts, [near(v) for v in a_parts], a_far, [near(v) for v in a_far]), outs, "attention_sum")
    return (output, input_grad, ga_att, g_query_b, g_kv_b, g_out_a, g_out_b, ga_ffn, g_ffn_b, g_down_a, g_down_b)


def solution(mesh):
    in_specs = (
        P(None, "dp", "mp"), P("mp"), P(None, "mp"), P(None, None, "mp"), P("mp", None), P("mp"),
        P(None, None, "mp"), P("mp", None), P(), P(None, None, "mp"), P(None, None, None, "mp"),
        P(None, None, "mp"), P(), P(), P(None, None, None, "mp"), P(None, None, "mp"), P(), P(), P(), P(),
        P("dp", None, "mp"),
    )
    out_specs = (
        P(None, "dp", "mp"), P(None, "dp", "mp"), P(), P(None, None, "mp"), P(None, None, None, "mp"),
        P(None, None, "mp"), P(), P(), P(None, None, None, "mp"), P(None, None, "mp"), P(),
    )
    return jax.shard_map(
        functools.partial(shards, mesh.shape["dp"]), mesh=mesh, in_specs=in_specs, out_specs=out_specs,
        check_vma=False)
```

```python
import functools

import jax
import jax.numpy as jnp
import numpy as np
from jax import lax
from jax.experimental import pallas as pl
from jax.experimental.pallas import tpu as pltpu
from jax.sharding import PartitionSpec as P

WIDTH = 2048
HEAD = 64
HALF = HEAD // 2
RANK = 16
EPS = 1e-05
ROPE_BASE = 500000.0
NEG_FILL = -1e30
PARTS = 4
LANES = 128
SPARE = 32
ROW_BLOCK = 64
QUARTER = WIDTH // PARTS
CHUNKS = 2
MIB = 1024 * 1024
F32 = jnp.float32
BF16 = jnp.bfloat16


def nn(a, b):
    return lax.dot_general(a, b, (((1,), (0,)), ((), ())), preferred_element_type=F32)


def nt(a, b):
    return lax.dot_general(a, b, (((1,), (1,)), ((), ())), preferred_element_type=F32)


def rope_tables(length):
    freq = ROPE_BASE ** (-np.arange(HALF, dtype=np.float32) * np.float32(2.0 / HEAD))
    angles = (np.arange(length, dtype=np.float32)[None, :] * freq.astype(np.float32)[:, None]).astype(np.float32)
    return np.cos(angles).astype(np.float32), np.sin(angles).astype(np.float32)


def quarter(me, rel):
    return pl.ds(pl.multiple_of((me ^ rel) * QUARTER, QUARTER), QUARTER)


LO, HI = slice(0, QUARTER), slice(QUARTER, 2 * QUARTER)


def total_block(rel, rows_at, own, oth):
    return (own if rel in (0, 2) else oth)[rows_at, LO if rel in (0, 1) else HI].astype(F32)


def store_block(rel, value, rows_at, keep_ref, send_ref):
    to = pl.ds(pl.multiple_of((rel // 2) * QUARTER, QUARTER), QUARTER)

    @pl.when(rel % 2 == 0)
    def _():
        keep_ref[rows_at, to] = value[...]

    @pl.when(rel % 2 == 1)
    def _():
        send_ref[rows_at, to] = value[...].astype(BF16)


def chunk_of(ref, chunk, rows):
    return ref if ref.shape[0] == rows else ref.at[chunk * rows:(chunk + 1) * rows]


def row_block(i):
    return pl.ds(pl.multiple_of(i * ROW_BLOCK, ROW_BLOCK), ROW_BLOCK)


def is_valid(chunk, i, rows, length):
    return chunk * rows + i * ROW_BLOCK + lax.broadcasted_iota(jnp.int32, (ROW_BLOCK, 1), 0) < length


def copies_of(pairs, sems):
    made = [pltpu.make_async_copy(source, target, sems.at[i]) for i, (source, target) in enumerate(pairs)]
    for copy in made:
        copy.start()
    return made


def put_block(rel, value, keep_ref, send_ref):
    ref = keep_ref if rel in (0, 2) else send_ref
    ref[:, LO if rel in (0, 1) else HI] = value.astype(ref.dtype)


def rotate(value, cos, sin, out_ref):
    for i in range(value.shape[0] // HEAD):
        u1, u2 = value[i * HEAD:i * HEAD + HALF], value[i * HEAD + HALF:(i + 1) * HEAD]
        out_ref[i * HEAD:i * HEAD + HALF, :] = (u1 * cos - u2 * sin).astype(BF16)
        out_ref[i * HEAD + HALF:(i + 1) * HEAD, :] = (u2 * cos + u1 * sin).astype(BF16)


def turn_back(value, cos, sin, out_ref):
    for i in range(value.shape[0] // HEAD):
        w1, w2 = value[i * HEAD:i * HEAD + HALF], value[i * HEAD + HALF:(i + 1) * HEAD]
        out_ref[i * HEAD:i * HEAD + HALF, :] = (w1 * cos + w2 * sin).astype(BF16)
        out_ref[i * HEAD + HALF:(i + 1) * HEAD, :] = (w2 * cos - w1 * sin).astype(BF16)


def head_rows(i):
    return pl.ds(pl.multiple_of(i * HEAD, HEAD), HEAD)


def visible(key_start, query_start, rows, length):
    kpos = key_start + lax.broadcasted_iota(jnp.int32, (rows, rows), 0)
    qpos = query_start + lax.broadcasted_iota(jnp.int32, (rows, rows), 1)
    return (kpos <= qpos) & (kpos < length)


def project_kernel(chunk, info, wq_h, wkv_h, x0, x1, x2, x3, gains, a1, qb, kvb, cos_t, sin_t,
                   t1t_out, qt_out, kn_out, vn_out, kt_out, vt_out, h_out, wq, wkv, sems):
    copies = copies_of(((wkv_h, wkv), (wq_h, wq)), sems)
    me = info[0]
    rows = h_out.shape[0]
    kv_heads = kn_out.shape[0]
    xs = [chunk_of(x, chunk, rows) for x in (x0, x1, x2, x3)]

    def norm(i, carry):
        at = row_block(i)
        square = jnp.zeros((ROW_BLOCK, 1), F32)
        for r in range(PARTS):
            v = xs[r][at, :].astype(F32)
            square = square + jnp.sum(v * v, axis=1, keepdims=True)
        inv = lax.rsqrt(square / WIDTH + EPS)
        for r in range(PARTS):
            v = xs[r][at, :].astype(F32)
            h_out[at, quarter(me, r)] = (v * inv * gains[r, 0:1, :].astype(F32)).astype(BF16)
        return carry

    lax.fori_loop(0, rows // ROW_BLOCK, norm, 0)
    h = h_out[...]
    t1 = nt(h, a1[...])
    t1t_out[...] = t1.T.astype(BF16)
    t1b = t1.astype(BF16)
    cos, sin = cos_t[...], sin_t[...]
    copies[0].wait()
    k = nn(h, wkv[0]) + nn(t1b[:, RANK:2 * RANK], kvb[0])
    rotate(k.T, cos, sin, kt_out)
    k_n = kt_out[...].T
    v_n = (nn(h, wkv[1]) + nn(t1b[:, 2 * RANK:], kvb[1])).astype(BF16)
    vt_out[...] = v_n.T
    for i in range(kv_heads):
        kn_out[i] = k_n[:, i * HEAD:(i + 1) * HEAD]
        vn_out[i] = v_n[:, i * HEAD:(i + 1) * HEAD]
    copies[1].wait()
    q = nn(h, wq[...]) + nn(t1b[:, :RANK], qb[...])
    rotate(q.T * (HEAD ** -0.5), cos, sin, qt_out)


def attend_kernel(chunk, info, wo_h, qt, oa, ob, *rest):
    pairs, rest = rest[:2 * (chunk + 1)], rest[2 * (chunk + 1):]
    z_keep, z_send, ot_out, lse_out, tot_out, wo, sems = rest
    copies = copies_of(((wo_h, wo),), sems)
    keys, values = pairs[0::2], pairs[1::2]
    me, length = info[0], info[1]
    rows = qt.shape[1]
    kv_heads = keys[0].shape[0]
    heads = qt.shape[0] // HEAD
    group = heads // kv_heads

    kept = [jnp.concatenate([visible(c * rows, chunk * rows, rows, length)] * group, axis=1) for c in range(chunk + 1)]

    def one_group(j, carry):
        q_g = jnp.concatenate([qt[head_rows(j * group + g), :] for g in range(group)], axis=1)
        parts = [jnp.where(kept[c], nn(keys[c][j], q_g), NEG_FILL) for c in range(chunk + 1)]
        top = functools.reduce(jnp.maximum, [jnp.max(s, axis=0, keepdims=True) for s in parts])
        es = [jnp.exp(s - top) for s in parts]
        total = sum(jnp.sum(e, axis=0, keepdims=True) for e in es)
        low = top + jnp.log(total)
        o_t = sum(nn(value[head_rows(j), :], e.astype(BF16)) for value, e in zip(values, es))
        o_t = (o_t / total).astype(BF16)
        for g in range(group):
            cols = slice(g * rows, (g + 1) * rows)
            lse_out[pl.ds(j * group + g, 1), :] = low[:, cols]
            ot_out[head_rows(j * group + g), :] = o_t[:, cols]
        return carry

    lax.fori_loop(0, kv_heads, one_group, 0)
    o = ot_out[...].T
    to = nt(o, oa[...])
    tot_out[...] = to.T.astype(BF16)
    to = to.astype(BF16)
    copies[0].wait()
    for r in range(PARTS):
        at = quarter(me, r)
        put_block(r, nn(o, wo[:, at]) + nn(to, ob[:, at]), z_keep, z_send)


def front_kernel(chunk, last, info, wgu_in, wd_in, x0, x1, x2, x3, zo, zp, g0, g1, g2, g3, gains, a2, bd, fb, da,
                 *rest):
    units = wd_in.shape[0]
    if chunk:
        wgu, wd = wgu_in, wd_in
    else:
        (wgu, wd, f_s, sems), rest = rest[-4:], rest[:-4]
        rest = (*rest, f_s)

    def copies(i):
        c = pl.ds(pl.multiple_of(i * QUARTER, QUARTER), QUARTER)
        return (pltpu.make_async_copy(wgu_in.at[:, :, c], wgu.at[:, :, c], sems.at[0, i]),
                pltpu.make_async_copy(wd_in.at[c, :], wd.at[c, :], sems.at[1, i]))

    if not chunk:
        for i in range(units // QUARTER):
            for copy in copies(i):
                copy.start()
    f_s = rest[-1]
    xm_out, xq_out, h_out, g_out, act_out, dg_out, du_out, t2_s, dtd_s, b_out = rest[-11:-1]
    me, length = info[0], info[1]
    rows = h_out.shape[0]
    xs, gs = ([chunk_of(v, chunk, rows) for v in vs] for vs in ((x0, x1, x2, x3), (g0, g1, g2, g3)))

    def norm(i, carry):
        at = row_block(i)
        valid = is_valid(chunk, i, rows, length)
        square = jnp.zeros((ROW_BLOCK, 1), F32)
        for r in range(PARTS):
            v = xs[r][at, :].astype(F32) + total_block(r, at, zo, zp)
            if r == 0:
                xq_out[at, :] = v
            f_s[:, quarter(me, r)] = v
            square = square + jnp.sum(v * v, axis=1, keepdims=True)
            g_out[at, quarter(me, r)] = jnp.where(valid, gs[r][at, :], jnp.zeros((), BF16))
        inv = lax.rsqrt(square / WIDTH + EPS)
        for r in range(PARTS):
            v = f_s[:, quarter(me, r)]
            xm_out[at, quarter(me, r)] = v.astype(BF16)
            h_out[at, quarter(me, r)] = (v * inv * gains[r, 1:2, :].astype(F32)).astype(BF16)
        return carry

    lax.fori_loop(0, rows // ROW_BLOCK, norm, 0)
    t2 = nt(h_out[...], a2[...])
    t2_s[...] = t2.astype(BF16)
    dtd = nt(g_out[...], bd[...])
    dtd_s[...] = dtd.astype(BF16)
    t2t, dtdt = t2.T.astype(BF16), dtd.T.astype(BF16)

    def block(i, carry):
        c = pl.ds(pl.multiple_of(i * QUARTER, QUARTER), QUARTER)
        if not chunk:
            for copy in copies(i):
                copy.wait()
        h, g = h_out[...], g_out[...]
        gate = nn(h, wgu[0, :, c]) + nn(t2_s[:, :RANK], fb[0, :, c])
        up = nn(h, wgu[1, :, c]) + nn(t2_s[:, RANK:], fb[1, :, c])
        dact = nt(g, wd[c, :]) + nn(dtd_s[...], da[:, c])
        sig = 1.0 / (1.0 + jnp.exp(-gate))
        silu = gate * sig
        act = (silu * up).astype(BF16)
        dgate = (dact * up * sig * (1.0 + gate * (1.0 - sig))).astype(BF16)
        dup = (dact * silu).astype(BF16)
        act_out[:, c], dg_out[:, c], du_out[:, c] = act, dgate, dup
        for k, value in enumerate((nn(t2t[:RANK], dgate), nn(t2t[RANK:], dup), nn(dtdt, act))):
            at = pl.ds(pl.multiple_of((3 * i + k) * RANK, RANK), RANK)
            if last:
                value = value + rest[0][at, :]
            b_out[at, :] = value.astype(b_out.dtype)
        return carry

    lax.fori_loop(0, units // QUARTER, block, 0)


def back_kernel(last, info, wgu, h, g, act, dg, du, a2, fb, da, *rest):
    (value_s, low_s), rest = rest[-2:], rest[:-2]
    outs, rest = (rest[-3:], rest[:-3]) if last else (rest[-4:], rest[:-4])
    td_out, d_keep, d_send = outs[:3]
    me = info[0]
    rows = h.shape[0]
    dt2 = jnp.concatenate([nt(dg[...], fb[0]), nt(du[...], fb[1])], axis=1)
    td = nt(act[...], da[...])
    td_out[...] = td
    dt2b = dt2.astype(BF16)
    dt2t, tdt = dt2.T.astype(BF16), td.T.astype(BF16)

    def block(r, carry):
        at = quarter(me, r)
        value_s[...] = nt(dg[...], wgu[0, at, :]) + nt(du[...], wgu[1, at, :]) + nn(dt2b, a2[:, at])
        store_block(r, value_s, slice(0, rows), d_keep, d_send)
        low_s[:2 * RANK, :] = nn(dt2t, h[:, at])
        low_s[2 * RANK:, :] = nn(tdt, g[:, at])
        if last:
            low_s[...] += rest[0][:, at]
            store_block(r, low_s, slice(rows, rows + 3 * RANK), d_keep, d_send)
        else:
            outs[3][:, at] = low_s[...]
        return carry

    lax.fori_loop(0, PARTS, block, 0)


def down_kernel(info, wd, act, td, bd, xq, y_keep, y_send, value_s):
    me = info[0]
    tdb = td[...].astype(BF16)

    def block(r, carry):
        at = quarter(me, r)
        value_s[...] = nn(act[...], wd[:, at]) + nn(tdb, bd[:, at])
        store_block(r, value_s, slice(0, act.shape[0]), y_keep, y_send)
        return carry

    lax.fori_loop(0, PARTS, block, 0)
    y_keep[:, LO] += xq[...]


def attend_back_kernel(chunk, last, info, wq_h, wkv_h, wo_h, x0, x1, x2, x3, g0, g1, g2, g3, xm, do_, dp, gains, a1,
                       qb, kvb, oa, ob, cos_t, sin_t, t1t, qt, ot, lse, tot, *rest):
    scratch, rest = rest[-14:], rest[:-14]
    h_in, z_s, f_s, dot_s, dqt_s, dkt_s, dvt_s, dq_s, value_s, low_s, wq, wkv, wo, sems = scratch
    copies = copies_of(((wo_h, wo), (wq_h, wq), (wkv_h, wkv)), sems)
    n_out = 7 if last else 9
    outs, rest = rest[-n_out:], rest[:-n_out]
    dxq_out, h_keep, h_send, inv_out, b_out = outs[:5]
    triples, rest = rest[:3 * (chunk + 1)], rest[3 * (chunk + 1):]
    keys, values, keys_t = triples[0::3], triples[1::3], triples[2::3]
    me, length = info[0], info[1]
    rows = xm.shape[0]
    kv_heads = keys[0].shape[0]
    heads = qt.shape[0] // HEAD
    group = heads // kv_heads
    q_cols, kv_cols = heads * HEAD, kv_heads * HEAD
    xs, gs = ([chunk_of(v, chunk, rows) for v in vs] for vs in ((x0, x1, x2, x3), (g0, g1, g2, g3)))

    def norm_back(i, carry):
        at = row_block(i)
        valid = is_valid(chunk, i, rows, length)
        square, first, inner = (jnp.zeros((ROW_BLOCK, 1), F32) for _ in range(3))
        for r in range(PARTS):
            v = xm[at, quarter(me, r)].astype(F32)
            square = square + jnp.sum(v * v, axis=1, keepdims=True)
            w = total_block(r, at, do_, dp) * gains[r, 1:2, :].astype(F32)
            f_s[:, quarter(me, r)] = w
            inner = inner + jnp.sum(v * w, axis=1, keepdims=True)
            u = xs[r][at, :].astype(F32)
            first = first + jnp.sum(u * u, axis=1, keepdims=True)
        inv_one = lax.rsqrt(first / WIDTH + EPS)
        inv_out[at, :] = inv_one
        inv = lax.rsqrt(square / WIDTH + EPS)
        back = inv * inv * inv * inner / WIDTH
        for r in range(PARTS):
            v = xm[at, quarter(me, r)].astype(F32)
            g = jnp.where(valid, gs[r][at, :].astype(F32), 0.0)
            d = g + inv * f_s[:, quarter(me, r)] - v * back
            if r == 0:
                dxq_out[at, :] = d
            z_s[at, quarter(me, r)] = d.astype(BF16)
            u = xs[r][at, :].astype(F32)
            h_in[at, quarter(me, r)] = (u * inv_one * gains[r, 0:1, :].astype(F32)).astype(BF16)
        return carry

    lax.fori_loop(0, rows // ROW_BLOCK, norm_back, 0)
    dz = z_s[...]
    dto = nt(dz, ob[...])
    copies[0].wait()
    d_o = nt(dz, wo[...]) + nn(dto.astype(BF16), oa[...])
    dot_s[...] = d_o.T.astype(BF16)
    kept = [jnp.concatenate([visible(c * rows, chunk * rows, rows, length)] * group, axis=1) for c in range(chunk + 1)]

    def one_group(j, carry):
        places = [head_rows(j * group + g) for g in range(group)]
        q_g = jnp.concatenate([qt[at, :] for at in places], axis=1)
        do_g = jnp.concatenate([dot_s[at, :] for at in places], axis=1)
        o_g = jnp.concatenate([ot[at, :] for at in places], axis=1)
        low = jnp.concatenate([lse[pl.ds(j * group + g, 1), :] for g in range(group)], axis=1)
        dots = jnp.sum(do_g.astype(F32) * o_g.astype(F32), axis=0, keepdims=True)
        dq_g = 0.0
        for c in range(chunk + 1):
            prob = jnp.where(kept[c], jnp.exp(nn(keys[c][j], q_g) - low), 0.0)
            ds = (prob * (nn(values[c][j], do_g) - dots)).astype(BF16)
            dq_g = dq_g + nn(keys_t[c][head_rows(j), :], ds)
            dk, dv = nt(q_g, ds), nt(do_g, prob.astype(BF16))
            if last:
                dk, dv = dk + rest[2][head_rows(j), :], dv + rest[3][head_rows(j), :]
            dkt_s[c, head_rows(j), :], dvt_s[c, head_rows(j), :] = dk, dv
        for g in range(group):
            dqt_s[places[g], :] = dq_g[:, g * rows:(g + 1) * rows]
        return carry

    lax.fori_loop(0, kv_heads, one_group, 0)
    if not last:
        outs[6][...], outs[7][...] = dkt_s[0], dvt_s[0]
    cos, sin = cos_t[...], sin_t[...]
    dto_t, o_t = dto.T.astype(BF16), ot[...]
    d_out_a = nt(dto_t, o_t)
    turn_back(dqt_s[...], cos * (HEAD ** -0.5), sin * (HEAD ** -0.5), dot_s)
    dq_s[:, :q_cols] = dot_s[...].T
    turn_back(dkt_s[chunk], cos, sin, dot_s)
    dq_s[:, q_cols:q_cols + kv_cols] = dot_s[:kv_cols, :].T
    dq_s[:, q_cols + kv_cols:] = dvt_s[chunk].T.astype(BF16)
    dq, dk, dv = dq_s[:, :q_cols], dq_s[:, q_cols:q_cols + kv_cols], dq_s[:, q_cols + kv_cols:]
    dt1 = jnp.concatenate([nt(dq, qb[...]), nt(dk, kvb[0]), nt(dv, kvb[1])], axis=1)
    dt1b = dt1.astype(BF16)
    kv_pad = jnp.zeros((RANK, QUARTER - 2 * kv_cols), F32)
    d_kv = jnp.concatenate([nn(t1t[RANK:2 * RANK, :], dk), nn(t1t[2 * RANK:, :], dv), kv_pad], axis=1)
    for k, value in enumerate((nn(t1t[:RANK, :], dq), d_out_a, d_kv)):
        at = slice(k * RANK, (k + 1) * RANK)
        if last:
            value = value + rest[0][at, :]
        b_out[at, :] = value.astype(b_out.dtype)
    dt1t = dt1.T.astype(BF16)
    copies[1].wait()
    copies[2].wait()

    def block(r, inner):
        at = quarter(me, r)
        d = nt(dq_s[:, :q_cols], wq[at, :]) + nn(dt1b, a1[:, at])
        d = d + nt(dq_s[:, q_cols:q_cols + kv_cols], wkv[0, at, :]) + nt(dq_s[:, q_cols + kv_cols:], wkv[1, at, :])
        value_s[...] = d
        store_block(r, value_s, slice(0, rows), h_keep, h_send)
        low_s[:3 * RANK, :] = nn(dt1t, h_in[:, at])
        low_s[3 * RANK:, :] = nn(tot[...], z_s[:, at])
        if last:
            low_s[...] += rest[1][:, at]
            store_block(r, low_s, slice(0, 4 * RANK), outs[5], outs[6])
        else:
            outs[5][:, at] = low_s[...]
        return inner + jnp.sum(d * h_in[:, at].astype(F32), axis=1, keepdims=True)

    inner = lax.fori_loop(0, PARTS, block, jnp.zeros((rows, 1), F32))
    inner = jnp.broadcast_to(inner, (rows, LANES)).T[:SPARE // 2, :]
    if last:
        for ref in outs[5:7]:
            for c, value in enumerate((inner, rest[4][...])):
                at = slice(4 * RANK + c * SPARE // 2, 4 * RANK + (c + 1) * SPARE // 2)
                ref[at, QUARTER:QUARTER + rows] = value.astype(ref.dtype)
                ref[at, QUARTER + rows:] = jnp.zeros((SPARE // 2, QUARTER - rows), ref.dtype)
                ref[at, :QUARTER] = jnp.zeros((SPARE // 2, QUARTER), ref.dtype)
    else:
        outs[8][...] = inner


def output_kernel(info, y_far, *refs):
    out = refs[-1]
    rows = out.shape[0] // CHUNKS
    for c in range(CHUNKS):
        y_keep, y_got = refs[2 * c:2 * (c + 1)]
        at = slice(c * rows, (c + 1) * rows)
        valid = c * rows + lax.broadcasted_iota(jnp.int32, (rows, 1), 0) < info[1]
        y = y_keep[:, LO] + y_got[:, LO].astype(F32) + y_far[at, :].astype(F32)
        out[at, :] = jnp.where(valid, y, 0.0).astype(BF16)


def finish_kernel(gains, x_all, aa_high, aa_far, *refs):
    out = refs[-1]
    gain = gains[0, 0:1, :].astype(F32)
    rows = out.shape[0] // CHUNKS
    inner = aa_high[4 * RANK:, :].astype(F32) + aa_far[4 * RANK:, :].astype(F32)
    for c in range(CHUNKS):
        dx, keep, got, there, inv = refs[5 * c:5 * (c + 1)]
        x = chunk_of(x_all, c, rows)
        mine = inner[c * SPARE // 2:c * SPARE // 2 + 8, :rows].T[:, 0:1]
        inv = inv[...]
        grad = keep[:, LO] + got[:, LO].astype(F32) + there[...].astype(F32)
        grad = inv * (gain * grad) - x[...].astype(F32) * (inv * inv * mine / WIDTH)
        out[c * rows:(c + 1) * rows, :] = (dx[...] + grad).astype(BF16)


def high_sum_kernel(*refs):
    out = refs[-1]
    rows = out.shape[0] // (len(refs) // 2)
    for c in range(len(refs) // 2):
        keep, got = refs[2 * c:2 * c + 2]
        out[c * rows:(c + 1) * rows, :] = (keep[:, HI] + got[:, HI].astype(F32)).astype(BF16)


def high_sum(*pairs):
    args = [v for pair in pairs for v in pair]
    rows = sum(keep.shape[0] for keep, _ in pairs)
    return call(high_sum_kernel, None, (), args, [((rows, QUARTER), BF16)], [], "high_sum", 8)[0]


def split_refs(refs, counts):
    groups = []
    for count in counts:
        groups.append(refs[:count])
        refs = refs[count:]
    return groups, refs


def with_entry(parts, at, use):
    start = 0
    for ref in parts:
        @pl.when((at >= start) & (at < start + ref.shape[0]))
        def _(ref=ref, start=start):
            use(ref, at - start)
        start += ref.shape[0]


def sum_slots(info, owners, out_refs, one_slot):
    count = out_refs[0].shape[0]
    base = pl.program_id(0) * count
    slots = owners.shape[0]
    for ref in out_refs:
        ref[...] = jnp.zeros_like(ref)

    def add(slot, carry):
        owner = owners[slot] - base

        @pl.when((owner >= 0) & (owner < count))
        def _():
            one_slot(owner, entry_of(slot, info[3], slots))
        return carry

    lax.fori_loop(0, slots, add, 0)


def feedforward_sum_kernel(counts, info, owners, *refs):
    (b_parts, *a_parts), outs = split_refs(refs, counts)
    ga, gdb, gb, gda = outs
    me = info[0]

    def one_slot(owner, at):
        def add_b(ref, e):
            for i in range(gda.shape[2] // QUARTER):
                cols = slice(i * QUARTER, (i + 1) * QUARTER)
                base = i * 3 * RANK
                gb[owner, 0, :, cols] += ref[e, base:base + RANK, :].astype(F32)
                gb[owner, 1, :, cols] += ref[e, base + RANK:base + 2 * RANK, :].astype(F32)
                gda[owner, :, cols] += ref[e, base + 2 * RANK:base + 3 * RANK, :].astype(F32)

        with_entry(b_parts, at, add_b)
        for near_bit, parts in enumerate(a_parts):
            def add_a(ref, e, near_bit=near_bit):
                for r, cols in ((near_bit, LO), (near_bit ^ 2, HI)):
                    ga[owner, :, quarter(me, r)] += ref[e, :2 * RANK, cols].astype(F32)
                    gdb[owner, :, quarter(me, r)] += ref[e, 2 * RANK:, cols].astype(F32)

            with_entry(parts, at, add_a)

    sum_slots(info, owners, outs, one_slot)


def attention_sum_kernel(counts, info, owners, *refs):
    (b_parts, *a_parts), outs = split_refs(refs, counts)
    ga, gob, gq, gkv, goa = outs
    me = info[0]
    kv_cols = gkv.shape[3]

    def one_slot(owner, at):
        def add_b(ref, e):
            gq[owner] += ref[e, :RANK, :].astype(F32)
            goa[owner] += ref[e, RANK:2 * RANK, :].astype(F32)
            gkv[owner, 0] += ref[e, 2 * RANK:3 * RANK, :kv_cols].astype(F32)
            gkv[owner, 1] += ref[e, 2 * RANK:3 * RANK, kv_cols:2 * kv_cols].astype(F32)

        with_entry(b_parts, at, add_b)
        for r, parts in enumerate(a_parts):
            def add_a(ref, e, r=r):
                ga[owner, :, quarter(me, r)] += ref[e, :3 * RANK, :].astype(F32)
                gob[owner, :, quarter(me, r)] += ref[e, 3 * RANK:, :].astype(F32)

            with_entry(parts, at, add_a)

    sum_slots(info, owners, outs, one_slot)


def deal_kernel(slots, source, out, sems):
    made = [pltpu.make_async_copy(source.at[i], out.at[slots[i]], sems.at[i]) for i in range(source.shape[0])]
    for copy in made:
        copy.start()
    for copy in made:
        copy.wait()


def collect_kernel(slots, source, out, sems):
    made = [pltpu.make_async_copy(source.at[slots[i]], out.at[i], sems.at[i]) for i in range(source.shape[0])]
    for copy in made:
        copy.start()
    for copy in made:
        copy.wait()


def adapter_kernel(count, info, *refs):
    made = [pltpu.make_async_copy(refs[i].at[info[2]], refs[count + i], refs[-1].at[i]) for i in range(count)]
    for copy in made:
        copy.start()
    for copy in made:
        copy.wait()


def load_adapters(arrays, info):
    count = len(arrays)
    return pl.pallas_call(
        functools.partial(adapter_kernel, count),
        in_specs=[pl.BlockSpec(memory_space=pltpu.SMEM)] + [pl.BlockSpec(memory_space=pltpu.HBM)] * count,
        out_specs=[pl.BlockSpec(memory_space=pltpu.VMEM)] * count,
        out_shape=[pltpu.VMEM(a.shape[1:], a.dtype) for a in arrays],
        scratch_shapes=[pltpu.SemaphoreType.DMA((count,))],
        compiler_params=pltpu.CompilerParams(vmem_limit_bytes=MIB),
        cost_estimate=pl.CostEstimate(flops=1000, transcendentals=0, bytes_accessed=1000),
        name="adapters",
    )(info, *(in_hbm(a) for a in arrays))


def move_rows(kernel, value, slots, name, outs, in_space, out_space, sems):
    return pl.pallas_call(
        kernel,
        in_specs=[pl.BlockSpec(memory_space=pltpu.SMEM), pl.BlockSpec(memory_space=in_space)],
        out_specs=[pl.BlockSpec(memory_space=out_space)] * len(outs),
        out_shape=outs,
        scratch_shapes=[pltpu.SemaphoreType.DMA(sems)],
        compiler_params=pltpu.CompilerParams(vmem_limit_bytes=MIB),
        cost_estimate=pl.CostEstimate(flops=1000, transcendentals=0, bytes_accessed=1000),
        name=name,
    )(slots, pltpu.with_memory_space_constraint(value, in_space))


def sds(shape, dtype):
    return jax.ShapeDtypeStruct(tuple(shape), dtype)


def in_vmem(value):
    return pltpu.with_memory_space_constraint(value, pltpu.VMEM)


def in_hbm(value):
    return pltpu.with_memory_space_constraint(value, pltpu.HBM)


def call(kernel, info, weights, args, outs, scratch, name, mib, after=(), sems=()):
    vmem = pl.BlockSpec(memory_space=pltpu.VMEM)
    scalars = () if info is None else (info,)
    n, w = len(scalars), len(weights)

    def body(*refs):
        at = n + w + len(args)
        kernel(*refs[:at], *refs[at + len(after):])

    return pl.pallas_call(
        body,
        in_specs=[pl.BlockSpec(memory_space=pltpu.SMEM)] * n + [pl.BlockSpec(memory_space=pltpu.HBM)] * w + [vmem] * len(args)
        + [pl.BlockSpec(memory_space=pl.ANY)] * len(after),
        out_specs=[vmem] * len(outs),
        out_shape=[pltpu.VMEM(tuple(s), d) for s, d in outs],
        scratch_shapes=[pltpu.VMEM(s, d) for s, d in scratch] + ([pltpu.SemaphoreType.DMA(sems)] if sems else []),
        compiler_params=pltpu.CompilerParams(vmem_limit_bytes=mib * MIB),
        cost_estimate=pl.CostEstimate(flops=1000, transcendentals=0, bytes_accessed=1000),
        name=name,
    )(*scalars, *(in_hbm(a) for a in weights), *(in_vmem(a) for a in args), *after)


def whole_spec(value):
    zeros = (0,) * value.ndim
    return pl.BlockSpec(value.shape, lambda i, *_: zeros)


def sum_call(kernel, scalars, groups, outs, name):
    args = [v for group in groups for v in group]
    steps = 2
    specs = [pl.BlockSpec((o.shape[0] // steps,) + o.shape[1:], (lambda n: lambda i, *_: (i,) + (0,) * n)(o.ndim - 1))
             for o in outs]
    return pl.pallas_call(
        functools.partial(kernel, [len(group) for group in groups]),
        grid_spec=pltpu.PrefetchScalarGridSpec(
            num_scalar_prefetch=len(scalars), grid=(steps,),
            in_specs=[whole_spec(a) for a in args], out_specs=specs),
        out_shape=outs,
        compiler_params=pltpu.CompilerParams(
            dimension_semantics=("arbitrary",),
            vmem_limit_bytes=4 * MIB + 2 * sum(a.size * a.dtype.itemsize for a in args)
            + sum(o.size * o.dtype.itemsize for o in outs)),
        cost_estimate=pl.CostEstimate(flops=0, transcendentals=0, bytes_accessed=12000000),
        name=name,
    )(*scalars, *args)


def swap(value, bit, axis, size):
    return lax.ppermute(value, axis, [(i, i ^ bit) for i in range(size)])


def near(value):
    return swap(value, 1, "mp", PARTS)


def far(value):
    return swap(value, 2, "mp", PARTS)


def spread(value):
    there = far(value)
    return (value, near(value), there, near(there))


def far_sum_kernel(own, got, out):
    for to, other in ((LO, HI), (HI, LO)):
        out[:, to] = (own[:, to].astype(F32) + got[:, other].astype(F32)).astype(BF16)


def far_sum(own, got):
    return call(far_sum_kernel, None, (), (own, got), [(own.shape, BF16)], [], "far_sum", 6)[0]


def pair_sum_kernel(keep, got, out):
    out[...] = (keep[...] + got[...].astype(F32)).astype(BF16)


def pair_sum(keep, send, *before):
    got = near(send)
    got = late(got, *before) if before else got
    return call(pair_sum_kernel, None, (), (keep, got), [(send.shape, BF16)], [], "pair_sum", 6)[0]


def late(value, *others):
    return lax.optimization_barrier((value, *others))[0]


def doubled(stack, bit, size):
    return jnp.concatenate([stack, swap(stack, bit, "dp", size)], axis=0)


def entry_of(slot, place, size):
    bits = size.bit_length() - 1
    apart = slot ^ place
    return sum(((apart >> b) & 1) << (bits - 1 - b) for b in range(bits))


def shards(dp, residual, attention_gain, query_matrix, key_value_matrix, output_matrix, feedfwd_gain,
           gate_up_matrix, down_matrix, attention_adapter_input, query_adapter_output,
           key_value_adapter_output, output_adapter_input, output_adapter_output, feedfwd_adapter_input,
           feedfwd_adapter_output, down_adapter_input, down_adapter_output, lengths, adapter_index,
           dealing_slots, cotangent):
    seqs = residual.shape[0]
    length = cotangent.shape[1]
    units = down_matrix.shape[0]
    adapters = attention_adapter_input.shape[0]
    q_cols = query_matrix.shape[1]
    kv_cols = key_value_matrix.shape[2]
    kv_heads = kv_cols // HEAD
    heads = q_cols // HEAD
    rows = length // CHUNKS
    half = 2 * QUARTER
    me = lax.axis_index("mp")
    place = lax.axis_index("dp")

    is_there = dealing_slots[None, :] == jnp.arange(seqs, dtype=jnp.int32)[:, None]
    owners = jnp.sum(jnp.where(is_there, adapter_index[None, :], 0), axis=1)
    spans = jnp.sum(jnp.where(is_there, lengths[None, :], 0), axis=1)
    mine = jnp.arange(seqs, dtype=jnp.int32) == place
    my_length = jnp.sum(jnp.where(mine, spans, 0))
    my_adapter = jnp.sum(jnp.where(mine, owners, 0))
    info = jnp.stack([me.astype(jnp.int32), my_length, my_adapter, place.astype(jnp.int32)])

    gs = spread(cotangent[0])
    gains = jnp.stack(spread(jnp.stack([attention_gain, feedfwd_gain])))
    ordered, = move_rows(deal_kernel, residual, dealing_slots, "deal", [pltpu.VMEM(residual.shape, BF16)], pltpu.HBM,
                         pltpu.VMEM, (seqs,))
    dealt = lax.all_to_all(ordered, "dp", split_axis=0, concat_axis=1, tiled=True)[0]
    adapters_here = load_adapters(
        (attention_adapter_input, query_adapter_output, key_value_adapter_output, output_adapter_input,
         output_adapter_output, feedfwd_adapter_input, feedfwd_adapter_output, down_adapter_input,
         down_adapter_output), info)
    a1, qb, kvb, oa, ob, a2, fba, da, bd = adapters_here
    dealt = late(dealt, gs[2], a1, gains)
    beside = near(dealt)
    there = [far(dealt[c * rows:(c + 1) * rows]) for c in range(CHUNKS)]
    xs = [None] * CHUNKS
    cos_np, sin_np = rope_tables(length)
    cos = [jnp.asarray(cos_np[:, c * rows:(c + 1) * rows]) for c in range(CHUNKS)]
    sin = [jnp.asarray(sin_np[:, c * rows:(c + 1) * rows]) for c in range(CHUNKS)]
    wq, wkv, wo = query_matrix, key_value_matrix, output_matrix

    def like(*arrays):
        return [(a.shape, a.dtype) for a in arrays]

    wide, col, block, thin = (rows, WIDTH), (rows, half), (rows, QUARTER), (rows, 1)
    saved, kept, z_own, z_far = ([None] * CHUNKS for _ in range(4))
    order = ()
    for c in range(CHUNKS):
        xs[c] = (dealt, beside, there[c], near(late(there[c], saved[0][0]) if c else there[c]))
        outs = [((3 * RANK, rows), BF16), ((q_cols, rows), BF16), ((kv_heads, rows, HEAD), BF16),
                ((kv_heads, rows, HEAD), BF16), ((kv_cols, rows), BF16), ((kv_cols, rows), BF16)]
        saved[c] = call(
            functools.partial(project_kernel, c), info, (wq, wkv), (*xs[c], gains, a1, qb, kvb, cos[c], sin[c]), outs,
            [(wide, BF16)] + like(wq, wkv), "project_%d" % c, 12, order, (2,))
        outs = [(col, F32), (col, BF16), ((q_cols, rows), BF16), ((heads, rows), F32), ((RANK, rows), BF16)]
        pairs = [v for p in saved[:c + 1] for v in (p[2], p[5])]
        z_keep, z_send, *kept[c] = call(
            functools.partial(attend_kernel, c), info, (wo,), (saved[c][1], oa, ob, *pairs), outs, like(wo),
            "attend_%d" % c, 10, (saved[c][0],), (1,))
        z_own[c] = pair_sum(z_keep, late(z_send, z_far[0] if c else there[-1]))
        z_far[c] = far(z_own[c])
        order = (kept[c][1], z_own[c])
    def front(c, total, partial, order):
        hidden = (rows, units)
        outs = [(wide, BF16), (block, F32), (wide, BF16), (wide, BF16), (hidden, BF16), (hidden, BF16), (hidden, BF16),
                ((rows, 2 * RANK), BF16), ((rows, RANK), BF16),
                ((3 * RANK * units // QUARTER, QUARTER), BF16 if c else F32)]
        args = (*xs[c], total, near(total), *gs, gains, a2, bd, fba, da, *partial)
        weights = () if c else (gate_up_matrix, down_matrix)
        outs += like(*weights)
        return call(
            functools.partial(front_kernel, c, c == CHUNKS - 1), info, weights, (wgu, wd, *args) if c else args, outs,
            [((ROW_BLOCK, WIDTH), F32)], "front_%d" % c, 8, order, () if c else (2, units // QUARTER))

    def back(c, hidden, partial, order):
        first = col if c else (rows + 3 * RANK, half)
        outs = [((rows, RANK), F32), (first, F32), (first, BF16)]
        outs += [((3 * RANK, WIDTH), F32)] if c else []
        return call(
            functools.partial(back_kernel, c == 0), info, (), (wgu, *hidden[2:7], a2, fba, da, *partial), outs,
            [(block, F32), ((3 * RANK, QUARTER), F32)], "back_%d" % c, 8, order)

    def down(c, td, order):
        return call(down_kernel, info, (), (wd, hidden[c][4], td, bd, hidden[c][1]), [(col, F32), (col, BF16)],
                    [(block, F32)], "down_%d" % c, 6, order)

    def attend_back(c, total, partial, order):
        outs = [(block, F32), (col, F32), (col, BF16), (thin, F32), ((3 * RANK, QUARTER), F32 if c else BF16)]
        low = (4 * RANK + SPARE, half)
        outs += ([((4 * RANK, WIDTH), F32), ((kv_cols, rows), F32), ((kv_cols, rows), F32), ((SPARE // 2, rows), F32)]
                 if c else [(low, F32), (low, BF16)])
        scratch = [(wide, BF16), (wide, BF16), ((ROW_BLOCK, WIDTH), F32), ((q_cols, rows), BF16), ((q_cols, rows), F32),
                   ((c + 1, kv_cols, rows), F32), ((c + 1, kv_cols, rows), F32), ((rows, q_cols + 2 * kv_cols), BF16),
                   (block, F32), ((4 * RANK, QUARTER), F32)]
        triples = [v for p in saved[:c + 1] for v in (p[2], p[3], p[4])]
        return call(
            functools.partial(attend_back_kernel, c, c == 0), info, (wq, wkv, wo),
            (*xs[c], *gs, hidden[c][0], total, near(total), gains, a1, qb, kvb, oa, ob, cos[c], sin[c], *saved[c][:2],
             *kept[c], *triples, *partial), outs, scratch + like(wq, wkv, wo), "attend_back_%d" % c, 18, order, (3,))

    bits = [1 << b for b in reversed(range(dp.bit_length() - 1))]
    def to_bands(value):
        return lax.all_to_all(value.reshape(dp, length // dp, QUARTER), "dp", split_axis=0, concat_axis=0, tiled=True)

    def collect(value, name, *before):
        rows_out = sds((seqs, length // dp, QUARTER), BF16)
        return move_rows(collect_kernel, value, late(dealing_slots, *before), name, [rows_out], pltpu.VMEM, pl.ANY,
                         (seqs,))[0]

    hidden, d_own, d_far, y_keep, y_got = ([None] * CHUNKS for _ in range(5))
    *hidden[0], wgu, wd = front(0, far_sum(z_own[0], z_far[0]), (), order)
    step = hidden[0][8]
    hidden[1] = front(1, far_sum(z_own[1], late(z_far[1], step)), hidden[0][9:], (step,))
    fb = hidden[1][9][None]
    fb_first = swap(fb, bits[0], "dp", dp)
    td, d_keep, d_send, fa = back(1, hidden[1], (), (hidden[1][8],))
    d_own[1] = pair_sum(d_keep, late(d_send, fb_first))
    d_far[1] = far(d_own[1])
    fb = fb_more = jnp.concatenate([fb, fb_first], axis=0)
    for bit in bits[1:-1]:
        fb_more = doubled(fb_more, bit, dp)
    fb_more = fb_more[2:]
    fb_side = swap(fb, bits[-1], "dp", dp)
    td_0, d_keep, d_send = back(0, hidden[0], (fa,), (d_own[1],))
    y_keep[1], y_send = down(1, td, (td_0,))
    total = far_sum(d_own[1], late(d_far[1], y_send))
    d_own[0] = pair_sum(d_keep, late(d_send, fb_more, fb_side), total)
    d_far[0] = far(d_own[0])
    fb_more_side = swap(fb_more, bits[-1], "dp", dp)
    y_got[1] = near(late(y_send, d_own[0]))
    dxq, h_keep, h_send, inv, *sums = attend_back(1, total, (), (d_own[0], y_send))
    total = far_sum(d_own[0], late(d_far[0], inv))
    h_got = near(late(h_send, fb_more_side))
    h_high = high_sum((h_keep, h_got))
    h_far = far(h_high)
    final = [None, (dxq, h_keep, h_got, h_far, inv)]
    fa = total[rows:][None]
    fa_first = swap(fa, bits[0], "dp", dp)
    dxq, h_keep, h_send, inv, att_b, aa_keep, aa_send = attend_back(0, total, sums, (h_high,))
    ready = (fa_first, h_far)
    aa_got = near(late(aa_send, *ready))
    aa_high = high_sum((aa_keep, aa_got))
    aa_far = far(aa_high)
    h_got = near(late(h_send, *ready))
    h_high = high_sum((h_keep, h_got))
    h_far = far(h_high)
    final[0] = (dxq, h_keep, h_got, h_far, inv)
    att_a = aa_keep[:4 * RANK, :QUARTER] + aa_got[:4 * RANK, :QUARTER].astype(F32)
    att_a = (att_a + late(aa_far, h_high)[:4 * RANK].astype(F32)).astype(BF16)
    n_b = att_b.shape[0]
    att = jnp.concatenate([att_b, att_a], axis=0)[None]
    y_keep[0], y_send = down(0, td_0, (att,))
    y_got[0] = near(y_send)
    att = doubled(att, bits[0], dp)
    att = late(att, h_far, y_send)
    for bit in bits[1:-1]:
        att = doubled(att, bit, dp)
    fa = late(jnp.concatenate([fa, fa_first], axis=0), aa_high)
    for bit in bits[1:-1]:
        fa = doubled(fa, bit, dp)
    fa_side = swap(fa, bits[-1], "dp", dp)
    y_far = far(high_sum(*((k, late(g, h_far)) for k, g in zip(y_keep, y_got))))

    dinput, = call(finish_kernel, None, (), (gains, dealt, aa_high, aa_far, *(v for f in final for v in f)),
                   [((length, QUARTER), BF16)], [], "finish", 8, (att, fa_side))
    input_grad = collect(to_bands(dinput), "collect_grad")
    outs = [sds((adapters, 2 * RANK, WIDTH), F32), sds((adapters, RANK, WIDTH), F32),
            sds((adapters, 2, RANK, units), F32), sds((adapters, RANK, units), F32)]
    ga_ffn, g_down_b, g_ffn_b, g_down_a = sum_call(
        feedforward_sum_kernel, (info, owners),
        ((fb, fb_more, fb_side, fb_more_side), (fa, fa_side), (near(fa), near(fa_side))), outs, "feedforward_sum")

    result, = call(output_kernel, info, (), (late(y_far, dinput, g_down_a), *(v for p in zip(y_keep, y_got) for v in p)),
                   [((length, QUARTER), BF16)], [], "output", 8)
    output = collect(to_bands(result), "collect_out", input_grad)

    att_side = swap(att, bits[-1], "dp", dp)
    a_parts = [att[:, n_b:], att_side[:, n_b:]]
    a_far = [far(v) for v in a_parts]
    outs = [sds((adapters, 3 * RANK, WIDTH), F32), sds((adapters, RANK, WIDTH), F32),
            sds((adapters, RANK, q_cols), F32), sds((adapters, 2, RANK, kv_cols), F32),
            sds((adapters, RANK, q_cols), F32)]
    ga_att, g_out_b, g_query_b, g_kv_b, g_out_a = sum_call(
        attention_sum_kernel, (info, owners),
        ((att, att_side), a_parts, [near(v) for v in a_parts], a_far, [near(v) for v in a_far]), outs, "attention_sum")
    return (output, input_grad, ga_att, g_query_b, g_kv_b, g_out_a, g_out_b, ga_ffn, g_ffn_b, g_down_a, g_down_b)


def solution(mesh):
    in_specs = (
        P(None, "dp", "mp"), P("mp"), P(None, "mp"), P(None, None, "mp"), P("mp", None), P("mp"),
        P(None, None, "mp"), P("mp", None), P(), P(None, None, "mp"), P(None, None, None, "mp"),
        P(None, None, "mp"), P(), P(), P(None, None, None, "mp"), P(None, None, "mp"), P(), P(), P(), P(),
        P("dp", None, "mp"),
    )
    out_specs = (
        P(None, "dp", "mp"), P(None, "dp", "mp"), P(), P(None, None, "mp"), P(None, None, None, "mp"),
        P(None, None, "mp"), P(), P(), P(None, None, None, "mp"), P(None, None, "mp"), P(),
    )
    return jax.shard_map(
        functools.partial(shards, mesh.shape["dp"]), mesh=mesh, in_specs=in_specs, out_specs=out_specs,
        check_vma=False)
```

```python
import functools

import jax
import jax.numpy as jnp
import numpy as np
from jax import lax
from jax.experimental import pallas as pl
from jax.experimental.pallas import tpu as pltpu
from jax.sharding import PartitionSpec as P

WIDTH = 2048
HEAD = 64
HALF = HEAD // 2
RANK = 16
EPS = 1e-05
ROPE_BASE = 500000.0
NEG_FILL = -1e30
PARTS = 4
LANES = 128
SPARE = 32
ROW_BLOCK = 64
QUARTER = WIDTH // PARTS
CHUNKS = 2
MIB = 1024 * 1024
F32 = jnp.float32
BF16 = jnp.bfloat16


def nn(a, b):
    return lax.dot_general(a, b, (((1,), (0,)), ((), ())), preferred_element_type=F32)


def nt(a, b):
    return lax.dot_general(a, b, (((1,), (1,)), ((), ())), preferred_element_type=F32)


def rope_tables(length):
    freq = ROPE_BASE ** (-np.arange(HALF, dtype=np.float32) * np.float32(2.0 / HEAD))
    angles = (np.arange(length, dtype=np.float32)[None, :] * freq.astype(np.float32)[:, None]).astype(np.float32)
    return np.cos(angles).astype(np.float32), np.sin(angles).astype(np.float32)


def quarter(me, rel):
    return pl.ds(pl.multiple_of((me ^ rel) * QUARTER, QUARTER), QUARTER)


LO, HI = slice(0, QUARTER), slice(QUARTER, 2 * QUARTER)


def total_block(rel, rows_at, own, oth):
    return (own if rel in (0, 2) else oth)[rows_at, LO if rel in (0, 1) else HI].astype(F32)


def store_block(rel, value, rows_at, keep_ref, send_ref):
    to = pl.ds(pl.multiple_of((rel // 2) * QUARTER, QUARTER), QUARTER)

    @pl.when(rel % 2 == 0)
    def _():
        keep_ref[rows_at, to] = value[...]

    @pl.when(rel % 2 == 1)
    def _():
        send_ref[rows_at, to] = value[...].astype(BF16)


def chunk_of(ref, chunk, rows):
    return ref if ref.shape[0] == rows else ref.at[chunk * rows:(chunk + 1) * rows]


def row_block(i):
    return pl.ds(pl.multiple_of(i * ROW_BLOCK, ROW_BLOCK), ROW_BLOCK)


def is_valid(chunk, i, rows, length):
    return chunk * rows + i * ROW_BLOCK + lax.broadcasted_iota(jnp.int32, (ROW_BLOCK, 1), 0) < length


def copies_of(pairs, sems):
    made = [pltpu.make_async_copy(source, target, sems.at[i]) for i, (source, target) in enumerate(pairs)]
    for copy in made:
        copy.start()
    return made


def put_block(rel, value, keep_ref, send_ref):
    ref = keep_ref if rel in (0, 2) else send_ref
    ref[:, LO if rel in (0, 1) else HI] = value.astype(ref.dtype)


def rotate(value, cos, sin, out_ref):
    for i in range(value.shape[0] // HEAD):
        u1, u2 = value[i * HEAD:i * HEAD + HALF], value[i * HEAD + HALF:(i + 1) * HEAD]
        out_ref[i * HEAD:i * HEAD + HALF, :] = (u1 * cos - u2 * sin).astype(BF16)
        out_ref[i * HEAD + HALF:(i + 1) * HEAD, :] = (u2 * cos + u1 * sin).astype(BF16)


def turn_back(value, cos, sin, out_ref):
    for i in range(value.shape[0] // HEAD):
        w1, w2 = value[i * HEAD:i * HEAD + HALF], value[i * HEAD + HALF:(i + 1) * HEAD]
        out_ref[i * HEAD:i * HEAD + HALF, :] = (w1 * cos + w2 * sin).astype(BF16)
        out_ref[i * HEAD + HALF:(i + 1) * HEAD, :] = (w2 * cos - w1 * sin).astype(BF16)


def head_rows(i):
    return pl.ds(pl.multiple_of(i * HEAD, HEAD), HEAD)


def visible(key_start, query_start, rows, length):
    kpos = key_start + lax.broadcasted_iota(jnp.int32, (rows, rows), 0)
    qpos = query_start + lax.broadcasted_iota(jnp.int32, (rows, rows), 1)
    return (kpos <= qpos) & (kpos < length)


def project_kernel(chunk, info, wq_h, wkv_h, x0, x1, x2, x3, gains, a1, qb, kvb, cos_t, sin_t,
                   t1t_out, qt_out, kn_out, vn_out, kt_out, vt_out, h_out, wq, wkv, sems):
    copies = copies_of(((wkv_h, wkv), (wq_h, wq)), sems)
    me = info[0]
    rows = h_out.shape[0]
    kv_heads = kn_out.shape[0]
    xs = [chunk_of(x, chunk, rows) for x in (x0, x1, x2, x3)]

    def norm(i, carry):
        at = row_block(i)
        square = jnp.zeros((ROW_BLOCK, 1), F32)
        for r in range(PARTS):
            v = xs[r][at, :].astype(F32)
            square = square + jnp.sum(v * v, axis=1, keepdims=True)
        inv = lax.rsqrt(square / WIDTH + EPS)
        for r in range(PARTS):
            v = xs[r][at, :].astype(F32)
            h_out[at, quarter(me, r)] = (v * inv * gains[r, 0:1, :].astype(F32)).astype(BF16)
        return carry

    lax.fori_loop(0, rows // ROW_BLOCK, norm, 0)
    h = h_out[...]
    t1 = nt(h, a1[...])
    t1t_out[...] = t1.T.astype(BF16)
    t1b = t1.astype(BF16)
    cos, sin = cos_t[...], sin_t[...]
    copies[0].wait()
    k = nn(h, wkv[0]) + nn(t1b[:, RANK:2 * RANK], kvb[0])
    rotate(k.T, cos, sin, kt_out)
    k_n = kt_out[...].T
    v_n = (nn(h, wkv[1]) + nn(t1b[:, 2 * RANK:], kvb[1])).astype(BF16)
    vt_out[...] = v_n.T
    for i in range(kv_heads):
        kn_out[i] = k_n[:, i * HEAD:(i + 1) * HEAD]
        vn_out[i] = v_n[:, i * HEAD:(i + 1) * HEAD]
    copies[1].wait()
    q = nn(h, wq[...]) + nn(t1b[:, :RANK], qb[...])
    rotate(q.T * (HEAD ** -0.5), cos, sin, qt_out)


def attend_kernel(chunk, info, wo_h, qt, oa, ob, *rest):
    pairs, rest = rest[:2 * (chunk + 1)], rest[2 * (chunk + 1):]
    z_keep, z_send, ot_out, lse_out, tot_out, wo, sems = rest
    copies = copies_of(((wo_h, wo),), sems)
    keys, values = pairs[0::2], pairs[1::2]
    me, length = info[0], info[1]
    rows = qt.shape[1]
    kv_heads = keys[0].shape[0]
    heads = qt.shape[0] // HEAD
    group = heads // kv_heads

    kept = [jnp.concatenate([visible(c * rows, chunk * rows, rows, length)] * group, axis=1) for c in range(chunk + 1)]

    def one_group(j, carry):
        q_g = jnp.concatenate([qt[head_rows(j * group + g), :] for g in range(group)], axis=1)
        parts = [jnp.where(kept[c], nn(keys[c][j], q_g), NEG_FILL) for c in range(chunk + 1)]
        top = functools.reduce(jnp.maximum, [jnp.max(s, axis=0, keepdims=True) for s in parts])
        es = [jnp.exp(s - top) for s in parts]
        total = sum(jnp.sum(e, axis=0, keepdims=True) for e in es)
        low = top + jnp.log(total)
        o_t = sum(nn(value[head_rows(j), :], e.astype(BF16)) for value, e in zip(values, es))
        o_t = (o_t / total).astype(BF16)
        for g in range(group):
            cols = slice(g * rows, (g + 1) * rows)
            lse_out[pl.ds(j * group + g, 1), :] = low[:, cols]
            ot_out[head_rows(j * group + g), :] = o_t[:, cols]
        return carry

    lax.fori_loop(0, kv_heads, one_group, 0)
    o = ot_out[...].T
    to = nt(o, oa[...])
    tot_out[...] = to.T.astype(BF16)
    to = to.astype(BF16)
    copies[0].wait()
    for r in range(PARTS):
        at = quarter(me, r)
        put_block(r, nn(o, wo[:, at]) + nn(to, ob[:, at]), z_keep, z_send)


def front_kernel(chunk, last, info, wgu_in, wd_in, x0, x1, x2, x3, zo, zp, g0, g1, g2, g3, gains, a2, bd, fb, da,
                 *rest):
    units = wd_in.shape[0]
    if chunk:
        wgu, wd = wgu_in, wd_in
    else:
        (wgu, wd, f_s, sems), rest = rest[-4:], rest[:-4]
        rest = (*rest, f_s)

    def copies(i):
        c = pl.ds(pl.multiple_of(i * QUARTER, QUARTER), QUARTER)
        return (pltpu.make_async_copy(wgu_in.at[:, :, c], wgu.at[:, :, c], sems.at[0, i]),
                pltpu.make_async_copy(wd_in.at[c, :], wd.at[c, :], sems.at[1, i]))

    if not chunk:
        for i in range(units // QUARTER):
            for copy in copies(i):
                copy.start()
    f_s = rest[-1]
    xm_out, xq_out, h_out, g_out, act_out, dg_out, du_out, t2_s, dtd_s, b_out = rest[-11:-1]
    me, length = info[0], info[1]
    rows = h_out.shape[0]
    xs, gs = ([chunk_of(v, chunk, rows) for v in vs] for vs in ((x0, x1, x2, x3), (g0, g1, g2, g3)))

    def norm(i, carry):
        at = row_block(i)
        valid = is_valid(chunk, i, rows, length)
        square = jnp.zeros((ROW_BLOCK, 1), F32)
        for r in range(PARTS):
            v = xs[r][at, :].astype(F32) + total_block(r, at, zo, zp)
            if r == 0:
                xq_out[at, :] = v
            f_s[:, quarter(me, r)] = v
            square = square + jnp.sum(v * v, axis=1, keepdims=True)
            g_out[at, quarter(me, r)] = jnp.where(valid, gs[r][at, :], jnp.zeros((), BF16))
        inv = lax.rsqrt(square / WIDTH + EPS)
        for r in range(PARTS):
            v = f_s[:, quarter(me, r)]
            xm_out[at, quarter(me, r)] = v.astype(BF16)
            h_out[at, quarter(me, r)] = (v * inv * gains[r, 1:2, :].astype(F32)).astype(BF16)
        return carry

    lax.fori_loop(0, rows // ROW_BLOCK, norm, 0)
    t2 = nt(h_out[...], a2[...])
    t2_s[...] = t2.astype(BF16)
    dtd = nt(g_out[...], bd[...])
    dtd_s[...] = dtd.astype(BF16)
    t2t, dtdt = t2.T.astype(BF16), dtd.T.astype(BF16)

    def block(i, carry):
        c = pl.ds(pl.multiple_of(i * QUARTER, QUARTER), QUARTER)
        if not chunk:
            for copy in copies(i):
                copy.wait()
        h, g = h_out[...], g_out[...]
        gate = nn(h, wgu[0, :, c]) + nn(t2_s[:, :RANK], fb[0, :, c])
        up = nn(h, wgu[1, :, c]) + nn(t2_s[:, RANK:], fb[1, :, c])
        dact = nt(g, wd[c, :]) + nn(dtd_s[...], da[:, c])
        sig = 1.0 / (1.0 + jnp.exp(-gate))
        silu = gate * sig
        act = (silu * up).astype(BF16)
        dgate = (dact * up * sig * (1.0 + gate * (1.0 - sig))).astype(BF16)
        dup = (dact * silu).astype(BF16)
        act_out[:, c], dg_out[:, c], du_out[:, c] = act, dgate, dup
        for k, value in enumerate((nn(t2t[:RANK], dgate), nn(t2t[RANK:], dup), nn(dtdt, act))):
            at = pl.ds(pl.multiple_of((3 * i + k) * RANK, RANK), RANK)
            if last:
                value = value + rest[0][at, :]
            b_out[at, :] = value.astype(b_out.dtype)
        return carry

    lax.fori_loop(0, units // QUARTER, block, 0)


def back_kernel(last, info, wgu, h, g, act, dg, du, a2, fb, da, *rest):
    (value_s, low_s), rest = rest[-2:], rest[:-2]
    outs, rest = (rest[-3:], rest[:-3]) if last else (rest[-4:], rest[:-4])
    td_out, d_keep, d_send = outs[:3]
    me = info[0]
    rows = h.shape[0]
    dt2 = jnp.concatenate([nt(dg[...], fb[0]), nt(du[...], fb[1])], axis=1)
    td = nt(act[...], da[...])
    td_out[...] = td
    dt2b = dt2.astype(BF16)
    dt2t, tdt = dt2.T.astype(BF16), td.T.astype(BF16)

    def block(r, carry):
        at = quarter(me, r)
        value_s[...] = nt(dg[...], wgu[0, at, :]) + nt(du[...], wgu[1, at, :]) + nn(dt2b, a2[:, at])
        store_block(r, value_s, slice(0, rows), d_keep, d_send)
        low_s[:2 * RANK, :] = nn(dt2t, h[:, at])
        low_s[2 * RANK:, :] = nn(tdt, g[:, at])
        if last:
            low_s[...] += rest[0][:, at]
            store_block(r, low_s, slice(rows, rows + 3 * RANK), d_keep, d_send)
        else:
            outs[3][:, at] = low_s[...]
        return carry

    lax.fori_loop(0, PARTS, block, 0)


def down_kernel(info, wd, act, td, bd, xq, y_keep, y_send, value_s):
    me = info[0]
    tdb = td[...].astype(BF16)

    def block(r, carry):
        at = quarter(me, r)
        value_s[...] = nn(act[...], wd[:, at]) + nn(tdb, bd[:, at])
        store_block(r, value_s, slice(0, act.shape[0]), y_keep, y_send)
        return carry

    lax.fori_loop(0, PARTS, block, 0)
    y_keep[:, LO] += xq[...]


def attend_back_kernel(chunk, last, info, wq_h, wkv_h, wo_h, x0, x1, x2, x3, g0, g1, g2, g3, xm, do_, dp, gains, a1,
                       qb, kvb, oa, ob, cos_t, sin_t, t1t, qt, ot, lse, tot, *rest):
    scratch, rest = rest[-14:], rest[:-14]
    h_in, z_s, f_s, dot_s, dqt_s, dkt_s, dvt_s, dq_s, value_s, low_s, wq, wkv, wo, sems = scratch
    copies = copies_of(((wo_h, wo), (wq_h, wq), (wkv_h, wkv)), sems)
    n_out = 7 if last else 9
    outs, rest = rest[-n_out:], rest[:-n_out]
    dxq_out, h_keep, h_send, inv_out, b_out = outs[:5]
    triples, rest = rest[:3 * (chunk + 1)], rest[3 * (chunk + 1):]
    keys, values, keys_t = triples[0::3], triples[1::3], triples[2::3]
    me, length = info[0], info[1]
    rows = xm.shape[0]
    kv_heads = keys[0].shape[0]
    heads = qt.shape[0] // HEAD
    group = heads // kv_heads
    q_cols, kv_cols = heads * HEAD, kv_heads * HEAD
    xs, gs = ([chunk_of(v, chunk, rows) for v in vs] for vs in ((x0, x1, x2, x3), (g0, g1, g2, g3)))

    def norm_back(i, carry):
        at = row_block(i)
        valid = is_valid(chunk, i, rows, length)
        square, first, inner = (jnp.zeros((ROW_BLOCK, 1), F32) for _ in range(3))
        for r in range(PARTS):
            v = xm[at, quarter(me, r)].astype(F32)
            square = square + jnp.sum(v * v, axis=1, keepdims=True)
            w = total_block(r, at, do_, dp) * gains[r, 1:2, :].astype(F32)
            f_s[:, quarter(me, r)] = w
            inner = inner + jnp.sum(v * w, axis=1, keepdims=True)
            u = xs[r][at, :].astype(F32)
            first = first + jnp.sum(u * u, axis=1, keepdims=True)
        inv_one = lax.rsqrt(first / WIDTH + EPS)
        inv_out[at, :] = inv_one
        inv = lax.rsqrt(square / WIDTH + EPS)
        back = inv * inv * inv * inner / WIDTH
        for r in range(PARTS):
            v = xm[at, quarter(me, r)].astype(F32)
            g = jnp.where(valid, gs[r][at, :].astype(F32), 0.0)
            d = g + inv * f_s[:, quarter(me, r)] - v * back
            if r == 0:
                dxq_out[at, :] = d
            z_s[at, quarter(me, r)] = d.astype(BF16)
            u = xs[r][at, :].astype(F32)
            h_in[at, quarter(me, r)] = (u * inv_one * gains[r, 0:1, :].astype(F32)).astype(BF16)
        return carry

    lax.fori_loop(0, rows // ROW_BLOCK, norm_back, 0)
    dz = z_s[...]
    dto = nt(dz, ob[...])
    copies[0].wait()
    d_o = nt(dz, wo[...]) + nn(dto.astype(BF16), oa[...])
    dot_s[...] = d_o.T.astype(BF16)
    kept = [jnp.concatenate([visible(c * rows, chunk * rows, rows, length)] * group, axis=1) for c in range(chunk + 1)]

    def one_group(j, carry):
        places = [head_rows(j * group + g) for g in range(group)]
        q_g = jnp.concatenate([qt[at, :] for at in places], axis=1)
        do_g = jnp.concatenate([dot_s[at, :] for at in places], axis=1)
        o_g = jnp.concatenate([ot[at, :] for at in places], axis=1)
        low = jnp.concatenate([lse[pl.ds(j * group + g, 1), :] for g in range(group)], axis=1)
        dots = jnp.sum(do_g.astype(F32) * o_g.astype(F32), axis=0, keepdims=True)
        dq_g = 0.0
        for c in range(chunk + 1):
            prob = jnp.where(kept[c], jnp.exp(nn(keys[c][j], q_g) - low), 0.0)
            ds = (prob * (nn(values[c][j], do_g) - dots)).astype(BF16)
            dq_g = dq_g + nn(keys_t[c][head_rows(j), :], ds)
            dk, dv = nt(q_g, ds), nt(do_g, prob.astype(BF16))
            if last:
                dk, dv = dk + rest[2][head_rows(j), :], dv + rest[3][head_rows(j), :]
            dkt_s[c, head_rows(j), :], dvt_s[c, head_rows(j), :] = dk, dv
        for g in range(group):
            dqt_s[places[g], :] = dq_g[:, g * rows:(g + 1) * rows]
        return carry

    lax.fori_loop(0, kv_heads, one_group, 0)
    if not last:
        outs[6][...], outs[7][...] = dkt_s[0], dvt_s[0]
    cos, sin = cos_t[...], sin_t[...]
    dto_t, o_t = dto.T.astype(BF16), ot[...]
    d_out_a = nt(dto_t, o_t)
    turn_back(dqt_s[...], cos * (HEAD ** -0.5), sin * (HEAD ** -0.5), dot_s)
    dq_s[:, :q_cols] = dot_s[...].T
    turn_back(dkt_s[chunk], cos, sin, dot_s)
    dq_s[:, q_cols:q_cols + kv_cols] = dot_s[:kv_cols, :].T
    dq_s[:, q_cols + kv_cols:] = dvt_s[chunk].T.astype(BF16)
    dq, dk, dv = dq_s[:, :q_cols], dq_s[:, q_cols:q_cols + kv_cols], dq_s[:, q_cols + kv_cols:]
    dt1 = jnp.concatenate([nt(dq, qb[...]), nt(dk, kvb[0]), nt(dv, kvb[1])], axis=1)
    dt1b = dt1.astype(BF16)
    kv_pad = jnp.zeros((RANK, QUARTER - 2 * kv_cols), F32)
    d_kv = jnp.concatenate([nn(t1t[RANK:2 * RANK, :], dk), nn(t1t[2 * RANK:, :], dv), kv_pad], axis=1)
    for k, value in enumerate((nn(t1t[:RANK, :], dq), d_out_a, d_kv)):
        at = slice(k * RANK, (k + 1) * RANK)
        if last:
            value = value + rest[0][at, :]
        b_out[at, :] = value.astype(b_out.dtype)
    dt1t = dt1.T.astype(BF16)
    copies[1].wait()
    copies[2].wait()

    def block(r, inner):
        at = quarter(me, r)
        d = nt(dq_s[:, :q_cols], wq[at, :]) + nn(dt1b, a1[:, at])
        d = d + nt(dq_s[:, q_cols:q_cols + kv_cols], wkv[0, at, :]) + nt(dq_s[:, q_cols + kv_cols:], wkv[1, at, :])
        value_s[...] = d
        store_block(r, value_s, slice(0, rows), h_keep, h_send)
        low_s[:3 * RANK, :] = nn(dt1t, h_in[:, at])
        low_s[3 * RANK:, :] = nn(tot[...], z_s[:, at])
        if last:
            low_s[...] += rest[1][:, at]
            store_block(r, low_s, slice(0, 4 * RANK), outs[5], outs[6])
        else:
            outs[5][:, at] = low_s[...]
        return inner + jnp.sum(d * h_in[:, at].astype(F32), axis=1, keepdims=True)

    inner = lax.fori_loop(0, PARTS, block, jnp.zeros((rows, 1), F32))
    inner = jnp.broadcast_to(inner, (rows, LANES)).T[:SPARE // 2, :]
    if last:
        for ref in outs[5:7]:
            for c, value in enumerate((inner, rest[4][...])):
                at = slice(4 * RANK + c * SPARE // 2, 4 * RANK + (c + 1) * SPARE // 2)
                ref[at, QUARTER:QUARTER + rows] = value.astype(ref.dtype)
                ref[at, QUARTER + rows:] = jnp.zeros((SPARE // 2, QUARTER - rows), ref.dtype)
                ref[at, :QUARTER] = jnp.zeros((SPARE // 2, QUARTER), ref.dtype)
    else:
        outs[8][...] = inner


def output_kernel(info, y_far, *refs):
    out = refs[-1]
    rows = out.shape[0] // CHUNKS
    for c in range(CHUNKS):
        y_keep, y_got = refs[2 * c:2 * (c + 1)]
        at = slice(c * rows, (c + 1) * rows)
        valid = c * rows + lax.broadcasted_iota(jnp.int32, (rows, 1), 0) < info[1]
        y = y_keep[:, LO] + y_got[:, LO].astype(F32) + y_far[at, :].astype(F32)
        out[at, :] = jnp.where(valid, y, 0.0).astype(BF16)


def finish_kernel(gains, x_all, aa_high, aa_far, *refs):
    out = refs[-1]
    gain = gains[0, 0:1, :].astype(F32)
    rows = out.shape[0] // CHUNKS
    inner = aa_high[4 * RANK:, :].astype(F32) + aa_far[4 * RANK:, :].astype(F32)
    for c in range(CHUNKS):
        dx, keep, got, there, inv = refs[5 * c:5 * (c + 1)]
        x = chunk_of(x_all, c, rows)
        mine = inner[c * SPARE // 2:c * SPARE // 2 + 8, :rows].T[:, 0:1]
        inv = inv[...]
        grad = keep[:, LO] + got[:, LO].astype(F32) + there[...].astype(F32)
        grad = inv * (gain * grad) - x[...].astype(F32) * (inv * inv * mine / WIDTH)
        out[c * rows:(c + 1) * rows, :] = (dx[...] + grad).astype(BF16)


def high_sum_kernel(*refs):
    out = refs[-1]
    rows = out.shape[0] // (len(refs) // 2)
    for c in range(len(refs) // 2):
        keep, got = refs[2 * c:2 * c + 2]
        out[c * rows:(c + 1) * rows, :] = (keep[:, HI] + got[:, HI].astype(F32)).astype(BF16)


def high_sum(*pairs):
    args = [v for pair in pairs for v in pair]
    rows = sum(keep.shape[0] for keep, _ in pairs)
    return call(high_sum_kernel, None, (), args, [((rows, QUARTER), BF16)], [], "high_sum", 8)[0]


def split_refs(refs, counts):
    groups = []
    for count in counts:
        groups.append(refs[:count])
        refs = refs[count:]
    return groups, refs


def with_entry(parts, at, use):
    start = 0
    for ref in parts:
        @pl.when((at >= start) & (at < start + ref.shape[0]))
        def _(ref=ref, start=start):
            use(ref, at - start)
        start += ref.shape[0]


def sum_slots(info, owners, out_refs, one_slot):
    count = out_refs[0].shape[0]
    base = pl.program_id(0) * count
    slots = owners.shape[0]
    for ref in out_refs:
        ref[...] = jnp.zeros_like(ref)

    def add(slot, carry):
        owner = owners[slot] - base

        @pl.when((owner >= 0) & (owner < count))
        def _():
            one_slot(owner, entry_of(slot, info[3], slots))
        return carry

    lax.fori_loop(0, slots, add, 0)


def feedforward_sum_kernel(counts, info, owners, *refs):
    (b_parts, *a_parts), outs = split_refs(refs, counts)
    ga, gdb, gb, gda = outs
    me = info[0]

    def one_slot(owner, at):
        def add_b(ref, e):
            for i in range(gda.shape[2] // QUARTER):
                cols = slice(i * QUARTER, (i + 1) * QUARTER)
                base = i * 3 * RANK
                gb[owner, 0, :, cols] += ref[e, base:base + RANK, :].astype(F32)
                gb[owner, 1, :, cols] += ref[e, base + RANK:base + 2 * RANK, :].astype(F32)
                gda[owner, :, cols] += ref[e, base + 2 * RANK:base + 3 * RANK, :].astype(F32)

        with_entry(b_parts, at, add_b)
        for near_bit, parts in enumerate(a_parts):
            def add_a(ref, e, near_bit=near_bit):
                for r, cols in ((near_bit, LO), (near_bit ^ 2, HI)):
                    ga[owner, :, quarter(me, r)] += ref[e, :2 * RANK, cols].astype(F32)
                    gdb[owner, :, quarter(me, r)] += ref[e, 2 * RANK:, cols].astype(F32)

            with_entry(parts, at, add_a)

    sum_slots(info, owners, outs, one_slot)


def attention_sum_kernel(counts, info, owners, *refs):
    (b_parts, *a_parts), outs = split_refs(refs, counts)
    ga, gob, gq, gkv, goa = outs
    me = info[0]
    kv_cols = gkv.shape[3]

    def one_slot(owner, at):
        def add_b(ref, e):
            gq[owner] += ref[e, :RANK, :].astype(F32)
            goa[owner] += ref[e, RANK:2 * RANK, :].astype(F32)
            gkv[owner, 0] += ref[e, 2 * RANK:3 * RANK, :kv_cols].astype(F32)
            gkv[owner, 1] += ref[e, 2 * RANK:3 * RANK, kv_cols:2 * kv_cols].astype(F32)

        with_entry(b_parts, at, add_b)
        for r, parts in enumerate(a_parts):
            def add_a(ref, e, r=r):
                ga[owner, :, quarter(me, r)] += ref[e, :3 * RANK, :].astype(F32)
                gob[owner, :, quarter(me, r)] += ref[e, 3 * RANK:, :].astype(F32)

            with_entry(parts, at, add_a)

    sum_slots(info, owners, outs, one_slot)


def deal_kernel(slots, source, out, sems):
    made = [pltpu.make_async_copy(source.at[i], out.at[slots[i]], sems.at[i]) for i in range(source.shape[0])]
    for copy in made:
        copy.start()
    for copy in made:
        copy.wait()


def collect_kernel(slots, source, out, sems):
    made = [pltpu.make_async_copy(source.at[slots[i]], out.at[i], sems.at[i]) for i in range(source.shape[0])]
    for copy in made:
        copy.start()
    for copy in made:
        copy.wait()


def adapter_kernel(count, info, *refs):
    made = [pltpu.make_async_copy(refs[i].at[info[2]], refs[count + i], refs[-1].at[i]) for i in range(count)]
    for copy in made:
        copy.start()
    for copy in made:
        copy.wait()


def load_adapters(arrays, info):
    count = len(arrays)
    return pl.pallas_call(
        functools.partial(adapter_kernel, count),
        in_specs=[pl.BlockSpec(memory_space=pltpu.SMEM)] + [pl.BlockSpec(memory_space=pltpu.HBM)] * count,
        out_specs=[pl.BlockSpec(memory_space=pltpu.VMEM)] * count,
        out_shape=[pltpu.VMEM(a.shape[1:], a.dtype) for a in arrays],
        scratch_shapes=[pltpu.SemaphoreType.DMA((count,))],
        compiler_params=pltpu.CompilerParams(vmem_limit_bytes=MIB),
        cost_estimate=pl.CostEstimate(flops=1000, transcendentals=0, bytes_accessed=1000),
        name="adapters",
    )(info, *(in_hbm(a) for a in arrays))


def move_rows(kernel, value, slots, name, outs, in_space, out_space, sems):
    return pl.pallas_call(
        kernel,
        in_specs=[pl.BlockSpec(memory_space=pltpu.SMEM), pl.BlockSpec(memory_space=in_space)],
        out_specs=[pl.BlockSpec(memory_space=out_space)] * len(outs),
        out_shape=outs,
        scratch_shapes=[pltpu.SemaphoreType.DMA(sems)],
        compiler_params=pltpu.CompilerParams(vmem_limit_bytes=MIB),
        cost_estimate=pl.CostEstimate(flops=1000, transcendentals=0, bytes_accessed=1000),
        name=name,
    )(slots, pltpu.with_memory_space_constraint(value, in_space))


def sds(shape, dtype):
    return jax.ShapeDtypeStruct(tuple(shape), dtype)


def in_vmem(value):
    return pltpu.with_memory_space_constraint(value, pltpu.VMEM)


def in_hbm(value):
    return pltpu.with_memory_space_constraint(value, pltpu.HBM)


def call(kernel, info, weights, args, outs, scratch, name, mib, after=(), sems=()):
    vmem = pl.BlockSpec(memory_space=pltpu.VMEM)
    scalars = () if info is None else (info,)
    n, w = len(scalars), len(weights)

    def body(*refs):
        at = n + w + len(args)
        kernel(*refs[:at], *refs[at + len(after):])

    return pl.pallas_call(
        body,
        in_specs=[pl.BlockSpec(memory_space=pltpu.SMEM)] * n + [pl.BlockSpec(memory_space=pltpu.HBM)] * w + [vmem] * len(args)
        + [pl.BlockSpec(memory_space=pl.ANY)] * len(after),
        out_specs=[vmem] * len(outs),
        out_shape=[pltpu.VMEM(tuple(s), d) for s, d in outs],
        scratch_shapes=[pltpu.VMEM(s, d) for s, d in scratch] + ([pltpu.SemaphoreType.DMA(sems)] if sems else []),
        compiler_params=pltpu.CompilerParams(vmem_limit_bytes=mib * MIB),
        cost_estimate=pl.CostEstimate(flops=1000, transcendentals=0, bytes_accessed=1000),
        name=name,
    )(*scalars, *(in_hbm(a) for a in weights), *(in_vmem(a) for a in args), *after)


def whole_spec(value):
    zeros = (0,) * value.ndim
    return pl.BlockSpec(value.shape, lambda i, *_: zeros)


def sum_call(kernel, scalars, groups, outs, name):
    args = [v for group in groups for v in group]
    steps = 2
    specs = [pl.BlockSpec((o.shape[0] // steps,) + o.shape[1:], (lambda n: lambda i, *_: (i,) + (0,) * n)(o.ndim - 1))
             for o in outs]
    return pl.pallas_call(
        functools.partial(kernel, [len(group) for group in groups]),
        grid_spec=pltpu.PrefetchScalarGridSpec(
            num_scalar_prefetch=len(scalars), grid=(steps,),
            in_specs=[whole_spec(a) for a in args], out_specs=specs),
        out_shape=outs,
        compiler_params=pltpu.CompilerParams(
            dimension_semantics=("arbitrary",),
            vmem_limit_bytes=4 * MIB + 2 * sum(a.size * a.dtype.itemsize for a in args)
            + sum(o.size * o.dtype.itemsize for o in outs)),
        cost_estimate=pl.CostEstimate(flops=0, transcendentals=0, bytes_accessed=12000000),
        name=name,
    )(*scalars, *args)


def swap(value, bit, axis, size):
    return lax.ppermute(value, axis, [(i, i ^ bit) for i in range(size)])


def near(value):
    return swap(value, 1, "mp", PARTS)


def far(value):
    return swap(value, 2, "mp", PARTS)


def spread(value):
    there = far(value)
    return (value, near(value), there, near(there))


def far_sum_kernel(own, got, out):
    for to, other in ((LO, HI), (HI, LO)):
        out[:, to] = (own[:, to].astype(F32) + got[:, other].astype(F32)).astype(BF16)


def far_sum(own, got):
    return call(far_sum_kernel, None, (), (own, got), [(own.shape, BF16)], [], "far_sum", 6)[0]


def pair_sum_kernel(keep, got, out):
    out[...] = (keep[...] + got[...].astype(F32)).astype(BF16)


def pair_sum(keep, send, *before):
    got = near(send)
    got = late(got, *before) if before else got
    return call(pair_sum_kernel, None, (), (keep, got), [(send.shape, BF16)], [], "pair_sum", 6)[0]


def late(value, *others):
    return lax.optimization_barrier((value, *others))[0]


def doubled(stack, bit, size):
    return jnp.concatenate([stack, swap(stack, bit, "dp", size)], axis=0)


def entry_of(slot, place, size):
    bits = size.bit_length() - 1
    apart = slot ^ place
    return sum(((apart >> b) & 1) << (bits - 1 - b) for b in range(bits))


def shards(dp, residual, attention_gain, query_matrix, key_value_matrix, output_matrix, feedfwd_gain,
           gate_up_matrix, down_matrix, attention_adapter_input, query_adapter_output,
           key_value_adapter_output, output_adapter_input, output_adapter_output, feedfwd_adapter_input,
           feedfwd_adapter_output, down_adapter_input, down_adapter_output, lengths, adapter_index,
           dealing_slots, cotangent):
    seqs = residual.shape[0]
    length = cotangent.shape[1]
    units = down_matrix.shape[0]
    adapters = attention_adapter_input.shape[0]
    q_cols = query_matrix.shape[1]
    kv_cols = key_value_matrix.shape[2]
    kv_heads = kv_cols // HEAD
    heads = q_cols // HEAD
    rows = length // CHUNKS
    half = 2 * QUARTER
    me = lax.axis_index("mp")
    place = lax.axis_index("dp")

    is_there = dealing_slots[None, :] == jnp.arange(seqs, dtype=jnp.int32)[:, None]
    owners = jnp.sum(jnp.where(is_there, adapter_index[None, :], 0), axis=1)
    spans = jnp.sum(jnp.where(is_there, lengths[None, :], 0), axis=1)
    mine = jnp.arange(seqs, dtype=jnp.int32) == place
    my_length = jnp.sum(jnp.where(mine, spans, 0))
    my_adapter = jnp.sum(jnp.where(mine, owners, 0))
    info = jnp.stack([me.astype(jnp.int32), my_length, my_adapter, place.astype(jnp.int32)])

    gs = spread(cotangent[0])
    gains = jnp.stack(spread(jnp.stack([attention_gain, feedfwd_gain])))
    ordered, = move_rows(deal_kernel, residual, dealing_slots, "deal", [pltpu.VMEM(residual.shape, BF16)], pltpu.HBM,
                         pltpu.VMEM, (seqs,))
    dealt = lax.all_to_all(ordered, "dp", split_axis=0, concat_axis=1, tiled=True)[0]
    adapters_here = load_adapters(
        (attention_adapter_input, query_adapter_output, key_value_adapter_output, output_adapter_input,
         output_adapter_output, feedfwd_adapter_input, feedfwd_adapter_output, down_adapter_input,
         down_adapter_output), info)
    a1, qb, kvb, oa, ob, a2, fba, da, bd = adapters_here
    dealt = late(dealt, gs[2], a1, gains)
    beside = near(dealt)
    there = [far(dealt[c * rows:(c + 1) * rows]) for c in range(CHUNKS)]
    xs = [None] * CHUNKS
    cos_np, sin_np = rope_tables(length)
    cos = [jnp.asarray(cos_np[:, c * rows:(c + 1) * rows]) for c in range(CHUNKS)]
    sin = [jnp.asarray(sin_np[:, c * rows:(c + 1) * rows]) for c in range(CHUNKS)]
    wq, wkv, wo = query_matrix, key_value_matrix, output_matrix

    def like(*arrays):
        return [(a.shape, a.dtype) for a in arrays]

    wide, col, block, thin = (rows, WIDTH), (rows, half), (rows, QUARTER), (rows, 1)
    saved, kept, z_own, z_far = ([None] * CHUNKS for _ in range(4))
    order = ()
    for c in range(CHUNKS):
        xs[c] = (dealt, beside, there[c], near(late(there[c], saved[0][0]) if c else there[c]))
        outs = [((3 * RANK, rows), BF16), ((q_cols, rows), BF16), ((kv_heads, rows, HEAD), BF16),
                ((kv_heads, rows, HEAD), BF16), ((kv_cols, rows), BF16), ((kv_cols, rows), BF16)]
        saved[c] = call(
            functools.partial(project_kernel, c), info, (wq, wkv), (*xs[c], gains, a1, qb, kvb, cos[c], sin[c]), outs,
            [(wide, BF16)] + like(wq, wkv), "project_%d" % c, 12, order, (2,))
        outs = [(col, F32), (col, BF16), ((q_cols, rows), BF16), ((heads, rows), F32), ((RANK, rows), BF16)]
        pairs = [v for p in saved[:c + 1] for v in (p[2], p[5])]
        z_keep, z_send, *kept[c] = call(
            functools.partial(attend_kernel, c), info, (wo,), (saved[c][1], oa, ob, *pairs), outs, like(wo),
            "attend_%d" % c, 10, (saved[c][0],), (1,))
        z_own[c] = pair_sum(z_keep, late(z_send, z_far[0] if c else there[-1]))
        z_far[c] = far(z_own[c])
        order = (kept[c][1], z_own[c])
    def front(c, total, partial, order):
        hidden = (rows, units)
        outs = [(wide, BF16), (block, F32), (wide, BF16), (wide, BF16), (hidden, BF16), (hidden, BF16), (hidden, BF16),
                ((rows, 2 * RANK), BF16), ((rows, RANK), BF16),
                ((3 * RANK * units // QUARTER, QUARTER), BF16 if c else F32)]
        args = (*xs[c], total, near(total), *gs, gains, a2, bd, fba, da, *partial)
        weights = () if c else (gate_up_matrix, down_matrix)
        outs += like(*weights)
        return call(
            functools.partial(front_kernel, c, c == CHUNKS - 1), info, weights, (wgu, wd, *args) if c else args, outs,
            [((ROW_BLOCK, WIDTH), F32)], "front_%d" % c, 8, order, () if c else (2, units // QUARTER))

    def back(c, hidden, partial, order):
        first = col if c else (rows + 3 * RANK, half)
        outs = [((rows, RANK), F32), (first, F32), (first, BF16)]
        outs += [((3 * RANK, WIDTH), F32)] if c else []
        return call(
            functools.partial(back_kernel, c == 0), info, (), (wgu, *hidden[2:7], a2, fba, da, *partial), outs,
            [(block, F32), ((3 * RANK, QUARTER), F32)], "back_%d" % c, 8, order)

    def down(c, td, order):
        return call(down_kernel, info, (), (wd, hidden[c][4], td, bd, hidden[c][1]), [(col, F32), (col, BF16)],
                    [(block, F32)], "down_%d" % c, 6, order)

    def attend_back(c, total, partial, order):
        outs = [(block, F32), (col, F32), (col, BF16), (thin, F32), ((3 * RANK, QUARTER), F32 if c else BF16)]
        low = (4 * RANK + SPARE, half)
        outs += ([((4 * RANK, WIDTH), F32), ((kv_cols, rows), F32), ((kv_cols, rows), F32), ((SPARE // 2, rows), F32)]
                 if c else [(low, F32), (low, BF16)])
        scratch = [(wide, BF16), (wide, BF16), ((ROW_BLOCK, WIDTH), F32), ((q_cols, rows), BF16), ((q_cols, rows), F32),
                   ((c + 1, kv_cols, rows), F32), ((c + 1, kv_cols, rows), F32), ((rows, q_cols + 2 * kv_cols), BF16),
                   (block, F32), ((4 * RANK, QUARTER), F32)]
        triples = [v for p in saved[:c + 1] for v in (p[2], p[3], p[4])]
        return call(
            functools.partial(attend_back_kernel, c, c == 0), info, (wq, wkv, wo),
            (*xs[c], *gs, hidden[c][0], total, near(total), gains, a1, qb, kvb, oa, ob, cos[c], sin[c], *saved[c][:2],
             *kept[c], *triples, *partial), outs, scratch + like(wq, wkv, wo), "attend_back_%d" % c, 18, order, (3,))

    bits = [1 << b for b in reversed(range(dp.bit_length() - 1))]
    def to_bands(value):
        return lax.all_to_all(value.reshape(dp, length // dp, QUARTER), "dp", split_axis=0, concat_axis=0, tiled=True)

    def collect(value, name, *before):
        rows_out = sds((seqs, length // dp, QUARTER), BF16)
        return move_rows(collect_kernel, value, late(dealing_slots, *before), name, [rows_out], pltpu.VMEM, pl.ANY,
                         (seqs,))[0]

    hidden, d_own, d_far, y_keep, y_got = ([None] * CHUNKS for _ in range(5))
    *hidden[0], wgu, wd = front(0, far_sum(z_own[0], z_far[0]), (), order)
    step = hidden[0][8]
    hidden[1] = front(1, far_sum(z_own[1], late(z_far[1], step)), hidden[0][9:], (step,))
    td_1, d_keep, d_send, fa = back(1, hidden[1], (), (hidden[1][8],))
    d_own[1] = pair_sum(d_keep, d_send)
    d_far[1] = far(d_own[1])
    fb = late(hidden[1][9], d_own[1])[None]
    fb_first = swap(fb, bits[0], "dp", dp)
    td_0, d_keep, d_send = back(0, hidden[0], (fa,), (d_own[1],))
    total = far_sum(d_own[1], late(d_far[1], td_0))
    d_own[0] = pair_sum(d_keep, late(d_send, fb_first, d_far[1]))
    d_far[0] = far(d_own[0])
    fb = fb_more = jnp.concatenate([fb, late(fb_first, d_own[0])], axis=0)
    for bit in bits[1:-1]:
        fb_more = doubled(fb_more, bit, dp)
    fb_more = fb_more[2:]
    fb_side = swap(fb, bits[-1], "dp", dp)
    dxq, h_keep, h_send, inv, *sums = attend_back(1, total, (), (d_own[0],))
    total = far_sum(d_own[0], late(d_far[0], inv))
    h_got = near(late(h_send, fb_more, fb_side))
    fb_more_side = swap(fb_more, bits[-1], "dp", dp)
    h_high = high_sum((h_keep, h_got))
    h_far = far(h_high)
    final = [None, (dxq, h_keep, h_got, h_far, inv)]
    fa = total[rows:][None]
    fa_first = swap(fa, bits[0], "dp", dp)
    dxq, h_keep, h_send, inv, att_b, aa_keep, aa_send = attend_back(0, total, sums, (h_high,))
    ready = (fa_first, h_far, fb_more_side)
    aa_got = near(late(aa_send, *ready))
    aa_high = high_sum((aa_keep, aa_got))
    aa_far = far(aa_high)
    h_got = near(late(h_send, *ready))
    h_high = high_sum((h_keep, h_got))
    h_far = far(h_high)
    final[0] = (dxq, h_keep, h_got, h_far, inv)
    att_a = aa_keep[:4 * RANK, :QUARTER] + aa_got[:4 * RANK, :QUARTER].astype(F32)
    att_a = (att_a + late(aa_far, h_high)[:4 * RANK].astype(F32)).astype(BF16)
    n_b = att_b.shape[0]
    att = jnp.concatenate([att_b, att_a], axis=0)[None]
    y_keep[0], y_send = down(0, td_0, (att,))
    y_got[0] = near(y_send)
    att = first = doubled(att, bits[0], dp)
    att = late(att, h_far, y_send)
    for bit in bits[1:-1]:
        att = doubled(att, bit, dp)
    fa = late(jnp.concatenate([fa, fa_first], axis=0), aa_high)
    for bit in bits[1:-1]:
        fa = doubled(fa, bit, dp)
    fa_side = swap(fa, bits[-1], "dp", dp)
    y_keep[1], y_send = down(1, td_1, (first, y_send))
    y_got[1] = near(y_send)
    y_far = far(high_sum(*((k, late(g, h_far)) for k, g in zip(y_keep, y_got))))

    dinput, = call(finish_kernel, None, (), (gains, dealt, aa_high, aa_far, *(v for f in final for v in f)),
                   [((length, QUARTER), BF16)], [], "finish", 8, (att, fa_side, y_send))
    input_grad = collect(to_bands(dinput), "collect_grad")
    outs = [sds((adapters, 2 * RANK, WIDTH), F32), sds((adapters, RANK, WIDTH), F32),
            sds((adapters, 2, RANK, units), F32), sds((adapters, RANK, units), F32)]
    ga_ffn, g_down_b, g_ffn_b, g_down_a = sum_call(
        feedforward_sum_kernel, (info, owners),
        ((fb, fb_more, fb_side, fb_more_side), (fa, fa_side), (near(fa), near(fa_side))), outs, "feedforward_sum")

    result, = call(output_kernel, info, (), (late(y_far, dinput, g_down_a), *(v for p in zip(y_keep, y_got) for v in p)),
                   [((length, QUARTER), BF16)], [], "output", 8)
    output = collect(to_bands(result), "collect_out", input_grad)

    att_side = swap(att, bits[-1], "dp", dp)
    a_parts = [att[:, n_b:], att_side[:, n_b:]]
    a_far = [far(v) for v in a_parts]
    outs = [sds((adapters, 3 * RANK, WIDTH), F32), sds((adapters, RANK, WIDTH), F32),
            sds((adapters, RANK, q_cols), F32), sds((adapters, 2, RANK, kv_cols), F32),
            sds((adapters, RANK, q_cols), F32)]
    ga_att, g_out_b, g_query_b, g_kv_b, g_out_a = sum_call(
        attention_sum_kernel, (info, owners),
        ((att, att_side), a_parts, [near(v) for v in a_parts], a_far, [near(v) for v in a_far]), outs, "attention_sum")
    return (output, input_grad, ga_att, g_query_b, g_kv_b, g_out_a, g_out_b, ga_ffn, g_ffn_b, g_down_a, g_down_b)


def solution(mesh):
    in_specs = (
        P(None, "dp", "mp"), P("mp"), P(None, "mp"), P(None, None, "mp"), P("mp", None), P("mp"),
        P(None, None, "mp"), P("mp", None), P(), P(None, None, "mp"), P(None, None, None, "mp"),
        P(None, None, "mp"), P(), P(), P(None, None, None, "mp"), P(None, None, "mp"), P(), P(), P(), P(),
        P("dp", None, "mp"),
    )
    out_specs = (
        P(None, "dp", "mp"), P(None, "dp", "mp"), P(), P(None, None, "mp"), P(None, None, None, "mp"),
        P(None, None, "mp"), P(), P(), P(None, None, None, "mp"), P(None, None, "mp"), P(),
    )
    return jax.shard_map(
        functools.partial(shards, mesh.shape["dp"]), mesh=mesh, in_specs=in_specs, out_specs=out_specs,
        check_vma=False)
```

```python
import functools

import jax
import jax.numpy as jnp
import numpy as np
from jax import lax
from jax.experimental import pallas as pl
from jax.experimental.pallas import tpu as pltpu
from jax.sharding import PartitionSpec as P

WIDTH = 2048
HEAD = 64
HALF = HEAD // 2
RANK = 16
EPS = 1e-05
ROPE_BASE = 500000.0
NEG_FILL = -1e30
PARTS = 4
LANES = 128
SPARE = 32
ROW_BLOCK = 64
QUARTER = WIDTH // PARTS
CHUNKS = 2
MIB = 1024 * 1024
F32 = jnp.float32
BF16 = jnp.bfloat16


def nn(a, b):
    return lax.dot_general(a, b, (((1,), (0,)), ((), ())), preferred_element_type=F32)


def nt(a, b):
    return lax.dot_general(a, b, (((1,), (1,)), ((), ())), preferred_element_type=F32)


def rope_tables(length):
    freq = ROPE_BASE ** (-np.arange(HALF, dtype=np.float32) * np.float32(2.0 / HEAD))
    angles = (np.arange(length, dtype=np.float32)[None, :] * freq.astype(np.float32)[:, None]).astype(np.float32)
    return np.cos(angles).astype(np.float32), np.sin(angles).astype(np.float32)


def quarter(me, rel):
    return pl.ds(pl.multiple_of((me ^ rel) * QUARTER, QUARTER), QUARTER)


LO, HI = slice(0, QUARTER), slice(QUARTER, 2 * QUARTER)


def total_block(rel, rows_at, own, oth):
    return (own if rel in (0, 2) else oth)[rows_at, LO if rel in (0, 1) else HI].astype(F32)


def store_block(rel, value, rows_at, keep_ref, send_ref):
    to = pl.ds(pl.multiple_of((rel // 2) * QUARTER, QUARTER), QUARTER)

    @pl.when(rel % 2 == 0)
    def _():
        keep_ref[rows_at, to] = value[...]

    @pl.when(rel % 2 == 1)
    def _():
        send_ref[rows_at, to] = value[...].astype(BF16)


def chunk_of(ref, chunk, rows):
    return ref if ref.shape[0] == rows else ref.at[chunk * rows:(chunk + 1) * rows]


def row_block(i):
    return pl.ds(pl.multiple_of(i * ROW_BLOCK, ROW_BLOCK), ROW_BLOCK)


def is_valid(chunk, i, rows, length):
    return chunk * rows + i * ROW_BLOCK + lax.broadcasted_iota(jnp.int32, (ROW_BLOCK, 1), 0) < length


def copies_of(pairs, sems):
    made = [pltpu.make_async_copy(source, target, sems.at[i]) for i, (source, target) in enumerate(pairs)]
    for copy in made:
        copy.start()
    return made


def put_block(rel, value, keep_ref, send_ref):
    ref = keep_ref if rel in (0, 2) else send_ref
    ref[:, LO if rel in (0, 1) else HI] = value.astype(ref.dtype)


def rotate(value, cos, sin, out_ref):
    for i in range(value.shape[0] // HEAD):
        u1, u2 = value[i * HEAD:i * HEAD + HALF], value[i * HEAD + HALF:(i + 1) * HEAD]
        out_ref[i * HEAD:i * HEAD + HALF, :] = (u1 * cos - u2 * sin).astype(BF16)
        out_ref[i * HEAD + HALF:(i + 1) * HEAD, :] = (u2 * cos + u1 * sin).astype(BF16)


def turn_back(value, cos, sin, out_ref):
    for i in range(value.shape[0] // HEAD):
        w1, w2 = value[i * HEAD:i * HEAD + HALF], value[i * HEAD + HALF:(i + 1) * HEAD]
        out_ref[i * HEAD:i * HEAD + HALF, :] = (w1 * cos + w2 * sin).astype(BF16)
        out_ref[i * HEAD + HALF:(i + 1) * HEAD, :] = (w2 * cos - w1 * sin).astype(BF16)


def head_rows(i):
    return pl.ds(pl.multiple_of(i * HEAD, HEAD), HEAD)


def visible(key_start, query_start, rows, length):
    kpos = key_start + lax.broadcasted_iota(jnp.int32, (rows, rows), 0)
    qpos = query_start + lax.broadcasted_iota(jnp.int32, (rows, rows), 1)
    return (kpos <= qpos) & (kpos < length)


def project_kernel(chunk, info, wq_h, wkv_h, x0, x1, x2, x3, gains, a1, qb, kvb, cos_t, sin_t,
                   t1t_out, qt_out, kn_out, vn_out, kt_out, vt_out, h_out, wq, wkv, sems):
    copies = copies_of(((wkv_h, wkv), (wq_h, wq)), sems)
    me = info[0]
    rows = h_out.shape[0]
    kv_heads = kn_out.shape[0]
    xs = [chunk_of(x, chunk, rows) for x in (x0, x1, x2, x3)]

    def norm(i, carry):
        at = row_block(i)
        square = jnp.zeros((ROW_BLOCK, 1), F32)
        for r in range(PARTS):
            v = xs[r][at, :].astype(F32)
            square = square + jnp.sum(v * v, axis=1, keepdims=True)
        inv = lax.rsqrt(square / WIDTH + EPS)
        for r in range(PARTS):
            v = xs[r][at, :].astype(F32)
            h_out[at, quarter(me, r)] = (v * inv * gains[r, 0:1, :].astype(F32)).astype(BF16)
        return carry

    lax.fori_loop(0, rows // ROW_BLOCK, norm, 0)
    h = h_out[...]
    t1 = nt(h, a1[...])
    t1t_out[...] = t1.T.astype(BF16)
    t1b = t1.astype(BF16)
    cos, sin = cos_t[...], sin_t[...]
    copies[0].wait()
    k = nn(h, wkv[0]) + nn(t1b[:, RANK:2 * RANK], kvb[0])
    rotate(k.T, cos, sin, kt_out)
    k_n = kt_out[...].T
    v_n = (nn(h, wkv[1]) + nn(t1b[:, 2 * RANK:], kvb[1])).astype(BF16)
    vt_out[...] = v_n.T
    for i in range(kv_heads):
        kn_out[i] = k_n[:, i * HEAD:(i + 1) * HEAD]
        vn_out[i] = v_n[:, i * HEAD:(i + 1) * HEAD]
    copies[1].wait()
    q = nn(h, wq[...]) + nn(t1b[:, :RANK], qb[...])
    rotate(q.T * (HEAD ** -0.5), cos, sin, qt_out)


def attend_kernel(chunk, info, wo_h, qt, oa, ob, *rest):
    pairs, rest = rest[:2 * (chunk + 1)], rest[2 * (chunk + 1):]
    z_keep, z_send, ot_out, lse_out, tot_out, wo, sems = rest
    copies = copies_of(((wo_h, wo),), sems)
    keys, values = pairs[0::2], pairs[1::2]
    me, length = info[0], info[1]
    rows = qt.shape[1]
    kv_heads = keys[0].shape[0]
    heads = qt.shape[0] // HEAD
    group = heads // kv_heads

    kept = [jnp.concatenate([visible(c * rows, chunk * rows, rows, length)] * group, axis=1) for c in range(chunk + 1)]

    def one_group(j, carry):
        q_g = jnp.concatenate([qt[head_rows(j * group + g), :] for g in range(group)], axis=1)
        parts = [jnp.where(kept[c], nn(keys[c][j], q_g), NEG_FILL) for c in range(chunk + 1)]
        top = functools.reduce(jnp.maximum, [jnp.max(s, axis=0, keepdims=True) for s in parts])
        es = [jnp.exp(s - top) for s in parts]
        total = sum(jnp.sum(e, axis=0, keepdims=True) for e in es)
        low = top + jnp.log(total)
        o_t = sum(nn(value[head_rows(j), :], e.astype(BF16)) for value, e in zip(values, es))
        o_t = (o_t / total).astype(BF16)
        for g in range(group):
            cols = slice(g * rows, (g + 1) * rows)
            lse_out[pl.ds(j * group + g, 1), :] = low[:, cols]
            ot_out[head_rows(j * group + g), :] = o_t[:, cols]
        return carry

    lax.fori_loop(0, kv_heads, one_group, 0)
    o = ot_out[...].T
    to = nt(o, oa[...])
    tot_out[...] = to.T.astype(BF16)
    to = to.astype(BF16)
    copies[0].wait()
    for r in range(PARTS):
        at = quarter(me, r)
        put_block(r, nn(o, wo[:, at]) + nn(to, ob[:, at]), z_keep, z_send)


def front_kernel(chunk, last, info, wgu_in, wd_in, x0, x1, x2, x3, zo, zp, g0, g1, g2, g3, gains, a2, bd, fb, da,
                 *rest):
    units = wd_in.shape[0]
    if chunk:
        wgu, wd = wgu_in, wd_in
    else:
        (wgu, wd, f_s, sems), rest = rest[-4:], rest[:-4]
        rest = (*rest, f_s)

    def copies(i):
        c = pl.ds(pl.multiple_of(i * QUARTER, QUARTER), QUARTER)
        return (pltpu.make_async_copy(wgu_in.at[:, :, c], wgu.at[:, :, c], sems.at[0, i]),
                pltpu.make_async_copy(wd_in.at[c, :], wd.at[c, :], sems.at[1, i]))

    if not chunk:
        for i in range(units // QUARTER):
            for copy in copies(i):
                copy.start()
    f_s = rest[-1]
    xm_out, xq_out, h_out, g_out, act_out, dg_out, du_out, t2_s, dtd_s, b_out = rest[-11:-1]
    me, length = info[0], info[1]
    rows = h_out.shape[0]
    xs, gs = ([chunk_of(v, chunk, rows) for v in vs] for vs in ((x0, x1, x2, x3), (g0, g1, g2, g3)))

    def norm(i, carry):
        at = row_block(i)
        valid = is_valid(chunk, i, rows, length)
        square = jnp.zeros((ROW_BLOCK, 1), F32)
        for r in range(PARTS):
            v = xs[r][at, :].astype(F32) + total_block(r, at, zo, zp)
            if r == 0:
                xq_out[at, :] = v
            f_s[:, quarter(me, r)] = v
            square = square + jnp.sum(v * v, axis=1, keepdims=True)
            g_out[at, quarter(me, r)] = jnp.where(valid, gs[r][at, :], jnp.zeros((), BF16))
        inv = lax.rsqrt(square / WIDTH + EPS)
        for r in range(PARTS):
            v = f_s[:, quarter(me, r)]
            xm_out[at, quarter(me, r)] = v.astype(BF16)
            h_out[at, quarter(me, r)] = (v * inv * gains[r, 1:2, :].astype(F32)).astype(BF16)
        return carry

    lax.fori_loop(0, rows // ROW_BLOCK, norm, 0)
    t2 = nt(h_out[...], a2[...])
    t2_s[...] = t2.astype(BF16)
    dtd = nt(g_out[...], bd[...])
    dtd_s[...] = dtd.astype(BF16)
    t2t, dtdt = t2.T.astype(BF16), dtd.T.astype(BF16)

    def block(i, carry):
        c = pl.ds(pl.multiple_of(i * QUARTER, QUARTER), QUARTER)
        if not chunk:
            for copy in copies(i):
                copy.wait()
        h, g = h_out[...], g_out[...]
        gate = nn(h, wgu[0, :, c]) + nn(t2_s[:, :RANK], fb[0, :, c])
        up = nn(h, wgu[1, :, c]) + nn(t2_s[:, RANK:], fb[1, :, c])
        dact = nt(g, wd[c, :]) + nn(dtd_s[...], da[:, c])
        sig = 1.0 / (1.0 + jnp.exp(-gate))
        silu = gate * sig
        act = (silu * up).astype(BF16)
        dgate = (dact * up * sig * (1.0 + gate * (1.0 - sig))).astype(BF16)
        dup = (dact * silu).astype(BF16)
        act_out[:, c], dg_out[:, c], du_out[:, c] = act, dgate, dup
        for k, value in enumerate((nn(t2t[:RANK], dgate), nn(t2t[RANK:], dup), nn(dtdt, act))):
            at = pl.ds(pl.multiple_of((3 * i + k) * RANK, RANK), RANK)
            if last:
                value = value + rest[0][at, :]
            b_out[at, :] = value.astype(b_out.dtype)
        return carry

    lax.fori_loop(0, units // QUARTER, block, 0)


def back_kernel(last, info, wgu, h, g, act, dg, du, a2, fb, da, *rest):
    (value_s, low_s), rest = rest[-2:], rest[:-2]
    outs, rest = (rest[-3:], rest[:-3]) if last else (rest[-4:], rest[:-4])
    td_out, d_keep, d_send = outs[:3]
    me = info[0]
    rows = h.shape[0]
    dt2 = jnp.concatenate([nt(dg[...], fb[0]), nt(du[...], fb[1])], axis=1)
    td = nt(act[...], da[...])
    td_out[...] = td
    dt2b = dt2.astype(BF16)
    dt2t, tdt = dt2.T.astype(BF16), td.T.astype(BF16)

    def block(r, carry):
        at = quarter(me, r)
        value_s[...] = nt(dg[...], wgu[0, at, :]) + nt(du[...], wgu[1, at, :]) + nn(dt2b, a2[:, at])
        store_block(r, value_s, slice(0, rows), d_keep, d_send)
        low_s[:2 * RANK, :] = nn(dt2t, h[:, at])
        low_s[2 * RANK:, :] = nn(tdt, g[:, at])
        if last:
            low_s[...] += rest[0][:, at]
            store_block(r, low_s, slice(rows, rows + 3 * RANK), d_keep, d_send)
        else:
            outs[3][:, at] = low_s[...]
        return carry

    lax.fori_loop(0, PARTS, block, 0)


def down_kernel(info, wd, act, td, bd, xq, y_keep, y_send, value_s):
    me = info[0]
    tdb = td[...].astype(BF16)

    def block(r, carry):
        at = quarter(me, r)
        value_s[...] = nn(act[...], wd[:, at]) + nn(tdb, bd[:, at])
        store_block(r, value_s, slice(0, act.shape[0]), y_keep, y_send)
        return carry

    lax.fori_loop(0, PARTS, block, 0)
    y_keep[:, LO] += xq[...]


def attend_back_kernel(chunk, last, info, wq_h, wkv_h, wo_h, x0, x1, x2, x3, g0, g1, g2, g3, xm, do_, dp, gains, a1,
                       qb, kvb, oa, ob, cos_t, sin_t, t1t, qt, ot, lse, tot, *rest):
    scratch, rest = rest[-14:], rest[:-14]
    h_in, z_s, f_s, dot_s, dqt_s, dkt_s, dvt_s, dq_s, value_s, low_s, wq, wkv, wo, sems = scratch
    copies = copies_of(((wo_h, wo), (wq_h, wq), (wkv_h, wkv)), sems)
    n_out = 7 if last else 9
    outs, rest = rest[-n_out:], rest[:-n_out]
    dxq_out, h_keep, h_send, inv_out, b_out = outs[:5]
    triples, rest = rest[:3 * (chunk + 1)], rest[3 * (chunk + 1):]
    keys, values, keys_t = triples[0::3], triples[1::3], triples[2::3]
    me, length = info[0], info[1]
    rows = xm.shape[0]
    kv_heads = keys[0].shape[0]
    heads = qt.shape[0] // HEAD
    group = heads // kv_heads
    q_cols, kv_cols = heads * HEAD, kv_heads * HEAD
    xs, gs = ([chunk_of(v, chunk, rows) for v in vs] for vs in ((x0, x1, x2, x3), (g0, g1, g2, g3)))

    def norm_back(i, carry):
        at = row_block(i)
        valid = is_valid(chunk, i, rows, length)
        square, first, inner = (jnp.zeros((ROW_BLOCK, 1), F32) for _ in range(3))
        for r in range(PARTS):
            v = xm[at, quarter(me, r)].astype(F32)
            square = square + jnp.sum(v * v, axis=1, keepdims=True)
            w = total_block(r, at, do_, dp) * gains[r, 1:2, :].astype(F32)
            f_s[:, quarter(me, r)] = w
            inner = inner + jnp.sum(v * w, axis=1, keepdims=True)
            u = xs[r][at, :].astype(F32)
            first = first + jnp.sum(u * u, axis=1, keepdims=True)
        inv_one = lax.rsqrt(first / WIDTH + EPS)
        inv_out[at, :] = inv_one
        inv = lax.rsqrt(square / WIDTH + EPS)
        back = inv * inv * inv * inner / WIDTH
        for r in range(PARTS):
            v = xm[at, quarter(me, r)].astype(F32)
            g = jnp.where(valid, gs[r][at, :].astype(F32), 0.0)
            d = g + inv * f_s[:, quarter(me, r)] - v * back
            if r == 0:
                dxq_out[at, :] = d
            z_s[at, quarter(me, r)] = d.astype(BF16)
            u = xs[r][at, :].astype(F32)
            h_in[at, quarter(me, r)] = (u * inv_one * gains[r, 0:1, :].astype(F32)).astype(BF16)
        return carry

    lax.fori_loop(0, rows // ROW_BLOCK, norm_back, 0)
    dz = z_s[...]
    dto = nt(dz, ob[...])
    copies[0].wait()
    d_o = nt(dz, wo[...]) + nn(dto.astype(BF16), oa[...])
    dot_s[...] = d_o.T.astype(BF16)
    kept = [jnp.concatenate([visible(c * rows, chunk * rows, rows, length)] * group, axis=1) for c in range(chunk + 1)]

    def one_group(j, carry):
        places = [head_rows(j * group + g) for g in range(group)]
        q_g = jnp.concatenate([qt[at, :] for at in places], axis=1)
        do_g = jnp.concatenate([dot_s[at, :] for at in places], axis=1)
        o_g = jnp.concatenate([ot[at, :] for at in places], axis=1)
        low = jnp.concatenate([lse[pl.ds(j * group + g, 1), :] for g in range(group)], axis=1)
        dots = jnp.sum(do_g.astype(F32) * o_g.astype(F32), axis=0, keepdims=True)
        dq_g = 0.0
        for c in range(chunk + 1):
            prob = jnp.where(kept[c], jnp.exp(nn(keys[c][j], q_g) - low), 0.0)
            ds = (prob * (nn(values[c][j], do_g) - dots)).astype(BF16)
            dq_g = dq_g + nn(keys_t[c][head_rows(j), :], ds)
            dk, dv = nt(q_g, ds), nt(do_g, prob.astype(BF16))
            if last:
                dk, dv = dk + rest[2][head_rows(j), :], dv + rest[3][head_rows(j), :]
            dkt_s[c, head_rows(j), :], dvt_s[c, head_rows(j), :] = dk, dv
        for g in range(group):
            dqt_s[places[g], :] = dq_g[:, g * rows:(g + 1) * rows]
        return carry

    lax.fori_loop(0, kv_heads, one_group, 0)
    if not last:
        outs[6][...], outs[7][...] = dkt_s[0], dvt_s[0]
    cos, sin = cos_t[...], sin_t[...]
    dto_t, o_t = dto.T.astype(BF16), ot[...]
    d_out_a = nt(dto_t, o_t)
    turn_back(dqt_s[...], cos * (HEAD ** -0.5), sin * (HEAD ** -0.5), dot_s)
    dq_s[:, :q_cols] = dot_s[...].T
    turn_back(dkt_s[chunk], cos, sin, dot_s)
    dq_s[:, q_cols:q_cols + kv_cols] = dot_s[:kv_cols, :].T
    dq_s[:, q_cols + kv_cols:] = dvt_s[chunk].T.astype(BF16)
    dq, dk, dv = dq_s[:, :q_cols], dq_s[:, q_cols:q_cols + kv_cols], dq_s[:, q_cols + kv_cols:]
    dt1 = jnp.concatenate([nt(dq, qb[...]), nt(dk, kvb[0]), nt(dv, kvb[1])], axis=1)
    dt1b = dt1.astype(BF16)
    kv_pad = jnp.zeros((RANK, QUARTER - 2 * kv_cols), F32)
    d_kv = jnp.concatenate([nn(t1t[RANK:2 * RANK, :], dk), nn(t1t[2 * RANK:, :], dv), kv_pad], axis=1)
    for k, value in enumerate((nn(t1t[:RANK, :], dq), d_out_a, d_kv)):
        at = slice(k * RANK, (k + 1) * RANK)
        if last:
            value = value + rest[0][at, :]
        b_out[at, :] = value.astype(b_out.dtype)
    dt1t = dt1.T.astype(BF16)
    copies[1].wait()
    copies[2].wait()

    def block(r, inner):
        at = quarter(me, r)
        d = nt(dq_s[:, :q_cols], wq[at, :]) + nn(dt1b, a1[:, at])
        d = d + nt(dq_s[:, q_cols:q_cols + kv_cols], wkv[0, at, :]) + nt(dq_s[:, q_cols + kv_cols:], wkv[1, at, :])
        value_s[...] = d
        store_block(r, value_s, slice(0, rows), h_keep, h_send)
        low_s[:3 * RANK, :] = nn(dt1t, h_in[:, at])
        low_s[3 * RANK:, :] = nn(tot[...], z_s[:, at])
        if last:
            low_s[...] += rest[1][:, at]
            store_block(r, low_s, slice(0, 4 * RANK), outs[5], outs[6])
        else:
            outs[5][:, at] = low_s[...]
        return inner + jnp.sum(d * h_in[:, at].astype(F32), axis=1, keepdims=True)

    inner = lax.fori_loop(0, PARTS, block, jnp.zeros((rows, 1), F32))
    inner = jnp.broadcast_to(inner, (rows, LANES)).T[:SPARE // 2, :]
    if last:
        for ref in outs[5:7]:
            for c, value in enumerate((inner, rest[4][...])):
                at = slice(4 * RANK + c * SPARE // 2, 4 * RANK + (c + 1) * SPARE // 2)
                ref[at, QUARTER:QUARTER + rows] = value.astype(ref.dtype)
                ref[at, QUARTER + rows:] = jnp.zeros((SPARE // 2, QUARTER - rows), ref.dtype)
                ref[at, :QUARTER] = jnp.zeros((SPARE // 2, QUARTER), ref.dtype)
    else:
        outs[8][...] = inner


def output_kernel(info, y_far, *refs):
    out = refs[-1]
    rows = out.shape[0] // CHUNKS
    for c in range(CHUNKS):
        y_keep, y_got = refs[2 * c:2 * (c + 1)]
        at = slice(c * rows, (c + 1) * rows)
        valid = c * rows + lax.broadcasted_iota(jnp.int32, (rows, 1), 0) < info[1]
        y = y_keep[:, LO] + y_got[:, LO].astype(F32) + y_far[at, :].astype(F32)
        out[at, :] = jnp.where(valid, y, 0.0).astype(BF16)


def finish_kernel(gains, x_all, aa_high, aa_far, *refs):
    out = refs[-1]
    gain = gains[0, 0:1, :].astype(F32)
    rows = out.shape[0] // CHUNKS
    inner = aa_high[4 * RANK:, :].astype(F32) + aa_far[4 * RANK:, :].astype(F32)
    for c in range(CHUNKS):
        dx, keep, got, there, inv = refs[5 * c:5 * (c + 1)]
        x = chunk_of(x_all, c, rows)
        mine = inner[c * SPARE // 2:c * SPARE // 2 + 8, :rows].T[:, 0:1]
        inv = inv[...]
        grad = keep[:, LO] + got[:, LO].astype(F32) + there[...].astype(F32)
        grad = inv * (gain * grad) - x[...].astype(F32) * (inv * inv * mine / WIDTH)
        out[c * rows:(c + 1) * rows, :] = (dx[...] + grad).astype(BF16)


def high_sum_kernel(*refs):
    out = refs[-1]
    rows = out.shape[0] // (len(refs) // 2)
    for c in range(len(refs) // 2):
        keep, got = refs[2 * c:2 * c + 2]
        out[c * rows:(c + 1) * rows, :] = (keep[:, HI] + got[:, HI].astype(F32)).astype(BF16)


def high_sum(*pairs):
    args = [v for pair in pairs for v in pair]
    rows = sum(keep.shape[0] for keep, _ in pairs)
    return call(high_sum_kernel, None, (), args, [((rows, QUARTER), BF16)], [], "high_sum", 8)[0]


def split_refs(refs, counts):
    groups = []
    for count in counts:
        groups.append(refs[:count])
        refs = refs[count:]
    return groups, refs


def with_entry(parts, at, use):
    start = 0
    for ref in parts:
        @pl.when((at >= start) & (at < start + ref.shape[0]))
        def _(ref=ref, start=start):
            use(ref, at - start)
        start += ref.shape[0]


def sum_slots(info, owners, out_refs, one_slot):
    count = out_refs[0].shape[0]
    base = pl.program_id(0) * count
    slots = owners.shape[0]
    for ref in out_refs:
        ref[...] = jnp.zeros_like(ref)

    def add(slot, carry):
        owner = owners[slot] - base

        @pl.when((owner >= 0) & (owner < count))
        def _():
            one_slot(owner, entry_of(slot, info[3], slots))
        return carry

    lax.fori_loop(0, slots, add, 0)


def feedforward_sum_kernel(counts, info, owners, *refs):
    (b_parts, *a_parts), outs = split_refs(refs, counts)
    ga, gdb, gb, gda = outs
    me = info[0]

    def one_slot(owner, at):
        def add_b(ref, e):
            for i in range(gda.shape[2] // QUARTER):
                cols = slice(i * QUARTER, (i + 1) * QUARTER)
                base = i * 3 * RANK
                gb[owner, 0, :, cols] += ref[e, base:base + RANK, :].astype(F32)
                gb[owner, 1, :, cols] += ref[e, base + RANK:base + 2 * RANK, :].astype(F32)
                gda[owner, :, cols] += ref[e, base + 2 * RANK:base + 3 * RANK, :].astype(F32)

        with_entry(b_parts, at, add_b)
        for near_bit, parts in enumerate(a_parts):
            def add_a(ref, e, near_bit=near_bit):
                for r, cols in ((near_bit, LO), (near_bit ^ 2, HI)):
                    ga[owner, :, quarter(me, r)] += ref[e, :2 * RANK, cols].astype(F32)
                    gdb[owner, :, quarter(me, r)] += ref[e, 2 * RANK:, cols].astype(F32)

            with_entry(parts, at, add_a)

    sum_slots(info, owners, outs, one_slot)


def attention_sum_kernel(counts, info, owners, *refs):
    (b_parts, *a_parts), outs = split_refs(refs, counts)
    ga, gob, gq, gkv, goa = outs
    me = info[0]
    kv_cols = gkv.shape[3]

    def one_slot(owner, at):
        def add_b(ref, e):
            gq[owner] += ref[e, :RANK, :].astype(F32)
            goa[owner] += ref[e, RANK:2 * RANK, :].astype(F32)
            gkv[owner, 0] += ref[e, 2 * RANK:3 * RANK, :kv_cols].astype(F32)
            gkv[owner, 1] += ref[e, 2 * RANK:3 * RANK, kv_cols:2 * kv_cols].astype(F32)

        with_entry(b_parts, at, add_b)
        for r, parts in enumerate(a_parts):
            def add_a(ref, e, r=r):
                ga[owner, :, quarter(me, r)] += ref[e, :3 * RANK, :].astype(F32)
                gob[owner, :, quarter(me, r)] += ref[e, 3 * RANK:, :].astype(F32)

            with_entry(parts, at, add_a)

    sum_slots(info, owners, outs, one_slot)


def deal_kernel(slots, source, out, sems):
    made = [pltpu.make_async_copy(source.at[i], out.at[slots[i]], sems.at[i]) for i in range(source.shape[0])]
    for copy in made:
        copy.start()
    for copy in made:
        copy.wait()


def collect_kernel(slots, source, out, sems):
    made = [pltpu.make_async_copy(source.at[slots[i]], out.at[i], sems.at[i]) for i in range(source.shape[0])]
    for copy in made:
        copy.start()
    for copy in made:
        copy.wait()


def adapter_kernel(count, info, *refs):
    made = [pltpu.make_async_copy(refs[i].at[info[2]], refs[count + i], refs[-1].at[i]) for i in range(count)]
    for copy in made:
        copy.start()
    for copy in made:
        copy.wait()


def load_adapters(arrays, info):
    count = len(arrays)
    return pl.pallas_call(
        functools.partial(adapter_kernel, count),
        in_specs=[pl.BlockSpec(memory_space=pltpu.SMEM)] + [pl.BlockSpec(memory_space=pltpu.HBM)] * count,
        out_specs=[pl.BlockSpec(memory_space=pltpu.VMEM)] * count,
        out_shape=[pltpu.VMEM(a.shape[1:], a.dtype) for a in arrays],
        scratch_shapes=[pltpu.SemaphoreType.DMA((count,))],
        compiler_params=pltpu.CompilerParams(vmem_limit_bytes=MIB),
        cost_estimate=pl.CostEstimate(flops=1000, transcendentals=0, bytes_accessed=1000),
        name="adapters",
    )(info, *(in_hbm(a) for a in arrays))


def move_rows(kernel, value, slots, name, outs, in_space, out_space, sems):
    return pl.pallas_call(
        kernel,
        in_specs=[pl.BlockSpec(memory_space=pltpu.SMEM), pl.BlockSpec(memory_space=in_space)],
        out_specs=[pl.BlockSpec(memory_space=out_space)] * len(outs),
        out_shape=outs,
        scratch_shapes=[pltpu.SemaphoreType.DMA(sems)],
        compiler_params=pltpu.CompilerParams(vmem_limit_bytes=MIB),
        cost_estimate=pl.CostEstimate(flops=1000, transcendentals=0, bytes_accessed=1000),
        name=name,
    )(slots, pltpu.with_memory_space_constraint(value, in_space))


def sds(shape, dtype):
    return jax.ShapeDtypeStruct(tuple(shape), dtype)


def in_vmem(value):
    return pltpu.with_memory_space_constraint(value, pltpu.VMEM)


def in_hbm(value):
    return pltpu.with_memory_space_constraint(value, pltpu.HBM)


def call(kernel, info, weights, args, outs, scratch, name, mib, after=(), sems=()):
    vmem = pl.BlockSpec(memory_space=pltpu.VMEM)
    scalars = () if info is None else (info,)
    n, w = len(scalars), len(weights)

    def body(*refs):
        at = n + w + len(args)
        kernel(*refs[:at], *refs[at + len(after):])

    return pl.pallas_call(
        body,
        in_specs=[pl.BlockSpec(memory_space=pltpu.SMEM)] * n + [pl.BlockSpec(memory_space=pltpu.HBM)] * w + [vmem] * len(args)
        + [pl.BlockSpec(memory_space=pl.ANY)] * len(after),
        out_specs=[vmem] * len(outs),
        out_shape=[pltpu.VMEM(tuple(s), d) for s, d in outs],
        scratch_shapes=[pltpu.VMEM(s, d) for s, d in scratch] + ([pltpu.SemaphoreType.DMA(sems)] if sems else []),
        compiler_params=pltpu.CompilerParams(vmem_limit_bytes=mib * MIB),
        cost_estimate=pl.CostEstimate(flops=1000, transcendentals=0, bytes_accessed=1000),
        name=name,
    )(*scalars, *(in_hbm(a) for a in weights), *(in_vmem(a) for a in args), *after)


def whole_spec(value):
    zeros = (0,) * value.ndim
    return pl.BlockSpec(value.shape, lambda i, *_: zeros)


def sum_call(kernel, scalars, groups, outs, name):
    args = [v for group in groups for v in group]
    steps = 2
    specs = [pl.BlockSpec((o.shape[0] // steps,) + o.shape[1:], (lambda n: lambda i, *_: (i,) + (0,) * n)(o.ndim - 1))
             for o in outs]
    return pl.pallas_call(
        functools.partial(kernel, [len(group) for group in groups]),
        grid_spec=pltpu.PrefetchScalarGridSpec(
            num_scalar_prefetch=len(scalars), grid=(steps,),
            in_specs=[whole_spec(a) for a in args], out_specs=specs),
        out_shape=outs,
        compiler_params=pltpu.CompilerParams(
            dimension_semantics=("arbitrary",),
            vmem_limit_bytes=4 * MIB + 2 * sum(a.size * a.dtype.itemsize for a in args)
            + sum(o.size * o.dtype.itemsize for o in outs)),
        cost_estimate=pl.CostEstimate(flops=0, transcendentals=0, bytes_accessed=12000000),
        name=name,
    )(*scalars, *args)


def swap(value, bit, axis, size):
    return lax.ppermute(value, axis, [(i, i ^ bit) for i in range(size)])


def near(value):
    return swap(value, 1, "mp", PARTS)


def far(value):
    return swap(value, 2, "mp", PARTS)


def spread(value):
    there = far(value)
    return (value, near(value), there, near(there))


def far_sum_kernel(own, got, out):
    for to, other in ((LO, HI), (HI, LO)):
        out[:, to] = (own[:, to].astype(F32) + got[:, other].astype(F32)).astype(BF16)


def far_sum(own, got):
    return call(far_sum_kernel, None, (), (own, got), [(own.shape, BF16)], [], "far_sum", 6)[0]


def pair_sum_kernel(keep, got, out):
    out[...] = (keep[...] + got[...].astype(F32)).astype(BF16)


def pair_sum(keep, send, *before):
    got = near(send)
    got = late(got, *before) if before else got
    return call(pair_sum_kernel, None, (), (keep, got), [(send.shape, BF16)], [], "pair_sum", 6)[0]


def late(value, *others):
    return lax.optimization_barrier((value, *others))[0]


def doubled(stack, bit, size):
    return jnp.concatenate([stack, swap(stack, bit, "dp", size)], axis=0)


def entry_of(slot, place, size):
    bits = size.bit_length() - 1
    apart = slot ^ place
    return sum(((apart >> b) & 1) << (bits - 1 - b) for b in range(bits))


def shards(dp, residual, attention_gain, query_matrix, key_value_matrix, output_matrix, feedfwd_gain,
           gate_up_matrix, down_matrix, attention_adapter_input, query_adapter_output,
           key_value_adapter_output, output_adapter_input, output_adapter_output, feedfwd_adapter_input,
           feedfwd_adapter_output, down_adapter_input, down_adapter_output, lengths, adapter_index,
           dealing_slots, cotangent):
    seqs = residual.shape[0]
    length = cotangent.shape[1]
    units = down_matrix.shape[0]
    adapters = attention_adapter_input.shape[0]
    q_cols = query_matrix.shape[1]
    kv_cols = key_value_matrix.shape[2]
    kv_heads = kv_cols // HEAD
    heads = q_cols // HEAD
    rows = length // CHUNKS
    half = 2 * QUARTER
    me = lax.axis_index("mp")
    place = lax.axis_index("dp")

    is_there = dealing_slots[None, :] == jnp.arange(seqs, dtype=jnp.int32)[:, None]
    owners = jnp.sum(jnp.where(is_there, adapter_index[None, :], 0), axis=1)
    spans = jnp.sum(jnp.where(is_there, lengths[None, :], 0), axis=1)
    mine = jnp.arange(seqs, dtype=jnp.int32) == place
    my_length = jnp.sum(jnp.where(mine, spans, 0))
    my_adapter = jnp.sum(jnp.where(mine, owners, 0))
    info = jnp.stack([me.astype(jnp.int32), my_length, my_adapter, place.astype(jnp.int32)])

    gs = spread(cotangent[0])
    gains = jnp.stack(spread(jnp.stack([attention_gain, feedfwd_gain])))
    ordered, = move_rows(deal_kernel, residual, dealing_slots, "deal", [pltpu.VMEM(residual.shape, BF16)], pltpu.HBM,
                         pltpu.VMEM, (seqs,))
    dealt = lax.all_to_all(ordered, "dp", split_axis=0, concat_axis=1, tiled=True)[0]
    adapters_here = load_adapters(
        (attention_adapter_input, query_adapter_output, key_value_adapter_output, output_adapter_input,
         output_adapter_output, feedfwd_adapter_input, feedfwd_adapter_output, down_adapter_input,
         down_adapter_output), info)
    a1, qb, kvb, oa, ob, a2, fba, da, bd = adapters_here
    dealt = late(dealt, gs[2], a1, gains)
    beside = near(dealt)
    there = [far(dealt[c * rows:(c + 1) * rows]) for c in range(CHUNKS)]
    xs = [None] * CHUNKS
    cos_np, sin_np = rope_tables(length)
    cos = [jnp.asarray(cos_np[:, c * rows:(c + 1) * rows]) for c in range(CHUNKS)]
    sin = [jnp.asarray(sin_np[:, c * rows:(c + 1) * rows]) for c in range(CHUNKS)]
    wq, wkv, wo = query_matrix, key_value_matrix, output_matrix

    def like(*arrays):
        return [(a.shape, a.dtype) for a in arrays]

    wide, col, block, thin = (rows, WIDTH), (rows, half), (rows, QUARTER), (rows, 1)
    saved, kept, z_own, z_far = ([None] * CHUNKS for _ in range(4))
    order = ()
    for c in range(CHUNKS):
        xs[c] = (dealt, beside, there[c], near(late(there[c], saved[0][0]) if c else there[c]))
        outs = [((3 * RANK, rows), BF16), ((q_cols, rows), BF16), ((kv_heads, rows, HEAD), BF16),
                ((kv_heads, rows, HEAD), BF16), ((kv_cols, rows), BF16), ((kv_cols, rows), BF16)]
        saved[c] = call(
            functools.partial(project_kernel, c), info, (wq, wkv), (*xs[c], gains, a1, qb, kvb, cos[c], sin[c]), outs,
            [(wide, BF16)] + like(wq, wkv), "project_%d" % c, 12, order, (2,))
        outs = [(col, F32), (col, BF16), ((q_cols, rows), BF16), ((heads, rows), F32), ((RANK, rows), BF16)]
        pairs = [v for p in saved[:c + 1] for v in (p[2], p[5])]
        z_keep, z_send, *kept[c] = call(
            functools.partial(attend_kernel, c), info, (wo,), (saved[c][1], oa, ob, *pairs), outs, like(wo),
            "attend_%d" % c, 10, (saved[c][0],), (1,))
        z_own[c] = pair_sum(z_keep, late(z_send, z_far[0] if c else there[-1]))
        z_far[c] = far(z_own[c])
        order = (kept[c][1], z_own[c])
    def front(c, total, partial, order):
        hidden = (rows, units)
        outs = [(wide, BF16), (block, F32), (wide, BF16), (wide, BF16), (hidden, BF16), (hidden, BF16), (hidden, BF16),
                ((rows, 2 * RANK), BF16), ((rows, RANK), BF16),
                ((3 * RANK * units // QUARTER, QUARTER), BF16 if c else F32)]
        args = (*xs[c], total, near(total), *gs, gains, a2, bd, fba, da, *partial)
        weights = () if c else (gate_up_matrix, down_matrix)
        outs += like(*weights)
        return call(
            functools.partial(front_kernel, c, c == CHUNKS - 1), info, weights, (wgu, wd, *args) if c else args, outs,
            [((ROW_BLOCK, WIDTH), F32)], "front_%d" % c, 8, order, () if c else (2, units // QUARTER))

    def back(c, hidden, partial, order):
        first = col if c else (rows + 3 * RANK, half)
        outs = [((rows, RANK), F32), (first, F32), (first, BF16)]
        outs += [((3 * RANK, WIDTH), F32)] if c else []
        return call(
            functools.partial(back_kernel, c == 0), info, (), (wgu, *hidden[2:7], a2, fba, da, *partial), outs,
            [(block, F32), ((3 * RANK, QUARTER), F32)], "back_%d" % c, 8, order)

    def down(c, td, order):
        return call(down_kernel, info, (), (wd, hidden[c][4], td, bd, hidden[c][1]), [(col, F32), (col, BF16)],
                    [(block, F32)], "down_%d" % c, 6, order)

    def attend_back(c, total, partial, order):
        outs = [(block, F32), (col, F32), (col, BF16), (thin, F32), ((3 * RANK, QUARTER), F32 if c else BF16)]
        low = (4 * RANK + SPARE, half)
        outs += ([((4 * RANK, WIDTH), F32), ((kv_cols, rows), F32), ((kv_cols, rows), F32), ((SPARE // 2, rows), F32)]
                 if c else [(low, F32), (low, BF16)])
        scratch = [(wide, BF16), (wide, BF16), ((ROW_BLOCK, WIDTH), F32), ((q_cols, rows), BF16), ((q_cols, rows), F32),
                   ((c + 1, kv_cols, rows), F32), ((c + 1, kv_cols, rows), F32), ((rows, q_cols + 2 * kv_cols), BF16),
                   (block, F32), ((4 * RANK, QUARTER), F32)]
        triples = [v for p in saved[:c + 1] for v in (p[2], p[3], p[4])]
        return call(
            functools.partial(attend_back_kernel, c, c == 0), info, (wq, wkv, wo),
            (*xs[c], *gs, hidden[c][0], total, near(total), gains, a1, qb, kvb, oa, ob, cos[c], sin[c], *saved[c][:2],
             *kept[c], *triples, *partial), outs, scratch + like(wq, wkv, wo), "attend_back_%d" % c, 18, order, (3,))

    bits = [1 << b for b in reversed(range(dp.bit_length() - 1))]
    def to_bands(value):
        return lax.all_to_all(value.reshape(dp, length // dp, QUARTER), "dp", split_axis=0, concat_axis=0, tiled=True)

    def collect(value, name, *before):
        rows_out = sds((seqs, length // dp, QUARTER), BF16)
        return move_rows(collect_kernel, value, late(dealing_slots, *before), name, [rows_out], pltpu.VMEM, pl.ANY,
                         (seqs,))[0]

    hidden, d_own, d_far, y_keep, y_got = ([None] * CHUNKS for _ in range(5))
    *hidden[0], wgu, wd = front(0, far_sum(z_own[0], z_far[0]), (), order)
    step = hidden[0][8]
    hidden[1] = front(1, far_sum(z_own[1], late(z_far[1], step)), hidden[0][9:], (step,))
    fb = hidden[1][9][None]
    fb_first = swap(fb, bits[0], "dp", dp)
    td, d_keep, d_send, fa = back(1, hidden[1], (), (hidden[1][8],))
    d_own[1] = pair_sum(d_keep, late(d_send, fb_first))
    d_far[1] = far(d_own[1])
    fb = fb_more = jnp.concatenate([fb, fb_first], axis=0)
    for bit in bits[1:-1]:
        fb_more = doubled(fb_more, bit, dp)
    fb_more = fb_more[2:]
    fb_side = swap(fb, bits[-1], "dp", dp)
    td_0, d_keep, d_send = back(0, hidden[0], (fa,), (d_own[1],))
    y_keep[1], y_send = down(1, td, (td_0,))
    total = far_sum(d_own[1], late(d_far[1], y_send))
    d_own[0] = pair_sum(d_keep, late(d_send, fb_more, fb_side), total)
    d_far[0] = far(d_own[0])
    fb_more_side = swap(fb_more, bits[-1], "dp", dp)
    y_got[1] = near(late(y_send, d_own[0]))
    dxq, h_keep, h_send, inv, *sums = attend_back(1, total, (), (d_own[0], y_send))
    total = far_sum(d_own[0], late(d_far[0], inv))
    h_got = near(late(h_send, fb_more_side))
    h_high = high_sum((h_keep, h_got))
    h_far = far(h_high)
    final = [None, (dxq, h_keep, h_got, h_far, inv)]
    fa = total[rows:][None]
    fa_first = swap(fa, bits[0], "dp", dp)
    dxq, h_keep, h_send, inv, att_b, aa_keep, aa_send = attend_back(0, total, sums, (h_high,))
    ready = (fa_first, h_far)
    aa_got = near(late(aa_send, *ready))
    aa_high = high_sum((aa_keep, aa_got))
    aa_far = far(aa_high)
    h_got = near(late(h_send, *ready))
    h_high = high_sum((h_keep, h_got))
    h_far = far(h_high)
    final[0] = (dxq, h_keep, h_got, h_far, inv)
    att_a = aa_keep[:4 * RANK, :QUARTER] + aa_got[:4 * RANK, :QUARTER].astype(F32)
    att_a = (att_a + late(aa_far, h_high)[:4 * RANK].astype(F32)).astype(BF16)
    n_b = att_b.shape[0]
    att = jnp.concatenate([att_b, att_a], axis=0)[None]
    y_keep[0], y_send = down(0, td_0, (att,))
    y_got[0] = near(y_send)
    att = first = doubled(att, bits[0], dp)
    att = late(att, h_far, y_send)
    for bit in bits[1:-1]:
        att = doubled(att, bit, dp)
    fa = late(jnp.concatenate([fa, fa_first], axis=0), aa_high, y_send)
    for bit in bits[1:-1]:
        fa = doubled(fa, bit, dp)
    fa_side = swap(fa, bits[-1], "dp", dp)

    dinput, = call(finish_kernel, None, (), (gains, dealt, aa_high, aa_far, *(v for f in final for v in f)),
                   [((length, QUARTER), BF16)], [], "finish", 8, (first, y_send))
    y_far = far(high_sum(*((k, late(g, dinput)) for k, g in zip(y_keep, y_got))))
    input_grad = collect(to_bands(dinput), "collect_grad")
    outs = [sds((adapters, 2 * RANK, WIDTH), F32), sds((adapters, RANK, WIDTH), F32),
            sds((adapters, 2, RANK, units), F32), sds((adapters, RANK, units), F32)]
    ga_ffn, g_down_b, g_ffn_b, g_down_a = sum_call(
        feedforward_sum_kernel, (info, owners),
        ((fb, fb_more, fb_side, fb_more_side), (fa, fa_side), (near(fa), near(fa_side))), outs, "feedforward_sum")

    result, = call(output_kernel, info, (), (late(y_far, dinput, g_down_a), *(v for p in zip(y_keep, y_got) for v in p)),
                   [((length, QUARTER), BF16)], [], "output", 8)
    output = collect(to_bands(result), "collect_out", input_grad)

    att_side = swap(att, bits[-1], "dp", dp)
    a_parts = [att[:, n_b:], att_side[:, n_b:]]
    a_far = [far(v) for v in a_parts]
    outs = [sds((adapters, 3 * RANK, WIDTH), F32), sds((adapters, RANK, WIDTH), F32),
            sds((adapters, RANK, q_cols), F32), sds((adapters, 2, RANK, kv_cols), F32),
            sds((adapters, RANK, q_cols), F32)]
    ga_att, g_out_b, g_query_b, g_kv_b, g_out_a = sum_call(
        attention_sum_kernel, (info, owners),
        ((att, att_side), a_parts, [near(v) for v in a_parts], a_far, [near(v) for v in a_far]), outs, "attention_sum")
    return (output, input_grad, ga_att, g_query_b, g_kv_b, g_out_a, g_out_b, ga_ffn, g_ffn_b, g_down_a, g_down_b)


def solution(mesh):
    in_specs = (
        P(None, "dp", "mp"), P("mp"), P(None, "mp"), P(None, None, "mp"), P("mp", None), P("mp"),
        P(None, None, "mp"), P("mp", None), P(), P(None, None, "mp"), P(None, None, None, "mp"),
        P(None, None, "mp"), P(), P(), P(None, None, None, "mp"), P(None, None, "mp"), P(), P(), P(), P(),
        P("dp", None, "mp"),
    )
    out_specs = (
        P(None, "dp", "mp"), P(None, "dp", "mp"), P(), P(None, None, "mp"), P(None, None, None, "mp"),
        P(None, None, "mp"), P(), P(), P(None, None, None, "mp"), P(None, None, "mp"), P(),
    )
    return jax.shard_map(
        functools.partial(shards, mesh.shape["dp"]), mesh=mesh, in_specs=in_specs, out_specs=out_specs,
        check_vma=False)
```

```python
import functools

import jax
import jax.numpy as jnp
import numpy as np
from jax import lax
from jax.experimental import pallas as pl
from jax.experimental.pallas import tpu as pltpu
from jax.sharding import PartitionSpec as P

WIDTH = 2048
HEAD = 64
HALF = HEAD // 2
RANK = 16
EPS = 1e-05
ROPE_BASE = 500000.0
NEG_FILL = -1e30
PARTS = 4
LANES = 128
SPARE = 32
ROW_BLOCK = 64
QUARTER = WIDTH // PARTS
CHUNKS = 2
MIB = 1024 * 1024
F32 = jnp.float32
BF16 = jnp.bfloat16


def nn(a, b):
    return lax.dot_general(a, b, (((1,), (0,)), ((), ())), preferred_element_type=F32)


def nt(a, b):
    return lax.dot_general(a, b, (((1,), (1,)), ((), ())), preferred_element_type=F32)


def rope_tables(length):
    freq = ROPE_BASE ** (-np.arange(HALF, dtype=np.float32) * np.float32(2.0 / HEAD))
    angles = (np.arange(length, dtype=np.float32)[None, :] * freq.astype(np.float32)[:, None]).astype(np.float32)
    return np.cos(angles).astype(np.float32), np.sin(angles).astype(np.float32)


def quarter(me, rel):
    return pl.ds(pl.multiple_of((me ^ rel) * QUARTER, QUARTER), QUARTER)


LO, HI = slice(0, QUARTER), slice(QUARTER, 2 * QUARTER)


def total_block(rel, rows_at, own, oth):
    return (own if rel in (0, 2) else oth)[rows_at, LO if rel in (0, 1) else HI].astype(F32)


def store_block(rel, value, rows_at, keep_ref, send_ref):
    to = pl.ds(pl.multiple_of((rel // 2) * QUARTER, QUARTER), QUARTER)

    @pl.when(rel % 2 == 0)
    def _():
        keep_ref[rows_at, to] = value[...]

    @pl.when(rel % 2 == 1)
    def _():
        send_ref[rows_at, to] = value[...].astype(BF16)


def chunk_of(ref, chunk, rows):
    return ref if ref.shape[0] == rows else ref.at[chunk * rows:(chunk + 1) * rows]


def row_block(i):
    return pl.ds(pl.multiple_of(i * ROW_BLOCK, ROW_BLOCK), ROW_BLOCK)


def is_valid(chunk, i, rows, length):
    return chunk * rows + i * ROW_BLOCK + lax.broadcasted_iota(jnp.int32, (ROW_BLOCK, 1), 0) < length


def copies_of(pairs, sems):
    made = [pltpu.make_async_copy(source, target, sems.at[i]) for i, (source, target) in enumerate(pairs)]
    for copy in made:
        copy.start()
    return made


def put_block(rel, value, keep_ref, send_ref):
    ref = keep_ref if rel in (0, 2) else send_ref
    ref[:, LO if rel in (0, 1) else HI] = value.astype(ref.dtype)


def rotate(value, cos, sin, out_ref):
    for i in range(value.shape[0] // HEAD):
        u1, u2 = value[i * HEAD:i * HEAD + HALF], value[i * HEAD + HALF:(i + 1) * HEAD]
        out_ref[i * HEAD:i * HEAD + HALF, :] = (u1 * cos - u2 * sin).astype(BF16)
        out_ref[i * HEAD + HALF:(i + 1) * HEAD, :] = (u2 * cos + u1 * sin).astype(BF16)


def turn_back(value, cos, sin, out_ref):
    for i in range(value.shape[0] // HEAD):
        w1, w2 = value[i * HEAD:i * HEAD + HALF], value[i * HEAD + HALF:(i + 1) * HEAD]
        out_ref[i * HEAD:i * HEAD + HALF, :] = (w1 * cos + w2 * sin).astype(BF16)
        out_ref[i * HEAD + HALF:(i + 1) * HEAD, :] = (w2 * cos - w1 * sin).astype(BF16)


def head_rows(i):
    return pl.ds(pl.multiple_of(i * HEAD, HEAD), HEAD)


def visible(key_start, query_start, rows, length):
    kpos = key_start + lax.broadcasted_iota(jnp.int32, (rows, rows), 0)
    qpos = query_start + lax.broadcasted_iota(jnp.int32, (rows, rows), 1)
    return (kpos <= qpos) & (kpos < length)


def project_kernel(chunk, info, wq_h, wkv_h, x0, x1, x2, x3, gains, a1, qb, kvb, cos_t, sin_t,
                   t1t_out, qt_out, kn_out, vn_out, kt_out, vt_out, h_out, wq, wkv, sems):
    copies = copies_of(((wkv_h, wkv), (wq_h, wq)), sems)
    me = info[0]
    rows = h_out.shape[0]
    kv_heads = kn_out.shape[0]
    xs = [chunk_of(x, chunk, rows) for x in (x0, x1, x2, x3)]

    def norm(i, carry):
        at = row_block(i)
        square = jnp.zeros((ROW_BLOCK, 1), F32)
        for r in range(PARTS):
            v = xs[r][at, :].astype(F32)
            square = square + jnp.sum(v * v, axis=1, keepdims=True)
        inv = lax.rsqrt(square / WIDTH + EPS)
        for r in range(PARTS):
            v = xs[r][at, :].astype(F32)
            h_out[at, quarter(me, r)] = (v * inv * gains[r, 0:1, :].astype(F32)).astype(BF16)
        return carry

    lax.fori_loop(0, rows // ROW_BLOCK, norm, 0)
    h = h_out[...]
    t1 = nt(h, a1[...])
    t1t_out[...] = t1.T.astype(BF16)
    t1b = t1.astype(BF16)
    cos, sin = cos_t[...], sin_t[...]
    copies[0].wait()
    k = nn(h, wkv[0]) + nn(t1b[:, RANK:2 * RANK], kvb[0])
    rotate(k.T, cos, sin, kt_out)
    k_n = kt_out[...].T
    v_n = (nn(h, wkv[1]) + nn(t1b[:, 2 * RANK:], kvb[1])).astype(BF16)
    vt_out[...] = v_n.T
    for i in range(kv_heads):
        kn_out[i] = k_n[:, i * HEAD:(i + 1) * HEAD]
        vn_out[i] = v_n[:, i * HEAD:(i + 1) * HEAD]
    copies[1].wait()
    q = nn(h, wq[...]) + nn(t1b[:, :RANK], qb[...])
    rotate(q.T * (HEAD ** -0.5), cos, sin, qt_out)


def attend_kernel(chunk, info, wo_h, qt, oa, ob, *rest):
    pairs, rest = rest[:2 * (chunk + 1)], rest[2 * (chunk + 1):]
    z_keep, z_send, ot_out, lse_out, tot_out, wo, sems = rest
    copies = copies_of(((wo_h, wo),), sems)
    keys, values = pairs[0::2], pairs[1::2]
    me, length = info[0], info[1]
    rows = qt.shape[1]
    kv_heads = keys[0].shape[0]
    heads = qt.shape[0] // HEAD
    group = heads // kv_heads

    kept = [jnp.concatenate([visible(c * rows, chunk * rows, rows, length)] * group, axis=1) for c in range(chunk + 1)]

    def one_group(j, carry):
        q_g = jnp.concatenate([qt[head_rows(j * group + g), :] for g in range(group)], axis=1)
        parts = [jnp.where(kept[c], nn(keys[c][j], q_g), NEG_FILL) for c in range(chunk + 1)]
        top = functools.reduce(jnp.maximum, [jnp.max(s, axis=0, keepdims=True) for s in parts])
        es = [jnp.exp(s - top) for s in parts]
        total = sum(jnp.sum(e, axis=0, keepdims=True) for e in es)
        low = top + jnp.log(total)
        o_t = sum(nn(value[head_rows(j), :], e.astype(BF16)) for value, e in zip(values, es))
        o_t = (o_t / total).astype(BF16)
        for g in range(group):
            cols = slice(g * rows, (g + 1) * rows)
            lse_out[pl.ds(j * group + g, 1), :] = low[:, cols]
            ot_out[head_rows(j * group + g), :] = o_t[:, cols]
        return carry

    lax.fori_loop(0, kv_heads, one_group, 0)
    o = ot_out[...].T
    to = nt(o, oa[...])
    tot_out[...] = to.T.astype(BF16)
    to = to.astype(BF16)
    copies[0].wait()
    for r in range(PARTS):
        at = quarter(me, r)
        put_block(r, nn(o, wo[:, at]) + nn(to, ob[:, at]), z_keep, z_send)


def front_kernel(chunk, last, info, wgu_in, wd_in, x0, x1, x2, x3, zo, zp, g0, g1, g2, g3, gains, a2, bd, fb, da,
                 *rest):
    units = wd_in.shape[0]
    if chunk:
        wgu, wd = wgu_in, wd_in
    else:
        (wgu, wd, f_s, sems), rest = rest[-4:], rest[:-4]
        rest = (*rest, f_s)

    def copies(i):
        c = pl.ds(pl.multiple_of(i * QUARTER, QUARTER), QUARTER)
        return (pltpu.make_async_copy(wgu_in.at[:, :, c], wgu.at[:, :, c], sems.at[0, i]),
                pltpu.make_async_copy(wd_in.at[c, :], wd.at[c, :], sems.at[1, i]))

    if not chunk:
        for i in range(units // QUARTER):
            for copy in copies(i):
                copy.start()
    f_s = rest[-1]
    xm_out, xq_out, h_out, g_out, act_out, dg_out, du_out, t2_s, dtd_s, b_out = rest[-11:-1]
    me, length = info[0], info[1]
    rows = h_out.shape[0]
    xs, gs = ([chunk_of(v, chunk, rows) for v in vs] for vs in ((x0, x1, x2, x3), (g0, g1, g2, g3)))

    def norm(i, carry):
        at = row_block(i)
        valid = is_valid(chunk, i, rows, length)
        square = jnp.zeros((ROW_BLOCK, 1), F32)
        for r in range(PARTS):
            v = xs[r][at, :].astype(F32) + total_block(r, at, zo, zp)
            if r == 0:
                xq_out[at, :] = v
            f_s[:, quarter(me, r)] = v
            square = square + jnp.sum(v * v, axis=1, keepdims=True)
            g_out[at, quarter(me, r)] = jnp.where(valid, gs[r][at, :], jnp.zeros((), BF16))
        inv = lax.rsqrt(square / WIDTH + EPS)
        for r in range(PARTS):
            v = f_s[:, quarter(me, r)]
            xm_out[at, quarter(me, r)] = v.astype(BF16)
            h_out[at, quarter(me, r)] = (v * inv * gains[r, 1:2, :].astype(F32)).astype(BF16)
        return carry

    lax.fori_loop(0, rows // ROW_BLOCK, norm, 0)
    t2 = nt(h_out[...], a2[...])
    t2_s[...] = t2.astype(BF16)
    dtd = nt(g_out[...], bd[...])
    dtd_s[...] = dtd.astype(BF16)
    t2t, dtdt = t2.T.astype(BF16), dtd.T.astype(BF16)

    def block(i, carry):
        c = pl.ds(pl.multiple_of(i * QUARTER, QUARTER), QUARTER)
        if not chunk:
            for copy in copies(i):
                copy.wait()
        h, g = h_out[...], g_out[...]
        gate = nn(h, wgu[0, :, c]) + nn(t2_s[:, :RANK], fb[0, :, c])
        up = nn(h, wgu[1, :, c]) + nn(t2_s[:, RANK:], fb[1, :, c])
        dact = nt(g, wd[c, :]) + nn(dtd_s[...], da[:, c])
        sig = 1.0 / (1.0 + jnp.exp(-gate))
        silu = gate * sig
        act = (silu * up).astype(BF16)
        dgate = (dact * up * sig * (1.0 + gate * (1.0 - sig))).astype(BF16)
        dup = (dact * silu).astype(BF16)
        act_out[:, c], dg_out[:, c], du_out[:, c] = act, dgate, dup
        for k, value in enumerate((nn(t2t[:RANK], dgate), nn(t2t[RANK:], dup), nn(dtdt, act))):
            at = pl.ds(pl.multiple_of((3 * i + k) * RANK, RANK), RANK)
            if last:
                value = value + rest[0][at, :]
            b_out[at, :] = value.astype(b_out.dtype)
        return carry

    lax.fori_loop(0, units // QUARTER, block, 0)


def back_kernel(last, info, wgu, h, g, act, dg, du, a2, fb, da, *rest):
    (value_s, low_s), rest = rest[-2:], rest[:-2]
    outs, rest = (rest[-3:], rest[:-3]) if last else (rest[-4:], rest[:-4])
    td_out, d_keep, d_send = outs[:3]
    me = info[0]
    rows = h.shape[0]
    dt2 = jnp.concatenate([nt(dg[...], fb[0]), nt(du[...], fb[1])], axis=1)
    td = nt(act[...], da[...])
    td_out[...] = td
    dt2b = dt2.astype(BF16)
    dt2t, tdt = dt2.T.astype(BF16), td.T.astype(BF16)

    def block(r, carry):
        at = quarter(me, r)
        value_s[...] = nt(dg[...], wgu[0, at, :]) + nt(du[...], wgu[1, at, :]) + nn(dt2b, a2[:, at])
        store_block(r, value_s, slice(0, rows), d_keep, d_send)
        low_s[:2 * RANK, :] = nn(dt2t, h[:, at])
        low_s[2 * RANK:, :] = nn(tdt, g[:, at])
        if last:
            low_s[...] += rest[0][:, at]
            store_block(r, low_s, slice(rows, rows + 3 * RANK), d_keep, d_send)
        else:
            outs[3][:, at] = low_s[...]
        return carry

    lax.fori_loop(0, PARTS, block, 0)


def down_kernel(info, wd, act, td, bd, xq, y_keep, y_send, value_s):
    me = info[0]
    tdb = td[...].astype(BF16)

    def block(r, carry):
        at = quarter(me, r)
        value_s[...] = nn(act[...], wd[:, at]) + nn(tdb, bd[:, at])
        store_block(r, value_s, slice(0, act.shape[0]), y_keep, y_send)
        return carry

    lax.fori_loop(0, PARTS, block, 0)
    y_keep[:, LO] += xq[...]


def attend_back_kernel(chunk, last, info, wq_h, wkv_h, wo_h, x0, x1, x2, x3, g0, g1, g2, g3, xm, do_, dp, gains, a1,
                       qb, kvb, oa, ob, cos_t, sin_t, t1t, qt, ot, lse, tot, *rest):
    scratch, rest = rest[-14:], rest[:-14]
    h_in, z_s, f_s, dot_s, dqt_s, dkt_s, dvt_s, dq_s, value_s, low_s, wq, wkv, wo, sems = scratch
    copies = copies_of(((wo_h, wo), (wq_h, wq), (wkv_h, wkv)), sems)
    n_out = 7 if last else 9
    outs, rest = rest[-n_out:], rest[:-n_out]
    dxq_out, h_keep, h_send, inv_out, b_out = outs[:5]
    triples, rest = rest[:3 * (chunk + 1)], rest[3 * (chunk + 1):]
    keys, values, keys_t = triples[0::3], triples[1::3], triples[2::3]
    me, length = info[0], info[1]
    rows = xm.shape[0]
    kv_heads = keys[0].shape[0]
    heads = qt.shape[0] // HEAD
    group = heads // kv_heads
    q_cols, kv_cols = heads * HEAD, kv_heads * HEAD
    xs, gs = ([chunk_of(v, chunk, rows) for v in vs] for vs in ((x0, x1, x2, x3), (g0, g1, g2, g3)))

    def norm_back(i, carry):
        at = row_block(i)
        valid = is_valid(chunk, i, rows, length)
        square, first, inner = (jnp.zeros((ROW_BLOCK, 1), F32) for _ in range(3))
        for r in range(PARTS):
            v = xm[at, quarter(me, r)].astype(F32)
            square = square + jnp.sum(v * v, axis=1, keepdims=True)
            w = total_block(r, at, do_, dp) * gains[r, 1:2, :].astype(F32)
            f_s[:, quarter(me, r)] = w
            inner = inner + jnp.sum(v * w, axis=1, keepdims=True)
            u = xs[r][at, :].astype(F32)
            first = first + jnp.sum(u * u, axis=1, keepdims=True)
        inv_one = lax.rsqrt(first / WIDTH + EPS)
        inv_out[at, :] = inv_one
        inv = lax.rsqrt(square / WIDTH + EPS)
        back = inv * inv * inv * inner / WIDTH
        for r in range(PARTS):
            v = xm[at, quarter(me, r)].astype(F32)
            g = jnp.where(valid, gs[r][at, :].astype(F32), 0.0)
            d = g + inv * f_s[:, quarter(me, r)] - v * back
            if r == 0:
                dxq_out[at, :] = d
            z_s[at, quarter(me, r)] = d.astype(BF16)
            u = xs[r][at, :].astype(F32)
            h_in[at, quarter(me, r)] = (u * inv_one * gains[r, 0:1, :].astype(F32)).astype(BF16)
        return carry

    lax.fori_loop(0, rows // ROW_BLOCK, norm_back, 0)
    dz = z_s[...]
    dto = nt(dz, ob[...])
    copies[0].wait()
    d_o = nt(dz, wo[...]) + nn(dto.astype(BF16), oa[...])
    dot_s[...] = d_o.T.astype(BF16)
    kept = [jnp.concatenate([visible(c * rows, chunk * rows, rows, length)] * group, axis=1) for c in range(chunk + 1)]

    def one_group(j, carry):
        places = [head_rows(j * group + g) for g in range(group)]
        q_g = jnp.concatenate([qt[at, :] for at in places], axis=1)
        do_g = jnp.concatenate([dot_s[at, :] for at in places], axis=1)
        o_g = jnp.concatenate([ot[at, :] for at in places], axis=1)
        low = jnp.concatenate([lse[pl.ds(j * group + g, 1), :] for g in range(group)], axis=1)
        dots = jnp.sum(do_g.astype(F32) * o_g.astype(F32), axis=0, keepdims=True)
        dq_g = 0.0
        for c in range(chunk + 1):
            prob = jnp.where(kept[c], jnp.exp(nn(keys[c][j], q_g) - low), 0.0)
            ds = (prob * (nn(values[c][j], do_g) - dots)).astype(BF16)
            dq_g = dq_g + nn(keys_t[c][head_rows(j), :], ds)
            dk, dv = nt(q_g, ds), nt(do_g, prob.astype(BF16))
            if last:
                dk, dv = dk + rest[2][head_rows(j), :], dv + rest[3][head_rows(j), :]
            dkt_s[c, head_rows(j), :], dvt_s[c, head_rows(j), :] = dk, dv
        for g in range(group):
            dqt_s[places[g], :] = dq_g[:, g * rows:(g + 1) * rows]
        return carry

    lax.fori_loop(0, kv_heads, one_group, 0)
    if not last:
        outs[6][...], outs[7][...] = dkt_s[0], dvt_s[0]
    cos, sin = cos_t[...], sin_t[...]
    dto_t, o_t = dto.T.astype(BF16), ot[...]
    d_out_a = nt(dto_t, o_t)
    turn_back(dqt_s[...], cos * (HEAD ** -0.5), sin * (HEAD ** -0.5), dot_s)
    dq_s[:, :q_cols] = dot_s[...].T
    turn_back(dkt_s[chunk], cos, sin, dot_s)
    dq_s[:, q_cols:q_cols + kv_cols] = dot_s[:kv_cols, :].T
    dq_s[:, q_cols + kv_cols:] = dvt_s[chunk].T.astype(BF16)
    dq, dk, dv = dq_s[:, :q_cols], dq_s[:, q_cols:q_cols + kv_cols], dq_s[:, q_cols + kv_cols:]
    dt1 = jnp.concatenate([nt(dq, qb[...]), nt(dk, kvb[0]), nt(dv, kvb[1])], axis=1)
    dt1b = dt1.astype(BF16)
    kv_pad = jnp.zeros((RANK, QUARTER - 2 * kv_cols), F32)
    d_kv = jnp.concatenate([nn(t1t[RANK:2 * RANK, :], dk), nn(t1t[2 * RANK:, :], dv), kv_pad], axis=1)
    for k, value in enumerate((nn(t1t[:RANK, :], dq), d_out_a, d_kv)):
        at = slice(k * RANK, (k + 1) * RANK)
        if last:
            value = value + rest[0][at, :]
        b_out[at, :] = value.astype(b_out.dtype)
    dt1t = dt1.T.astype(BF16)
    copies[1].wait()
    copies[2].wait()

    def block(r, inner):
        at = quarter(me, r)
        d = nt(dq_s[:, :q_cols], wq[at, :]) + nn(dt1b, a1[:, at])
        d = d + nt(dq_s[:, q_cols:q_cols + kv_cols], wkv[0, at, :]) + nt(dq_s[:, q_cols + kv_cols:], wkv[1, at, :])
        value_s[...] = d
        store_block(r, value_s, slice(0, rows), h_keep, h_send)
        low_s[:3 * RANK, :] = nn(dt1t, h_in[:, at])
        low_s[3 * RANK:, :] = nn(tot[...], z_s[:, at])
        if last:
            low_s[...] += rest[1][:, at]
            store_block(r, low_s, slice(0, 4 * RANK), outs[5], outs[6])
        else:
            outs[5][:, at] = low_s[...]
        return inner + jnp.sum(d * h_in[:, at].astype(F32), axis=1, keepdims=True)

    inner = lax.fori_loop(0, PARTS, block, jnp.zeros((rows, 1), F32))
    inner = jnp.broadcast_to(inner, (rows, LANES)).T[:SPARE // 2, :]
    if last:
        for ref in outs[5:7]:
            for c, value in enumerate((inner, rest[4][...])):
                at = slice(4 * RANK + c * SPARE // 2, 4 * RANK + (c + 1) * SPARE // 2)
                ref[at, QUARTER:QUARTER + rows] = value.astype(ref.dtype)
                ref[at, QUARTER + rows:] = jnp.zeros((SPARE // 2, QUARTER - rows), ref.dtype)
                ref[at, :QUARTER] = jnp.zeros((SPARE // 2, QUARTER), ref.dtype)
    else:
        outs[8][...] = inner


def output_kernel(info, y_far, *refs):
    out = refs[-1]
    rows = out.shape[0] // CHUNKS
    for c in range(CHUNKS):
        y_keep, y_got = refs[2 * c:2 * (c + 1)]
        at = slice(c * rows, (c + 1) * rows)
        valid = c * rows + lax.broadcasted_iota(jnp.int32, (rows, 1), 0) < info[1]
        y = y_keep[:, LO] + y_got[:, LO].astype(F32) + y_far[at, :].astype(F32)
        out[at, :] = jnp.where(valid, y, 0.0).astype(BF16)


def finish_kernel(gains, x_all, aa_high, aa_far, *refs):
    out = refs[-1]
    gain = gains[0, 0:1, :].astype(F32)
    rows = out.shape[0] // CHUNKS
    inner = aa_high[4 * RANK:, :].astype(F32) + aa_far[4 * RANK:, :].astype(F32)
    for c in range(CHUNKS):
        dx, keep, got, there, inv = refs[5 * c:5 * (c + 1)]
        x = chunk_of(x_all, c, rows)
        mine = inner[c * SPARE // 2:c * SPARE // 2 + 8, :rows].T[:, 0:1]
        inv = inv[...]
        grad = keep[:, LO] + got[:, LO].astype(F32) + there[...].astype(F32)
        grad = inv * (gain * grad) - x[...].astype(F32) * (inv * inv * mine / WIDTH)
        out[c * rows:(c + 1) * rows, :] = (dx[...] + grad).astype(BF16)


def high_sum_kernel(*refs):
    out = refs[-1]
    rows = out.shape[0] // (len(refs) // 2)
    for c in range(len(refs) // 2):
        keep, got = refs[2 * c:2 * c + 2]
        out[c * rows:(c + 1) * rows, :] = (keep[:, HI] + got[:, HI].astype(F32)).astype(BF16)


def high_sum(*pairs):
    args = [v for pair in pairs for v in pair]
    rows = sum(keep.shape[0] for keep, _ in pairs)
    return call(high_sum_kernel, None, (), args, [((rows, QUARTER), BF16)], [], "high_sum", 8)[0]


def split_refs(refs, counts):
    groups = []
    for count in counts:
        groups.append(refs[:count])
        refs = refs[count:]
    return groups, refs


def with_entry(parts, at, use):
    start = 0
    for ref in parts:
        @pl.when((at >= start) & (at < start + ref.shape[0]))
        def _(ref=ref, start=start):
            use(ref, at - start)
        start += ref.shape[0]


def sum_slots(info, owners, out_refs, one_slot):
    count = out_refs[0].shape[0]
    base = pl.program_id(0) * count
    slots = owners.shape[0]
    for ref in out_refs:
        ref[...] = jnp.zeros_like(ref)

    def add(slot, carry):
        owner = owners[slot] - base

        @pl.when((owner >= 0) & (owner < count))
        def _():
            one_slot(owner, entry_of(slot, info[3], slots))
        return carry

    lax.fori_loop(0, slots, add, 0)


def feedforward_sum_kernel(counts, info, owners, *refs):
    (b_parts, *a_parts), outs = split_refs(refs, counts)
    ga, gdb, gb, gda = outs
    me = info[0]

    def one_slot(owner, at):
        def add_b(ref, e):
            for i in range(gda.shape[2] // QUARTER):
                cols = slice(i * QUARTER, (i + 1) * QUARTER)
                base = i * 3 * RANK
                gb[owner, 0, :, cols] += ref[e, base:base + RANK, :].astype(F32)
                gb[owner, 1, :, cols] += ref[e, base + RANK:base + 2 * RANK, :].astype(F32)
                gda[owner, :, cols] += ref[e, base + 2 * RANK:base + 3 * RANK, :].astype(F32)

        with_entry(b_parts, at, add_b)
        for near_bit, parts in enumerate(a_parts):
            def add_a(ref, e, near_bit=near_bit):
                for r, cols in ((near_bit, LO), (near_bit ^ 2, HI)):
                    ga[owner, :, quarter(me, r)] += ref[e, :2 * RANK, cols].astype(F32)
                    gdb[owner, :, quarter(me, r)] += ref[e, 2 * RANK:, cols].astype(F32)

            with_entry(parts, at, add_a)

    sum_slots(info, owners, outs, one_slot)


def attention_sum_kernel(counts, info, owners, *refs):
    (b_parts, *a_parts), outs = split_refs(refs, counts)
    ga, gob, gq, gkv, goa = outs
    me = info[0]
    kv_cols = gkv.shape[3]

    def one_slot(owner, at):
        def add_b(ref, e):
            gq[owner] += ref[e, :RANK, :].astype(F32)
            goa[owner] += ref[e, RANK:2 * RANK, :].astype(F32)
            gkv[owner, 0] += ref[e, 2 * RANK:3 * RANK, :kv_cols].astype(F32)
            gkv[owner, 1] += ref[e, 2 * RANK:3 * RANK, kv_cols:2 * kv_cols].astype(F32)

        with_entry(b_parts, at, add_b)
        for r, parts in enumerate(a_parts):
            def add_a(ref, e, r=r):
                ga[owner, :, quarter(me, r)] += ref[e, :3 * RANK, :].astype(F32)
                gob[owner, :, quarter(me, r)] += ref[e, 3 * RANK:, :].astype(F32)

            with_entry(parts, at, add_a)

    sum_slots(info, owners, outs, one_slot)


def deal_kernel(slots, source, out, sems):
    made = [pltpu.make_async_copy(source.at[i], out.at[slots[i]], sems.at[i]) for i in range(source.shape[0])]
    for copy in made:
        copy.start()
    for copy in made:
        copy.wait()


def collect_kernel(slots, source, out, sems):
    made = [pltpu.make_async_copy(source.at[slots[i]], out.at[i], sems.at[i]) for i in range(source.shape[0])]
    for copy in made:
        copy.start()
    for copy in made:
        copy.wait()


def adapter_kernel(count, info, *refs):
    made = [pltpu.make_async_copy(refs[i].at[info[2]], refs[count + i], refs[-1].at[i]) for i in range(count)]
    for copy in made:
        copy.start()
    for copy in made:
        copy.wait()


def load_adapters(arrays, info):
    count = len(arrays)
    return pl.pallas_call(
        functools.partial(adapter_kernel, count),
        in_specs=[pl.BlockSpec(memory_space=pltpu.SMEM)] + [pl.BlockSpec(memory_space=pltpu.HBM)] * count,
        out_specs=[pl.BlockSpec(memory_space=pltpu.VMEM)] * count,
        out_shape=[pltpu.VMEM(a.shape[1:], a.dtype) for a in arrays],
        scratch_shapes=[pltpu.SemaphoreType.DMA((count,))],
        compiler_params=pltpu.CompilerParams(vmem_limit_bytes=MIB),
        cost_estimate=pl.CostEstimate(flops=1000, transcendentals=0, bytes_accessed=1000),
        name="adapters",
    )(info, *(in_hbm(a) for a in arrays))


def move_rows(kernel, value, slots, name, outs, in_space, out_space, sems):
    return pl.pallas_call(
        kernel,
        in_specs=[pl.BlockSpec(memory_space=pltpu.SMEM), pl.BlockSpec(memory_space=in_space)],
        out_specs=[pl.BlockSpec(memory_space=out_space)] * len(outs),
        out_shape=outs,
        scratch_shapes=[pltpu.SemaphoreType.DMA(sems)],
        compiler_params=pltpu.CompilerParams(vmem_limit_bytes=MIB),
        cost_estimate=pl.CostEstimate(flops=1000, transcendentals=0, bytes_accessed=1000),
        name=name,
    )(slots, pltpu.with_memory_space_constraint(value, in_space))


def sds(shape, dtype):
    return jax.ShapeDtypeStruct(tuple(shape), dtype)


def in_vmem(value):
    return pltpu.with_memory_space_constraint(value, pltpu.VMEM)


def in_hbm(value):
    return pltpu.with_memory_space_constraint(value, pltpu.HBM)


def call(kernel, info, weights, args, outs, scratch, name, mib, after=(), sems=()):
    vmem = pl.BlockSpec(memory_space=pltpu.VMEM)
    scalars = () if info is None else (info,)
    n, w = len(scalars), len(weights)

    def body(*refs):
        at = n + w + len(args)
        kernel(*refs[:at], *refs[at + len(after):])

    return pl.pallas_call(
        body,
        in_specs=[pl.BlockSpec(memory_space=pltpu.SMEM)] * n + [pl.BlockSpec(memory_space=pltpu.HBM)] * w + [vmem] * len(args)
        + [pl.BlockSpec(memory_space=pl.ANY)] * len(after),
        out_specs=[vmem] * len(outs),
        out_shape=[pltpu.VMEM(tuple(s), d) for s, d in outs],
        scratch_shapes=[pltpu.VMEM(s, d) for s, d in scratch] + ([pltpu.SemaphoreType.DMA(sems)] if sems else []),
        compiler_params=pltpu.CompilerParams(vmem_limit_bytes=mib * MIB),
        cost_estimate=pl.CostEstimate(flops=1000, transcendentals=0, bytes_accessed=1000),
        name=name,
    )(*scalars, *(in_hbm(a) for a in weights), *(in_vmem(a) for a in args), *after)


def whole_spec(value):
    zeros = (0,) * value.ndim
    return pl.BlockSpec(value.shape, lambda i, *_: zeros)


def sum_call(kernel, scalars, groups, outs, name):
    args = [v for group in groups for v in group]
    steps = 2
    specs = [pl.BlockSpec((o.shape[0] // steps,) + o.shape[1:], (lambda n: lambda i, *_: (i,) + (0,) * n)(o.ndim - 1))
             for o in outs]
    return pl.pallas_call(
        functools.partial(kernel, [len(group) for group in groups]),
        grid_spec=pltpu.PrefetchScalarGridSpec(
            num_scalar_prefetch=len(scalars), grid=(steps,),
            in_specs=[whole_spec(a) for a in args], out_specs=specs),
        out_shape=outs,
        compiler_params=pltpu.CompilerParams(
            dimension_semantics=("arbitrary",),
            vmem_limit_bytes=4 * MIB + 2 * sum(a.size * a.dtype.itemsize for a in args)
            + sum(o.size * o.dtype.itemsize for o in outs)),
        cost_estimate=pl.CostEstimate(flops=0, transcendentals=0, bytes_accessed=12000000),
        name=name,
    )(*scalars, *args)


def swap(value, bit, axis, size):
    return lax.ppermute(value, axis, [(i, i ^ bit) for i in range(size)])


def near(value):
    return swap(value, 1, "mp", PARTS)


def far(value):
    return swap(value, 2, "mp", PARTS)


def spread(value):
    there = far(value)
    return (value, near(value), there, near(there))


def far_sum_kernel(own, got, out):
    for to, other in ((LO, HI), (HI, LO)):
        out[:, to] = (own[:, to].astype(F32) + got[:, other].astype(F32)).astype(BF16)


def far_sum(own, got):
    return call(far_sum_kernel, None, (), (own, got), [(own.shape, BF16)], [], "far_sum", 6)[0]


def pair_sum_kernel(keep, got, out):
    out[...] = (keep[...] + got[...].astype(F32)).astype(BF16)


def pair_sum(keep, send, *before):
    got = near(send)
    got = late(got, *before) if before else got
    return call(pair_sum_kernel, None, (), (keep, got), [(send.shape, BF16)], [], "pair_sum", 6)[0]


def late(value, *others):
    return lax.optimization_barrier((value, *others))[0]


def doubled(stack, bit, size):
    return jnp.concatenate([stack, swap(stack, bit, "dp", size)], axis=0)


def entry_of(slot, place, size):
    bits = size.bit_length() - 1
    apart = slot ^ place
    return sum(((apart >> b) & 1) << (bits - 1 - b) for b in range(bits))


def shards(dp, residual, attention_gain, query_matrix, key_value_matrix, output_matrix, feedfwd_gain,
           gate_up_matrix, down_matrix, attention_adapter_input, query_adapter_output,
           key_value_adapter_output, output_adapter_input, output_adapter_output, feedfwd_adapter_input,
           feedfwd_adapter_output, down_adapter_input, down_adapter_output, lengths, adapter_index,
           dealing_slots, cotangent):
    seqs = residual.shape[0]
    length = cotangent.shape[1]
    units = down_matrix.shape[0]
    adapters = attention_adapter_input.shape[0]
    q_cols = query_matrix.shape[1]
    kv_cols = key_value_matrix.shape[2]
    kv_heads = kv_cols // HEAD
    heads = q_cols // HEAD
    rows = length // CHUNKS
    half = 2 * QUARTER
    me = lax.axis_index("mp")
    place = lax.axis_index("dp")

    is_there = dealing_slots[None, :] == jnp.arange(seqs, dtype=jnp.int32)[:, None]
    owners = jnp.sum(jnp.where(is_there, adapter_index[None, :], 0), axis=1)
    spans = jnp.sum(jnp.where(is_there, lengths[None, :], 0), axis=1)
    mine = jnp.arange(seqs, dtype=jnp.int32) == place
    my_length = jnp.sum(jnp.where(mine, spans, 0))
    my_adapter = jnp.sum(jnp.where(mine, owners, 0))
    info = jnp.stack([me.astype(jnp.int32), my_length, my_adapter, place.astype(jnp.int32)])

    gs = spread(cotangent[0])
    gains = jnp.stack(spread(jnp.stack([attention_gain, feedfwd_gain])))
    ordered, = move_rows(deal_kernel, residual, dealing_slots, "deal", [pltpu.VMEM(residual.shape, BF16)], pltpu.HBM,
                         pltpu.VMEM, (seqs,))
    dealt = lax.all_to_all(ordered, "dp", split_axis=0, concat_axis=1, tiled=True)[0]
    adapters_here = load_adapters(
        (attention_adapter_input, query_adapter_output, key_value_adapter_output, output_adapter_input,
         output_adapter_output, feedfwd_adapter_input, feedfwd_adapter_output, down_adapter_input,
         down_adapter_output), info)
    a1, qb, kvb, oa, ob, a2, fba, da, bd = adapters_here
    dealt = late(dealt, gs[2], a1, gains)
    beside = near(dealt)
    there = [far(dealt[c * rows:(c + 1) * rows]) for c in range(CHUNKS)]
    xs = [None] * CHUNKS
    cos_np, sin_np = rope_tables(length)
    cos = [jnp.asarray(cos_np[:, c * rows:(c + 1) * rows]) for c in range(CHUNKS)]
    sin = [jnp.asarray(sin_np[:, c * rows:(c + 1) * rows]) for c in range(CHUNKS)]
    wq, wkv, wo = query_matrix, key_value_matrix, output_matrix

    def like(*arrays):
        return [(a.shape, a.dtype) for a in arrays]

    wide, col, block, thin = (rows, WIDTH), (rows, half), (rows, QUARTER), (rows, 1)
    saved, kept, z_own, z_far = ([None] * CHUNKS for _ in range(4))
    order = ()
    for c in range(CHUNKS):
        xs[c] = (dealt, beside, there[c], near(late(there[c], saved[0][0]) if c else there[c]))
        outs = [((3 * RANK, rows), BF16), ((q_cols, rows), BF16), ((kv_heads, rows, HEAD), BF16),
                ((kv_heads, rows, HEAD), BF16), ((kv_cols, rows), BF16), ((kv_cols, rows), BF16)]
        saved[c] = call(
            functools.partial(project_kernel, c), info, (wq, wkv), (*xs[c], gains, a1, qb, kvb, cos[c], sin[c]), outs,
            [(wide, BF16)] + like(wq, wkv), "project_%d" % c, 12, order, (2,))
        outs = [(col, F32), (col, BF16), ((q_cols, rows), BF16), ((heads, rows), F32), ((RANK, rows), BF16)]
        pairs = [v for p in saved[:c + 1] for v in (p[2], p[5])]
        z_keep, z_send, *kept[c] = call(
            functools.partial(attend_kernel, c), info, (wo,), (saved[c][1], oa, ob, *pairs), outs, like(wo),
            "attend_%d" % c, 10, (saved[c][0],), (1,))
        z_own[c] = pair_sum(z_keep, late(z_send, z_far[0] if c else there[-1]))
        z_far[c] = far(z_own[c])
        order = (kept[c][1], z_own[c])
    def front(c, total, partial, order):
        hidden = (rows, units)
        outs = [(wide, BF16), (block, F32), (wide, BF16), (wide, BF16), (hidden, BF16), (hidden, BF16), (hidden, BF16),
                ((rows, 2 * RANK), BF16), ((rows, RANK), BF16),
                ((3 * RANK * units // QUARTER, QUARTER), BF16 if c else F32)]
        args = (*xs[c], total, near(total), *gs, gains, a2, bd, fba, da, *partial)
        weights = () if c else (gate_up_matrix, down_matrix)
        outs += like(*weights)
        return call(
            functools.partial(front_kernel, c, c == CHUNKS - 1), info, weights, (wgu, wd, *args) if c else args, outs,
            [((ROW_BLOCK, WIDTH), F32)], "front_%d" % c, 8, order, () if c else (2, units // QUARTER))

    def back(c, hidden, partial, order):
        first = col if c else (rows + 3 * RANK, half)
        outs = [((rows, RANK), F32), (first, F32), (first, BF16)]
        outs += [((3 * RANK, WIDTH), F32)] if c else []
        return call(
            functools.partial(back_kernel, c == 0), info, (), (wgu, *hidden[2:7], a2, fba, da, *partial), outs,
            [(block, F32), ((3 * RANK, QUARTER), F32)], "back_%d" % c, 8, order)

    def down(c, td, order):
        return call(down_kernel, info, (), (wd, hidden[c][4], td, bd, hidden[c][1]), [(col, F32), (col, BF16)],
                    [(block, F32)], "down_%d" % c, 6, order)

    def attend_back(c, total, partial, order):
        outs = [(block, F32), (col, F32), (col, BF16), (thin, F32), ((3 * RANK, QUARTER), F32 if c else BF16)]
        low = (4 * RANK + SPARE, half)
        outs += ([((4 * RANK, WIDTH), F32), ((kv_cols, rows), F32), ((kv_cols, rows), F32), ((SPARE // 2, rows), F32)]
                 if c else [(low, F32), (low, BF16)])
        scratch = [(wide, BF16), (wide, BF16), ((ROW_BLOCK, WIDTH), F32), ((q_cols, rows), BF16), ((q_cols, rows), F32),
                   ((c + 1, kv_cols, rows), F32), ((c + 1, kv_cols, rows), F32), ((rows, q_cols + 2 * kv_cols), BF16),
                   (block, F32), ((4 * RANK, QUARTER), F32)]
        triples = [v for p in saved[:c + 1] for v in (p[2], p[3], p[4])]
        return call(
            functools.partial(attend_back_kernel, c, c == 0), info, (wq, wkv, wo),
            (*xs[c], *gs, hidden[c][0], total, near(total), gains, a1, qb, kvb, oa, ob, cos[c], sin[c], *saved[c][:2],
             *kept[c], *triples, *partial), outs, scratch + like(wq, wkv, wo), "attend_back_%d" % c, 18, order, (3,))

    bits = [1 << b for b in reversed(range(dp.bit_length() - 1))]
    def to_bands(value):
        return lax.all_to_all(value.reshape(dp, length // dp, QUARTER), "dp", split_axis=0, concat_axis=0, tiled=True)

    def collect(value, name, *before):
        rows_out = sds((seqs, length // dp, QUARTER), BF16)
        return move_rows(collect_kernel, value, late(dealing_slots, *before), name, [rows_out], pltpu.VMEM, pl.ANY,
                         (seqs,))[0]

    hidden, d_own, d_far, y_keep, y_got = ([None] * CHUNKS for _ in range(5))
    *hidden[0], wgu, wd = front(0, far_sum(z_own[0], z_far[0]), (), order)
    step = hidden[0][8]
    hidden[1] = front(1, far_sum(z_own[1], late(z_far[1], step)), hidden[0][9:], (step,))
    fb = hidden[1][9][None]
    fb_first = swap(fb, bits[0], "dp", dp)
    td, d_keep, d_send, fa = back(1, hidden[1], (), (hidden[1][8],))
    d_own[1] = pair_sum(d_keep, late(d_send, fb_first))
    d_far[1] = far(d_own[1])
    fb = fb_more = jnp.concatenate([fb, fb_first], axis=0)
    for bit in bits[1:-1]:
        fb_more = doubled(fb_more, bit, dp)
    fb_more = fb_more[2:]
    fb_side = swap(fb, bits[-1], "dp", dp)
    td_0, d_keep, d_send = back(0, hidden[0], (fa,), (d_own[1],))
    y_keep[1], y_send = down(1, td, (td_0,))
    total = far_sum(d_own[1], late(d_far[1], y_send))
    d_own[0] = pair_sum(d_keep, late(d_send, fb_more, fb_side), total)
    d_far[0] = far(d_own[0])
    fb_more_side = swap(fb_more, bits[-1], "dp", dp)
    y_got[1] = near(late(y_send, d_own[0]))
    dxq, h_keep, h_send, inv, *sums = attend_back(1, total, (), (d_own[0], y_send))
    total = far_sum(d_own[0], late(d_far[0], inv))
    h_got = near(late(h_send, fb_more_side))
    h_high = high_sum((h_keep, h_got))
    h_far = far(h_high)
    final = [None, (dxq, h_keep, h_got, h_far, inv)]
    fa = total[rows:][None]
    fa_first = swap(fa, bits[0], "dp", dp)
    dxq, h_keep, h_send, inv, att_b, aa_keep, aa_send = attend_back(0, total, sums, (h_high,))
    ready = (fa_first, h_far)
    aa_got = near(late(aa_send, *ready))
    aa_high = high_sum((aa_keep, aa_got))
    aa_far = far(aa_high)
    h_got = near(late(h_send, *ready))
    h_high = high_sum((h_keep, h_got))
    h_far = far(h_high)
    final[0] = (dxq, h_keep, h_got, h_far, inv)
    att_a = aa_keep[:4 * RANK, :QUARTER] + aa_got[:4 * RANK, :QUARTER].astype(F32)
    att_a = (att_a + late(aa_far, h_high)[:4 * RANK].astype(F32)).astype(BF16)
    n_b = att_b.shape[0]
    att = jnp.concatenate([att_b, att_a], axis=0)[None]
    y_keep[0], y_send = down(0, td_0, (att,))
    y_got[0] = near(y_send)
    att = first = doubled(att, bits[0], dp)
    att = late(att, h_far, y_send)
    for bit in bits[1:-1]:
        att = doubled(att, bit, dp)
    fa = late(jnp.concatenate([fa, fa_first], axis=0), aa_high)
    for bit in bits[1:-1]:
        fa = doubled(fa, bit, dp)
    fa_side = swap(fa, bits[-1], "dp", dp)

    dinput, = call(finish_kernel, None, (), (gains, dealt, aa_high, aa_far, *(v for f in final for v in f)),
                   [((length, QUARTER), BF16)], [], "finish", 8, (first, y_send, fa_side))
    y_far = far(high_sum(*((k, late(g, dinput)) for k, g in zip(y_keep, y_got))))
    input_grad = collect(to_bands(dinput), "collect_grad")
    outs = [sds((adapters, 2 * RANK, WIDTH), F32), sds((adapters, RANK, WIDTH), F32),
            sds((adapters, 2, RANK, units), F32), sds((adapters, RANK, units), F32)]
    ga_ffn, g_down_b, g_ffn_b, g_down_a = sum_call(
        feedforward_sum_kernel, (info, owners),
        ((fb, fb_more, fb_side, fb_more_side), (fa, fa_side), (near(fa), near(fa_side))), outs, "feedforward_sum")

    result, = call(output_kernel, info, (), (late(y_far, dinput, g_down_a), *(v for p in zip(y_keep, y_got) for v in p)),
                   [((length, QUARTER), BF16)], [], "output", 8)
    output = collect(to_bands(result), "collect_out", input_grad)

    att_side = swap(att, bits[-1], "dp", dp)
    a_parts = [att[:, n_b:], att_side[:, n_b:]]
    a_far = [far(v) for v in a_parts]
    outs = [sds((adapters, 3 * RANK, WIDTH), F32), sds((adapters, RANK, WIDTH), F32),
            sds((adapters, RANK, q_cols), F32), sds((adapters, 2, RANK, kv_cols), F32),
            sds((adapters, RANK, q_cols), F32)]
    ga_att, g_out_b, g_query_b, g_kv_b, g_out_a = sum_call(
        attention_sum_kernel, (info, owners),
        ((att, att_side), a_parts, [near(v) for v in a_parts], a_far, [near(v) for v in a_far]), outs, "attention_sum")
    return (output, input_grad, ga_att, g_query_b, g_kv_b, g_out_a, g_out_b, ga_ffn, g_ffn_b, g_down_a, g_down_b)


def solution(mesh):
    in_specs = (
        P(None, "dp", "mp"), P("mp"), P(None, "mp"), P(None, None, "mp"), P("mp", None), P("mp"),
        P(None, None, "mp"), P("mp", None), P(), P(None, None, "mp"), P(None, None, None, "mp"),
        P(None, None, "mp"), P(), P(), P(None, None, None, "mp"), P(None, None, "mp"), P(), P(), P(), P(),
        P("dp", None, "mp"),
    )
    out_specs = (
        P(None, "dp", "mp"), P(None, "dp", "mp"), P(), P(None, None, "mp"), P(None, None, None, "mp"),
        P(None, None, "mp"), P(), P(), P(None, None, None, "mp"), P(None, None, "mp"), P(),
    )
    return jax.shard_map(
        functools.partial(shards, mesh.shape["dp"]), mesh=mesh, in_specs=in_specs, out_specs=out_specs,
        check_vma=False)
```

```python
import functools

import jax
import jax.numpy as jnp
import numpy as np
from jax import lax
from jax.experimental import pallas as pl
from jax.experimental.pallas import tpu as pltpu
from jax.sharding import PartitionSpec as P

WIDTH = 2048
HEAD = 64
HALF = HEAD // 2
RANK = 16
EPS = 1e-05
ROPE_BASE = 500000.0
NEG_FILL = -1e30
PARTS = 4
LANES = 128
SPARE = 32
ROW_BLOCK = 64
QUARTER = WIDTH // PARTS
CHUNKS = 2
MIB = 1024 * 1024
F32 = jnp.float32
BF16 = jnp.bfloat16


def nn(a, b):
    return lax.dot_general(a, b, (((1,), (0,)), ((), ())), preferred_element_type=F32)


def nt(a, b):
    return lax.dot_general(a, b, (((1,), (1,)), ((), ())), preferred_element_type=F32)


def rope_tables(length):
    freq = ROPE_BASE ** (-np.arange(HALF, dtype=np.float32) * np.float32(2.0 / HEAD))
    angles = (np.arange(length, dtype=np.float32)[None, :] * freq.astype(np.float32)[:, None]).astype(np.float32)
    return np.cos(angles).astype(np.float32), np.sin(angles).astype(np.float32)


def quarter(me, rel):
    return pl.ds(pl.multiple_of((me ^ rel) * QUARTER, QUARTER), QUARTER)


LO, HI = slice(0, QUARTER), slice(QUARTER, 2 * QUARTER)


def total_block(rel, rows_at, own, oth):
    return (own if rel in (0, 2) else oth)[rows_at, LO if rel in (0, 1) else HI].astype(F32)


def store_block(rel, value, rows_at, keep_ref, send_ref):
    to = pl.ds(pl.multiple_of((rel // 2) * QUARTER, QUARTER), QUARTER)

    @pl.when(rel % 2 == 0)
    def _():
        keep_ref[rows_at, to] = value[...]

    @pl.when(rel % 2 == 1)
    def _():
        send_ref[rows_at, to] = value[...].astype(BF16)


def chunk_of(ref, chunk, rows):
    return ref if ref.shape[0] == rows else ref.at[chunk * rows:(chunk + 1) * rows]


def row_block(i):
    return pl.ds(pl.multiple_of(i * ROW_BLOCK, ROW_BLOCK), ROW_BLOCK)


def is_valid(chunk, i, rows, length):
    return chunk * rows + i * ROW_BLOCK + lax.broadcasted_iota(jnp.int32, (ROW_BLOCK, 1), 0) < length


def copies_of(pairs, sems):
    made = [pltpu.make_async_copy(source, target, sems.at[i]) for i, (source, target) in enumerate(pairs)]
    for copy in made:
        copy.start()
    return made


def put_block(rel, value, keep_ref, send_ref):
    ref = keep_ref if rel in (0, 2) else send_ref
    ref[:, LO if rel in (0, 1) else HI] = value.astype(ref.dtype)


def rotate(value, cos, sin, out_ref):
    for i in range(value.shape[0] // HEAD):
        u1, u2 = value[i * HEAD:i * HEAD + HALF], value[i * HEAD + HALF:(i + 1) * HEAD]
        out_ref[i * HEAD:i * HEAD + HALF, :] = (u1 * cos - u2 * sin).astype(BF16)
        out_ref[i * HEAD + HALF:(i + 1) * HEAD, :] = (u2 * cos + u1 * sin).astype(BF16)


def turn_back(value, cos, sin, out_ref):
    for i in range(value.shape[0] // HEAD):
        w1, w2 = value[i * HEAD:i * HEAD + HALF], value[i * HEAD + HALF:(i + 1) * HEAD]
        out_ref[i * HEAD:i * HEAD + HALF, :] = (w1 * cos + w2 * sin).astype(BF16)
        out_ref[i * HEAD + HALF:(i + 1) * HEAD, :] = (w2 * cos - w1 * sin).astype(BF16)


def head_rows(i):
    return pl.ds(pl.multiple_of(i * HEAD, HEAD), HEAD)


def visible(key_start, query_start, rows, length):
    kpos = key_start + lax.broadcasted_iota(jnp.int32, (rows, rows), 0)
    qpos = query_start + lax.broadcasted_iota(jnp.int32, (rows, rows), 1)
    return (kpos <= qpos) & (kpos < length)


def project_kernel(chunk, info, wq_h, wkv_h, x0, x1, x2, x3, gains, a1, qb, kvb, cos_t, sin_t,
                   t1t_out, qt_out, kn_out, vn_out, kt_out, vt_out, h_out, wq, wkv, sems):
    copies = copies_of(((wkv_h, wkv), (wq_h, wq)), sems)
    me = info[0]
    rows = h_out.shape[0]
    kv_heads = kn_out.shape[0]
    xs = [chunk_of(x, chunk, rows) for x in (x0, x1, x2, x3)]

    def norm(i, carry):
        at = row_block(i)
        square = jnp.zeros((ROW_BLOCK, 1), F32)
        for r in range(PARTS):
            v = xs[r][at, :].astype(F32)
            square = square + jnp.sum(v * v, axis=1, keepdims=True)
        inv = lax.rsqrt(square / WIDTH + EPS)
        for r in range(PARTS):
            v = xs[r][at, :].astype(F32)
            h_out[at, quarter(me, r)] = (v * inv * gains[r, 0:1, :].astype(F32)).astype(BF16)
        return carry

    lax.fori_loop(0, rows // ROW_BLOCK, norm, 0)
    h = h_out[...]
    t1 = nt(h, a1[...])
    t1t_out[...] = t1.T.astype(BF16)
    t1b = t1.astype(BF16)
    cos, sin = cos_t[...], sin_t[...]
    copies[0].wait()
    k = nn(h, wkv[0]) + nn(t1b[:, RANK:2 * RANK], kvb[0])
    rotate(k.T, cos, sin, kt_out)
    k_n = kt_out[...].T
    v_n = (nn(h, wkv[1]) + nn(t1b[:, 2 * RANK:], kvb[1])).astype(BF16)
    vt_out[...] = v_n.T
    for i in range(kv_heads):
        kn_out[i] = k_n[:, i * HEAD:(i + 1) * HEAD]
        vn_out[i] = v_n[:, i * HEAD:(i + 1) * HEAD]
    copies[1].wait()
    q = nn(h, wq[...]) + nn(t1b[:, :RANK], qb[...])
    rotate(q.T * (HEAD ** -0.5), cos, sin, qt_out)


def attend_kernel(chunk, info, wo_h, qt, oa, ob, *rest):
    pairs, rest = rest[:2 * (chunk + 1)], rest[2 * (chunk + 1):]
    z_keep, z_send, ot_out, lse_out, tot_out, wo, sems = rest
    copies = copies_of(((wo_h, wo),), sems)
    keys, values = pairs[0::2], pairs[1::2]
    me, length = info[0], info[1]
    rows = qt.shape[1]
    kv_heads = keys[0].shape[0]
    heads = qt.shape[0] // HEAD
    group = heads // kv_heads

    kept = [jnp.concatenate([visible(c * rows, chunk * rows, rows, length)] * group, axis=1) for c in range(chunk + 1)]

    def one_group(j, carry):
        q_g = jnp.concatenate([qt[head_rows(j * group + g), :] for g in range(group)], axis=1)
        parts = [jnp.where(kept[c], nn(keys[c][j], q_g), NEG_FILL) for c in range(chunk + 1)]
        top = functools.reduce(jnp.maximum, [jnp.max(s, axis=0, keepdims=True) for s in parts])
        es = [jnp.exp(s - top) for s in parts]
        total = sum(jnp.sum(e, axis=0, keepdims=True) for e in es)
        low = top + jnp.log(total)
        o_t = sum(nn(value[head_rows(j), :], e.astype(BF16)) for value, e in zip(values, es))
        o_t = (o_t / total).astype(BF16)
        for g in range(group):
            cols = slice(g * rows, (g + 1) * rows)
            lse_out[pl.ds(j * group + g, 1), :] = low[:, cols]
            ot_out[head_rows(j * group + g), :] = o_t[:, cols]
        return carry

    lax.fori_loop(0, kv_heads, one_group, 0)
    o = ot_out[...].T
    to = nt(o, oa[...])
    tot_out[...] = to.T.astype(BF16)
    to = to.astype(BF16)
    copies[0].wait()
    for r in range(PARTS):
        at = quarter(me, r)
        put_block(r, nn(o, wo[:, at]) + nn(to, ob[:, at]), z_keep, z_send)


def front_kernel(chunk, last, info, wgu_in, wd_in, x0, x1, x2, x3, zo, zp, g0, g1, g2, g3, gains, a2, bd, fb, da,
                 *rest):
    units = wd_in.shape[0]
    if chunk:
        wgu, wd = wgu_in, wd_in
    else:
        (wgu, wd, f_s, sems), rest = rest[-4:], rest[:-4]
        rest = (*rest, f_s)

    def copies(i):
        c = pl.ds(pl.multiple_of(i * QUARTER, QUARTER), QUARTER)
        return (pltpu.make_async_copy(wgu_in.at[:, :, c], wgu.at[:, :, c], sems.at[0, i]),
                pltpu.make_async_copy(wd_in.at[c, :], wd.at[c, :], sems.at[1, i]))

    if not chunk:
        for i in range(units // QUARTER):
            for copy in copies(i):
                copy.start()
    f_s = rest[-1]
    xm_out, xq_out, h_out, g_out, act_out, dg_out, du_out, t2_s, dtd_s, b_out = rest[-11:-1]
    me, length = info[0], info[1]
    rows = h_out.shape[0]
    xs, gs = ([chunk_of(v, chunk, rows) for v in vs] for vs in ((x0, x1, x2, x3), (g0, g1, g2, g3)))

    def norm(i, carry):
        at = row_block(i)
        valid = is_valid(chunk, i, rows, length)
        square = jnp.zeros((ROW_BLOCK, 1), F32)
        for r in range(PARTS):
            v = xs[r][at, :].astype(F32) + total_block(r, at, zo, zp)
            if r == 0:
                xq_out[at, :] = v
            f_s[:, quarter(me, r)] = v
            square = square + jnp.sum(v * v, axis=1, keepdims=True)
            g_out[at, quarter(me, r)] = jnp.where(valid, gs[r][at, :], jnp.zeros((), BF16))
        inv = lax.rsqrt(square / WIDTH + EPS)
        for r in range(PARTS):
            v = f_s[:, quarter(me, r)]
            xm_out[at, quarter(me, r)] = v.astype(BF16)
            h_out[at, quarter(me, r)] = (v * inv * gains[r, 1:2, :].astype(F32)).astype(BF16)
        return carry

    lax.fori_loop(0, rows // ROW_BLOCK, norm, 0)
    t2 = nt(h_out[...], a2[...])
    t2_s[...] = t2.astype(BF16)
    dtd = nt(g_out[...], bd[...])
    dtd_s[...] = dtd.astype(BF16)
    t2t, dtdt = t2.T.astype(BF16), dtd.T.astype(BF16)

    def block(i, carry):
        c = pl.ds(pl.multiple_of(i * QUARTER, QUARTER), QUARTER)
        if not chunk:
            for copy in copies(i):
                copy.wait()
        h, g = h_out[...], g_out[...]
        gate = nn(h, wgu[0, :, c]) + nn(t2_s[:, :RANK], fb[0, :, c])
        up = nn(h, wgu[1, :, c]) + nn(t2_s[:, RANK:], fb[1, :, c])
        dact = nt(g, wd[c, :]) + nn(dtd_s[...], da[:, c])
        sig = 1.0 / (1.0 + jnp.exp(-gate))
        silu = gate * sig
        act = (silu * up).astype(BF16)
        dgate = (dact * up * sig * (1.0 + gate * (1.0 - sig))).astype(BF16)
        dup = (dact * silu).astype(BF16)
        act_out[:, c], dg_out[:, c], du_out[:, c] = act, dgate, dup
        for k, value in enumerate((nn(t2t[:RANK], dgate), nn(t2t[RANK:], dup), nn(dtdt, act))):
            at = pl.ds(pl.multiple_of((3 * i + k) * RANK, RANK), RANK)
            if last:
                value = value + rest[0][at, :]
            b_out[at, :] = value.astype(b_out.dtype)
        return carry

    lax.fori_loop(0, units // QUARTER, block, 0)


def back_kernel(last, info, wgu, h, g, act, dg, du, a2, fb, da, *rest):
    (value_s, low_s), rest = rest[-2:], rest[:-2]
    outs, rest = (rest[-3:], rest[:-3]) if last else (rest[-4:], rest[:-4])
    td_out, d_keep, d_send = outs[:3]
    me = info[0]
    rows = h.shape[0]
    dt2 = jnp.concatenate([nt(dg[...], fb[0]), nt(du[...], fb[1])], axis=1)
    td = nt(act[...], da[...])
    td_out[...] = td
    dt2b = dt2.astype(BF16)
    dt2t, tdt = dt2.T.astype(BF16), td.T.astype(BF16)

    def block(r, carry):
        at = quarter(me, r)
        value_s[...] = nt(dg[...], wgu[0, at, :]) + nt(du[...], wgu[1, at, :]) + nn(dt2b, a2[:, at])
        store_block(r, value_s, slice(0, rows), d_keep, d_send)
        low_s[:2 * RANK, :] = nn(dt2t, h[:, at])
        low_s[2 * RANK:, :] = nn(tdt, g[:, at])
        if last:
            low_s[...] += rest[0][:, at]
            store_block(r, low_s, slice(rows, rows + 3 * RANK), d_keep, d_send)
        else:
            outs[3][:, at] = low_s[...]
        return carry

    lax.fori_loop(0, PARTS, block, 0)


def down_kernel(info, wd, act, td, bd, xq, y_keep, y_send, value_s):
    me = info[0]
    tdb = td[...].astype(BF16)

    def block(r, carry):
        at = quarter(me, r)
        value_s[...] = nn(act[...], wd[:, at]) + nn(tdb, bd[:, at])
        store_block(r, value_s, slice(0, act.shape[0]), y_keep, y_send)
        return carry

    lax.fori_loop(0, PARTS, block, 0)
    y_keep[:, LO] += xq[...]


def attend_back_kernel(chunk, last, info, wq_h, wkv_h, wo_h, x0, x1, x2, x3, g0, g1, g2, g3, xm, do_, dp, gains, a1,
                       qb, kvb, oa, ob, cos_t, sin_t, t1t, qt, ot, lse, tot, *rest):
    scratch, rest = rest[-14:], rest[:-14]
    h_in, z_s, f_s, dot_s, dqt_s, dkt_s, dvt_s, dq_s, value_s, low_s, wq, wkv, wo, sems = scratch
    copies = copies_of(((wo_h, wo), (wq_h, wq), (wkv_h, wkv)), sems)
    n_out = 7 if last else 9
    outs, rest = rest[-n_out:], rest[:-n_out]
    dxq_out, h_keep, h_send, inv_out, b_out = outs[:5]
    triples, rest = rest[:3 * (chunk + 1)], rest[3 * (chunk + 1):]
    keys, values, keys_t = triples[0::3], triples[1::3], triples[2::3]
    me, length = info[0], info[1]
    rows = xm.shape[0]
    kv_heads = keys[0].shape[0]
    heads = qt.shape[0] // HEAD
    group = heads // kv_heads
    q_cols, kv_cols = heads * HEAD, kv_heads * HEAD
    xs, gs = ([chunk_of(v, chunk, rows) for v in vs] for vs in ((x0, x1, x2, x3), (g0, g1, g2, g3)))

    def norm_back(i, carry):
        at = row_block(i)
        valid = is_valid(chunk, i, rows, length)
        square, first, inner = (jnp.zeros((ROW_BLOCK, 1), F32) for _ in range(3))
        for r in range(PARTS):
            v = xm[at, quarter(me, r)].astype(F32)
            square = square + jnp.sum(v * v, axis=1, keepdims=True)
            w = total_block(r, at, do_, dp) * gains[r, 1:2, :].astype(F32)
            f_s[:, quarter(me, r)] = w
            inner = inner + jnp.sum(v * w, axis=1, keepdims=True)
            u = xs[r][at, :].astype(F32)
            first = first + jnp.sum(u * u, axis=1, keepdims=True)
        inv_one = lax.rsqrt(first / WIDTH + EPS)
        inv_out[at, :] = inv_one
        inv = lax.rsqrt(square / WIDTH + EPS)
        back = inv * inv * inv * inner / WIDTH
        for r in range(PARTS):
            v = xm[at, quarter(me, r)].astype(F32)
            g = jnp.where(valid, gs[r][at, :].astype(F32), 0.0)
            d = g + inv * f_s[:, quarter(me, r)] - v * back
            if r == 0:
                dxq_out[at, :] = d
            z_s[at, quarter(me, r)] = d.astype(BF16)
            u = xs[r][at, :].astype(F32)
            h_in[at, quarter(me, r)] = (u * inv_one * gains[r, 0:1, :].astype(F32)).astype(BF16)
        return carry

    lax.fori_loop(0, rows // ROW_BLOCK, norm_back, 0)
    dz = z_s[...]
    dto = nt(dz, ob[...])
    copies[0].wait()
    d_o = nt(dz, wo[...]) + nn(dto.astype(BF16), oa[...])
    dot_s[...] = d_o.T.astype(BF16)
    kept = [jnp.concatenate([visible(c * rows, chunk * rows, rows, length)] * group, axis=1) for c in range(chunk + 1)]

    def one_group(j, carry):
        places = [head_rows(j * group + g) for g in range(group)]
        q_g = jnp.concatenate([qt[at, :] for at in places], axis=1)
        do_g = jnp.concatenate([dot_s[at, :] for at in places], axis=1)
        o_g = jnp.concatenate([ot[at, :] for at in places], axis=1)
        low = jnp.concatenate([lse[pl.ds(j * group + g, 1), :] for g in range(group)], axis=1)
        dots = jnp.sum(do_g.astype(F32) * o_g.astype(F32), axis=0, keepdims=True)
        dq_g = 0.0
        for c in range(chunk + 1):
            prob = jnp.where(kept[c], jnp.exp(nn(keys[c][j], q_g) - low), 0.0)
            ds = (prob * (nn(values[c][j], do_g) - dots)).astype(BF16)
            dq_g = dq_g + nn(keys_t[c][head_rows(j), :], ds)
            dk, dv = nt(q_g, ds), nt(do_g, prob.astype(BF16))
            if last:
                dk, dv = dk + rest[2][head_rows(j), :], dv + rest[3][head_rows(j), :]
            dkt_s[c, head_rows(j), :], dvt_s[c, head_rows(j), :] = dk, dv
        for g in range(group):
            dqt_s[places[g], :] = dq_g[:, g * rows:(g + 1) * rows]
        return carry

    lax.fori_loop(0, kv_heads, one_group, 0)
    if not last:
        outs[6][...], outs[7][...] = dkt_s[0], dvt_s[0]
    cos, sin = cos_t[...], sin_t[...]
    dto_t, o_t = dto.T.astype(BF16), ot[...]
    d_out_a = nt(dto_t, o_t)
    turn_back(dqt_s[...], cos * (HEAD ** -0.5), sin * (HEAD ** -0.5), dot_s)
    dq_s[:, :q_cols] = dot_s[...].T
    turn_back(dkt_s[chunk], cos, sin, dot_s)
    dq_s[:, q_cols:q_cols + kv_cols] = dot_s[:kv_cols, :].T
    dq_s[:, q_cols + kv_cols:] = dvt_s[chunk].T.astype(BF16)
    dq, dk, dv = dq_s[:, :q_cols], dq_s[:, q_cols:q_cols + kv_cols], dq_s[:, q_cols + kv_cols:]
    dt1 = jnp.concatenate([nt(dq, qb[...]), nt(dk, kvb[0]), nt(dv, kvb[1])], axis=1)
    dt1b = dt1.astype(BF16)
    kv_pad = jnp.zeros((RANK, QUARTER - 2 * kv_cols), F32)
    d_kv = jnp.concatenate([nn(t1t[RANK:2 * RANK, :], dk), nn(t1t[2 * RANK:, :], dv), kv_pad], axis=1)
    for k, value in enumerate((nn(t1t[:RANK, :], dq), d_out_a, d_kv)):
        at = slice(k * RANK, (k + 1) * RANK)
        if last:
            value = value + rest[0][at, :]
        b_out[at, :] = value.astype(b_out.dtype)
    dt1t = dt1.T.astype(BF16)
    copies[1].wait()
    copies[2].wait()

    def block(r, inner):
        at = quarter(me, r)
        d = nt(dq_s[:, :q_cols], wq[at, :]) + nn(dt1b, a1[:, at])
        d = d + nt(dq_s[:, q_cols:q_cols + kv_cols], wkv[0, at, :]) + nt(dq_s[:, q_cols + kv_cols:], wkv[1, at, :])
        value_s[...] = d
        store_block(r, value_s, slice(0, rows), h_keep, h_send)
        low_s[:3 * RANK, :] = nn(dt1t, h_in[:, at])
        low_s[3 * RANK:, :] = nn(tot[...], z_s[:, at])
        if last:
            low_s[...] += rest[1][:, at]
            store_block(r, low_s, slice(0, 4 * RANK), outs[5], outs[6])
        else:
            outs[5][:, at] = low_s[...]
        return inner + jnp.sum(d * h_in[:, at].astype(F32), axis=1, keepdims=True)

    inner = lax.fori_loop(0, PARTS, block, jnp.zeros((rows, 1), F32))
    inner = jnp.broadcast_to(inner, (rows, LANES)).T[:SPARE // 2, :]
    if last:
        for ref in outs[5:7]:
            for c, value in enumerate((inner, rest[4][...])):
                at = slice(4 * RANK + c * SPARE // 2, 4 * RANK + (c + 1) * SPARE // 2)
                ref[at, QUARTER:QUARTER + rows] = value.astype(ref.dtype)
                ref[at, QUARTER + rows:] = jnp.zeros((SPARE // 2, QUARTER - rows), ref.dtype)
                ref[at, :QUARTER] = jnp.zeros((SPARE // 2, QUARTER), ref.dtype)
    else:
        outs[8][...] = inner


def output_kernel(info, y_far, *refs):
    out = refs[-1]
    rows = out.shape[0] // CHUNKS
    for c in range(CHUNKS):
        y_keep, y_got = refs[2 * c:2 * (c + 1)]
        at = slice(c * rows, (c + 1) * rows)
        valid = c * rows + lax.broadcasted_iota(jnp.int32, (rows, 1), 0) < info[1]
        y = y_keep[:, LO] + y_got[:, LO].astype(F32) + y_far[at, :].astype(F32)
        out[at, :] = jnp.where(valid, y, 0.0).astype(BF16)


def finish_kernel(gains, x_all, aa_high, aa_far, *refs):
    out = refs[-1]
    gain = gains[0, 0:1, :].astype(F32)
    rows = out.shape[0] // CHUNKS
    inner = aa_high[4 * RANK:, :].astype(F32) + aa_far[4 * RANK:, :].astype(F32)
    for c in range(CHUNKS):
        dx, keep, got, there, inv = refs[5 * c:5 * (c + 1)]
        x = chunk_of(x_all, c, rows)
        mine = inner[c * SPARE // 2:c * SPARE // 2 + 8, :rows].T[:, 0:1]
        inv = inv[...]
        grad = keep[:, LO] + got[:, LO].astype(F32) + there[...].astype(F32)
        grad = inv * (gain * grad) - x[...].astype(F32) * (inv * inv * mine / WIDTH)
        out[c * rows:(c + 1) * rows, :] = (dx[...] + grad).astype(BF16)


def high_sum_kernel(*refs):
    out = refs[-1]
    rows = out.shape[0] // (len(refs) // 2)
    for c in range(len(refs) // 2):
        keep, got = refs[2 * c:2 * c + 2]
        out[c * rows:(c + 1) * rows, :] = (keep[:, HI] + got[:, HI].astype(F32)).astype(BF16)


def high_sum(*pairs):
    args = [v for pair in pairs for v in pair]
    rows = sum(keep.shape[0] for keep, _ in pairs)
    return call(high_sum_kernel, None, (), args, [((rows, QUARTER), BF16)], [], "high_sum", 8)[0]


def split_refs(refs, counts):
    groups = []
    for count in counts:
        groups.append(refs[:count])
        refs = refs[count:]
    return groups, refs


def with_entry(parts, at, use):
    start = 0
    for ref in parts:
        @pl.when((at >= start) & (at < start + ref.shape[0]))
        def _(ref=ref, start=start):
            use(ref, at - start)
        start += ref.shape[0]


def sum_slots(info, owners, out_refs, one_slot):
    count = out_refs[0].shape[0]
    base = pl.program_id(0) * count
    slots = owners.shape[0]
    for ref in out_refs:
        ref[...] = jnp.zeros_like(ref)

    def add(slot, carry):
        owner = owners[slot] - base

        @pl.when((owner >= 0) & (owner < count))
        def _():
            one_slot(owner, entry_of(slot, info[3], slots))
        return carry

    lax.fori_loop(0, slots, add, 0)


def feedforward_sum_kernel(counts, info, owners, *refs):
    (b_parts, *a_parts), outs = split_refs(refs, counts)
    ga, gdb, gb, gda = outs
    me = info[0]

    def one_slot(owner, at):
        def add_b(ref, e):
            for i in range(gda.shape[2] // QUARTER):
                cols = slice(i * QUARTER, (i + 1) * QUARTER)
                base = i * 3 * RANK
                gb[owner, 0, :, cols] += ref[e, base:base + RANK, :].astype(F32)
                gb[owner, 1, :, cols] += ref[e, base + RANK:base + 2 * RANK, :].astype(F32)
                gda[owner, :, cols] += ref[e, base + 2 * RANK:base + 3 * RANK, :].astype(F32)

        with_entry(b_parts, at, add_b)
        for near_bit, parts in enumerate(a_parts):
            def add_a(ref, e, near_bit=near_bit):
                for r, cols in ((near_bit, LO), (near_bit ^ 2, HI)):
                    ga[owner, :, quarter(me, r)] += ref[e, :2 * RANK, cols].astype(F32)
                    gdb[owner, :, quarter(me, r)] += ref[e, 2 * RANK:, cols].astype(F32)

            with_entry(parts, at, add_a)

    sum_slots(info, owners, outs, one_slot)


def attention_sum_kernel(counts, info, owners, *refs):
    (b_parts, *a_parts), outs = split_refs(refs, counts)
    ga, gob, gq, gkv, goa = outs
    me = info[0]
    kv_cols = gkv.shape[3]

    def one_slot(owner, at):
        def add_b(ref, e):
            gq[owner] += ref[e, :RANK, :].astype(F32)
            goa[owner] += ref[e, RANK:2 * RANK, :].astype(F32)
            gkv[owner, 0] += ref[e, 2 * RANK:3 * RANK, :kv_cols].astype(F32)
            gkv[owner, 1] += ref[e, 2 * RANK:3 * RANK, kv_cols:2 * kv_cols].astype(F32)

        with_entry(b_parts, at, add_b)
        for r, parts in enumerate(a_parts):
            def add_a(ref, e, r=r):
                ga[owner, :, quarter(me, r)] += ref[e, :3 * RANK, :].astype(F32)
                gob[owner, :, quarter(me, r)] += ref[e, 3 * RANK:, :].astype(F32)

            with_entry(parts, at, add_a)

    sum_slots(info, owners, outs, one_slot)


def deal_kernel(slots, source, out, sems):
    made = [pltpu.make_async_copy(source.at[i], out.at[slots[i]], sems.at[i]) for i in range(source.shape[0])]
    for copy in made:
        copy.start()
    for copy in made:
        copy.wait()


def collect_kernel(slots, source, out, sems):
    made = [pltpu.make_async_copy(source.at[slots[i]], out.at[i], sems.at[i]) for i in range(source.shape[0])]
    for copy in made:
        copy.start()
    for copy in made:
        copy.wait()


def adapter_kernel(count, info, *refs):
    made = [pltpu.make_async_copy(refs[i].at[info[2]], refs[count + i], refs[-1].at[i]) for i in range(count)]
    for copy in made:
        copy.start()
    for copy in made:
        copy.wait()


def load_adapters(arrays, info):
    count = len(arrays)
    return pl.pallas_call(
        functools.partial(adapter_kernel, count),
        in_specs=[pl.BlockSpec(memory_space=pltpu.SMEM)] + [pl.BlockSpec(memory_space=pltpu.HBM)] * count,
        out_specs=[pl.BlockSpec(memory_space=pltpu.VMEM)] * count,
        out_shape=[pltpu.VMEM(a.shape[1:], a.dtype) for a in arrays],
        scratch_shapes=[pltpu.SemaphoreType.DMA((count,))],
        compiler_params=pltpu.CompilerParams(vmem_limit_bytes=MIB),
        cost_estimate=pl.CostEstimate(flops=1000, transcendentals=0, bytes_accessed=1000),
        name="adapters",
    )(info, *(in_hbm(a) for a in arrays))


def move_rows(kernel, value, slots, name, outs, in_space, out_space, sems):
    return pl.pallas_call(
        kernel,
        in_specs=[pl.BlockSpec(memory_space=pltpu.SMEM), pl.BlockSpec(memory_space=in_space)],
        out_specs=[pl.BlockSpec(memory_space=out_space)] * len(outs),
        out_shape=outs,
        scratch_shapes=[pltpu.SemaphoreType.DMA(sems)],
        compiler_params=pltpu.CompilerParams(vmem_limit_bytes=MIB),
        cost_estimate=pl.CostEstimate(flops=1000, transcendentals=0, bytes_accessed=1000),
        name=name,
    )(slots, pltpu.with_memory_space_constraint(value, in_space))


def sds(shape, dtype):
    return jax.ShapeDtypeStruct(tuple(shape), dtype)


def in_vmem(value):
    return pltpu.with_memory_space_constraint(value, pltpu.VMEM)


def in_hbm(value):
    return pltpu.with_memory_space_constraint(value, pltpu.HBM)


def call(kernel, info, weights, args, outs, scratch, name, mib, after=(), sems=()):
    vmem = pl.BlockSpec(memory_space=pltpu.VMEM)
    scalars = () if info is None else (info,)
    n, w = len(scalars), len(weights)

    def body(*refs):
        at = n + w + len(args)
        kernel(*refs[:at], *refs[at + len(after):])

    return pl.pallas_call(
        body,
        in_specs=[pl.BlockSpec(memory_space=pltpu.SMEM)] * n + [pl.BlockSpec(memory_space=pltpu.HBM)] * w + [vmem] * len(args)
        + [pl.BlockSpec(memory_space=pl.ANY)] * len(after),
        out_specs=[vmem] * len(outs),
        out_shape=[pltpu.VMEM(tuple(s), d) for s, d in outs],
        scratch_shapes=[pltpu.VMEM(s, d) for s, d in scratch] + ([pltpu.SemaphoreType.DMA(sems)] if sems else []),
        compiler_params=pltpu.CompilerParams(vmem_limit_bytes=mib * MIB),
        cost_estimate=pl.CostEstimate(flops=1000, transcendentals=0, bytes_accessed=1000),
        name=name,
    )(*scalars, *(in_hbm(a) for a in weights), *(in_vmem(a) for a in args), *after)


def whole_spec(value):
    zeros = (0,) * value.ndim
    return pl.BlockSpec(value.shape, lambda i, *_: zeros)


def sum_call(kernel, scalars, groups, outs, name):
    args = [v for group in groups for v in group]
    steps = 2
    specs = [pl.BlockSpec((o.shape[0] // steps,) + o.shape[1:], (lambda n: lambda i, *_: (i,) + (0,) * n)(o.ndim - 1))
             for o in outs]
    return pl.pallas_call(
        functools.partial(kernel, [len(group) for group in groups]),
        grid_spec=pltpu.PrefetchScalarGridSpec(
            num_scalar_prefetch=len(scalars), grid=(steps,),
            in_specs=[whole_spec(a) for a in args], out_specs=specs),
        out_shape=outs,
        compiler_params=pltpu.CompilerParams(
            dimension_semantics=("arbitrary",),
            vmem_limit_bytes=4 * MIB + 2 * sum(a.size * a.dtype.itemsize for a in args)
            + sum(o.size * o.dtype.itemsize for o in outs)),
        cost_estimate=pl.CostEstimate(flops=0, transcendentals=0, bytes_accessed=12000000),
        name=name,
    )(*scalars, *args)


def swap(value, bit, axis, size):
    return lax.ppermute(value, axis, [(i, i ^ bit) for i in range(size)])


def near(value):
    return swap(value, 1, "mp", PARTS)


def far(value):
    return swap(value, 2, "mp", PARTS)


def spread(value):
    there = far(value)
    return (value, near(value), there, near(there))


def far_sum_kernel(own, got, out):
    for to, other in ((LO, HI), (HI, LO)):
        out[:, to] = (own[:, to].astype(F32) + got[:, other].astype(F32)).astype(BF16)


def far_sum(own, got):
    return call(far_sum_kernel, None, (), (own, got), [(own.shape, BF16)], [], "far_sum", 6)[0]


def pair_sum_kernel(keep, got, out):
    out[...] = (keep[...] + got[...].astype(F32)).astype(BF16)


def pair_sum(keep, send, *before):
    got = near(send)
    got = late(got, *before) if before else got
    return call(pair_sum_kernel, None, (), (keep, got), [(send.shape, BF16)], [], "pair_sum", 6)[0]


def late(value, *others):
    return lax.optimization_barrier((value, *others))[0]


def doubled(stack, bit, size):
    return jnp.concatenate([stack, swap(stack, bit, "dp", size)], axis=0)


def entry_of(slot, place, size):
    bits = size.bit_length() - 1
    apart = slot ^ place
    return sum(((apart >> b) & 1) << (bits - 1 - b) for b in range(bits))


def shards(dp, residual, attention_gain, query_matrix, key_value_matrix, output_matrix, feedfwd_gain,
           gate_up_matrix, down_matrix, attention_adapter_input, query_adapter_output,
           key_value_adapter_output, output_adapter_input, output_adapter_output, feedfwd_adapter_input,
           feedfwd_adapter_output, down_adapter_input, down_adapter_output, lengths, adapter_index,
           dealing_slots, cotangent):
    seqs = residual.shape[0]
    length = cotangent.shape[1]
    units = down_matrix.shape[0]
    adapters = attention_adapter_input.shape[0]
    q_cols = query_matrix.shape[1]
    kv_cols = key_value_matrix.shape[2]
    kv_heads = kv_cols // HEAD
    heads = q_cols // HEAD
    rows = length // CHUNKS
    half = 2 * QUARTER
    me = lax.axis_index("mp")
    place = lax.axis_index("dp")

    is_there = dealing_slots[None, :] == jnp.arange(seqs, dtype=jnp.int32)[:, None]
    owners = jnp.sum(jnp.where(is_there, adapter_index[None, :], 0), axis=1)
    spans = jnp.sum(jnp.where(is_there, lengths[None, :], 0), axis=1)
    mine = jnp.arange(seqs, dtype=jnp.int32) == place
    my_length = jnp.sum(jnp.where(mine, spans, 0))
    my_adapter = jnp.sum(jnp.where(mine, owners, 0))
    info = jnp.stack([me.astype(jnp.int32), my_length, my_adapter, place.astype(jnp.int32)])

    gs = spread(cotangent[0])
    gains = jnp.stack(spread(jnp.stack([attention_gain, feedfwd_gain])))
    ordered, = move_rows(deal_kernel, residual, dealing_slots, "deal", [pltpu.VMEM(residual.shape, BF16)], pltpu.HBM,
                         pltpu.VMEM, (seqs,))
    dealt = lax.all_to_all(ordered, "dp", split_axis=0, concat_axis=1, tiled=True)[0]
    adapters_here = load_adapters(
        (attention_adapter_input, query_adapter_output, key_value_adapter_output, output_adapter_input,
         output_adapter_output, feedfwd_adapter_input, feedfwd_adapter_output, down_adapter_input,
         down_adapter_output), info)
    a1, qb, kvb, oa, ob, a2, fba, da, bd = adapters_here
    dealt = late(dealt, a1, gains)
    beside = near(dealt)
    there = [far(dealt[c * rows:(c + 1) * rows]) for c in range(CHUNKS)]
    xs = [None] * CHUNKS
    cos_np, sin_np = rope_tables(length)
    cos = [jnp.asarray(cos_np[:, c * rows:(c + 1) * rows]) for c in range(CHUNKS)]
    sin = [jnp.asarray(sin_np[:, c * rows:(c + 1) * rows]) for c in range(CHUNKS)]
    wq, wkv, wo = query_matrix, key_value_matrix, output_matrix

    def like(*arrays):
        return [(a.shape, a.dtype) for a in arrays]

    wide, col, block, thin = (rows, WIDTH), (rows, half), (rows, QUARTER), (rows, 1)
    saved, kept, z_own, z_far = ([None] * CHUNKS for _ in range(4))
    order = ()
    for c in range(CHUNKS):
        xs[c] = (dealt, beside, there[c], near(late(there[c], saved[0][0]) if c else late(there[c], gs[2])))
        outs = [((3 * RANK, rows), BF16), ((q_cols, rows), BF16), ((kv_heads, rows, HEAD), BF16),
                ((kv_heads, rows, HEAD), BF16), ((kv_cols, rows), BF16), ((kv_cols, rows), BF16)]
        saved[c] = call(
            functools.partial(project_kernel, c), info, (wq, wkv), (*xs[c], gains, a1, qb, kvb, cos[c], sin[c]), outs,
            [(wide, BF16)] + like(wq, wkv), "project_%d" % c, 12, order, (2,))
        outs = [(col, F32), (col, BF16), ((q_cols, rows), BF16), ((heads, rows), F32), ((RANK, rows), BF16)]
        pairs = [v for p in saved[:c + 1] for v in (p[2], p[5])]
        z_keep, z_send, *kept[c] = call(
            functools.partial(attend_kernel, c), info, (wo,), (saved[c][1], oa, ob, *pairs), outs, like(wo),
            "attend_%d" % c, 10, (saved[c][0],), (1,))
        z_own[c] = pair_sum(z_keep, late(z_send, z_far[0] if c else there[-1]))
        z_far[c] = far(z_own[c])
        order = (kept[c][1], z_own[c])
    def front(c, total, partial, order):
        hidden = (rows, units)
        outs = [(wide, BF16), (block, F32), (wide, BF16), (wide, BF16), (hidden, BF16), (hidden, BF16), (hidden, BF16),
                ((rows, 2 * RANK), BF16), ((rows, RANK), BF16),
                ((3 * RANK * units // QUARTER, QUARTER), BF16 if c else F32)]
        args = (*xs[c], total, near(total), *gs, gains, a2, bd, fba, da, *partial)
        weights = () if c else (gate_up_matrix, down_matrix)
        outs += like(*weights)
        return call(
            functools.partial(front_kernel, c, c == CHUNKS - 1), info, weights, (wgu, wd, *args) if c else args, outs,
            [((ROW_BLOCK, WIDTH), F32)], "front_%d" % c, 8, order, () if c else (2, units // QUARTER))

    def back(c, hidden, partial, order):
        first = col if c else (rows + 3 * RANK, half)
        outs = [((rows, RANK), F32), (first, F32), (first, BF16)]
        outs += [((3 * RANK, WIDTH), F32)] if c else []
        return call(
            functools.partial(back_kernel, c == 0), info, (), (wgu, *hidden[2:7], a2, fba, da, *partial), outs,
            [(block, F32), ((3 * RANK, QUARTER), F32)], "back_%d" % c, 8, order)

    def down(c, td, order):
        return call(down_kernel, info, (), (wd, hidden[c][4], td, bd, hidden[c][1]), [(col, F32), (col, BF16)],
                    [(block, F32)], "down_%d" % c, 6, order)

    def attend_back(c, total, partial, order):
        outs = [(block, F32), (col, F32), (col, BF16), (thin, F32), ((3 * RANK, QUARTER), F32 if c else BF16)]
        low = (4 * RANK + SPARE, half)
        outs += ([((4 * RANK, WIDTH), F32), ((kv_cols, rows), F32), ((kv_cols, rows), F32), ((SPARE // 2, rows), F32)]
                 if c else [(low, F32), (low, BF16)])
        scratch = [(wide, BF16), (wide, BF16), ((ROW_BLOCK, WIDTH), F32), ((q_cols, rows), BF16), ((q_cols, rows), F32),
                   ((c + 1, kv_cols, rows), F32), ((c + 1, kv_cols, rows), F32), ((rows, q_cols + 2 * kv_cols), BF16),
                   (block, F32), ((4 * RANK, QUARTER), F32)]
        triples = [v for p in saved[:c + 1] for v in (p[2], p[3], p[4])]
        return call(
            functools.partial(attend_back_kernel, c, c == 0), info, (wq, wkv, wo),
            (*xs[c], *gs, hidden[c][0], total, near(total), gains, a1, qb, kvb, oa, ob, cos[c], sin[c], *saved[c][:2],
             *kept[c], *triples, *partial), outs, scratch + like(wq, wkv, wo), "attend_back_%d" % c, 18, order, (3,))

    bits = [1 << b for b in reversed(range(dp.bit_length() - 1))]
    def to_bands(value):
        return lax.all_to_all(value.reshape(dp, length // dp, QUARTER), "dp", split_axis=0, concat_axis=0, tiled=True)

    def collect(value, name, *before):
        rows_out = sds((seqs, length // dp, QUARTER), BF16)
        return move_rows(collect_kernel, value, late(dealing_slots, *before), name, [rows_out], pltpu.VMEM, pl.ANY,
                         (seqs,))[0]

    hidden, d_own, d_far, y_keep, y_got = ([None] * CHUNKS for _ in range(5))
    *hidden[0], wgu, wd = front(0, far_sum(z_own[0], z_far[0]), (), order)
    step = hidden[0][8]
    hidden[1] = front(1, far_sum(z_own[1], late(z_far[1], step)), hidden[0][9:], (step,))
    fb = hidden[1][9][None]
    fb_first = swap(fb, bits[0], "dp", dp)
    td, d_keep, d_send, fa = back(1, hidden[1], (), (hidden[1][8],))
    d_own[1] = pair_sum(d_keep, late(d_send, fb_first))
    d_far[1] = far(d_own[1])
    fb = fb_more = jnp.concatenate([fb, fb_first], axis=0)
    for bit in bits[1:-1]:
        fb_more = doubled(fb_more, bit, dp)
    fb_more = fb_more[2:]
    fb_side = swap(fb, bits[-1], "dp", dp)
    td_0, d_keep, d_send = back(0, hidden[0], (fa,), (d_own[1],))
    y_keep[1], y_send = down(1, td, (td_0,))
    total = far_sum(d_own[1], late(d_far[1], y_send))
    d_own[0] = pair_sum(d_keep, late(d_send, fb_more, fb_side), total)
    d_far[0] = far(d_own[0])
    fb_more_side = swap(fb_more, bits[-1], "dp", dp)
    y_got[1] = near(late(y_send, d_own[0]))
    dxq, h_keep, h_send, inv, *sums = attend_back(1, total, (), (d_own[0], y_send))
    total = far_sum(d_own[0], late(d_far[0], inv))
    h_got = near(late(h_send, fb_more_side))
    h_high = high_sum((h_keep, h_got))
    h_far = far(h_high)
    final = [None, (dxq, h_keep, h_got, h_far, inv)]
    fa = total[rows:][None]
    fa_first = swap(fa, bits[0], "dp", dp)
    dxq, h_keep, h_send, inv, att_b, aa_keep, aa_send = attend_back(0, total, sums, (h_high,))
    ready = (fa_first, h_far)
    aa_got = near(late(aa_send, *ready))
    aa_high = high_sum((aa_keep, aa_got))
    aa_far = far(aa_high)
    h_got = near(late(h_send, *ready))
    h_high = high_sum((h_keep, h_got))
    h_far = far(h_high)
    final[0] = (dxq, h_keep, h_got, h_far, inv)
    att_a = aa_keep[:4 * RANK, :QUARTER] + aa_got[:4 * RANK, :QUARTER].astype(F32)
    att_a = (att_a + late(aa_far, h_high)[:4 * RANK].astype(F32)).astype(BF16)
    n_b = att_b.shape[0]
    att = jnp.concatenate([att_b, att_a], axis=0)[None]
    y_keep[0], y_send = down(0, td_0, (att,))
    y_got[0] = near(y_send)
    att = doubled(att, bits[0], dp)
    att = late(att, h_far, y_send)
    for bit in bits[1:-1]:
        att = doubled(att, bit, dp)
    fa = late(jnp.concatenate([fa, fa_first], axis=0), aa_high)
    for bit in bits[1:-1]:
        fa = doubled(fa, bit, dp)
    fa_side = swap(fa, bits[-1], "dp", dp)
    y_far = far(high_sum(*((k, late(g, h_far)) for k, g in zip(y_keep, y_got))))

    dinput, = call(finish_kernel, None, (), (gains, dealt, aa_high, aa_far, *(v for f in final for v in f)),
                   [((length, QUARTER), BF16)], [], "finish", 8, (att, fa_side))
    input_grad = collect(to_bands(dinput), "collect_grad")
    outs = [sds((adapters, 2 * RANK, WIDTH), F32), sds((adapters, RANK, WIDTH), F32),
            sds((adapters, 2, RANK, units), F32), sds((adapters, RANK, units), F32)]
    ga_ffn, g_down_b, g_ffn_b, g_down_a = sum_call(
        feedforward_sum_kernel, (info, owners),
        ((fb, fb_more, fb_side, fb_more_side), (fa, fa_side), (near(fa), near(fa_side))), outs, "feedforward_sum")

    result, = call(output_kernel, info, (), (late(y_far, dinput, g_down_a), *(v for p in zip(y_keep, y_got) for v in p)),
                   [((length, QUARTER), BF16)], [], "output", 8)
    output = collect(to_bands(result), "collect_out", input_grad)

    att_side = swap(att, bits[-1], "dp", dp)
    a_parts = [att[:, n_b:], att_side[:, n_b:]]
    a_far = [far(v) for v in a_parts]
    outs = [sds((adapters, 3 * RANK, WIDTH), F32), sds((adapters, RANK, WIDTH), F32),
            sds((adapters, RANK, q_cols), F32), sds((adapters, 2, RANK, kv_cols), F32),
            sds((adapters, RANK, q_cols), F32)]
    ga_att, g_out_b, g_query_b, g_kv_b, g_out_a = sum_call(
        attention_sum_kernel, (info, owners),
        ((att, att_side), a_parts, [near(v) for v in a_parts], a_far, [near(v) for v in a_far]), outs, "attention_sum")
    return (output, input_grad, ga_att, g_query_b, g_kv_b, g_out_a, g_out_b, ga_ffn, g_ffn_b, g_down_a, g_down_b)


def solution(mesh):
    in_specs = (
        P(None, "dp", "mp"), P("mp"), P(None, "mp"), P(None, None, "mp"), P("mp", None), P("mp"),
        P(None, None, "mp"), P("mp", None), P(), P(None, None, "mp"), P(None, None, None, "mp"),
        P(None, None, "mp"), P(), P(), P(None, None, None, "mp"), P(None, None, "mp"), P(), P(), P(), P(),
        P("dp", None, "mp"),
    )
    out_specs = (
        P(None, "dp", "mp"), P(None, "dp", "mp"), P(), P(None, None, "mp"), P(None, None, None, "mp"),
        P(None, None, "mp"), P(), P(), P(None, None, None, "mp"), P(None, None, "mp"), P(),
    )
    return jax.shard_map(
        functools.partial(shards, mesh.shape["dp"]), mesh=mesh, in_specs=in_specs, out_specs=out_specs,
        check_vma=False)
```

```python
import functools

import jax
import jax.numpy as jnp
import numpy as np
from jax import lax
from jax.experimental import pallas as pl
from jax.experimental.pallas import tpu as pltpu
from jax.sharding import PartitionSpec as P

WIDTH = 2048
HEAD = 64
HALF = HEAD // 2
RANK = 16
EPS = 1e-05
ROPE_BASE = 500000.0
NEG_FILL = -1e30
PARTS = 4
LANES = 128
SPARE = 32
ROW_BLOCK = 64
QUARTER = WIDTH // PARTS
CHUNKS = 2
MIB = 1024 * 1024
F32 = jnp.float32
BF16 = jnp.bfloat16


def nn(a, b):
    return lax.dot_general(a, b, (((1,), (0,)), ((), ())), preferred_element_type=F32)


def nt(a, b):
    return lax.dot_general(a, b, (((1,), (1,)), ((), ())), preferred_element_type=F32)


def rope_tables(length):
    freq = ROPE_BASE ** (-np.arange(HALF, dtype=np.float32) * np.float32(2.0 / HEAD))
    angles = (np.arange(length, dtype=np.float32)[None, :] * freq.astype(np.float32)[:, None]).astype(np.float32)
    return np.cos(angles).astype(np.float32), np.sin(angles).astype(np.float32)


def quarter(me, rel):
    return pl.ds(pl.multiple_of((me ^ rel) * QUARTER, QUARTER), QUARTER)


LO, HI = slice(0, QUARTER), slice(QUARTER, 2 * QUARTER)


def total_block(rel, rows_at, own, oth):
    return (own if rel in (0, 2) else oth)[rows_at, LO if rel in (0, 1) else HI].astype(F32)


def store_block(rel, value, rows_at, keep_ref, send_ref):
    to = pl.ds(pl.multiple_of((rel // 2) * QUARTER, QUARTER), QUARTER)

    @pl.when(rel % 2 == 0)
    def _():
        keep_ref[rows_at, to] = value[...]

    @pl.when(rel % 2 == 1)
    def _():
        send_ref[rows_at, to] = value[...].astype(BF16)


def chunk_of(ref, chunk, rows):
    return ref if ref.shape[0] == rows else ref.at[chunk * rows:(chunk + 1) * rows]


def row_block(i):
    return pl.ds(pl.multiple_of(i * ROW_BLOCK, ROW_BLOCK), ROW_BLOCK)


def is_valid(chunk, i, rows, length):
    return chunk * rows + i * ROW_BLOCK + lax.broadcasted_iota(jnp.int32, (ROW_BLOCK, 1), 0) < length


def copies_of(pairs, sems):
    made = [pltpu.make_async_copy(source, target, sems.at[i]) for i, (source, target) in enumerate(pairs)]
    for copy in made:
        copy.start()
    return made


def put_block(rel, value, keep_ref, send_ref):
    ref = keep_ref if rel in (0, 2) else send_ref
    ref[:, LO if rel in (0, 1) else HI] = value.astype(ref.dtype)


def rotate(value, cos, sin, out_ref):
    for i in range(value.shape[0] // HEAD):
        u1, u2 = value[i * HEAD:i * HEAD + HALF], value[i * HEAD + HALF:(i + 1) * HEAD]
        out_ref[i * HEAD:i * HEAD + HALF, :] = (u1 * cos - u2 * sin).astype(BF16)
        out_ref[i * HEAD + HALF:(i + 1) * HEAD, :] = (u2 * cos + u1 * sin).astype(BF16)


def turn_back(value, cos, sin, out_ref):
    for i in range(value.shape[0] // HEAD):
        w1, w2 = value[i * HEAD:i * HEAD + HALF], value[i * HEAD + HALF:(i + 1) * HEAD]
        out_ref[i * HEAD:i * HEAD + HALF, :] = (w1 * cos + w2 * sin).astype(BF16)
        out_ref[i * HEAD + HALF:(i + 1) * HEAD, :] = (w2 * cos - w1 * sin).astype(BF16)


def head_rows(i):
    return pl.ds(pl.multiple_of(i * HEAD, HEAD), HEAD)


def visible(key_start, query_start, rows, length):
    kpos = key_start + lax.broadcasted_iota(jnp.int32, (rows, rows), 0)
    qpos = query_start + lax.broadcasted_iota(jnp.int32, (rows, rows), 1)
    return (kpos <= qpos) & (kpos < length)


def project_kernel(chunk, info, wq_h, wkv_h, x0, x1, x2, x3, gains, a1, qb, kvb, cos_t, sin_t,
                   t1t_out, qt_out, kn_out, vn_out, kt_out, vt_out, h_out, wq, wkv, sems):
    copies = copies_of(((wkv_h, wkv), (wq_h, wq)), sems)
    me = info[0]
    rows = h_out.shape[0]
    kv_heads = kn_out.shape[0]
    xs = [chunk_of(x, chunk, rows) for x in (x0, x1, x2, x3)]

    def norm(i, carry):
        at = row_block(i)
        square = jnp.zeros((ROW_BLOCK, 1), F32)
        for r in range(PARTS):
            v = xs[r][at, :].astype(F32)
            square = square + jnp.sum(v * v, axis=1, keepdims=True)
        inv = lax.rsqrt(square / WIDTH + EPS)
        for r in range(PARTS):
            v = xs[r][at, :].astype(F32)
            h_out[at, quarter(me, r)] = (v * inv * gains[r, 0:1, :].astype(F32)).astype(BF16)
        return carry

    lax.fori_loop(0, rows // ROW_BLOCK, norm, 0)
    h = h_out[...]
    t1 = nt(h, a1[...])
    t1t_out[...] = t1.T.astype(BF16)
    t1b = t1.astype(BF16)
    cos, sin = cos_t[...], sin_t[...]
    copies[0].wait()
    k = nn(h, wkv[0]) + nn(t1b[:, RANK:2 * RANK], kvb[0])
    rotate(k.T, cos, sin, kt_out)
    k_n = kt_out[...].T
    v_n = (nn(h, wkv[1]) + nn(t1b[:, 2 * RANK:], kvb[1])).astype(BF16)
    vt_out[...] = v_n.T
    for i in range(kv_heads):
        kn_out[i] = k_n[:, i * HEAD:(i + 1) * HEAD]
        vn_out[i] = v_n[:, i * HEAD:(i + 1) * HEAD]
    copies[1].wait()
    q = nn(h, wq[...]) + nn(t1b[:, :RANK], qb[...])
    rotate(q.T * (HEAD ** -0.5), cos, sin, qt_out)


def attend_kernel(chunk, info, wo_h, qt, oa, ob, *rest):
    pairs, rest = rest[:2 * (chunk + 1)], rest[2 * (chunk + 1):]
    z_keep, z_send, ot_out, lse_out, tot_out, wo, sems = rest
    copies = copies_of(((wo_h, wo),), sems)
    keys, values = pairs[0::2], pairs[1::2]
    me, length = info[0], info[1]
    rows = qt.shape[1]
    kv_heads = keys[0].shape[0]
    heads = qt.shape[0] // HEAD
    group = heads // kv_heads

    kept = [jnp.concatenate([visible(c * rows, chunk * rows, rows, length)] * group, axis=1) for c in range(chunk + 1)]

    def one_group(j, carry):
        q_g = jnp.concatenate([qt[head_rows(j * group + g), :] for g in range(group)], axis=1)
        parts = [jnp.where(kept[c], nn(keys[c][j], q_g), NEG_FILL) for c in range(chunk + 1)]
        top = functools.reduce(jnp.maximum, [jnp.max(s, axis=0, keepdims=True) for s in parts])
        es = [jnp.exp(s - top) for s in parts]
        total = sum(jnp.sum(e, axis=0, keepdims=True) for e in es)
        low = top + jnp.log(total)
        o_t = sum(nn(value[head_rows(j), :], e.astype(BF16)) for value, e in zip(values, es))
        o_t = (o_t / total).astype(BF16)
        for g in range(group):
            cols = slice(g * rows, (g + 1) * rows)
            lse_out[pl.ds(j * group + g, 1), :] = low[:, cols]
            ot_out[head_rows(j * group + g), :] = o_t[:, cols]
        return carry

    lax.fori_loop(0, kv_heads, one_group, 0)
    o = ot_out[...].T
    to = nt(o, oa[...])
    tot_out[...] = to.T.astype(BF16)
    to = to.astype(BF16)
    copies[0].wait()
    for r in range(PARTS):
        at = quarter(me, r)
        put_block(r, nn(o, wo[:, at]) + nn(to, ob[:, at]), z_keep, z_send)


def front_kernel(chunk, last, info, wgu_in, wd_in, x0, x1, x2, x3, zo, zp, g0, g1, g2, g3, gains, a2, bd, fb, da,
                 *rest):
    units = wd_in.shape[0]
    if chunk:
        wgu, wd = wgu_in, wd_in
    else:
        (wgu, wd, f_s, sems), rest = rest[-4:], rest[:-4]
        rest = (*rest, f_s)

    def copies(i):
        c = pl.ds(pl.multiple_of(i * QUARTER, QUARTER), QUARTER)
        return (pltpu.make_async_copy(wgu_in.at[:, :, c], wgu.at[:, :, c], sems.at[0, i]),
                pltpu.make_async_copy(wd_in.at[c, :], wd.at[c, :], sems.at[1, i]))

    if not chunk:
        for i in range(units // QUARTER):
            for copy in copies(i):
                copy.start()
    f_s = rest[-1]
    xm_out, xq_out, h_out, g_out, act_out, dg_out, du_out, t2_s, dtd_s, b_out = rest[-11:-1]
    me, length = info[0], info[1]
    rows = h_out.shape[0]
    xs, gs = ([chunk_of(v, chunk, rows) for v in vs] for vs in ((x0, x1, x2, x3), (g0, g1, g2, g3)))

    def norm(i, carry):
        at = row_block(i)
        valid = is_valid(chunk, i, rows, length)
        square = jnp.zeros((ROW_BLOCK, 1), F32)
        for r in range(PARTS):
            v = xs[r][at, :].astype(F32) + total_block(r, at, zo, zp)
            if r == 0:
                xq_out[at, :] = v
            f_s[:, quarter(me, r)] = v
            square = square + jnp.sum(v * v, axis=1, keepdims=True)
            g_out[at, quarter(me, r)] = jnp.where(valid, gs[r][at, :], jnp.zeros((), BF16))
        inv = lax.rsqrt(square / WIDTH + EPS)
        for r in range(PARTS):
            v = f_s[:, quarter(me, r)]
            xm_out[at, quarter(me, r)] = v.astype(BF16)
            h_out[at, quarter(me, r)] = (v * inv * gains[r, 1:2, :].astype(F32)).astype(BF16)
        return carry

    lax.fori_loop(0, rows // ROW_BLOCK, norm, 0)
    t2 = nt(h_out[...], a2[...])
    t2_s[...] = t2.astype(BF16)
    dtd = nt(g_out[...], bd[...])
    dtd_s[...] = dtd.astype(BF16)
    t2t, dtdt = t2.T.astype(BF16), dtd.T.astype(BF16)

    def block(i, carry):
        c = pl.ds(pl.multiple_of(i * QUARTER, QUARTER), QUARTER)
        if not chunk:
            for copy in copies(i):
                copy.wait()
        h, g = h_out[...], g_out[...]
        gate = nn(h, wgu[0, :, c]) + nn(t2_s[:, :RANK], fb[0, :, c])
        up = nn(h, wgu[1, :, c]) + nn(t2_s[:, RANK:], fb[1, :, c])
        dact = nt(g, wd[c, :]) + nn(dtd_s[...], da[:, c])
        sig = 1.0 / (1.0 + jnp.exp(-gate))
        silu = gate * sig
        act = (silu * up).astype(BF16)
        dgate = (dact * up * sig * (1.0 + gate * (1.0 - sig))).astype(BF16)
        dup = (dact * silu).astype(BF16)
        act_out[:, c], dg_out[:, c], du_out[:, c] = act, dgate, dup
        for k, value in enumerate((nn(t2t[:RANK], dgate), nn(t2t[RANK:], dup), nn(dtdt, act))):
            at = pl.ds(pl.multiple_of((3 * i + k) * RANK, RANK), RANK)
            if last:
                value = value + rest[0][at, :]
            b_out[at, :] = value.astype(b_out.dtype)
        return carry

    lax.fori_loop(0, units // QUARTER, block, 0)


def back_kernel(last, info, wgu, h, g, act, dg, du, a2, fb, da, *rest):
    (value_s, low_s), rest = rest[-2:], rest[:-2]
    outs, rest = (rest[-3:], rest[:-3]) if last else (rest[-4:], rest[:-4])
    td_out, d_keep, d_send = outs[:3]
    me = info[0]
    rows = h.shape[0]
    dt2 = jnp.concatenate([nt(dg[...], fb[0]), nt(du[...], fb[1])], axis=1)
    td = nt(act[...], da[...])
    td_out[...] = td
    dt2b = dt2.astype(BF16)
    dt2t, tdt = dt2.T.astype(BF16), td.T.astype(BF16)

    def block(r, carry):
        at = quarter(me, r)
        value_s[...] = nt(dg[...], wgu[0, at, :]) + nt(du[...], wgu[1, at, :]) + nn(dt2b, a2[:, at])
        store_block(r, value_s, slice(0, rows), d_keep, d_send)
        low_s[:2 * RANK, :] = nn(dt2t, h[:, at])
        low_s[2 * RANK:, :] = nn(tdt, g[:, at])
        if last:
            low_s[...] += rest[0][:, at]
            store_block(r, low_s, slice(rows, rows + 3 * RANK), d_keep, d_send)
        else:
            outs[3][:, at] = low_s[...]
        return carry

    lax.fori_loop(0, PARTS, block, 0)


def down_kernel(info, wd, act, td, bd, xq, y_keep, y_send, value_s):
    me = info[0]
    tdb = td[...].astype(BF16)

    def block(r, carry):
        at = quarter(me, r)
        value_s[...] = nn(act[...], wd[:, at]) + nn(tdb, bd[:, at])
        store_block(r, value_s, slice(0, act.shape[0]), y_keep, y_send)
        return carry

    lax.fori_loop(0, PARTS, block, 0)
    y_keep[:, LO] += xq[...]


def attend_back_kernel(chunk, last, info, wq_h, wkv_h, wo_h, x0, x1, x2, x3, g0, g1, g2, g3, xm, do_, dp, gains, a1,
                       qb, kvb, oa, ob, cos_t, sin_t, t1t, qt, ot, lse, tot, *rest):
    scratch, rest = rest[-14:], rest[:-14]
    h_in, z_s, f_s, dot_s, dqt_s, dkt_s, dvt_s, dq_s, value_s, low_s, wq, wkv, wo, sems = scratch
    copies = copies_of(((wo_h, wo), (wq_h, wq), (wkv_h, wkv)), sems)
    n_out = 7 if last else 9
    outs, rest = rest[-n_out:], rest[:-n_out]
    dxq_out, h_keep, h_send, inv_out, b_out = outs[:5]
    triples, rest = rest[:3 * (chunk + 1)], rest[3 * (chunk + 1):]
    keys, values, keys_t = triples[0::3], triples[1::3], triples[2::3]
    me, length = info[0], info[1]
    rows = xm.shape[0]
    kv_heads = keys[0].shape[0]
    heads = qt.shape[0] // HEAD
    group = heads // kv_heads
    q_cols, kv_cols = heads * HEAD, kv_heads * HEAD
    xs, gs = ([chunk_of(v, chunk, rows) for v in vs] for vs in ((x0, x1, x2, x3), (g0, g1, g2, g3)))

    def norm_back(i, carry):
        at = row_block(i)
        valid = is_valid(chunk, i, rows, length)
        square, first, inner = (jnp.zeros((ROW_BLOCK, 1), F32) for _ in range(3))
        for r in range(PARTS):
            v = xm[at, quarter(me, r)].astype(F32)
            square = square + jnp.sum(v * v, axis=1, keepdims=True)
            w = total_block(r, at, do_, dp) * gains[r, 1:2, :].astype(F32)
            f_s[:, quarter(me, r)] = w
            inner = inner + jnp.sum(v * w, axis=1, keepdims=True)
            u = xs[r][at, :].astype(F32)
            first = first + jnp.sum(u * u, axis=1, keepdims=True)
        inv_one = lax.rsqrt(first / WIDTH + EPS)
        inv_out[at, :] = inv_one
        inv = lax.rsqrt(square / WIDTH + EPS)
        back = inv * inv * inv * inner / WIDTH
        for r in range(PARTS):
            v = xm[at, quarter(me, r)].astype(F32)
            g = jnp.where(valid, gs[r][at, :].astype(F32), 0.0)
            d = g + inv * f_s[:, quarter(me, r)] - v * back
            if r == 0:
                dxq_out[at, :] = d
            z_s[at, quarter(me, r)] = d.astype(BF16)
            u = xs[r][at, :].astype(F32)
            h_in[at, quarter(me, r)] = (u * inv_one * gains[r, 0:1, :].astype(F32)).astype(BF16)
        return carry

    lax.fori_loop(0, rows // ROW_BLOCK, norm_back, 0)
    dz = z_s[...]
    dto = nt(dz, ob[...])
    copies[0].wait()
    d_o = nt(dz, wo[...]) + nn(dto.astype(BF16), oa[...])
    dot_s[...] = d_o.T.astype(BF16)
    kept = [jnp.concatenate([visible(c * rows, chunk * rows, rows, length)] * group, axis=1) for c in range(chunk + 1)]

    def one_group(j, carry):
        places = [head_rows(j * group + g) for g in range(group)]
        q_g = jnp.concatenate([qt[at, :] for at in places], axis=1)
        do_g = jnp.concatenate([dot_s[at, :] for at in places], axis=1)
        o_g = jnp.concatenate([ot[at, :] for at in places], axis=1)
        low = jnp.concatenate([lse[pl.ds(j * group + g, 1), :] for g in range(group)], axis=1)
        dots = jnp.sum(do_g.astype(F32) * o_g.astype(F32), axis=0, keepdims=True)
        dq_g = 0.0
        for c in range(chunk + 1):
            prob = jnp.where(kept[c], jnp.exp(nn(keys[c][j], q_g) - low), 0.0)
            ds = (prob * (nn(values[c][j], do_g) - dots)).astype(BF16)
            dq_g = dq_g + nn(keys_t[c][head_rows(j), :], ds)
            dk, dv = nt(q_g, ds), nt(do_g, prob.astype(BF16))
            if last:
                dk, dv = dk + rest[2][head_rows(j), :], dv + rest[3][head_rows(j), :]
            dkt_s[c, head_rows(j), :], dvt_s[c, head_rows(j), :] = dk, dv
        for g in range(group):
            dqt_s[places[g], :] = dq_g[:, g * rows:(g + 1) * rows]
        return carry

    lax.fori_loop(0, kv_heads, one_group, 0)
    if not last:
        outs[6][...], outs[7][...] = dkt_s[0], dvt_s[0]
    cos, sin = cos_t[...], sin_t[...]
    dto_t, o_t = dto.T.astype(BF16), ot[...]
    d_out_a = nt(dto_t, o_t)
    turn_back(dqt_s[...], cos * (HEAD ** -0.5), sin * (HEAD ** -0.5), dot_s)
    dq_s[:, :q_cols] = dot_s[...].T
    turn_back(dkt_s[chunk], cos, sin, dot_s)
    dq_s[:, q_cols:q_cols + kv_cols] = dot_s[:kv_cols, :].T
    dq_s[:, q_cols + kv_cols:] = dvt_s[chunk].T.astype(BF16)
    dq, dk, dv = dq_s[:, :q_cols], dq_s[:, q_cols:q_cols + kv_cols], dq_s[:, q_cols + kv_cols:]
    dt1 = jnp.concatenate([nt(dq, qb[...]), nt(dk, kvb[0]), nt(dv, kvb[1])], axis=1)
    dt1b = dt1.astype(BF16)
    kv_pad = jnp.zeros((RANK, QUARTER - 2 * kv_cols), F32)
    d_kv = jnp.concatenate([nn(t1t[RANK:2 * RANK, :], dk), nn(t1t[2 * RANK:, :], dv), kv_pad], axis=1)
    for k, value in enumerate((nn(t1t[:RANK, :], dq), d_out_a, d_kv)):
        at = slice(k * RANK, (k + 1) * RANK)
        if last:
            value = value + rest[0][at, :]
        b_out[at, :] = value.astype(b_out.dtype)
    dt1t = dt1.T.astype(BF16)
    copies[1].wait()
    copies[2].wait()

    def block(r, inner):
        at = quarter(me, r)
        d = nt(dq_s[:, :q_cols], wq[at, :]) + nn(dt1b, a1[:, at])
        d = d + nt(dq_s[:, q_cols:q_cols + kv_cols], wkv[0, at, :]) + nt(dq_s[:, q_cols + kv_cols:], wkv[1, at, :])
        value_s[...] = d
        store_block(r, value_s, slice(0, rows), h_keep, h_send)
        low_s[:3 * RANK, :] = nn(dt1t, h_in[:, at])
        low_s[3 * RANK:, :] = nn(tot[...], z_s[:, at])
        if last:
            low_s[...] += rest[1][:, at]
            store_block(r, low_s, slice(0, 4 * RANK), outs[5], outs[6])
        else:
            outs[5][:, at] = low_s[...]
        return inner + jnp.sum(d * h_in[:, at].astype(F32), axis=1, keepdims=True)

    inner = lax.fori_loop(0, PARTS, block, jnp.zeros((rows, 1), F32))
    inner = jnp.broadcast_to(inner, (rows, LANES)).T[:SPARE // 2, :]
    if last:
        for ref in outs[5:7]:
            for c, value in enumerate((inner, rest[4][...])):
                at = slice(4 * RANK + c * SPARE // 2, 4 * RANK + (c + 1) * SPARE // 2)
                ref[at, QUARTER:QUARTER + rows] = value.astype(ref.dtype)
                ref[at, QUARTER + rows:] = jnp.zeros((SPARE // 2, QUARTER - rows), ref.dtype)
                ref[at, :QUARTER] = jnp.zeros((SPARE // 2, QUARTER), ref.dtype)
    else:
        outs[8][...] = inner


def output_kernel(info, y_far, *refs):
    out = refs[-1]
    rows = out.shape[0] // CHUNKS
    for c in range(CHUNKS):
        y_keep, y_got = refs[2 * c:2 * (c + 1)]
        at = slice(c * rows, (c + 1) * rows)
        valid = c * rows + lax.broadcasted_iota(jnp.int32, (rows, 1), 0) < info[1]
        y = y_keep[:, LO] + y_got[:, LO].astype(F32) + y_far[at, :].astype(F32)
        out[at, :] = jnp.where(valid, y, 0.0).astype(BF16)


def finish_kernel(gains, x_all, aa_high, aa_far, *refs):
    out = refs[-1]
    gain = gains[0, 0:1, :].astype(F32)
    rows = out.shape[0] // CHUNKS
    inner = aa_high[4 * RANK:, :].astype(F32) + aa_far[4 * RANK:, :].astype(F32)
    for c in range(CHUNKS):
        dx, keep, got, there, inv = refs[5 * c:5 * (c + 1)]
        x = chunk_of(x_all, c, rows)
        mine = inner[c * SPARE // 2:c * SPARE // 2 + 8, :rows].T[:, 0:1]
        inv = inv[...]
        grad = keep[:, LO] + got[:, LO].astype(F32) + there[...].astype(F32)
        grad = inv * (gain * grad) - x[...].astype(F32) * (inv * inv * mine / WIDTH)
        out[c * rows:(c + 1) * rows, :] = (dx[...] + grad).astype(BF16)


def high_sum_kernel(*refs):
    out = refs[-1]
    rows = out.shape[0] // (len(refs) // 2)
    for c in range(len(refs) // 2):
        keep, got = refs[2 * c:2 * c + 2]
        out[c * rows:(c + 1) * rows, :] = (keep[:, HI] + got[:, HI].astype(F32)).astype(BF16)


def high_sum(*pairs):
    args = [v for pair in pairs for v in pair]
    rows = sum(keep.shape[0] for keep, _ in pairs)
    return call(high_sum_kernel, None, (), args, [((rows, QUARTER), BF16)], [], "high_sum", 8)[0]


def split_refs(refs, counts):
    groups = []
    for count in counts:
        groups.append(refs[:count])
        refs = refs[count:]
    return groups, refs


def with_entry(parts, at, use):
    start = 0
    for ref in parts:
        @pl.when((at >= start) & (at < start + ref.shape[0]))
        def _(ref=ref, start=start):
            use(ref, at - start)
        start += ref.shape[0]


def sum_slots(info, owners, out_refs, one_slot):
    count = out_refs[0].shape[0]
    base = pl.program_id(0) * count
    slots = owners.shape[0]
    for ref in out_refs:
        ref[...] = jnp.zeros_like(ref)

    def add(slot, carry):
        owner = owners[slot] - base

        @pl.when((owner >= 0) & (owner < count))
        def _():
            one_slot(owner, entry_of(slot, info[3], slots))
        return carry

    lax.fori_loop(0, slots, add, 0)


def feedforward_sum_kernel(counts, info, owners, *refs):
    (b_parts, *a_parts), outs = split_refs(refs, counts)
    ga, gdb, gb, gda = outs
    me = info[0]

    def one_slot(owner, at):
        def add_b(ref, e):
            for i in range(gda.shape[2] // QUARTER):
                cols = slice(i * QUARTER, (i + 1) * QUARTER)
                base = i * 3 * RANK
                gb[owner, 0, :, cols] += ref[e, base:base + RANK, :].astype(F32)
                gb[owner, 1, :, cols] += ref[e, base + RANK:base + 2 * RANK, :].astype(F32)
                gda[owner, :, cols] += ref[e, base + 2 * RANK:base + 3 * RANK, :].astype(F32)

        with_entry(b_parts, at, add_b)
        for near_bit, parts in enumerate(a_parts):
            def add_a(ref, e, near_bit=near_bit):
                for r, cols in ((near_bit, LO), (near_bit ^ 2, HI)):
                    ga[owner, :, quarter(me, r)] += ref[e, :2 * RANK, cols].astype(F32)
                    gdb[owner, :, quarter(me, r)] += ref[e, 2 * RANK:, cols].astype(F32)

            with_entry(parts, at, add_a)

    sum_slots(info, owners, outs, one_slot)


def attention_sum_kernel(counts, info, owners, *refs):
    (b_parts, *a_parts), outs = split_refs(refs, counts)
    ga, gob, gq, gkv, goa = outs
    me = info[0]
    kv_cols = gkv.shape[3]

    def one_slot(owner, at):
        def add_b(ref, e):
            gq[owner] += ref[e, :RANK, :].astype(F32)
            goa[owner] += ref[e, RANK:2 * RANK, :].astype(F32)
            gkv[owner, 0] += ref[e, 2 * RANK:3 * RANK, :kv_cols].astype(F32)
            gkv[owner, 1] += ref[e, 2 * RANK:3 * RANK, kv_cols:2 * kv_cols].astype(F32)

        with_entry(b_parts, at, add_b)
        for r, parts in enumerate(a_parts):
            def add_a(ref, e, r=r):
                ga[owner, :, quarter(me, r)] += ref[e, :3 * RANK, :].astype(F32)
                gob[owner, :, quarter(me, r)] += ref[e, 3 * RANK:, :].astype(F32)

            with_entry(parts, at, add_a)

    sum_slots(info, owners, outs, one_slot)


def deal_kernel(slots, source, out, sems):
    made = [pltpu.make_async_copy(source.at[i], out.at[slots[i]], sems.at[i]) for i in range(source.shape[0])]
    for copy in made:
        copy.start()
    for copy in made:
        copy.wait()


def collect_kernel(slots, source, out, sems):
    made = [pltpu.make_async_copy(source.at[slots[i]], out.at[i], sems.at[i]) for i in range(source.shape[0])]
    for copy in made:
        copy.start()
    for copy in made:
        copy.wait()


def adapter_kernel(count, info, *refs):
    made = [pltpu.make_async_copy(refs[i].at[info[2]], refs[count + i], refs[-1].at[i]) for i in range(count)]
    for copy in made:
        copy.start()
    for copy in made:
        copy.wait()


def load_adapters(arrays, info):
    count = len(arrays)
    return pl.pallas_call(
        functools.partial(adapter_kernel, count),
        in_specs=[pl.BlockSpec(memory_space=pltpu.SMEM)] + [pl.BlockSpec(memory_space=pltpu.HBM)] * count,
        out_specs=[pl.BlockSpec(memory_space=pltpu.VMEM)] * count,
        out_shape=[pltpu.VMEM(a.shape[1:], a.dtype) for a in arrays],
        scratch_shapes=[pltpu.SemaphoreType.DMA((count,))],
        compiler_params=pltpu.CompilerParams(vmem_limit_bytes=MIB),
        cost_estimate=pl.CostEstimate(flops=1000, transcendentals=0, bytes_accessed=1000),
        name="adapters",
    )(info, *(in_hbm(a) for a in arrays))


def move_rows(kernel, value, slots, name, outs, in_space, out_space, sems):
    return pl.pallas_call(
        kernel,
        in_specs=[pl.BlockSpec(memory_space=pltpu.SMEM), pl.BlockSpec(memory_space=in_space)],
        out_specs=[pl.BlockSpec(memory_space=out_space)] * len(outs),
        out_shape=outs,
        scratch_shapes=[pltpu.SemaphoreType.DMA(sems)],
        compiler_params=pltpu.CompilerParams(vmem_limit_bytes=MIB),
        cost_estimate=pl.CostEstimate(flops=1000, transcendentals=0, bytes_accessed=1000),
        name=name,
    )(slots, pltpu.with_memory_space_constraint(value, in_space))


def sds(shape, dtype):
    return jax.ShapeDtypeStruct(tuple(shape), dtype)


def in_vmem(value):
    return pltpu.with_memory_space_constraint(value, pltpu.VMEM)


def in_hbm(value):
    return pltpu.with_memory_space_constraint(value, pltpu.HBM)


def call(kernel, info, weights, args, outs, scratch, name, mib, after=(), sems=()):
    vmem = pl.BlockSpec(memory_space=pltpu.VMEM)
    scalars = () if info is None else (info,)
    n, w = len(scalars), len(weights)

    def body(*refs):
        at = n + w + len(args)
        kernel(*refs[:at], *refs[at + len(after):])

    return pl.pallas_call(
        body,
        in_specs=[pl.BlockSpec(memory_space=pltpu.SMEM)] * n + [pl.BlockSpec(memory_space=pltpu.HBM)] * w + [vmem] * len(args)
        + [pl.BlockSpec(memory_space=pl.ANY)] * len(after),
        out_specs=[vmem] * len(outs),
        out_shape=[pltpu.VMEM(tuple(s), d) for s, d in outs],
        scratch_shapes=[pltpu.VMEM(s, d) for s, d in scratch] + ([pltpu.SemaphoreType.DMA(sems)] if sems else []),
        compiler_params=pltpu.CompilerParams(vmem_limit_bytes=mib * MIB),
        cost_estimate=pl.CostEstimate(flops=1000, transcendentals=0, bytes_accessed=1000),
        name=name,
    )(*scalars, *(in_hbm(a) for a in weights), *(in_vmem(a) for a in args), *after)


def whole_spec(value):
    zeros = (0,) * value.ndim
    return pl.BlockSpec(value.shape, lambda i, *_: zeros)


def sum_call(kernel, scalars, groups, outs, name):
    args = [v for group in groups for v in group]
    steps = 2
    specs = [pl.BlockSpec((o.shape[0] // steps,) + o.shape[1:], (lambda n: lambda i, *_: (i,) + (0,) * n)(o.ndim - 1))
             for o in outs]
    return pl.pallas_call(
        functools.partial(kernel, [len(group) for group in groups]),
        grid_spec=pltpu.PrefetchScalarGridSpec(
            num_scalar_prefetch=len(scalars), grid=(steps,),
            in_specs=[whole_spec(a) for a in args], out_specs=specs),
        out_shape=outs,
        compiler_params=pltpu.CompilerParams(
            dimension_semantics=("arbitrary",),
            vmem_limit_bytes=4 * MIB + 2 * sum(a.size * a.dtype.itemsize for a in args)
            + sum(o.size * o.dtype.itemsize for o in outs)),
        cost_estimate=pl.CostEstimate(flops=0, transcendentals=0, bytes_accessed=12000000),
        name=name,
    )(*scalars, *args)


def swap(value, bit, axis, size):
    return lax.ppermute(value, axis, [(i, i ^ bit) for i in range(size)])


def near(value):
    return swap(value, 1, "mp", PARTS)


def far(value):
    return swap(value, 2, "mp", PARTS)


def spread(value):
    there = far(value)
    return (value, near(value), there, near(there))


def far_sum_kernel(own, got, out):
    for to, other in ((LO, HI), (HI, LO)):
        out[:, to] = (own[:, to].astype(F32) + got[:, other].astype(F32)).astype(BF16)


def far_sum(own, got):
    return call(far_sum_kernel, None, (), (own, got), [(own.shape, BF16)], [], "far_sum", 6)[0]


def pair_sum_kernel(keep, got, out):
    out[...] = (keep[...] + got[...].astype(F32)).astype(BF16)


def pair_sum(keep, send, *before):
    got = near(send)
    got = late(got, *before) if before else got
    return call(pair_sum_kernel, None, (), (keep, got), [(send.shape, BF16)], [], "pair_sum", 6)[0]


def late(value, *others):
    return lax.optimization_barrier((value, *others))[0]


def doubled(stack, bit, size):
    return jnp.concatenate([stack, swap(stack, bit, "dp", size)], axis=0)


def entry_of(slot, place, size):
    bits = size.bit_length() - 1
    apart = slot ^ place
    return sum(((apart >> b) & 1) << (bits - 1 - b) for b in range(bits))


def shards(dp, residual, attention_gain, query_matrix, key_value_matrix, output_matrix, feedfwd_gain,
           gate_up_matrix, down_matrix, attention_adapter_input, query_adapter_output,
           key_value_adapter_output, output_adapter_input, output_adapter_output, feedfwd_adapter_input,
           feedfwd_adapter_output, down_adapter_input, down_adapter_output, lengths, adapter_index,
           dealing_slots, cotangent):
    seqs = residual.shape[0]
    length = cotangent.shape[1]
    units = down_matrix.shape[0]
    adapters = attention_adapter_input.shape[0]
    q_cols = query_matrix.shape[1]
    kv_cols = key_value_matrix.shape[2]
    kv_heads = kv_cols // HEAD
    heads = q_cols // HEAD
    rows = length // CHUNKS
    half = 2 * QUARTER
    me = lax.axis_index("mp")
    place = lax.axis_index("dp")

    is_there = dealing_slots[None, :] == jnp.arange(seqs, dtype=jnp.int32)[:, None]
    owners = jnp.sum(jnp.where(is_there, adapter_index[None, :], 0), axis=1)
    spans = jnp.sum(jnp.where(is_there, lengths[None, :], 0), axis=1)
    mine = jnp.arange(seqs, dtype=jnp.int32) == place
    my_length = jnp.sum(jnp.where(mine, spans, 0))
    my_adapter = jnp.sum(jnp.where(mine, owners, 0))
    info = jnp.stack([me.astype(jnp.int32), my_length, my_adapter, place.astype(jnp.int32)])

    gs = spread(cotangent[0])
    gains = jnp.stack(spread(jnp.stack([attention_gain, feedfwd_gain])))
    ordered, = move_rows(deal_kernel, residual, dealing_slots, "deal", [pltpu.VMEM(residual.shape, BF16)], pltpu.HBM,
                         pltpu.VMEM, (seqs,))
    dealt = lax.all_to_all(ordered, "dp", split_axis=0, concat_axis=1, tiled=True)[0]
    adapters_here = load_adapters(
        (attention_adapter_input, query_adapter_output, key_value_adapter_output, output_adapter_input,
         output_adapter_output, feedfwd_adapter_input, feedfwd_adapter_output, down_adapter_input,
         down_adapter_output), info)
    a1, qb, kvb, oa, ob, a2, fba, da, bd = adapters_here
    dealt = late(dealt, a1, gains)
    beside = near(dealt)
    there = [far(dealt[c * rows:(c + 1) * rows]) for c in range(CHUNKS)]
    xs = [None] * CHUNKS
    cos_np, sin_np = rope_tables(length)
    cos = [jnp.asarray(cos_np[:, c * rows:(c + 1) * rows]) for c in range(CHUNKS)]
    sin = [jnp.asarray(sin_np[:, c * rows:(c + 1) * rows]) for c in range(CHUNKS)]
    wq, wkv, wo = query_matrix, key_value_matrix, output_matrix

    def like(*arrays):
        return [(a.shape, a.dtype) for a in arrays]

    wide, col, block, thin = (rows, WIDTH), (rows, half), (rows, QUARTER), (rows, 1)
    saved, kept, z_own, z_far = ([None] * CHUNKS for _ in range(4))
    order = ()
    for c in range(CHUNKS):
        xs[c] = (dealt, beside, there[c], near(late(there[c], saved[0][0]) if c else late(there[c], gs[2])))
        outs = [((3 * RANK, rows), BF16), ((q_cols, rows), BF16), ((kv_heads, rows, HEAD), BF16),
                ((kv_heads, rows, HEAD), BF16), ((kv_cols, rows), BF16), ((kv_cols, rows), BF16)]
        saved[c] = call(
            functools.partial(project_kernel, c), info, (wq, wkv), (*xs[c], gains, a1, qb, kvb, cos[c], sin[c]), outs,
            [(wide, BF16)] + like(wq, wkv), "project_%d" % c, 12, order, (2,))
        outs = [(col, F32), (col, BF16), ((q_cols, rows), BF16), ((heads, rows), F32), ((RANK, rows), BF16)]
        pairs = [v for p in saved[:c + 1] for v in (p[2], p[5])]
        z_keep, z_send, *kept[c] = call(
            functools.partial(attend_kernel, c), info, (wo,), (saved[c][1], oa, ob, *pairs), outs, like(wo),
            "attend_%d" % c, 10, (saved[c][0], gs[1], gs[3]) if c else (saved[c][0],), (1,))
        z_own[c] = pair_sum(z_keep, late(z_send, z_far[0] if c else there[-1]))
        z_far[c] = far(z_own[c])
        order = (kept[c][1], z_own[c])
    def front(c, total, partial, order):
        hidden = (rows, units)
        outs = [(wide, BF16), (block, F32), (wide, BF16), (wide, BF16), (hidden, BF16), (hidden, BF16), (hidden, BF16),
                ((rows, 2 * RANK), BF16), ((rows, RANK), BF16),
                ((3 * RANK * units // QUARTER, QUARTER), BF16 if c else F32)]
        args = (*xs[c], total, near(total), *gs, gains, a2, bd, fba, da, *partial)
        weights = () if c else (gate_up_matrix, down_matrix)
        outs += like(*weights)
        return call(
            functools.partial(front_kernel, c, c == CHUNKS - 1), info, weights, (wgu, wd, *args) if c else args, outs,
            [((ROW_BLOCK, WIDTH), F32)], "front_%d" % c, 8, order, () if c else (2, units // QUARTER))

    def back(c, hidden, partial, order):
        first = col if c else (rows + 3 * RANK, half)
        outs = [((rows, RANK), F32), (first, F32), (first, BF16)]
        outs += [((3 * RANK, WIDTH), F32)] if c else []
        return call(
            functools.partial(back_kernel, c == 0), info, (), (wgu, *hidden[2:7], a2, fba, da, *partial), outs,
            [(block, F32), ((3 * RANK, QUARTER), F32)], "back_%d" % c, 8, order)

    def down(c, td, order):
        return call(down_kernel, info, (), (wd, hidden[c][4], td, bd, hidden[c][1]), [(col, F32), (col, BF16)],
                    [(block, F32)], "down_%d" % c, 6, order)

    def attend_back(c, total, partial, order):
        outs = [(block, F32), (col, F32), (col, BF16), (thin, F32), ((3 * RANK, QUARTER), F32 if c else BF16)]
        low = (4 * RANK + SPARE, half)
        outs += ([((4 * RANK, WIDTH), F32), ((kv_cols, rows), F32), ((kv_cols, rows), F32), ((SPARE // 2, rows), F32)]
                 if c else [(low, F32), (low, BF16)])
        scratch = [(wide, BF16), (wide, BF16), ((ROW_BLOCK, WIDTH), F32), ((q_cols, rows), BF16), ((q_cols, rows), F32),
                   ((c + 1, kv_cols, rows), F32), ((c + 1, kv_cols, rows), F32), ((rows, q_cols + 2 * kv_cols), BF16),
                   (block, F32), ((4 * RANK, QUARTER), F32)]
        triples = [v for p in saved[:c + 1] for v in (p[2], p[3], p[4])]
        return call(
            functools.partial(attend_back_kernel, c, c == 0), info, (wq, wkv, wo),
            (*xs[c], *gs, hidden[c][0], total, near(total), gains, a1, qb, kvb, oa, ob, cos[c], sin[c], *saved[c][:2],
             *kept[c], *triples, *partial), outs, scratch + like(wq, wkv, wo), "attend_back_%d" % c, 18, order, (3,))

    bits = [1 << b for b in reversed(range(dp.bit_length() - 1))]
    def to_bands(value):
        return lax.all_to_all(value.reshape(dp, length // dp, QUARTER), "dp", split_axis=0, concat_axis=0, tiled=True)

    def collect(value, name, *before):
        rows_out = sds((seqs, length // dp, QUARTER), BF16)
        return move_rows(collect_kernel, value, late(dealing_slots, *before), name, [rows_out], pltpu.VMEM, pl.ANY,
                         (seqs,))[0]

    hidden, d_own, d_far, y_keep, y_got = ([None] * CHUNKS for _ in range(5))
    *hidden[0], wgu, wd = front(0, far_sum(z_own[0], z_far[0]), (), order)
    step = hidden[0][8]
    hidden[1] = front(1, far_sum(z_own[1], late(z_far[1], step)), hidden[0][9:], (step,))
    fb = hidden[1][9][None]
    fb_first = swap(fb, bits[0], "dp", dp)
    td, d_keep, d_send, fa = back(1, hidden[1], (), (hidden[1][8],))
    d_own[1] = pair_sum(d_keep, late(d_send, fb_first))
    d_far[1] = far(d_own[1])
    fb = fb_more = jnp.concatenate([fb, fb_first], axis=0)
    for bit in bits[1:-1]:
        fb_more = doubled(fb_more, bit, dp)
    fb_more = fb_more[2:]
    fb_side = swap(fb, bits[-1], "dp", dp)
    td_0, d_keep, d_send = back(0, hidden[0], (fa,), (d_own[1],))
    y_keep[1], y_send = down(1, td, (td_0,))
    total = far_sum(d_own[1], late(d_far[1], y_send))
    d_own[0] = pair_sum(d_keep, late(d_send, fb_more, fb_side), total)
    d_far[0] = far(d_own[0])
    fb_more_side = swap(fb_more, bits[-1], "dp", dp)
    y_got[1] = near(late(y_send, d_own[0]))
    dxq, h_keep, h_send, inv, *sums = attend_back(1, total, (), (d_own[0], y_send))
    total = far_sum(d_own[0], late(d_far[0], inv))
    h_got = near(late(h_send, fb_more_side))
    h_high = high_sum((h_keep, h_got))
    h_far = far(h_high)
    final = [None, (dxq, h_keep, h_got, h_far, inv)]
    fa = total[rows:][None]
    fa_first = swap(fa, bits[0], "dp", dp)
    dxq, h_keep, h_send, inv, att_b, aa_keep, aa_send = attend_back(0, total, sums, (h_high,))
    ready = (fa_first, h_far)
    aa_got = near(late(aa_send, *ready))
    aa_high = high_sum((aa_keep, aa_got))
    aa_far = far(aa_high)
    h_got = near(late(h_send, *ready))
    h_high = high_sum((h_keep, h_got))
    h_far = far(h_high)
    final[0] = (dxq, h_keep, h_got, h_far, inv)
    att_a = aa_keep[:4 * RANK, :QUARTER] + aa_got[:4 * RANK, :QUARTER].astype(F32)
    att_a = (att_a + late(aa_far, h_high)[:4 * RANK].astype(F32)).astype(BF16)
    n_b = att_b.shape[0]
    att = jnp.concatenate([att_b, att_a], axis=0)[None]
    y_keep[0], y_send = down(0, td_0, (att,))
    y_got[0] = near(y_send)
    att = doubled(att, bits[0], dp)
    att = late(att, h_far, y_send)
    for bit in bits[1:-1]:
        att = doubled(att, bit, dp)
    fa = late(jnp.concatenate([fa, fa_first], axis=0), aa_high)
    for bit in bits[1:-1]:
        fa = doubled(fa, bit, dp)
    fa_side = swap(fa, bits[-1], "dp", dp)
    y_far = far(high_sum(*((k, late(g, h_far)) for k, g in zip(y_keep, y_got))))

    dinput, = call(finish_kernel, None, (), (gains, dealt, aa_high, aa_far, *(v for f in final for v in f)),
                   [((length, QUARTER), BF16)], [], "finish", 8, (att, fa_side))
    input_grad = collect(to_bands(dinput), "collect_grad")
    outs = [sds((adapters, 2 * RANK, WIDTH), F32), sds((adapters, RANK, WIDTH), F32),
            sds((adapters, 2, RANK, units), F32), sds((adapters, RANK, units), F32)]
    ga_ffn, g_down_b, g_ffn_b, g_down_a = sum_call(
        feedforward_sum_kernel, (info, owners),
        ((fb, fb_more, fb_side, fb_more_side), (fa, fa_side), (near(fa), near(fa_side))), outs, "feedforward_sum")

    result, = call(output_kernel, info, (), (late(y_far, dinput, g_down_a), *(v for p in zip(y_keep, y_got) for v in p)),
                   [((length, QUARTER), BF16)], [], "output", 8)
    output = collect(to_bands(result), "collect_out", input_grad)

    att_side = swap(att, bits[-1], "dp", dp)
    a_parts = [att[:, n_b:], att_side[:, n_b:]]
    a_far = [far(v) for v in a_parts]
    outs = [sds((adapters, 3 * RANK, WIDTH), F32), sds((adapters, RANK, WIDTH), F32),
            sds((adapters, RANK, q_cols), F32), sds((adapters, 2, RANK, kv_cols), F32),
            sds((adapters, RANK, q_cols), F32)]
    ga_att, g_out_b, g_query_b, g_kv_b, g_out_a = sum_call(
        attention_sum_kernel, (info, owners),
        ((att, att_side), a_parts, [near(v) for v in a_parts], a_far, [near(v) for v in a_far]), outs, "attention_sum")
    return (output, input_grad, ga_att, g_query_b, g_kv_b, g_out_a, g_out_b, ga_ffn, g_ffn_b, g_down_a, g_down_b)


def solution(mesh):
    in_specs = (
        P(None, "dp", "mp"), P("mp"), P(None, "mp"), P(None, None, "mp"), P("mp", None), P("mp"),
        P(None, None, "mp"), P("mp", None), P(), P(None, None, "mp"), P(None, None, None, "mp"),
        P(None, None, "mp"), P(), P(), P(None, None, None, "mp"), P(None, None, "mp"), P(), P(), P(), P(),
        P("dp", None, "mp"),
    )
    out_specs = (
        P(None, "dp", "mp"), P(None, "dp", "mp"), P(), P(None, None, "mp"), P(None, None, None, "mp"),
        P(None, None, "mp"), P(), P(), P(None, None, None, "mp"), P(None, None, "mp"), P(),
    )
    return jax.shard_map(
        functools.partial(shards, mesh.shape["dp"]), mesh=mesh, in_specs=in_specs, out_specs=out_specs,
        check_vma=False)
```

```python
import functools

import jax
import jax.numpy as jnp
import numpy as np
from jax import lax
from jax.experimental import pallas as pl
from jax.experimental.pallas import tpu as pltpu
from jax.sharding import PartitionSpec as P

WIDTH = 2048
HEAD = 64
HALF = HEAD // 2
RANK = 16
EPS = 1e-05
ROPE_BASE = 500000.0
NEG_FILL = -1e30
PARTS = 4
LANES = 128
SPARE = 32
ROW_BLOCK = 64
QUARTER = WIDTH // PARTS
CHUNKS = 2
MIB = 1024 * 1024
F32 = jnp.float32
BF16 = jnp.bfloat16


def nn(a, b):
    return lax.dot_general(a, b, (((1,), (0,)), ((), ())), preferred_element_type=F32)


def nt(a, b):
    return lax.dot_general(a, b, (((1,), (1,)), ((), ())), preferred_element_type=F32)


def rope_tables(length):
    freq = ROPE_BASE ** (-np.arange(HALF, dtype=np.float32) * np.float32(2.0 / HEAD))
    angles = (np.arange(length, dtype=np.float32)[None, :] * freq.astype(np.float32)[:, None]).astype(np.float32)
    return np.cos(angles).astype(np.float32), np.sin(angles).astype(np.float32)


def quarter(me, rel):
    return pl.ds(pl.multiple_of((me ^ rel) * QUARTER, QUARTER), QUARTER)


LO, HI = slice(0, QUARTER), slice(QUARTER, 2 * QUARTER)


def total_block(rel, rows_at, own, oth):
    return (own if rel in (0, 2) else oth)[rows_at, LO if rel in (0, 1) else HI].astype(F32)


def store_block(rel, value, rows_at, keep_ref, send_ref):
    to = pl.ds(pl.multiple_of((rel // 2) * QUARTER, QUARTER), QUARTER)

    @pl.when(rel % 2 == 0)
    def _():
        keep_ref[rows_at, to] = value[...]

    @pl.when(rel % 2 == 1)
    def _():
        send_ref[rows_at, to] = value[...].astype(BF16)


def chunk_of(ref, chunk, rows):
    return ref if ref.shape[0] == rows else ref.at[chunk * rows:(chunk + 1) * rows]


def row_block(i):
    return pl.ds(pl.multiple_of(i * ROW_BLOCK, ROW_BLOCK), ROW_BLOCK)


def is_valid(chunk, i, rows, length):
    return chunk * rows + i * ROW_BLOCK + lax.broadcasted_iota(jnp.int32, (ROW_BLOCK, 1), 0) < length


def copies_of(pairs, sems):
    made = [pltpu.make_async_copy(source, target, sems.at[i]) for i, (source, target) in enumerate(pairs)]
    for copy in made:
        copy.start()
    return made


def put_block(rel, value, keep_ref, send_ref):
    ref = keep_ref if rel in (0, 2) else send_ref
    ref[:, LO if rel in (0, 1) else HI] = value.astype(ref.dtype)


def rotate(value, cos, sin, out_ref):
    for i in range(value.shape[0] // HEAD):
        u1, u2 = value[i * HEAD:i * HEAD + HALF], value[i * HEAD + HALF:(i + 1) * HEAD]
        out_ref[i * HEAD:i * HEAD + HALF, :] = (u1 * cos - u2 * sin).astype(BF16)
        out_ref[i * HEAD + HALF:(i + 1) * HEAD, :] = (u2 * cos + u1 * sin).astype(BF16)


def turn_back(value, cos, sin, out_ref):
    for i in range(value.shape[0] // HEAD):
        w1, w2 = value[i * HEAD:i * HEAD + HALF], value[i * HEAD + HALF:(i + 1) * HEAD]
        out_ref[i * HEAD:i * HEAD + HALF, :] = (w1 * cos + w2 * sin).astype(BF16)
        out_ref[i * HEAD + HALF:(i + 1) * HEAD, :] = (w2 * cos - w1 * sin).astype(BF16)


def head_rows(i):
    return pl.ds(pl.multiple_of(i * HEAD, HEAD), HEAD)


def visible(key_start, query_start, rows, length):
    kpos = key_start + lax.broadcasted_iota(jnp.int32, (rows, rows), 0)
    qpos = query_start + lax.broadcasted_iota(jnp.int32, (rows, rows), 1)
    return (kpos <= qpos) & (kpos < length)


def project_kernel(chunk, info, wq_h, wkv_h, x0, x1, x2, x3, gains, a1, qb, kvb, cos_t, sin_t,
                   t1t_out, qt_out, kn_out, vn_out, kt_out, vt_out, h_out, wq, wkv, sems):
    copies = copies_of(((wkv_h, wkv), (wq_h, wq)), sems)
    me = info[0]
    rows = h_out.shape[0]
    kv_heads = kn_out.shape[0]
    xs = [chunk_of(x, chunk, rows) for x in (x0, x1, x2, x3)]

    def norm(i, carry):
        at = row_block(i)
        square = jnp.zeros((ROW_BLOCK, 1), F32)
        for r in range(PARTS):
            v = xs[r][at, :].astype(F32)
            square = square + jnp.sum(v * v, axis=1, keepdims=True)
        inv = lax.rsqrt(square / WIDTH + EPS)
        for r in range(PARTS):
            v = xs[r][at, :].astype(F32)
            h_out[at, quarter(me, r)] = (v * inv * gains[r, 0:1, :].astype(F32)).astype(BF16)
        return carry

    lax.fori_loop(0, rows // ROW_BLOCK, norm, 0)
    h = h_out[...]
    t1 = nt(h, a1[...])
    t1t_out[...] = t1.T.astype(BF16)
    t1b = t1.astype(BF16)
    cos, sin = cos_t[...], sin_t[...]
    copies[0].wait()
    k = nn(h, wkv[0]) + nn(t1b[:, RANK:2 * RANK], kvb[0])
    rotate(k.T, cos, sin, kt_out)
    k_n = kt_out[...].T
    v_n = (nn(h, wkv[1]) + nn(t1b[:, 2 * RANK:], kvb[1])).astype(BF16)
    vt_out[...] = v_n.T
    for i in range(kv_heads):
        kn_out[i] = k_n[:, i * HEAD:(i + 1) * HEAD]
        vn_out[i] = v_n[:, i * HEAD:(i + 1) * HEAD]
    copies[1].wait()
    q = nn(h, wq[...]) + nn(t1b[:, :RANK], qb[...])
    rotate(q.T * (HEAD ** -0.5), cos, sin, qt_out)


def attend_kernel(chunk, info, wo_h, qt, oa, ob, *rest):
    pairs, rest = rest[:2 * (chunk + 1)], rest[2 * (chunk + 1):]
    z_keep, z_send, ot_out, lse_out, tot_out, wo, sems = rest
    copies = copies_of(((wo_h, wo),), sems)
    keys, values = pairs[0::2], pairs[1::2]
    me, length = info[0], info[1]
    rows = qt.shape[1]
    kv_heads = keys[0].shape[0]
    heads = qt.shape[0] // HEAD
    group = heads // kv_heads

    kept = [jnp.concatenate([visible(c * rows, chunk * rows, rows, length)] * group, axis=1) for c in range(chunk + 1)]

    def one_group(j, carry):
        q_g = jnp.concatenate([qt[head_rows(j * group + g), :] for g in range(group)], axis=1)
        parts = [jnp.where(kept[c], nn(keys[c][j], q_g), NEG_FILL) for c in range(chunk + 1)]
        top = functools.reduce(jnp.maximum, [jnp.max(s, axis=0, keepdims=True) for s in parts])
        es = [jnp.exp(s - top) for s in parts]
        total = sum(jnp.sum(e, axis=0, keepdims=True) for e in es)
        low = top + jnp.log(total)
        o_t = sum(nn(value[head_rows(j), :], e.astype(BF16)) for value, e in zip(values, es))
        o_t = (o_t / total).astype(BF16)
        for g in range(group):
            cols = slice(g * rows, (g + 1) * rows)
            lse_out[pl.ds(j * group + g, 1), :] = low[:, cols]
            ot_out[head_rows(j * group + g), :] = o_t[:, cols]
        return carry

    lax.fori_loop(0, kv_heads, one_group, 0)
    o = ot_out[...].T
    to = nt(o, oa[...])
    tot_out[...] = to.T.astype(BF16)
    to = to.astype(BF16)
    copies[0].wait()
    for r in range(PARTS):
        at = quarter(me, r)
        put_block(r, nn(o, wo[:, at]) + nn(to, ob[:, at]), z_keep, z_send)


def front_kernel(chunk, last, info, wgu_in, wd_in, x0, x1, x2, x3, zo, zp, g0, g1, g2, g3, gains, a2, bd, fb, da,
                 *rest):
    units = wd_in.shape[0]
    if chunk:
        wgu, wd = wgu_in, wd_in
    else:
        (wgu, wd, f_s, sems), rest = rest[-4:], rest[:-4]
        rest = (*rest, f_s)

    def copies(i):
        c = pl.ds(pl.multiple_of(i * QUARTER, QUARTER), QUARTER)
        return (pltpu.make_async_copy(wgu_in.at[:, :, c], wgu.at[:, :, c], sems.at[0, i]),
                pltpu.make_async_copy(wd_in.at[c, :], wd.at[c, :], sems.at[1, i]))

    if not chunk:
        for i in range(units // QUARTER):
            for copy in copies(i):
                copy.start()
    f_s = rest[-1]
    xm_out, xq_out, h_out, g_out, act_out, dg_out, du_out, t2_s, dtd_s, b_out = rest[-11:-1]
    me, length = info[0], info[1]
    rows = h_out.shape[0]
    xs, gs = ([chunk_of(v, chunk, rows) for v in vs] for vs in ((x0, x1, x2, x3), (g0, g1, g2, g3)))

    def norm(i, carry):
        at = row_block(i)
        valid = is_valid(chunk, i, rows, length)
        square = jnp.zeros((ROW_BLOCK, 1), F32)
        for r in range(PARTS):
            v = xs[r][at, :].astype(F32) + total_block(r, at, zo, zp)
            if r == 0:
                xq_out[at, :] = v
            f_s[:, quarter(me, r)] = v
            square = square + jnp.sum(v * v, axis=1, keepdims=True)
            g_out[at, quarter(me, r)] = jnp.where(valid, gs[r][at, :], jnp.zeros((), BF16))
        inv = lax.rsqrt(square / WIDTH + EPS)
        for r in range(PARTS):
            v = f_s[:, quarter(me, r)]
            xm_out[at, quarter(me, r)] = v.astype(BF16)
            h_out[at, quarter(me, r)] = (v * inv * gains[r, 1:2, :].astype(F32)).astype(BF16)
        return carry

    lax.fori_loop(0, rows // ROW_BLOCK, norm, 0)
    t2 = nt(h_out[...], a2[...])
    t2_s[...] = t2.astype(BF16)
    dtd = nt(g_out[...], bd[...])
    dtd_s[...] = dtd.astype(BF16)
    t2t, dtdt = t2.T.astype(BF16), dtd.T.astype(BF16)

    def block(i, carry):
        c = pl.ds(pl.multiple_of(i * QUARTER, QUARTER), QUARTER)
        if not chunk:
            for copy in copies(i):
                copy.wait()
        h, g = h_out[...], g_out[...]
        gate = nn(h, wgu[0, :, c]) + nn(t2_s[:, :RANK], fb[0, :, c])
        up = nn(h, wgu[1, :, c]) + nn(t2_s[:, RANK:], fb[1, :, c])
        dact = nt(g, wd[c, :]) + nn(dtd_s[...], da[:, c])
        sig = 1.0 / (1.0 + jnp.exp(-gate))
        silu = gate * sig
        act = (silu * up).astype(BF16)
        dgate = (dact * up * sig * (1.0 + gate * (1.0 - sig))).astype(BF16)
        dup = (dact * silu).astype(BF16)
        act_out[:, c], dg_out[:, c], du_out[:, c] = act, dgate, dup
        for k, value in enumerate((nn(t2t[:RANK], dgate), nn(t2t[RANK:], dup), nn(dtdt, act))):
            at = pl.ds(pl.multiple_of((3 * i + k) * RANK, RANK), RANK)
            if last:
                value = value + rest[0][at, :]
            b_out[at, :] = value.astype(b_out.dtype)
        return carry

    lax.fori_loop(0, units // QUARTER, block, 0)


def back_kernel(last, info, wgu, h, g, act, dg, du, a2, fb, da, *rest):
    (value_s, low_s), rest = rest[-2:], rest[:-2]
    outs, rest = (rest[-3:], rest[:-3]) if last else (rest[-4:], rest[:-4])
    td_out, d_keep, d_send = outs[:3]
    me = info[0]
    rows = h.shape[0]
    dt2 = jnp.concatenate([nt(dg[...], fb[0]), nt(du[...], fb[1])], axis=1)
    td = nt(act[...], da[...])
    td_out[...] = td
    dt2b = dt2.astype(BF16)
    dt2t, tdt = dt2.T.astype(BF16), td.T.astype(BF16)

    def block(r, carry):
        at = quarter(me, r)
        value_s[...] = nt(dg[...], wgu[0, at, :]) + nt(du[...], wgu[1, at, :]) + nn(dt2b, a2[:, at])
        store_block(r, value_s, slice(0, rows), d_keep, d_send)
        low_s[:2 * RANK, :] = nn(dt2t, h[:, at])
        low_s[2 * RANK:, :] = nn(tdt, g[:, at])
        if last:
            low_s[...] += rest[0][:, at]
            store_block(r, low_s, slice(rows, rows + 3 * RANK), d_keep, d_send)
        else:
            outs[3][:, at] = low_s[...]
        return carry

    lax.fori_loop(0, PARTS, block, 0)


def down_kernel(info, wd, act, td, bd, xq, y_keep, y_send, value_s):
    me = info[0]
    tdb = td[...].astype(BF16)

    def block(r, carry):
        at = quarter(me, r)
        value_s[...] = nn(act[...], wd[:, at]) + nn(tdb, bd[:, at])
        store_block(r, value_s, slice(0, act.shape[0]), y_keep, y_send)
        return carry

    lax.fori_loop(0, PARTS, block, 0)
    y_keep[:, LO] += xq[...]


def attend_back_kernel(chunk, last, info, wq_h, wkv_h, wo_h, x0, x1, x2, x3, g0, g1, g2, g3, xm, do_, dp, gains, a1,
                       qb, kvb, oa, ob, cos_t, sin_t, t1t, qt, ot, lse, tot, *rest):
    scratch, rest = rest[-14:], rest[:-14]
    h_in, z_s, f_s, dot_s, dqt_s, dkt_s, dvt_s, dq_s, value_s, low_s, wq, wkv, wo, sems = scratch
    copies = copies_of(((wo_h, wo), (wq_h, wq), (wkv_h, wkv)), sems)
    n_out = 7 if last else 9
    outs, rest = rest[-n_out:], rest[:-n_out]
    dxq_out, h_keep, h_send, inv_out, b_out = outs[:5]
    triples, rest = rest[:3 * (chunk + 1)], rest[3 * (chunk + 1):]
    keys, values, keys_t = triples[0::3], triples[1::3], triples[2::3]
    me, length = info[0], info[1]
    rows = xm.shape[0]
    kv_heads = keys[0].shape[0]
    heads = qt.shape[0] // HEAD
    group = heads // kv_heads
    q_cols, kv_cols = heads * HEAD, kv_heads * HEAD
    xs, gs = ([chunk_of(v, chunk, rows) for v in vs] for vs in ((x0, x1, x2, x3), (g0, g1, g2, g3)))

    def norm_back(i, carry):
        at = row_block(i)
        valid = is_valid(chunk, i, rows, length)
        square, first, inner = (jnp.zeros((ROW_BLOCK, 1), F32) for _ in range(3))
        for r in range(PARTS):
            v = xm[at, quarter(me, r)].astype(F32)
            square = square + jnp.sum(v * v, axis=1, keepdims=True)
            w = total_block(r, at, do_, dp) * gains[r, 1:2, :].astype(F32)
            f_s[:, quarter(me, r)] = w
            inner = inner + jnp.sum(v * w, axis=1, keepdims=True)
            u = xs[r][at, :].astype(F32)
            first = first + jnp.sum(u * u, axis=1, keepdims=True)
        inv_one = lax.rsqrt(first / WIDTH + EPS)
        inv_out[at, :] = inv_one
        inv = lax.rsqrt(square / WIDTH + EPS)
        back = inv * inv * inv * inner / WIDTH
        for r in range(PARTS):
            v = xm[at, quarter(me, r)].astype(F32)
            g = jnp.where(valid, gs[r][at, :].astype(F32), 0.0)
            d = g + inv * f_s[:, quarter(me, r)] - v * back
            if r == 0:
                dxq_out[at, :] = d
            z_s[at, quarter(me, r)] = d.astype(BF16)
            u = xs[r][at, :].astype(F32)
            h_in[at, quarter(me, r)] = (u * inv_one * gains[r, 0:1, :].astype(F32)).astype(BF16)
        return carry

    lax.fori_loop(0, rows // ROW_BLOCK, norm_back, 0)
    dz = z_s[...]
    dto = nt(dz, ob[...])
    copies[0].wait()
    d_o = nt(dz, wo[...]) + nn(dto.astype(BF16), oa[...])
    dot_s[...] = d_o.T.astype(BF16)
    kept = [jnp.concatenate([visible(c * rows, chunk * rows, rows, length)] * group, axis=1) for c in range(chunk + 1)]

    def one_group(j, carry):
        places = [head_rows(j * group + g) for g in range(group)]
        q_g = jnp.concatenate([qt[at, :] for at in places], axis=1)
        do_g = jnp.concatenate([dot_s[at, :] for at in places], axis=1)
        o_g = jnp.concatenate([ot[at, :] for at in places], axis=1)
        low = jnp.concatenate([lse[pl.ds(j * group + g, 1), :] for g in range(group)], axis=1)
        dots = jnp.sum(do_g.astype(F32) * o_g.astype(F32), axis=0, keepdims=True)
        dq_g = 0.0
        for c in range(chunk + 1):
            prob = jnp.where(kept[c], jnp.exp(nn(keys[c][j], q_g) - low), 0.0)
            ds = (prob * (nn(values[c][j], do_g) - dots)).astype(BF16)
            dq_g = dq_g + nn(keys_t[c][head_rows(j), :], ds)
            dk, dv = nt(q_g, ds), nt(do_g, prob.astype(BF16))
            if last:
                dk, dv = dk + rest[2][head_rows(j), :], dv + rest[3][head_rows(j), :]
            dkt_s[c, head_rows(j), :], dvt_s[c, head_rows(j), :] = dk, dv
        for g in range(group):
            dqt_s[places[g], :] = dq_g[:, g * rows:(g + 1) * rows]
        return carry

    lax.fori_loop(0, kv_heads, one_group, 0)
    if not last:
        outs[6][...], outs[7][...] = dkt_s[0], dvt_s[0]
    cos, sin = cos_t[...], sin_t[...]
    dto_t, o_t = dto.T.astype(BF16), ot[...]
    d_out_a = nt(dto_t, o_t)
    turn_back(dqt_s[...], cos * (HEAD ** -0.5), sin * (HEAD ** -0.5), dot_s)
    dq_s[:, :q_cols] = dot_s[...].T
    turn_back(dkt_s[chunk], cos, sin, dot_s)
    dq_s[:, q_cols:q_cols + kv_cols] = dot_s[:kv_cols, :].T
    dq_s[:, q_cols + kv_cols:] = dvt_s[chunk].T.astype(BF16)
    dq, dk, dv = dq_s[:, :q_cols], dq_s[:, q_cols:q_cols + kv_cols], dq_s[:, q_cols + kv_cols:]
    dt1 = jnp.concatenate([nt(dq, qb[...]), nt(dk, kvb[0]), nt(dv, kvb[1])], axis=1)
    dt1b = dt1.astype(BF16)
    kv_pad = jnp.zeros((RANK, QUARTER - 2 * kv_cols), F32)
    d_kv = jnp.concatenate([nn(t1t[RANK:2 * RANK, :], dk), nn(t1t[2 * RANK:, :], dv), kv_pad], axis=1)
    for k, value in enumerate((nn(t1t[:RANK, :], dq), d_out_a, d_kv)):
        at = slice(k * RANK, (k + 1) * RANK)
        if last:
            value = value + rest[0][at, :]
        b_out[at, :] = value.astype(b_out.dtype)
    dt1t = dt1.T.astype(BF16)
    copies[1].wait()
    copies[2].wait()

    def block(r, inner):
        at = quarter(me, r)
        d = nt(dq_s[:, :q_cols], wq[at, :]) + nn(dt1b, a1[:, at])
        d = d + nt(dq_s[:, q_cols:q_cols + kv_cols], wkv[0, at, :]) + nt(dq_s[:, q_cols + kv_cols:], wkv[1, at, :])
        value_s[...] = d
        store_block(r, value_s, slice(0, rows), h_keep, h_send)
        low_s[:3 * RANK, :] = nn(dt1t, h_in[:, at])
        low_s[3 * RANK:, :] = nn(tot[...], z_s[:, at])
        if last:
            low_s[...] += rest[1][:, at]
            store_block(r, low_s, slice(0, 4 * RANK), outs[5], outs[6])
        else:
            outs[5][:, at] = low_s[...]
        return inner + jnp.sum(d * h_in[:, at].astype(F32), axis=1, keepdims=True)

    inner = lax.fori_loop(0, PARTS, block, jnp.zeros((rows, 1), F32))
    inner = jnp.broadcast_to(inner, (rows, LANES)).T[:SPARE // 2, :]
    if last:
        for ref in outs[5:7]:
            for c, value in enumerate((inner, rest[4][...])):
                at = slice(4 * RANK + c * SPARE // 2, 4 * RANK + (c + 1) * SPARE // 2)
                ref[at, QUARTER:QUARTER + rows] = value.astype(ref.dtype)
                ref[at, QUARTER + rows:] = jnp.zeros((SPARE // 2, QUARTER - rows), ref.dtype)
                ref[at, :QUARTER] = jnp.zeros((SPARE // 2, QUARTER), ref.dtype)
    else:
        outs[8][...] = inner


def output_kernel(info, y_far, *refs):
    out = refs[-1]
    rows = out.shape[0] // CHUNKS
    for c in range(CHUNKS):
        y_keep, y_got = refs[2 * c:2 * (c + 1)]
        at = slice(c * rows, (c + 1) * rows)
        valid = c * rows + lax.broadcasted_iota(jnp.int32, (rows, 1), 0) < info[1]
        y = y_keep[:, LO] + y_got[:, LO].astype(F32) + y_far[at, :].astype(F32)
        out[at, :] = jnp.where(valid, y, 0.0).astype(BF16)


def finish_kernel(gains, x_all, aa_high, aa_far, *refs):
    out = refs[-1]
    gain = gains[0, 0:1, :].astype(F32)
    rows = out.shape[0] // CHUNKS
    inner = aa_high[4 * RANK:, :].astype(F32) + aa_far[4 * RANK:, :].astype(F32)
    for c in range(CHUNKS):
        dx, keep, got, there, inv = refs[5 * c:5 * (c + 1)]
        x = chunk_of(x_all, c, rows)
        mine = inner[c * SPARE // 2:c * SPARE // 2 + 8, :rows].T[:, 0:1]
        inv = inv[...]
        grad = keep[:, LO] + got[:, LO].astype(F32) + there[...].astype(F32)
        grad = inv * (gain * grad) - x[...].astype(F32) * (inv * inv * mine / WIDTH)
        out[c * rows:(c + 1) * rows, :] = (dx[...] + grad).astype(BF16)


def high_sum_kernel(*refs):
    out = refs[-1]
    rows = out.shape[0] // (len(refs) // 2)
    for c in range(len(refs) // 2):
        keep, got = refs[2 * c:2 * c + 2]
        out[c * rows:(c + 1) * rows, :] = (keep[:, HI] + got[:, HI].astype(F32)).astype(BF16)


def high_sum(*pairs):
    args = [v for pair in pairs for v in pair]
    rows = sum(keep.shape[0] for keep, _ in pairs)
    return call(high_sum_kernel, None, (), args, [((rows, QUARTER), BF16)], [], "high_sum", 8)[0]


def split_refs(refs, counts):
    groups = []
    for count in counts:
        groups.append(refs[:count])
        refs = refs[count:]
    return groups, refs


def with_entry(parts, at, use):
    start = 0
    for ref in parts:
        @pl.when((at >= start) & (at < start + ref.shape[0]))
        def _(ref=ref, start=start):
            use(ref, at - start)
        start += ref.shape[0]


def sum_slots(info, owners, out_refs, one_slot):
    count = out_refs[0].shape[0]
    base = pl.program_id(0) * count
    slots = owners.shape[0]
    for ref in out_refs:
        ref[...] = jnp.zeros_like(ref)

    def add(slot, carry):
        owner = owners[slot] - base

        @pl.when((owner >= 0) & (owner < count))
        def _():
            one_slot(owner, entry_of(slot, info[3], slots))
        return carry

    lax.fori_loop(0, slots, add, 0)


def feedforward_sum_kernel(counts, info, owners, *refs):
    (b_parts, *a_parts), outs = split_refs(refs, counts)
    ga, gdb, gb, gda = outs
    me = info[0]

    def one_slot(owner, at):
        def add_b(ref, e):
            for i in range(gda.shape[2] // QUARTER):
                cols = slice(i * QUARTER, (i + 1) * QUARTER)
                base = i * 3 * RANK
                gb[owner, 0, :, cols] += ref[e, base:base + RANK, :].astype(F32)
                gb[owner, 1, :, cols] += ref[e, base + RANK:base + 2 * RANK, :].astype(F32)
                gda[owner, :, cols] += ref[e, base + 2 * RANK:base + 3 * RANK, :].astype(F32)

        with_entry(b_parts, at, add_b)
        for near_bit, parts in enumerate(a_parts):
            def add_a(ref, e, near_bit=near_bit):
                for r, cols in ((near_bit, LO), (near_bit ^ 2, HI)):
                    ga[owner, :, quarter(me, r)] += ref[e, :2 * RANK, cols].astype(F32)
                    gdb[owner, :, quarter(me, r)] += ref[e, 2 * RANK:, cols].astype(F32)

            with_entry(parts, at, add_a)

    sum_slots(info, owners, outs, one_slot)


def attention_sum_kernel(counts, info, owners, *refs):
    (b_parts, *a_parts), outs = split_refs(refs, counts)
    ga, gob, gq, gkv, goa = outs
    me = info[0]
    kv_cols = gkv.shape[3]

    def one_slot(owner, at):
        def add_b(ref, e):
            gq[owner] += ref[e, :RANK, :].astype(F32)
            goa[owner] += ref[e, RANK:2 * RANK, :].astype(F32)
            gkv[owner, 0] += ref[e, 2 * RANK:3 * RANK, :kv_cols].astype(F32)
            gkv[owner, 1] += ref[e, 2 * RANK:3 * RANK, kv_cols:2 * kv_cols].astype(F32)

        with_entry(b_parts, at, add_b)
        for r, parts in enumerate(a_parts):
            def add_a(ref, e, r=r):
                ga[owner, :, quarter(me, r)] += ref[e, :3 * RANK, :].astype(F32)
                gob[owner, :, quarter(me, r)] += ref[e, 3 * RANK:, :].astype(F32)

            with_entry(parts, at, add_a)

    sum_slots(info, owners, outs, one_slot)


def deal_kernel(slots, source, out, sems):
    made = [pltpu.make_async_copy(source.at[i], out.at[slots[i]], sems.at[i]) for i in range(source.shape[0])]
    for copy in made:
        copy.start()
    for copy in made:
        copy.wait()


def collect_kernel(slots, source, out, sems):
    made = [pltpu.make_async_copy(source.at[slots[i]], out.at[i], sems.at[i]) for i in range(source.shape[0])]
    for copy in made:
        copy.start()
    for copy in made:
        copy.wait()


def adapter_kernel(count, info, *refs):
    made = [pltpu.make_async_copy(refs[i].at[info[2]], refs[count + i], refs[-1].at[i]) for i in range(count)]
    for copy in made:
        copy.start()
    for copy in made:
        copy.wait()


def load_adapters(arrays, info):
    count = len(arrays)
    return pl.pallas_call(
        functools.partial(adapter_kernel, count),
        in_specs=[pl.BlockSpec(memory_space=pltpu.SMEM)] + [pl.BlockSpec(memory_space=pltpu.HBM)] * count,
        out_specs=[pl.BlockSpec(memory_space=pltpu.VMEM)] * count,
        out_shape=[pltpu.VMEM(a.shape[1:], a.dtype) for a in arrays],
        scratch_shapes=[pltpu.SemaphoreType.DMA((count,))],
        compiler_params=pltpu.CompilerParams(vmem_limit_bytes=MIB),
        cost_estimate=pl.CostEstimate(flops=1000, transcendentals=0, bytes_accessed=1000),
        name="adapters",
    )(info, *(in_hbm(a) for a in arrays))


def move_rows(kernel, value, slots, name, outs, in_space, out_space, sems):
    return pl.pallas_call(
        kernel,
        in_specs=[pl.BlockSpec(memory_space=pltpu.SMEM), pl.BlockSpec(memory_space=in_space)],
        out_specs=[pl.BlockSpec(memory_space=out_space)] * len(outs),
        out_shape=outs,
        scratch_shapes=[pltpu.SemaphoreType.DMA(sems)],
        compiler_params=pltpu.CompilerParams(vmem_limit_bytes=MIB),
        cost_estimate=pl.CostEstimate(flops=1000, transcendentals=0, bytes_accessed=1000),
        name=name,
    )(slots, pltpu.with_memory_space_constraint(value, in_space))


def sds(shape, dtype):
    return jax.ShapeDtypeStruct(tuple(shape), dtype)


def in_vmem(value):
    return pltpu.with_memory_space_constraint(value, pltpu.VMEM)


def in_hbm(value):
    return pltpu.with_memory_space_constraint(value, pltpu.HBM)


def call(kernel, info, weights, args, outs, scratch, name, mib, after=(), sems=()):
    vmem = pl.BlockSpec(memory_space=pltpu.VMEM)
    scalars = () if info is None else (info,)
    n, w = len(scalars), len(weights)

    def body(*refs):
        at = n + w + len(args)
        kernel(*refs[:at], *refs[at + len(after):])

    return pl.pallas_call(
        body,
        in_specs=[pl.BlockSpec(memory_space=pltpu.SMEM)] * n + [pl.BlockSpec(memory_space=pltpu.HBM)] * w + [vmem] * len(args)
        + [pl.BlockSpec(memory_space=pl.ANY)] * len(after),
        out_specs=[vmem] * len(outs),
        out_shape=[pltpu.VMEM(tuple(s), d) for s, d in outs],
        scratch_shapes=[pltpu.VMEM(s, d) for s, d in scratch] + ([pltpu.SemaphoreType.DMA(sems)] if sems else []),
        compiler_params=pltpu.CompilerParams(vmem_limit_bytes=mib * MIB),
        cost_estimate=pl.CostEstimate(flops=1000, transcendentals=0, bytes_accessed=1000),
        name=name,
    )(*scalars, *(in_hbm(a) for a in weights), *(in_vmem(a) for a in args), *after)


def whole_spec(value):
    zeros = (0,) * value.ndim
    return pl.BlockSpec(value.shape, lambda i, *_: zeros)


def sum_call(kernel, scalars, groups, outs, name):
    args = [v for group in groups for v in group]
    steps = 2
    specs = [pl.BlockSpec((o.shape[0] // steps,) + o.shape[1:], (lambda n: lambda i, *_: (i,) + (0,) * n)(o.ndim - 1))
             for o in outs]
    return pl.pallas_call(
        functools.partial(kernel, [len(group) for group in groups]),
        grid_spec=pltpu.PrefetchScalarGridSpec(
            num_scalar_prefetch=len(scalars), grid=(steps,),
            in_specs=[whole_spec(a) for a in args], out_specs=specs),
        out_shape=outs,
        compiler_params=pltpu.CompilerParams(
            dimension_semantics=("arbitrary",),
            vmem_limit_bytes=4 * MIB + 2 * sum(a.size * a.dtype.itemsize for a in args)
            + sum(o.size * o.dtype.itemsize for o in outs)),
        cost_estimate=pl.CostEstimate(flops=0, transcendentals=0, bytes_accessed=12000000),
        name=name,
    )(*scalars, *args)


def swap(value, bit, axis, size):
    return lax.ppermute(value, axis, [(i, i ^ bit) for i in range(size)])


def near(value):
    return swap(value, 1, "mp", PARTS)


def far(value):
    return swap(value, 2, "mp", PARTS)


def spread(value):
    there = far(value)
    return (value, near(value), there, near(there))


def far_sum_kernel(own, got, out):
    for to, other in ((LO, HI), (HI, LO)):
        out[:, to] = (own[:, to].astype(F32) + got[:, other].astype(F32)).astype(BF16)


def far_sum(own, got):
    return call(far_sum_kernel, None, (), (own, got), [(own.shape, BF16)], [], "far_sum", 6)[0]


def pair_sum_kernel(keep, got, out):
    out[...] = (keep[...] + got[...].astype(F32)).astype(BF16)


def pair_sum(keep, send, *before):
    got = near(send)
    got = late(got, *before) if before else got
    return call(pair_sum_kernel, None, (), (keep, got), [(send.shape, BF16)], [], "pair_sum", 6)[0]


def late(value, *others):
    return lax.optimization_barrier((value, *others))[0]


def doubled(stack, bit, size):
    return jnp.concatenate([stack, swap(stack, bit, "dp", size)], axis=0)


def entry_of(slot, place, size):
    bits = size.bit_length() - 1
    apart = slot ^ place
    return sum(((apart >> b) & 1) << (bits - 1 - b) for b in range(bits))


def shards(dp, residual, attention_gain, query_matrix, key_value_matrix, output_matrix, feedfwd_gain,
           gate_up_matrix, down_matrix, attention_adapter_input, query_adapter_output,
           key_value_adapter_output, output_adapter_input, output_adapter_output, feedfwd_adapter_input,
           feedfwd_adapter_output, down_adapter_input, down_adapter_output, lengths, adapter_index,
           dealing_slots, cotangent):
    seqs = residual.shape[0]
    length = cotangent.shape[1]
    units = down_matrix.shape[0]
    adapters = attention_adapter_input.shape[0]
    q_cols = query_matrix.shape[1]
    kv_cols = key_value_matrix.shape[2]
    kv_heads = kv_cols // HEAD
    heads = q_cols // HEAD
    rows = length // CHUNKS
    half = 2 * QUARTER
    me = lax.axis_index("mp")
    place = lax.axis_index("dp")

    is_there = dealing_slots[None, :] == jnp.arange(seqs, dtype=jnp.int32)[:, None]
    owners = jnp.sum(jnp.where(is_there, adapter_index[None, :], 0), axis=1)
    spans = jnp.sum(jnp.where(is_there, lengths[None, :], 0), axis=1)
    mine = jnp.arange(seqs, dtype=jnp.int32) == place
    my_length = jnp.sum(jnp.where(mine, spans, 0))
    my_adapter = jnp.sum(jnp.where(mine, owners, 0))
    info = jnp.stack([me.astype(jnp.int32), my_length, my_adapter, place.astype(jnp.int32)])

    gs = spread(cotangent[0])
    gains = jnp.stack(spread(jnp.stack([attention_gain, feedfwd_gain])))
    ordered, = move_rows(deal_kernel, residual, dealing_slots, "deal", [pltpu.VMEM(residual.shape, BF16)], pltpu.HBM,
                         pltpu.VMEM, (seqs,))
    dealt = lax.all_to_all(ordered, "dp", split_axis=0, concat_axis=1, tiled=True)[0]
    adapters_here = load_adapters(
        (attention_adapter_input, query_adapter_output, key_value_adapter_output, output_adapter_input,
         output_adapter_output, feedfwd_adapter_input, feedfwd_adapter_output, down_adapter_input,
         down_adapter_output), info)
    a1, qb, kvb, oa, ob, a2, fba, da, bd = adapters_here
    dealt = late(dealt, a1, gains)
    beside = near(dealt)
    there = [far(dealt[c * rows:(c + 1) * rows]) for c in range(CHUNKS)]
    xs = [None] * CHUNKS
    cos_np, sin_np = rope_tables(length)
    cos = [jnp.asarray(cos_np[:, c * rows:(c + 1) * rows]) for c in range(CHUNKS)]
    sin = [jnp.asarray(sin_np[:, c * rows:(c + 1) * rows]) for c in range(CHUNKS)]
    wq, wkv, wo = query_matrix, key_value_matrix, output_matrix

    def like(*arrays):
        return [(a.shape, a.dtype) for a in arrays]

    wide, col, block, thin = (rows, WIDTH), (rows, half), (rows, QUARTER), (rows, 1)
    saved, kept, z_own, z_far = ([None] * CHUNKS for _ in range(4))
    order = ()
    for c in range(CHUNKS):
        xs[c] = (dealt, beside, there[c], near(late(there[c], saved[0][0]) if c else late(there[c], gs[2])))
        outs = [((3 * RANK, rows), BF16), ((q_cols, rows), BF16), ((kv_heads, rows, HEAD), BF16),
                ((kv_heads, rows, HEAD), BF16), ((kv_cols, rows), BF16), ((kv_cols, rows), BF16)]
        saved[c] = call(
            functools.partial(project_kernel, c), info, (wq, wkv), (*xs[c], gains, a1, qb, kvb, cos[c], sin[c]), outs,
            [(wide, BF16)] + like(wq, wkv), "project_%d" % c, 12, order, (2,))
        outs = [(col, F32), (col, BF16), ((q_cols, rows), BF16), ((heads, rows), F32), ((RANK, rows), BF16)]
        pairs = [v for p in saved[:c + 1] for v in (p[2], p[5])]
        z_keep, z_send, *kept[c] = call(
            functools.partial(attend_kernel, c), info, (wo,), (saved[c][1], oa, ob, *pairs), outs, like(wo),
            "attend_%d" % c, 10, (saved[c][0], gs[1], gs[3]) if c else (saved[c][0],), (1,))
        z_own[c] = pair_sum(z_keep, late(z_send, z_far[0] if c else there[-1]))
        z_far[c] = far(z_own[c])
        order = (kept[c][1], z_own[c])
    def front(c, total, partial, order):
        hidden = (rows, units)
        outs = [(wide, BF16), (block, F32), (wide, BF16), (wide, BF16), (hidden, BF16), (hidden, BF16), (hidden, BF16),
                ((rows, 2 * RANK), BF16), ((rows, RANK), BF16),
                ((3 * RANK * units // QUARTER, QUARTER), BF16 if c else F32)]
        args = (*xs[c], total, near(total), *gs, gains, a2, bd, fba, da, *partial)
        weights = () if c else (gate_up_matrix, down_matrix)
        outs += like(*weights)
        return call(
            functools.partial(front_kernel, c, c == CHUNKS - 1), info, weights, (wgu, wd, *args) if c else args, outs,
            [((ROW_BLOCK, WIDTH), F32)], "front_%d" % c, 8, order, () if c else (2, units // QUARTER))

    def back(c, hidden, partial, order):
        first = col if c else (rows + 3 * RANK, half)
        outs = [((rows, RANK), F32), (first, F32), (first, BF16)]
        outs += [((3 * RANK, WIDTH), F32)] if c else []
        return call(
            functools.partial(back_kernel, c == 0), info, (), (wgu, *hidden[2:7], a2, fba, da, *partial), outs,
            [(block, F32), ((3 * RANK, QUARTER), F32)], "back_%d" % c, 8, order)

    def down(c, td, order):
        return call(down_kernel, info, (), (wd, hidden[c][4], td, bd, hidden[c][1]), [(col, F32), (col, BF16)],
                    [(block, F32)], "down_%d" % c, 6, order)

    def attend_back(c, total, partial, order):
        outs = [(block, F32), (col, F32), (col, BF16), (thin, F32), ((3 * RANK, QUARTER), F32 if c else BF16)]
        low = (4 * RANK + SPARE, half)
        outs += ([((4 * RANK, WIDTH), F32), ((kv_cols, rows), F32), ((kv_cols, rows), F32), ((SPARE // 2, rows), F32)]
                 if c else [(low, F32), (low, BF16)])
        scratch = [(wide, BF16), (wide, BF16), ((ROW_BLOCK, WIDTH), F32), ((q_cols, rows), BF16), ((q_cols, rows), F32),
                   ((c + 1, kv_cols, rows), F32), ((c + 1, kv_cols, rows), F32), ((rows, q_cols + 2 * kv_cols), BF16),
                   (block, F32), ((4 * RANK, QUARTER), F32)]
        triples = [v for p in saved[:c + 1] for v in (p[2], p[3], p[4])]
        return call(
            functools.partial(attend_back_kernel, c, c == 0), info, (wq, wkv, wo),
            (*xs[c], *gs, hidden[c][0], total, near(total), gains, a1, qb, kvb, oa, ob, cos[c], sin[c], *saved[c][:2],
             *kept[c], *triples, *partial), outs, scratch + like(wq, wkv, wo), "attend_back_%d" % c, 18, order, (3,))

    bits = [1 << b for b in reversed(range(dp.bit_length() - 1))]
    def to_bands(value):
        return lax.all_to_all(value.reshape(dp, length // dp, QUARTER), "dp", split_axis=0, concat_axis=0, tiled=True)

    def collect(value, name, *before):
        rows_out = sds((seqs, length // dp, QUARTER), BF16)
        return move_rows(collect_kernel, value, late(dealing_slots, *before), name, [rows_out], pltpu.VMEM, pl.ANY,
                         (seqs,))[0]

    hidden, d_own, d_far, y_keep, y_got = ([None] * CHUNKS for _ in range(5))
    *hidden[0], wgu, wd = front(0, far_sum(z_own[0], z_far[0]), (), order)
    step = hidden[0][8]
    hidden[1] = front(1, far_sum(z_own[1], late(z_far[1], step)), hidden[0][9:], (step,))
    fb = hidden[1][9][None]
    fb_first = swap(fb, bits[0], "dp", dp)
    td, d_keep, d_send, fa = back(1, hidden[1], (), (hidden[1][8],))
    d_own[1] = pair_sum(d_keep, late(d_send, fb_first))
    d_far[1] = far(d_own[1])
    fb = fb_more = jnp.concatenate([fb, fb_first], axis=0)
    for bit in bits[1:-1]:
        fb_more = doubled(fb_more, bit, dp)
    fb_more = fb_more[2:]
    fb_side = swap(fb, bits[-1], "dp", dp)
    td_0, d_keep, d_send = back(0, hidden[0], (fa,), (d_own[1],))
    y_keep[1], y_send = down(1, td, (td_0,))
    total = far_sum(d_own[1], late(d_far[1], y_send))
    d_own[0] = pair_sum(d_keep, late(d_send, fb_more, fb_side), total)
    d_far[0] = far(d_own[0])
    fb_more_side = swap(fb_more, bits[-1], "dp", dp)
    y_got[1] = near(late(y_send, d_own[0]))
    dxq, h_keep, h_send, inv, *sums = attend_back(1, total, (), (d_own[0], y_send))
    total = far_sum(d_own[0], late(d_far[0], inv))
    h_got = near(late(h_send, fb_more_side))
    h_high = high_sum((h_keep, h_got))
    h_far = far(h_high)
    final = [None, (dxq, h_keep, h_got, h_far, inv)]
    fa = total[rows:][None]
    fa_first = swap(fa, bits[0], "dp", dp)
    dxq, h_keep, h_send, inv, att_b, aa_keep, aa_send = attend_back(0, total, sums, (h_high,))
    ready = (fa_first, h_far)
    aa_got = near(late(aa_send, *ready))
    aa_high = high_sum((aa_keep, aa_got))
    aa_far = far(aa_high)
    h_got = near(late(h_send, *ready))
    h_high = high_sum((h_keep, h_got))
    h_far = far(h_high)
    final[0] = (dxq, h_keep, h_got, h_far, inv)
    att_a = aa_keep[:4 * RANK, :QUARTER] + aa_got[:4 * RANK, :QUARTER].astype(F32)
    att_a = (att_a + late(aa_far, h_high)[:4 * RANK].astype(F32)).astype(BF16)
    n_b = att_b.shape[0]
    att = jnp.concatenate([att_b, att_a], axis=0)[None]
    y_keep[0], y_send = down(0, td_0, (att,))
    y_got[0] = near(y_send)
    att = doubled(att, bits[0], dp)
    att = late(att, h_far, y_send)
    for bit in bits[1:-1]:
        att = doubled(att, bit, dp)
    fa = late(jnp.concatenate([fa, fa_first], axis=0), aa_high)
    for bit in bits[1:-1]:
        fa = doubled(fa, bit, dp)
    fa_side = swap(fa, bits[-1], "dp", dp)
    y_far = far(high_sum(*((k, late(g, h_far)) for k, g in zip(y_keep, y_got))))

    dinput, = call(finish_kernel, None, (), (gains, dealt, aa_high, aa_far, *(v for f in final for v in f)),
                   [((length, QUARTER), BF16)], [], "finish", 8, (att, fa_side))
    input_grad = collect(to_bands(dinput), "collect_grad")
    outs = [sds((adapters, 2 * RANK, WIDTH), F32), sds((adapters, RANK, WIDTH), F32),
            sds((adapters, 2, RANK, units), F32), sds((adapters, RANK, units), F32)]
    ga_ffn, g_down_b, g_ffn_b, g_down_a = sum_call(
        feedforward_sum_kernel, (info, owners),
        ((fb, fb_more, fb_side, fb_more_side), (fa, fa_side), (near(fa), near(fa_side))), outs, "feedforward_sum")

    result, = call(output_kernel, info, (), (late(y_far, dinput, g_down_a), *(v for p in zip(y_keep, y_got) for v in p)),
                   [((length, QUARTER), BF16)], [], "output", 8)
    output = collect(to_bands(result), "collect_out", input_grad)

    att_side = swap(att, bits[-1], "dp", dp)
    a_parts = [att[:, n_b:], att_side[:, n_b:]]
    a_far = [far(v) for v in a_parts]
    a_far[0] = late(a_far[0], input_grad)
    outs = [sds((adapters, 3 * RANK, WIDTH), F32), sds((adapters, RANK, WIDTH), F32),
            sds((adapters, RANK, q_cols), F32), sds((adapters, 2, RANK, kv_cols), F32),
            sds((adapters, RANK, q_cols), F32)]
    ga_att, g_out_b, g_query_b, g_kv_b, g_out_a = sum_call(
        attention_sum_kernel, (info, owners),
        ((att, att_side), a_parts, [near(v) for v in a_parts], a_far, [near(v) for v in a_far]), outs, "attention_sum")
    return (output, input_grad, ga_att, g_query_b, g_kv_b, g_out_a, g_out_b, ga_ffn, g_ffn_b, g_down_a, g_down_b)


def solution(mesh):
    in_specs = (
        P(None, "dp", "mp"), P("mp"), P(None, "mp"), P(None, None, "mp"), P("mp", None), P("mp"),
        P(None, None, "mp"), P("mp", None), P(), P(None, None, "mp"), P(None, None, None, "mp"),
        P(None, None, "mp"), P(), P(), P(None, None, None, "mp"), P(None, None, "mp"), P(), P(), P(), P(),
        P("dp", None, "mp"),
    )
    out_specs = (
        P(None, "dp", "mp"), P(None, "dp", "mp"), P(), P(None, None, "mp"), P(None, None, None, "mp"),
        P(None, None, "mp"), P(), P(), P(None, None, None, "mp"), P(None, None, "mp"), P(),
    )
    return jax.shard_map(
        functools.partial(shards, mesh.shape["dp"]), mesh=mesh, in_specs=in_specs, out_specs=out_specs,
        check_vma=False)
```
